32 devices in a mesh: ctx: 4 (over x, core), exp: 8 (over z, y).
Axes of the slice: x: 2, y: 2, z: 4, core: 2. Of those that a mesh axis runs over, the one named last changes fastest.
Arguments:
- inputs: bfloat16 [8, 1536, 768], P('exp', 'ctx'), may hold values from -6 to 6
- segments: int32 [8, 1536], P('exp', 'ctx'), may hold values from 0 to 15, as said below
- routes: int32 [8, 1536, 1], P('exp', 'ctx'), may hold values from 0 to 7; in each aligned block of 384 rows (0 to 383, 384 to 767, ..., all dimensions but the last counted through in order) at most 60 rows name the same one
- cotangent: bfloat16 [8, 1536, 768], P('exp', 'ctx'), may hold values from -6 to 6
- norm_gain: bfloat16 [768], P(('ctx', 'exp')), may hold values from 0.5 to 1.5
- in_proj: bfloat16 [768, 3072], P(('ctx', 'exp')), may hold values from -0.21875 to 0.21875
- conv_taps: bfloat16 [1536, 4], P(('ctx', 'exp')), may hold values from -3 to 3
- conv_bias: bfloat16 [1536], P(('ctx', 'exp')), may hold values from -1.5 to 1.5
- x_proj: bfloat16 [1536, 80], P(('ctx', 'exp')), may hold values from -0.15625 to 0.15625
- dt_proj: bfloat16 [48, 1536], P(None, ('ctx', 'exp')), may hold values from -0.875 to 0.875
- dt_bias: bfloat16 [1536], P(('ctx', 'exp')), may hold values from -5.5 to -3.5
- log_decay: bfloat16 [1536, 16], P(('ctx', 'exp')), may hold values from -4 to 1.1953125
- skip_gain: bfloat16 [1536], P(('ctx', 'exp')), may hold values from 0.5 to 1.5
- out_proj: bfloat16 [1536, 768], P(('ctx', 'exp')), may hold values from -0.3125 to 0.3125
- moe_gain: bfloat16 [768], P(('ctx', 'exp')), may hold values from 0.5 to 1.5
- router: bfloat16 [768, 8], P(('ctx', 'exp')), may hold values from -0.15625 to 0.15625
- expert_in: bfloat16 [8, 768, 3072], P('exp', None, 'ctx'), may hold values from -0.21875 to 0.21875
- expert_out: bfloat16 [8, 3072, 768], P('exp', 'ctx'), may hold values from -0.875 to 0.875
Outputs:
- outputs: bfloat16 [8, 1536, 768], P('exp', 'ctx')
- grad_inputs: float32 [8, 1536, 768], P('exp', 'ctx')
- grad_norm_gain: float32 [768], P(('ctx', 'exp'))
- grad_in_proj: float32 [768, 3072], P(('ctx', 'exp'))
- grad_conv_taps: float32 [1536, 4], P(('ctx', 'exp'))
- grad_conv_bias: float32 [1536], P(('ctx', 'exp'))
- grad_x_proj: float32 [1536, 80], P(('ctx', 'exp'))
- grad_dt_proj: float32 [48, 1536], P(None, ('ctx', 'exp'))
- grad_dt_bias: float32 [1536], P(('ctx', 'exp'))
- grad_log_decay: float32 [1536, 16], P(('ctx', 'exp'))
- grad_skip_gain: float32 [1536], P(('ctx', 'exp'))
- grad_out_proj: float32 [1536, 768], P(('ctx', 'exp'))
- grad_moe_gain: float32 [768], P(('ctx', 'exp'))
- grad_router: float32 [768, 8], P(('ctx', 'exp'))
- grad_expert_in: float32 [8, 768, 3072], P('exp', None, 'ctx')
- grad_expert_out: float32 [8, 3072, 768], P('exp', 'ctx')
The draws below stay inside these ranges and needn't reach their ends.
Inputs may be any that keep to these rules, and one draw needn't show every extreme that they name: `segments`: segment numbers start at 0 and never fall along a sequence; each sequence holds one document that begins among its first 192 positions and ends within its last 192 positions, and each sequence's last document is number 16 - 1. `routes`: among the tokens of one device (aligned blocks of 384 positions), no expert is named more than 60 times, and some expert exactly that many.
All inputs are finite; a program needn't handle non-finite values.
Results may differ from the reference program's by a relative error of at most 0.017.
Values may be sent and summed in bfloat16 or wider, within the bound.
A program may use at most 192 MiB of HBM per device.

```python
import math
import jax
import jax.numpy as jnp
import numpy as np
from jax import lax

D = 768
DI = 1536
NS = 16
R = 48
KC = 4
FF = 3072
TOK_DEV = 384
STATE_BLOCK = 32
DOCS = 16
EXPERTS = 8
SEQS = 8
LEN = 1536
CAPACITY = 60


def draw_segments(key, part):
    first_key = jax.random.fold_in(key, 11)
    second_key = jax.random.fold_in(key, 12)
    third_key = jax.random.fold_in(key, 13)
    long_start = jax.random.randint(first_key, (SEQS, 1), TOK_DEV // 4, TOK_DEV // 2 + 1)
    long_stop = jax.random.randint(second_key, (SEQS, 1), LEN - TOK_DEV // 2, LEN - TOK_DEV // 4 + 1)
    place = jnp.arange(LEN, dtype=jnp.int32)[None, :]
    allowed = (place > 0) & (place < long_start) | (place > long_stop)
    scores = jax.random.randint(third_key, (SEQS, LEN), 0, 1024) * LEN + place
    scores = jnp.where(allowed, scores, -1)
    unused_values, chosen = lax.top_k(scores, DOCS - 3)
    marks = jnp.sum((chosen[:, :, None] == place[:, None, :]).astype(jnp.int32), axis=1)
    marks = marks + (place == long_start).astype(jnp.int32) + (place == long_stop).astype(jnp.int32)
    return jnp.cumsum(marks, axis=1).astype(jnp.int32)


def shard_levels(rng, shape, cuts, least, top_value):
    factor_of, own = 1.0, jax.random.fold_in(rng, 6)
    for axis_at, shards_of in cuts:
        draws = jnp.exp(jax.random.uniform(jax.random.fold_in(own, axis_at), (shards_of,), jnp.float32, least / len(cuts), top_value / len(cuts)))
        factor_of = factor_of * jnp.repeat(draws, shape[axis_at] // shards_of).reshape([-1 if axis == axis_at else 1 for axis in range(len(shape))])
    return factor_of


def shared_out(own_key, own, number, rows, number_of, top, limit, slope):
    order = jax.random.permutation(own_key, number_of)
    heavy_load, usual = portions_of(number_of, rows * top, limit, slope, True), portions_of(number_of, rows * top, limit, slope, False)
    places = jnp.arange(number_of)

    def named(sizes, rotation):
        used = int((sizes > 0).sum())
        fixed = max(1, used // 4)
        moved = fixed + (places - fixed + rotation * (used - fixed)) % max(1, number_of - fixed)
        return jnp.zeros((number_of,), jnp.int32).at[order[jnp.where(places < fixed, places, moved)]].set(jnp.asarray(sizes, jnp.int32))

    sizes = jnp.where(number % 4 == 0, named(heavy_load, number // 4), named(usual, number - number // 4 - 1))
    mixed = jax.random.permutation(jax.random.fold_in(own, 3), number_of)
    donor, receiver = mixed[0:number_of // 2 * 2:2], mixed[1:number_of // 2 * 2:2]
    margin = jnp.minimum(sizes[donor] - 1, limit - sizes[receiver]) // 2
    margin = jnp.where((donor == order[0]) | (receiver == order[0]) | (sizes[receiver] == 0), 0, jnp.maximum(margin, 0))
    moved = jax.random.randint(jax.random.fold_in(own, 4), (number_of // 2,), 0, 1 << 20) % (margin + 1)
    sizes = sizes.at[donor].add(-moved).at[receiver].add(moved)
    items = jnp.searchsorted(jnp.cumsum(sizes), jnp.arange(rows * top), side="right").astype(jnp.int32)
    table = items.reshape(top, rows).T
    table = table[jax.random.permutation(jax.random.fold_in(own, 1), rows)]
    rotation = jax.random.randint(jax.random.fold_in(own, 2), (rows, 1), 0, top)
    return jnp.take_along_axis(table, (jnp.arange(top)[None, :] + rotation) % top, axis=1)


def portions_of(amount, total, limit, lean, full):
    weights = [(1 << 20) // math.isqrt(rank ** lean) + 1 for rank in range(1, amount + 1)]
    largest = limit if full else min(limit, max(-(-total // amount), total * weights[0] // sum(weights)))
    least = 1 if total - largest >= amount - 1 else 0
    counts, spare = [largest] + [least] * (amount - 1), total - largest - least * (amount - 1)
    while spare > 0:
        movable = [i for i in range(1, amount) if counts[i] < largest] or [i for i in range(1, amount) if counts[i] < limit]
        pool, left = sum([weights[i] for i in movable]), spare
        for i in movable:
            more = min(limit - counts[i], max(1, left * weights[i] // pool), spare)
            counts[i] = counts[i] + more
            spare = spare - more
    return np.array(counts)


def scatter_about(key, shape, spread, reach, shards=(), kind=jnp.bfloat16):
    loudness = shard_levels(key, shape, shards, -0.22, 0.18) if shards else 1.0
    drawn = jax.random.normal(key, shape, jnp.float32) * spread * loudness
    return jnp.minimum(jnp.maximum(drawn, -reach), reach).astype(kind)


def setup_inputs(seed: int = 0) -> dict:
    streams_of = jax.random.split(jax.random.key(seed), 19)
    inputs = scatter_about(streams_of[0], (SEQS, LEN, D), 1.0, 6.0, ((0, 8), (1, 4)))
    segments = draw_segments(jax.random.fold_in(streams_of[18], 71), 0)
    routes_keys = jax.random.split(jax.random.fold_in(streams_of[2], 1), SEQS * LEN // TOK_DEV)
    routes_turns = jax.random.permutation(jax.random.fold_in(streams_of[2], 3), SEQS * LEN // TOK_DEV)
    routes = jax.vmap(lambda own, number: shared_out(jax.random.fold_in(streams_of[2], 2), own, number, TOK_DEV, EXPERTS, 1, CAPACITY, 2))(routes_keys, routes_turns).reshape((SEQS, LEN, 1))
    cotangent = scatter_about(streams_of[3], (SEQS, LEN, D), 1.0, 6.0, ((0, 8), (1, 4)))
    norm_gain = jnp.clip(1.0 + 0.1 * jax.random.normal(streams_of[4], (D,), jnp.float32), 0.5, 1.5).astype(jnp.bfloat16)
    in_proj = scatter_about(streams_of[5], (D, 2 * DI), D ** -0.5, 0.21875, ((0, 32),))
    conv_taps = scatter_about(streams_of[6], (DI, KC), KC ** -0.5, 3.0, ((0, 32),))
    conv_bias = scatter_about(streams_of[7], (DI,), 0.3, 1.5, ((0, 32),))
    x_proj = scatter_about(streams_of[8], (DI, R + 2 * NS), DI ** -0.5, 0.15625, ((0, 32),))
    dt_proj = scatter_about(streams_of[9], (R, DI), R ** -0.5, 0.875, ((1, 32),))
    dt_bias = jnp.clip(-5.5 + 2.0 * jax.random.uniform(streams_of[10], (DI,), jnp.float32) ** shard_levels(streams_of[10], (DI,), ((0, 32),), -0.2, 0.2), -5.5, -3.5).astype(jnp.bfloat16)
    log_decay = jnp.clip(-4.0 + 5.1953125 * jax.random.uniform(streams_of[11], (DI, NS), jnp.float32) ** shard_levels(streams_of[11], (DI, NS), ((0, 32),), -0.2, 0.2), -4.0, 1.1953125).astype(jnp.bfloat16)
    skip_gain = jnp.clip(0.5 + 1.0 * jax.random.uniform(streams_of[12], (DI,), jnp.float32) ** shard_levels(streams_of[12], (DI,), ((0, 32),), -0.2, 0.2), 0.5, 1.5).astype(jnp.bfloat16)
    out_proj = scatter_about(streams_of[13], (DI, D), (DI // 4) ** -0.5, 0.3125, ((0, 32),))
    moe_gain = jnp.clip(1.0 + 0.1 * jax.random.normal(streams_of[14], (D,), jnp.float32), 0.5, 1.5).astype(jnp.bfloat16)
    router = scatter_about(streams_of[15], (D, EXPERTS), (2 * D) ** -0.5, 0.15625, ((0, 32),))
    expert_in = scatter_about(streams_of[16], (EXPERTS, D, FF), D ** -0.5, 0.21875, ((0, 8), (2, 4)))
    expert_out = scatter_about(streams_of[17], (EXPERTS, FF, D), (max(FF // (EXPERTS * EXPERTS), 1)) ** -0.5, 0.875, ((0, 8), (1, 4)))
    return {"inputs": inputs, "segments": segments, "routes": routes, "cotangent": cotangent, "norm_gain": norm_gain, "in_proj": in_proj, "conv_taps": conv_taps, "conv_bias": conv_bias, "x_proj": x_proj, "dt_proj": dt_proj, "dt_bias": dt_bias, "log_decay": log_decay, "skip_gain": skip_gain, "out_proj": out_proj, "moe_gain": moe_gain, "router": router, "expert_in": expert_in, "expert_out": expert_out}


EPS = 1e-05
HIGH = lax.Precision.HIGHEST

@jax.custom_vjp
def low(v):
    return lax.optimization_barrier(v.astype(jnp.bfloat16)).astype(jnp.float32)

@jax.custom_vjp
def low_back(v):
    return v

def low_keep(v):
    return (low(v), None)

def low_pass(kept, grad):
    return (grad,)

def back_keep(v):
    return (v, None)

def back_low(kept, grad):
    return (low(grad),)
low.defvjp(low_keep, low_pass)
low_back.defvjp(back_keep, back_low)

def product(left, right):
    return jnp.dot(left, right, precision=HIGH, preferred_element_type=jnp.float32)

def rms_scale(values, gain):
    return values * lax.rsqrt(lax.optimization_barrier(jnp.mean(values * values, axis=-1, keepdims=True)) + EPS) * gain

def conv_mixed(rows, seg_row, taps, bias):
    result = bias[None, :] + taps[:, KC - 1][None, :] * rows
    for offset in range(1, KC):
        moved = jnp.concatenate([jnp.zeros((offset, rows.shape[1]), jnp.float32), rows[:-offset]], axis=0)
        earlier = jnp.concatenate([jnp.full((offset,), -1, jnp.int32), seg_row[:-offset]])
        same_doc = (earlier == seg_row).astype(jnp.float32)
        result = result + taps[:, KC - 1 - offset][None, :] * moved * same_doc[:, None]
    return result

def state_block(state_in, block_in, a_negative):

    def advance(state_now, element):
        step_t, bmat_t, cmat_t, xs_t, keep_t = element
        decay_now = jnp.exp(step_t[:, None] * a_negative) * keep_t
        state_now = decay_now * state_now + (step_t * xs_t)[:, None] * bmat_t[None, :]
        return (state_now, lax.optimization_barrier(jnp.sum(state_now * cmat_t[None, :], axis=1)))
    return lax.scan(advance, state_in, block_in)

def selective(step_size, b_rows, c_rows, xs_val, keep_mask, a_negative):
    block_count = step_size.shape[0] // STATE_BLOCK
    blocks = jax.tree.map(lambda values: values.reshape((block_count, STATE_BLOCK) + values.shape[1:]), (step_size, b_rows, c_rows, xs_val, keep_mask))
    runner = jax.checkpoint(state_block)
    final_state, outputs = lax.scan(lambda state_now, block_in: runner(state_now, block_in, a_negative), jnp.zeros((DI, NS), jnp.float32), blocks)
    return outputs.reshape(step_size.shape[0], DI)

def mixer_sequence(params, row_in, seg_row):
    norm_gain, in_proj, conv_taps, conv_bias, x_proj, dt_proj, dt_bias, log_decay, skip_gain, out_proj = params
    normed = low(rms_scale(row_in, norm_gain))
    mixed_in = low_back(product(normed, in_proj))
    conv_in = low(mixed_in[:, :DI])
    gate_z = mixed_in[:, DI:]
    xs_val = low(jax.nn.silu(conv_mixed(conv_in, seg_row, conv_taps, conv_bias)))
    projected = low_back(product(xs_val, x_proj))
    delta_low = low(projected[:, :R])
    b_rows = projected[:, R:R + NS]
    c_rows = projected[:, R + NS:]
    step_size = jax.nn.softplus(low_back(product(delta_low, dt_proj)) + dt_bias)
    a_negative = -jnp.exp(log_decay)
    earlier = jnp.concatenate([jnp.full((1,), -1, jnp.int32), seg_row[:-1]])
    keep_mask = (earlier == seg_row).astype(jnp.float32)
    scanned = selective(step_size, b_rows, c_rows, xs_val, keep_mask, a_negative) + skip_gain * xs_val
    gated = low(scanned * jax.nn.silu(gate_z))
    return low_back(product(gated, out_proj))

def forward(values_in, segments, routes):
    inputs, norm_gain, in_proj, conv_taps, conv_bias, x_proj, dt_proj, dt_bias, log_decay, skip_gain, out_proj, moe_gain, router, expert_in, expert_out = values_in
    mixer_params = (norm_gain, in_proj, conv_taps, conv_bias, x_proj, dt_proj, dt_bias, log_decay, skip_gain, out_proj)
    mixed = lax.map(lambda paired: mixer_sequence(mixer_params, paired[0], paired[1]), (inputs, segments))
    residual = inputs + mixed
    flat_rows = residual.reshape(-1, D)
    normed = low(rms_scale(flat_rows, moe_gain))
    logits = low_back(product(normed, router))
    probability = jax.nn.softmax(logits, axis=-1)
    chosen = routes.reshape(-1)
    one_hot = chosen[:, None] == jnp.arange(EXPERTS, dtype=jnp.int32)[None, :]
    gate_val = lax.optimization_barrier(jnp.sum(probability * one_hot.astype(jnp.float32), axis=1))
    block_count = flat_rows.shape[0] // TOK_DEV
    running = jnp.cumsum(one_hot.astype(jnp.int32).reshape(block_count, TOK_DEV, EXPERTS), axis=1).reshape(-1, EXPERTS)
    slot_index = lax.optimization_barrier(jnp.sum(running * one_hot.astype(jnp.int32), axis=1)) - 1
    owner_block = jnp.arange(flat_rows.shape[0], dtype=jnp.int32) // TOK_DEV
    target = chosen * (block_count * CAPACITY) + owner_block * CAPACITY + slot_index
    sent_rows = low_back(normed)
    buffer = jnp.zeros((EXPERTS * block_count * CAPACITY, D), jnp.float32).at[target].set(sent_rows)
    buffer = buffer.reshape(EXPERTS, block_count * CAPACITY, D)
    hidden = low_back(jnp.einsum('erd,edf->erf', buffer, expert_in, precision=HIGH))
    active = low(jax.nn.gelu(hidden, approximate=False))
    returned = low(low_back(jnp.einsum('erf,efd->erd', active, expert_out, precision=HIGH)))
    picked = returned.reshape(-1, D)[target]
    outcome = flat_rows + gate_val[:, None] * picked
    return outcome.reshape(inputs.shape)

def reference(inputs, segments, routes, cotangent, norm_gain, in_proj, conv_taps, conv_bias, x_proj, dt_proj, dt_bias, log_decay, skip_gain, out_proj, moe_gain, router, expert_in, expert_out):
    weights = tuple((values.astype(jnp.float32) for values in (inputs, norm_gain, in_proj, conv_taps, conv_bias, x_proj, dt_proj, dt_bias, log_decay, skip_gain, out_proj, moe_gain, router, expert_in, expert_out)))
    outcome, pullback = jax.vjp(lambda *values: forward(values, segments, routes), *weights)
    gradients = pullback(cotangent.astype(jnp.float32))
    return (outcome.astype(jnp.bfloat16), gradients[0], gradients[1], gradients[2], gradients[3], gradients[4], gradients[5], gradients[6], gradients[7], gradients[8], gradients[9], gradients[10], gradients[11], gradients[12], gradients[13], gradients[14])
```

```python
import functools

import jax
import jax.numpy as jnp
from jax import lax
from jax.experimental import pallas as pl
from jax.experimental.pallas import tpu as pltpu
from jax.sharding import PartitionSpec as P

D = 768
DI = 1536
NS = 16
R = 48
KC = 4
LANES = 128
UNROLL = 8
LOG2E = 1.4426950408889634


EPS = 1e-05

def tile(ref, base, lanes):
    return ref[pl.ds(pl.multiple_of(base, UNROLL), UNROLL), lanes]

def row(rows_now, place):
    return jnp.broadcast_to(rows_now[place : place + 1], (NS, LANES))

def put_row(rows_now, place, value):
    at = lax.broadcasted_iota(jnp.int32, (UNROLL, LANES), 0)
    value = jnp.broadcast_to(value, (UNROLL, LANES))
    return value if rows_now is None else jnp.where(at == place, value, rows_now)

def end_kernel(width, step_ref, push_ref, b_ref, rate_ref, end_ref):
    rows, channels = step_ref.shape

    @pl.when(pl.program_id(0) == 0)
    def _():
        end_ref[...] = jnp.zeros_like(end_ref)

    for group in range(0, channels, width):
        pieces = [slice(at, at + LANES) for at in range(group, group + width, LANES)]
        rates = [rate_ref[:, lanes] for lanes in pieces]

        def block(index, states):
            states = list(states)
            steps = [tile(step_ref, index * UNROLL, lanes) for lanes in pieces]
            pushes = [tile(push_ref, index * UNROLL, lanes) for lanes in pieces]
            for place in range(UNROLL):
                t = index * UNROLL + place
                b_now = b_ref[t]
                for k, lanes in enumerate(pieces):
                    decay = jnp.exp2(row(steps[k], place) * rates[k])
                    states[k] = decay * states[k] + b_now * row(pushes[k], place)
            return tuple(states)

        states = lax.fori_loop(0, rows // UNROLL, block, tuple(end_ref[:, lanes] for lanes in pieces))
        for k, lanes in enumerate(pieces):
            end_ref[:, lanes] = states[k]

def out_kernel(width, step_ref, push_ref, b_ref, c_ref, rate_ref, start_ref, y_ref, kept_ref, first_ref, state_ref):
    rows, channels = step_ref.shape

    @pl.when(pl.program_id(0) == 0)
    def _():
        state_ref[...] = start_ref[...]

    first_ref[0] = state_ref[...].astype(first_ref.dtype)
    for group in range(0, channels, width):
        pieces = [slice(at, at + LANES) for at in range(group, group + width, LANES)]
        rates = [rate_ref[:, lanes] for lanes in pieces]

        def block(index, states):
            states = list(states)
            steps = [tile(step_ref, index * UNROLL, lanes) for lanes in pieces]
            pushes = [tile(push_ref, index * UNROLL, lanes) for lanes in pieces]
            outs = [None] * len(pieces)
            for place in range(UNROLL):
                t = index * UNROLL + place
                b_now = b_ref[t]
                c_now = c_ref[t]
                for k, lanes in enumerate(pieces):
                    decay = jnp.exp2(row(steps[k], place) * rates[k])
                    states[k] = decay * states[k] + b_now * row(pushes[k], place)
                    kept_ref[t, :, lanes] = states[k].astype(kept_ref.dtype)
                    outs[k] = put_row(outs[k], place, jnp.sum(states[k] * c_now, axis=0, keepdims=True))
            for k, lanes in enumerate(pieces):
                y_ref[pl.ds(pl.multiple_of(index * UNROLL, UNROLL), UNROLL), lanes] = outs[k]
            return tuple(states)

        states = lax.fori_loop(0, rows // UNROLL, block, tuple(state_ref[:, lanes] for lanes in pieces))
        for k, lanes in enumerate(pieces):
            state_ref[:, lanes] = states[k]

def inflow_kernel(width, step_ref, grad_ref, c_ref, rate_ref, end_ref):
    rows, channels = step_ref.shape

    @pl.when(pl.program_id(0) == 0)
    def _():
        end_ref[...] = jnp.zeros_like(end_ref)

    for group in range(0, channels, width):
        pieces = [slice(at, at + LANES) for at in range(group, group + width, LANES)]
        rates = [rate_ref[:, lanes] for lanes in pieces]

        def block(index, flows):
            flows = list(flows)
            base = rows - UNROLL - index * UNROLL
            steps = [tile(step_ref, base, lanes) for lanes in pieces]
            grads = [tile(grad_ref, base, lanes) for lanes in pieces]
            for place in reversed(range(UNROLL)):
                c_now = c_ref[base + place]
                for k, lanes in enumerate(pieces):
                    decay = jnp.exp2(row(steps[k], place) * rates[k])
                    flows[k] = decay * (c_now * row(grads[k], place) + flows[k])
            return tuple(flows)

        flows = lax.fori_loop(0, rows // UNROLL, block, tuple(end_ref[:, lanes] for lanes in pieces))
        for k, lanes in enumerate(pieces):
            end_ref[:, lanes] = flows[k]

def adjoint_kernel(width, step_ref, push_ref, grad_ref, b_ref, c_ref, kept_ref, first_ref, rate_ref, end_ref,
                   along_ref, slope_ref, gb_ref, gc_ref, ga_ref, flow_ref):
    rows, channels = step_ref.shape

    @pl.when(pl.program_id(0) == 0)
    def _():
        flow_ref[...] = end_ref[...]
        ga_ref[...] = jnp.zeros_like(ga_ref)

    for group in range(0, channels, width):
        pieces = [slice(at, at + LANES) for at in range(group, group + width, LANES)]
        rates = [rate_ref[:, lanes] for lanes in pieces]
        count = len(pieces)

        def block(index, carried, last):
            flows, sums, current = list(carried[:count]), list(carried[count:2*count]), list(carried[2*count:])
            base = rows - UNROLL - index * UNROLL
            steps = [tile(step_ref, base, lanes) for lanes in pieces]
            pushes = [tile(push_ref, base, lanes) for lanes in pieces]
            grads = [tile(grad_ref, base, lanes) for lanes in pieces]
            alongs = [None] * count
            slopes = [None] * count
            for place in reversed(range(UNROLL)):
                t = base + place
                b_now = b_ref[t]
                c_now = c_ref[t]
                gb = gc = None
                for k, lanes in enumerate(pieces):
                    if last and place == 0:
                        prior = first_ref[0, :, lanes].astype(jnp.float32)
                    else:
                        prior = kept_ref[t - 1, :, lanes].astype(jnp.float32)
                    step = row(steps[k], place)
                    grad = row(grads[k], place)
                    decay = jnp.exp2(step * rates[k])
                    adjoint = c_now * grad + flows[k]
                    flows[k] = decay * adjoint
                    decay_grad = flows[k] * prior
                    alongs[k] = put_row(alongs[k], place, jnp.sum(adjoint * b_now, axis=0, keepdims=True))
                    slopes[k] = put_row(slopes[k], place, jnp.sum(decay_grad * rates[k], axis=0, keepdims=True))
                    sums[k] = sums[k] + decay_grad * step
                    part_b = adjoint * row(pushes[k], place)
                    part_c = current[k] * grad
                    gb = part_b if gb is None else gb + part_b
                    gc = part_c if gc is None else gc + part_c
                    current[k] = prior
                if group == 0:
                    gb_ref[t] = gb
                    gc_ref[t] = gc
                else:
                    gb_ref[t] += gb
                    gc_ref[t] += gc
            where = pl.ds(pl.multiple_of(base, UNROLL), UNROLL)
            for k, lanes in enumerate(pieces):
                along_ref[where, lanes] = alongs[k]
                slope_ref[where, lanes] = slopes[k]
            return tuple(flows + sums + current)

        carried = (tuple(flow_ref[:, lanes] for lanes in pieces) + tuple(ga_ref[:, lanes] for lanes in pieces)
                   + tuple(kept_ref[rows - 1, :, lanes].astype(jnp.float32) for lanes in pieces))
        steps = rows // UNROLL
        carried = lax.fori_loop(0, steps - 1, functools.partial(block, last=False), carried)
        carried = block(steps - 1, carried, True)
        for k, lanes in enumerate(pieces):
            flow_ref[:, lanes] = carried[k]
            ga_ref[:, lanes] = carried[count + k]

def over_time(rows, width):
    return pl.BlockSpec((rows, width), lambda i: (i, 0))

PARAMS = pltpu.CompilerParams(vmem_limit_bytes=48 * 1024 * 1024, dimension_semantics=("arbitrary",))

def pick(channels):
    return 512 if channels % 512 == 0 else 128

def scan_end(step, push, b_wide, rates, rows=64):
    tokens, channels = step.shape
    return pl.pallas_call(
        functools.partial(end_kernel, pick(channels)),
        grid=(tokens // rows,),
        in_specs=[pl.BlockSpec((rows, channels), lambda i: (i, 0))] * 2
        + [pl.BlockSpec((rows, NS, LANES), lambda i: (i, 0, 0)), pl.BlockSpec((NS, channels), lambda i: (0, 0))],
        out_specs=pl.BlockSpec((NS, channels), lambda i: (0, 0)),
        out_shape=jax.ShapeDtypeStruct((NS, channels), jnp.float32),
        compiler_params=PARAMS,
    )(step, push, b_wide, rates)

def scan_out(step, push, b_wide, c_wide, rates, start, rows=64):
    tokens, channels = step.shape
    wide = pl.BlockSpec((rows, channels), lambda i: (i, 0))
    cast = pl.BlockSpec((rows, NS, LANES), lambda i: (i, 0, 0))
    fixed = pl.BlockSpec((NS, channels), lambda i: (0, 0))
    return pl.pallas_call(
        functools.partial(out_kernel, pick(channels)),
        grid=(tokens // rows,),
        in_specs=[wide, wide, cast, cast, fixed, fixed],
        out_specs=[wide, pl.BlockSpec((rows, NS, channels), lambda i: (i, 0, 0)), pl.BlockSpec((1, NS, channels), lambda i: (i, 0, 0))],
        out_shape=[jax.ShapeDtypeStruct((tokens, channels), jnp.float32),
                   jax.ShapeDtypeStruct((tokens, NS, channels), jnp.bfloat16),
                   jax.ShapeDtypeStruct((tokens // rows, NS, channels), jnp.bfloat16)],
        scratch_shapes=[pltpu.VMEM((NS, channels), jnp.float32)],
        compiler_params=PARAMS,
    )(step, push, b_wide, c_wide, rates, start)

def scan_inflow(step, grad, c_wide, rates, rows=64):
    tokens, channels = step.shape
    last = tokens // rows - 1
    return pl.pallas_call(
        functools.partial(inflow_kernel, pick(channels)),
        grid=(tokens // rows,),
        in_specs=[pl.BlockSpec((rows, channels), lambda i: (last - i, 0))] * 2
        + [pl.BlockSpec((rows, NS, LANES), lambda i: (last - i, 0, 0)), pl.BlockSpec((NS, channels), lambda i: (0, 0))],
        out_specs=pl.BlockSpec((NS, channels), lambda i: (0, 0)),
        out_shape=jax.ShapeDtypeStruct((NS, channels), jnp.float32),
        compiler_params=PARAMS,
    )(step, grad, c_wide, rates)

def scan_adjoint(step, push, grad, b_wide, c_wide, kept, firsts, rates, end, rows=64):
    tokens, channels = step.shape
    last = tokens // rows - 1
    wide = pl.BlockSpec((rows, channels), lambda i: (last - i, 0))
    cast = pl.BlockSpec((rows, NS, LANES), lambda i: (last - i, 0, 0))
    fixed = pl.BlockSpec((NS, channels), lambda i: (0, 0))
    return pl.pallas_call(
        functools.partial(adjoint_kernel, pick(channels)),
        grid=(tokens // rows,),
        in_specs=[wide, wide, wide, cast, cast, pl.BlockSpec((rows, NS, channels), lambda i: (last - i, 0, 0)),
                  pl.BlockSpec((1, NS, channels), lambda i: (last - i, 0, 0)), fixed, fixed],
        out_specs=[wide, wide, cast, cast, fixed],
        out_shape=[jax.ShapeDtypeStruct((tokens, channels), jnp.float32)] * 2
        + [jax.ShapeDtypeStruct((tokens, NS, LANES), jnp.float32)] * 2
        + [jax.ShapeDtypeStruct((NS, channels), jnp.float32)],
        scratch_shapes=[pltpu.VMEM((NS, channels), jnp.float32)],
        compiler_params=PARAMS,
    )(step, push, grad, b_wide, c_wide, kept, firsts, rates, end)


def shifted(value, axis, steps):
    count = lax.axis_size(axis)
    initial, last = (max(0, -steps), min(count, count - steps))
    return lax.ppermute(value, axis, [(source, source + steps) for source in range(initial, last)])


def rms_scale(values, gain):
    return values * lax.rsqrt(jnp.mean(values * values, axis=-1, keepdims=True) + EPS) * gain


def conv_local(ext_rows, taps, bias, ext_ids):
    length = ext_rows.shape[0] - (KC - 1)
    own_ids = ext_ids[KC - 1 :]
    result = jnp.zeros((length, ext_rows.shape[1]), jnp.float32) + bias[None, :]
    for offset in range(KC):
        same_doc = (ext_ids[offset : offset + length] == own_ids).astype(jnp.float32)
        result = (
            result
            + taps[:, offset][None, :] * ext_rows[offset : offset + length] * same_doc[:, None]
        )
    return result


def body(
    inputs,
    segments,
    routes,
    cotangent,
    norm_gain,
    in_proj,
    conv_taps,
    conv_bias,
    x_proj,
    dt_proj,
    dt_bias,
    log_decay,
    skip_gain,
    out_proj,
    moe_gain,
    router,
    expert_in,
    expert_out,
):
    everyone = ("ctx", "exp")
    experts = router.shape[1]
    half_rows = norm_gain.shape[0]
    columns = (
        x_proj,
        dt_proj.T,
        conv_taps,
        conv_bias[:, None],
        dt_bias[:, None],
        log_decay,
        skip_gain[:, None],
        jnp.concatenate([norm_gain, moe_gain])[:, None],
        router.reshape(2 * half_rows, experts // 2),
    )
    widths = [part.shape[1] for part in columns]
    ends = [sum(widths[: k + 1]) for k in range(len(widths))]
    full_small = lax.all_gather(jnp.concatenate(columns, axis=1), everyone, axis=0, tiled=True)
    full_in = lax.all_gather(in_proj, everyone, axis=0, tiled=True)
    full_out = lax.all_gather(out_proj, everyone, axis=0, tiled=True)
    full_xproj, full_dt, full_taps, full_bias, full_dtbias, full_decay, full_skip, gains, full_router = [
        full_small[:, end - width : end] for end, width in zip(ends, widths)
    ]
    full_dt = full_dt.T
    full_bias, full_dtbias, full_skip = full_bias[:, 0], full_dtbias[:, 0], full_skip[:, 0]
    gains = gains.reshape(-1, 2, half_rows)
    full_norm, full_moe = gains[:, 0].reshape(-1), gains[:, 1].reshape(-1)
    full_router = full_router.reshape(-1, experts)
    tokens_here = inputs.shape[1]
    capacity = 5 * tokens_here // (4 * experts)
    flat_in = inputs[0].astype(jnp.float32)
    seg_row = segments[0]
    position = lax.axis_index("ctx")
    norm_one_value, norm_one_pull = jax.vjp(rms_scale, flat_in, full_norm.astype(jnp.float32))
    normed_one = norm_one_value.astype(jnp.bfloat16)
    mixed_in = jnp.dot(normed_one, full_in, preferred_element_type=jnp.float32)
    conv_in = mixed_in[:, :DI].astype(jnp.bfloat16)
    gate_z = mixed_in[:, DI:]
    edge_rows, edge_ids = shifted(
        (conv_in[tokens_here - (KC - 1) :], seg_row[tokens_here - (KC - 1) :].astype(jnp.bfloat16)),
        "ctx",
        1,
    )
    prior_ids = jnp.where(position > 0, edge_ids.astype(jnp.int32), -1)
    ext_ids = jnp.concatenate([prior_ids, seg_row])
    ext_rows = jnp.concatenate([edge_rows, conv_in], axis=0).astype(jnp.float32)
    conv_out, conv_pull = jax.vjp(
        lambda rows_in, taps_in, bias_in: conv_local(rows_in, taps_in, bias_in, ext_ids),
        ext_rows,
        full_taps.astype(jnp.float32),
        full_bias.astype(jnp.float32),
    )
    silu_value, silu_pull = jax.vjp(jax.nn.silu, conv_out)
    xs_val = silu_value.astype(jnp.bfloat16)
    xs_wide = xs_val.astype(jnp.float32)
    projected = jnp.dot(xs_val, full_xproj, preferred_element_type=jnp.float32)
    delta_low = projected[:, :R].astype(jnp.bfloat16)
    b_rows = projected[:, R : R + NS]
    c_rows = projected[:, R + NS :]
    dt_pre = jnp.dot(delta_low, full_dt, preferred_element_type=jnp.float32) + full_dtbias.astype(
        jnp.float32
    )
    step_size = jax.nn.softplus(dt_pre)
    a_swap = -jnp.exp(full_decay.astype(jnp.float32)).T
    earlier = jnp.concatenate([prior_ids[KC - 2 :], seg_row[:-1]])
    keep_mask = (earlier == seg_row).astype(jnp.float32)
    masked_step = jnp.where(keep_mask[:, None] > 0, step_size, 1e30)
    push = step_size * xs_wide
    b_wide = jnp.broadcast_to(b_rows[:, :, None], (tokens_here, NS, LANES))
    c_wide = jnp.broadcast_to(c_rows[:, :, None], (tokens_here, NS, LANES))
    rates = a_swap * LOG2E
    block_end = scan_end(masked_step, push, b_wide, rates)
    block_product = jnp.exp2(jnp.sum(masked_step, axis=0)[None, :] * rates)
    gathered = lax.all_gather(
        jnp.stack([block_product, block_end]).astype(jnp.bfloat16)[None], "ctx", axis=0, tiled=True
    ).astype(jnp.float32)
    all_products, all_ends = gathered[:, 0], gathered[:, 1]
    zeros_state = jnp.zeros((NS, DI), jnp.float32)

    def fold_start(index_now, start_now):
        return jnp.where(
            index_now < position,
            all_products[index_now] * start_now + all_ends[index_now],
            start_now,
        )

    start_state = zeros_state
    for index_now in range(all_products.shape[0]):
        start_state = fold_start(index_now, start_state)
    scan_rows, kept, firsts = scan_out(masked_step, push, b_wide, c_wide, rates, start_state)
    skip_wide = full_skip.astype(jnp.float32)
    scanned_y = scan_rows + skip_wide * xs_wide
    gated_wide, gated_pull = jax.vjp(
        lambda scan_in, gate_in: scan_in * jax.nn.silu(gate_in), scanned_y, gate_z
    )
    gated = gated_wide.astype(jnp.bfloat16)
    mixed = jnp.dot(gated, full_out, preferred_element_type=jnp.float32)
    residual = flat_in + mixed
    norm_two_value, norm_two_pull = jax.vjp(rms_scale, residual, full_moe.astype(jnp.float32))
    normed_two = norm_two_value.astype(jnp.bfloat16)
    logits = jnp.dot(normed_two, full_router, preferred_element_type=jnp.float32)
    probability = jax.nn.softmax(logits, axis=-1)
    route_ids = routes[0, :, 0]
    one_hot = route_ids[:, None] == jnp.arange(experts, dtype=jnp.int32)[None, :]
    one_float = one_hot.astype(jnp.float32)
    gate_val = jnp.sum(probability * one_float, axis=1)
    running = jnp.cumsum(one_hot.astype(jnp.int32), axis=0)
    slot_index = jnp.sum(running * one_hot.astype(jnp.int32), axis=1) - 1
    target = route_ids * capacity + slot_index
    buffer = (
        jnp.zeros((experts * capacity, D), jnp.bfloat16)
        .at[target]
        .set(normed_two)
        .reshape(experts, capacity, D)
    )
    full_expert_in, full_expert_out = (
        lax.all_gather(expert_in, "ctx", axis=2, tiled=True),
        lax.all_gather(expert_out, "ctx", axis=1, tiled=True),
    )
    weight_in = full_expert_in[0]
    weight_out = full_expert_out[0]
    rows_in = lax.all_to_all(buffer, "exp", split_axis=0, concat_axis=0, tiled=True)
    hidden_pre = jnp.einsum("srd,df->srf", rows_in, weight_in, preferred_element_type=jnp.float32)
    active = jax.nn.gelu(hidden_pre, approximate=False).astype(jnp.bfloat16)
    result = jnp.einsum(
        "srf,fd->srd", active, weight_out, preferred_element_type=jnp.float32
    ).astype(jnp.bfloat16)
    expert_result, hidden_pre, active, received = (result, hidden_pre, active, rows_in)
    returned = lax.all_to_all(expert_result, "exp", split_axis=0, concat_axis=0, tiled=True)
    picked = returned.reshape(-1, D)[target].astype(jnp.float32)
    outcome = residual + gate_val[:, None] * picked
    out_block = outcome.astype(jnp.bfloat16)[None]
    grad_out = cotangent[0].astype(jnp.float32)
    grad_gate = jnp.sum(grad_out * picked, axis=1)
    grad_pick = (grad_out * gate_val[:, None]).astype(jnp.bfloat16)
    grad_buffer = (
        jnp.zeros((experts * capacity, D), jnp.bfloat16)
        .at[target]
        .set(grad_pick)
        .reshape(experts, capacity, D)
    )
    grad_result = lax.all_to_all(grad_buffer, "exp", split_axis=0, concat_axis=0, tiled=True)
    grad_active = jnp.einsum(
        "srd,fd->srf", grad_result, weight_out, preferred_element_type=jnp.float32
    )
    grad_expert_out = jnp.einsum(
        "srf,srd->fd", active, grad_result, preferred_element_type=jnp.float32
    )
    gelu_value, gelu_pull = jax.vjp(
        lambda values: jax.nn.gelu(values, approximate=False), hidden_pre
    )
    grad_hidden = gelu_pull(grad_active)[0].astype(jnp.bfloat16)
    grad_expert_in = jnp.einsum(
        "srd,srf->df", received, grad_hidden, preferred_element_type=jnp.float32
    )
    grad_rows = jnp.einsum(
        "srf,df->srd", grad_hidden, weight_in, preferred_element_type=jnp.float32
    ).astype(jnp.bfloat16)
    grad_sent = lax.all_to_all(grad_rows, "exp", split_axis=0, concat_axis=0, tiled=True)
    grad_from_experts = grad_sent.reshape(-1, D)[target].astype(jnp.float32)
    grad_w_in, grad_w_out = (
        lax.psum_scatter(
            grad_expert_in[None].astype(jnp.bfloat16), "ctx", scatter_dimension=2, tiled=True
        ).astype(jnp.float32),
        lax.psum_scatter(
            grad_expert_out[None].astype(jnp.bfloat16), "ctx", scatter_dimension=1, tiled=True
        ).astype(jnp.float32),
    )
    grad_probs = grad_gate[:, None] * one_float
    grad_logits = (
        probability * (grad_probs - jnp.sum(grad_probs * probability, axis=1, keepdims=True))
    ).astype(jnp.bfloat16)
    grad_router = jnp.dot(normed_two.T, grad_logits, preferred_element_type=jnp.float32)
    grad_normed_two = grad_from_experts + jnp.dot(
        grad_logits, full_router.T, preferred_element_type=jnp.float32
    )
    grad_resid_norm, grad_moe_gain = norm_two_pull(grad_normed_two)
    grad_resid = grad_out + grad_resid_norm
    grad_mixed = grad_resid.astype(jnp.bfloat16)
    grad_gated = jnp.dot(grad_mixed, full_out.T, preferred_element_type=jnp.float32)
    grad_out_proj = jnp.dot(gated.T, grad_mixed, preferred_element_type=jnp.float32)
    grad_y, grad_z = gated_pull(grad_gated)
    grad_skip = jnp.sum(grad_y * xs_wide, axis=0)
    local_inflow = scan_inflow(masked_step, grad_y, c_wide, rates)
    all_inflows = lax.all_gather(
        local_inflow[None].astype(jnp.bfloat16), "ctx", axis=0, tiled=True
    ).astype(jnp.float32)
    total_ctx = all_inflows.shape[0]

    def fold_end(step_index, end_now):
        source = total_ctx - 1 - step_index
        return jnp.where(
            source > position, all_inflows[source] + all_products[source] * end_now, end_now
        )

    end_inflow = zeros_state
    for step_index in range(total_ctx):
        end_inflow = fold_end(step_index, end_inflow)
    along_b, slope, wide_b, wide_c, grad_a = scan_adjoint(
        masked_step, push, grad_y, b_wide, c_wide, kept, firsts, rates, end_inflow
    )
    grad_step_all = along_b * xs_wide + slope * (1.0 / LOG2E)
    grad_xss = along_b * step_size
    grad_bs = jnp.sum(wide_b, axis=2)
    grad_cs = jnp.sum(wide_c, axis=2)
    grad_log_decay = (grad_a * a_swap).T
    soft_slope = jax.nn.sigmoid(dt_pre)
    grad_pre_wide = grad_step_all * soft_slope
    grad_dt_bias = jnp.sum(grad_pre_wide, axis=0)
    grad_dt_pre = grad_pre_wide.astype(jnp.bfloat16)
    grad_dt_proj = jnp.dot(delta_low.T, grad_dt_pre, preferred_element_type=jnp.float32)
    grad_delta = jnp.dot(grad_dt_pre, full_dt.T, preferred_element_type=jnp.float32)
    grad_projected = jnp.concatenate(
        [grad_delta, grad_bs, grad_cs], axis=1
    ).astype(jnp.bfloat16)
    grad_x_proj = jnp.dot(xs_val.T, grad_projected, preferred_element_type=jnp.float32)
    grad_xs_total = (
        skip_wide * grad_y
        + grad_xss
        + jnp.dot(grad_projected, full_xproj.T, preferred_element_type=jnp.float32)
    )
    grad_conv = silu_pull(grad_xs_total)[0]
    grad_ext, grad_taps, grad_cbias = conv_pull(grad_conv)
    from_next = shifted(grad_ext[: KC - 1], "ctx", -1)
    grad_conv_in = grad_ext[KC - 1 :] + jnp.concatenate(
        [jnp.zeros((tokens_here - (KC - 1), DI), jnp.float32), from_next], axis=0
    )
    grad_mixed_in = jnp.concatenate([grad_conv_in, grad_z], axis=1).astype(jnp.bfloat16)
    grad_in_proj = jnp.dot(normed_one.T, grad_mixed_in, preferred_element_type=jnp.float32)
    grad_normed_one = jnp.dot(grad_mixed_in, full_in.T, preferred_element_type=jnp.float32)
    grad_inputs_norm, grad_norm_gain = norm_one_pull(grad_normed_one)
    grad_inputs = grad_resid + grad_inputs_norm
    sums = (
        grad_x_proj,
        grad_dt_proj.T,
        grad_taps,
        grad_cbias[:, None],
        grad_dt_bias[:, None],
        grad_log_decay,
        grad_skip[:, None],
        jnp.stack(
            [grad_norm_gain.reshape(-1, half_rows), grad_moe_gain.reshape(-1, half_rows)], axis=1
        ).reshape(-1, 1),
        grad_router.reshape(-1, experts // 2),
    )

    def scatter(values):
        return lax.psum_scatter(values, everyone, scatter_dimension=0, tiled=True)

    own_in = scatter(grad_in_proj.astype(jnp.bfloat16)).astype(jnp.float32)
    own_out = scatter(grad_out_proj.astype(jnp.bfloat16)).astype(jnp.float32)
    own_small = scatter(jnp.concatenate(sums, axis=1))
    own_x, own_dt, own_taps, own_bias, own_dtbias, own_decay, own_skip, own_gains, own_router = [
        own_small[:, end - width : end] for end, width in zip(ends, widths)
    ]
    return (
        out_block,
        grad_inputs[None],
        own_gains[:half_rows, 0],
        own_in,
        own_taps,
        own_bias[:, 0],
        own_x,
        own_dt.T,
        own_dtbias[:, 0],
        own_decay,
        own_skip[:, 0],
        own_out,
        own_gains[half_rows:, 0],
        own_router.reshape(half_rows, experts),
        grad_w_in,
        grad_w_out,
    )


def solution(mesh):
    placed = (
        P("exp", "ctx", None),
        P("exp", "ctx"),
        P("exp", "ctx", None),
        P("exp", "ctx", None),
        P(("ctx", "exp")),
        P(("ctx", "exp"), None),
        P(("ctx", "exp"), None),
        P(("ctx", "exp")),
        P(("ctx", "exp"), None),
        P(None, ("ctx", "exp")),
        P(("ctx", "exp")),
        P(("ctx", "exp"), None),
        P(("ctx", "exp")),
        P(("ctx", "exp"), None),
        P(("ctx", "exp")),
        P(("ctx", "exp"), None),
        P("exp", None, "ctx"),
        P("exp", "ctx", None),
    )
    return jax.shard_map(
        body,
        mesh=mesh,
        in_specs=placed,
        out_specs=(
            P("exp", "ctx", None),
            P("exp", "ctx", None),
            P(("ctx", "exp")),
            P(("ctx", "exp"), None),
            P(("ctx", "exp"), None),
            P(("ctx", "exp")),
            P(("ctx", "exp"), None),
            P(None, ("ctx", "exp")),
            P(("ctx", "exp")),
            P(("ctx", "exp"), None),
            P(("ctx", "exp")),
            P(("ctx", "exp"), None),
            P(("ctx", "exp")),
            P(("ctx", "exp"), None),
            P("exp", None, "ctx"),
            P("exp", "ctx", None),
        ),
        check_vma=False,
    )
```

```python
import functools

import jax
import jax.numpy as jnp
from jax import lax
from jax.experimental import pallas as pl
from jax.experimental.pallas import tpu as pltpu
from jax.sharding import PartitionSpec as P

D = 768
DI = 1536
NS = 16
R = 48
KC = 4
LANES = 128
UNROLL = 8
LOG2E = 1.4426950408889634


EPS = 1e-05
MESH = pl.DeviceIdType.MESH

def tile(ref, base, lanes):
    return ref[pl.ds(pl.multiple_of(base, UNROLL), UNROLL), lanes]

def row(rows_now, place):
    return jnp.broadcast_to(rows_now[place : place + 1], (NS, LANES))

def put_row(rows_now, place, value):
    at = lax.broadcasted_iota(jnp.int32, (UNROLL, LANES), 0)
    value = jnp.broadcast_to(value, (UNROLL, LANES))
    return value if rows_now is None else jnp.where(at == place, value, rows_now)

def end_kernel(width, step_ref, push_ref, b_ref, rate_ref, end_ref):
    rows, channels = step_ref.shape

    @pl.when(pl.program_id(0) == 0)
    def _():
        end_ref[...] = jnp.zeros_like(end_ref)

    for group in range(0, channels, width):
        pieces = [slice(at, at + LANES) for at in range(group, group + width, LANES)]
        rates = [rate_ref[:, lanes] for lanes in pieces]

        def block(index, states):
            states = list(states)
            steps = [tile(step_ref, index * UNROLL, lanes) for lanes in pieces]
            pushes = [tile(push_ref, index * UNROLL, lanes) for lanes in pieces]
            for place in range(UNROLL):
                t = index * UNROLL + place
                b_now = b_ref[t]
                for k, lanes in enumerate(pieces):
                    decay = jnp.exp2(row(steps[k], place) * rates[k])
                    states[k] = decay * states[k] + b_now * row(pushes[k], place)
            return tuple(states)

        states = lax.fori_loop(0, rows // UNROLL, block, tuple(end_ref[:, lanes] for lanes in pieces))
        for k, lanes in enumerate(pieces):
            end_ref[:, lanes] = states[k]

def out_kernel(width, step_ref, push_ref, b_ref, c_ref, rate_ref, start_ref, y_ref, kept_ref, first_ref, state_ref):
    rows, channels = step_ref.shape

    @pl.when(pl.program_id(0) == 0)
    def _():
        state_ref[...] = start_ref[...]

    first_ref[0] = state_ref[...].astype(first_ref.dtype)
    for group in range(0, channels, width):
        pieces = [slice(at, at + LANES) for at in range(group, group + width, LANES)]
        rates = [rate_ref[:, lanes] for lanes in pieces]

        def block(index, states):
            states = list(states)
            steps = [tile(step_ref, index * UNROLL, lanes) for lanes in pieces]
            pushes = [tile(push_ref, index * UNROLL, lanes) for lanes in pieces]
            outs = [None] * len(pieces)
            for place in range(UNROLL):
                t = index * UNROLL + place
                b_now = b_ref[t]
                c_now = c_ref[t]
                for k, lanes in enumerate(pieces):
                    decay = jnp.exp2(row(steps[k], place) * rates[k])
                    states[k] = decay * states[k] + b_now * row(pushes[k], place)
                    kept_ref[t, :, lanes] = states[k].astype(kept_ref.dtype)
                    outs[k] = put_row(outs[k], place, jnp.sum(states[k] * c_now, axis=0, keepdims=True))
            for k, lanes in enumerate(pieces):
                y_ref[pl.ds(pl.multiple_of(index * UNROLL, UNROLL), UNROLL), lanes] = outs[k]
            return tuple(states)

        states = lax.fori_loop(0, rows // UNROLL, block, tuple(state_ref[:, lanes] for lanes in pieces))
        for k, lanes in enumerate(pieces):
            state_ref[:, lanes] = states[k]

def inflow_kernel(width, step_ref, grad_ref, c_ref, rate_ref, end_ref):
    rows, channels = step_ref.shape

    @pl.when(pl.program_id(0) == 0)
    def _():
        end_ref[...] = jnp.zeros_like(end_ref)

    for group in range(0, channels, width):
        pieces = [slice(at, at + LANES) for at in range(group, group + width, LANES)]
        rates = [rate_ref[:, lanes] for lanes in pieces]

        def block(index, flows):
            flows = list(flows)
            base = rows - UNROLL - index * UNROLL
            steps = [tile(step_ref, base, lanes) for lanes in pieces]
            grads = [tile(grad_ref, base, lanes) for lanes in pieces]
            for place in reversed(range(UNROLL)):
                c_now = c_ref[base + place]
                for k, lanes in enumerate(pieces):
                    decay = jnp.exp2(row(steps[k], place) * rates[k])
                    flows[k] = decay * (c_now * row(grads[k], place) + flows[k])
            return tuple(flows)

        flows = lax.fori_loop(0, rows // UNROLL, block, tuple(end_ref[:, lanes] for lanes in pieces))
        for k, lanes in enumerate(pieces):
            end_ref[:, lanes] = flows[k]

def adjoint_kernel(width, step_ref, push_ref, grad_ref, b_ref, c_ref, kept_ref, first_ref, rate_ref, end_ref,
                   along_ref, slope_ref, gb_ref, gc_ref, ga_ref, flow_ref):
    rows, channels = step_ref.shape

    @pl.when(pl.program_id(0) == 0)
    def _():
        flow_ref[...] = end_ref[...]
        ga_ref[...] = jnp.zeros_like(ga_ref)

    for group in range(0, channels, width):
        pieces = [slice(at, at + LANES) for at in range(group, group + width, LANES)]
        rates = [rate_ref[:, lanes] for lanes in pieces]
        count = len(pieces)

        def block(index, carried, last):
            flows, sums, current = list(carried[:count]), list(carried[count:2*count]), list(carried[2*count:])
            base = rows - UNROLL - index * UNROLL
            steps = [tile(step_ref, base, lanes) for lanes in pieces]
            pushes = [tile(push_ref, base, lanes) for lanes in pieces]
            grads = [tile(grad_ref, base, lanes) for lanes in pieces]
            alongs = [None] * count
            slopes = [None] * count
            for place in reversed(range(UNROLL)):
                t = base + place
                b_now = b_ref[t]
                c_now = c_ref[t]
                gb = gc = None
                for k, lanes in enumerate(pieces):
                    if last and place == 0:
                        prior = first_ref[0, :, lanes].astype(jnp.float32)
                    else:
                        prior = kept_ref[t - 1, :, lanes].astype(jnp.float32)
                    step = row(steps[k], place)
                    grad = row(grads[k], place)
                    decay = jnp.exp2(step * rates[k])
                    adjoint = c_now * grad + flows[k]
                    flows[k] = decay * adjoint
                    decay_grad = flows[k] * prior
                    alongs[k] = put_row(alongs[k], place, jnp.sum(adjoint * b_now, axis=0, keepdims=True))
                    slopes[k] = put_row(slopes[k], place, jnp.sum(decay_grad * rates[k], axis=0, keepdims=True))
                    sums[k] = sums[k] + decay_grad * step
                    part_b = adjoint * row(pushes[k], place)
                    part_c = current[k] * grad
                    gb = part_b if gb is None else gb + part_b
                    gc = part_c if gc is None else gc + part_c
                    current[k] = prior
                if group == 0:
                    gb_ref[t] = gb
                    gc_ref[t] = gc
                else:
                    gb_ref[t] += gb
                    gc_ref[t] += gc
            where = pl.ds(pl.multiple_of(base, UNROLL), UNROLL)
            for k, lanes in enumerate(pieces):
                along_ref[where, lanes] = alongs[k]
                slope_ref[where, lanes] = slopes[k]
            return tuple(flows + sums + current)

        carried = (tuple(flow_ref[:, lanes] for lanes in pieces) + tuple(ga_ref[:, lanes] for lanes in pieces)
                   + tuple(kept_ref[rows - 1, :, lanes].astype(jnp.float32) for lanes in pieces))
        steps = rows // UNROLL
        carried = lax.fori_loop(0, steps - 1, functools.partial(block, last=False), carried)
        carried = block(steps - 1, carried, True)
        for k, lanes in enumerate(pieces):
            flow_ref[:, lanes] = carried[k]
            ga_ref[:, lanes] = carried[count + k]

def over_time(rows, width):
    return pl.BlockSpec((rows, width), lambda i: (i, 0))

PARAMS = pltpu.CompilerParams(vmem_limit_bytes=48 * 1024 * 1024, dimension_semantics=("arbitrary",))

def pick(channels):
    return 512 if channels % 512 == 0 else 128

def scan_end(step, push, b_wide, rates, rows=64):
    tokens, channels = step.shape
    return pl.pallas_call(
        functools.partial(end_kernel, pick(channels)),
        grid=(tokens // rows,),
        in_specs=[pl.BlockSpec((rows, channels), lambda i: (i, 0))] * 2
        + [pl.BlockSpec((rows, NS, LANES), lambda i: (i, 0, 0)), pl.BlockSpec((NS, channels), lambda i: (0, 0))],
        out_specs=pl.BlockSpec((NS, channels), lambda i: (0, 0)),
        out_shape=jax.ShapeDtypeStruct((NS, channels), jnp.float32),
        compiler_params=PARAMS,
    )(step, push, b_wide, rates)

def scan_out(step, push, b_wide, c_wide, rates, start, rows=64):
    tokens, channels = step.shape
    wide = pl.BlockSpec((rows, channels), lambda i: (i, 0))
    cast = pl.BlockSpec((rows, NS, LANES), lambda i: (i, 0, 0))
    fixed = pl.BlockSpec((NS, channels), lambda i: (0, 0))
    return pl.pallas_call(
        functools.partial(out_kernel, pick(channels)),
        grid=(tokens // rows,),
        in_specs=[wide, wide, cast, cast, fixed, fixed],
        out_specs=[wide, pl.BlockSpec((rows, NS, channels), lambda i: (i, 0, 0)), pl.BlockSpec((1, NS, channels), lambda i: (i, 0, 0))],
        out_shape=[jax.ShapeDtypeStruct((tokens, channels), jnp.float32),
                   jax.ShapeDtypeStruct((tokens, NS, channels), jnp.bfloat16),
                   jax.ShapeDtypeStruct((tokens // rows, NS, channels), jnp.bfloat16)],
        scratch_shapes=[pltpu.VMEM((NS, channels), jnp.float32)],
        compiler_params=PARAMS,
    )(step, push, b_wide, c_wide, rates, start)

def scan_inflow(step, grad, c_wide, rates, rows=64):
    tokens, channels = step.shape
    last = tokens // rows - 1
    return pl.pallas_call(
        functools.partial(inflow_kernel, pick(channels)),
        grid=(tokens // rows,),
        in_specs=[pl.BlockSpec((rows, channels), lambda i: (last - i, 0))] * 2
        + [pl.BlockSpec((rows, NS, LANES), lambda i: (last - i, 0, 0)), pl.BlockSpec((NS, channels), lambda i: (0, 0))],
        out_specs=pl.BlockSpec((NS, channels), lambda i: (0, 0)),
        out_shape=jax.ShapeDtypeStruct((NS, channels), jnp.float32),
        compiler_params=PARAMS,
    )(step, grad, c_wide, rates)

def scan_adjoint(step, push, grad, b_wide, c_wide, kept, firsts, rates, end, rows=64):
    tokens, channels = step.shape
    last = tokens // rows - 1
    wide = pl.BlockSpec((rows, channels), lambda i: (last - i, 0))
    cast = pl.BlockSpec((rows, NS, LANES), lambda i: (last - i, 0, 0))
    fixed = pl.BlockSpec((NS, channels), lambda i: (0, 0))
    return pl.pallas_call(
        functools.partial(adjoint_kernel, pick(channels)),
        grid=(tokens // rows,),
        in_specs=[wide, wide, wide, cast, cast, pl.BlockSpec((rows, NS, channels), lambda i: (last - i, 0, 0)),
                  pl.BlockSpec((1, NS, channels), lambda i: (last - i, 0, 0)), fixed, fixed],
        out_specs=[wide, wide, cast, cast, fixed],
        out_shape=[jax.ShapeDtypeStruct((tokens, channels), jnp.float32)] * 2
        + [jax.ShapeDtypeStruct((tokens, NS, LANES), jnp.float32)] * 2
        + [jax.ShapeDtypeStruct((NS, channels), jnp.float32)],
        scratch_shapes=[pltpu.VMEM((NS, channels), jnp.float32)],
        compiler_params=PARAMS,
    )(step, push, grad, b_wide, c_wide, kept, firsts, rates, end)


def shifted(value, axis, steps):
    count = lax.axis_size(axis)
    initial, last = (max(0, -steps), min(count, count - steps))
    return lax.ppermute(value, axis, [(source, source + steps) for source in range(initial, last)])


def rms_scale(values, gain):
    return values * lax.rsqrt(jnp.mean(values * values, axis=-1, keepdims=True) + EPS) * gain


def conv_local(ext_rows, taps, bias, ext_ids):
    length = ext_rows.shape[0] - (KC - 1)
    own_ids = ext_ids[KC - 1 :]
    result = jnp.zeros((length, ext_rows.shape[1]), jnp.float32) + bias[None, :]
    for offset in range(KC):
        same_doc = (ext_ids[offset : offset + length] == own_ids).astype(jnp.float32)
        result = (
            result
            + taps[:, offset][None, :] * ext_rows[offset : offset + length] * same_doc[:, None]
        )
    return result


def bit_positions(sizes):
    return [(axis, size.bit_length() - 2 - k) for axis, size in sizes for k in range(size.bit_length() - 1)]


def own_bit(place):
    axis, level = place
    return lax.rem(lax.axis_index(axis) // 2**level, 2)


def partner(place):
    axis, level = place
    where = {"ctx": lax.axis_index("ctx"), "exp": lax.axis_index("exp")}
    where[axis] = where[axis] + (1 - 2 * own_bit(place)) * 2**level
    return (where["ctx"], where["exp"])


def meet(places):
    barrier = pltpu.get_barrier_semaphore()
    for place in places:
        pl.semaphore_signal(barrier, inc=1, device_id=partner(place), device_id_type=MESH)
    pl.semaphore_wait(barrier, len(places))


def gather_kernel(places, streams, count, *refs):
    shards, wholes = refs[:count], refs[count : 2 * count]
    send_sems, recv_sems, local_sems = refs[2 * count :]
    bits = [own_bit(place) for place in places]

    def view(stream, have):
        array, cols, order = stream
        index = tuple(slice(None) if p in have else bits[p] for p in range(len(places)))
        return wholes[array].at[index + (slice(None), cols)]

    meet(places)
    locals_ = []
    for number, stream in enumerate(streams):
        array, cols, order = stream
        copy = pltpu.make_async_copy(shards[array].at[:, cols], view(stream, ()), local_sems.at[number])
        copy.start()
        locals_.append(copy)

    def send(number, stage):
        stream = streams[number]
        array, cols, order = stream
        source = shards[array].at[:, cols] if stage == 0 else view(stream, order[:stage])
        copy = pltpu.make_async_remote_copy(
            src_ref=source,
            dst_ref=view(stream, order[:stage]),
            send_sem=send_sems.at[number, stage],
            recv_sem=recv_sems.at[number, stage],
            device_id=partner(places[order[stage]]),
            device_id_type=MESH,
        )
        copy.start()
        return copy

    stages = len(places)
    flights = [[send(number, 0)] for number in range(len(streams))]
    for copy in locals_:
        copy.wait()
    for stage in range(stages):
        for number in range(len(streams)):
            flights[number][stage].wait_recv()
            if stage + 1 < stages:
                flights[number].append(send(number, stage + 1))
    for flight in flights:
        for copy in flight:
            copy.wait_send()


def orders_of(places):
    core = places.index(("ctx", 0))
    rows = [k for k, place in enumerate(places) if place[0] == "ctx" and place[1] > 0]
    near = places.index(("exp", 0))
    far = [k for k, place in sorted(enumerate(places), key=lambda item: item[1][1]) if place[0] == "exp" and place[1] > 0]
    return [core] + rows + [near] + far, [core, near] + rows + far


def gather_all(sizes, shards, identity):
    places = bit_positions(sizes)
    first, second = [tuple(reversed(order)) for order in orders_of(places)]
    streams = []
    for array, shard in enumerate(shards):
        width = shard.shape[1]
        if width % 256 == 0:
            streams.append((array, slice(0, width // 2), first))
            streams.append((array, slice(width // 2, width), second))
        else:
            streams.append((array, slice(0, width), first if array % 2 else second))
    stages = len(places)
    anywhere = pl.BlockSpec(memory_space=pl.ANY)
    wholes = pl.pallas_call(
        functools.partial(gather_kernel, places, streams, len(shards)),
        in_specs=[anywhere] * len(shards),
        out_specs=[anywhere] * len(shards),
        out_shape=[jax.ShapeDtypeStruct((2,) * stages + shard.shape, shard.dtype) for shard in shards],
        scratch_shapes=[
            pltpu.SemaphoreType.DMA((len(streams), stages)),
            pltpu.SemaphoreType.DMA((len(streams), stages)),
            pltpu.SemaphoreType.DMA((len(streams),)),
        ],
        compiler_params=pltpu.CompilerParams(collective_id=identity, has_side_effects=True),
        name="gather_all",
    )(*shards)
    return [whole.reshape((-1,) + whole.shape[stages + 1 :]) for whole in wholes]


def reduce_kernel(places, streams, count, *refs):
    parts, totals = refs[:count], refs[count : 2 * count]
    stages = len(places)
    landing = refs[2 * count : 2 * count + len(streams) * stages]
    send_sems, recv_sems = refs[2 * count + len(streams) * stages :]
    bits = [own_bit(place) for place in places]

    def spot(number, stage):
        return landing[number * stages + stage]

    def side(number, stage, value):
        array, cols, order = streams[number]
        left = [p for p in range(stages) if p not in order[:stage]]
        index = tuple(value if p == order[stage] else slice(None) for p in left)
        if stage == 0:
            return parts[array].at[index + (slice(None), cols)]
        return spot(number, stage - 1).at[index]

    meet(places)

    def send(number, stage):
        order = streams[number][2]
        copy = pltpu.make_async_remote_copy(
            src_ref=side(number, stage, 1 - bits[order[stage]]),
            dst_ref=spot(number, stage),
            send_sem=send_sems.at[number, stage],
            recv_sem=recv_sems.at[number, stage],
            device_id=partner(places[order[stage]]),
            device_id_type=MESH,
        )
        copy.start()
        return copy

    flights = [[send(number, 0)] for number in range(len(streams))]
    for stage in range(stages):
        for number, (array, cols, order) in enumerate(streams):
            flights[number][stage].wait_recv()
            mine = side(number, stage, bits[order[stage]])
            there = spot(number, stage)
            if stage + 1 < stages:
                depth = stages - stage - 1

                def add(index, unused):
                    at = tuple(lax.rem(index // 2 ** (depth - 1 - k), 2) for k in range(depth))
                    there[at] = (there[at].astype(jnp.float32) + mine[at].astype(jnp.float32)).astype(there.dtype)
                    return unused

                lax.fori_loop(0, 2**depth, add, 0)
                flights[number].append(send(number, stage + 1))
            else:
                totals[array][:, cols] = there[...].astype(jnp.float32) + mine[...].astype(jnp.float32)
    for flight in flights:
        for copy in flight:
            copy.wait_send()


def reduce_all(sizes, parts, identity):
    places = bit_positions(sizes)
    first, second = [tuple(order) for order in orders_of(places)]
    stages = len(places)
    streams = []
    blocks = []
    for array, part in enumerate(parts):
        width = part.shape[1]
        blocks.append(part.reshape((2,) * stages + (-1, width)))
        if width % 256 == 0:
            streams.append((array, slice(0, width // 2), first))
            streams.append((array, slice(width // 2, width), second))
        else:
            streams.append((array, slice(0, width), first if array % 2 else second))
    inside = pl.BlockSpec(memory_space=pltpu.VMEM)
    landing = []
    for array, cols, order in streams:
        for stage in range(stages):
            rows = blocks[array].shape[-2]
            landing.append(pltpu.VMEM((2,) * (stages - stage - 1) + (rows, cols.stop - cols.start), jnp.bfloat16))
    return pl.pallas_call(
        functools.partial(reduce_kernel, places, streams, len(parts)),
        in_specs=[inside] * len(parts),
        out_specs=[inside] * len(parts),
        out_shape=[jax.ShapeDtypeStruct(block.shape[-2:], jnp.float32) for block in blocks],
        scratch_shapes=landing
        + [
            pltpu.SemaphoreType.DMA((len(streams), stages)),
            pltpu.SemaphoreType.DMA((len(streams), stages)),
        ],
        compiler_params=pltpu.CompilerParams(
            collective_id=identity, has_side_effects=True, vmem_limit_bytes=48 * 1024 * 1024
        ),
        name="reduce_all",
    )(*blocks)


def dot(left, right):
    return jnp.dot(left, right, preferred_element_type=jnp.float32)


def flipped(value, level):
    count = lax.axis_size("ctx")
    return lax.ppermute(value, "ctx", [(source, source ^ (1 << level)) for source in range(count)])


def spread_slices(own):
    levels = lax.axis_size("ctx").bit_length() - 1
    slices = {0: own}
    for level in reversed(range(levels)):
        for offset in sorted(slices):
            slices[offset + (1 << level)] = flipped(slices[offset], level)
    return [slices[offset] for offset in sorted(slices)]


def collect_slices(sums):
    levels = lax.axis_size("ctx").bit_length() - 1
    for level in range(levels):
        step = 1 << level
        kept = {}
        for offset in range(0, len(sums), 2 * step):
            arrived = flipped(sums[offset + step].astype(jnp.bfloat16), level)
            kept[offset] = sums[offset] + arrived.astype(jnp.float32)
        sums = [kept.get(offset) for offset in range(len(sums))]
    return sums[0]


def body(
    inputs,
    segments,
    routes,
    cotangent,
    norm_gain,
    in_proj,
    conv_taps,
    conv_bias,
    x_proj,
    dt_proj,
    dt_bias,
    log_decay,
    skip_gain,
    out_proj,
    moe_gain,
    router,
    expert_in,
    expert_out,
):
    experts = router.shape[1]
    half_rows = norm_gain.shape[0]
    columns = (
        x_proj,
        dt_proj.T,
        conv_taps,
        conv_bias[:, None],
        dt_bias[:, None],
        log_decay,
        skip_gain[:, None],
        jnp.concatenate([norm_gain, moe_gain])[:, None],
        router.reshape(2 * half_rows, experts // 2),
    )
    widths = [part.shape[1] for part in columns]
    ends = [sum(widths[: k + 1]) for k in range(len(widths))]
    sizes = [(name, lax.axis_size(name)) for name in ("ctx", "exp")]
    full_in, full_out, full_small = gather_all(
        sizes, (in_proj, out_proj, jnp.concatenate(columns, axis=1)), 0
    )
    full_xproj, full_dt, full_taps, full_bias, full_dtbias, full_decay, full_skip, gains, full_router = [
        full_small[:, end - width : end] for end, width in zip(ends, widths)
    ]
    full_dt = full_dt.T
    full_bias, full_dtbias, full_skip = full_bias[:, 0], full_dtbias[:, 0], full_skip[:, 0]
    gains = gains.reshape(-1, 2, half_rows)
    full_norm, full_moe = gains[:, 0].reshape(-1), gains[:, 1].reshape(-1)
    full_router = full_router.reshape(-1, experts)
    tokens_here = inputs.shape[1]
    capacity = 5 * tokens_here // (4 * experts)
    flat_in = inputs[0].astype(jnp.float32)
    seg_row = segments[0]
    position = lax.axis_index("ctx")
    norm_one_value, norm_one_pull = jax.vjp(rms_scale, flat_in, full_norm.astype(jnp.float32))
    normed_one = norm_one_value.astype(jnp.bfloat16)
    mixed_in = jnp.dot(normed_one, full_in, preferred_element_type=jnp.float32)
    conv_in = mixed_in[:, :DI].astype(jnp.bfloat16)
    gate_z = mixed_in[:, DI:]
    edge_rows, edge_ids = shifted(
        (conv_in[tokens_here - (KC - 1) :], seg_row[tokens_here - (KC - 1) :].astype(jnp.bfloat16)),
        "ctx",
        1,
    )
    prior_ids = jnp.where(position > 0, edge_ids.astype(jnp.int32), -1)
    ext_ids = jnp.concatenate([prior_ids, seg_row])
    ext_rows = jnp.concatenate([edge_rows, conv_in], axis=0).astype(jnp.float32)
    conv_out, conv_pull = jax.vjp(
        lambda rows_in, taps_in, bias_in: conv_local(rows_in, taps_in, bias_in, ext_ids),
        ext_rows,
        full_taps.astype(jnp.float32),
        full_bias.astype(jnp.float32),
    )
    silu_value, silu_pull = jax.vjp(jax.nn.silu, conv_out)
    xs_val = silu_value.astype(jnp.bfloat16)
    xs_wide = xs_val.astype(jnp.float32)
    projected = jnp.dot(xs_val, full_xproj, preferred_element_type=jnp.float32)
    delta_low = projected[:, :R].astype(jnp.bfloat16)
    b_rows = projected[:, R : R + NS]
    c_rows = projected[:, R + NS :]
    dt_pre = jnp.dot(delta_low, full_dt, preferred_element_type=jnp.float32) + full_dtbias.astype(
        jnp.float32
    )
    step_size = jax.nn.softplus(dt_pre)
    a_swap = -jnp.exp(full_decay.astype(jnp.float32)).T
    earlier = jnp.concatenate([prior_ids[KC - 2 :], seg_row[:-1]])
    keep_mask = (earlier == seg_row).astype(jnp.float32)
    masked_step = jnp.where(keep_mask[:, None] > 0, step_size, 1e30)
    push = step_size * xs_wide
    b_wide = jnp.broadcast_to(b_rows[:, :, None], (tokens_here, NS, LANES))
    c_wide = jnp.broadcast_to(c_rows[:, :, None], (tokens_here, NS, LANES))
    rates = a_swap * LOG2E
    block_end = scan_end(masked_step, push, b_wide, rates)
    block_product = jnp.exp2(jnp.sum(masked_step, axis=0)[None, :] * rates)
    gathered = lax.all_gather(
        jnp.stack([block_product, block_end]).astype(jnp.bfloat16)[None], "ctx", axis=0, tiled=True
    ).astype(jnp.float32)
    all_products, all_ends = gathered[:, 0], gathered[:, 1]
    zeros_state = jnp.zeros((NS, DI), jnp.float32)

    def fold_start(index_now, start_now):
        return jnp.where(
            index_now < position,
            all_products[index_now] * start_now + all_ends[index_now],
            start_now,
        )

    start_state = zeros_state
    for index_now in range(all_products.shape[0]):
        start_state = fold_start(index_now, start_state)
    scan_rows, kept, firsts = scan_out(masked_step, push, b_wide, c_wide, rates, start_state)
    skip_wide = full_skip.astype(jnp.float32)
    scanned_y = scan_rows + skip_wide * xs_wide
    gated_wide, gated_pull = jax.vjp(
        lambda scan_in, gate_in: scan_in * jax.nn.silu(gate_in), scanned_y, gate_z
    )
    gated = gated_wide.astype(jnp.bfloat16)
    mixed = jnp.dot(gated, full_out, preferred_element_type=jnp.float32)
    residual = flat_in + mixed
    norm_two_value, norm_two_pull = jax.vjp(rms_scale, residual, full_moe.astype(jnp.float32))
    normed_two = norm_two_value.astype(jnp.bfloat16)
    logits = jnp.dot(normed_two, full_router, preferred_element_type=jnp.float32)
    probability = jax.nn.softmax(logits, axis=-1)
    route_ids = routes[0, :, 0]
    one_hot = route_ids[:, None] == jnp.arange(experts, dtype=jnp.int32)[None, :]
    one_float = one_hot.astype(jnp.float32)
    gate_val = jnp.sum(probability * one_float, axis=1)
    running = jnp.cumsum(one_hot.astype(jnp.int32), axis=0)
    slot_index = jnp.sum(running * one_hot.astype(jnp.int32), axis=1) - 1
    target = route_ids * capacity + slot_index
    buffer = (
        jnp.zeros((experts * capacity, D), jnp.bfloat16)
        .at[target]
        .set(normed_two)
        .reshape(experts, capacity, D)
    )
    weights_in = spread_slices(expert_in[0])
    weights_out = spread_slices(expert_out[0])
    rows_in = lax.all_to_all(buffer, "exp", split_axis=0, concat_axis=0, tiled=True)
    rows_in = rows_in.reshape(experts * capacity, D)
    hidden_pre = [dot(rows_in, weight) for weight in weights_in]
    active = [jax.nn.gelu(values, approximate=False).astype(jnp.bfloat16) for values in hidden_pre]
    result = sum(dot(values, weight) for values, weight in zip(active, weights_out)).astype(jnp.bfloat16)
    expert_result = result.reshape(experts, capacity, D)
    returned = lax.all_to_all(expert_result, "exp", split_axis=0, concat_axis=0, tiled=True)
    picked = returned.reshape(-1, D)[target].astype(jnp.float32)
    outcome = residual + gate_val[:, None] * picked
    out_block = outcome.astype(jnp.bfloat16)[None]
    grad_out = cotangent[0].astype(jnp.float32)
    grad_gate = jnp.sum(grad_out * picked, axis=1)
    grad_pick = (grad_out * gate_val[:, None]).astype(jnp.bfloat16)
    grad_buffer = (
        jnp.zeros((experts * capacity, D), jnp.bfloat16)
        .at[target]
        .set(grad_pick)
        .reshape(experts, capacity, D)
    )
    grad_result = lax.all_to_all(grad_buffer, "exp", split_axis=0, concat_axis=0, tiled=True)
    grad_result = grad_result.reshape(experts * capacity, D)
    grad_expert_out = [dot(values.T, grad_result) for values in active]
    grad_hidden = []
    for values, weight in zip(hidden_pre, weights_out):
        gelu_value, gelu_pull = jax.vjp(lambda inner: jax.nn.gelu(inner, approximate=False), values)
        grad_hidden.append(gelu_pull(dot(grad_result, weight.T))[0].astype(jnp.bfloat16))
    grad_expert_in = [dot(rows_in.T, values) for values in grad_hidden]
    grad_rows = sum(dot(values, weight.T) for values, weight in zip(grad_hidden, weights_in))
    grad_rows = grad_rows.astype(jnp.bfloat16).reshape(experts, capacity, D)
    grad_sent = lax.all_to_all(grad_rows, "exp", split_axis=0, concat_axis=0, tiled=True)
    grad_from_experts = grad_sent.reshape(-1, D)[target].astype(jnp.float32)
    grad_w_in = collect_slices(grad_expert_in)[None]
    grad_w_out = collect_slices(grad_expert_out)[None]
    grad_probs = grad_gate[:, None] * one_float
    grad_logits = (
        probability * (grad_probs - jnp.sum(grad_probs * probability, axis=1, keepdims=True))
    ).astype(jnp.bfloat16)
    grad_router = jnp.dot(normed_two.T, grad_logits, preferred_element_type=jnp.float32)
    grad_normed_two = grad_from_experts + jnp.dot(
        grad_logits, full_router.T, preferred_element_type=jnp.float32
    )
    grad_resid_norm, grad_moe_gain = norm_two_pull(grad_normed_two)
    grad_resid = grad_out + grad_resid_norm
    grad_mixed = grad_resid.astype(jnp.bfloat16)
    grad_gated = jnp.dot(grad_mixed, full_out.T, preferred_element_type=jnp.float32)
    grad_out_proj = jnp.dot(gated.T, grad_mixed, preferred_element_type=jnp.float32)
    grad_y, grad_z = gated_pull(grad_gated)
    grad_skip = jnp.sum(grad_y * xs_wide, axis=0)
    local_inflow = scan_inflow(masked_step, grad_y, c_wide, rates)
    all_inflows = lax.all_gather(
        local_inflow[None].astype(jnp.bfloat16), "ctx", axis=0, tiled=True
    ).astype(jnp.float32)
    total_ctx = all_inflows.shape[0]

    def fold_end(step_index, end_now):
        source = total_ctx - 1 - step_index
        return jnp.where(
            source > position, all_inflows[source] + all_products[source] * end_now, end_now
        )

    end_inflow = zeros_state
    for step_index in range(total_ctx):
        end_inflow = fold_end(step_index, end_inflow)
    along_b, slope, wide_b, wide_c, grad_a = scan_adjoint(
        masked_step, push, grad_y, b_wide, c_wide, kept, firsts, rates, end_inflow
    )
    grad_step_all = along_b * xs_wide + slope * (1.0 / LOG2E)
    grad_xss = along_b * step_size
    grad_bs = jnp.sum(wide_b, axis=2)
    grad_cs = jnp.sum(wide_c, axis=2)
    grad_log_decay = (grad_a * a_swap).T
    soft_slope = jax.nn.sigmoid(dt_pre)
    grad_pre_wide = grad_step_all * soft_slope
    grad_dt_bias = jnp.sum(grad_pre_wide, axis=0)
    grad_dt_pre = grad_pre_wide.astype(jnp.bfloat16)
    grad_dt_proj = jnp.dot(delta_low.T, grad_dt_pre, preferred_element_type=jnp.float32)
    grad_delta = jnp.dot(grad_dt_pre, full_dt.T, preferred_element_type=jnp.float32)
    grad_projected = jnp.concatenate(
        [grad_delta, grad_bs, grad_cs], axis=1
    ).astype(jnp.bfloat16)
    grad_x_proj = jnp.dot(xs_val.T, grad_projected, preferred_element_type=jnp.float32)
    grad_xs_total = (
        skip_wide * grad_y
        + grad_xss
        + jnp.dot(grad_projected, full_xproj.T, preferred_element_type=jnp.float32)
    )
    grad_conv = silu_pull(grad_xs_total)[0]
    grad_ext, grad_taps, grad_cbias = conv_pull(grad_conv)
    from_next = shifted(grad_ext[: KC - 1], "ctx", -1)
    grad_conv_in = grad_ext[KC - 1 :] + jnp.concatenate(
        [jnp.zeros((tokens_here - (KC - 1), DI), jnp.float32), from_next], axis=0
    )
    grad_mixed_in = jnp.concatenate([grad_conv_in, grad_z], axis=1).astype(jnp.bfloat16)
    grad_in_proj = jnp.dot(normed_one.T, grad_mixed_in, preferred_element_type=jnp.float32)
    grad_normed_one = jnp.dot(grad_mixed_in, full_in.T, preferred_element_type=jnp.float32)
    grad_inputs_norm, grad_norm_gain = norm_one_pull(grad_normed_one)
    grad_inputs = grad_resid + grad_inputs_norm
    sums = (
        grad_x_proj,
        grad_dt_proj.T,
        grad_taps,
        grad_cbias[:, None],
        grad_dt_bias[:, None],
        grad_log_decay,
        grad_skip[:, None],
        jnp.stack(
            [grad_norm_gain.reshape(-1, half_rows), grad_moe_gain.reshape(-1, half_rows)], axis=1
        ).reshape(-1, 1),
        grad_router.reshape(-1, experts // 2),
    )

    own_in, own_out, own_small = reduce_all(
        sizes,
        (
            grad_in_proj.astype(jnp.bfloat16),
            grad_out_proj.astype(jnp.bfloat16),
            jnp.concatenate(sums, axis=1).astype(jnp.bfloat16),
        ),
        1,
    )
    own_x, own_dt, own_taps, own_bias, own_dtbias, own_decay, own_skip, own_gains, own_router = [
        own_small[:, end - width : end] for end, width in zip(ends, widths)
    ]
    return (
        out_block,
        grad_inputs[None],
        own_gains[:half_rows, 0],
        own_in,
        own_taps,
        own_bias[:, 0],
        own_x,
        own_dt.T,
        own_dtbias[:, 0],
        own_decay,
        own_skip[:, 0],
        own_out,
        own_gains[half_rows:, 0],
        own_router.reshape(half_rows, experts),
        grad_w_in,
        grad_w_out,
    )


def solution(mesh):
    placed = (
        P("exp", "ctx", None),
        P("exp", "ctx"),
        P("exp", "ctx", None),
        P("exp", "ctx", None),
        P(("ctx", "exp")),
        P(("ctx", "exp"), None),
        P(("ctx", "exp"), None),
        P(("ctx", "exp")),
        P(("ctx", "exp"), None),
        P(None, ("ctx", "exp")),
        P(("ctx", "exp")),
        P(("ctx", "exp"), None),
        P(("ctx", "exp")),
        P(("ctx", "exp"), None),
        P(("ctx", "exp")),
        P(("ctx", "exp"), None),
        P("exp", None, "ctx"),
        P("exp", "ctx", None),
    )
    return jax.shard_map(
        body,
        mesh=mesh,
        in_specs=placed,
        out_specs=(
            P("exp", "ctx", None),
            P("exp", "ctx", None),
            P(("ctx", "exp")),
            P(("ctx", "exp"), None),
            P(("ctx", "exp"), None),
            P(("ctx", "exp")),
            P(("ctx", "exp"), None),
            P(None, ("ctx", "exp")),
            P(("ctx", "exp")),
            P(("ctx", "exp"), None),
            P(("ctx", "exp")),
            P(("ctx", "exp"), None),
            P(("ctx", "exp")),
            P(("ctx", "exp"), None),
            P("exp", None, "ctx"),
            P("exp", "ctx", None),
        ),
        check_vma=False,
    )
```

```python
import functools

import jax
import jax.numpy as jnp
from jax import lax
from jax.experimental import pallas as pl
from jax.experimental.pallas import tpu as pltpu
from jax.sharding import PartitionSpec as P

D = 768
DI = 1536
NS = 16
R = 48
KC = 4
LANES = 128
UNROLL = 8
LOG2E = 1.4426950408889634


EPS = 1e-05
MESH = pl.DeviceIdType.MESH
ROWS_AT_ONCE = 16

def tile(ref, base, lanes):
    return ref[pl.ds(pl.multiple_of(base, UNROLL), UNROLL), lanes]

def row(rows_now, place):
    return jnp.broadcast_to(rows_now[place : place + 1], (NS, LANES))

def put_row(rows_now, place, value):
    at = lax.broadcasted_iota(jnp.int32, (UNROLL, LANES), 0)
    value = jnp.broadcast_to(value, (UNROLL, LANES))
    return value if rows_now is None else jnp.where(at == place, value, rows_now)

def end_kernel(width, step_ref, push_ref, b_ref, rate_ref, end_ref):
    rows, channels = step_ref.shape

    @pl.when(pl.program_id(0) == 0)
    def _():
        end_ref[...] = jnp.zeros_like(end_ref)

    for group in range(0, channels, width):
        pieces = [slice(at, at + LANES) for at in range(group, group + width, LANES)]
        rates = [rate_ref[:, lanes] for lanes in pieces]

        def block(index, states):
            states = list(states)
            steps = [tile(step_ref, index * UNROLL, lanes) for lanes in pieces]
            pushes = [tile(push_ref, index * UNROLL, lanes) for lanes in pieces]
            for place in range(UNROLL):
                t = index * UNROLL + place
                b_now = b_ref[t]
                for k, lanes in enumerate(pieces):
                    decay = jnp.exp2(row(steps[k], place) * rates[k])
                    states[k] = decay * states[k] + b_now * row(pushes[k], place)
            return tuple(states)

        states = lax.fori_loop(0, rows // UNROLL, block, tuple(end_ref[:, lanes] for lanes in pieces))
        for k, lanes in enumerate(pieces):
            end_ref[:, lanes] = states[k]

def out_kernel(width, step_ref, push_ref, b_ref, c_ref, rate_ref, start_ref, y_ref, kept_ref, first_ref, state_ref):
    rows, channels = step_ref.shape

    @pl.when(pl.program_id(0) == 0)
    def _():
        state_ref[...] = start_ref[...]

    first_ref[0] = state_ref[...].astype(first_ref.dtype)
    for group in range(0, channels, width):
        pieces = [slice(at, at + LANES) for at in range(group, group + width, LANES)]
        rates = [rate_ref[:, lanes] for lanes in pieces]

        def block(index, states):
            states = list(states)
            steps = [tile(step_ref, index * UNROLL, lanes) for lanes in pieces]
            pushes = [tile(push_ref, index * UNROLL, lanes) for lanes in pieces]
            outs = [None] * len(pieces)
            for place in range(UNROLL):
                t = index * UNROLL + place
                b_now = b_ref[t]
                c_now = c_ref[t]
                for k, lanes in enumerate(pieces):
                    decay = jnp.exp2(row(steps[k], place) * rates[k])
                    states[k] = decay * states[k] + b_now * row(pushes[k], place)
                    kept_ref[t, :, lanes] = states[k].astype(kept_ref.dtype)
                    outs[k] = put_row(outs[k], place, jnp.sum(states[k] * c_now, axis=0, keepdims=True))
            for k, lanes in enumerate(pieces):
                y_ref[pl.ds(pl.multiple_of(index * UNROLL, UNROLL), UNROLL), lanes] = outs[k]
            return tuple(states)

        states = lax.fori_loop(0, rows // UNROLL, block, tuple(state_ref[:, lanes] for lanes in pieces))
        for k, lanes in enumerate(pieces):
            state_ref[:, lanes] = states[k]

def inflow_kernel(width, step_ref, grad_ref, c_ref, rate_ref, end_ref):
    rows, channels = step_ref.shape

    @pl.when(pl.program_id(0) == 0)
    def _():
        end_ref[...] = jnp.zeros_like(end_ref)

    for group in range(0, channels, width):
        pieces = [slice(at, at + LANES) for at in range(group, group + width, LANES)]
        rates = [rate_ref[:, lanes] for lanes in pieces]

        def block(index, flows):
            flows = list(flows)
            base = rows - UNROLL - index * UNROLL
            steps = [tile(step_ref, base, lanes) for lanes in pieces]
            grads = [tile(grad_ref, base, lanes) for lanes in pieces]
            for place in reversed(range(UNROLL)):
                c_now = c_ref[base + place]
                for k, lanes in enumerate(pieces):
                    decay = jnp.exp2(row(steps[k], place) * rates[k])
                    flows[k] = decay * (c_now * row(grads[k], place) + flows[k])
            return tuple(flows)

        flows = lax.fori_loop(0, rows // UNROLL, block, tuple(end_ref[:, lanes] for lanes in pieces))
        for k, lanes in enumerate(pieces):
            end_ref[:, lanes] = flows[k]

def adjoint_kernel(width, step_ref, push_ref, grad_ref, b_ref, c_ref, kept_ref, first_ref, rate_ref, end_ref,
                   along_ref, slope_ref, gb_ref, gc_ref, ga_ref, flow_ref):
    rows, channels = step_ref.shape

    @pl.when(pl.program_id(0) == 0)
    def _():
        flow_ref[...] = end_ref[...]
        ga_ref[...] = jnp.zeros_like(ga_ref)

    for group in range(0, channels, width):
        pieces = [slice(at, at + LANES) for at in range(group, group + width, LANES)]
        rates = [rate_ref[:, lanes] for lanes in pieces]
        count = len(pieces)

        def block(index, carried, last):
            flows, sums, current = list(carried[:count]), list(carried[count:2*count]), list(carried[2*count:])
            base = rows - UNROLL - index * UNROLL
            steps = [tile(step_ref, base, lanes) for lanes in pieces]
            pushes = [tile(push_ref, base, lanes) for lanes in pieces]
            grads = [tile(grad_ref, base, lanes) for lanes in pieces]
            alongs = [None] * count
            slopes = [None] * count
            for place in reversed(range(UNROLL)):
                t = base + place
                b_now = b_ref[t]
                c_now = c_ref[t]
                gb = gc = None
                for k, lanes in enumerate(pieces):
                    if last and place == 0:
                        prior = first_ref[0, :, lanes].astype(jnp.float32)
                    else:
                        prior = kept_ref[t - 1, :, lanes].astype(jnp.float32)
                    step = row(steps[k], place)
                    grad = row(grads[k], place)
                    decay = jnp.exp2(step * rates[k])
                    adjoint = c_now * grad + flows[k]
                    flows[k] = decay * adjoint
                    decay_grad = flows[k] * prior
                    alongs[k] = put_row(alongs[k], place, jnp.sum(adjoint * b_now, axis=0, keepdims=True))
                    slopes[k] = put_row(slopes[k], place, jnp.sum(decay_grad * rates[k], axis=0, keepdims=True))
                    sums[k] = sums[k] + decay_grad * step
                    part_b = adjoint * row(pushes[k], place)
                    part_c = current[k] * grad
                    gb = part_b if gb is None else gb + part_b
                    gc = part_c if gc is None else gc + part_c
                    current[k] = prior
                if group == 0:
                    gb_ref[t] = gb
                    gc_ref[t] = gc
                else:
                    gb_ref[t] += gb
                    gc_ref[t] += gc
            where = pl.ds(pl.multiple_of(base, UNROLL), UNROLL)
            for k, lanes in enumerate(pieces):
                along_ref[where, lanes] = alongs[k]
                slope_ref[where, lanes] = slopes[k]
            return tuple(flows + sums + current)

        carried = (tuple(flow_ref[:, lanes] for lanes in pieces) + tuple(ga_ref[:, lanes] for lanes in pieces)
                   + tuple(kept_ref[rows - 1, :, lanes].astype(jnp.float32) for lanes in pieces))
        steps = rows // UNROLL
        carried = lax.fori_loop(0, steps - 1, functools.partial(block, last=False), carried)
        carried = block(steps - 1, carried, True)
        for k, lanes in enumerate(pieces):
            flow_ref[:, lanes] = carried[k]
            ga_ref[:, lanes] = carried[count + k]

def over_time(rows, width):
    return pl.BlockSpec((rows, width), lambda i: (i, 0))

PARAMS = pltpu.CompilerParams(vmem_limit_bytes=48 * 1024 * 1024, dimension_semantics=("arbitrary",))

def pick(channels):
    return 512 if channels % 512 == 0 else 128

def scan_end(step, push, b_wide, rates, rows=64):
    tokens, channels = step.shape
    return pl.pallas_call(
        functools.partial(end_kernel, pick(channels)),
        grid=(tokens // rows,),
        in_specs=[pl.BlockSpec((rows, channels), lambda i: (i, 0))] * 2
        + [pl.BlockSpec((rows, NS, LANES), lambda i: (i, 0, 0)), pl.BlockSpec((NS, channels), lambda i: (0, 0))],
        out_specs=pl.BlockSpec((NS, channels), lambda i: (0, 0)),
        out_shape=jax.ShapeDtypeStruct((NS, channels), jnp.float32),
        compiler_params=PARAMS,
    )(step, push, b_wide, rates)

def scan_out(step, push, b_wide, c_wide, rates, start, rows=64):
    tokens, channels = step.shape
    wide = pl.BlockSpec((rows, channels), lambda i: (i, 0))
    cast = pl.BlockSpec((rows, NS, LANES), lambda i: (i, 0, 0))
    fixed = pl.BlockSpec((NS, channels), lambda i: (0, 0))
    return pl.pallas_call(
        functools.partial(out_kernel, pick(channels)),
        grid=(tokens // rows,),
        in_specs=[wide, wide, cast, cast, fixed, fixed],
        out_specs=[wide, pl.BlockSpec((rows, NS, channels), lambda i: (i, 0, 0)), pl.BlockSpec((1, NS, channels), lambda i: (i, 0, 0))],
        out_shape=[jax.ShapeDtypeStruct((tokens, channels), jnp.float32),
                   jax.ShapeDtypeStruct((tokens, NS, channels), jnp.bfloat16),
                   jax.ShapeDtypeStruct((tokens // rows, NS, channels), jnp.bfloat16)],
        scratch_shapes=[pltpu.VMEM((NS, channels), jnp.float32)],
        compiler_params=PARAMS,
    )(step, push, b_wide, c_wide, rates, start)

def scan_inflow(step, grad, c_wide, rates, rows=64):
    tokens, channels = step.shape
    last = tokens // rows - 1
    return pl.pallas_call(
        functools.partial(inflow_kernel, pick(channels)),
        grid=(tokens // rows,),
        in_specs=[pl.BlockSpec((rows, channels), lambda i: (last - i, 0))] * 2
        + [pl.BlockSpec((rows, NS, LANES), lambda i: (last - i, 0, 0)), pl.BlockSpec((NS, channels), lambda i: (0, 0))],
        out_specs=pl.BlockSpec((NS, channels), lambda i: (0, 0)),
        out_shape=jax.ShapeDtypeStruct((NS, channels), jnp.float32),
        compiler_params=PARAMS,
    )(step, grad, c_wide, rates)

def scan_adjoint(step, push, grad, b_wide, c_wide, kept, firsts, rates, end, rows=64):
    tokens, channels = step.shape
    last = tokens // rows - 1
    wide = pl.BlockSpec((rows, channels), lambda i: (last - i, 0))
    cast = pl.BlockSpec((rows, NS, LANES), lambda i: (last - i, 0, 0))
    fixed = pl.BlockSpec((NS, channels), lambda i: (0, 0))
    return pl.pallas_call(
        functools.partial(adjoint_kernel, pick(channels)),
        grid=(tokens // rows,),
        in_specs=[wide, wide, wide, cast, cast, pl.BlockSpec((rows, NS, channels), lambda i: (last - i, 0, 0)),
                  pl.BlockSpec((1, NS, channels), lambda i: (last - i, 0, 0)), fixed, fixed],
        out_specs=[wide, wide, cast, cast, fixed],
        out_shape=[jax.ShapeDtypeStruct((tokens, channels), jnp.float32)] * 2
        + [jax.ShapeDtypeStruct((tokens, NS, LANES), jnp.float32)] * 2
        + [jax.ShapeDtypeStruct((NS, channels), jnp.float32)],
        scratch_shapes=[pltpu.VMEM((NS, channels), jnp.float32)],
        compiler_params=PARAMS,
    )(step, push, grad, b_wide, c_wide, kept, firsts, rates, end)


def shifted(value, axis, steps):
    count = lax.axis_size(axis)
    initial, last = (max(0, -steps), min(count, count - steps))
    return lax.ppermute(value, axis, [(source, source + steps) for source in range(initial, last)])


def rms_scale(values, gain):
    return values * lax.rsqrt(jnp.mean(values * values, axis=-1, keepdims=True) + EPS) * gain


def conv_local(ext_rows, taps, bias, ext_ids):
    length = ext_rows.shape[0] - (KC - 1)
    own_ids = ext_ids[KC - 1 :]
    result = jnp.zeros((length, ext_rows.shape[1]), jnp.float32) + bias[None, :]
    for offset in range(KC):
        same_doc = (ext_ids[offset : offset + length] == own_ids).astype(jnp.float32)
        result = (
            result
            + taps[:, offset][None, :] * ext_rows[offset : offset + length] * same_doc[:, None]
        )
    return result


def bit_positions(sizes):
    return [(axis, size.bit_length() - 2 - k) for axis, size in sizes for k in range(size.bit_length() - 1)]


def own_bit(place):
    axis, level = place
    return lax.rem(lax.axis_index(axis) // 2**level, 2)


def partner(place):
    axis, level = place
    where = {"ctx": lax.axis_index("ctx"), "exp": lax.axis_index("exp")}
    where[axis] = where[axis] + (1 - 2 * own_bit(place)) * 2**level
    return (where["ctx"], where["exp"])


def meet(places):
    barrier = pltpu.get_barrier_semaphore()
    for place in places:
        pl.semaphore_signal(barrier, inc=1, device_id=partner(place), device_id_type=MESH)
    pl.semaphore_wait(barrier, len(places))


def gather_kernel(places, streams, count, *refs):
    shards, wholes = refs[:count], refs[count : 2 * count]
    send_sems, recv_sems, local_sems = refs[2 * count :]
    bits = [own_bit(place) for place in places]

    def view(stream, have):
        array, cols, order = stream
        index = tuple(slice(None) if p in have else bits[p] for p in range(len(places)))
        return wholes[array].at[index + (slice(None), cols)]

    meet(places)
    locals_ = []
    for number, stream in enumerate(streams):
        array, cols, order = stream
        copy = pltpu.make_async_copy(shards[array].at[:, cols], view(stream, ()), local_sems.at[number])
        copy.start()
        locals_.append(copy)

    def send(number, stage):
        stream = streams[number]
        array, cols, order = stream
        source = shards[array].at[:, cols] if stage == 0 else view(stream, order[:stage])
        copy = pltpu.make_async_remote_copy(
            src_ref=source,
            dst_ref=view(stream, order[:stage]),
            send_sem=send_sems.at[number, stage],
            recv_sem=recv_sems.at[number, stage],
            device_id=partner(places[order[stage]]),
            device_id_type=MESH,
        )
        copy.start()
        return copy

    stages = len(places)
    flights = [[send(number, 0)] for number in range(len(streams))]
    for copy in locals_:
        copy.wait()
    for stage in range(stages):
        for number in range(len(streams)):
            flights[number][stage].wait_recv()
            if stage + 1 < stages:
                flights[number].append(send(number, stage + 1))
    for flight in flights:
        for copy in flight:
            copy.wait_send()


def orders_of(places):
    core = places.index(("ctx", 0))
    rows = [k for k, place in enumerate(places) if place[0] == "ctx" and place[1] > 0]
    near = places.index(("exp", 0))
    far = [k for k, place in sorted(enumerate(places), key=lambda item: item[1][1]) if place[0] == "exp" and place[1] > 0]
    return [core] + rows + [near] + far, [core, near] + rows + far


def gather_all(sizes, shards, identity):
    places = bit_positions(sizes)
    first, second = [tuple(reversed(order)) for order in orders_of(places)]
    streams = []
    for array, shard in enumerate(shards):
        width = shard.shape[1]
        if width % 256 == 0:
            streams.append((array, slice(0, width // 2), first))
            streams.append((array, slice(width // 2, width), second))
        else:
            streams.append((array, slice(0, width), first if array % 2 else second))
    stages = len(places)
    anywhere = pl.BlockSpec(memory_space=pl.ANY)
    wholes = pl.pallas_call(
        functools.partial(gather_kernel, places, streams, len(shards)),
        in_specs=[anywhere] * len(shards),
        out_specs=[anywhere] * len(shards),
        out_shape=[jax.ShapeDtypeStruct((2,) * stages + shard.shape, shard.dtype) for shard in shards],
        scratch_shapes=[
            pltpu.SemaphoreType.DMA((len(streams), stages)),
            pltpu.SemaphoreType.DMA((len(streams), stages)),
            pltpu.SemaphoreType.DMA((len(streams),)),
        ],
        compiler_params=pltpu.CompilerParams(collective_id=identity, has_side_effects=True),
        name="gather_all",
    )(*shards)
    return [whole.reshape((-1,) + whole.shape[stages + 1 :]) for whole in wholes]


def reduce_kernel(places, streams, count, *refs):
    parts, totals = refs[:count], refs[count : 2 * count]
    stages = len(places)
    landing = refs[2 * count : 2 * count + len(streams) * stages]
    send_sems, recv_sems = refs[2 * count + len(streams) * stages :]
    bits = [own_bit(place) for place in places]

    def spot(number, stage):
        return landing[number * stages + stage]

    def side(number, stage, value):
        array, cols, order = streams[number]
        left = [p for p in range(stages) if p not in order[:stage]]
        index = tuple(value if p == order[stage] else slice(None) for p in left)
        if stage == 0:
            return parts[array].at[index + (slice(None), cols)]
        return spot(number, stage - 1).at[index]

    meet(places)

    def send(number, stage):
        order = streams[number][2]
        copy = pltpu.make_async_remote_copy(
            src_ref=side(number, stage, 1 - bits[order[stage]]),
            dst_ref=spot(number, stage),
            send_sem=send_sems.at[number, stage],
            recv_sem=recv_sems.at[number, stage],
            device_id=partner(places[order[stage]]),
            device_id_type=MESH,
        )
        copy.start()
        return copy

    flights = [[send(number, 0)] for number in range(len(streams))]
    for stage in range(stages):
        for number, (array, cols, order) in enumerate(streams):
            flights[number][stage].wait_recv()
            mine = side(number, stage, bits[order[stage]])
            there = spot(number, stage)
            if stage + 1 < stages:
                depth = stages - stage - 1

                def add(index, unused):
                    at = tuple(lax.rem(index // 2 ** (depth - 1 - k), 2) for k in range(depth))
                    there[at] = (there[at].astype(jnp.float32) + mine[at].astype(jnp.float32)).astype(there.dtype)
                    return unused

                lax.fori_loop(0, 2**depth, add, 0)
                flights[number].append(send(number, stage + 1))
            else:
                totals[array][:, cols] = there[...].astype(jnp.float32) + mine[...].astype(jnp.float32)
    for flight in flights:
        for copy in flight:
            copy.wait_send()


def reduce_all(sizes, parts, identity):
    places = bit_positions(sizes)
    first, second = [tuple(order) for order in orders_of(places)]
    stages = len(places)
    streams = []
    blocks = []
    for array, part in enumerate(parts):
        width = part.shape[1]
        blocks.append(part.reshape((2,) * stages + (-1, width)))
        if width % 256 == 0:
            streams.append((array, slice(0, width // 2), first))
            streams.append((array, slice(width // 2, width), second))
        else:
            streams.append((array, slice(0, width), first if array % 2 else second))
    inside = pl.BlockSpec(memory_space=pltpu.VMEM)
    landing = []
    for array, cols, order in streams:
        for stage in range(stages):
            rows = blocks[array].shape[-2]
            landing.append(pltpu.VMEM((2,) * (stages - stage - 1) + (rows, cols.stop - cols.start), jnp.bfloat16))
    return pl.pallas_call(
        functools.partial(reduce_kernel, places, streams, len(parts)),
        in_specs=[inside] * len(parts),
        out_specs=[inside] * len(parts),
        out_shape=[jax.ShapeDtypeStruct(block.shape[-2:], jnp.float32) for block in blocks],
        scratch_shapes=landing
        + [
            pltpu.SemaphoreType.DMA((len(streams), stages)),
            pltpu.SemaphoreType.DMA((len(streams), stages)),
        ],
        compiler_params=pltpu.CompilerParams(
            collective_id=identity, has_side_effects=True, vmem_limit_bytes=48 * 1024 * 1024
        ),
        name="reduce_all",
    )(*blocks)


def dot(left, right):
    return jnp.dot(left, right, preferred_element_type=jnp.float32)


def contract(left, right, left_dim, right_dim):
    return lax.dot_general(left, right, (((left_dim,), (right_dim,)), ((), ())), preferred_element_type=jnp.float32)


def expert_kernel(slices, *refs):
    tokens_ref, grads_ref, column_ref, row_ref = refs[:4]
    weights_in, weights_out = refs[4 : 4 + slices], refs[4 + slices : 4 + 2 * slices]
    outs = refs[4 + 2 * slices :]
    picked_ref, back_ref = outs[:2]
    sums_in, sums_out = outs[2 : 2 + slices], outs[2 + slices : 2 + 2 * slices]
    (sent, got, answer, returned, w_in, w_out, hidden, total, active, slope, inner,
     send_sems, recv_sems, weight_sems, sum_sems) = outs[2 + 2 * slices :]
    experts, room, width = sent.shape[1:]
    places = experts * room
    me = lax.axis_index("exp")
    here = lax.axis_index("ctx")

    loads = []
    for s in range(slices):
        loads.append(pltpu.make_async_copy(weights_in[s], w_in.at[s], weight_sems.at[0, s]))
        loads.append(pltpu.make_async_copy(weights_out[s], w_out.at[s], weight_sems.at[1, s]))
    for load in loads:
        load.start()

    barrier = pltpu.get_barrier_semaphore()
    for step in range(1, experts):
        pl.semaphore_signal(barrier, inc=1, device_id=(here, lax.rem(me + step, experts)), device_id_type=MESH)
    pl.semaphore_wait(barrier, experts - 1)

    def exchange(source, target, kind):
        copies = []
        for step in range(1, experts):
            peer = lax.rem(me + step, experts)
            copy = pltpu.make_async_remote_copy(
                src_ref=source.at[peer],
                dst_ref=target.at[me],
                send_sem=send_sems.at[kind, step],
                recv_sem=recv_sems.at[kind, step],
                device_id=(here, peer),
                device_id_type=MESH,
            )
            copy.start()
            copies.append(copy)
        target[me] = source[me]
        return copies

    def arrive(copies):
        for copy in copies:
            copy.wait_recv()

    chooser = (lax.broadcasted_iota(jnp.int32, (places, row_ref.shape[1]), 0) == row_ref[...]).astype(jnp.float32).astype(jnp.bfloat16)
    sent[0] = dot(chooser, tokens_ref[...]).astype(jnp.bfloat16).reshape(experts, room, width)
    first = exchange(sent.at[0], got.at[0], 0)
    sent[1] = dot(chooser, grads_ref[...]).astype(jnp.bfloat16).reshape(experts, room, width)
    second = exchange(sent.at[1], got.at[1], 1)

    for load in loads:
        load.wait()
    arrive(first)
    rows = got[0].reshape(places, width)
    for s in range(slices):
        hidden[...] = dot(rows, w_in[s])

        def curve(index, unused):
            at = pl.ds(pl.multiple_of(index * ROWS_AT_ONCE, ROWS_AT_ONCE), ROWS_AT_ONCE)
            value = hidden[at, :]
            bell = 0.5 + 0.5 * lax.erf(value * 0.7071067811865476)
            active[s, at, :] = (value * bell).astype(jnp.bfloat16)
            slope[s, at, :] = bell + value * (jnp.exp(-0.5 * value * value) * 0.3989422804014327)
            return unused

        lax.fori_loop(0, places // ROWS_AT_ONCE, curve, 0)
        product = dot(active[s], w_out[s])
        total[...] = product if s == 0 else total[...] + product
    answer[0] = total[...].astype(jnp.bfloat16).reshape(experts, room, width)
    third = exchange(answer.at[0], returned.at[0], 2)

    arrive(second)
    pulled = got[1].reshape(places, width)
    for s in range(slices):
        inner[s] = (contract(pulled, w_out[s], 1, 1) * slope[s]).astype(jnp.bfloat16)
        product = contract(inner[s], w_in[s], 1, 1)
        total[...] = product if s == 0 else total[...] + product
    answer[1] = total[...].astype(jnp.bfloat16).reshape(experts, room, width)
    fourth = exchange(answer.at[1], returned.at[1], 3)

    stores = []
    for s in range(slices):
        w_out[s] = contract(active[s], pulled, 0, 0).astype(jnp.bfloat16)
        stores.append(pltpu.make_async_copy(w_out.at[s], sums_out[s], sum_sems.at[0, s]))
        stores[-1].start()
        w_in[s] = contract(rows, inner[s], 0, 0).astype(jnp.bfloat16)
        stores.append(pltpu.make_async_copy(w_in.at[s], sums_in[s], sum_sems.at[1, s]))
        stores[-1].start()

    finder = (lax.broadcasted_iota(jnp.int32, (column_ref.shape[0], places), 1) == column_ref[...]).astype(jnp.float32).astype(jnp.bfloat16)
    arrive(third)
    picked_ref[...] = dot(finder, returned[0].reshape(places, width)).astype(jnp.bfloat16)
    arrive(fourth)
    back_ref[...] = dot(finder, returned[1].reshape(places, width)).astype(jnp.bfloat16)
    for store in stores:
        store.wait()
    for copies in (first, second, third, fourth):
        for copy in copies:
            copy.wait_send()


def run_experts(rows, grads, target, weights_in, weights_out, experts, room, identity):
    slices = len(weights_in)
    tokens, width = rows.shape
    inner_width = weights_in[0].shape[1]
    places = experts * room
    inside = pl.BlockSpec(memory_space=pltpu.VMEM)
    anywhere = pl.BlockSpec(memory_space=pl.ANY)
    half = jnp.bfloat16
    out = pl.pallas_call(
        functools.partial(expert_kernel, slices),
        in_specs=[inside] * 4 + [anywhere] * (2 * slices),
        out_specs=[inside] * 2 + [anywhere] * (2 * slices),
        out_shape=[jax.ShapeDtypeStruct(rows.shape, half)] * 2
        + [jax.ShapeDtypeStruct(weight.shape, half) for weight in weights_in + weights_out],
        scratch_shapes=[pltpu.VMEM((2, experts, room, width), half)] * 4
        + [
            pltpu.VMEM((slices, width, inner_width), half),
            pltpu.VMEM((slices, inner_width, width), half),
            pltpu.VMEM((places, inner_width), jnp.float32),
            pltpu.VMEM((places, width), jnp.float32),
            pltpu.VMEM((slices, places, inner_width), half),
            pltpu.VMEM((slices, places, inner_width), jnp.float32),
            pltpu.VMEM((slices, places, inner_width), half),
            pltpu.SemaphoreType.DMA((4, experts)),
            pltpu.SemaphoreType.DMA((4, experts)),
            pltpu.SemaphoreType.DMA((2, slices)),
            pltpu.SemaphoreType.DMA((2, slices)),
        ],
        compiler_params=pltpu.CompilerParams(
            collective_id=identity, has_side_effects=True, vmem_limit_bytes=52 * 1024 * 1024
        ),
        name="run_experts",
    )(rows, grads, target[:, None], target[None, :], *weights_in, *weights_out)
    return out[0], out[1], list(out[2 : 2 + slices]), list(out[2 + slices :])


def flipped(value, level):
    count = lax.axis_size("ctx")
    return lax.ppermute(value, "ctx", [(source, source ^ (1 << level)) for source in range(count)])


def spread_slices(own):
    levels = lax.axis_size("ctx").bit_length() - 1
    slices = {0: own}
    for level in reversed(range(levels)):
        for offset in sorted(slices):
            slices[offset + (1 << level)] = flipped(slices[offset], level)
    return [slices[offset] for offset in sorted(slices)]


def collect_slices(sums):
    levels = lax.axis_size("ctx").bit_length() - 1
    for level in range(levels):
        step = 1 << level
        kept = {}
        for offset in range(0, len(sums), 2 * step):
            arrived = flipped(sums[offset + step].astype(jnp.bfloat16), level)
            kept[offset] = sums[offset].astype(jnp.float32) + arrived.astype(jnp.float32)
        sums = [kept.get(offset) for offset in range(len(sums))]
    return sums[0]


def body(
    inputs,
    segments,
    routes,
    cotangent,
    norm_gain,
    in_proj,
    conv_taps,
    conv_bias,
    x_proj,
    dt_proj,
    dt_bias,
    log_decay,
    skip_gain,
    out_proj,
    moe_gain,
    router,
    expert_in,
    expert_out,
):
    experts = router.shape[1]
    half_rows = norm_gain.shape[0]
    columns = (
        x_proj,
        dt_proj.T,
        conv_taps,
        conv_bias[:, None],
        dt_bias[:, None],
        log_decay,
        skip_gain[:, None],
        jnp.concatenate([norm_gain, moe_gain])[:, None],
        router.reshape(2 * half_rows, experts // 2),
    )
    widths = [part.shape[1] for part in columns]
    ends = [sum(widths[: k + 1]) for k in range(len(widths))]
    sizes = [(name, lax.axis_size(name)) for name in ("ctx", "exp")]
    full_in, full_out, full_small = gather_all(
        sizes, (in_proj, out_proj, jnp.concatenate(columns, axis=1)), 0
    )
    later_in, later_out, full_small = lax.optimization_barrier((expert_in[0], expert_out[0], full_small))
    weights_in = spread_slices(later_in)
    weights_out = spread_slices(later_out)
    full_xproj, full_dt, full_taps, full_bias, full_dtbias, full_decay, full_skip, gains, full_router = [
        full_small[:, end - width : end] for end, width in zip(ends, widths)
    ]
    full_dt = full_dt.T
    full_bias, full_dtbias, full_skip = full_bias[:, 0], full_dtbias[:, 0], full_skip[:, 0]
    gains = gains.reshape(-1, 2, half_rows)
    full_norm, full_moe = gains[:, 0].reshape(-1), gains[:, 1].reshape(-1)
    full_router = full_router.reshape(-1, experts)
    tokens_here = inputs.shape[1]
    capacity = 5 * tokens_here // (4 * experts)
    flat_in = inputs[0].astype(jnp.float32)
    seg_row = segments[0]
    position = lax.axis_index("ctx")
    norm_one_value, norm_one_pull = jax.vjp(rms_scale, flat_in, full_norm.astype(jnp.float32))
    normed_one = norm_one_value.astype(jnp.bfloat16)
    mixed_in = jnp.dot(normed_one, full_in, preferred_element_type=jnp.float32)
    conv_in = mixed_in[:, :DI].astype(jnp.bfloat16)
    gate_z = mixed_in[:, DI:]
    edge_rows, edge_ids = shifted(
        (conv_in[tokens_here - (KC - 1) :], seg_row[tokens_here - (KC - 1) :].astype(jnp.bfloat16)),
        "ctx",
        1,
    )
    prior_ids = jnp.where(position > 0, edge_ids.astype(jnp.int32), -1)
    ext_ids = jnp.concatenate([prior_ids, seg_row])
    ext_rows = jnp.concatenate([edge_rows, conv_in], axis=0).astype(jnp.float32)
    conv_out, conv_pull = jax.vjp(
        lambda rows_in, taps_in, bias_in: conv_local(rows_in, taps_in, bias_in, ext_ids),
        ext_rows,
        full_taps.astype(jnp.float32),
        full_bias.astype(jnp.float32),
    )
    silu_value, silu_pull = jax.vjp(jax.nn.silu, conv_out)
    xs_val = silu_value.astype(jnp.bfloat16)
    xs_wide = xs_val.astype(jnp.float32)
    projected = jnp.dot(xs_val, full_xproj, preferred_element_type=jnp.float32)
    delta_low = projected[:, :R].astype(jnp.bfloat16)
    b_rows = projected[:, R : R + NS]
    c_rows = projected[:, R + NS :]
    dt_pre = jnp.dot(delta_low, full_dt, preferred_element_type=jnp.float32) + full_dtbias.astype(
        jnp.float32
    )
    step_size = jax.nn.softplus(dt_pre)
    a_swap = -jnp.exp(full_decay.astype(jnp.float32)).T
    earlier = jnp.concatenate([prior_ids[KC - 2 :], seg_row[:-1]])
    keep_mask = (earlier == seg_row).astype(jnp.float32)
    masked_step = jnp.where(keep_mask[:, None] > 0, step_size, 1e30)
    push = step_size * xs_wide
    b_wide = jnp.broadcast_to(b_rows[:, :, None], (tokens_here, NS, LANES))
    c_wide = jnp.broadcast_to(c_rows[:, :, None], (tokens_here, NS, LANES))
    rates = a_swap * LOG2E
    block_end = scan_end(masked_step, push, b_wide, rates)
    block_product = jnp.exp2(jnp.sum(masked_step, axis=0)[None, :] * rates)
    gathered = lax.all_gather(
        jnp.stack([block_product, block_end]).astype(jnp.bfloat16)[None], "ctx", axis=0, tiled=True
    ).astype(jnp.float32)
    all_products, all_ends = gathered[:, 0], gathered[:, 1]
    zeros_state = jnp.zeros((NS, DI), jnp.float32)

    def fold_start(index_now, start_now):
        return jnp.where(
            index_now < position,
            all_products[index_now] * start_now + all_ends[index_now],
            start_now,
        )

    start_state = zeros_state
    for index_now in range(all_products.shape[0]):
        start_state = fold_start(index_now, start_state)
    scan_rows, kept, firsts = scan_out(masked_step, push, b_wide, c_wide, rates, start_state)
    skip_wide = full_skip.astype(jnp.float32)
    scanned_y = scan_rows + skip_wide * xs_wide
    gated_wide, gated_pull = jax.vjp(
        lambda scan_in, gate_in: scan_in * jax.nn.silu(gate_in), scanned_y, gate_z
    )
    gated = gated_wide.astype(jnp.bfloat16)
    mixed = jnp.dot(gated, full_out, preferred_element_type=jnp.float32)
    residual = flat_in + mixed
    norm_two_value, norm_two_pull = jax.vjp(rms_scale, residual, full_moe.astype(jnp.float32))
    normed_two = norm_two_value.astype(jnp.bfloat16)
    logits = jnp.dot(normed_two, full_router, preferred_element_type=jnp.float32)
    probability = jax.nn.softmax(logits, axis=-1)
    route_ids = routes[0, :, 0]
    one_hot = route_ids[:, None] == jnp.arange(experts, dtype=jnp.int32)[None, :]
    one_float = one_hot.astype(jnp.float32)
    gate_val = jnp.sum(probability * one_float, axis=1)
    running = jnp.cumsum(one_hot.astype(jnp.int32), axis=0)
    slot_index = jnp.sum(running * one_hot.astype(jnp.int32), axis=1) - 1
    room = -(-capacity // 16) * 16
    target = route_ids * room + slot_index
    grad_out = cotangent[0].astype(jnp.float32)
    grad_pick = (grad_out * gate_val[:, None]).astype(jnp.bfloat16)
    picked, grad_from_experts, grad_expert_in, grad_expert_out = run_experts(
        normed_two, grad_pick, target, weights_in, weights_out, experts, room, 2
    )
    picked = picked.astype(jnp.float32)
    grad_from_experts = grad_from_experts.astype(jnp.float32)
    outcome = residual + gate_val[:, None] * picked
    out_block = outcome.astype(jnp.bfloat16)[None]
    grad_gate = jnp.sum(grad_out * picked, axis=1)
    grad_w_in = collect_slices(grad_expert_in)[None]
    grad_w_out = collect_slices(grad_expert_out)[None]
    grad_probs = grad_gate[:, None] * one_float
    grad_logits = (
        probability * (grad_probs - jnp.sum(grad_probs * probability, axis=1, keepdims=True))
    ).astype(jnp.bfloat16)
    grad_router = jnp.dot(normed_two.T, grad_logits, preferred_element_type=jnp.float32)
    grad_normed_two = grad_from_experts + jnp.dot(
        grad_logits, full_router.T, preferred_element_type=jnp.float32
    )
    grad_resid_norm, grad_moe_gain = norm_two_pull(grad_normed_two)
    grad_resid = grad_out + grad_resid_norm
    grad_mixed = grad_resid.astype(jnp.bfloat16)
    grad_gated = jnp.dot(grad_mixed, full_out.T, preferred_element_type=jnp.float32)
    grad_out_proj = jnp.dot(gated.T, grad_mixed, preferred_element_type=jnp.float32)
    grad_y, grad_z = gated_pull(grad_gated)
    grad_skip = jnp.sum(grad_y * xs_wide, axis=0)
    local_inflow = scan_inflow(masked_step, grad_y, c_wide, rates)
    all_inflows = lax.all_gather(
        local_inflow[None].astype(jnp.bfloat16), "ctx", axis=0, tiled=True
    ).astype(jnp.float32)
    total_ctx = all_inflows.shape[0]

    def fold_end(step_index, end_now):
        source = total_ctx - 1 - step_index
        return jnp.where(
            source > position, all_inflows[source] + all_products[source] * end_now, end_now
        )

    end_inflow = zeros_state
    for step_index in range(total_ctx):
        end_inflow = fold_end(step_index, end_inflow)
    along_b, slope, wide_b, wide_c, grad_a = scan_adjoint(
        masked_step, push, grad_y, b_wide, c_wide, kept, firsts, rates, end_inflow
    )
    grad_step_all = along_b * xs_wide + slope * (1.0 / LOG2E)
    grad_xss = along_b * step_size
    grad_bs = jnp.sum(wide_b, axis=2)
    grad_cs = jnp.sum(wide_c, axis=2)
    grad_log_decay = (grad_a * a_swap).T
    soft_slope = jax.nn.sigmoid(dt_pre)
    grad_pre_wide = grad_step_all * soft_slope
    grad_dt_bias = jnp.sum(grad_pre_wide, axis=0)
    grad_dt_pre = grad_pre_wide.astype(jnp.bfloat16)
    grad_dt_proj = jnp.dot(delta_low.T, grad_dt_pre, preferred_element_type=jnp.float32)
    grad_delta = jnp.dot(grad_dt_pre, full_dt.T, preferred_element_type=jnp.float32)
    grad_projected = jnp.concatenate(
        [grad_delta, grad_bs, grad_cs], axis=1
    ).astype(jnp.bfloat16)
    grad_x_proj = jnp.dot(xs_val.T, grad_projected, preferred_element_type=jnp.float32)
    grad_xs_total = (
        skip_wide * grad_y
        + grad_xss
        + jnp.dot(grad_projected, full_xproj.T, preferred_element_type=jnp.float32)
    )
    grad_conv = silu_pull(grad_xs_total)[0]
    grad_ext, grad_taps, grad_cbias = conv_pull(grad_conv)
    from_next = shifted(grad_ext[: KC - 1], "ctx", -1)
    grad_conv_in = grad_ext[KC - 1 :] + jnp.concatenate(
        [jnp.zeros((tokens_here - (KC - 1), DI), jnp.float32), from_next], axis=0
    )
    grad_mixed_in = jnp.concatenate([grad_conv_in, grad_z], axis=1).astype(jnp.bfloat16)
    grad_in_proj = jnp.dot(normed_one.T, grad_mixed_in, preferred_element_type=jnp.float32)
    grad_normed_one = jnp.dot(grad_mixed_in, full_in.T, preferred_element_type=jnp.float32)
    grad_inputs_norm, grad_norm_gain = norm_one_pull(grad_normed_one)
    grad_inputs = grad_resid + grad_inputs_norm
    sums = (
        grad_x_proj,
        grad_dt_proj.T,
        grad_taps,
        grad_cbias[:, None],
        grad_dt_bias[:, None],
        grad_log_decay,
        grad_skip[:, None],
        jnp.stack(
            [grad_norm_gain.reshape(-1, half_rows), grad_moe_gain.reshape(-1, half_rows)], axis=1
        ).reshape(-1, 1),
        grad_router.reshape(-1, experts // 2),
    )

    own_in, own_out, own_small = reduce_all(
        sizes,
        (
            grad_in_proj.astype(jnp.bfloat16),
            grad_out_proj.astype(jnp.bfloat16),
            jnp.concatenate(sums, axis=1).astype(jnp.bfloat16),
        ),
        1,
    )
    own_x, own_dt, own_taps, own_bias, own_dtbias, own_decay, own_skip, own_gains, own_router = [
        own_small[:, end - width : end] for end, width in zip(ends, widths)
    ]
    return (
        out_block,
        grad_inputs[None],
        own_gains[:half_rows, 0],
        own_in,
        own_taps,
        own_bias[:, 0],
        own_x,
        own_dt.T,
        own_dtbias[:, 0],
        own_decay,
        own_skip[:, 0],
        own_out,
        own_gains[half_rows:, 0],
        own_router.reshape(half_rows, experts),
        grad_w_in,
        grad_w_out,
    )


def solution(mesh):
    placed = (
        P("exp", "ctx", None),
        P("exp", "ctx"),
        P("exp", "ctx", None),
        P("exp", "ctx", None),
        P(("ctx", "exp")),
        P(("ctx", "exp"), None),
        P(("ctx", "exp"), None),
        P(("ctx", "exp")),
        P(("ctx", "exp"), None),
        P(None, ("ctx", "exp")),
        P(("ctx", "exp")),
        P(("ctx", "exp"), None),
        P(("ctx", "exp")),
        P(("ctx", "exp"), None),
        P(("ctx", "exp")),
        P(("ctx", "exp"), None),
        P("exp", None, "ctx"),
        P("exp", "ctx", None),
    )
    return jax.shard_map(
        body,
        mesh=mesh,
        in_specs=placed,
        out_specs=(
            P("exp", "ctx", None),
            P("exp", "ctx", None),
            P(("ctx", "exp")),
            P(("ctx", "exp"), None),
            P(("ctx", "exp"), None),
            P(("ctx", "exp")),
            P(("ctx", "exp"), None),
            P(None, ("ctx", "exp")),
            P(("ctx", "exp")),
            P(("ctx", "exp"), None),
            P(("ctx", "exp")),
            P(("ctx", "exp"), None),
            P(("ctx", "exp")),
            P(("ctx", "exp"), None),
            P("exp", None, "ctx"),
            P("exp", "ctx", None),
        ),
        check_vma=False,
    )
```

```python
import functools

import jax
import jax.numpy as jnp
from jax import lax
from jax.experimental import pallas as pl
from jax.experimental.pallas import tpu as pltpu
from jax.sharding import PartitionSpec as P

D = 768
DI = 1536
NS = 16
R = 48
KC = 4
LANES = 128
UNROLL = 8
LOG2E = 1.4426950408889634


EPS = 1e-05
MESH = pl.DeviceIdType.MESH
ROWS_AT_ONCE = 16
EDGE = 16

def tile(ref, base, lanes):
    return ref[pl.ds(pl.multiple_of(base, UNROLL), UNROLL), lanes]

def row(rows_now, place):
    return jnp.broadcast_to(rows_now[place : place + 1], (NS, LANES))

def put_row(rows_now, place, value):
    at = lax.broadcasted_iota(jnp.int32, (UNROLL, LANES), 0)
    value = jnp.broadcast_to(value, (UNROLL, LANES))
    return value if rows_now is None else jnp.where(at == place, value, rows_now)

def end_kernel(width, step_ref, push_ref, b_ref, rate_ref, end_ref):
    rows, channels = step_ref.shape

    @pl.when(pl.program_id(0) == 0)
    def _():
        end_ref[...] = jnp.zeros_like(end_ref)

    for group in range(0, channels, width):
        pieces = [slice(at, at + LANES) for at in range(group, group + width, LANES)]
        rates = [rate_ref[:, lanes] for lanes in pieces]

        def block(index, states):
            states = list(states)
            steps = [tile(step_ref, index * UNROLL, lanes) for lanes in pieces]
            pushes = [tile(push_ref, index * UNROLL, lanes) for lanes in pieces]
            for place in range(UNROLL):
                t = index * UNROLL + place
                b_now = b_ref[t]
                for k, lanes in enumerate(pieces):
                    decay = jnp.exp2(row(steps[k], place) * rates[k])
                    states[k] = decay * states[k] + b_now * row(pushes[k], place)
            return tuple(states)

        states = lax.fori_loop(0, rows // UNROLL, block, tuple(end_ref[:, lanes] for lanes in pieces))
        for k, lanes in enumerate(pieces):
            end_ref[:, lanes] = states[k]

def out_kernel(width, step_ref, push_ref, b_ref, c_ref, rate_ref, start_ref, y_ref, kept_ref, first_ref, state_ref):
    rows, channels = step_ref.shape

    @pl.when(pl.program_id(0) == 0)
    def _():
        state_ref[...] = start_ref[...]

    first_ref[0] = state_ref[...].astype(first_ref.dtype)
    for group in range(0, channels, width):
        pieces = [slice(at, at + LANES) for at in range(group, group + width, LANES)]
        rates = [rate_ref[:, lanes] for lanes in pieces]

        def block(index, states):
            states = list(states)
            steps = [tile(step_ref, index * UNROLL, lanes) for lanes in pieces]
            pushes = [tile(push_ref, index * UNROLL, lanes) for lanes in pieces]
            outs = [None] * len(pieces)
            for place in range(UNROLL):
                t = index * UNROLL + place
                b_now = b_ref[t]
                c_now = c_ref[t]
                for k, lanes in enumerate(pieces):
                    decay = jnp.exp2(row(steps[k], place) * rates[k])
                    states[k] = decay * states[k] + b_now * row(pushes[k], place)
                    kept_ref[t, :, lanes] = states[k].astype(kept_ref.dtype)
                    outs[k] = put_row(outs[k], place, jnp.sum(states[k] * c_now, axis=0, keepdims=True))
            for k, lanes in enumerate(pieces):
                y_ref[pl.ds(pl.multiple_of(index * UNROLL, UNROLL), UNROLL), lanes] = outs[k]
            return tuple(states)

        states = lax.fori_loop(0, rows // UNROLL, block, tuple(state_ref[:, lanes] for lanes in pieces))
        for k, lanes in enumerate(pieces):
            state_ref[:, lanes] = states[k]

def inflow_kernel(width, step_ref, grad_ref, c_ref, rate_ref, end_ref):
    rows, channels = step_ref.shape

    @pl.when(pl.program_id(0) == 0)
    def _():
        end_ref[...] = jnp.zeros_like(end_ref)

    for group in range(0, channels, width):
        pieces = [slice(at, at + LANES) for at in range(group, group + width, LANES)]
        rates = [rate_ref[:, lanes] for lanes in pieces]

        def block(index, flows):
            flows = list(flows)
            base = rows - UNROLL - index * UNROLL
            steps = [tile(step_ref, base, lanes) for lanes in pieces]
            grads = [tile(grad_ref, base, lanes) for lanes in pieces]
            for place in reversed(range(UNROLL)):
                c_now = c_ref[base + place]
                for k, lanes in enumerate(pieces):
                    decay = jnp.exp2(row(steps[k], place) * rates[k])
                    flows[k] = decay * (c_now * row(grads[k], place) + flows[k])
            return tuple(flows)

        flows = lax.fori_loop(0, rows // UNROLL, block, tuple(end_ref[:, lanes] for lanes in pieces))
        for k, lanes in enumerate(pieces):
            end_ref[:, lanes] = flows[k]

def adjoint_kernel(width, step_ref, push_ref, grad_ref, b_ref, c_ref, kept_ref, first_ref, rate_ref, end_ref,
                   along_ref, slope_ref, gb_ref, gc_ref, ga_ref, flow_ref):
    rows, channels = step_ref.shape

    @pl.when(pl.program_id(0) == 0)
    def _():
        flow_ref[...] = end_ref[...]
        ga_ref[...] = jnp.zeros_like(ga_ref)

    for group in range(0, channels, width):
        pieces = [slice(at, at + LANES) for at in range(group, group + width, LANES)]
        rates = [rate_ref[:, lanes] for lanes in pieces]
        count = len(pieces)

        def block(index, carried, last):
            flows, sums, current = list(carried[:count]), list(carried[count:2*count]), list(carried[2*count:])
            base = rows - UNROLL - index * UNROLL
            steps = [tile(step_ref, base, lanes) for lanes in pieces]
            pushes = [tile(push_ref, base, lanes) for lanes in pieces]
            grads = [tile(grad_ref, base, lanes) for lanes in pieces]
            alongs = [None] * count
            slopes = [None] * count
            for place in reversed(range(UNROLL)):
                t = base + place
                b_now = b_ref[t]
                c_now = c_ref[t]
                gb = gc = None
                for k, lanes in enumerate(pieces):
                    if last and place == 0:
                        prior = first_ref[0, :, lanes].astype(jnp.float32)
                    else:
                        prior = kept_ref[t - 1, :, lanes].astype(jnp.float32)
                    step = row(steps[k], place)
                    grad = row(grads[k], place)
                    decay = jnp.exp2(step * rates[k])
                    adjoint = c_now * grad + flows[k]
                    flows[k] = decay * adjoint
                    decay_grad = flows[k] * prior
                    alongs[k] = put_row(alongs[k], place, jnp.sum(adjoint * b_now, axis=0, keepdims=True))
                    slopes[k] = put_row(slopes[k], place, jnp.sum(decay_grad * rates[k], axis=0, keepdims=True))
                    sums[k] = sums[k] + decay_grad * step
                    part_b = adjoint * row(pushes[k], place)
                    part_c = current[k] * grad
                    gb = part_b if gb is None else gb + part_b
                    gc = part_c if gc is None else gc + part_c
                    current[k] = prior
                if group == 0:
                    gb_ref[t] = gb
                    gc_ref[t] = gc
                else:
                    gb_ref[t] += gb
                    gc_ref[t] += gc
            where = pl.ds(pl.multiple_of(base, UNROLL), UNROLL)
            for k, lanes in enumerate(pieces):
                along_ref[where, lanes] = alongs[k]
                slope_ref[where, lanes] = slopes[k]
            return tuple(flows + sums + current)

        carried = (tuple(flow_ref[:, lanes] for lanes in pieces) + tuple(ga_ref[:, lanes] for lanes in pieces)
                   + tuple(kept_ref[rows - 1, :, lanes].astype(jnp.float32) for lanes in pieces))
        steps = rows // UNROLL
        carried = lax.fori_loop(0, steps - 1, functools.partial(block, last=False), carried)
        carried = block(steps - 1, carried, True)
        for k, lanes in enumerate(pieces):
            flow_ref[:, lanes] = carried[k]
            ga_ref[:, lanes] = carried[count + k]

def over_time(rows, width):
    return pl.BlockSpec((rows, width), lambda i: (i, 0))

PARAMS = pltpu.CompilerParams(vmem_limit_bytes=48 * 1024 * 1024, dimension_semantics=("arbitrary",))

def cost(tokens, channels, share):
    size = tokens * channels * NS
    return pl.CostEstimate(flops=size * share, transcendentals=size, bytes_accessed=size * share)


def pick(channels):
    return 512 if channels % 512 == 0 else 128

def scan_end(step, push, b_wide, rates, rows=64):
    tokens, channels = step.shape
    return pl.pallas_call(
        functools.partial(end_kernel, pick(channels)),
        grid=(tokens // rows,),
        in_specs=[pl.BlockSpec((rows, channels), lambda i: (i, 0))] * 2
        + [pl.BlockSpec((rows, NS, LANES), lambda i: (i, 0, 0)), pl.BlockSpec((NS, channels), lambda i: (0, 0))],
        out_specs=pl.BlockSpec((NS, channels), lambda i: (0, 0)),
        out_shape=jax.ShapeDtypeStruct((NS, channels), jnp.float32),
        cost_estimate=cost(tokens, channels, 3),
        compiler_params=PARAMS,
    )(step, push, b_wide, rates)

def scan_out(step, push, b_wide, c_wide, rates, start, rows=64):
    tokens, channels = step.shape
    wide = pl.BlockSpec((rows, channels), lambda i: (i, 0))
    cast = pl.BlockSpec((rows, NS, LANES), lambda i: (i, 0, 0))
    fixed = pl.BlockSpec((NS, channels), lambda i: (0, 0))
    return pl.pallas_call(
        functools.partial(out_kernel, pick(channels)),
        grid=(tokens // rows,),
        in_specs=[wide, wide, cast, cast, fixed, fixed],
        out_specs=[wide, pl.BlockSpec((rows, NS, channels), lambda i: (i, 0, 0)), pl.BlockSpec((1, NS, channels), lambda i: (i, 0, 0))],
        out_shape=[jax.ShapeDtypeStruct((tokens, channels), jnp.float32),
                   jax.ShapeDtypeStruct((tokens, NS, channels), jnp.bfloat16),
                   jax.ShapeDtypeStruct((tokens // rows, NS, channels), jnp.bfloat16)],
        scratch_shapes=[pltpu.VMEM((NS, channels), jnp.float32)],
        cost_estimate=cost(tokens, channels, 6),
        compiler_params=PARAMS,
    )(step, push, b_wide, c_wide, rates, start)

def scan_inflow(step, grad, c_wide, rates, rows=64):
    tokens, channels = step.shape
    last = tokens // rows - 1
    return pl.pallas_call(
        functools.partial(inflow_kernel, pick(channels)),
        grid=(tokens // rows,),
        in_specs=[pl.BlockSpec((rows, channels), lambda i: (last - i, 0))] * 2
        + [pl.BlockSpec((rows, NS, LANES), lambda i: (last - i, 0, 0)), pl.BlockSpec((NS, channels), lambda i: (0, 0))],
        out_specs=pl.BlockSpec((NS, channels), lambda i: (0, 0)),
        out_shape=jax.ShapeDtypeStruct((NS, channels), jnp.float32),
        cost_estimate=cost(tokens, channels, 3),
        compiler_params=PARAMS,
    )(step, grad, c_wide, rates)

def scan_adjoint(step, push, grad, b_wide, c_wide, kept, firsts, rates, end, rows=64):
    tokens, channels = step.shape
    last = tokens // rows - 1
    wide = pl.BlockSpec((rows, channels), lambda i: (last - i, 0))
    cast = pl.BlockSpec((rows, NS, LANES), lambda i: (last - i, 0, 0))
    fixed = pl.BlockSpec((NS, channels), lambda i: (0, 0))
    return pl.pallas_call(
        functools.partial(adjoint_kernel, pick(channels)),
        grid=(tokens // rows,),
        in_specs=[wide, wide, wide, cast, cast, pl.BlockSpec((rows, NS, channels), lambda i: (last - i, 0, 0)),
                  pl.BlockSpec((1, NS, channels), lambda i: (last - i, 0, 0)), fixed, fixed],
        out_specs=[wide, wide, cast, cast, fixed],
        out_shape=[jax.ShapeDtypeStruct((tokens, channels), jnp.float32)] * 2
        + [jax.ShapeDtypeStruct((tokens, NS, LANES), jnp.float32)] * 2
        + [jax.ShapeDtypeStruct((NS, channels), jnp.float32)],
        scratch_shapes=[pltpu.VMEM((NS, channels), jnp.float32)],
        cost_estimate=cost(tokens, channels, 12),
        compiler_params=PARAMS,
    )(step, push, grad, b_wide, c_wide, kept, firsts, rates, end)


def shifted(value, axis, steps):
    count = lax.axis_size(axis)
    initial, last = (max(0, -steps), min(count, count - steps))
    return lax.ppermute(value, axis, [(source, source + steps) for source in range(initial, last)])


def rms_scale(values, gain):
    return values * lax.rsqrt(jnp.mean(values * values, axis=-1, keepdims=True) + EPS) * gain


def conv_local(ext_rows, taps, bias, ext_ids):
    length = ext_rows.shape[0] - (KC - 1)
    own_ids = ext_ids[KC - 1 :]
    result = jnp.zeros((length, ext_rows.shape[1]), jnp.float32) + bias[None, :]
    for offset in range(KC):
        same_doc = (ext_ids[offset : offset + length] == own_ids).astype(jnp.float32)
        result = (
            result
            + taps[:, offset][None, :] * ext_rows[offset : offset + length] * same_doc[:, None]
        )
    return result


def bit_positions(sizes):
    return [(axis, size.bit_length() - 2 - k) for axis, size in sizes for k in range(size.bit_length() - 1)]


def own_bit(place):
    axis, level = place
    return lax.rem(lax.axis_index(axis) // 2**level, 2)


def partner(place):
    axis, level = place
    where = {"ctx": lax.axis_index("ctx"), "exp": lax.axis_index("exp")}
    where[axis] = where[axis] + (1 - 2 * own_bit(place)) * 2**level
    return (where["ctx"], where["exp"])


def meet(places, *others):
    barrier = pltpu.get_barrier_semaphore()
    for device in [partner(place) for place in places] + list(others):
        pl.semaphore_signal(barrier, inc=1, device_id=device, device_id_type=MESH)
    pl.semaphore_wait(barrier, len(places) + len(others))


def gather_kernel(places, streams, count, *refs):
    shards, edge_ref, wholes, prior_ref = refs[:count], refs[count], refs[count + 1 : 2 * count + 1], refs[2 * count + 1]
    send_sems, recv_sems, local_sems, edge_sems = refs[2 * count + 2 :]
    bits = [own_bit(place) for place in places]

    def view(stream, have):
        array, cols, order = stream
        index = tuple(slice(None) if p in have else bits[p] for p in range(len(places)))
        return wholes[array].at[index + (slice(None), cols)]

    blocks = lax.axis_size("ctx")
    here, line = lax.axis_index("ctx"), lax.axis_index("exp")
    meet(places, (lax.rem(here + 1, blocks), line), (lax.rem(here + blocks - 1, blocks), line))
    edge = pltpu.make_async_remote_copy(
        src_ref=edge_ref,
        dst_ref=prior_ref,
        send_sem=edge_sems.at[0],
        recv_sem=edge_sems.at[1],
        device_id=(lax.rem(here + 1, blocks), line),
        device_id_type=MESH,
    )
    edge.start()
    locals_ = []
    for number, stream in enumerate(streams):
        array, cols, order = stream
        copy = pltpu.make_async_copy(shards[array].at[:, cols], view(stream, ()), local_sems.at[number])
        copy.start()
        locals_.append(copy)

    def send(number, stage):
        stream = streams[number]
        array, cols, order = stream
        source = shards[array].at[:, cols] if stage == 0 else view(stream, order[:stage])
        copy = pltpu.make_async_remote_copy(
            src_ref=source,
            dst_ref=view(stream, order[:stage]),
            send_sem=send_sems.at[number, stage],
            recv_sem=recv_sems.at[number, stage],
            device_id=partner(places[order[stage]]),
            device_id_type=MESH,
        )
        copy.start()
        return copy

    stages = len(places)
    flights = [[send(number, 0)] for number in range(len(streams))]
    for copy in locals_:
        copy.wait()
    for stage in range(stages):
        for number in range(len(streams)):
            flights[number][stage].wait_recv()
            if stage + 1 < stages:
                flights[number].append(send(number, stage + 1))
    edge.wait()
    for flight in flights:
        for copy in flight:
            copy.wait_send()


def orders_of(places):
    core = places.index(("ctx", 0))
    rows = [k for k, place in enumerate(places) if place[0] == "ctx" and place[1] > 0]
    near = places.index(("exp", 0))
    far = [k for k, place in sorted(enumerate(places), key=lambda item: item[1][1]) if place[0] == "exp" and place[1] > 0]
    return [core] + rows + [near] + far, [core, near] + rows + far


def gather_all(sizes, shards, edge, identity):
    places = bit_positions(sizes)
    first, second = [tuple(reversed(order)) for order in orders_of(places)]
    streams = []
    for array, shard in enumerate(shards):
        width = shard.shape[1]
        if width % 256 == 0:
            streams.append((array, slice(0, width // 2), first))
            streams.append((array, slice(width // 2, width), second))
        else:
            streams.append((array, slice(0, width), first if array % 2 else second))
    stages = len(places)
    anywhere = pl.BlockSpec(memory_space=pl.ANY)
    *wholes, prior = pl.pallas_call(
        functools.partial(gather_kernel, places, streams, len(shards)),
        in_specs=[anywhere] * (len(shards) + 1),
        out_specs=[anywhere] * (len(shards) + 1),
        out_shape=[jax.ShapeDtypeStruct((2,) * stages + shard.shape, shard.dtype) for shard in shards]
        + [jax.ShapeDtypeStruct(edge.shape, edge.dtype)],
        scratch_shapes=[
            pltpu.SemaphoreType.DMA((len(streams), stages)),
            pltpu.SemaphoreType.DMA((len(streams), stages)),
            pltpu.SemaphoreType.DMA((len(streams),)),
            pltpu.SemaphoreType.DMA((2,)),
        ],
        compiler_params=pltpu.CompilerParams(collective_id=identity, has_side_effects=True),
        name="gather_all",
    )(*shards, edge)
    return [whole.reshape((-1,) + whole.shape[stages + 1 :]) for whole in wholes], prior


def reduce_kernel(places, streams, count, *refs):
    parts, totals = refs[:count], refs[count : 2 * count]
    stages = len(places)
    landing = refs[2 * count : 2 * count + len(streams) * stages]
    send_sems, recv_sems = refs[2 * count + len(streams) * stages :]
    bits = [own_bit(place) for place in places]

    def spot(number, stage):
        return landing[number * stages + stage]

    def side(number, stage, value):
        array, cols, order = streams[number]
        left = [p for p in range(stages) if p not in order[:stage]]
        index = tuple(value if p == order[stage] else slice(None) for p in left)
        if stage == 0:
            return parts[array].at[index + (slice(None), cols)]
        return spot(number, stage - 1).at[index]

    meet(places)

    def send(number, stage):
        order = streams[number][2]
        copy = pltpu.make_async_remote_copy(
            src_ref=side(number, stage, 1 - bits[order[stage]]),
            dst_ref=spot(number, stage),
            send_sem=send_sems.at[number, stage],
            recv_sem=recv_sems.at[number, stage],
            device_id=partner(places[order[stage]]),
            device_id_type=MESH,
        )
        copy.start()
        return copy

    flights = [[send(number, 0)] for number in range(len(streams))]
    for stage in range(stages):
        for number, (array, cols, order) in enumerate(streams):
            flights[number][stage].wait_recv()
            mine = side(number, stage, bits[order[stage]])
            there = spot(number, stage)
            if stage + 1 < stages:
                depth = stages - stage - 1

                def add(index, unused):
                    at = tuple(lax.rem(index // 2 ** (depth - 1 - k), 2) for k in range(depth))
                    there[at] = (there[at].astype(jnp.float32) + mine[at].astype(jnp.float32)).astype(there.dtype)
                    return unused

                lax.fori_loop(0, 2**depth, add, 0)
                flights[number].append(send(number, stage + 1))
            else:
                totals[array][:, cols] = there[...].astype(jnp.float32) + mine[...].astype(jnp.float32)
    for flight in flights:
        for copy in flight:
            copy.wait_send()


def reduce_all(sizes, parts, identity):
    places = bit_positions(sizes)
    first, second = [tuple(order) for order in orders_of(places)]
    stages = len(places)
    streams = []
    blocks = []
    for array, part in enumerate(parts):
        width = part.shape[1]
        blocks.append(part.reshape((2,) * stages + (-1, width)))
        if width % 256 == 0:
            streams.append((array, slice(0, width // 2), first))
            streams.append((array, slice(width // 2, width), second))
        else:
            streams.append((array, slice(0, width), first if array % 2 else second))
    inside = pl.BlockSpec(memory_space=pltpu.VMEM)
    landing = []
    for array, cols, order in streams:
        for stage in range(stages):
            rows = blocks[array].shape[-2]
            landing.append(pltpu.VMEM((2,) * (stages - stage - 1) + (rows, cols.stop - cols.start), jnp.bfloat16))
    return pl.pallas_call(
        functools.partial(reduce_kernel, places, streams, len(parts)),
        in_specs=[inside] * len(parts),
        out_specs=[inside] * len(parts),
        out_shape=[jax.ShapeDtypeStruct(block.shape[-2:], jnp.float32) for block in blocks],
        scratch_shapes=landing
        + [
            pltpu.SemaphoreType.DMA((len(streams), stages)),
            pltpu.SemaphoreType.DMA((len(streams), stages)),
        ],
        compiler_params=pltpu.CompilerParams(
            collective_id=identity, has_side_effects=True, vmem_limit_bytes=48 * 1024 * 1024
        ),
        name="reduce_all",
    )(*blocks)


def dot(left, right):
    return jnp.dot(left, right, preferred_element_type=jnp.float32)


def contract(left, right, left_dim, right_dim):
    return lax.dot_general(left, right, (((left_dim,), (right_dim,)), ((), ())), preferred_element_type=jnp.float32)


def expert_kernel(slices, *refs):
    tokens_ref, grads_ref, column_ref, row_ref = refs[:4]
    weights_in, weights_out = refs[4 : 4 + slices], refs[4 + slices : 4 + 2 * slices]
    outs = refs[4 + 2 * slices :]
    picked_ref, back_ref = outs[:2]
    sums_in, sums_out = outs[2 : 2 + slices], outs[2 + slices : 2 + 2 * slices]
    (sent, got, answer, returned, w_in, w_out, hidden, total, active, slope, inner,
     send_sems, recv_sems, weight_sems, sum_sems) = outs[2 + 2 * slices :]
    experts, room, width = sent.shape[1:]
    places = experts * room
    me = lax.axis_index("exp")
    here = lax.axis_index("ctx")

    loads = []
    for s in range(slices):
        loads.append(pltpu.make_async_copy(weights_in[s], w_in.at[s], weight_sems.at[0, s]))
        loads.append(pltpu.make_async_copy(weights_out[s], w_out.at[s], weight_sems.at[1, s]))
    for load in loads:
        load.start()

    barrier = pltpu.get_barrier_semaphore()
    for step in range(1, experts):
        pl.semaphore_signal(barrier, inc=1, device_id=(here, lax.rem(me + step, experts)), device_id_type=MESH)
    pl.semaphore_wait(barrier, experts - 1)

    def exchange(source, target, kind):
        copies = []
        for step in range(1, experts):
            peer = lax.rem(me + step, experts)
            copy = pltpu.make_async_remote_copy(
                src_ref=source.at[peer],
                dst_ref=target.at[me],
                send_sem=send_sems.at[kind, step],
                recv_sem=recv_sems.at[kind, step],
                device_id=(here, peer),
                device_id_type=MESH,
            )
            copy.start()
            copies.append(copy)
        target[me] = source[me]
        return copies

    def arrive(copies):
        for copy in copies:
            copy.wait_recv()

    chooser = (lax.broadcasted_iota(jnp.int32, (places, row_ref.shape[1]), 0) == row_ref[...]).astype(jnp.float32).astype(jnp.bfloat16)
    sent[0] = dot(chooser, tokens_ref[...]).astype(jnp.bfloat16).reshape(experts, room, width)
    first = exchange(sent.at[0], got.at[0], 0)
    sent[1] = dot(chooser, grads_ref[...]).astype(jnp.bfloat16).reshape(experts, room, width)
    second = exchange(sent.at[1], got.at[1], 1)

    for load in loads:
        load.wait()
    arrive(first)
    rows = got[0].reshape(places, width)
    for s in range(slices):
        hidden[...] = dot(rows, w_in[s])

        def curve(index, unused):
            at = pl.ds(pl.multiple_of(index * ROWS_AT_ONCE, ROWS_AT_ONCE), ROWS_AT_ONCE)
            value = hidden[at, :]
            bell = 0.5 + 0.5 * lax.erf(value * 0.7071067811865476)
            active[s, at, :] = (value * bell).astype(jnp.bfloat16)
            slope[s, at, :] = bell + value * (jnp.exp(-0.5 * value * value) * 0.3989422804014327)
            return unused

        lax.fori_loop(0, places // ROWS_AT_ONCE, curve, 0)
        product = dot(active[s], w_out[s])
        total[...] = product if s == 0 else total[...] + product
    answer[0] = total[...].astype(jnp.bfloat16).reshape(experts, room, width)
    third = exchange(answer.at[0], returned.at[0], 2)

    arrive(second)
    pulled = got[1].reshape(places, width)
    for s in range(slices):
        inner[s] = (contract(pulled, w_out[s], 1, 1) * slope[s]).astype(jnp.bfloat16)
        product = contract(inner[s], w_in[s], 1, 1)
        total[...] = product if s == 0 else total[...] + product
    answer[1] = total[...].astype(jnp.bfloat16).reshape(experts, room, width)
    fourth = exchange(answer.at[1], returned.at[1], 3)

    stores = []
    for s in range(slices):
        w_out[s] = contract(active[s], pulled, 0, 0).astype(jnp.bfloat16)
        stores.append(pltpu.make_async_copy(w_out.at[s], sums_out[s], sum_sems.at[0, s]))
        stores[-1].start()
        w_in[s] = contract(rows, inner[s], 0, 0).astype(jnp.bfloat16)
        stores.append(pltpu.make_async_copy(w_in.at[s], sums_in[s], sum_sems.at[1, s]))
        stores[-1].start()

    finder = (lax.broadcasted_iota(jnp.int32, (column_ref.shape[0], places), 1) == column_ref[...]).astype(jnp.float32).astype(jnp.bfloat16)
    arrive(third)
    picked_ref[...] = dot(finder, returned[0].reshape(places, width)).astype(jnp.bfloat16)
    arrive(fourth)
    back_ref[...] = dot(finder, returned[1].reshape(places, width)).astype(jnp.bfloat16)
    for store in stores:
        store.wait()
    for copies in (first, second, third, fourth):
        for copy in copies:
            copy.wait_send()


def run_experts(rows, grads, target, weights_in, weights_out, experts, room, identity):
    slices = len(weights_in)
    tokens, width = rows.shape
    inner_width = weights_in[0].shape[1]
    places = experts * room
    inside = pl.BlockSpec(memory_space=pltpu.VMEM)
    anywhere = pl.BlockSpec(memory_space=pl.ANY)
    half = jnp.bfloat16
    out = pl.pallas_call(
        functools.partial(expert_kernel, slices),
        in_specs=[inside] * 4 + [anywhere] * (2 * slices),
        out_specs=[inside] * 2 + [anywhere] * (2 * slices),
        out_shape=[jax.ShapeDtypeStruct(rows.shape, half)] * 2
        + [jax.ShapeDtypeStruct(weight.shape, half) for weight in weights_in + weights_out],
        scratch_shapes=[pltpu.VMEM((2, experts, room, width), half)] * 4
        + [
            pltpu.VMEM((slices, width, inner_width), half),
            pltpu.VMEM((slices, inner_width, width), half),
            pltpu.VMEM((places, inner_width), jnp.float32),
            pltpu.VMEM((places, width), jnp.float32),
            pltpu.VMEM((slices, places, inner_width), half),
            pltpu.VMEM((slices, places, inner_width), jnp.float32),
            pltpu.VMEM((slices, places, inner_width), half),
            pltpu.SemaphoreType.DMA((4, experts)),
            pltpu.SemaphoreType.DMA((4, experts)),
            pltpu.SemaphoreType.DMA((2, slices)),
            pltpu.SemaphoreType.DMA((2, slices)),
        ],
        compiler_params=pltpu.CompilerParams(
            collective_id=identity, has_side_effects=True, vmem_limit_bytes=52 * 1024 * 1024
        ),
        name="run_experts",
    )(rows, grads, target[:, None], target[None, :], *weights_in, *weights_out)
    return out[0], out[1], list(out[2 : 2 + slices]), list(out[2 + slices :])


def flipped(value, level):
    count = lax.axis_size("ctx")
    return lax.ppermute(value, "ctx", [(source, source ^ (1 << level)) for source in range(count)])


def spread_slices(own):
    levels = lax.axis_size("ctx").bit_length() - 1
    slices = {0: own}
    for level in reversed(range(levels)):
        for offset in sorted(slices):
            slices[offset + (1 << level)] = flipped(slices[offset], level)
    return [slices[offset] for offset in sorted(slices)]


def collect_slices(sums, levels):
    for level in levels:
        step = 1 << level
        kept = {}
        for offset in range(0, len(sums), 2 * step):
            arrived = flipped(sums[offset + step].astype(jnp.bfloat16), level)
            kept[offset] = sums[offset].astype(jnp.float32) + arrived.astype(jnp.float32)
        sums = [kept.get(offset) for offset in range(len(sums))]
    return sums


def body(
    inputs,
    segments,
    routes,
    cotangent,
    norm_gain,
    in_proj,
    conv_taps,
    conv_bias,
    x_proj,
    dt_proj,
    dt_bias,
    log_decay,
    skip_gain,
    out_proj,
    moe_gain,
    router,
    expert_in,
    expert_out,
):
    experts = router.shape[1]
    half_rows = norm_gain.shape[0]
    columns = (
        x_proj,
        dt_proj.T,
        conv_taps,
        conv_bias[:, None],
        dt_bias[:, None],
        log_decay,
        skip_gain[:, None],
        jnp.concatenate([norm_gain, moe_gain])[:, None],
        router.reshape(2 * half_rows, experts // 2),
    )
    widths = [part.shape[1] for part in columns]
    ends = [sum(widths[: k + 1]) for k in range(len(widths))]
    sizes = [(name, lax.axis_size(name)) for name in ("ctx", "exp")]
    tail_ids = segments[0, -EDGE:, None].astype(jnp.bfloat16)
    edge = jnp.concatenate([inputs[0, -EDGE:], jnp.broadcast_to(tail_ids, (EDGE, LANES))], axis=1)
    (full_in, full_out, full_small), prior = gather_all(
        sizes, (in_proj, out_proj, jnp.concatenate(columns, axis=1)), edge, 0
    )
    later_in, later_out, full_small = lax.optimization_barrier((expert_in[0], expert_out[0], full_small))
    weights_in = spread_slices(later_in)
    weights_out = spread_slices(later_out)
    full_xproj, full_dt, full_taps, full_bias, full_dtbias, full_decay, full_skip, gains, full_router = [
        full_small[:, end - width : end] for end, width in zip(ends, widths)
    ]
    full_dt = full_dt.T
    full_bias, full_dtbias, full_skip = full_bias[:, 0], full_dtbias[:, 0], full_skip[:, 0]
    gains = gains.reshape(-1, 2, half_rows)
    full_norm, full_moe = gains[:, 0].reshape(-1), gains[:, 1].reshape(-1)
    full_router = full_router.reshape(-1, experts)
    tokens_here = inputs.shape[1]
    capacity = 5 * tokens_here // (4 * experts)
    flat_in = inputs[0].astype(jnp.float32)
    seg_row = segments[0]
    position = lax.axis_index("ctx")
    norm_one_value, norm_one_pull = jax.vjp(rms_scale, flat_in, full_norm.astype(jnp.float32))
    normed_one = norm_one_value.astype(jnp.bfloat16)
    mixed_in = jnp.dot(normed_one, full_in, preferred_element_type=jnp.float32)
    conv_in = mixed_in[:, :DI].astype(jnp.bfloat16)
    gate_z = mixed_in[:, DI:]
    edge_one = rms_scale(prior[:, :D].astype(jnp.float32), full_norm.astype(jnp.float32)).astype(jnp.bfloat16)
    edge_rows = dot(edge_one, full_in[:, :DI])[EDGE - (KC - 1) :].astype(jnp.bfloat16)
    prior_ids = jnp.where(position > 0, prior[EDGE - (KC - 1) :, D].astype(jnp.int32), -1)
    ext_ids = jnp.concatenate([prior_ids, seg_row])
    ext_rows = jnp.concatenate([edge_rows, conv_in], axis=0).astype(jnp.float32)
    conv_out, conv_pull = jax.vjp(
        lambda rows_in, taps_in, bias_in: conv_local(rows_in, taps_in, bias_in, ext_ids),
        ext_rows,
        full_taps.astype(jnp.float32),
        full_bias.astype(jnp.float32),
    )
    silu_value, silu_pull = jax.vjp(jax.nn.silu, conv_out)
    xs_val = silu_value.astype(jnp.bfloat16)
    xs_wide = xs_val.astype(jnp.float32)
    projected = jnp.dot(xs_val, full_xproj, preferred_element_type=jnp.float32)
    delta_low = projected[:, :R].astype(jnp.bfloat16)
    b_rows = projected[:, R : R + NS]
    c_rows = projected[:, R + NS :]
    dt_pre = jnp.dot(delta_low, full_dt, preferred_element_type=jnp.float32) + full_dtbias.astype(
        jnp.float32
    )
    step_size = jax.nn.softplus(dt_pre)
    a_swap = -jnp.exp(full_decay.astype(jnp.float32)).T
    earlier = jnp.concatenate([prior_ids[KC - 2 :], seg_row[:-1]])
    keep_mask = (earlier == seg_row).astype(jnp.float32)
    masked_step = jnp.where(keep_mask[:, None] > 0, step_size, 1e30)
    push = step_size * xs_wide
    b_wide = jnp.broadcast_to(b_rows[:, :, None], (tokens_here, NS, LANES))
    c_wide = jnp.broadcast_to(c_rows[:, :, None], (tokens_here, NS, LANES))
    rates = a_swap * LOG2E
    block_end = scan_end(masked_step, push, b_wide, rates)
    block_product = jnp.exp2(jnp.sum(masked_step, axis=0)[None, :] * rates)
    gathered = lax.all_gather(
        jnp.stack([block_product, block_end]).astype(jnp.bfloat16)[None], "ctx", axis=0, tiled=True
    ).astype(jnp.float32)
    all_products, all_ends = gathered[:, 0], gathered[:, 1]
    zeros_state = jnp.zeros((NS, DI), jnp.float32)

    def fold_start(index_now, start_now):
        return jnp.where(
            index_now < position,
            all_products[index_now] * start_now + all_ends[index_now],
            start_now,
        )

    start_state = zeros_state
    for index_now in range(all_products.shape[0]):
        start_state = fold_start(index_now, start_state)
    scan_rows, kept, firsts = scan_out(masked_step, push, b_wide, c_wide, rates, start_state)
    skip_wide = full_skip.astype(jnp.float32)
    scanned_y = scan_rows + skip_wide * xs_wide
    gated_wide, gated_pull = jax.vjp(
        lambda scan_in, gate_in: scan_in * jax.nn.silu(gate_in), scanned_y, gate_z
    )
    gated = gated_wide.astype(jnp.bfloat16)
    mixed = jnp.dot(gated, full_out, preferred_element_type=jnp.float32)
    residual = flat_in + mixed
    norm_two_value, norm_two_pull = jax.vjp(rms_scale, residual, full_moe.astype(jnp.float32))
    normed_two = norm_two_value.astype(jnp.bfloat16)
    logits = jnp.dot(normed_two, full_router, preferred_element_type=jnp.float32)
    probability = jax.nn.softmax(logits, axis=-1)
    route_ids = routes[0, :, 0]
    one_hot = route_ids[:, None] == jnp.arange(experts, dtype=jnp.int32)[None, :]
    one_float = one_hot.astype(jnp.float32)
    gate_val = jnp.sum(probability * one_float, axis=1)
    running = jnp.cumsum(one_hot.astype(jnp.int32), axis=0)
    slot_index = jnp.sum(running * one_hot.astype(jnp.int32), axis=1) - 1
    room = -(-capacity // 16) * 16
    target = route_ids * room + slot_index
    grad_out = cotangent[0].astype(jnp.float32)
    grad_pick = (grad_out * gate_val[:, None]).astype(jnp.bfloat16)
    picked, grad_from_experts, grad_expert_in, grad_expert_out = run_experts(
        normed_two, grad_pick, target, weights_in, weights_out, experts, room, 2
    )
    picked = picked.astype(jnp.float32)
    grad_from_experts = grad_from_experts.astype(jnp.float32)
    outcome = residual + gate_val[:, None] * picked
    out_block = outcome.astype(jnp.bfloat16)[None]
    grad_gate = jnp.sum(grad_out * picked, axis=1)
    levels = lax.axis_size("ctx").bit_length() - 1
    grad_expert_in = collect_slices(grad_expert_in, range(1))
    grad_expert_out = collect_slices(grad_expert_out, range(1))
    grad_probs = grad_gate[:, None] * one_float
    grad_logits = (
        probability * (grad_probs - jnp.sum(grad_probs * probability, axis=1, keepdims=True))
    ).astype(jnp.bfloat16)
    grad_router = jnp.dot(normed_two.T, grad_logits, preferred_element_type=jnp.float32)
    grad_normed_two = grad_from_experts + jnp.dot(
        grad_logits, full_router.T, preferred_element_type=jnp.float32
    )
    grad_resid_norm, grad_moe_gain = norm_two_pull(grad_normed_two)
    grad_resid = grad_out + grad_resid_norm
    grad_mixed = grad_resid.astype(jnp.bfloat16)
    grad_gated = jnp.dot(grad_mixed, full_out.T, preferred_element_type=jnp.float32)
    grad_out_proj = jnp.dot(gated.T, grad_mixed, preferred_element_type=jnp.float32)
    grad_y, grad_z = gated_pull(grad_gated)
    grad_skip = jnp.sum(grad_y * xs_wide, axis=0)
    grad_y, grad_expert_in, grad_expert_out = lax.optimization_barrier(
        (grad_y, grad_expert_in, grad_expert_out)
    )
    local_inflow = scan_inflow(masked_step, grad_y, c_wide, rates)
    all_inflows = lax.all_gather(
        local_inflow[None].astype(jnp.bfloat16), "ctx", axis=0, tiled=True
    ).astype(jnp.float32)
    all_inflows, grad_expert_in, grad_expert_out = lax.optimization_barrier(
        (all_inflows, grad_expert_in, grad_expert_out)
    )
    grad_w_in = collect_slices(grad_expert_in, range(1, levels))[0]
    grad_w_out = collect_slices(grad_expert_out, range(1, levels))[0]
    total_ctx = all_inflows.shape[0]

    def fold_end(step_index, end_now):
        source = total_ctx - 1 - step_index
        return jnp.where(
            source > position, all_inflows[source] + all_products[source] * end_now, end_now
        )

    end_inflow = zeros_state
    for step_index in range(total_ctx):
        end_inflow = fold_end(step_index, end_inflow)
    along_b, slope, wide_b, wide_c, grad_a = scan_adjoint(
        masked_step, push, grad_y, b_wide, c_wide, kept, firsts, rates, end_inflow
    )
    along_b, slope, grad_w_in, grad_w_out = lax.optimization_barrier((along_b, slope, grad_w_in, grad_w_out))
    grad_step_all = along_b * xs_wide + slope * (1.0 / LOG2E)
    grad_xss = along_b * step_size
    grad_bs = jnp.sum(wide_b, axis=2)
    grad_cs = jnp.sum(wide_c, axis=2)
    grad_log_decay = (grad_a * a_swap).T
    soft_slope = jax.nn.sigmoid(dt_pre)
    grad_pre_wide = grad_step_all * soft_slope
    grad_dt_bias = jnp.sum(grad_pre_wide, axis=0)
    grad_dt_pre = grad_pre_wide.astype(jnp.bfloat16)
    grad_dt_proj = jnp.dot(delta_low.T, grad_dt_pre, preferred_element_type=jnp.float32)
    grad_delta = jnp.dot(grad_dt_pre, full_dt.T, preferred_element_type=jnp.float32)
    grad_projected = jnp.concatenate(
        [grad_delta, grad_bs, grad_cs], axis=1
    ).astype(jnp.bfloat16)
    grad_x_proj = jnp.dot(xs_val.T, grad_projected, preferred_element_type=jnp.float32)
    grad_xs_total = (
        skip_wide * grad_y
        + grad_xss
        + jnp.dot(grad_projected, full_xproj.T, preferred_element_type=jnp.float32)
    )
    grad_conv = silu_pull(grad_xs_total)[0]
    grad_ext, grad_taps, grad_cbias = conv_pull(grad_conv)
    from_next = shifted(grad_ext[: KC - 1], "ctx", -1)
    grad_conv_in = grad_ext[KC - 1 :] + jnp.concatenate(
        [jnp.zeros((tokens_here - (KC - 1), DI), jnp.float32), from_next], axis=0
    )
    grad_mixed_in = jnp.concatenate([grad_conv_in, grad_z], axis=1).astype(jnp.bfloat16)
    grad_normed_one = jnp.dot(grad_mixed_in, full_in.T, preferred_element_type=jnp.float32)
    grad_inputs_norm, grad_norm_gain = norm_one_pull(grad_normed_one)
    grad_inputs = grad_resid + grad_inputs_norm
    sums = (
        grad_x_proj,
        grad_dt_proj.T,
        grad_taps,
        grad_cbias[:, None],
        grad_dt_bias[:, None],
        grad_log_decay,
        grad_skip[:, None],
        jnp.stack(
            [grad_norm_gain.reshape(-1, half_rows), grad_moe_gain.reshape(-1, half_rows)], axis=1
        ).reshape(-1, 1),
        grad_router.reshape(-1, experts // 2),
    )

    grad_in_proj = dot(normed_one.T, grad_mixed_in)
    own_in, own_out, own_small = reduce_all(
        sizes,
        (
            grad_in_proj.astype(jnp.bfloat16),
            grad_out_proj.astype(jnp.bfloat16),
            jnp.concatenate(sums, axis=1).astype(jnp.bfloat16),
        ),
        1,
    )
    own_x, own_dt, own_taps, own_bias, own_dtbias, own_decay, own_skip, own_gains, own_router = [
        own_small[:, end - width : end] for end, width in zip(ends, widths)
    ]
    return (
        out_block,
        grad_inputs[None],
        own_gains[:half_rows, 0],
        own_in,
        own_taps,
        own_bias[:, 0],
        own_x,
        own_dt.T,
        own_dtbias[:, 0],
        own_decay,
        own_skip[:, 0],
        own_out,
        own_gains[half_rows:, 0],
        own_router.reshape(half_rows, experts),
        grad_w_in[None],
        grad_w_out[None],
    )


def solution(mesh):
    placed = (
        P("exp", "ctx", None),
        P("exp", "ctx"),
        P("exp", "ctx", None),
        P("exp", "ctx", None),
        P(("ctx", "exp")),
        P(("ctx", "exp"), None),
        P(("ctx", "exp"), None),
        P(("ctx", "exp")),
        P(("ctx", "exp"), None),
        P(None, ("ctx", "exp")),
        P(("ctx", "exp")),
        P(("ctx", "exp"), None),
        P(("ctx", "exp")),
        P(("ctx", "exp"), None),
        P(("ctx", "exp")),
        P(("ctx", "exp"), None),
        P("exp", None, "ctx"),
        P("exp", "ctx", None),
    )
    return jax.shard_map(
        body,
        mesh=mesh,
        in_specs=placed,
        out_specs=(
            P("exp", "ctx", None),
            P("exp", "ctx", None),
            P(("ctx", "exp")),
            P(("ctx", "exp"), None),
            P(("ctx", "exp"), None),
            P(("ctx", "exp")),
            P(("ctx", "exp"), None),
            P(None, ("ctx", "exp")),
            P(("ctx", "exp")),
            P(("ctx", "exp"), None),
            P(("ctx", "exp")),
            P(("ctx", "exp"), None),
            P(("ctx", "exp")),
            P(("ctx", "exp"), None),
            P("exp", None, "ctx"),
            P("exp", "ctx", None),
        ),
        check_vma=False,
    )
```

```python
import functools

import jax
import jax.numpy as jnp
from jax import lax
from jax.experimental import pallas as pl
from jax.experimental.pallas import tpu as pltpu
from jax.sharding import PartitionSpec as P

D = 768
DI = 1536
NS = 16
R = 48
KC = 4
LANES = 128
UNROLL = 8
LOG2E = 1.4426950408889634


EPS = 1e-05
MESH = pl.DeviceIdType.MESH
ROWS_AT_ONCE = 16
EDGE = 16

def tile(ref, base, lanes):
    return ref[pl.ds(pl.multiple_of(base, UNROLL), UNROLL), lanes]

def row(rows_now, place):
    return jnp.broadcast_to(rows_now[place : place + 1], (NS, LANES))

def put_row(rows_now, place, value):
    at = lax.broadcasted_iota(jnp.int32, (UNROLL, LANES), 0)
    value = jnp.broadcast_to(value, (UNROLL, LANES))
    return value if rows_now is None else jnp.where(at == place, value, rows_now)

def cost(tokens, channels, share):
    size = tokens * channels * NS
    return pl.CostEstimate(flops=size * share, transcendentals=size, bytes_accessed=size * share)


def pick(channels):
    return 512 if channels % 512 == 0 else 128


def shifted(value, axis, steps):
    count = lax.axis_size(axis)
    initial, last = (max(0, -steps), min(count, count - steps))
    return lax.ppermute(value, axis, [(source, source + steps) for source in range(initial, last)])


def rms_scale(values, gain):
    return values * lax.rsqrt(jnp.mean(values * values, axis=-1, keepdims=True) + EPS) * gain


def conv_local(ext_rows, taps, bias, ext_ids):
    length = ext_rows.shape[0] - (KC - 1)
    own_ids = ext_ids[KC - 1 :]
    result = jnp.zeros((length, ext_rows.shape[1]), jnp.float32) + bias[None, :]
    for offset in range(KC):
        same_doc = (ext_ids[offset : offset + length] == own_ids).astype(jnp.float32)
        result = (
            result
            + taps[:, offset][None, :] * ext_rows[offset : offset + length] * same_doc[:, None]
        )
    return result


def bit_positions(sizes):
    return [(axis, size.bit_length() - 2 - k) for axis, size in sizes for k in range(size.bit_length() - 1)]


def own_bit(place):
    axis, level = place
    return lax.rem(lax.axis_index(axis) // 2**level, 2)


def partner(place):
    axis, level = place
    where = {"ctx": lax.axis_index("ctx"), "exp": lax.axis_index("exp")}
    where[axis] = where[axis] + (1 - 2 * own_bit(place)) * 2**level
    return (where["ctx"], where["exp"])


def meet(places, *others):
    barrier = pltpu.get_barrier_semaphore()
    for device in [partner(place) for place in places] + list(others):
        pl.semaphore_signal(barrier, inc=1, device_id=device, device_id_type=MESH)
    pl.semaphore_wait(barrier, len(places) + len(others))


class GatherFlow:
    def __init__(self, places, streams, shards, wholes, send_sems, recv_sems, local_sems):
        self.places, self.streams, self.shards, self.wholes = places, streams, shards, wholes
        self.sems = send_sems, recv_sems, local_sems
        self.bits = [own_bit(place) for place in places]

    def view(self, number, have):
        array, cols, order = self.streams[number]
        index = tuple(slice(None) if p in have else self.bits[p] for p in range(len(self.places)))
        return self.wholes[array].at[index + (slice(None), cols)]

    def own(self, number):
        array, cols, order = self.streams[number]
        return pltpu.make_async_copy(
            self.shards[array].at[:, cols], self.view(number, ()), self.sems[2].at[number]
        )

    def flight(self, number, stage):
        array, cols, order = self.streams[number]
        target = self.view(number, order[:stage])
        return pltpu.make_async_remote_copy(
            src_ref=self.shards[array].at[:, cols] if stage == 0 else target,
            dst_ref=target,
            send_sem=self.sems[0].at[number, stage],
            recv_sem=self.sems[1].at[number, stage],
            device_id=partner(self.places[order[stage]]),
            device_id_type=MESH,
        )

    def start(self):
        for number in range(len(self.streams)):
            self.flight(number, 0).start()
        for number in range(len(self.streams)):
            self.own(number).start()

    def advance(self, stage):
        for number in range(len(self.streams)):
            if stage == 0:
                self.own(number).wait()
            self.flight(number, stage).wait_recv()
            if stage + 1 < len(self.places):
                self.flight(number, stage + 1).start()

    def finish(self):
        for number in range(len(self.streams)):
            for stage in range(len(self.places)):
                self.flight(number, stage).wait_send()


def gather_kernel(places, streams, count, *refs):
    shards, edge_ref, wholes, prior_ref = refs[:count], refs[count], refs[count + 1 : 2 * count + 1], refs[2 * count + 1]
    send_sems, recv_sems, local_sems, edge_sems = refs[2 * count + 2 :]
    flow = GatherFlow(places, streams, shards, wholes, send_sems, recv_sems, local_sems)
    blocks = lax.axis_size("ctx")
    here, line = lax.axis_index("ctx"), lax.axis_index("exp")
    meet(places, (lax.rem(here + 1, blocks), line), (lax.rem(here + blocks - 1, blocks), line))
    flow.start()
    edge = pltpu.make_async_remote_copy(
        src_ref=edge_ref,
        dst_ref=prior_ref,
        send_sem=edge_sems.at[0],
        recv_sem=edge_sems.at[1],
        device_id=(lax.rem(here + 1, blocks), line),
        device_id_type=MESH,
    )
    edge.start()
    for stage in range(len(places)):
        flow.advance(stage)
    flow.finish()
    edge.wait()


def orders_of(places):
    core = places.index(("ctx", 0))
    rows = [k for k, place in enumerate(places) if place[0] == "ctx" and place[1] > 0]
    near = places.index(("exp", 0))
    far = [k for k, place in sorted(enumerate(places), key=lambda item: item[1][1]) if place[0] == "exp" and place[1] > 0]
    return [core] + rows + [near] + far, [core, near] + rows + far


def streams_of(places, arrays, gathering):
    first, second = [tuple(reversed(order)) if gathering else tuple(order) for order in orders_of(places)]
    streams = []
    for array, values in enumerate(arrays):
        width = values.shape[1]
        if width % 256 == 0:
            streams.append((array, slice(0, width // 2), first))
            streams.append((array, slice(width // 2, width), second))
        else:
            streams.append((array, slice(0, width), first if array % 2 else second))
    return streams


def gather_all(sizes, shards, edge, identity):
    places = bit_positions(sizes)
    streams = streams_of(places, shards, True)
    stages = len(places)
    anywhere = pl.BlockSpec(memory_space=pl.ANY)
    *wholes, prior = pl.pallas_call(
        functools.partial(gather_kernel, places, streams, len(shards)),
        in_specs=[anywhere] * (len(shards) + 1),
        out_specs=[anywhere] * (len(shards) + 1),
        out_shape=[jax.ShapeDtypeStruct((2,) * stages + shard.shape, shard.dtype) for shard in shards]
        + [jax.ShapeDtypeStruct(edge.shape, edge.dtype)],
        scratch_shapes=[
            pltpu.SemaphoreType.DMA((len(streams), stages)),
            pltpu.SemaphoreType.DMA((len(streams), stages)),
            pltpu.SemaphoreType.DMA((len(streams),)),
            pltpu.SemaphoreType.DMA((2,)),
        ],
        compiler_params=pltpu.CompilerParams(collective_id=identity, has_side_effects=True),
        name="gather_all",
    )(*shards, edge)
    return [whole.reshape((-1,) + whole.shape[stages + 1 :]) for whole in wholes], prior


class ReduceFlow:
    def __init__(self, places, streams, parts, totals, landing, send_sems, recv_sems):
        self.places, self.streams, self.parts, self.totals = places, streams, parts, totals
        self.landing, self.sems = landing, (send_sems, recv_sems)
        self.bits = [own_bit(place) for place in places]

    def spot(self, number, stage):
        return self.landing[number * len(self.places) + stage]

    def side(self, number, stage, value):
        array, cols, order = self.streams[number]
        left = [p for p in range(len(self.places)) if p not in order[:stage]]
        index = tuple(value if p == order[stage] else slice(None) for p in left)
        if stage == 0:
            return self.parts[array].at[index + (slice(None), cols)]
        return self.spot(number, stage - 1).at[index]

    def flight(self, number, stage):
        order = self.streams[number][2]
        return pltpu.make_async_remote_copy(
            src_ref=self.side(number, stage, 1 - self.bits[order[stage]]),
            dst_ref=self.spot(number, stage),
            send_sem=self.sems[0].at[number, stage],
            recv_sem=self.sems[1].at[number, stage],
            device_id=partner(self.places[order[stage]]),
            device_id_type=MESH,
        )

    def start(self):
        for number in range(len(self.streams)):
            self.flight(number, 0).start()

    def advance(self, stage):
        stages = len(self.places)
        for number, (array, cols, order) in enumerate(self.streams):
            self.flight(number, stage).wait_recv()
            mine = self.side(number, stage, self.bits[order[stage]])
            there = self.spot(number, stage)
            if stage + 1 == stages:
                self.totals[array][:, cols] = there[...].astype(jnp.float32) + mine[...].astype(jnp.float32)
                continue
            depth = stages - stage - 1

            def add(index, unused, there=there, mine=mine, depth=depth):
                at = tuple(lax.rem(index // 2 ** (depth - 1 - k), 2) for k in range(depth))
                there[at] = (there[at].astype(jnp.float32) + mine[at].astype(jnp.float32)).astype(there.dtype)
                return unused

            lax.fori_loop(0, 2**depth, add, 0)
            self.flight(number, stage + 1).start()

    def finish(self):
        for number in range(len(self.streams)):
            for stage in range(len(self.places)):
                self.flight(number, stage).wait_send()


def reduce_kernel(places, streams, count, *refs):
    parts, totals = refs[:count], refs[count : 2 * count]
    landing = refs[2 * count : 2 * count + len(streams) * len(places)]
    send_sems, recv_sems = refs[2 * count + len(streams) * len(places) :]
    flow = ReduceFlow(places, streams, parts, totals, landing, send_sems, recv_sems)
    meet(places)
    flow.start()
    for stage in range(len(places)):
        flow.advance(stage)
    flow.finish()


def landing_of(places, streams, divided):
    stages = len(places)
    landing = []
    for array, cols, order in streams:
        for stage in range(stages):
            rows = divided[array].shape[-2]
            landing.append(pltpu.VMEM((2,) * (stages - stage - 1) + (rows, cols.stop - cols.start), jnp.bfloat16))
    return landing


def reduce_all(sizes, parts, identity):
    places = bit_positions(sizes)
    stages = len(places)
    streams = streams_of(places, parts, False)
    divided = [part.reshape((2,) * stages + (-1, part.shape[1])) for part in parts]
    inside = pl.BlockSpec(memory_space=pltpu.VMEM)
    return pl.pallas_call(
        functools.partial(reduce_kernel, places, streams, len(parts)),
        in_specs=[inside] * len(parts),
        out_specs=[inside] * len(parts),
        out_shape=[jax.ShapeDtypeStruct(block.shape[-2:], jnp.float32) for block in divided],
        scratch_shapes=landing_of(places, streams, divided)
        + [
            pltpu.SemaphoreType.DMA((len(streams), stages)),
            pltpu.SemaphoreType.DMA((len(streams), stages)),
        ],
        compiler_params=pltpu.CompilerParams(
            collective_id=identity, has_side_effects=True, vmem_limit_bytes=48 * 1024 * 1024
        ),
        name="reduce_all",
    )(*divided)


def dot(left, right):
    return jnp.dot(left, right, preferred_element_type=jnp.float32)


def contract(left, right, left_dim, right_dim):
    return lax.dot_general(left, right, (((left_dim,), (right_dim,)), ((), ())), preferred_element_type=jnp.float32)


def lanes_of(group, width, k):
    return pl.ds(pl.multiple_of(group * width + k * LANES, LANES), LANES)


def spread_columns(source_ref, wide_ref):
    def chunk(index, unused):
        base = pl.multiple_of(index * LANES, LANES)
        now = source_ref[:, pl.ds(base, LANES)]
        for place in range(LANES):
            wide_ref[base + place] = jnp.broadcast_to(now[:, place : place + 1], (NS, LANES))
        return unused

    lax.fori_loop(0, source_ref.shape[1] // LANES, chunk, 0)


def end_pass(width, step_ref, push_ref, wide_b, rate_ref, state_ref, hook):
    rows, channels = step_ref.shape
    count = width // LANES

    def group_body(group, unused):
        pieces = [lanes_of(group, width, k) for k in range(count)]
        rates = [rate_ref[:, lanes] for lanes in pieces]

        def block(index, states):
            states = list(states)
            steps = [tile(step_ref, index * UNROLL, lanes) for lanes in pieces]
            pushes = [tile(push_ref, index * UNROLL, lanes) for lanes in pieces]
            for place in range(UNROLL):
                b_now = wide_b[index * UNROLL + place]
                for k in range(count):
                    decay = jnp.exp2(row(steps[k], place) * rates[k])
                    states[k] = decay * states[k] + b_now * row(pushes[k], place)
            return tuple(states)

        zero = jnp.zeros((NS, LANES), jnp.float32)
        states = lax.fori_loop(0, rows // UNROLL, block, (zero,) * count)
        for k, lanes in enumerate(pieces):
            state_ref[:, lanes] = states[k]
        hook(group)
        return unused

    lax.fori_loop(0, channels // width, group_body, 0)


def out_pass(width, step_ref, push_ref, wide_b, wide_c, rate_ref, state_ref, y_ref, kept_buf, kept_copy, hook):
    rows, channels = step_ref.shape
    count = width // LANES
    span = kept_buf.shape[1]
    blocks = rows // span

    def time_body(number, unused):
        slot = lax.rem(number, 2)

        @pl.when(number >= 2)
        def _():
            kept_copy(number - 2, slot).wait()

        def group_body(group, unused_inner):
            pieces = [lanes_of(group, width, k) for k in range(count)]
            rates = [rate_ref[:, lanes] for lanes in pieces]

            def block(index, states):
                states = list(states)
                base = number * span + index * UNROLL
                steps = [tile(step_ref, base, lanes) for lanes in pieces]
                pushes = [tile(push_ref, base, lanes) for lanes in pieces]
                outs = [None] * count
                for place in range(UNROLL):
                    b_now = wide_b[base + place]
                    c_now = wide_c[base + place]
                    for k, lanes in enumerate(pieces):
                        decay = jnp.exp2(row(steps[k], place) * rates[k])
                        states[k] = decay * states[k] + b_now * row(pushes[k], place)
                        kept_buf[slot, index * UNROLL + place, :, lanes] = states[k].astype(kept_buf.dtype)
                        outs[k] = put_row(outs[k], place, jnp.sum(states[k] * c_now, axis=0, keepdims=True))
                for k, lanes in enumerate(pieces):
                    y_ref[pl.ds(pl.multiple_of(base, UNROLL), UNROLL), lanes] = outs[k]
                return tuple(states)

            states = lax.fori_loop(0, span // UNROLL, block, tuple(state_ref[:, lanes] for lanes in pieces))
            for k, lanes in enumerate(pieces):
                state_ref[:, lanes] = states[k]
            return unused_inner

        lax.fori_loop(0, channels // width, group_body, 0)
        kept_copy(number, slot).start()
        hook(number)
        return unused

    lax.fori_loop(0, blocks, time_body, 0)
    for number in range(max(0, blocks - 2), blocks):
        kept_copy(number, number % 2).wait()


def inflow_pass(width, step_ref, grad_ref, wide_c, rate_ref, flow_ref, hook):
    rows, channels = step_ref.shape
    count = width // LANES

    def group_body(group, unused):
        pieces = [lanes_of(group, width, k) for k in range(count)]
        rates = [rate_ref[:, lanes] for lanes in pieces]

        def block(index, flows):
            flows = list(flows)
            base = rows - UNROLL - index * UNROLL
            steps = [tile(step_ref, base, lanes) for lanes in pieces]
            grads = [tile(grad_ref, base, lanes) for lanes in pieces]
            for place in reversed(range(UNROLL)):
                c_now = wide_c[base + place]
                for k in range(count):
                    decay = jnp.exp2(row(steps[k], place) * rates[k])
                    flows[k] = decay * (c_now * row(grads[k], place) + flows[k])
            return tuple(flows)

        zero = jnp.zeros((NS, LANES), jnp.float32)
        flows = lax.fori_loop(0, rows // UNROLL, block, (zero,) * count)
        for k, lanes in enumerate(pieces):
            flow_ref[:, lanes] = flows[k]
        hook(group)
        return unused

    lax.fori_loop(0, channels // width, group_body, 0)


def lane_sums(part_ref):
    values = part_ref[...].reshape(-1, LANES)
    high = values.astype(jnp.bfloat16)
    low = (values - high.astype(jnp.float32)).astype(jnp.bfloat16)
    ones = jnp.ones((UNROLL, LANES), jnp.bfloat16)
    return contract(ones, high, 1, 1) + contract(ones, low, 1, 1)


def adjoint_pass(width, step_ref, push_ref, grad_ref, wide_b, wide_c, rate_ref, flow_ref, kept_buf, kept_copy,
                 along_ref, slope_ref, gb_ref, gc_ref, ga_ref, part_b, part_c, hook):
    rows, channels = step_ref.shape
    count = width // LANES
    span = kept_buf.shape[1] - 1
    blocks = rows // span
    ga_ref[...] = jnp.zeros_like(ga_ref)

    def time_body(order, unused):
        slot = lax.rem(order, 2)
        number = blocks - 1 - order
        kept_copy(number, slot).wait()
        part_b[...] = jnp.zeros_like(part_b)
        part_c[...] = jnp.zeros_like(part_c)

        def group_body(group, unused_inner):
            pieces = [lanes_of(group, width, k) for k in range(count)]
            rates = [rate_ref[:, lanes] for lanes in pieces]

            def block(index, carried):
                flows = list(carried[:count])
                sums = list(carried[count : 2 * count])
                current = list(carried[2 * count :])
                local = span - UNROLL - index * UNROLL
                base = number * span + local
                steps = [tile(step_ref, base, lanes) for lanes in pieces]
                pushes = [tile(push_ref, base, lanes) for lanes in pieces]
                grads = [tile(grad_ref, base, lanes) for lanes in pieces]
                alongs = [None] * count
                slopes = [None] * count
                for place in reversed(range(UNROLL)):
                    b_now = wide_b[base + place]
                    c_now = wide_c[base + place]
                    gb = gc = None
                    for k, lanes in enumerate(pieces):
                        prior = kept_buf[slot, local + place, :, lanes].astype(jnp.float32)
                        step = row(steps[k], place)
                        grad = row(grads[k], place)
                        decay = jnp.exp2(step * rates[k])
                        adjoint = c_now * grad + flows[k]
                        flows[k] = decay * adjoint
                        decay_grad = flows[k] * prior
                        alongs[k] = put_row(alongs[k], place, jnp.sum(adjoint * b_now, axis=0, keepdims=True))
                        slopes[k] = put_row(slopes[k], place, jnp.sum(decay_grad * rates[k], axis=0, keepdims=True))
                        sums[k] = sums[k] + decay_grad * step
                        here_b = adjoint * row(pushes[k], place)
                        here_c = current[k] * grad
                        gb = here_b if gb is None else gb + here_b
                        gc = here_c if gc is None else gc + here_c
                        current[k] = prior
                    part_b[local + place] += gb
                    part_c[local + place] += gc
                where = pl.ds(pl.multiple_of(base, UNROLL), UNROLL)
                for k, lanes in enumerate(pieces):
                    along_ref[where, lanes] = alongs[k]
                    slope_ref[where, lanes] = slopes[k]
                return tuple(flows + sums + current)

            carried = lax.fori_loop(
                0,
                span // UNROLL,
                block,
                tuple(flow_ref[:, lanes] for lanes in pieces)
                + tuple(ga_ref[:, lanes] for lanes in pieces)
                + tuple(kept_buf[slot, span, :, lanes].astype(jnp.float32) for lanes in pieces),
            )
            for k, lanes in enumerate(pieces):
                flow_ref[:, lanes] = carried[k]
                ga_ref[:, lanes] = carried[count + k]
            return unused_inner

        lax.fori_loop(0, channels // width, group_body, 0)
        gb_ref[number] = lane_sums(part_b)
        gc_ref[number] = lane_sums(part_c)

        @pl.when(order + 2 < blocks)
        def _():
            kept_copy(number - 2, slot).start()

        hook(order)
        return unused

    lax.fori_loop(0, blocks, time_body, 0)


def share(source, target, send_sems, recv_sems):
    blocks = lax.axis_size("ctx")
    here, line = lax.axis_index("ctx"), lax.axis_index("exp")
    copies = []
    for step in range(1, blocks):
        copies.append(
            pltpu.make_async_remote_copy(
                src_ref=source,
                dst_ref=target.at[here],
                send_sem=send_sems.at[step],
                recv_sem=recv_sems.at[step],
                device_id=(lax.rem(here + step, blocks), line),
                device_id_type=MESH,
            )
        )
        copies[-1].start()
    target[here] = source[...]
    return copies


def row_peers():
    blocks = lax.axis_size("ctx")
    here, line = lax.axis_index("ctx"), lax.axis_index("exp")
    return [(lax.rem(here + step, blocks), line) for step in range(1, blocks)]


def forward_kernel(places, streams, width, *refs):
    step_ref, push_ref, bt_ref, ct_ref, rate_ref = refs[:5]
    shards = refs[5:7]
    y_ref, start_ref, product_ref, kept_ref = refs[7:11]
    wholes = refs[11:13]
    (wide_b, wide_c, kept_buf, first_buf, state_ref, message, products, ends,
     kept_sems, first_sem, share_sems, send_sems, recv_sems, local_sems) = refs[13:]
    blocks = lax.axis_size("ctx")
    position = lax.axis_index("ctx")
    span = kept_buf.shape[1]
    flow = GatherFlow(places, streams, shards, wholes, send_sems, recv_sems, local_sems)
    meet([place for place in places if place[0] == "exp"], *row_peers())
    flow.start()

    message[0] = jnp.exp2(jnp.sum(step_ref[...], axis=0, keepdims=True) * rate_ref[...]).astype(jnp.bfloat16)
    early = share(message.at[0], products, share_sems.at[0], share_sems.at[1])
    spread_columns(bt_ref, wide_b)
    spread_columns(ct_ref, wide_c)

    def first_hook(group):
        @pl.when(group == 1)
        def _():
            flow.advance(0)

    end_pass(width, step_ref, push_ref, wide_b, rate_ref, state_ref, first_hook)
    message[1] = state_ref[...].astype(jnp.bfloat16)
    late = share(message.at[1], ends, share_sems.at[2], share_sems.at[3])
    for copy in early + late:
        copy.wait_recv()
    start = jnp.zeros(state_ref.shape, jnp.float32)
    for index in range(blocks):
        folded = products[index].astype(jnp.float32) * start + ends[index].astype(jnp.float32)
        start = jnp.where(index < position, folded, start)
    state_ref[...] = start
    start_ref[...] = start
    product_ref[...] = products[...]
    first_buf[0] = start.astype(jnp.bfloat16)
    first_copy = pltpu.make_async_copy(first_buf, kept_ref.at[pl.ds(0, 1)], first_sem)
    first_copy.start()
    flow.advance(1)

    def kept_copy(number, slot):
        return pltpu.make_async_copy(
            kept_buf.at[slot], kept_ref.at[pl.ds(1 + number * span, span)], kept_sems.at[slot]
        )

    def second_hook(number):
        @pl.when(number == 1)
        def _():
            flow.advance(2)

    out_pass(width, step_ref, push_ref, wide_b, wide_c, rate_ref, state_ref, y_ref, kept_buf, kept_copy, second_hook)
    for stage in range(3, len(places)):
        flow.advance(stage)
    flow.finish()
    first_copy.wait()
    for copy in early + late:
        copy.wait_send()


def scan_forward(sizes, step, push, b_turned, c_turned, rates, shards, identity, span=64):
    places = bit_positions(sizes)
    streams = streams_of(places, shards, True)
    stages = len(places)
    tokens, channels = step.shape
    blocks = sizes[0][1]
    inside = pl.BlockSpec(memory_space=pltpu.VMEM)
    anywhere = pl.BlockSpec(memory_space=pl.ANY)
    half = jnp.bfloat16
    y, start, products, kept, *wholes = pl.pallas_call(
        functools.partial(forward_kernel, places, streams, pick(channels)),
        in_specs=[inside] * 5 + [anywhere] * 2,
        out_specs=[inside] * 3 + [anywhere] * 3,
        out_shape=[
            jax.ShapeDtypeStruct((tokens, channels), jnp.float32),
            jax.ShapeDtypeStruct((NS, channels), jnp.float32),
            jax.ShapeDtypeStruct((blocks, NS, channels), half),
            jax.ShapeDtypeStruct((tokens + 1, NS, channels), half),
        ]
        + [jax.ShapeDtypeStruct((2,) * stages + shard.shape, shard.dtype) for shard in shards],
        scratch_shapes=[
            pltpu.VMEM((tokens, NS, LANES), jnp.float32),
            pltpu.VMEM((tokens, NS, LANES), jnp.float32),
            pltpu.VMEM((2, span, NS, channels), half),
            pltpu.VMEM((1, NS, channels), half),
            pltpu.VMEM((NS, channels), jnp.float32),
            pltpu.VMEM((2, NS, channels), half),
            pltpu.VMEM((blocks, NS, channels), half),
            pltpu.VMEM((blocks, NS, channels), half),
            pltpu.SemaphoreType.DMA((2,)),
            pltpu.SemaphoreType.DMA,
            pltpu.SemaphoreType.DMA((4, blocks)),
            pltpu.SemaphoreType.DMA((len(streams), stages)),
            pltpu.SemaphoreType.DMA((len(streams), stages)),
            pltpu.SemaphoreType.DMA((len(streams),)),
        ],
        compiler_params=pltpu.CompilerParams(
            collective_id=identity, has_side_effects=True, vmem_limit_bytes=48 * 1024 * 1024
        ),
        cost_estimate=cost(tokens, channels, 9),
        name="scan_forward",
    )(step, push, b_turned, c_turned, rates, *shards)
    return y, start, products, kept, [whole.reshape((-1,) + whole.shape[stages + 1 :]) for whole in wholes]


def backward_kernel(places, streams, width, moved, *refs):
    step_ref, push_ref, grad_ref, bt_ref, ct_ref, rate_ref, product_ref = refs[:7]
    parts = refs[7:9]
    kept_ref = refs[9]
    leaving = refs[10 : 10 + moved]
    outs = refs[10 + moved :]
    along_ref, slope_ref, gb_ref, gc_ref, ga_ref = outs[:5]
    totals = outs[5:7]
    arriving = outs[7 : 7 + moved]
    scratch = outs[7 + moved :]
    landing = scratch[: len(streams) * len(places)]
    (wide_b, wide_c, part_b, part_c, kept_buf, flow_ref, message, inflows,
     kept_sems, share_sems, moved_sems, send_sems, recv_sems) = scratch[len(streams) * len(places) :]
    blocks = lax.axis_size("ctx")
    position = lax.axis_index("ctx")
    span = kept_buf.shape[1] - 1
    steps = step_ref.shape[0] // span
    flow = ReduceFlow(places, streams, parts, totals, landing, send_sems, recv_sems)

    def kept_copy(number, slot):
        return pltpu.make_async_copy(
            kept_ref.at[pl.ds(number * span, span + 1)], kept_buf.at[slot], kept_sems.at[slot]
        )

    for order in range(min(2, steps)):
        kept_copy(steps - 1 - order, order).start()
    meet([place for place in places if place[0] == "exp"], *row_peers())
    flow.start()
    spread_columns(bt_ref, wide_b)
    spread_columns(ct_ref, wide_c)
    inflow_pass(width, step_ref, grad_ref, wide_c, rate_ref, flow_ref, lambda group: None)
    message[...] = flow_ref[...].astype(jnp.bfloat16)
    copies = share(message, inflows, share_sems.at[0], share_sems.at[1])
    for copy in copies:
        copy.wait_recv()
    end = jnp.zeros(flow_ref.shape, jnp.float32)
    for index in reversed(range(blocks)):
        folded = inflows[index].astype(jnp.float32) + product_ref[index].astype(jnp.float32) * end
        end = jnp.where(index > position, folded, end)
    flow_ref[...] = end
    flow.advance(0)
    last = ("ctx", blocks.bit_length() - 2)
    moves = []
    for k in range(moved):
        moves.append(
            pltpu.make_async_remote_copy(
                src_ref=leaving[k],
                dst_ref=arriving[k],
                send_sem=moved_sems.at[0, k],
                recv_sem=moved_sems.at[1, k],
                device_id=partner(last),
                device_id_type=MESH,
            )
        )
        moves[-1].start()

    def hook(order):
        @pl.when(order == 2)
        def _():
            flow.advance(1)

        @pl.when(order == 4)
        def _():
            flow.advance(2)

    adjoint_pass(width, step_ref, push_ref, grad_ref, wide_b, wide_c, rate_ref, flow_ref, kept_buf, kept_copy,
                 along_ref, slope_ref, gb_ref, gc_ref, ga_ref, part_b, part_c, hook)
    for stage in range(3, len(places)):
        flow.advance(stage)
    flow.finish()
    for copy in copies:
        copy.wait_send()
    for move in moves:
        move.wait()


def scan_backward(sizes, step, push, grad, b_turned, c_turned, rates, products, parts, kept, leaving, identity, span=64):
    places = bit_positions(sizes)
    stages = len(places)
    streams = streams_of(places, parts, False)
    divided = [part.reshape((2,) * stages + (-1, part.shape[1])) for part in parts]
    tokens, channels = step.shape
    blocks = sizes[0][1]
    inside = pl.BlockSpec(memory_space=pltpu.VMEM)
    anywhere = pl.BlockSpec(memory_space=pl.ANY)
    half = jnp.bfloat16
    moved = len(leaving)
    row_sums = jax.ShapeDtypeStruct((tokens // span, UNROLL, span * NS), jnp.float32)
    out = pl.pallas_call(
        functools.partial(backward_kernel, places, streams, pick(channels), moved),
        in_specs=[inside] * 9 + [anywhere] * (1 + moved),
        out_specs=[inside] * 7 + [anywhere] * moved,
        out_shape=[jax.ShapeDtypeStruct((tokens, channels), jnp.float32)] * 2
        + [row_sums, row_sums, jax.ShapeDtypeStruct((NS, channels), jnp.float32)]
        + [jax.ShapeDtypeStruct(block.shape[-2:], jnp.float32) for block in divided]
        + [jax.ShapeDtypeStruct(value.shape, value.dtype) for value in leaving],
        scratch_shapes=landing_of(places, streams, divided)
        + [
            pltpu.VMEM((tokens, NS, LANES), jnp.float32),
            pltpu.VMEM((tokens, NS, LANES), jnp.float32),
            pltpu.VMEM((span, NS, LANES), jnp.float32),
            pltpu.VMEM((span, NS, LANES), jnp.float32),
            pltpu.VMEM((2, span + 1, NS, channels), half),
            pltpu.VMEM((NS, channels), jnp.float32),
            pltpu.VMEM((NS, channels), half),
            pltpu.VMEM((blocks, NS, channels), half),
            pltpu.SemaphoreType.DMA((2,)),
            pltpu.SemaphoreType.DMA((2, blocks)),
            pltpu.SemaphoreType.DMA((2, max(1, moved))),
            pltpu.SemaphoreType.DMA((len(streams), stages)),
            pltpu.SemaphoreType.DMA((len(streams), stages)),
        ],
        compiler_params=pltpu.CompilerParams(
            collective_id=identity, has_side_effects=True, vmem_limit_bytes=56 * 1024 * 1024
        ),
        cost_estimate=cost(tokens, channels, 15),
        name="scan_backward",
    )(step, push, grad, b_turned, c_turned, rates, products, *divided, kept, *leaving)
    along, slope, wide_b, wide_c, grad_a = out[:5]
    grad_bs, grad_cs = [values[:, 0].reshape(tokens, NS) for values in (wide_b, wide_c)]
    return along, slope, grad_bs, grad_cs, grad_a, out[5:7], list(out[7:])


def expert_kernel(slices, *refs):
    tokens_ref, grads_ref, column_ref, row_ref = refs[:4]
    weights_in, weights_out = refs[4 : 4 + slices], refs[4 + slices : 4 + 2 * slices]
    outs = refs[4 + 2 * slices :]
    picked_ref, back_ref = outs[:2]
    sums_in, sums_out = outs[2 : 2 + slices], outs[2 + slices : 2 + 2 * slices]
    (sent, got, answer, returned, w_in, w_out, hidden, total, active, slope, inner,
     send_sems, recv_sems, weight_sems, sum_sems) = outs[2 + 2 * slices :]
    experts, room, width = sent.shape[1:]
    places = experts * room
    me = lax.axis_index("exp")
    here = lax.axis_index("ctx")

    loads = []
    for s in range(slices):
        loads.append(pltpu.make_async_copy(weights_in[s], w_in.at[s], weight_sems.at[0, s]))
        loads.append(pltpu.make_async_copy(weights_out[s], w_out.at[s], weight_sems.at[1, s]))
    for load in loads:
        load.start()

    barrier = pltpu.get_barrier_semaphore()
    for step in range(1, experts):
        pl.semaphore_signal(barrier, inc=1, device_id=(here, lax.rem(me + step, experts)), device_id_type=MESH)
    pl.semaphore_wait(barrier, experts - 1)

    def exchange(source, target, kind):
        copies = []
        for step in range(1, experts):
            peer = lax.rem(me + step, experts)
            copy = pltpu.make_async_remote_copy(
                src_ref=source.at[peer],
                dst_ref=target.at[me],
                send_sem=send_sems.at[kind, step],
                recv_sem=recv_sems.at[kind, step],
                device_id=(here, peer),
                device_id_type=MESH,
            )
            copy.start()
            copies.append(copy)
        target[me] = source[me]
        return copies

    def arrive(copies):
        for copy in copies:
            copy.wait_recv()

    chooser = (lax.broadcasted_iota(jnp.int32, (places, row_ref.shape[1]), 0) == row_ref[...]).astype(jnp.float32).astype(jnp.bfloat16)
    sent[0] = dot(chooser, tokens_ref[...]).astype(jnp.bfloat16).reshape(experts, room, width)
    first = exchange(sent.at[0], got.at[0], 0)
    sent[1] = dot(chooser, grads_ref[...]).astype(jnp.bfloat16).reshape(experts, room, width)
    second = exchange(sent.at[1], got.at[1], 1)

    for load in loads:
        load.wait()
    arrive(first)
    rows = got[0].reshape(places, width)
    for s in range(slices):
        hidden[...] = dot(rows, w_in[s])

        def curve(index, unused):
            at = pl.ds(pl.multiple_of(index * ROWS_AT_ONCE, ROWS_AT_ONCE), ROWS_AT_ONCE)
            value = hidden[at, :]
            bell = 0.5 + 0.5 * lax.erf(value * 0.7071067811865476)
            active[s, at, :] = (value * bell).astype(jnp.bfloat16)
            slope[s, at, :] = bell + value * (jnp.exp(-0.5 * value * value) * 0.3989422804014327)
            return unused

        lax.fori_loop(0, places // ROWS_AT_ONCE, curve, 0)
        product = dot(active[s], w_out[s])
        total[...] = product if s == 0 else total[...] + product
    answer[0] = total[...].astype(jnp.bfloat16).reshape(experts, room, width)
    third = exchange(answer.at[0], returned.at[0], 2)

    arrive(second)
    pulled = got[1].reshape(places, width)
    for s in range(slices):
        inner[s] = (contract(pulled, w_out[s], 1, 1) * slope[s]).astype(jnp.bfloat16)
        product = contract(inner[s], w_in[s], 1, 1)
        total[...] = product if s == 0 else total[...] + product
    answer[1] = total[...].astype(jnp.bfloat16).reshape(experts, room, width)
    fourth = exchange(answer.at[1], returned.at[1], 3)

    stores = []
    for s in range(slices):
        w_out[s] = contract(active[s], pulled, 0, 0).astype(jnp.bfloat16)
        stores.append(pltpu.make_async_copy(w_out.at[s], sums_out[s], sum_sems.at[0, s]))
        stores[-1].start()
        w_in[s] = contract(rows, inner[s], 0, 0).astype(jnp.bfloat16)
        stores.append(pltpu.make_async_copy(w_in.at[s], sums_in[s], sum_sems.at[1, s]))
        stores[-1].start()

    finder = (lax.broadcasted_iota(jnp.int32, (column_ref.shape[0], places), 1) == column_ref[...]).astype(jnp.float32).astype(jnp.bfloat16)
    arrive(third)
    picked_ref[...] = dot(finder, returned[0].reshape(places, width)).astype(jnp.bfloat16)
    arrive(fourth)
    back_ref[...] = dot(finder, returned[1].reshape(places, width)).astype(jnp.bfloat16)
    for store in stores:
        store.wait()
    for copies in (first, second, third, fourth):
        for copy in copies:
            copy.wait_send()


def run_experts(rows, grads, target, weights_in, weights_out, experts, room, identity):
    slices = len(weights_in)
    tokens, width = rows.shape
    inner_width = weights_in[0].shape[1]
    places = experts * room
    inside = pl.BlockSpec(memory_space=pltpu.VMEM)
    anywhere = pl.BlockSpec(memory_space=pl.ANY)
    half = jnp.bfloat16
    out = pl.pallas_call(
        functools.partial(expert_kernel, slices),
        in_specs=[inside] * 4 + [anywhere] * (2 * slices),
        out_specs=[inside] * 2 + [anywhere] * (2 * slices),
        out_shape=[jax.ShapeDtypeStruct(rows.shape, half)] * 2
        + [jax.ShapeDtypeStruct(weight.shape, half) for weight in weights_in + weights_out],
        scratch_shapes=[pltpu.VMEM((2, experts, room, width), half)] * 4
        + [
            pltpu.VMEM((slices, width, inner_width), half),
            pltpu.VMEM((slices, inner_width, width), half),
            pltpu.VMEM((places, inner_width), jnp.float32),
            pltpu.VMEM((places, width), jnp.float32),
            pltpu.VMEM((slices, places, inner_width), half),
            pltpu.VMEM((slices, places, inner_width), jnp.float32),
            pltpu.VMEM((slices, places, inner_width), half),
            pltpu.SemaphoreType.DMA((4, experts)),
            pltpu.SemaphoreType.DMA((4, experts)),
            pltpu.SemaphoreType.DMA((2, slices)),
            pltpu.SemaphoreType.DMA((2, slices)),
        ],
        compiler_params=pltpu.CompilerParams(
            collective_id=identity, has_side_effects=True, vmem_limit_bytes=52 * 1024 * 1024
        ),
        name="run_experts",
    )(rows, grads, target[:, None], target[None, :], *weights_in, *weights_out)
    return out[0], out[1], list(out[2 : 2 + slices]), list(out[2 + slices :])


def flipped(value, level):
    count = lax.axis_size("ctx")
    return lax.ppermute(value, "ctx", [(source, source ^ (1 << level)) for source in range(count)])


def spread_slices(own):
    levels = lax.axis_size("ctx").bit_length() - 1
    slices = {0: own}
    for level in reversed(range(levels)):
        for offset in sorted(slices):
            slices[offset + (1 << level)] = flipped(slices[offset], level)
    return [slices[offset] for offset in sorted(slices)]


def collect_slices(sums, levels):
    for level in levels:
        step = 1 << level
        kept = {}
        for offset in range(0, len(sums), 2 * step):
            arrived = flipped(sums[offset + step].astype(jnp.bfloat16), level)
            kept[offset] = sums[offset].astype(jnp.float32) + arrived.astype(jnp.float32)
        sums = [kept.get(offset) for offset in range(len(sums))]
    return sums


def body(
    inputs,
    segments,
    routes,
    cotangent,
    norm_gain,
    in_proj,
    conv_taps,
    conv_bias,
    x_proj,
    dt_proj,
    dt_bias,
    log_decay,
    skip_gain,
    out_proj,
    moe_gain,
    router,
    expert_in,
    expert_out,
):
    experts = router.shape[1]
    half_rows = norm_gain.shape[0]
    columns = (
        x_proj,
        dt_proj.T,
        conv_taps,
        conv_bias[:, None],
        dt_bias[:, None],
        log_decay,
        skip_gain[:, None],
        jnp.concatenate([norm_gain, moe_gain])[:, None],
        router.reshape(2 * half_rows, experts // 2),
    )
    widths = [part.shape[1] for part in columns]
    ends = [sum(widths[: k + 1]) for k in range(len(widths))]
    sizes = [(name, lax.axis_size(name)) for name in ("ctx", "exp")]
    tail_ids = segments[0, -EDGE:, None].astype(jnp.bfloat16)
    edge = jnp.concatenate([inputs[0, -EDGE:], jnp.broadcast_to(tail_ids, (EDGE, LANES))], axis=1)
    (full_conv, full_small), prior = gather_all(
        sizes, (in_proj[:, :DI], jnp.concatenate(columns, axis=1)), edge, 0
    )
    later_in, later_out, full_small = lax.optimization_barrier((expert_in[0], expert_out[0], full_small))
    weights_in = spread_slices(later_in)
    weights_out = spread_slices(later_out)
    full_xproj, full_dt, full_taps, full_bias, full_dtbias, full_decay, full_skip, gains, full_router = [
        full_small[:, end - width : end] for end, width in zip(ends, widths)
    ]
    full_dt = full_dt.T
    full_bias, full_dtbias, full_skip = full_bias[:, 0], full_dtbias[:, 0], full_skip[:, 0]
    gains = gains.reshape(-1, 2, half_rows)
    full_norm, full_moe = gains[:, 0].reshape(-1), gains[:, 1].reshape(-1)
    full_router = full_router.reshape(-1, experts)
    tokens_here = inputs.shape[1]
    capacity = 5 * tokens_here // (4 * experts)
    flat_in = inputs[0].astype(jnp.float32)
    seg_row = segments[0]
    position = lax.axis_index("ctx")
    norm_one_value, norm_one_pull = jax.vjp(rms_scale, flat_in, full_norm.astype(jnp.float32))
    normed_one = norm_one_value.astype(jnp.bfloat16)
    conv_in = dot(normed_one, full_conv).astype(jnp.bfloat16)
    edge_one = rms_scale(prior[:, :D].astype(jnp.float32), full_norm.astype(jnp.float32)).astype(jnp.bfloat16)
    edge_rows = dot(edge_one, full_conv)[EDGE - (KC - 1) :].astype(jnp.bfloat16)
    prior_ids = jnp.where(position > 0, prior[EDGE - (KC - 1) :, D].astype(jnp.int32), -1)
    ext_ids = jnp.concatenate([prior_ids, seg_row])
    ext_rows = jnp.concatenate([edge_rows, conv_in], axis=0).astype(jnp.float32)
    conv_out, conv_pull = jax.vjp(
        lambda rows_in, taps_in, bias_in: conv_local(rows_in, taps_in, bias_in, ext_ids),
        ext_rows,
        full_taps.astype(jnp.float32),
        full_bias.astype(jnp.float32),
    )
    silu_value, silu_pull = jax.vjp(jax.nn.silu, conv_out)
    xs_val = silu_value.astype(jnp.bfloat16)
    xs_wide = xs_val.astype(jnp.float32)
    projected = jnp.dot(xs_val, full_xproj, preferred_element_type=jnp.float32)
    delta_low = projected[:, :R].astype(jnp.bfloat16)
    b_rows = projected[:, R : R + NS]
    c_rows = projected[:, R + NS :]
    dt_pre = jnp.dot(delta_low, full_dt, preferred_element_type=jnp.float32) + full_dtbias.astype(
        jnp.float32
    )
    step_size = jax.nn.softplus(dt_pre)
    a_swap = -jnp.exp(full_decay.astype(jnp.float32)).T
    earlier = jnp.concatenate([prior_ids[KC - 2 :], seg_row[:-1]])
    keep_mask = (earlier == seg_row).astype(jnp.float32)
    masked_step = jnp.where(keep_mask[:, None] > 0, step_size, 1e30)
    push = step_size * xs_wide
    rates = a_swap * LOG2E
    b_turned, c_turned = b_rows.T, c_rows.T
    scan_rows, start_state, products, kept, (full_gate, full_out) = scan_forward(
        sizes, masked_step, push, b_turned, c_turned, rates, (in_proj[:, DI:], out_proj), 3
    )
    gate_z = dot(normed_one, full_gate)
    skip_wide = full_skip.astype(jnp.float32)
    scanned_y = scan_rows + skip_wide * xs_wide
    gated_wide, gated_pull = jax.vjp(
        lambda scan_in, gate_in: scan_in * jax.nn.silu(gate_in), scanned_y, gate_z
    )
    gated = gated_wide.astype(jnp.bfloat16)
    mixed = jnp.dot(gated, full_out, preferred_element_type=jnp.float32)
    residual = flat_in + mixed
    norm_two_value, norm_two_pull = jax.vjp(rms_scale, residual, full_moe.astype(jnp.float32))
    normed_two = norm_two_value.astype(jnp.bfloat16)
    logits = jnp.dot(normed_two, full_router, preferred_element_type=jnp.float32)
    probability = jax.nn.softmax(logits, axis=-1)
    route_ids = routes[0, :, 0]
    one_hot = route_ids[:, None] == jnp.arange(experts, dtype=jnp.int32)[None, :]
    one_float = one_hot.astype(jnp.float32)
    gate_val = jnp.sum(probability * one_float, axis=1)
    running = jnp.cumsum(one_hot.astype(jnp.int32), axis=0)
    slot_index = jnp.sum(running * one_hot.astype(jnp.int32), axis=1) - 1
    room = -(-capacity // 16) * 16
    target = route_ids * room + slot_index
    grad_out = cotangent[0].astype(jnp.float32)
    grad_pick = (grad_out * gate_val[:, None]).astype(jnp.bfloat16)
    picked, grad_from_experts, grad_expert_in, grad_expert_out = run_experts(
        normed_two, grad_pick, target, weights_in, weights_out, experts, room, 2
    )
    picked = picked.astype(jnp.float32)
    grad_from_experts = grad_from_experts.astype(jnp.float32)
    outcome = residual + gate_val[:, None] * picked
    out_block = outcome.astype(jnp.bfloat16)[None]
    grad_gate = jnp.sum(grad_out * picked, axis=1)
    levels = lax.axis_size("ctx").bit_length() - 1
    grad_expert_in = collect_slices(grad_expert_in, range(1))
    grad_expert_out = collect_slices(grad_expert_out, range(1))
    grad_probs = grad_gate[:, None] * one_float
    grad_logits = (
        probability * (grad_probs - jnp.sum(grad_probs * probability, axis=1, keepdims=True))
    ).astype(jnp.bfloat16)
    grad_router = jnp.dot(normed_two.T, grad_logits, preferred_element_type=jnp.float32)
    grad_normed_two = grad_from_experts + jnp.dot(
        grad_logits, full_router.T, preferred_element_type=jnp.float32
    )
    grad_resid_norm, grad_moe_gain = norm_two_pull(grad_normed_two)
    grad_resid = grad_out + grad_resid_norm
    grad_mixed = grad_resid.astype(jnp.bfloat16)
    grad_gated = jnp.dot(grad_mixed, full_out.T, preferred_element_type=jnp.float32)
    grad_out_proj = jnp.dot(gated.T, grad_mixed, preferred_element_type=jnp.float32)
    grad_y, grad_z = gated_pull(grad_gated)
    grad_skip = jnp.sum(grad_y * xs_wide, axis=0)
    grad_z = grad_z.astype(jnp.bfloat16)
    grad_y, grad_expert_in, grad_expert_out = lax.optimization_barrier(
        (grad_y, grad_expert_in, grad_expert_out)
    )
    grad_expert_in = collect_slices(grad_expert_in, range(1, levels - 1))
    grad_expert_out = collect_slices(grad_expert_out, range(1, levels - 1))
    last = 1 << (levels - 1)
    leaving = [values[last].astype(jnp.bfloat16) for values in (grad_expert_in, grad_expert_out)]
    along_b, slope, grad_bs, grad_cs, grad_a, (own_gate, own_out), arrived = scan_backward(
        sizes,
        masked_step,
        push,
        grad_y,
        b_turned,
        c_turned,
        rates,
        products,
        (dot(normed_one.T, grad_z).astype(jnp.bfloat16), grad_out_proj.astype(jnp.bfloat16)),
        kept,
        leaving,
        4,
    )
    grad_w_in, grad_w_out = [
        values[0].astype(jnp.float32) + other.astype(jnp.float32)
        for values, other in zip((grad_expert_in, grad_expert_out), arrived)
    ]
    grad_step_all = along_b * xs_wide + slope * (1.0 / LOG2E)
    grad_xss = along_b * step_size
    grad_log_decay = (grad_a * a_swap).T
    soft_slope = jax.nn.sigmoid(dt_pre)
    grad_pre_wide = grad_step_all * soft_slope
    grad_dt_bias = jnp.sum(grad_pre_wide, axis=0)
    grad_dt_pre = grad_pre_wide.astype(jnp.bfloat16)
    grad_dt_proj = jnp.dot(delta_low.T, grad_dt_pre, preferred_element_type=jnp.float32)
    grad_delta = jnp.dot(grad_dt_pre, full_dt.T, preferred_element_type=jnp.float32)
    grad_projected = jnp.concatenate(
        [grad_delta, grad_bs, grad_cs], axis=1
    ).astype(jnp.bfloat16)
    grad_x_proj = jnp.dot(xs_val.T, grad_projected, preferred_element_type=jnp.float32)
    grad_xs_total = (
        skip_wide * grad_y
        + grad_xss
        + jnp.dot(grad_projected, full_xproj.T, preferred_element_type=jnp.float32)
    )
    grad_conv = silu_pull(grad_xs_total)[0]
    grad_ext, grad_taps, grad_cbias = conv_pull(grad_conv)
    from_next = shifted(grad_ext[: KC - 1], "ctx", -1)
    grad_conv_in = grad_ext[KC - 1 :] + jnp.concatenate(
        [jnp.zeros((tokens_here - (KC - 1), DI), jnp.float32), from_next], axis=0
    )
    grad_conv_in = grad_conv_in.astype(jnp.bfloat16)
    grad_normed_one = dot(grad_conv_in, full_conv.T) + dot(grad_z, full_gate.T)
    grad_inputs_norm, grad_norm_gain = norm_one_pull(grad_normed_one)
    grad_inputs = grad_resid + grad_inputs_norm
    sums = (
        grad_x_proj,
        grad_dt_proj.T,
        grad_taps,
        grad_cbias[:, None],
        grad_dt_bias[:, None],
        grad_log_decay,
        grad_skip[:, None],
        jnp.stack(
            [grad_norm_gain.reshape(-1, half_rows), grad_moe_gain.reshape(-1, half_rows)], axis=1
        ).reshape(-1, 1),
        grad_router.reshape(-1, experts // 2),
    )

    own_conv, own_small = reduce_all(
        sizes,
        (
            dot(normed_one.T, grad_conv_in).astype(jnp.bfloat16),
            jnp.concatenate(sums, axis=1).astype(jnp.bfloat16),
        ),
        1,
    )
    own_x, own_dt, own_taps, own_bias, own_dtbias, own_decay, own_skip, own_gains, own_router = [
        own_small[:, end - width : end] for end, width in zip(ends, widths)
    ]
    return (
        out_block,
        grad_inputs[None],
        own_gains[:half_rows, 0],
        jnp.concatenate([own_conv, own_gate], axis=1),
        own_taps,
        own_bias[:, 0],
        own_x,
        own_dt.T,
        own_dtbias[:, 0],
        own_decay,
        own_skip[:, 0],
        own_out,
        own_gains[half_rows:, 0],
        own_router.reshape(half_rows, experts),
        grad_w_in[None],
        grad_w_out[None],
    )


def solution(mesh):
    placed = (
        P("exp", "ctx", None),
        P("exp", "ctx"),
        P("exp", "ctx", None),
        P("exp", "ctx", None),
        P(("ctx", "exp")),
        P(("ctx", "exp"), None),
        P(("ctx", "exp"), None),
        P(("ctx", "exp")),
        P(("ctx", "exp"), None),
        P(None, ("ctx", "exp")),
        P(("ctx", "exp")),
        P(("ctx", "exp"), None),
        P(("ctx", "exp")),
        P(("ctx", "exp"), None),
        P(("ctx", "exp")),
        P(("ctx", "exp"), None),
        P("exp", None, "ctx"),
        P("exp", "ctx", None),
    )
    return jax.shard_map(
        body,
        mesh=mesh,
        in_specs=placed,
        out_specs=(
            P("exp", "ctx", None),
            P("exp", "ctx", None),
            P(("ctx", "exp")),
            P(("ctx", "exp"), None),
            P(("ctx", "exp"), None),
            P(("ctx", "exp")),
            P(("ctx", "exp"), None),
            P(None, ("ctx", "exp")),
            P(("ctx", "exp")),
            P(("ctx", "exp"), None),
            P(("ctx", "exp")),
            P(("ctx", "exp"), None),
            P(("ctx", "exp")),
            P(("ctx", "exp"), None),
            P("exp", None, "ctx"),
            P("exp", "ctx", None),
        ),
        check_vma=False,
    )
```

```python
import functools

import jax
import jax.numpy as jnp
from jax import lax
from jax.experimental import pallas as pl
from jax.experimental.pallas import tpu as pltpu
from jax.sharding import PartitionSpec as P

D = 768
DI = 1536
NS = 16
R = 48
KC = 4
LANES = 128
UNROLL = 8
LOG2E = 1.4426950408889634


EPS = 1e-05
MESH = pl.DeviceIdType.MESH
ROWS_AT_ONCE = 16
EDGE = 16

def tile(ref, base, lanes):
    return ref[pl.ds(pl.multiple_of(base, UNROLL), UNROLL), lanes]

def row(rows_now, place):
    return jnp.broadcast_to(rows_now[place : place + 1], (NS, LANES))

def put_row(rows_now, place, value):
    at = lax.broadcasted_iota(jnp.int32, (UNROLL, LANES), 0)
    value = jnp.broadcast_to(value, (UNROLL, LANES))
    return value if rows_now is None else jnp.where(at == place, value, rows_now)

def cost(tokens, channels, share):
    size = tokens * channels * NS
    return pl.CostEstimate(flops=size * share, transcendentals=size, bytes_accessed=size * share)


def pick(channels):
    return 512 if channels % 512 == 0 else 128


def shifted(value, axis, steps):
    count = lax.axis_size(axis)
    initial, last = (max(0, -steps), min(count, count - steps))
    return lax.ppermute(value, axis, [(source, source + steps) for source in range(initial, last)])


def rms_scale(values, gain):
    return values * lax.rsqrt(jnp.mean(values * values, axis=-1, keepdims=True) + EPS) * gain


def conv_local(ext_rows, taps, bias, ext_ids):
    length = ext_rows.shape[0] - (KC - 1)
    own_ids = ext_ids[KC - 1 :]
    result = jnp.zeros((length, ext_rows.shape[1]), jnp.float32) + bias[None, :]
    for offset in range(KC):
        same_doc = (ext_ids[offset : offset + length] == own_ids).astype(jnp.float32)
        result = (
            result
            + taps[:, offset][None, :] * ext_rows[offset : offset + length] * same_doc[:, None]
        )
    return result


def bit_positions(sizes):
    return [(axis, size.bit_length() - 2 - k) for axis, size in sizes for k in range(size.bit_length() - 1)]


def own_bit(place):
    axis, level = place
    return lax.rem(lax.axis_index(axis) // 2**level, 2)


def partner(place):
    axis, level = place
    where = {"ctx": lax.axis_index("ctx"), "exp": lax.axis_index("exp")}
    where[axis] = where[axis] + (1 - 2 * own_bit(place)) * 2**level
    return (where["ctx"], where["exp"])


def meet(places, *others):
    barrier = pltpu.get_barrier_semaphore()
    for device in [partner(place) for place in places] + list(others):
        pl.semaphore_signal(barrier, inc=1, device_id=device, device_id_type=MESH)
    pl.semaphore_wait(barrier, len(places) + len(others))


class GatherFlow:
    def __init__(self, places, streams, dims, shards, wholes, send_sems, recv_sems, local_sems):
        self.places, self.streams, self.dims, self.shards, self.wholes = places, streams, dims, shards, wholes
        self.sems = send_sems, recv_sems, local_sems
        self.bits = [own_bit(place) for place in places]

    def view(self, number, have):
        array, cols, order, begin = self.streams[number]
        index = tuple(slice(None) if p in have else self.bits[p] for p in self.dims)
        return self.wholes[array].at[index + (slice(None), cols)]

    def shard(self, number):
        array, cols, order, begin = self.streams[number]
        return self.shards[array].at[(slice(None),) * (begin + 1) + (cols,)]

    def own(self, number):
        array, cols, order, begin = self.streams[number]
        return pltpu.make_async_copy(self.shard(number), self.view(number, order[:begin]), self.sems[2].at[number])

    def flight(self, number, stage):
        array, cols, order, begin = self.streams[number]
        target = self.view(number, order[: begin + stage])
        return pltpu.make_async_remote_copy(
            src_ref=self.shard(number) if stage == 0 else target,
            dst_ref=target,
            send_sem=self.sems[0].at[number, stage],
            recv_sem=self.sems[1].at[number, stage],
            device_id=partner(self.places[order[begin + stage]]),
            device_id_type=MESH,
        )

    def stages(self, number):
        array, cols, order, begin = self.streams[number]
        return len(order) - begin

    def start(self):
        for number in range(len(self.streams)):
            self.flight(number, 0).start()
        for number in range(len(self.streams)):
            self.own(number).start()

    def advance(self, stage):
        for number in range(len(self.streams)):
            if stage >= self.stages(number):
                continue
            if stage == 0:
                self.own(number).wait()
            self.flight(number, stage).wait_recv()
            if stage + 1 < self.stages(number):
                self.flight(number, stage + 1).start()

    def finish(self):
        for number in range(len(self.streams)):
            for stage in range(self.stages(number)):
                self.flight(number, stage).wait_send()


def gather_kernel(places, streams, extra_streams, far, count, extra, *refs):
    both = count + extra
    shards, edge_ref, wholes, prior_ref = refs[:both], refs[both], refs[both + 1 : 2 * both + 1], refs[2 * both + 1]
    send_sems, recv_sems, local_sems, late_send, late_recv, late_local, edge_sems = refs[2 * both + 2 :]
    flow = GatherFlow(
        places, streams, range(len(places)), shards[:count], wholes[:count], send_sems, recv_sems, local_sems
    )
    late = GatherFlow(
        places, extra_streams, far, shards[count:], wholes[count:], late_send, late_recv, late_local
    )
    blocks = lax.axis_size("ctx")
    here, line = lax.axis_index("ctx"), lax.axis_index("exp")
    meet(places, (lax.rem(here + 1, blocks), line), (lax.rem(here + blocks - 1, blocks), line))
    flow.start()
    edge = pltpu.make_async_remote_copy(
        src_ref=edge_ref,
        dst_ref=prior_ref,
        send_sem=edge_sems.at[0],
        recv_sem=edge_sems.at[1],
        device_id=(lax.rem(here + 1, blocks), line),
        device_id_type=MESH,
    )
    edge.start()
    stages, behind = len(places), len(far)
    for stage in range(stages):
        flow.advance(stage)
        if stage == behind - 2:
            late.start()
        if stage >= behind and stage - behind < behind:
            late.advance(stage - behind)
    for stage in range(stages - behind, behind):
        late.advance(stage)
    flow.finish()
    late.finish()
    edge.wait()


def orders_of(places):
    core = places.index(("ctx", 0))
    rows = [k for k, place in enumerate(places) if place[0] == "ctx" and place[1] > 0]
    near = places.index(("exp", 0))
    return [core] + rows + [near] + far_of(places), [core, near] + rows + far_of(places)


def far_of(places):
    return [k for k, place in sorted(enumerate(places), key=lambda item: item[1][1]) if place[0] == "exp" and place[1] > 0]


def halves(arrays, first, second, begin=None):
    streams = []
    for array, values in enumerate(arrays):
        width = values.shape[-1]
        rest = () if begin is None else (begin,)
        if width % 256 == 0:
            streams.append((array, slice(0, width // 2), first) + rest)
            streams.append((array, slice(width // 2, width), second) + rest)
        else:
            streams.append((array, slice(0, width), first if array % 2 else second) + rest)
    return streams


def gather_orders(places):
    return [tuple(reversed(order)) for order in orders_of(places)]


def gather_all(sizes, shards, extra, edge, identity):
    places = bit_positions(sizes)
    stages = len(places)
    far = sorted(far_of(places))
    streams = halves(shards, *gather_orders(places), begin=0)
    late = [(k, slice(0, part.shape[1]), tuple(reversed(far_of(places))), 0) for k, part in enumerate(extra)]
    anywhere = pl.BlockSpec(memory_space=pl.ANY)
    total = len(shards) + len(extra)
    *wholes, prior = pl.pallas_call(
        functools.partial(gather_kernel, places, streams, late, far, len(shards), len(extra)),
        in_specs=[anywhere] * (total + 1),
        out_specs=[anywhere] * (total + 1),
        out_shape=[jax.ShapeDtypeStruct((2,) * stages + shard.shape, shard.dtype) for shard in shards]
        + [jax.ShapeDtypeStruct((2,) * len(far) + part.shape, part.dtype) for part in extra]
        + [jax.ShapeDtypeStruct(edge.shape, edge.dtype)],
        scratch_shapes=[
            pltpu.SemaphoreType.DMA((len(streams), stages)),
            pltpu.SemaphoreType.DMA((len(streams), stages)),
            pltpu.SemaphoreType.DMA((len(streams),)),
            pltpu.SemaphoreType.DMA((len(late), len(far))),
            pltpu.SemaphoreType.DMA((len(late), len(far))),
            pltpu.SemaphoreType.DMA((len(late),)),
            pltpu.SemaphoreType.DMA((2,)),
        ],
        compiler_params=pltpu.CompilerParams(collective_id=identity, has_side_effects=True),
        name="gather_all",
    )(*shards, *extra, edge)
    ready = [whole.reshape((-1,) + whole.shape[stages + 1 :]) for whole in wholes[: len(shards)]]
    return ready, wholes[len(shards) :], prior


class ReduceFlow:
    def __init__(self, places, streams, dims, parts, totals, landing, send_sems, recv_sems):
        self.places, self.streams, self.dims, self.parts, self.totals = places, streams, dims, parts, totals
        self.landing, self.sems = landing, (send_sems, recv_sems)
        self.bits = [own_bit(place) for place in places]
        self.first = []
        for array, cols, order in streams:
            self.first.append(sum(len(other[2]) for other in streams[: len(self.first)]))

    def spot(self, number, stage):
        return self.landing[self.first[number] + stage]

    def side(self, number, stage, value):
        array, cols, order = self.streams[number]
        left = [p for p in self.dims if p not in order[:stage]]
        index = tuple(value if p == order[stage] else slice(None) for p in left)
        if stage == 0:
            return self.parts[array].at[index + (slice(None), cols)]
        return self.spot(number, stage - 1).at[index]

    def flight(self, number, stage):
        order = self.streams[number][2]
        return pltpu.make_async_remote_copy(
            src_ref=self.side(number, stage, 1 - self.bits[order[stage]]),
            dst_ref=self.spot(number, stage),
            send_sem=self.sems[0].at[number, stage],
            recv_sem=self.sems[1].at[number, stage],
            device_id=partner(self.places[order[stage]]),
            device_id_type=MESH,
        )

    def start(self):
        for number in range(len(self.streams)):
            self.flight(number, 0).start()

    def advance(self, stage):
        for number, (array, cols, order) in enumerate(self.streams):
            if stage >= len(order):
                continue
            self.flight(number, stage).wait_recv()
            mine = self.side(number, stage, self.bits[order[stage]])
            there = self.spot(number, stage)
            depth = len(self.dims) - stage - 1
            final = stage + 1 == len(order)
            if depth == 0:
                self.totals[array][:, cols] = there[...].astype(jnp.float32) + mine[...].astype(jnp.float32)
                continue

            def add(index, unused, there=there, mine=mine, depth=depth, final=final, array=array, cols=cols):
                at = tuple(lax.rem(index // 2 ** (depth - 1 - k), 2) for k in range(depth))
                value = (there[at].astype(jnp.float32) + mine[at].astype(jnp.float32)).astype(there.dtype)
                if final:
                    self.totals[array][at + (slice(None), cols)] = value
                else:
                    there[at] = value
                return unused

            lax.fori_loop(0, 2**depth, add, 0)
            if not final:
                self.flight(number, stage + 1).start()

    def finish(self):
        for number in range(len(self.streams)):
            for stage in range(len(self.streams[number][2])):
                self.flight(number, stage).wait_send()


def landing_of(streams, dims, divided):
    landing = []
    for array, cols, order in streams:
        for stage in range(len(order)):
            rows = divided[array].shape[-2]
            landing.append(pltpu.VMEM((2,) * (len(dims) - stage - 1) + (rows, cols.stop - cols.start), jnp.bfloat16))
    return landing


def flights(streams):
    shape = (len(streams), max(len(order) for array, cols, order in streams))
    return [pltpu.SemaphoreType.DMA(shape)] * 2


def reduce_kernel(places, streams, late, far, count, extra, marks, *refs):
    both = count + extra
    parts, totals, scratch = refs[:both], refs[both : 2 * both], refs[2 * both :]
    landing, late_landing = scratch[: marks[0]], scratch[marks[0] : marks[1]]
    send_sems, recv_sems, late_send, late_recv = scratch[marks[1] :]
    flow = ReduceFlow(
        places, streams, range(len(places)), parts[:count], totals[:count], landing, send_sems, recv_sems
    )
    rest = ReduceFlow(places, late, far, parts[count:], totals[count:], late_landing, late_send, late_recv)
    meet(places)
    flow.start()
    rest.start()
    for stage in range(len(places)):
        flow.advance(stage)
        rest.advance(stage)
    flow.finish()
    rest.finish()


def reduce_all(sizes, parts, extra, identity):
    places = bit_positions(sizes)
    stages = len(places)
    far = sorted(far_of(places))
    streams = halves(parts, *[tuple(order) for order in orders_of(places)])
    late = [(k, slice(0, part.shape[-1]), tuple(far_of(places))) for k, part in enumerate(extra)]
    divided = [part.reshape((2,) * stages + (-1, part.shape[1])) for part in parts]
    inside = pl.BlockSpec(memory_space=pltpu.VMEM)
    landing = landing_of(streams, range(stages), divided)
    late_landing = landing_of(late, far, extra)
    marks = len(landing), len(landing) + len(late_landing)
    total = len(parts) + len(extra)
    return pl.pallas_call(
        functools.partial(reduce_kernel, places, streams, late, far, len(parts), len(extra), marks),
        in_specs=[inside] * total,
        out_specs=[inside] * total,
        out_shape=[jax.ShapeDtypeStruct(block.shape[-2:], jnp.float32) for block in divided + list(extra)],
        scratch_shapes=landing + late_landing + flights(streams) + flights(late),
        compiler_params=pltpu.CompilerParams(
            collective_id=identity, has_side_effects=True, vmem_limit_bytes=48 * 1024 * 1024
        ),
        name="reduce_all",
    )(*divided, *extra)


def dot(left, right):
    return jnp.dot(left, right, preferred_element_type=jnp.float32)


def contract(left, right, left_dim, right_dim):
    return lax.dot_general(left, right, (((left_dim,), (right_dim,)), ((), ())), preferred_element_type=jnp.float32)


def lanes_of(group, width, k):
    return pl.ds(pl.multiple_of(group * width + k * LANES, LANES), LANES)


def spread_columns(source_ref, wide_ref):
    def chunk(index, unused):
        base = pl.multiple_of(index * LANES, LANES)
        now = source_ref[:, pl.ds(base, LANES)]
        for place in range(LANES):
            wide_ref[base + place] = jnp.broadcast_to(now[:, place : place + 1], (NS, LANES))
        return unused

    lax.fori_loop(0, source_ref.shape[1] // LANES, chunk, 0)


def end_pass(width, step_ref, push_ref, wide_b, rate_ref, state_ref, hook):
    rows, channels = step_ref.shape
    count = width // LANES

    def group_body(group, unused):
        pieces = [lanes_of(group, width, k) for k in range(count)]
        rates = [rate_ref[:, lanes] for lanes in pieces]

        def block(index, states):
            states = list(states)
            steps = [tile(step_ref, index * UNROLL, lanes) for lanes in pieces]
            pushes = [tile(push_ref, index * UNROLL, lanes) for lanes in pieces]
            for place in range(UNROLL):
                b_now = wide_b[index * UNROLL + place]
                for k in range(count):
                    decay = jnp.exp2(row(steps[k], place) * rates[k])
                    states[k] = decay * states[k] + b_now * row(pushes[k], place)
            return tuple(states)

        zero = jnp.zeros((NS, LANES), jnp.float32)
        states = lax.fori_loop(0, rows // UNROLL, block, (zero,) * count)
        for k, lanes in enumerate(pieces):
            state_ref[:, lanes] = states[k]
        hook(group)
        return unused

    lax.fori_loop(0, channels // width, group_body, 0)


def out_pass(width, step_ref, push_ref, wide_b, wide_c, rate_ref, state_ref, y_ref, kept_buf, kept_copy, hook):
    rows, channels = step_ref.shape
    count = width // LANES
    span = kept_buf.shape[1]
    blocks = rows // span

    def time_body(number, unused):
        slot = lax.rem(number, 2)

        @pl.when(number >= 2)
        def _():
            kept_copy(number - 2, slot).wait()

        def group_body(group, unused_inner):
            pieces = [lanes_of(group, width, k) for k in range(count)]
            rates = [rate_ref[:, lanes] for lanes in pieces]

            def block(index, states):
                states = list(states)
                base = number * span + index * UNROLL
                steps = [tile(step_ref, base, lanes) for lanes in pieces]
                pushes = [tile(push_ref, base, lanes) for lanes in pieces]
                outs = [None] * count
                for place in range(UNROLL):
                    b_now = wide_b[base + place]
                    c_now = wide_c[base + place]
                    for k, lanes in enumerate(pieces):
                        decay = jnp.exp2(row(steps[k], place) * rates[k])
                        states[k] = decay * states[k] + b_now * row(pushes[k], place)
                        kept_buf[slot, index * UNROLL + place, :, lanes] = states[k].astype(kept_buf.dtype)
                        outs[k] = put_row(outs[k], place, jnp.sum(states[k] * c_now, axis=0, keepdims=True))
                for k, lanes in enumerate(pieces):
                    y_ref[pl.ds(pl.multiple_of(base, UNROLL), UNROLL), lanes] = outs[k]
                return tuple(states)

            states = lax.fori_loop(0, span // UNROLL, block, tuple(state_ref[:, lanes] for lanes in pieces))
            for k, lanes in enumerate(pieces):
                state_ref[:, lanes] = states[k]
            return unused_inner

        lax.fori_loop(0, channels // width, group_body, 0)
        kept_copy(number, slot).start()
        hook(number)
        return unused

    lax.fori_loop(0, blocks, time_body, 0)
    for number in range(max(0, blocks - 2), blocks):
        kept_copy(number, number % 2).wait()


def inflow_pass(width, step_ref, grad_ref, wide_c, rate_ref, flow_ref, hook):
    rows, channels = step_ref.shape
    count = width // LANES

    def group_body(group, unused):
        pieces = [lanes_of(group, width, k) for k in range(count)]
        rates = [rate_ref[:, lanes] for lanes in pieces]

        def block(index, flows):
            flows = list(flows)
            base = rows - UNROLL - index * UNROLL
            steps = [tile(step_ref, base, lanes) for lanes in pieces]
            grads = [tile(grad_ref, base, lanes) for lanes in pieces]
            for place in reversed(range(UNROLL)):
                c_now = wide_c[base + place]
                for k in range(count):
                    decay = jnp.exp2(row(steps[k], place) * rates[k])
                    flows[k] = decay * (c_now * row(grads[k], place) + flows[k])
            return tuple(flows)

        zero = jnp.zeros((NS, LANES), jnp.float32)
        flows = lax.fori_loop(0, rows // UNROLL, block, (zero,) * count)
        for k, lanes in enumerate(pieces):
            flow_ref[:, lanes] = flows[k]
        hook(group)
        return unused

    lax.fori_loop(0, channels // width, group_body, 0)


def lane_sums(part_ref):
    values = part_ref[...].reshape(-1, LANES)
    high = values.astype(jnp.bfloat16)
    low = (values - high.astype(jnp.float32)).astype(jnp.bfloat16)
    ones = jnp.ones((UNROLL, LANES), jnp.bfloat16)
    return contract(ones, high, 1, 1) + contract(ones, low, 1, 1)


def adjoint_pass(width, step_ref, push_ref, grad_ref, wide_b, wide_c, rate_ref, flow_ref, kept_buf, kept_copy,
                 along_ref, slope_ref, gb_ref, gc_ref, ga_ref, part_b, part_c, hook):
    rows, channels = step_ref.shape
    count = width // LANES
    span = kept_buf.shape[1] - 1
    blocks = rows // span
    ga_ref[...] = jnp.zeros_like(ga_ref)

    def time_body(order, unused):
        slot = lax.rem(order, 2)
        number = blocks - 1 - order
        kept_copy(number, slot).wait()
        part_b[...] = jnp.zeros_like(part_b)
        part_c[...] = jnp.zeros_like(part_c)

        def group_body(group, unused_inner):
            pieces = [lanes_of(group, width, k) for k in range(count)]
            rates = [rate_ref[:, lanes] for lanes in pieces]

            def block(index, carried):
                flows = list(carried[:count])
                sums = list(carried[count : 2 * count])
                current = list(carried[2 * count :])
                local = span - UNROLL - index * UNROLL
                base = number * span + local
                steps = [tile(step_ref, base, lanes) for lanes in pieces]
                pushes = [tile(push_ref, base, lanes) for lanes in pieces]
                grads = [tile(grad_ref, base, lanes) for lanes in pieces]
                alongs = [None] * count
                slopes = [None] * count
                for place in reversed(range(UNROLL)):
                    b_now = wide_b[base + place]
                    c_now = wide_c[base + place]
                    gb = gc = None
                    for k, lanes in enumerate(pieces):
                        prior = kept_buf[slot, local + place, :, lanes].astype(jnp.float32)
                        step = row(steps[k], place)
                        grad = row(grads[k], place)
                        decay = jnp.exp2(step * rates[k])
                        adjoint = c_now * grad + flows[k]
                        flows[k] = decay * adjoint
                        decay_grad = flows[k] * prior
                        alongs[k] = put_row(alongs[k], place, jnp.sum(adjoint * b_now, axis=0, keepdims=True))
                        slopes[k] = put_row(slopes[k], place, jnp.sum(decay_grad * rates[k], axis=0, keepdims=True))
                        sums[k] = sums[k] + decay_grad * step
                        here_b = adjoint * row(pushes[k], place)
                        here_c = current[k] * grad
                        gb = here_b if gb is None else gb + here_b
                        gc = here_c if gc is None else gc + here_c
                        current[k] = prior
                    part_b[local + place] += gb
                    part_c[local + place] += gc
                where = pl.ds(pl.multiple_of(base, UNROLL), UNROLL)
                for k, lanes in enumerate(pieces):
                    along_ref[where, lanes] = alongs[k]
                    slope_ref[where, lanes] = slopes[k]
                return tuple(flows + sums + current)

            carried = lax.fori_loop(
                0,
                span // UNROLL,
                block,
                tuple(flow_ref[:, lanes] for lanes in pieces)
                + tuple(ga_ref[:, lanes] for lanes in pieces)
                + tuple(kept_buf[slot, span, :, lanes].astype(jnp.float32) for lanes in pieces),
            )
            for k, lanes in enumerate(pieces):
                flow_ref[:, lanes] = carried[k]
                ga_ref[:, lanes] = carried[count + k]
            return unused_inner

        lax.fori_loop(0, channels // width, group_body, 0)
        gb_ref[number] = lane_sums(part_b)
        gc_ref[number] = lane_sums(part_c)

        @pl.when(order + 2 < blocks)
        def _():
            kept_copy(number - 2, slot).start()

        hook(order)
        return unused

    lax.fori_loop(0, blocks, time_body, 0)


def share(source, target, send_sems, recv_sems):
    blocks = lax.axis_size("ctx")
    here, line = lax.axis_index("ctx"), lax.axis_index("exp")
    copies = []
    for step in range(1, blocks):
        copies.append(
            pltpu.make_async_remote_copy(
                src_ref=source,
                dst_ref=target.at[here],
                send_sem=send_sems.at[step],
                recv_sem=recv_sems.at[step],
                device_id=(lax.rem(here + step, blocks), line),
                device_id_type=MESH,
            )
        )
        copies[-1].start()
    target[here] = source[...]
    return copies


def row_peers():
    blocks = lax.axis_size("ctx")
    here, line = lax.axis_index("ctx"), lax.axis_index("exp")
    return [(lax.rem(here + step, blocks), line) for step in range(1, blocks)]


def forward_kernel(places, streams, width, *refs):
    step_ref, push_ref, bt_ref, ct_ref, rate_ref = refs[:5]
    shards = refs[5:7]
    y_ref, start_ref, product_ref, kept_ref = refs[7:11]
    wholes = refs[11:13]
    (wide_b, wide_c, kept_buf, first_buf, state_ref, message, products, ends,
     kept_sems, first_sem, share_sems, send_sems, recv_sems, local_sems) = refs[13:]
    blocks = lax.axis_size("ctx")
    position = lax.axis_index("ctx")
    span = kept_buf.shape[1]
    flow = GatherFlow(places, streams, range(len(places)), shards, wholes, send_sems, recv_sems, local_sems)
    meet([place for place in places if place[0] == "exp"], *row_peers())
    flow.start()

    message[0] = jnp.exp2(jnp.sum(step_ref[...], axis=0, keepdims=True) * rate_ref[...]).astype(jnp.bfloat16)
    early = share(message.at[0], products, share_sems.at[0], share_sems.at[1])
    spread_columns(bt_ref, wide_b)
    spread_columns(ct_ref, wide_c)

    end_pass(width, step_ref, push_ref, wide_b, rate_ref, state_ref, lambda group: None)
    message[1] = state_ref[...].astype(jnp.bfloat16)
    late = share(message.at[1], ends, share_sems.at[2], share_sems.at[3])
    for copy in early + late:
        copy.wait_recv()
    start = jnp.zeros(state_ref.shape, jnp.float32)
    for index in range(blocks):
        folded = products[index].astype(jnp.float32) * start + ends[index].astype(jnp.float32)
        start = jnp.where(index < position, folded, start)
    state_ref[...] = start
    start_ref[...] = start
    product_ref[...] = products[...]
    first_buf[0] = start.astype(jnp.bfloat16)
    first_copy = pltpu.make_async_copy(first_buf, kept_ref.at[pl.ds(0, 1)], first_sem)
    first_copy.start()
    flow.advance(0)

    def kept_copy(number, slot):
        return pltpu.make_async_copy(
            kept_buf.at[slot], kept_ref.at[pl.ds(1 + number * span, span)], kept_sems.at[slot]
        )

    def second_hook(number):
        @pl.when(number == 3)
        def _():
            flow.advance(1)

    out_pass(width, step_ref, push_ref, wide_b, wide_c, rate_ref, state_ref, y_ref, kept_buf, kept_copy, second_hook)
    for stage in range(2, max(flow.stages(number) for number in range(len(streams)))):
        flow.advance(stage)
    flow.finish()
    first_copy.wait()
    for copy in early + late:
        copy.wait_send()


def scan_forward(sizes, step, push, b_turned, c_turned, rates, shards, identity, span=64):
    places = bit_positions(sizes)
    stages = len(places)
    begin = len(far_of(places))
    streams = halves(shards, *gather_orders(places), begin=begin)
    tokens, channels = step.shape
    blocks = sizes[0][1]
    inside = pl.BlockSpec(memory_space=pltpu.VMEM)
    anywhere = pl.BlockSpec(memory_space=pl.ANY)
    half = jnp.bfloat16
    y, start, products, kept, *wholes = pl.pallas_call(
        functools.partial(forward_kernel, places, streams, pick(channels)),
        in_specs=[inside] * 5 + [anywhere] * 2,
        out_specs=[inside] * 3 + [anywhere] * 3,
        out_shape=[
            jax.ShapeDtypeStruct((tokens, channels), jnp.float32),
            jax.ShapeDtypeStruct((NS, channels), jnp.float32),
            jax.ShapeDtypeStruct((blocks, NS, channels), half),
            jax.ShapeDtypeStruct((tokens + 1, NS, channels), half),
        ]
        + [jax.ShapeDtypeStruct((2,) * stages + shard.shape[begin:], shard.dtype) for shard in shards],
        scratch_shapes=[
            pltpu.VMEM((tokens, NS, LANES), jnp.float32),
            pltpu.VMEM((tokens, NS, LANES), jnp.float32),
            pltpu.VMEM((2, span, NS, channels), half),
            pltpu.VMEM((1, NS, channels), half),
            pltpu.VMEM((NS, channels), jnp.float32),
            pltpu.VMEM((2, NS, channels), half),
            pltpu.VMEM((blocks, NS, channels), half),
            pltpu.VMEM((blocks, NS, channels), half),
            pltpu.SemaphoreType.DMA((2,)),
            pltpu.SemaphoreType.DMA,
            pltpu.SemaphoreType.DMA((4, blocks)),
            pltpu.SemaphoreType.DMA((len(streams), stages)),
            pltpu.SemaphoreType.DMA((len(streams), stages)),
            pltpu.SemaphoreType.DMA((len(streams),)),
        ],
        compiler_params=pltpu.CompilerParams(
            collective_id=identity, has_side_effects=True, vmem_limit_bytes=48 * 1024 * 1024
        ),
        cost_estimate=cost(tokens, channels, 9),
        name="scan_forward",
    )(step, push, b_turned, c_turned, rates, *shards)
    return y, start, products, kept, [whole.reshape((-1,) + whole.shape[stages + 1 :]) for whole in wholes]


def backward_kernel(places, streams, marks, width, *refs):
    step_ref, push_ref, grad_ref, bt_ref, ct_ref, rate_ref, product_ref = refs[:7]
    parts = refs[7:9]
    kept_ref = refs[9]
    outs = refs[10:]
    along_ref, slope_ref, gb_ref, gc_ref, ga_ref = outs[:5]
    totals = outs[5:7]
    scratch = outs[7:]
    landing = scratch[:marks]
    (wide_b, wide_c, part_b, part_c, kept_buf, flow_ref, message, inflows,
     kept_sems, share_sems, send_sems, recv_sems) = scratch[marks:]
    blocks = lax.axis_size("ctx")
    position = lax.axis_index("ctx")
    span = kept_buf.shape[1] - 1
    steps = step_ref.shape[0] // span
    flow = ReduceFlow(places, streams, range(len(places)), parts, totals, landing, send_sems, recv_sems)

    def kept_copy(number, slot):
        return pltpu.make_async_copy(
            kept_ref.at[pl.ds(number * span, span + 1)], kept_buf.at[slot], kept_sems.at[slot]
        )

    for order in range(min(2, steps)):
        kept_copy(steps - 1 - order, order).start()
    meet([place for place in places if place[0] == "exp"], *row_peers())
    flow.start()
    spread_columns(bt_ref, wide_b)
    spread_columns(ct_ref, wide_c)
    inflow_pass(width, step_ref, grad_ref, wide_c, rate_ref, flow_ref, lambda group: None)
    message[...] = flow_ref[...].astype(jnp.bfloat16)
    copies = share(message, inflows, share_sems.at[0], share_sems.at[1])
    for copy in copies:
        copy.wait_recv()
    end = jnp.zeros(flow_ref.shape, jnp.float32)
    for index in reversed(range(blocks)):
        folded = inflows[index].astype(jnp.float32) + product_ref[index].astype(jnp.float32) * end
        end = jnp.where(index > position, folded, end)
    flow_ref[...] = end
    flow.advance(0)
    def hook(order):
        @pl.when(order == 2)
        def _():
            flow.advance(1)

        @pl.when(order == 4)
        def _():
            flow.advance(2)

    adjoint_pass(width, step_ref, push_ref, grad_ref, wide_b, wide_c, rate_ref, flow_ref, kept_buf, kept_copy,
                 along_ref, slope_ref, gb_ref, gc_ref, ga_ref, part_b, part_c, hook)
    for stage in range(3, len(streams[0][2])):
        flow.advance(stage)
    flow.finish()
    for copy in copies:
        copy.wait_send()


def scan_backward(sizes, step, push, grad, b_turned, c_turned, rates, products, parts, kept, identity, span=64):
    places = bit_positions(sizes)
    stages = len(places)
    far = sorted(far_of(places))
    streams = halves(parts, *[tuple(order[: stages - len(far)]) for order in orders_of(places)])
    divided = [part.reshape((2,) * stages + (-1, part.shape[1])) for part in parts]
    tokens, channels = step.shape
    blocks = sizes[0][1]
    inside = pl.BlockSpec(memory_space=pltpu.VMEM)
    anywhere = pl.BlockSpec(memory_space=pl.ANY)
    half = jnp.bfloat16
    landing = landing_of(streams, range(stages), divided)
    row_sums = jax.ShapeDtypeStruct((tokens // span, UNROLL, span * NS), jnp.float32)
    out = pl.pallas_call(
        functools.partial(backward_kernel, places, streams, len(landing), pick(channels)),
        in_specs=[inside] * 9 + [anywhere],
        out_specs=[inside] * 7,
        out_shape=[jax.ShapeDtypeStruct((tokens, channels), jnp.float32)] * 2
        + [row_sums, row_sums, jax.ShapeDtypeStruct((NS, channels), jnp.float32)]
        + [jax.ShapeDtypeStruct((2,) * len(far) + block.shape[-2:], half) for block in divided],
        scratch_shapes=landing
        + [
            pltpu.VMEM((tokens, NS, LANES), jnp.float32),
            pltpu.VMEM((tokens, NS, LANES), jnp.float32),
            pltpu.VMEM((span, NS, LANES), jnp.float32),
            pltpu.VMEM((span, NS, LANES), jnp.float32),
            pltpu.VMEM((2, span + 1, NS, channels), half),
            pltpu.VMEM((NS, channels), jnp.float32),
            pltpu.VMEM((NS, channels), half),
            pltpu.VMEM((blocks, NS, channels), half),
            pltpu.SemaphoreType.DMA((2,)),
            pltpu.SemaphoreType.DMA((2, blocks)),
        ]
        + flights(streams),
        compiler_params=pltpu.CompilerParams(
            collective_id=identity, has_side_effects=True, vmem_limit_bytes=56 * 1024 * 1024
        ),
        cost_estimate=cost(tokens, channels, 15),
        name="scan_backward",
    )(step, push, grad, b_turned, c_turned, rates, products, *divided, kept)
    along, slope, wide_b, wide_c, grad_a = out[:5]
    grad_bs, grad_cs = [values[:, 0].reshape(tokens, NS) for values in (wide_b, wide_c)]
    return along, slope, grad_bs, grad_cs, grad_a, out[5:7]


def expert_kernel(slices, *refs):
    tokens_ref, grads_ref, column_ref, row_ref = refs[:4]
    even = range(0, slices, 2)
    odd = range(1, slices, 2)
    weights_in, weight_out = refs[4 : 4 + len(even)], refs[4 + len(even)]
    outs = refs[5 + len(even) :]
    picked_ref, back_ref, own_out = outs[:3]
    sums_in = outs[3 : 3 + len(even)]
    (sent, got, answer, returned, w_in, w_out, hidden, total, active, slope, inner, sum_out, pair_out, pair_in, far_out,
     send_sems, recv_sems, weight_sems, sum_sems, spread_sems, mate_sems, far_sems) = outs[3 + len(even) :]
    experts, room, width = sent.shape[1:]
    places = experts * room
    me = lax.axis_index("exp")
    here = lax.axis_index("ctx")
    levels = slices.bit_length() - 1

    loads = [pltpu.make_async_copy(weight_out, w_out.at[0], weight_sems.at[slices])]
    for k, s in enumerate(even):
        loads.append(pltpu.make_async_copy(weights_in[k], w_in.at[s], weight_sems.at[s]))
    for load in loads:
        load.start()

    barrier = pltpu.get_barrier_semaphore()
    mates = [partner(("ctx", level)) for level in range(levels)]
    for step in range(1, experts):
        pl.semaphore_signal(barrier, inc=1, device_id=(here, lax.rem(me + step, experts)), device_id_type=MESH)
    for mate in mates:
        pl.semaphore_signal(barrier, inc=1, device_id=mate, device_id_type=MESH)
    pl.semaphore_wait(barrier, experts - 1 + levels)

    def exchange(source, target, kind):
        copies = []
        for step in range(1, experts):
            peer = lax.rem(me + step, experts)
            copy = pltpu.make_async_remote_copy(
                src_ref=source.at[peer],
                dst_ref=target.at[me],
                send_sem=send_sems.at[kind, step],
                recv_sem=recv_sems.at[kind, step],
                device_id=(here, peer),
                device_id_type=MESH,
            )
            copy.start()
            copies.append(copy)
        target[me] = source[me]
        return copies

    def hand(source, target, sems, level):
        copy = pltpu.make_async_remote_copy(
            src_ref=source,
            dst_ref=target,
            send_sem=sems.at[0],
            recv_sem=sems.at[1],
            device_id=mates[level],
            device_id_type=MESH,
        )
        copy.start()
        return copy

    def arrive(copies):
        for copy in copies:
            copy.wait_recv()

    open_sends = []

    def spread(level):
        step = 2**level
        copies = [hand(w_out.at[s], w_out.at[s + step], spread_sems.at[1, s + step], level) for s in range(0, slices, 2 * step)]
        open_sends.extend(copies)
        return copies

    chooser = (lax.broadcasted_iota(jnp.int32, (places, row_ref.shape[1]), 0) == row_ref[...]).astype(jnp.float32).astype(jnp.bfloat16)
    sent[0] = dot(chooser, tokens_ref[...]).astype(jnp.bfloat16).reshape(experts, room, width)
    first = exchange(sent.at[0], got.at[0], 0)
    for load in loads:
        load.wait()
    widening = [spread(levels - 1)]
    paired = [hand(w_in.at[s], w_in.at[s + 1], spread_sems.at[0, s], 0) for s in even]
    sent[1] = dot(chooser, grads_ref[...]).astype(jnp.bfloat16).reshape(experts, room, width)
    second = exchange(sent.at[1], got.at[1], 1)

    arrive(first)
    rows = got[0].reshape(places, width)
    for s in list(even) + list(odd):
        if s == 1:
            arrive(paired)
        hidden[...] = dot(rows, w_in[s])

        def curve(index, unused):
            at = pl.ds(pl.multiple_of(index * ROWS_AT_ONCE, ROWS_AT_ONCE), ROWS_AT_ONCE)
            value = hidden[at, :]
            bell = 0.5 + 0.5 * lax.erf(value * 0.7071067811865476)
            active[s, at, :] = (value * bell).astype(jnp.bfloat16)
            slope[s, at, :] = bell + value * (jnp.exp(-0.5 * value * value) * 0.3989422804014327)
            return unused

        lax.fori_loop(0, places // ROWS_AT_ONCE, curve, 0)

    for level in reversed(range(levels - 1)):
        arrive(widening[-1])
        widening.append(spread(level))
    for s in list(even) + list(odd):
        if s == 1:
            arrive(widening[-1])
        product = dot(active[s], w_out[s])
        total[...] = product if s == 0 else total[...] + product
    answer[0] = total[...].astype(jnp.bfloat16).reshape(experts, room, width)
    third = exchange(answer.at[0], returned.at[0], 2)

    arrive(second)
    pulled = got[1].reshape(places, width)
    joining = []
    for s in list(odd) + list(even):
        sum_out[s] = contract(active[s], pulled, 0, 0).astype(jnp.bfloat16)
        if s % 2:
            joining.append(hand(sum_out.at[s], pair_out.at[s // 2], mate_sems.at[0, s // 2], 0))
    for s in range(slices):
        inner[s] = (contract(pulled, w_out[s], 1, 1) * slope[s]).astype(jnp.bfloat16)
        product = contract(inner[s], w_in[s], 1, 1)
        total[...] = product if s == 0 else total[...] + product
    answer[1] = total[...].astype(jnp.bfloat16).reshape(experts, room, width)
    fourth = exchange(answer.at[1], returned.at[1], 3)

    def add_into(target, addend):
        def some(index, unused):
            at = pl.ds(pl.multiple_of(index * 4 * ROWS_AT_ONCE, 4 * ROWS_AT_ONCE), 4 * ROWS_AT_ONCE)
            target[at, :] = (target[at, :].astype(jnp.float32) + addend[at, :].astype(jnp.float32)).astype(jnp.bfloat16)
            return unused

        lax.fori_loop(0, target.shape[0] // (4 * ROWS_AT_ONCE), some, 0)

    arrive(joining)
    for k, s in enumerate(even):
        add_into(sum_out.at[s], pair_out.at[k])

    def pass_on(level):
        step = 2**level
        return [
            hand(sum_out.at[s + step], far_out.at[slices // step // 2 - 1 + s // (2 * step)], far_sems.at[level, s // (2 * step)], level)
            for s in range(0, slices, 2 * step)
        ]

    passing = pass_on(1)
    open_sends.extend(joining)
    for copy in paired:
        copy.wait_send()
    joined = []
    for s in list(odd) + list(even):
        w_in[s] = contract(rows, inner[s], 0, 0).astype(jnp.bfloat16)
        if s % 2:
            joined.append(hand(w_in.at[s], pair_in.at[s // 2], mate_sems.at[1, s // 2], 0))
    arrive(joined)
    stores = []
    for k, s in enumerate(even):
        add_into(w_in.at[s], pair_in.at[k])
        stores.append(pltpu.make_async_copy(w_in.at[s], sums_in[k], sum_sems.at[k]))
        stores[-1].start()

    finder = (lax.broadcasted_iota(jnp.int32, (column_ref.shape[0], places), 1) == column_ref[...]).astype(jnp.float32).astype(jnp.bfloat16)
    arrive(third)
    picked_ref[...] = dot(finder, returned[0].reshape(places, width)).astype(jnp.bfloat16)
    for level in range(1, levels):
        arrive(passing)
        open_sends.extend(passing)
        step = 2**level
        if level + 1 < levels:
            for s in range(0, slices, 2 * step):
                add_into(sum_out.at[s], far_out.at[slices // step // 2 - 1 + s // (2 * step)])
            passing = pass_on(level + 1)
    own_out[...] = sum_out[0].astype(jnp.float32) + far_out[0].astype(jnp.float32)
    arrive(fourth)
    back_ref[...] = dot(finder, returned[1].reshape(places, width)).astype(jnp.bfloat16)
    for store in stores:
        store.wait()
    for copies in (first, second, third, fourth, joined, open_sends):
        for copy in copies:
            copy.wait_send()


def run_experts(rows, grads, target, weights_in, weight_out, experts, room, identity):
    slices = 2 * len(weights_in)
    tokens, width = rows.shape
    inner_width = weight_out.shape[0]
    places = experts * room
    inside = pl.BlockSpec(memory_space=pltpu.VMEM)
    anywhere = pl.BlockSpec(memory_space=pl.ANY)
    half = jnp.bfloat16
    count = len(weights_in)
    out = pl.pallas_call(
        functools.partial(expert_kernel, slices),
        in_specs=[inside] * 4 + [anywhere] * (count + 1),
        out_specs=[inside] * 3 + [anywhere] * count,
        out_shape=[jax.ShapeDtypeStruct(rows.shape, half)] * 2
        + [jax.ShapeDtypeStruct(weight_out.shape, jnp.float32)]
        + [jax.ShapeDtypeStruct(weight.shape, half) for weight in weights_in],
        scratch_shapes=[pltpu.VMEM((2, experts, room, width), half)] * 4
        + [
            pltpu.VMEM((slices, width, inner_width), half),
            pltpu.VMEM((slices, inner_width, width), half),
            pltpu.VMEM((places, inner_width), jnp.float32),
            pltpu.VMEM((places, width), jnp.float32),
            pltpu.VMEM((slices, places, inner_width), half),
            pltpu.VMEM((slices, places, inner_width), jnp.float32),
            pltpu.VMEM((slices, places, inner_width), half),
            pltpu.VMEM((slices, inner_width, width), half),
            pltpu.VMEM((count, inner_width, width), half),
            pltpu.VMEM((count, width, inner_width), half),
            pltpu.VMEM((count, inner_width, width), half),
            pltpu.SemaphoreType.DMA((4, experts)),
            pltpu.SemaphoreType.DMA((4, experts)),
            pltpu.SemaphoreType.DMA((slices + 1,)),
            pltpu.SemaphoreType.DMA((count,)),
            pltpu.SemaphoreType.DMA((2, slices, 2)),
            pltpu.SemaphoreType.DMA((2, count, 2)),
            pltpu.SemaphoreType.DMA((slices, count, 2)),
        ],
        compiler_params=pltpu.CompilerParams(
            collective_id=identity, has_side_effects=True, vmem_limit_bytes=60 * 1024 * 1024
        ),
        name="run_experts",
    )(rows, grads, target[:, None], target[None, :], *weights_in, weight_out)
    return out[0], out[1], list(out[3:]), out[2]


def flipped(value, level):
    count = lax.axis_size("ctx")
    return lax.ppermute(value, "ctx", [(source, source ^ (1 << level)) for source in range(count)])


def spread_slices(own):
    levels = lax.axis_size("ctx").bit_length() - 1
    slices = {0: own}
    for level in reversed(range(1, levels)):
        for offset in sorted(slices):
            slices[offset + (1 << level)] = flipped(slices[offset], level)
    return [slices[offset] for offset in sorted(slices)]


def collect_slices(sums):
    levels = lax.axis_size("ctx").bit_length() - 1
    for level in range(1, levels):
        arrived = [flipped(values, level).astype(jnp.float32) for values in sums[1::2]]
        sums = [values.astype(jnp.float32) + other for values, other in zip(sums[::2], arrived)]
        if level + 1 < levels:
            sums = [values.astype(jnp.bfloat16) for values in sums]
    return sums[0]


def body(
    inputs,
    segments,
    routes,
    cotangent,
    norm_gain,
    in_proj,
    conv_taps,
    conv_bias,
    x_proj,
    dt_proj,
    dt_bias,
    log_decay,
    skip_gain,
    out_proj,
    moe_gain,
    router,
    expert_in,
    expert_out,
):
    experts = router.shape[1]
    half_rows = norm_gain.shape[0]
    columns = (
        x_proj,
        dt_proj.T,
        conv_taps,
        conv_bias[:, None],
        dt_bias[:, None],
        log_decay,
        skip_gain[:, None],
        jnp.concatenate([norm_gain, moe_gain])[:, None],
        router.reshape(2 * half_rows, experts // 2),
    )
    widths = [part.shape[1] for part in columns]
    ends = [sum(widths[: k + 1]) for k in range(len(widths))]
    sizes = [(name, lax.axis_size(name)) for name in ("ctx", "exp")]
    tail_ids = segments[0, -EDGE:, None].astype(jnp.bfloat16)
    edge = jnp.concatenate([inputs[0, -EDGE:], jnp.broadcast_to(tail_ids, (EDGE, LANES))], axis=1)
    (full_conv, full_small), partial, prior = gather_all(
        sizes, (in_proj[:, :DI], jnp.concatenate(columns, axis=1)), (in_proj[:, DI:], out_proj), edge, 0
    )
    later_in, full_small = lax.optimization_barrier((expert_in[0], full_small))
    weights_in = spread_slices(later_in)
    full_xproj, full_dt, full_taps, full_bias, full_dtbias, full_decay, full_skip, gains, full_router = [
        full_small[:, end - width : end] for end, width in zip(ends, widths)
    ]
    full_dt = full_dt.T
    full_bias, full_dtbias, full_skip = full_bias[:, 0], full_dtbias[:, 0], full_skip[:, 0]
    gains = gains.reshape(-1, 2, half_rows)
    full_norm, full_moe = gains[:, 0].reshape(-1), gains[:, 1].reshape(-1)
    full_router = full_router.reshape(-1, experts)
    tokens_here = inputs.shape[1]
    capacity = 5 * tokens_here // (4 * experts)
    flat_in = inputs[0].astype(jnp.float32)
    seg_row = segments[0]
    position = lax.axis_index("ctx")
    norm_one_value, norm_one_pull = jax.vjp(rms_scale, flat_in, full_norm.astype(jnp.float32))
    normed_one = norm_one_value.astype(jnp.bfloat16)
    conv_in = dot(normed_one, full_conv).astype(jnp.bfloat16)
    edge_one = rms_scale(prior[:, :D].astype(jnp.float32), full_norm.astype(jnp.float32)).astype(jnp.bfloat16)
    edge_rows = dot(edge_one, full_conv)[EDGE - (KC - 1) :].astype(jnp.bfloat16)
    prior_ids = jnp.where(position > 0, prior[EDGE - (KC - 1) :, D].astype(jnp.int32), -1)
    ext_ids = jnp.concatenate([prior_ids, seg_row])
    ext_rows = jnp.concatenate([edge_rows, conv_in], axis=0).astype(jnp.float32)
    conv_out, conv_pull = jax.vjp(
        lambda rows_in, taps_in, bias_in: conv_local(rows_in, taps_in, bias_in, ext_ids),
        ext_rows,
        full_taps.astype(jnp.float32),
        full_bias.astype(jnp.float32),
    )
    silu_value, silu_pull = jax.vjp(jax.nn.silu, conv_out)
    xs_val = silu_value.astype(jnp.bfloat16)
    xs_wide = xs_val.astype(jnp.float32)
    projected = jnp.dot(xs_val, full_xproj, preferred_element_type=jnp.float32)
    delta_low = projected[:, :R].astype(jnp.bfloat16)
    b_rows = projected[:, R : R + NS]
    c_rows = projected[:, R + NS :]
    dt_pre = jnp.dot(delta_low, full_dt, preferred_element_type=jnp.float32) + full_dtbias.astype(
        jnp.float32
    )
    step_size = jax.nn.softplus(dt_pre)
    a_swap = -jnp.exp(full_decay.astype(jnp.float32)).T
    earlier = jnp.concatenate([prior_ids[KC - 2 :], seg_row[:-1]])
    keep_mask = (earlier == seg_row).astype(jnp.float32)
    push = step_size * xs_wide
    masked_step = jnp.where(keep_mask[:, None] > 0, step_size, 1e30)
    rates = a_swap * LOG2E
    b_turned, c_turned = b_rows.T, c_rows.T
    push, *weights_in = lax.optimization_barrier((push, *weights_in))
    scan_rows, start_state, products, kept, (full_gate, full_out) = scan_forward(
        sizes, masked_step, push, b_turned, c_turned, rates, partial, 3
    )
    gate_z = dot(normed_one, full_gate)
    skip_wide = full_skip.astype(jnp.float32)
    scanned_y = scan_rows + skip_wide * xs_wide
    gated_wide, gated_pull = jax.vjp(
        lambda scan_in, gate_in: scan_in * jax.nn.silu(gate_in), scanned_y, gate_z
    )
    gated = gated_wide.astype(jnp.bfloat16)
    mixed = jnp.dot(gated, full_out, preferred_element_type=jnp.float32)
    residual = flat_in + mixed
    norm_two_value, norm_two_pull = jax.vjp(rms_scale, residual, full_moe.astype(jnp.float32))
    normed_two = norm_two_value.astype(jnp.bfloat16)
    logits = jnp.dot(normed_two, full_router, preferred_element_type=jnp.float32)
    probability = jax.nn.softmax(logits, axis=-1)
    route_ids = routes[0, :, 0]
    one_hot = route_ids[:, None] == jnp.arange(experts, dtype=jnp.int32)[None, :]
    one_float = one_hot.astype(jnp.float32)
    gate_val = jnp.sum(probability * one_float, axis=1)
    running = jnp.cumsum(one_hot.astype(jnp.int32), axis=0)
    slot_index = jnp.sum(running * one_hot.astype(jnp.int32), axis=1) - 1
    room = -(-capacity // 16) * 16
    target = route_ids * room + slot_index
    grad_out = cotangent[0].astype(jnp.float32)
    grad_pick = (grad_out * gate_val[:, None]).astype(jnp.bfloat16)
    picked, grad_from_experts, grad_expert_in, grad_w_out = run_experts(
        normed_two, grad_pick, target, weights_in, expert_out[0], experts, room, 2
    )
    grad_w_in = collect_slices(grad_expert_in)
    picked = picked.astype(jnp.float32)
    grad_from_experts = grad_from_experts.astype(jnp.float32)
    outcome = residual + gate_val[:, None] * picked
    out_block = outcome.astype(jnp.bfloat16)[None]
    grad_gate = jnp.sum(grad_out * picked, axis=1)
    grad_probs = grad_gate[:, None] * one_float
    grad_logits = (
        probability * (grad_probs - jnp.sum(grad_probs * probability, axis=1, keepdims=True))
    ).astype(jnp.bfloat16)
    grad_router = jnp.dot(normed_two.T, grad_logits, preferred_element_type=jnp.float32)
    grad_normed_two = grad_from_experts + jnp.dot(
        grad_logits, full_router.T, preferred_element_type=jnp.float32
    )
    grad_resid_norm, grad_moe_gain = norm_two_pull(grad_normed_two)
    grad_resid = grad_out + grad_resid_norm
    grad_mixed = grad_resid.astype(jnp.bfloat16)
    grad_gated = jnp.dot(grad_mixed, full_out.T, preferred_element_type=jnp.float32)
    grad_out_proj = jnp.dot(gated.T, grad_mixed, preferred_element_type=jnp.float32)
    grad_y, grad_z = gated_pull(grad_gated)
    grad_skip = jnp.sum(grad_y * xs_wide, axis=0)
    grad_z = grad_z.astype(jnp.bfloat16)
    grad_y, grad_w_in = lax.optimization_barrier((grad_y, grad_w_in))
    along_b, slope, grad_bs, grad_cs, grad_a, partial_sums = scan_backward(
        sizes,
        masked_step,
        push,
        grad_y,
        b_turned,
        c_turned,
        rates,
        products,
        (dot(normed_one.T, grad_z).astype(jnp.bfloat16), grad_out_proj.astype(jnp.bfloat16)),
        kept,
        4,
    )
    grad_step_all = along_b * xs_wide + slope * (1.0 / LOG2E)
    grad_xss = along_b * step_size
    grad_log_decay = (grad_a * a_swap).T
    soft_slope = jax.nn.sigmoid(dt_pre)
    grad_pre_wide = grad_step_all * soft_slope
    grad_dt_bias = jnp.sum(grad_pre_wide, axis=0)
    grad_dt_pre = grad_pre_wide.astype(jnp.bfloat16)
    grad_dt_proj = jnp.dot(delta_low.T, grad_dt_pre, preferred_element_type=jnp.float32)
    grad_delta = jnp.dot(grad_dt_pre, full_dt.T, preferred_element_type=jnp.float32)
    grad_projected = jnp.concatenate(
        [grad_delta, grad_bs, grad_cs], axis=1
    ).astype(jnp.bfloat16)
    grad_x_proj = jnp.dot(xs_val.T, grad_projected, preferred_element_type=jnp.float32)
    grad_xs_total = (
        skip_wide * grad_y
        + grad_xss
        + jnp.dot(grad_projected, full_xproj.T, preferred_element_type=jnp.float32)
    )
    grad_conv = silu_pull(grad_xs_total)[0]
    grad_ext, grad_taps, grad_cbias = conv_pull(grad_conv)
    from_next = shifted(grad_ext[: KC - 1], "ctx", -1)
    grad_conv_in = grad_ext[KC - 1 :] + jnp.concatenate(
        [jnp.zeros((tokens_here - (KC - 1), DI), jnp.float32), from_next], axis=0
    )
    grad_conv_in = grad_conv_in.astype(jnp.bfloat16)
    grad_normed_one = dot(grad_conv_in, full_conv.T) + dot(grad_z, full_gate.T)
    grad_inputs_norm, grad_norm_gain = norm_one_pull(grad_normed_one)
    grad_inputs = grad_resid + grad_inputs_norm
    sums = (
        grad_x_proj,
        grad_dt_proj.T,
        grad_taps,
        grad_cbias[:, None],
        grad_dt_bias[:, None],
        grad_log_decay,
        grad_skip[:, None],
        jnp.stack(
            [grad_norm_gain.reshape(-1, half_rows), grad_moe_gain.reshape(-1, half_rows)], axis=1
        ).reshape(-1, 1),
        grad_router.reshape(-1, experts // 2),
    )

    own_conv, own_small, own_gate, own_out = reduce_all(
        sizes,
        (
            dot(normed_one.T, grad_conv_in).astype(jnp.bfloat16),
            jnp.concatenate(sums, axis=1).astype(jnp.bfloat16),
        ),
        partial_sums,
        1,
    )
    own_x, own_dt, own_taps, own_bias, own_dtbias, own_decay, own_skip, own_gains, own_router = [
        own_small[:, end - width : end] for end, width in zip(ends, widths)
    ]
    return (
        out_block,
        grad_inputs[None],
        own_gains[:half_rows, 0],
        jnp.concatenate([own_conv, own_gate], axis=1),
        own_taps,
        own_bias[:, 0],
        own_x,
        own_dt.T,
        own_dtbias[:, 0],
        own_decay,
        own_skip[:, 0],
        own_out,
        own_gains[half_rows:, 0],
        own_router.reshape(half_rows, experts),
        grad_w_in[None],
        grad_w_out[None],
    )


def solution(mesh):
    placed = (
        P("exp", "ctx", None),
        P("exp", "ctx"),
        P("exp", "ctx", None),
        P("exp", "ctx", None),
        P(("ctx", "exp")),
        P(("ctx", "exp"), None),
        P(("ctx", "exp"), None),
        P(("ctx", "exp")),
        P(("ctx", "exp"), None),
        P(None, ("ctx", "exp")),
        P(("ctx", "exp")),
        P(("ctx", "exp"), None),
        P(("ctx", "exp")),
        P(("ctx", "exp"), None),
        P(("ctx", "exp")),
        P(("ctx", "exp"), None),
        P("exp", None, "ctx"),
        P("exp", "ctx", None),
    )
    return jax.shard_map(
        body,
        mesh=mesh,
        in_specs=placed,
        out_specs=(
            P("exp", "ctx", None),
            P("exp", "ctx", None),
            P(("ctx", "exp")),
            P(("ctx", "exp"), None),
            P(("ctx", "exp"), None),
            P(("ctx", "exp")),
            P(("ctx", "exp"), None),
            P(None, ("ctx", "exp")),
            P(("ctx", "exp")),
            P(("ctx", "exp"), None),
            P(("ctx", "exp")),
            P(("ctx", "exp"), None),
            P(("ctx", "exp")),
            P(("ctx", "exp"), None),
            P("exp", None, "ctx"),
            P("exp", "ctx", None),
        ),
        check_vma=False,
    )
```

```python
import functools

import jax
import jax.numpy as jnp
from jax import lax
from jax.experimental import pallas as pl
from jax.experimental.pallas import tpu as pltpu
from jax.sharding import PartitionSpec as P

D = 768
DI = 1536
NS = 16
R = 48
KC = 4
LANES = 128
UNROLL = 8
LOG2E = 1.4426950408889634


EPS = 1e-05
MESH = pl.DeviceIdType.MESH
ROWS_AT_ONCE = 16
EDGE = 16

def tile(ref, base, lanes):
    return ref[pl.ds(pl.multiple_of(base, UNROLL), UNROLL), lanes]

def row(rows_now, place):
    return jnp.broadcast_to(rows_now[place : place + 1], (NS, LANES))

def put_row(rows_now, place, value):
    at = lax.broadcasted_iota(jnp.int32, (UNROLL, LANES), 0)
    value = jnp.broadcast_to(value, (UNROLL, LANES))
    return value if rows_now is None else jnp.where(at == place, value, rows_now)

def cost(tokens, channels, share):
    size = tokens * channels * NS
    return pl.CostEstimate(flops=size * share, transcendentals=size, bytes_accessed=size * share)


def pick(channels):
    return 512 if channels % 512 == 0 else 128


def rms_scale(values, gain):
    return values * lax.rsqrt(jnp.mean(values * values, axis=-1, keepdims=True) + EPS) * gain


def conv_local(ext_rows, taps, bias, ext_ids):
    length = ext_rows.shape[0] - (KC - 1)
    own_ids = ext_ids[KC - 1 :]
    result = jnp.zeros((length, ext_rows.shape[1]), jnp.float32) + bias[None, :]
    for offset in range(KC):
        same_doc = (ext_ids[offset : offset + length] == own_ids).astype(jnp.float32)
        result = (
            result
            + taps[:, offset][None, :] * ext_rows[offset : offset + length] * same_doc[:, None]
        )
    return result


def bit_positions(sizes):
    return [(axis, size.bit_length() - 2 - k) for axis, size in sizes for k in range(size.bit_length() - 1)]


def own_bit(place):
    axis, level = place
    return lax.rem(lax.axis_index(axis) // 2**level, 2)


def partner(place):
    axis, level = place
    where = {"ctx": lax.axis_index("ctx"), "exp": lax.axis_index("exp")}
    where[axis] = where[axis] + (1 - 2 * own_bit(place)) * 2**level
    return (where["ctx"], where["exp"])


def meet(places, *others):
    barrier = pltpu.get_barrier_semaphore()
    for device in [partner(place) for place in places] + list(others):
        pl.semaphore_signal(barrier, inc=1, device_id=device, device_id_type=MESH)
    pl.semaphore_wait(barrier, len(places) + len(others))


class GatherFlow:
    def __init__(self, places, streams, dims, shards, wholes, send_sems, recv_sems, local_sems):
        self.places, self.streams, self.dims, self.shards, self.wholes = places, streams, dims, shards, wholes
        self.sems = send_sems, recv_sems, local_sems
        self.bits = [own_bit(place) for place in places]

    def view(self, number, have):
        array, cols, order, begin = self.streams[number]
        index = tuple(slice(None) if p in have else self.bits[p] for p in self.dims)
        return self.wholes[array].at[index + (slice(None), cols)]

    def shard(self, number):
        array, cols, order, begin = self.streams[number]
        return self.shards[array].at[(slice(None),) * (begin + 1) + (cols,)]

    def own(self, number):
        array, cols, order, begin = self.streams[number]
        return pltpu.make_async_copy(self.shard(number), self.view(number, order[:begin]), self.sems[2].at[number])

    def flight(self, number, stage):
        array, cols, order, begin = self.streams[number]
        target = self.view(number, order[: begin + stage])
        return pltpu.make_async_remote_copy(
            src_ref=self.shard(number) if stage == 0 else target,
            dst_ref=target,
            send_sem=self.sems[0].at[number, stage],
            recv_sem=self.sems[1].at[number, stage],
            device_id=partner(self.places[order[begin + stage]]),
            device_id_type=MESH,
        )

    def stages(self, number):
        array, cols, order, begin = self.streams[number]
        return len(order) - begin

    def start(self):
        for number in range(len(self.streams)):
            self.flight(number, 0).start()
        for number in range(len(self.streams)):
            self.own(number).start()

    def advance(self, stage):
        for number in range(len(self.streams)):
            if stage >= self.stages(number):
                continue
            if stage == 0:
                self.own(number).wait()
            self.flight(number, stage).wait_recv()
            if stage + 1 < self.stages(number):
                self.flight(number, stage + 1).start()

    def finish(self):
        for number in range(len(self.streams)):
            for stage in range(self.stages(number)):
                self.flight(number, stage).wait_send()


def gather_kernel(places, streams, extra_streams, far, count, extra, *refs):
    both = count + extra
    shards, edge_ref, wholes, prior_ref = refs[:both], refs[both], refs[both + 1 : 2 * both + 1], refs[2 * both + 1]
    send_sems, recv_sems, local_sems, late_send, late_recv, late_local, edge_sems = refs[2 * both + 2 :]
    flow = GatherFlow(
        places, streams, range(len(places)), shards[:count], wholes[:count], send_sems, recv_sems, local_sems
    )
    late = GatherFlow(
        places, extra_streams, far, shards[count:], wholes[count:], late_send, late_recv, late_local
    )
    blocks = lax.axis_size("ctx")
    here, line = lax.axis_index("ctx"), lax.axis_index("exp")
    meet(places, (lax.rem(here + 1, blocks), line), (lax.rem(here + blocks - 1, blocks), line))
    flow.start()
    edge = pltpu.make_async_remote_copy(
        src_ref=edge_ref,
        dst_ref=prior_ref,
        send_sem=edge_sems.at[0],
        recv_sem=edge_sems.at[1],
        device_id=(lax.rem(here + 1, blocks), line),
        device_id_type=MESH,
    )
    edge.start()
    stages, behind = len(places), len(far)
    for stage in range(stages):
        flow.advance(stage)
        if stage == behind - 2:
            late.start()
        if stage >= behind and stage - behind < behind:
            late.advance(stage - behind)
    for stage in range(stages - behind, behind):
        late.advance(stage)
    flow.finish()
    late.finish()
    edge.wait()


def orders_of(places):
    core = places.index(("ctx", 0))
    rows = [k for k, place in enumerate(places) if place[0] == "ctx" and place[1] > 0]
    near = places.index(("exp", 0))
    return [core] + rows + [near] + far_of(places), [core, near] + rows + far_of(places)


def far_of(places):
    return [k for k, place in sorted(enumerate(places), key=lambda item: item[1][1]) if place[0] == "exp" and place[1] > 0]


def halves(arrays, first, second, begin=None):
    streams = []
    for array, values in enumerate(arrays):
        width = values.shape[-1]
        rest = () if begin is None else (begin,)
        if width % 256 == 0:
            streams.append((array, slice(0, width // 2), first) + rest)
            streams.append((array, slice(width // 2, width), second) + rest)
        else:
            streams.append((array, slice(0, width), first if array % 2 else second) + rest)
    return streams


def gather_orders(places):
    return [tuple(reversed(order)) for order in orders_of(places)]


def gather_all(sizes, shards, extra, edge, identity):
    places = bit_positions(sizes)
    stages = len(places)
    far = sorted(far_of(places))
    streams = halves(shards, *gather_orders(places), begin=0)
    late = [(k, slice(0, part.shape[1]), tuple(reversed(far_of(places))), 0) for k, part in enumerate(extra)]
    anywhere = pl.BlockSpec(memory_space=pl.ANY)
    total = len(shards) + len(extra)
    *wholes, prior = pl.pallas_call(
        functools.partial(gather_kernel, places, streams, late, far, len(shards), len(extra)),
        in_specs=[anywhere] * (total + 1),
        out_specs=[anywhere] * (total + 1),
        out_shape=[jax.ShapeDtypeStruct((2,) * stages + shard.shape, shard.dtype) for shard in shards]
        + [jax.ShapeDtypeStruct((2,) * len(far) + part.shape, part.dtype) for part in extra]
        + [jax.ShapeDtypeStruct(edge.shape, edge.dtype)],
        scratch_shapes=[
            pltpu.SemaphoreType.DMA((len(streams), stages)),
            pltpu.SemaphoreType.DMA((len(streams), stages)),
            pltpu.SemaphoreType.DMA((len(streams),)),
            pltpu.SemaphoreType.DMA((len(late), len(far))),
            pltpu.SemaphoreType.DMA((len(late), len(far))),
            pltpu.SemaphoreType.DMA((len(late),)),
            pltpu.SemaphoreType.DMA((2,)),
        ],
        compiler_params=pltpu.CompilerParams(collective_id=identity, has_side_effects=True),
        name="gather_all",
    )(*shards, *extra, edge)
    ready = [whole.reshape((-1,) + whole.shape[stages + 1 :]) for whole in wholes[: len(shards)]]
    return ready, wholes[len(shards) :], prior


class ReduceFlow:
    def __init__(self, places, streams, dims, parts, totals, landing, send_sems, recv_sems):
        self.places, self.streams, self.dims, self.parts, self.totals = places, streams, dims, parts, totals
        self.landing, self.sems = landing, (send_sems, recv_sems)
        self.bits = [own_bit(place) for place in places]
        self.first = []
        for array, cols, order in streams:
            self.first.append(sum(len(other[2]) for other in streams[: len(self.first)]))

    def spot(self, number, stage):
        return self.landing[self.first[number] + stage]

    def side(self, number, stage, value):
        array, cols, order = self.streams[number]
        left = [p for p in self.dims if p not in order[:stage]]
        index = tuple(value if p == order[stage] else slice(None) for p in left)
        if stage == 0:
            return self.parts[array].at[index + (slice(None), cols)]
        return self.spot(number, stage - 1).at[index]

    def flight(self, number, stage):
        order = self.streams[number][2]
        return pltpu.make_async_remote_copy(
            src_ref=self.side(number, stage, 1 - self.bits[order[stage]]),
            dst_ref=self.spot(number, stage),
            send_sem=self.sems[0].at[number, stage],
            recv_sem=self.sems[1].at[number, stage],
            device_id=partner(self.places[order[stage]]),
            device_id_type=MESH,
        )

    def start(self):
        for number in range(len(self.streams)):
            self.flight(number, 0).start()

    def advance(self, stage):
        for number, (array, cols, order) in enumerate(self.streams):
            if stage >= len(order):
                continue
            self.flight(number, stage).wait_recv()
            mine = self.side(number, stage, self.bits[order[stage]])
            there = self.spot(number, stage)
            depth = len(self.dims) - stage - 1
            final = stage + 1 == len(order)
            if depth == 0:
                self.totals[array][:, cols] = there[...].astype(jnp.float32) + mine[...].astype(jnp.float32)
                continue

            def add(index, unused, there=there, mine=mine, depth=depth, final=final, array=array, cols=cols):
                at = tuple(lax.rem(index // 2 ** (depth - 1 - k), 2) for k in range(depth))
                value = (there[at].astype(jnp.float32) + mine[at].astype(jnp.float32)).astype(there.dtype)
                if final:
                    self.totals[array][at + (slice(None), cols)] = value
                else:
                    there[at] = value
                return unused

            lax.fori_loop(0, 2**depth, add, 0)
            if not final:
                self.flight(number, stage + 1).start()

    def finish(self):
        for number in range(len(self.streams)):
            for stage in range(len(self.streams[number][2])):
                self.flight(number, stage).wait_send()


def landing_of(streams, dims, divided):
    landing = []
    for array, cols, order in streams:
        for stage in range(len(order)):
            rows = divided[array].shape[-2]
            landing.append(pltpu.VMEM((2,) * (len(dims) - stage - 1) + (rows, cols.stop - cols.start), jnp.bfloat16))
    return landing


def flights(streams):
    shape = (len(streams), max(len(order) for array, cols, order in streams))
    return [pltpu.SemaphoreType.DMA(shape)] * 2


def dot(left, right):
    return jnp.dot(left, right, preferred_element_type=jnp.float32)


def contract(left, right, left_dim, right_dim):
    return lax.dot_general(left, right, (((left_dim,), (right_dim,)), ((), ())), preferred_element_type=jnp.float32)


def lanes_of(group, width, k):
    return pl.ds(pl.multiple_of(group * width + k * LANES, LANES), LANES)


def spread_columns(source_ref, wide_ref):
    def chunk(index, unused):
        base = pl.multiple_of(index * LANES, LANES)
        now = source_ref[:, pl.ds(base, LANES)]
        for place in range(LANES):
            wide_ref[base + place] = jnp.broadcast_to(now[:, place : place + 1], (NS, LANES))
        return unused

    lax.fori_loop(0, source_ref.shape[1] // LANES, chunk, 0)


def end_pass(width, step_ref, push_ref, wide_b, rate_ref, state_ref, hook):
    rows, channels = step_ref.shape
    count = width // LANES

    def group_body(group, unused):
        pieces = [lanes_of(group, width, k) for k in range(count)]
        rates = [rate_ref[:, lanes] for lanes in pieces]

        def block(index, states):
            states = list(states)
            steps = [tile(step_ref, index * UNROLL, lanes) for lanes in pieces]
            pushes = [tile(push_ref, index * UNROLL, lanes) for lanes in pieces]
            for place in range(UNROLL):
                b_now = wide_b[index * UNROLL + place]
                for k in range(count):
                    decay = jnp.exp2(row(steps[k], place) * rates[k])
                    states[k] = decay * states[k] + b_now * row(pushes[k], place)
            return tuple(states)

        zero = jnp.zeros((NS, LANES), jnp.float32)
        states = lax.fori_loop(0, rows // UNROLL, block, (zero,) * count)
        for k, lanes in enumerate(pieces):
            state_ref[:, lanes] = states[k]
        hook(group)
        return unused

    lax.fori_loop(0, channels // width, group_body, 0)


def out_pass(width, step_ref, push_ref, wide_b, wide_c, rate_ref, state_ref, y_ref, kept_buf, kept_copy, hook):
    rows, channels = step_ref.shape
    count = width // LANES
    span = kept_buf.shape[1]
    blocks = rows // span

    def time_body(number, unused):
        slot = lax.rem(number, 2)

        @pl.when(number >= 2)
        def _():
            kept_copy(number - 2, slot).wait()

        def group_body(group, unused_inner):
            pieces = [lanes_of(group, width, k) for k in range(count)]
            rates = [rate_ref[:, lanes] for lanes in pieces]

            def block(index, states):
                states = list(states)
                base = number * span + index * UNROLL
                steps = [tile(step_ref, base, lanes) for lanes in pieces]
                pushes = [tile(push_ref, base, lanes) for lanes in pieces]
                outs = [None] * count
                for place in range(UNROLL):
                    b_now = wide_b[base + place]
                    c_now = wide_c[base + place]
                    for k, lanes in enumerate(pieces):
                        decay = jnp.exp2(row(steps[k], place) * rates[k])
                        states[k] = decay * states[k] + b_now * row(pushes[k], place)
                        kept_buf[slot, index * UNROLL + place, :, lanes] = states[k].astype(kept_buf.dtype)
                        outs[k] = put_row(outs[k], place, jnp.sum(states[k] * c_now, axis=0, keepdims=True))
                for k, lanes in enumerate(pieces):
                    y_ref[pl.ds(pl.multiple_of(base, UNROLL), UNROLL), lanes] = outs[k]
                return tuple(states)

            states = lax.fori_loop(0, span // UNROLL, block, tuple(state_ref[:, lanes] for lanes in pieces))
            for k, lanes in enumerate(pieces):
                state_ref[:, lanes] = states[k]
            return unused_inner

        lax.fori_loop(0, channels // width, group_body, 0)
        kept_copy(number, slot).start()
        hook(number)
        return unused

    lax.fori_loop(0, blocks, time_body, 0)
    for number in range(max(0, blocks - 2), blocks):
        kept_copy(number, number % 2).wait()


def inflow_pass(width, step_ref, grad_ref, wide_c, rate_ref, flow_ref, hook):
    rows, channels = step_ref.shape
    count = width // LANES

    def group_body(group, unused):
        pieces = [lanes_of(group, width, k) for k in range(count)]
        rates = [rate_ref[:, lanes] for lanes in pieces]

        def block(index, flows):
            flows = list(flows)
            base = rows - UNROLL - index * UNROLL
            steps = [tile(step_ref, base, lanes) for lanes in pieces]
            grads = [tile(grad_ref, base, lanes) for lanes in pieces]
            for place in reversed(range(UNROLL)):
                c_now = wide_c[base + place]
                for k in range(count):
                    decay = jnp.exp2(row(steps[k], place) * rates[k])
                    flows[k] = decay * (c_now * row(grads[k], place) + flows[k])
            return tuple(flows)

        zero = jnp.zeros((NS, LANES), jnp.float32)
        flows = lax.fori_loop(0, rows // UNROLL, block, (zero,) * count)
        for k, lanes in enumerate(pieces):
            flow_ref[:, lanes] = flows[k]
        hook(group)
        return unused

    lax.fori_loop(0, channels // width, group_body, 0)


def lane_sums(part_ref):
    values = part_ref[...].reshape(-1, LANES)
    high = values.astype(jnp.bfloat16)
    low = (values - high.astype(jnp.float32)).astype(jnp.bfloat16)
    ones = jnp.ones((UNROLL, LANES), jnp.bfloat16)
    return contract(ones, high, 1, 1) + contract(ones, low, 1, 1)


def adjoint_pass(width, step_ref, push_ref, grad_ref, wide_b, wide_c, rate_ref, flow_ref, kept_buf, kept_copy,
                 along_ref, slope_ref, gb_ref, gc_ref, ga_ref, part_b, part_c, hook):
    rows, channels = step_ref.shape
    count = width // LANES
    span = kept_buf.shape[1] - 1
    blocks = rows // span
    ga_ref[...] = jnp.zeros_like(ga_ref)

    def time_body(order, unused):
        slot = lax.rem(order, 2)
        number = blocks - 1 - order
        kept_copy(number, slot).wait()
        part_b[...] = jnp.zeros_like(part_b)
        part_c[...] = jnp.zeros_like(part_c)

        def group_body(group, unused_inner):
            pieces = [lanes_of(group, width, k) for k in range(count)]
            rates = [rate_ref[:, lanes] for lanes in pieces]

            def block(index, carried):
                flows = list(carried[:count])
                sums = list(carried[count : 2 * count])
                current = list(carried[2 * count :])
                local = span - UNROLL - index * UNROLL
                base = number * span + local
                steps = [tile(step_ref, base, lanes) for lanes in pieces]
                pushes = [tile(push_ref, base, lanes) for lanes in pieces]
                grads = [tile(grad_ref, base, lanes) for lanes in pieces]
                alongs = [None] * count
                slopes = [None] * count
                for place in reversed(range(UNROLL)):
                    b_now = wide_b[base + place]
                    c_now = wide_c[base + place]
                    gb = gc = None
                    for k, lanes in enumerate(pieces):
                        prior = kept_buf[slot, local + place, :, lanes].astype(jnp.float32)
                        step = row(steps[k], place)
                        grad = row(grads[k], place)
                        decay = jnp.exp2(step * rates[k])
                        adjoint = c_now * grad + flows[k]
                        flows[k] = decay * adjoint
                        decay_grad = flows[k] * prior
                        alongs[k] = put_row(alongs[k], place, jnp.sum(adjoint * b_now, axis=0, keepdims=True))
                        slopes[k] = put_row(slopes[k], place, jnp.sum(decay_grad * rates[k], axis=0, keepdims=True))
                        sums[k] = sums[k] + decay_grad * step
                        here_b = adjoint * row(pushes[k], place)
                        here_c = current[k] * grad
                        gb = here_b if gb is None else gb + here_b
                        gc = here_c if gc is None else gc + here_c
                        current[k] = prior
                    part_b[local + place] += gb
                    part_c[local + place] += gc
                where = pl.ds(pl.multiple_of(base, UNROLL), UNROLL)
                for k, lanes in enumerate(pieces):
                    along_ref[where, lanes] = alongs[k]
                    slope_ref[where, lanes] = slopes[k]
                return tuple(flows + sums + current)

            carried = lax.fori_loop(
                0,
                span // UNROLL,
                block,
                tuple(flow_ref[:, lanes] for lanes in pieces)
                + tuple(ga_ref[:, lanes] for lanes in pieces)
                + tuple(kept_buf[slot, span, :, lanes].astype(jnp.float32) for lanes in pieces),
            )
            for k, lanes in enumerate(pieces):
                flow_ref[:, lanes] = carried[k]
                ga_ref[:, lanes] = carried[count + k]
            return unused_inner

        lax.fori_loop(0, channels // width, group_body, 0)
        gb_ref[number] = lane_sums(part_b)
        gc_ref[number] = lane_sums(part_c)

        @pl.when(order + 2 < blocks)
        def _():
            kept_copy(number - 2, slot).start()

        hook(order)
        return unused

    lax.fori_loop(0, blocks, time_body, 0)


def share(source, target, send_sems, recv_sems):
    blocks = lax.axis_size("ctx")
    here, line = lax.axis_index("ctx"), lax.axis_index("exp")
    copies = []
    for step in range(1, blocks):
        copies.append(
            pltpu.make_async_remote_copy(
                src_ref=source,
                dst_ref=target.at[here],
                send_sem=send_sems.at[step],
                recv_sem=recv_sems.at[step],
                device_id=(lax.rem(here + step, blocks), line),
                device_id_type=MESH,
            )
        )
        copies[-1].start()
    target[here] = source[...]
    return copies


def row_peers():
    blocks = lax.axis_size("ctx")
    here, line = lax.axis_index("ctx"), lax.axis_index("exp")
    return [(lax.rem(here + step, blocks), line) for step in range(1, blocks)]


def forward_kernel(places, streams, width, *refs):
    step_ref, push_ref, bt_ref, ct_ref, rate_ref = refs[:5]
    shards = refs[5:7]
    y_ref, start_ref, product_ref, kept_ref = refs[7:11]
    wholes = refs[11:13]
    (wide_b, wide_c, kept_buf, first_buf, state_ref, message, products, ends,
     kept_sems, first_sem, share_sems, send_sems, recv_sems, local_sems) = refs[13:]
    blocks = lax.axis_size("ctx")
    position = lax.axis_index("ctx")
    span = kept_buf.shape[1]
    flow = GatherFlow(places, streams, range(len(places)), shards, wholes, send_sems, recv_sems, local_sems)
    meet([place for place in places if place[0] == "exp"], *row_peers())
    flow.start()

    message[0] = jnp.exp2(jnp.sum(step_ref[...], axis=0, keepdims=True) * rate_ref[...]).astype(jnp.bfloat16)
    early = share(message.at[0], products, share_sems.at[0], share_sems.at[1])
    spread_columns(bt_ref, wide_b)
    spread_columns(ct_ref, wide_c)

    end_pass(width, step_ref, push_ref, wide_b, rate_ref, state_ref, lambda group: None)
    message[1] = state_ref[...].astype(jnp.bfloat16)
    late = share(message.at[1], ends, share_sems.at[2], share_sems.at[3])
    for copy in early + late:
        copy.wait_recv()
    start = jnp.zeros(state_ref.shape, jnp.float32)
    for index in range(blocks):
        folded = products[index].astype(jnp.float32) * start + ends[index].astype(jnp.float32)
        start = jnp.where(index < position, folded, start)
    state_ref[...] = start
    start_ref[...] = start
    product_ref[...] = products[...]
    first_buf[0] = start.astype(jnp.bfloat16)
    first_copy = pltpu.make_async_copy(first_buf, kept_ref.at[pl.ds(0, 1)], first_sem)
    first_copy.start()
    flow.advance(0)

    def kept_copy(number, slot):
        return pltpu.make_async_copy(
            kept_buf.at[slot], kept_ref.at[pl.ds(1 + number * span, span)], kept_sems.at[slot]
        )

    def second_hook(number):
        @pl.when(number == 3)
        def _():
            flow.advance(1)

    out_pass(width, step_ref, push_ref, wide_b, wide_c, rate_ref, state_ref, y_ref, kept_buf, kept_copy, second_hook)
    for stage in range(2, max(flow.stages(number) for number in range(len(streams)))):
        flow.advance(stage)
    flow.finish()
    first_copy.wait()
    for copy in early + late:
        copy.wait_send()


def scan_forward(sizes, step, push, b_turned, c_turned, rates, shards, identity, span=64):
    places = bit_positions(sizes)
    stages = len(places)
    begin = len(far_of(places))
    streams = halves(shards, *gather_orders(places), begin=begin)
    tokens, channels = step.shape
    blocks = sizes[0][1]
    inside = pl.BlockSpec(memory_space=pltpu.VMEM)
    anywhere = pl.BlockSpec(memory_space=pl.ANY)
    half = jnp.bfloat16
    y, start, products, kept, *wholes = pl.pallas_call(
        functools.partial(forward_kernel, places, streams, pick(channels)),
        in_specs=[inside] * 5 + [anywhere] * 2,
        out_specs=[inside] * 3 + [anywhere] * 3,
        out_shape=[
            jax.ShapeDtypeStruct((tokens, channels), jnp.float32),
            jax.ShapeDtypeStruct((NS, channels), jnp.float32),
            jax.ShapeDtypeStruct((blocks, NS, channels), half),
            jax.ShapeDtypeStruct((tokens + 1, NS, channels), half),
        ]
        + [jax.ShapeDtypeStruct((2,) * stages + shard.shape[begin:], shard.dtype) for shard in shards],
        scratch_shapes=[
            pltpu.VMEM((tokens, NS, LANES), jnp.float32),
            pltpu.VMEM((tokens, NS, LANES), jnp.float32),
            pltpu.VMEM((2, span, NS, channels), half),
            pltpu.VMEM((1, NS, channels), half),
            pltpu.VMEM((NS, channels), jnp.float32),
            pltpu.VMEM((2, NS, channels), half),
            pltpu.VMEM((blocks, NS, channels), half),
            pltpu.VMEM((blocks, NS, channels), half),
            pltpu.SemaphoreType.DMA((2,)),
            pltpu.SemaphoreType.DMA,
            pltpu.SemaphoreType.DMA((4, blocks)),
            pltpu.SemaphoreType.DMA((len(streams), stages)),
            pltpu.SemaphoreType.DMA((len(streams), stages)),
            pltpu.SemaphoreType.DMA((len(streams),)),
        ],
        compiler_params=pltpu.CompilerParams(
            collective_id=identity, has_side_effects=True, vmem_limit_bytes=48 * 1024 * 1024
        ),
        cost_estimate=cost(tokens, channels, 9),
        name="scan_forward",
    )(step, push, b_turned, c_turned, rates, *shards)
    return y, start, products, kept, [whole.reshape((-1,) + whole.shape[stages + 1 :]) for whole in wholes]


def backward_kernel(places, streams, marks, width, *refs):
    step_ref, push_ref, grad_ref, bt_ref, ct_ref, rate_ref, product_ref = refs[:7]
    parts = refs[7:9]
    kept_ref = refs[9]
    outs = refs[10:]
    along_ref, slope_ref, gb_ref, gc_ref, ga_ref = outs[:5]
    totals = outs[5:7]
    scratch = outs[7:]
    landing = scratch[:marks]
    (wide_b, wide_c, part_b, part_c, kept_buf, flow_ref, message, inflows,
     kept_sems, share_sems, send_sems, recv_sems) = scratch[marks:]
    blocks = lax.axis_size("ctx")
    position = lax.axis_index("ctx")
    span = kept_buf.shape[1] - 1
    steps = step_ref.shape[0] // span
    flow = ReduceFlow(places, streams, range(len(places)), parts, totals, landing, send_sems, recv_sems)

    def kept_copy(number, slot):
        return pltpu.make_async_copy(
            kept_ref.at[pl.ds(number * span, span + 1)], kept_buf.at[slot], kept_sems.at[slot]
        )

    for order in range(min(2, steps)):
        kept_copy(steps - 1 - order, order).start()
    meet([place for place in places if place[0] == "exp"], *row_peers())
    flow.start()
    spread_columns(bt_ref, wide_b)
    spread_columns(ct_ref, wide_c)
    inflow_pass(width, step_ref, grad_ref, wide_c, rate_ref, flow_ref, lambda group: None)
    message[...] = flow_ref[...].astype(jnp.bfloat16)
    copies = share(message, inflows, share_sems.at[0], share_sems.at[1])
    for copy in copies:
        copy.wait_recv()
    end = jnp.zeros(flow_ref.shape, jnp.float32)
    for index in reversed(range(blocks)):
        folded = inflows[index].astype(jnp.float32) + product_ref[index].astype(jnp.float32) * end
        end = jnp.where(index > position, folded, end)
    flow_ref[...] = end
    flow.advance(0)
    def hook(order):
        @pl.when(order == 2)
        def _():
            flow.advance(1)

        @pl.when(order == 4)
        def _():
            flow.advance(2)

    adjoint_pass(width, step_ref, push_ref, grad_ref, wide_b, wide_c, rate_ref, flow_ref, kept_buf, kept_copy,
                 along_ref, slope_ref, gb_ref, gc_ref, ga_ref, part_b, part_c, hook)
    for stage in range(3, len(streams[0][2])):
        flow.advance(stage)
    flow.finish()
    for copy in copies:
        copy.wait_send()


def scan_backward(sizes, step, push, grad, b_turned, c_turned, rates, products, parts, kept, identity, span=64):
    places = bit_positions(sizes)
    stages = len(places)
    far = sorted(far_of(places))
    streams = halves(parts, *[tuple(order[: stages - len(far)]) for order in orders_of(places)])
    divided = [part.reshape((2,) * stages + (-1, part.shape[1])) for part in parts]
    tokens, channels = step.shape
    blocks = sizes[0][1]
    inside = pl.BlockSpec(memory_space=pltpu.VMEM)
    anywhere = pl.BlockSpec(memory_space=pl.ANY)
    half = jnp.bfloat16
    landing = landing_of(streams, range(stages), divided)
    row_sums = jax.ShapeDtypeStruct((tokens // span, UNROLL, span * NS), jnp.float32)
    out = pl.pallas_call(
        functools.partial(backward_kernel, places, streams, len(landing), pick(channels)),
        in_specs=[inside] * 9 + [anywhere],
        out_specs=[inside] * 7,
        out_shape=[jax.ShapeDtypeStruct((tokens, channels), jnp.float32)] * 2
        + [row_sums, row_sums, jax.ShapeDtypeStruct((NS, channels), jnp.float32)]
        + [jax.ShapeDtypeStruct((2,) * len(far) + block.shape[-2:], half) for block in divided],
        scratch_shapes=landing
        + [
            pltpu.VMEM((tokens, NS, LANES), jnp.float32),
            pltpu.VMEM((tokens, NS, LANES), jnp.float32),
            pltpu.VMEM((span, NS, LANES), jnp.float32),
            pltpu.VMEM((span, NS, LANES), jnp.float32),
            pltpu.VMEM((2, span + 1, NS, channels), half),
            pltpu.VMEM((NS, channels), jnp.float32),
            pltpu.VMEM((NS, channels), half),
            pltpu.VMEM((blocks, NS, channels), half),
            pltpu.SemaphoreType.DMA((2,)),
            pltpu.SemaphoreType.DMA((2, blocks)),
        ]
        + flights(streams),
        compiler_params=pltpu.CompilerParams(
            collective_id=identity, has_side_effects=True, vmem_limit_bytes=56 * 1024 * 1024
        ),
        cost_estimate=cost(tokens, channels, 15),
        name="scan_backward",
    )(step, push, grad, b_turned, c_turned, rates, products, *divided, kept)
    along, slope, wide_b, wide_c, grad_a = out[:5]
    grad_bs, grad_cs = [values[:, 0].reshape(tokens, NS) for values in (wide_b, wide_c)]
    return along, slope, grad_bs, grad_cs, grad_a, out[5:7]


class PackedReduce(ReduceFlow):
    def __init__(self, places, streams, heads, parts, totals, landing, blocks, send_sems, recv_sems):
        super().__init__(places, streams, range(len(places)), parts, totals, landing, send_sems, recv_sems)
        self.heads, self.blocks = heads, blocks

    def side(self, number, stage, value):
        array, cols, order = self.streams[number]
        if stage == 0:
            index = tuple(value if p == order[0] else slice(None) for p in range(self.heads))
            return self.parts[array].at[index + (slice(None), cols)]
        left = [p for p in self.dims if p not in order[:stage]]
        index = tuple(value if p == order[stage] else slice(None) for p in left)
        held = self.blocks[number] if stage == 1 else self.spot(number, stage - 1)
        return held.at[index]

    def advance(self, stage):
        if stage:
            super().advance(stage)
            return
        for number, (array, cols, order) in enumerate(self.streams):
            self.flight(number, 0).wait_recv()
            mine = self.side(number, 0, self.bits[order[0]])
            there, held = self.spot(number, 0), self.blocks[number]
            tails = len(self.places) - self.heads
            size = held.shape[-2]

            def add(index, unused, mine=mine, there=there, held=held, tails=tails, size=size):
                at = tuple(lax.rem(index // 2 ** (self.heads - 2 - k), 2) for k in range(self.heads - 1))
                value = there[at].astype(jnp.float32) + mine[at].astype(jnp.float32)
                for block in range(2**tails):
                    spot = tuple(block // 2 ** (tails - 1 - k) % 2 for k in range(tails))
                    held[at + spot] = value[block * size : (block + 1) * size].astype(held.dtype)
                return unused

            lax.fori_loop(0, 2 ** (self.heads - 1), add, 0)
            self.flight(number, 1).start()


def turned(values):
    return jnp.concatenate([values[:, at : at + LANES].T for at in range(0, values.shape[1], LANES)], axis=0)


def finish_kernel(places, streams, third, late, far, marks, *refs):
    (along_h, slope_h, grad_h, pre_h, conv_h, xs_h, ext_h, gz_h, wc_h, wg_h) = refs[:10]
    (normed_ref, in_ref, resid_ref, mix_ref, bc_ref, delta_ref, same_ref, chan_ref, decay_ref, wide_ref) = refs[10:20]
    rest_parts = refs[20:22]
    (gi_ref, own_conv, own_gate, own_out, own_x, own_dt, own_taps, own_decay, own_rows, own_pair, own_router) = refs[22:33]
    scratch = refs[33:]
    landing, scratch = scratch[: marks[0]], scratch[marks[0] :]
    blocks, scratch = scratch[: marks[1]], scratch[marks[1] :]
    landing3, scratch = scratch[: marks[2]], scratch[marks[2] :]
    blocks3, scratch = scratch[: marks[3]], scratch[marks[3] :]
    late_landing, scratch = scratch[: marks[4]], scratch[marks[4] :]
    (along, slope, grad, pre, conv, xs, ext, gz, wc, wg, gdt, gci, last, spill, arrived, sums, rows_s, wide_s, gn,
     part_conv, part_small, part_wide, tot_small, tot_wide,
     block_sems, whole_sems, spill_sems, send_sems, recv_sems, send3, recv3, late_send, late_recv) = scratch
    tokens, channels = xs.shape
    span = tokens // block_sems.shape[1]
    heads = len([place for place in places if place[0] == "ctx"])
    flow = PackedReduce(
        places, streams, heads, (part_conv, part_small), (own_conv, tot_small), landing, blocks, send_sems, recv_sems
    )
    flow3 = PackedReduce(places, third, heads, (part_wide,), (tot_wide,), landing3, blocks3, send3, recv3)
    rest = ReduceFlow(places, late, far, rest_parts, (own_gate, own_out), late_landing, late_send, late_recv)

    streamed = ((along_h, along), (slope_h, slope), (grad_h, grad), (pre_h, pre), (xs_h, xs))

    def block_copy(k, number):
        rows = pl.ds(number * span, span)
        source, target = streamed[k]
        return pltpu.make_async_copy(source.at[rows], target.at[rows], block_sems.at[k, number])

    for number in range(tokens // span):
        for k in range(len(streamed)):
            block_copy(k, number).start()
    wholes = [
        pltpu.make_async_copy(source, target, whole_sems.at[k])
        for k, (source, target) in enumerate(((conv_h, conv), (ext_h, ext), (gz_h, gz), (wc_h, wc), (wg_h, wg)))
    ]
    for copy in wholes:
        copy.start()
    count = lax.axis_size("ctx")
    here, line = lax.axis_index("ctx"), lax.axis_index("exp")
    before = (lax.rem(here + count - 1, count), line)
    meet(places, before, (lax.rem(here + 1, count), line))
    rest.start()

    sums[...] = jnp.zeros_like(sums)
    rows_s[...] = jnp.zeros_like(rows_s)

    def first_block(number, unused):
        for k in range(len(streamed)):
            block_copy(k, number).wait()

        def some(index, unused_inner):
            at = pl.ds(pl.multiple_of(number * span + index * 16, 16), 16)
            for low in range(0, channels, LANES):
                lanes = slice(low, low + LANES)
                a, g, x, p = along[at, lanes], grad[at, lanes], xs[at, lanes].astype(jnp.float32), pre[at, lanes]
                small = jnp.exp(-jnp.abs(p))
                gated = jnp.where(p >= 0, 1.0, small) / (1.0 + small)
                step = jnp.maximum(p, 0.0) + jnp.log1p(small)
                value = (a * x + slope[at, lanes] * (1.0 / LOG2E)) * gated
                gdt[at, lanes] = value.astype(jnp.bfloat16)
                sums[0, :, lanes] += value[:8] + value[8:]
                both = g * x
                sums[1, :, lanes] += both[:8] + both[8:]
                along[at, lanes] = chan_ref[4:5, lanes] * g + a * step
            return unused_inner

        lax.fori_loop(0, span // 16, some, 0)
        return unused

    lax.fori_loop(0, tokens // span, first_block, 0)
    rows_s[25:26, :] = jnp.sum(sums[0], axis=0, keepdims=True)
    rows_s[26:27, :] = jnp.sum(sums[1], axis=0, keepdims=True)
    rows_s[8:24, :] = decay_ref[...]

    lane = lax.broadcasted_iota(jnp.int32, (tokens, LANES), 1)
    mixed = pltpu.roll(dot(gdt[...], mix_ref[...]), R, 1)
    projected = jnp.where(lane < R, mixed, jnp.where(lane < R + 2 * NS, bc_ref[...], 0.0)).astype(jnp.bfloat16)
    wholes[0].wait()
    wholes[1].wait()
    piece = 2 * LANES
    tail_row = lax.broadcasted_iota(jnp.int32, (tokens, piece), 0)

    def conv_piece(index, unused):
        lanes = pl.ds(pl.multiple_of(index * piece, piece), piece)
        some = pl.ds(pl.multiple_of(index * piece, piece), piece)
        total = along[:, lanes] + contract(projected, mix_ref[some, :], 1, 1)
        value = conv[:, lanes]
        gate = 1.0 / (1.0 + jnp.exp(-value))
        out = total * gate * (1.0 + value * (1.0 - gate))
        rows_s[24:25, lanes] = jnp.sum(out, axis=0, keepdims=True)
        before_rows = ext[:, lanes].astype(jnp.float32)
        rows_s[3:4, lanes] = jnp.sum(out * before_rows[EDGE:], axis=0, keepdims=True)
        result = chan_ref[3:4, lanes] * out
        beyond = jnp.zeros((8, piece), jnp.float32)
        for j in range(1, KC):
            same = jnp.concatenate([same_ref[j - 1]] * 2, axis=1)
            masked = out * same
            shifted_rows = pltpu.roll(before_rows, j, 0)[EDGE:]
            rows_s[3 - j : 4 - j, lanes] = jnp.sum(masked * shifted_rows, axis=0, keepdims=True)
            moved = chan_ref[3 - j : 4 - j, lanes] * pltpu.roll(masked, tokens - j, 0)
            result = result + jnp.where(tail_row < tokens - j, moved, 0.0)
            beyond = beyond + jnp.where(tail_row < tokens - j, 0.0, moved)[tokens - 8 :]
        gci[:, lanes] = result.astype(jnp.bfloat16)
        last[:, lanes] = result[tokens - 16 :]
        spill[:, lanes] = beyond
        return unused

    lax.fori_loop(0, channels // piece, conv_piece, 0)
    handed = pltpu.make_async_remote_copy(
        src_ref=spill,
        dst_ref=arrived,
        send_sem=spill_sems.at[0],
        recv_sem=spill_sems.at[1],
        device_id=before,
        device_id_type=MESH,
    )
    handed.start()

    cut = part_small.shape[-2]
    for index in range(channels // cut):
        spot = tuple(index // 2 ** (heads - 1 - k) % 2 for k in range(heads))
        if cut % LANES == 0:
            some = slice(index * cut, (index + 1) * cut)
            value = contract(xs[:, some], projected, 0, 0) + contract(gdt[:, some], delta_ref[...], 0, 0)
        else:
            pair = slice(index // 2 * 2 * cut, (index // 2 * 2 + 2) * cut)
            value = contract(xs[:, pair], projected, 0, 0) + contract(gdt[:, pair], delta_ref[...], 0, 0)
            value = value[index % 2 * cut : (index % 2 + 1) * cut]
        part_small[spot + (slice(None), slice(0, LANES))] = value.astype(jnp.bfloat16)
    columns = turned(jnp.concatenate([rows_s[...], jnp.zeros((LANES - rows_s.shape[0], channels), jnp.float32)], axis=0))
    for index in range(channels // cut):
        spot = tuple(index // 2 ** (heads - 1 - k) % 2 for k in range(heads))
        part_small[spot + (slice(None), slice(LANES, 2 * LANES))] = columns[index * cut : (index + 1) * cut].astype(jnp.bfloat16)

    handed.wait_recv()
    closing = last[...] + jnp.concatenate([jnp.zeros((8, channels), jnp.float32), arrived[...]], axis=0)
    gci[tokens - 16 :, :] = closing.astype(jnp.bfloat16)

    long = part_conv.shape[-2]

    def product_piece(index, unused):
        lanes = pl.ds(pl.multiple_of(index * piece, piece), piece)
        value = contract(normed_ref[...], gci[:, lanes], 0, 0)
        for block in range(value.shape[0] // long):
            spot = tuple(block // 2 ** (heads - 1 - k) % 2 for k in range(heads))
            part_conv[spot + (slice(None), lanes)] = value[block * long : (block + 1) * long].astype(jnp.bfloat16)
        return unused

    lax.fori_loop(0, channels // piece, product_piece, 0)
    flow.start()

    for copy in wholes[2:]:
        copy.wait()
    width = gn.shape[1]

    def normed_piece(index, unused):
        lanes = pl.ds(pl.multiple_of(index * piece, piece), piece)
        gn[:, lanes] = contract(gci[...], wc[lanes, :], 1, 1) + contract(gz[...], wg[lanes, :], 1, 1)
        return unused

    lax.fori_loop(0, width // piece, normed_piece, 0)
    wide_s[...] = wide_ref[...]
    gain = wide_ref[0:1, :]

    def back(index, total):
        at = pl.ds(pl.multiple_of(index * 16, 16), 16)
        x, g = in_ref[at, :].astype(jnp.float32), gn[at, :]
        scale = lax.rsqrt(jnp.mean(x * x, axis=-1, keepdims=True) + EPS)
        scaled = g * gain
        share_of = jnp.mean(x * scaled, axis=-1, keepdims=True)
        gi_ref[at, :] = resid_ref[at, :] + scale * scaled - x * (scale * scale * scale * share_of)
        value = g * (x * scale)
        return total + value[:8] + value[8:]

    total = lax.fori_loop(0, tokens // 16, back, jnp.zeros((8, width), jnp.float32))
    wide_s[0:1, :] = jnp.sum(total, axis=0, keepdims=True)
    flow.advance(0)
    filler = jnp.zeros((LANES - wide_s.shape[0], width), jnp.float32)
    columns = turned(jnp.concatenate([wide_s[...], filler], axis=0))
    short = part_wide.shape[-2]
    for block in range(width // short):
        spot = tuple(block // 2 ** (heads - 1 - k) % 2 for k in range(heads))
        part_wide[spot] = columns[block * short : (block + 1) * short].astype(jnp.bfloat16)
    flow3.start()
    rest.advance(0)
    for stage in range(1, len(places)):
        flow.advance(stage)
        flow3.advance(stage - 1)
        rest.advance(stage)
    flow3.advance(len(places) - 1)

    def columns_of(values):
        return jnp.concatenate([values, jnp.zeros((LANES - values.shape[0], LANES), jnp.float32)], axis=0).T

    size = tot_small.shape[0]
    first, second, wide = tot_small[:, :LANES], tot_small[:, LANES:], tot_wide[...]
    own_x[...] = first[:, : R + 2 * NS]
    own_dt[...] = columns_of(first)[R + 2 * NS :, :size]
    own_taps[...] = second[:, :KC]
    own_decay[...] = pltpu.roll(second, LANES - 8, 1)[:, :NS]
    own_rows[...] = columns_of(second)[24:32, :size]
    own_pair[...] = columns_of(wide)[0:8, : wide.shape[0]]
    own_router[...] = pltpu.roll(wide, LANES - 8, 1)[:, : own_router.shape[1]]
    flow.finish()
    flow3.finish()
    rest.finish()
    handed.wait_send()


def finish(sizes, streamed, inside_values, parts, experts, identity, span=64):
    places = bit_positions(sizes)
    stages = len(places)
    far = sorted(far_of(places))
    heads = sizes[0][1].bit_length() - 1
    tails = stages - heads
    along, slope, grad, pre, conv, xs, ext, gz, wc, wg = streamed
    normed = inside_values[0]
    tokens, channels = xs.shape
    width = normed.shape[1]
    devices = 2**stages
    half, wide = jnp.bfloat16, jnp.float32
    rows, thin = channels // devices, width // devices
    orders = [tuple(order) for order in orders_of(places)]
    conv_like = jax.ShapeDtypeStruct((width, channels), half)
    small_like = jax.ShapeDtypeStruct((channels, 2 * LANES), half)
    wide_like = jax.ShapeDtypeStruct((width, LANES), half)
    streams = halves((conv_like, small_like), *orders)
    third = halves((wide_like,), *orders)
    late = [(k, slice(0, part.shape[-1]), tuple(far_of(places))) for k, part in enumerate(parts)]

    def room(of, sizes_of):
        landing, blocks = [], []
        for array, cols, order in of:
            size, many = sizes_of[array], cols.stop - cols.start
            landing.append(pltpu.VMEM((2,) * (heads - 1) + (size * 2**tails, many), half))
            landing += [pltpu.VMEM((2,) * (stages - stage - 1) + (size, many), half) for stage in range(1, stages)]
            blocks.append(pltpu.VMEM((2,) * (stages - 1) + (size, many), half))
        return landing, blocks

    landing, blocks = room(streams, (thin, rows))
    landing3, blocks3 = room(third, (thin,))
    late_landing = landing_of(late, far, parts)
    marks = [len(landing), len(blocks), len(landing3), len(blocks3), len(late_landing)]
    inside = pl.BlockSpec(memory_space=pltpu.VMEM)
    anywhere = pl.BlockSpec(memory_space=pl.ANY)
    return pl.pallas_call(
        functools.partial(finish_kernel, places, streams, third, late, far, marks),
        in_specs=[anywhere] * 10 + [inside] * (len(inside_values) + 2),
        out_specs=[inside] * 11,
        out_shape=[
            jax.ShapeDtypeStruct(normed.shape, wide),
            jax.ShapeDtypeStruct((thin, channels), wide),
            jax.ShapeDtypeStruct(parts[0].shape[-2:], wide),
            jax.ShapeDtypeStruct(parts[1].shape[-2:], wide),
            jax.ShapeDtypeStruct((rows, R + 2 * NS), wide),
            jax.ShapeDtypeStruct((R, rows), wide),
            jax.ShapeDtypeStruct((rows, KC), wide),
            jax.ShapeDtypeStruct((rows, NS), wide),
            jax.ShapeDtypeStruct((8, rows), wide),
            jax.ShapeDtypeStruct((8, thin), wide),
            jax.ShapeDtypeStruct((thin, experts), wide),
        ],
        scratch_shapes=landing + blocks + landing3 + blocks3 + late_landing
        + [pltpu.VMEM(value.shape, value.dtype) for value in streamed]
        + [
            pltpu.VMEM((tokens, channels), half),
            pltpu.VMEM((tokens, channels), half),
            pltpu.VMEM((16, channels), wide),
            pltpu.VMEM((8, channels), wide),
            pltpu.VMEM((8, channels), wide),
            pltpu.VMEM((2, 8, channels), wide),
            pltpu.VMEM((32, channels), wide),
            pltpu.VMEM(inside_values[-1].shape, wide),
            pltpu.VMEM((tokens, width), wide),
            pltpu.VMEM((2,) * heads + (thin * 2**tails, channels), half),
            pltpu.VMEM((2,) * heads + (rows * 2**tails, 2 * LANES), half),
            pltpu.VMEM((2,) * heads + (thin * 2**tails, LANES), half),
            pltpu.VMEM((rows, 2 * LANES), wide),
            pltpu.VMEM((thin, LANES), wide),
            pltpu.SemaphoreType.DMA((5, tokens // span)),
            pltpu.SemaphoreType.DMA((5,)),
            pltpu.SemaphoreType.DMA((2,)),
        ]
        + flights(streams)
        + flights(third)
        + flights(late),
        compiler_params=pltpu.CompilerParams(
            collective_id=identity, has_side_effects=True, vmem_limit_bytes=56 * 1024 * 1024
        ),
        name="finish",
    )(*streamed, *inside_values, *parts)


def expert_kernel(slices, *refs):
    tokens_ref, grads_ref, column_ref, row_ref = refs[:4]
    even = range(0, slices, 2)
    odd = range(1, slices, 2)
    weights_in, weight_out = refs[4 : 4 + len(even)], refs[4 + len(even)]
    outs = refs[5 + len(even) :]
    picked_ref, back_ref, own_out = outs[:3]
    sums_in = outs[3 : 3 + len(even)]
    (sent, got, answer, returned, w_in, w_out, hidden, total, active, slope, inner, sum_out, pair_out, pair_in, far_out,
     send_sems, recv_sems, weight_sems, sum_sems, spread_sems, mate_sems, far_sems) = outs[3 + len(even) :]
    experts, room, width = sent.shape[1:]
    places = experts * room
    me = lax.axis_index("exp")
    here = lax.axis_index("ctx")
    levels = slices.bit_length() - 1

    loads = [pltpu.make_async_copy(weight_out, w_out.at[0], weight_sems.at[slices])]
    for k, s in enumerate(even):
        loads.append(pltpu.make_async_copy(weights_in[k], w_in.at[s], weight_sems.at[s]))
    for load in loads:
        load.start()

    barrier = pltpu.get_barrier_semaphore()
    mates = [partner(("ctx", level)) for level in range(levels)]
    for step in range(1, experts):
        pl.semaphore_signal(barrier, inc=1, device_id=(here, lax.rem(me + step, experts)), device_id_type=MESH)
    for mate in mates:
        pl.semaphore_signal(barrier, inc=1, device_id=mate, device_id_type=MESH)
    pl.semaphore_wait(barrier, experts - 1 + levels)

    def exchange(source, target, kind):
        copies = []
        for step in range(1, experts):
            peer = lax.rem(me + step, experts)
            copy = pltpu.make_async_remote_copy(
                src_ref=source.at[peer],
                dst_ref=target.at[me],
                send_sem=send_sems.at[kind, step],
                recv_sem=recv_sems.at[kind, step],
                device_id=(here, peer),
                device_id_type=MESH,
            )
            copy.start()
            copies.append(copy)
        target[me] = source[me]
        return copies

    def hand(source, target, sems, level):
        copy = pltpu.make_async_remote_copy(
            src_ref=source,
            dst_ref=target,
            send_sem=sems.at[0],
            recv_sem=sems.at[1],
            device_id=mates[level],
            device_id_type=MESH,
        )
        copy.start()
        return copy

    def arrive(copies):
        for copy in copies:
            copy.wait_recv()

    open_sends = []

    def spread(level):
        step = 2**level
        copies = [hand(w_out.at[s], w_out.at[s + step], spread_sems.at[1, s + step], level) for s in range(0, slices, 2 * step)]
        open_sends.extend(copies)
        return copies

    chooser = (lax.broadcasted_iota(jnp.int32, (places, row_ref.shape[1]), 0) == row_ref[...]).astype(jnp.float32).astype(jnp.bfloat16)
    sent[0] = dot(chooser, tokens_ref[...]).astype(jnp.bfloat16).reshape(experts, room, width)
    first = exchange(sent.at[0], got.at[0], 0)
    for load in loads:
        load.wait()
    widening = [spread(levels - 1)]
    paired = [hand(w_in.at[s], w_in.at[s + 1], spread_sems.at[0, s], 0) for s in even]
    sent[1] = dot(chooser, grads_ref[...]).astype(jnp.bfloat16).reshape(experts, room, width)
    second = exchange(sent.at[1], got.at[1], 1)

    arrive(first)
    rows = got[0].reshape(places, width)
    for s in list(even) + list(odd):
        if s == 1:
            arrive(paired)
        hidden[...] = dot(rows, w_in[s])

        def curve(index, unused):
            at = pl.ds(pl.multiple_of(index * ROWS_AT_ONCE, ROWS_AT_ONCE), ROWS_AT_ONCE)
            value = hidden[at, :]
            bell = 0.5 + 0.5 * lax.erf(value * 0.7071067811865476)
            active[s, at, :] = (value * bell).astype(jnp.bfloat16)
            slope[s, at, :] = bell + value * (jnp.exp(-0.5 * value * value) * 0.3989422804014327)
            return unused

        lax.fori_loop(0, places // ROWS_AT_ONCE, curve, 0)

    for level in reversed(range(levels - 1)):
        arrive(widening[-1])
        widening.append(spread(level))
    for s in list(even) + list(odd):
        if s == 1:
            arrive(widening[-1])
        product = dot(active[s], w_out[s])
        total[...] = product if s == 0 else total[...] + product
    answer[0] = total[...].astype(jnp.bfloat16).reshape(experts, room, width)
    third = exchange(answer.at[0], returned.at[0], 2)

    arrive(second)
    pulled = got[1].reshape(places, width)
    joining = []
    for s in list(odd) + list(even):
        sum_out[s] = contract(active[s], pulled, 0, 0).astype(jnp.bfloat16)
        if s % 2:
            joining.append(hand(sum_out.at[s], pair_out.at[s // 2], mate_sems.at[0, s // 2], 0))
    for s in range(slices):
        inner[s] = (contract(pulled, w_out[s], 1, 1) * slope[s]).astype(jnp.bfloat16)
        product = contract(inner[s], w_in[s], 1, 1)
        total[...] = product if s == 0 else total[...] + product
    answer[1] = total[...].astype(jnp.bfloat16).reshape(experts, room, width)
    fourth = exchange(answer.at[1], returned.at[1], 3)

    def add_into(target, addend):
        def some(index, unused):
            at = pl.ds(pl.multiple_of(index * 4 * ROWS_AT_ONCE, 4 * ROWS_AT_ONCE), 4 * ROWS_AT_ONCE)
            target[at, :] = (target[at, :].astype(jnp.float32) + addend[at, :].astype(jnp.float32)).astype(jnp.bfloat16)
            return unused

        lax.fori_loop(0, target.shape[0] // (4 * ROWS_AT_ONCE), some, 0)

    arrive(joining)
    for k, s in enumerate(even):
        add_into(sum_out.at[s], pair_out.at[k])

    def pass_on(level):
        step = 2**level
        return [
            hand(sum_out.at[s + step], far_out.at[slices // step // 2 - 1 + s // (2 * step)], far_sems.at[level, s // (2 * step)], level)
            for s in range(0, slices, 2 * step)
        ]

    passing = pass_on(1)
    open_sends.extend(joining)
    for copy in paired:
        copy.wait_send()
    joined = []
    for s in list(odd) + list(even):
        w_in[s] = contract(rows, inner[s], 0, 0).astype(jnp.bfloat16)
        if s % 2:
            joined.append(hand(w_in.at[s], pair_in.at[s // 2], mate_sems.at[1, s // 2], 0))
    arrive(joined)
    stores = []
    for k, s in enumerate(even):
        add_into(w_in.at[s], pair_in.at[k])
        stores.append(pltpu.make_async_copy(w_in.at[s], sums_in[k], sum_sems.at[k]))
        stores[-1].start()

    finder = (lax.broadcasted_iota(jnp.int32, (column_ref.shape[0], places), 1) == column_ref[...]).astype(jnp.float32).astype(jnp.bfloat16)
    arrive(third)
    picked_ref[...] = dot(finder, returned[0].reshape(places, width)).astype(jnp.bfloat16)
    for level in range(1, levels):
        arrive(passing)
        open_sends.extend(passing)
        step = 2**level
        if level + 1 < levels:
            for s in range(0, slices, 2 * step):
                add_into(sum_out.at[s], far_out.at[slices // step // 2 - 1 + s // (2 * step)])
            passing = pass_on(level + 1)
    own_out[...] = sum_out[0].astype(jnp.float32) + far_out[0].astype(jnp.float32)
    arrive(fourth)
    back_ref[...] = dot(finder, returned[1].reshape(places, width)).astype(jnp.bfloat16)
    for store in stores:
        store.wait()
    for copies in (first, second, third, fourth, joined, open_sends):
        for copy in copies:
            copy.wait_send()


def run_experts(rows, grads, target, weights_in, weight_out, experts, room, identity):
    slices = 2 * len(weights_in)
    tokens, width = rows.shape
    inner_width = weight_out.shape[0]
    places = experts * room
    inside = pl.BlockSpec(memory_space=pltpu.VMEM)
    anywhere = pl.BlockSpec(memory_space=pl.ANY)
    half = jnp.bfloat16
    count = len(weights_in)
    out = pl.pallas_call(
        functools.partial(expert_kernel, slices),
        in_specs=[inside] * 4 + [anywhere] * (count + 1),
        out_specs=[inside] * 3 + [anywhere] * count,
        out_shape=[jax.ShapeDtypeStruct(rows.shape, half)] * 2
        + [jax.ShapeDtypeStruct(weight_out.shape, jnp.float32)]
        + [jax.ShapeDtypeStruct(weight.shape, half) for weight in weights_in],
        scratch_shapes=[pltpu.VMEM((2, experts, room, width), half)] * 4
        + [
            pltpu.VMEM((slices, width, inner_width), half),
            pltpu.VMEM((slices, inner_width, width), half),
            pltpu.VMEM((places, inner_width), jnp.float32),
            pltpu.VMEM((places, width), jnp.float32),
            pltpu.VMEM((slices, places, inner_width), half),
            pltpu.VMEM((slices, places, inner_width), jnp.float32),
            pltpu.VMEM((slices, places, inner_width), half),
            pltpu.VMEM((slices, inner_width, width), half),
            pltpu.VMEM((count, inner_width, width), half),
            pltpu.VMEM((count, width, inner_width), half),
            pltpu.VMEM((count, inner_width, width), half),
            pltpu.SemaphoreType.DMA((4, experts)),
            pltpu.SemaphoreType.DMA((4, experts)),
            pltpu.SemaphoreType.DMA((slices + 1,)),
            pltpu.SemaphoreType.DMA((count,)),
            pltpu.SemaphoreType.DMA((2, slices, 2)),
            pltpu.SemaphoreType.DMA((2, count, 2)),
            pltpu.SemaphoreType.DMA((slices, count, 2)),
        ],
        compiler_params=pltpu.CompilerParams(
            collective_id=identity, has_side_effects=True, vmem_limit_bytes=60 * 1024 * 1024
        ),
        name="run_experts",
    )(rows, grads, target[:, None], target[None, :], *weights_in, weight_out)
    return out[0], out[1], list(out[3:]), out[2]


def flipped(value, level):
    count = lax.axis_size("ctx")
    return lax.ppermute(value, "ctx", [(source, source ^ (1 << level)) for source in range(count)])


def spread_slices(own):
    levels = lax.axis_size("ctx").bit_length() - 1
    slices = {0: own}
    for level in reversed(range(1, levels)):
        for offset in sorted(slices):
            slices[offset + (1 << level)] = flipped(slices[offset], level)
    return [slices[offset] for offset in sorted(slices)]


def collect_slices(sums):
    levels = lax.axis_size("ctx").bit_length() - 1
    for level in range(1, levels):
        arrived = [flipped(values, level).astype(jnp.float32) for values in sums[1::2]]
        sums = [values.astype(jnp.float32) + other for values, other in zip(sums[::2], arrived)]
        if level + 1 < levels:
            sums = [values.astype(jnp.bfloat16) for values in sums]
    return sums[0]


def body(
    inputs,
    segments,
    routes,
    cotangent,
    norm_gain,
    in_proj,
    conv_taps,
    conv_bias,
    x_proj,
    dt_proj,
    dt_bias,
    log_decay,
    skip_gain,
    out_proj,
    moe_gain,
    router,
    expert_in,
    expert_out,
):
    experts = router.shape[1]
    half_rows = norm_gain.shape[0]
    half = jnp.bfloat16
    channel_part = jnp.concatenate(
        [
            x_proj,
            dt_proj.T,
            conv_taps,
            jnp.zeros((2 * half_rows, 4), half),
            log_decay,
            jnp.stack([conv_bias, dt_bias, skip_gain], axis=1),
            jnp.zeros((2 * half_rows, LANES - 27), half),
        ],
        axis=1,
    )
    width_part = jnp.concatenate(
        [
            jnp.stack([norm_gain, moe_gain], axis=1),
            jnp.zeros((half_rows, 6), half),
            router,
            jnp.zeros((half_rows, LANES - 8 - experts), half),
        ],
        axis=1,
    )
    sizes = [(name, lax.axis_size(name)) for name in ("ctx", "exp")]
    tail_ids = segments[0, -EDGE:, None].astype(jnp.bfloat16)
    edge = jnp.concatenate([inputs[0, -EDGE:], jnp.broadcast_to(tail_ids, (EDGE, LANES))], axis=1)
    (full_conv, full_channel, full_width), partial, prior = gather_all(
        sizes, (in_proj[:, :DI], channel_part, width_part), (in_proj[:, DI:], out_proj), edge, 0
    )
    later_in, full_channel = lax.optimization_barrier((expert_in[0], full_channel))
    weights_in = spread_slices(later_in)
    mix = full_channel[:, :LANES]
    full_xproj, full_dt = mix[:, : R + 2 * NS], mix[:, R + 2 * NS :].T
    by_channel = full_channel[:, LANES:].T
    full_taps, full_decay = by_channel[:KC].T, by_channel[8 : 8 + NS].T
    full_bias, full_dtbias, full_skip = by_channel[24], by_channel[25], by_channel[26]
    full_norm, full_moe, full_router = full_width[:, 0], full_width[:, 1], full_width[:, 8 : 8 + experts]
    tokens_here = inputs.shape[1]
    capacity = 5 * tokens_here // (4 * experts)
    flat_in = inputs[0].astype(jnp.float32)
    seg_row = segments[0]
    position = lax.axis_index("ctx")
    normed_one = rms_scale(flat_in, full_norm.astype(jnp.float32)).astype(jnp.bfloat16)
    conv_in = dot(normed_one, full_conv).astype(jnp.bfloat16)
    edge_one = rms_scale(prior[:, :D].astype(jnp.float32), full_norm.astype(jnp.float32)).astype(jnp.bfloat16)
    edge_all = dot(edge_one, full_conv).astype(jnp.bfloat16)
    edge_rows = edge_all[EDGE - (KC - 1) :]
    prior_ids = jnp.where(position > 0, prior[EDGE - (KC - 1) :, D].astype(jnp.int32), -1)
    ext_ids = jnp.concatenate([prior_ids, seg_row])
    ext_rows = jnp.concatenate([edge_rows, conv_in], axis=0).astype(jnp.float32)
    conv_out = conv_local(ext_rows, full_taps.astype(jnp.float32), full_bias.astype(jnp.float32), ext_ids)
    xs_val = jax.nn.silu(conv_out).astype(jnp.bfloat16)
    xs_wide = xs_val.astype(jnp.float32)
    projected = jnp.dot(xs_val, full_xproj, preferred_element_type=jnp.float32)
    delta_low = projected[:, :R].astype(jnp.bfloat16)
    b_rows = projected[:, R : R + NS]
    c_rows = projected[:, R + NS :]
    dt_pre = jnp.dot(delta_low, full_dt, preferred_element_type=jnp.float32) + full_dtbias.astype(
        jnp.float32
    )
    step_size = jax.nn.softplus(dt_pre)
    a_swap = -jnp.exp(full_decay.astype(jnp.float32)).T
    earlier = jnp.concatenate([prior_ids[KC - 2 :], seg_row[:-1]])
    keep_mask = (earlier == seg_row).astype(jnp.float32)
    push = step_size * xs_wide
    masked_step = jnp.where(keep_mask[:, None] > 0, step_size, 1e30)
    rates = a_swap * LOG2E
    b_turned, c_turned = b_rows.T, c_rows.T
    push, *weights_in = lax.optimization_barrier((push, *weights_in))
    scan_rows, start_state, products, kept, (full_gate, full_out) = scan_forward(
        sizes, masked_step, push, b_turned, c_turned, rates, partial, 3
    )
    gate_z = dot(normed_one, full_gate)
    skip_wide = full_skip.astype(jnp.float32)
    scanned_y = scan_rows + skip_wide * xs_wide
    gated_wide, gated_pull = jax.vjp(
        lambda scan_in, gate_in: scan_in * jax.nn.silu(gate_in), scanned_y, gate_z
    )
    gated = gated_wide.astype(jnp.bfloat16)
    mixed = jnp.dot(gated, full_out, preferred_element_type=jnp.float32)
    residual = flat_in + mixed
    norm_two_value, norm_two_pull = jax.vjp(rms_scale, residual, full_moe.astype(jnp.float32))
    normed_two = norm_two_value.astype(jnp.bfloat16)
    logits = jnp.dot(normed_two, full_router, preferred_element_type=jnp.float32)
    probability = jax.nn.softmax(logits, axis=-1)
    route_ids = routes[0, :, 0]
    one_hot = route_ids[:, None] == jnp.arange(experts, dtype=jnp.int32)[None, :]
    one_float = one_hot.astype(jnp.float32)
    gate_val = jnp.sum(probability * one_float, axis=1)
    running = jnp.cumsum(one_hot.astype(jnp.int32), axis=0)
    slot_index = jnp.sum(running * one_hot.astype(jnp.int32), axis=1) - 1
    room = -(-capacity // 16) * 16
    target = route_ids * room + slot_index
    grad_out = cotangent[0].astype(jnp.float32)
    grad_pick = (grad_out * gate_val[:, None]).astype(jnp.bfloat16)
    picked, grad_from_experts, grad_expert_in, grad_w_out = run_experts(
        normed_two, grad_pick, target, weights_in, expert_out[0], experts, room, 2
    )
    grad_w_in = collect_slices(grad_expert_in)
    picked = picked.astype(jnp.float32)
    grad_from_experts = grad_from_experts.astype(jnp.float32)
    outcome = residual + gate_val[:, None] * picked
    out_block = outcome.astype(jnp.bfloat16)[None]
    grad_gate = jnp.sum(grad_out * picked, axis=1)
    grad_probs = grad_gate[:, None] * one_float
    grad_logits = (
        probability * (grad_probs - jnp.sum(grad_probs * probability, axis=1, keepdims=True))
    ).astype(jnp.bfloat16)
    grad_router = contract(grad_logits, normed_two, 0, 0)
    grad_normed_two = grad_from_experts + jnp.dot(
        grad_logits, full_router.T, preferred_element_type=jnp.float32
    )
    grad_resid_norm, grad_moe_gain = norm_two_pull(grad_normed_two)
    grad_resid = grad_out + grad_resid_norm
    grad_mixed = grad_resid.astype(jnp.bfloat16)
    grad_gated = jnp.dot(grad_mixed, full_out.T, preferred_element_type=jnp.float32)
    grad_out_proj = jnp.dot(gated.T, grad_mixed, preferred_element_type=jnp.float32)
    grad_y, grad_z = gated_pull(grad_gated)
    grad_z = grad_z.astype(jnp.bfloat16)
    grad_y, grad_w_in = lax.optimization_barrier((grad_y, grad_w_in))
    along_b, slope, grad_bs, grad_cs, grad_a, partial_sums = scan_backward(
        sizes,
        masked_step,
        push,
        grad_y,
        b_turned,
        c_turned,
        rates,
        products,
        (dot(normed_one.T, grad_z).astype(jnp.bfloat16), grad_out_proj.astype(jnp.bfloat16)),
        kept,
        4,
    )
    same_rows = jnp.stack(
        [(ext_ids[KC - 1 - j : KC - 1 - j + tokens_here] == seg_row).astype(jnp.float32) for j in range(1, KC)]
    )
    wide_rows = jnp.concatenate(
        [full_norm.astype(jnp.float32)[None], grad_moe_gain[None], jnp.zeros((6, D), jnp.float32), grad_router]
    )
    grad_inputs, own_conv, own_gate, own_out, own_x, own_dt, own_taps, own_decay, own_rows, own_pair, own_router = finish(
        sizes,
        (
            along_b,
            slope,
            grad_y,
            dt_pre,
            conv_out,
            xs_val,
            jnp.concatenate([edge_all, conv_in], axis=0),
            grad_z,
            full_conv,
            full_gate,
        ),
        (
            normed_one,
            inputs[0],
            grad_resid,
            mix,
            jnp.pad(jnp.concatenate([grad_bs, grad_cs], axis=1), ((0, 0), (R, LANES - R - 2 * NS))),
            jnp.pad(delta_low, ((0, 0), (R + 2 * NS, 0))),
            jnp.broadcast_to(same_rows[:, :, None], (KC - 1, tokens_here, LANES)),
            jnp.concatenate([by_channel[:KC], by_channel[26:27], jnp.zeros((3, DI), half)]).astype(jnp.float32),
            grad_a * a_swap,
            wide_rows,
        ),
        partial_sums,
        experts,
        1,
    )
    return (
        out_block,
        grad_inputs[None],
        own_pair[0],
        jnp.concatenate([own_conv, own_gate], axis=1),
        own_taps,
        own_rows[0],
        own_x,
        own_dt,
        own_rows[1],
        own_decay,
        own_rows[2],
        own_out,
        own_pair[1],
        own_router,
        grad_w_in[None],
        grad_w_out[None],
    )


def solution(mesh):
    placed = (
        P("exp", "ctx", None),
        P("exp", "ctx"),
        P("exp", "ctx", None),
        P("exp", "ctx", None),
        P(("ctx", "exp")),
        P(("ctx", "exp"), None),
        P(("ctx", "exp"), None),
        P(("ctx", "exp")),
        P(("ctx", "exp"), None),
        P(None, ("ctx", "exp")),
        P(("ctx", "exp")),
        P(("ctx", "exp"), None),
        P(("ctx", "exp")),
        P(("ctx", "exp"), None),
        P(("ctx", "exp")),
        P(("ctx", "exp"), None),
        P("exp", None, "ctx"),
        P("exp", "ctx", None),
    )
    return jax.shard_map(
        body,
        mesh=mesh,
        in_specs=placed,
        out_specs=(
            P("exp", "ctx", None),
            P("exp", "ctx", None),
            P(("ctx", "exp")),
            P(("ctx", "exp"), None),
            P(("ctx", "exp"), None),
            P(("ctx", "exp")),
            P(("ctx", "exp"), None),
            P(None, ("ctx", "exp")),
            P(("ctx", "exp")),
            P(("ctx", "exp"), None),
            P(("ctx", "exp")),
            P(("ctx", "exp"), None),
            P(("ctx", "exp")),
            P(("ctx", "exp"), None),
            P("exp", None, "ctx"),
            P("exp", "ctx", None),
        ),
        check_vma=False,
    )
```

```python
import functools

import jax
import jax.numpy as jnp
from jax import lax
from jax.experimental import pallas as pl
from jax.experimental.pallas import tpu as pltpu
from jax.sharding import PartitionSpec as P

D = 768
DI = 1536
NS = 16
R = 48
KC = 4
LANES = 128
UNROLL = 8
LOG2E = 1.4426950408889634


EPS = 1e-05
MESH = pl.DeviceIdType.MESH
ROWS_AT_ONCE = 16
EDGE = 16

def tile(ref, base, lanes):
    return ref[pl.ds(pl.multiple_of(base, UNROLL), UNROLL), lanes]

def row(rows_now, place):
    return jnp.broadcast_to(rows_now[place : place + 1], (NS, LANES))

def put_row(rows_now, place, value):
    at = lax.broadcasted_iota(jnp.int32, (UNROLL, LANES), 0)
    value = jnp.broadcast_to(value, (UNROLL, LANES))
    return value if rows_now is None else jnp.where(at == place, value, rows_now)

def cost(tokens, channels, share):
    size = tokens * channels * NS
    return pl.CostEstimate(flops=size * share, transcendentals=size, bytes_accessed=size * share)


def pick(channels):
    return 512 if channels % 512 == 0 else 128


def rms_scale(values, gain):
    return values * lax.rsqrt(jnp.mean(values * values, axis=-1, keepdims=True) + EPS) * gain


def bit_positions(sizes):
    return [(axis, size.bit_length() - 2 - k) for axis, size in sizes for k in range(size.bit_length() - 1)]


def own_bit(place):
    axis, level = place
    return lax.rem(lax.axis_index(axis) // 2**level, 2)


def partner(place):
    axis, level = place
    where = {"ctx": lax.axis_index("ctx"), "exp": lax.axis_index("exp")}
    where[axis] = where[axis] + (1 - 2 * own_bit(place)) * 2**level
    return (where["ctx"], where["exp"])


def meet(places, *others):
    barrier = pltpu.get_barrier_semaphore()
    for device in [partner(place) for place in places] + list(others):
        pl.semaphore_signal(barrier, inc=1, device_id=device, device_id_type=MESH)
    pl.semaphore_wait(barrier, len(places) + len(others))


class GatherFlow:
    def __init__(self, places, streams, dims, shards, wholes, send_sems, recv_sems, local_sems):
        self.places, self.streams, self.dims, self.shards, self.wholes = places, streams, dims, shards, wholes
        self.sems = send_sems, recv_sems, local_sems
        self.bits = [own_bit(place) for place in places]

    def view(self, number, have):
        array, cols, order, begin = self.streams[number]
        index = tuple(slice(None) if p in have else self.bits[p] for p in self.dims)
        return self.wholes[array].at[index + (slice(None), cols)]

    def shard(self, number):
        array, cols, order, begin = self.streams[number]
        return self.shards[array].at[(slice(None),) * (begin + 1) + (cols,)]

    def own(self, number):
        array, cols, order, begin = self.streams[number]
        return pltpu.make_async_copy(self.shard(number), self.view(number, order[:begin]), self.sems[2].at[number])

    def flight(self, number, stage):
        array, cols, order, begin = self.streams[number]
        target = self.view(number, order[: begin + stage])
        return pltpu.make_async_remote_copy(
            src_ref=self.shard(number) if stage == 0 else target,
            dst_ref=target,
            send_sem=self.sems[0].at[number, stage],
            recv_sem=self.sems[1].at[number, stage],
            device_id=partner(self.places[order[begin + stage]]),
            device_id_type=MESH,
        )

    def stages(self, number):
        array, cols, order, begin = self.streams[number]
        return len(order) - begin

    def start(self):
        for number in range(len(self.streams)):
            self.flight(number, 0).start()
        for number in range(len(self.streams)):
            self.own(number).start()

    def advance(self, stage):
        for number in range(len(self.streams)):
            if stage >= self.stages(number):
                continue
            if stage == 0:
                self.own(number).wait()
            self.flight(number, stage).wait_recv()
            if stage + 1 < self.stages(number):
                self.flight(number, stage + 1).start()

    def finish(self):
        for number in range(len(self.streams)):
            for stage in range(self.stages(number)):
                self.flight(number, stage).wait_send()


def pack_small(x_ref, dt_ref, rows_ref, thin_ref, square, channel_pack, width_pack):
    def laid(values):
        square[...] = jnp.zeros_like(square)
        square[: values.shape[0], : values.shape[1]] = values.astype(jnp.float32)
        return square[...]

    rows, thin = channel_pack.shape[0], width_pack.shape[0]
    dt_part = pltpu.roll(laid(dt_ref[...]).T, R + 2 * NS, 1)
    mix = laid(x_ref[...]) + dt_part
    channel_pack[:, :LANES] = mix[:rows].astype(jnp.bfloat16)
    channel_pack[:, LANES:] = laid(rows_ref[...]).T[:rows].astype(jnp.bfloat16)
    width_pack[...] = laid(thin_ref[...]).T[:thin].astype(jnp.bfloat16)


def gather_kernel(places, streams, extra_streams, far, extra, *refs):
    x_ref, dt_ref, rows_ref, thin_ref, conv_ref = refs[:5]
    edge_ref = refs[5 + extra]
    wholes, prior_ref = refs[6 + extra : 9 + 2 * extra], refs[9 + 2 * extra]
    (square, channel_pack, width_pack, send_sems, recv_sems, local_sems, late_send, late_recv, late_local,
     edge_sems) = refs[10 + 2 * extra :]
    count = 3
    shards = (conv_ref, channel_pack, width_pack) + tuple(refs[5 : 5 + extra])
    pack_small(x_ref, dt_ref, rows_ref, thin_ref, square, channel_pack, width_pack)
    flow = GatherFlow(
        places, streams, range(len(places)), shards[:count], wholes[:count], send_sems, recv_sems, local_sems
    )
    late = GatherFlow(
        places, extra_streams, far, shards[count:], wholes[count:], late_send, late_recv, late_local
    )
    blocks = lax.axis_size("ctx")
    here, line = lax.axis_index("ctx"), lax.axis_index("exp")
    meet(places, (lax.rem(here + 1, blocks), line), (lax.rem(here + blocks - 1, blocks), line))
    flow.start()
    edge = pltpu.make_async_remote_copy(
        src_ref=edge_ref,
        dst_ref=prior_ref,
        send_sem=edge_sems.at[0],
        recv_sem=edge_sems.at[1],
        device_id=(lax.rem(here + 1, blocks), line),
        device_id_type=MESH,
    )
    edge.start()
    stages, behind = len(places), len(far)
    for stage in range(stages):
        flow.advance(stage)
        if stage == behind - 2:
            late.start()
        if stage >= behind and stage - behind < behind:
            late.advance(stage - behind)
    for stage in range(stages - behind, behind):
        late.advance(stage)
    flow.finish()
    late.finish()
    edge.wait()


def orders_of(places):
    core = places.index(("ctx", 0))
    rows = [k for k, place in enumerate(places) if place[0] == "ctx" and place[1] > 0]
    near = places.index(("exp", 0))
    return [core] + rows + [near] + far_of(places), [core, near] + rows + far_of(places)


def far_of(places):
    return [k for k, place in sorted(enumerate(places), key=lambda item: item[1][1]) if place[0] == "exp" and place[1] > 0]


def halves(arrays, first, second, begin=None):
    streams = []
    for array, values in enumerate(arrays):
        width = values.shape[-1]
        rest = () if begin is None else (begin,)
        if width % 256 == 0:
            streams.append((array, slice(0, width // 2), first) + rest)
            streams.append((array, slice(width // 2, width), second) + rest)
        else:
            streams.append((array, slice(0, width), first if array % 2 else second) + rest)
    return streams


def gather_orders(places):
    return [tuple(reversed(order)) for order in orders_of(places)]


def gather_all(sizes, small, conv_half, extra, edge, identity):
    places = bit_positions(sizes)
    stages = len(places)
    far = sorted(far_of(places))
    half = jnp.bfloat16
    rows, thin = small[0].shape[0], conv_half.shape[0]
    shards = (
        conv_half,
        jax.ShapeDtypeStruct((rows, 2 * LANES), half),
        jax.ShapeDtypeStruct((thin, LANES), half),
    )
    streams = halves(shards, *gather_orders(places), begin=0)
    late = [(k, slice(0, part.shape[1]), tuple(reversed(far_of(places))), 0) for k, part in enumerate(extra)]
    anywhere = pl.BlockSpec(memory_space=pl.ANY)
    inside = pl.BlockSpec(memory_space=pltpu.VMEM)
    total = len(shards) + len(extra)
    *wholes, prior = pl.pallas_call(
        functools.partial(gather_kernel, places, streams, late, far, len(extra)),
        in_specs=[inside] * 4 + [anywhere] * (2 + len(extra)),
        out_specs=[anywhere] * (total + 1),
        out_shape=[jax.ShapeDtypeStruct((2,) * stages + shard.shape, shard.dtype) for shard in shards]
        + [jax.ShapeDtypeStruct((2,) * len(far) + part.shape, part.dtype) for part in extra]
        + [jax.ShapeDtypeStruct(edge.shape, edge.dtype)],
        scratch_shapes=[
            pltpu.VMEM((LANES, LANES), jnp.float32),
            pltpu.VMEM((rows, 2 * LANES), half),
            pltpu.VMEM((thin, LANES), half),
            pltpu.SemaphoreType.DMA((len(streams), stages)),
            pltpu.SemaphoreType.DMA((len(streams), stages)),
            pltpu.SemaphoreType.DMA((len(streams),)),
            pltpu.SemaphoreType.DMA((len(late), len(far))),
            pltpu.SemaphoreType.DMA((len(late), len(far))),
            pltpu.SemaphoreType.DMA((len(late),)),
            pltpu.SemaphoreType.DMA((2,)),
        ],
        compiler_params=pltpu.CompilerParams(collective_id=identity, has_side_effects=True),
        name="gather_all",
    )(*small, conv_half, *extra, edge)
    ready = [whole.reshape((-1,) + whole.shape[stages + 1 :]) for whole in wholes[: len(shards)]]
    return ready, wholes[len(shards) :], prior


class ReduceFlow:
    def __init__(self, places, streams, dims, parts, totals, landing, send_sems, recv_sems):
        self.places, self.streams, self.dims, self.parts, self.totals = places, streams, dims, parts, totals
        self.landing, self.sems = landing, (send_sems, recv_sems)
        self.bits = [own_bit(place) for place in places]
        self.first = []
        for array, cols, order in streams:
            self.first.append(sum(len(other[2]) for other in streams[: len(self.first)]))

    def spot(self, number, stage):
        return self.landing[self.first[number] + stage]

    def side(self, number, stage, value):
        array, cols, order = self.streams[number]
        left = [p for p in self.dims if p not in order[:stage]]
        index = tuple(value if p == order[stage] else slice(None) for p in left)
        if stage == 0:
            return self.parts[array].at[index + (slice(None), cols)]
        return self.spot(number, stage - 1).at[index]

    def flight(self, number, stage):
        order = self.streams[number][2]
        return pltpu.make_async_remote_copy(
            src_ref=self.side(number, stage, 1 - self.bits[order[stage]]),
            dst_ref=self.spot(number, stage),
            send_sem=self.sems[0].at[number, stage],
            recv_sem=self.sems[1].at[number, stage],
            device_id=partner(self.places[order[stage]]),
            device_id_type=MESH,
        )

    def start(self):
        for number in range(len(self.streams)):
            self.flight(number, 0).start()

    def advance(self, stage):
        for number, (array, cols, order) in enumerate(self.streams):
            if stage >= len(order):
                continue
            self.flight(number, stage).wait_recv()
            mine = self.side(number, stage, self.bits[order[stage]])
            there = self.spot(number, stage)
            depth = len(self.dims) - stage - 1
            final = stage + 1 == len(order)
            if depth == 0:
                self.totals[array][:, cols] = there[...].astype(jnp.float32) + mine[...].astype(jnp.float32)
                continue

            def add(index, unused, there=there, mine=mine, depth=depth, final=final, array=array, cols=cols):
                at = tuple(lax.rem(index // 2 ** (depth - 1 - k), 2) for k in range(depth))
                value = (there[at].astype(jnp.float32) + mine[at].astype(jnp.float32)).astype(there.dtype)
                if final:
                    self.totals[array][at + (slice(None), cols)] = value
                else:
                    there[at] = value
                return unused

            lax.fori_loop(0, 2**depth, add, 0)
            if not final:
                self.flight(number, stage + 1).start()

    def finish(self):
        for number in range(len(self.streams)):
            for stage in range(len(self.streams[number][2])):
                self.flight(number, stage).wait_send()


def landing_of(streams, dims, divided):
    landing = []
    for array, cols, order in streams:
        for stage in range(len(order)):
            rows = divided[array].shape[-2]
            landing.append(pltpu.VMEM((2,) * (len(dims) - stage - 1) + (rows, cols.stop - cols.start), jnp.bfloat16))
    return landing


def flights(streams):
    shape = (len(streams), max(len(order) for array, cols, order in streams))
    return [pltpu.SemaphoreType.DMA(shape)] * 2


def dot(left, right):
    return jnp.dot(left, right, preferred_element_type=jnp.float32)


def contract(left, right, left_dim, right_dim):
    return lax.dot_general(left, right, (((left_dim,), (right_dim,)), ((), ())), preferred_element_type=jnp.float32)


def lanes_of(group, width, k):
    return pl.ds(pl.multiple_of(group * width + k * LANES, LANES), LANES)


def spread_columns(source_ref, wide_ref):
    def chunk(index, unused):
        base = pl.multiple_of(index * LANES, LANES)
        now = source_ref[:, pl.ds(base, LANES)]
        for place in range(LANES):
            wide_ref[base + place] = jnp.broadcast_to(now[:, place : place + 1], (NS, LANES))
        return unused

    lax.fori_loop(0, source_ref.shape[1] // LANES, chunk, 0)


def end_pass(width, step_ref, push_ref, wide_b, rate_ref, state_ref, hook):
    rows, channels = step_ref.shape
    count = width // LANES

    def group_body(group, unused):
        pieces = [lanes_of(group, width, k) for k in range(count)]
        rates = [rate_ref[:, lanes] for lanes in pieces]

        def block(index, states):
            states = list(states)
            steps = [tile(step_ref, index * UNROLL, lanes) for lanes in pieces]
            pushes = [tile(push_ref, index * UNROLL, lanes) for lanes in pieces]
            for place in range(UNROLL):
                b_now = wide_b[index * UNROLL + place]
                for k in range(count):
                    decay = jnp.exp2(row(steps[k], place) * rates[k])
                    states[k] = decay * states[k] + b_now * row(pushes[k], place)
            return tuple(states)

        zero = jnp.zeros((NS, LANES), jnp.float32)
        states = lax.fori_loop(0, rows // UNROLL, block, (zero,) * count)
        for k, lanes in enumerate(pieces):
            state_ref[:, lanes] = states[k]
        hook(group)
        return unused

    lax.fori_loop(0, channels // width, group_body, 0)


def out_pass(width, step_ref, push_ref, wide_b, wide_c, rate_ref, state_ref, y_ref, kept_buf, kept_copy, hook):
    rows, channels = step_ref.shape
    count = width // LANES
    span = kept_buf.shape[1]
    blocks = rows // span

    def time_body(number, unused):
        slot = lax.rem(number, 2)

        @pl.when(number >= 2)
        def _():
            kept_copy(number - 2, slot).wait()

        def group_body(group, unused_inner):
            pieces = [lanes_of(group, width, k) for k in range(count)]
            rates = [rate_ref[:, lanes] for lanes in pieces]

            def block(index, states):
                states = list(states)
                base = number * span + index * UNROLL
                steps = [tile(step_ref, base, lanes) for lanes in pieces]
                pushes = [tile(push_ref, base, lanes) for lanes in pieces]
                outs = [None] * count
                for place in range(UNROLL):
                    b_now = wide_b[base + place]
                    c_now = wide_c[base + place]
                    for k, lanes in enumerate(pieces):
                        decay = jnp.exp2(row(steps[k], place) * rates[k])
                        states[k] = decay * states[k] + b_now * row(pushes[k], place)
                        kept_buf[slot, index * UNROLL + place, :, lanes] = states[k].astype(kept_buf.dtype)
                        outs[k] = put_row(outs[k], place, jnp.sum(states[k] * c_now, axis=0, keepdims=True))
                for k, lanes in enumerate(pieces):
                    y_ref[pl.ds(pl.multiple_of(base, UNROLL), UNROLL), lanes] = outs[k]
                return tuple(states)

            states = lax.fori_loop(0, span // UNROLL, block, tuple(state_ref[:, lanes] for lanes in pieces))
            for k, lanes in enumerate(pieces):
                state_ref[:, lanes] = states[k]
            return unused_inner

        lax.fori_loop(0, channels // width, group_body, 0)
        kept_copy(number, slot).start()
        hook(number)
        return unused

    lax.fori_loop(0, blocks, time_body, 0)
    for number in range(max(0, blocks - 2), blocks):
        kept_copy(number, number % 2).wait()


def inflow_pass(width, step_ref, grad_ref, wide_c, rate_ref, flow_ref, hook):
    rows, channels = step_ref.shape
    count = width // LANES

    def group_body(group, unused):
        pieces = [lanes_of(group, width, k) for k in range(count)]
        rates = [rate_ref[:, lanes] for lanes in pieces]

        def block(index, flows):
            flows = list(flows)
            base = rows - UNROLL - index * UNROLL
            steps = [tile(step_ref, base, lanes) for lanes in pieces]
            grads = [tile(grad_ref, base, lanes) for lanes in pieces]
            for place in reversed(range(UNROLL)):
                c_now = wide_c[base + place]
                for k in range(count):
                    decay = jnp.exp2(row(steps[k], place) * rates[k])
                    flows[k] = decay * (c_now * row(grads[k], place) + flows[k])
            return tuple(flows)

        zero = jnp.zeros((NS, LANES), jnp.float32)
        flows = lax.fori_loop(0, rows // UNROLL, block, (zero,) * count)
        for k, lanes in enumerate(pieces):
            flow_ref[:, lanes] = flows[k]
        hook(group)
        return unused

    lax.fori_loop(0, channels // width, group_body, 0)


def lane_sums(part_ref):
    values = part_ref[...].reshape(-1, LANES)
    high = values.astype(jnp.bfloat16)
    low = (values - high.astype(jnp.float32)).astype(jnp.bfloat16)
    ones = jnp.ones((UNROLL, LANES), jnp.bfloat16)
    return contract(ones, high, 1, 1) + contract(ones, low, 1, 1)


def adjoint_pass(width, step_ref, push_ref, grad_ref, wide_b, wide_c, rate_ref, flow_ref, kept_buf, kept_copy,
                 along_ref, slope_ref, gb_ref, gc_ref, ga_ref, part_b, part_c, hook):
    rows, channels = step_ref.shape
    count = width // LANES
    span = kept_buf.shape[1] - 1
    blocks = rows // span
    ga_ref[...] = jnp.zeros_like(ga_ref)

    def time_body(order, unused):
        slot = lax.rem(order, 2)
        number = blocks - 1 - order
        kept_copy(number, slot).wait()
        part_b[...] = jnp.zeros_like(part_b)
        part_c[...] = jnp.zeros_like(part_c)

        def group_body(group, unused_inner):
            pieces = [lanes_of(group, width, k) for k in range(count)]
            rates = [rate_ref[:, lanes] for lanes in pieces]

            def block(index, carried):
                flows = list(carried[:count])
                sums = list(carried[count : 2 * count])
                current = list(carried[2 * count :])
                local = span - UNROLL - index * UNROLL
                base = number * span + local
                steps = [tile(step_ref, base, lanes) for lanes in pieces]
                pushes = [tile(push_ref, base, lanes) for lanes in pieces]
                grads = [tile(grad_ref, base, lanes) for lanes in pieces]
                alongs = [None] * count
                slopes = [None] * count
                for place in reversed(range(UNROLL)):
                    b_now = wide_b[base + place]
                    c_now = wide_c[base + place]
                    gb = gc = None
                    for k, lanes in enumerate(pieces):
                        prior = kept_buf[slot, local + place, :, lanes].astype(jnp.float32)
                        step = row(steps[k], place)
                        grad = row(grads[k], place)
                        decay = jnp.exp2(step * rates[k])
                        adjoint = c_now * grad + flows[k]
                        flows[k] = decay * adjoint
                        decay_grad = flows[k] * prior
                        alongs[k] = put_row(alongs[k], place, jnp.sum(adjoint * b_now, axis=0, keepdims=True))
                        slopes[k] = put_row(slopes[k], place, jnp.sum(decay_grad * rates[k], axis=0, keepdims=True))
                        sums[k] = sums[k] + decay_grad * step
                        here_b = adjoint * row(pushes[k], place)
                        here_c = current[k] * grad
                        gb = here_b if gb is None else gb + here_b
                        gc = here_c if gc is None else gc + here_c
                        current[k] = prior
                    part_b[local + place] += gb
                    part_c[local + place] += gc
                where = pl.ds(pl.multiple_of(base, UNROLL), UNROLL)
                for k, lanes in enumerate(pieces):
                    along_ref[where, lanes] = alongs[k]
                    slope_ref[where, lanes] = slopes[k]
                return tuple(flows + sums + current)

            carried = lax.fori_loop(
                0,
                span // UNROLL,
                block,
                tuple(flow_ref[:, lanes] for lanes in pieces)
                + tuple(ga_ref[:, lanes] for lanes in pieces)
                + tuple(kept_buf[slot, span, :, lanes].astype(jnp.float32) for lanes in pieces),
            )
            for k, lanes in enumerate(pieces):
                flow_ref[:, lanes] = carried[k]
                ga_ref[:, lanes] = carried[count + k]
            return unused_inner

        lax.fori_loop(0, channels // width, group_body, 0)
        gb_ref[number] = lane_sums(part_b)
        gc_ref[number] = lane_sums(part_c)

        @pl.when(order + 2 < blocks)
        def _():
            kept_copy(number - 2, slot).start()

        hook(order)
        return unused

    lax.fori_loop(0, blocks, time_body, 0)


def share(source, target, send_sems, recv_sems):
    blocks = lax.axis_size("ctx")
    here, line = lax.axis_index("ctx"), lax.axis_index("exp")
    copies = []
    for step in range(1, blocks):
        copies.append(
            pltpu.make_async_remote_copy(
                src_ref=source,
                dst_ref=target.at[here],
                send_sem=send_sems.at[step],
                recv_sem=recv_sems.at[step],
                device_id=(lax.rem(here + step, blocks), line),
                device_id_type=MESH,
            )
        )
        copies[-1].start()
    target[here] = source[...]
    return copies


def row_peers():
    blocks = lax.axis_size("ctx")
    here, line = lax.axis_index("ctx"), lax.axis_index("exp")
    return [(lax.rem(here + step, blocks), line) for step in range(1, blocks)]


def row_halves(source, target, sems, place):
    size = source.shape[0] // 2
    return [
        pltpu.make_async_remote_copy(
            src_ref=source.at[pl.ds(k * size, size)],
            dst_ref=target.at[pl.ds(k * size, size)],
            send_sem=sems.at[0, k],
            recv_sem=sems.at[1, k],
            device_id=partner(place),
            device_id_type=MESH,
        )
        for k in range(2)
    ]


def front(in_ref, prior_ref, conv_w, channel_ref, width_ref, seg_ref, outs, scratch, saves):
    normed_ref, bt_ref, ct_ref, rate_ref, chan_ref, gain_ref, delta_ref, same_ref = outs
    nx, ext, conv, xs, pre, step, push = scratch
    tokens, channels = xs.shape
    width = in_ref.shape[1]
    mine = lax.axis_index("ctx")
    gain_rows = jnp.concatenate(
        [width_ref[at : at + LANES, :].astype(jnp.float32).T for at in range(0, width, LANES)], axis=1
    )
    gain_ref[...] = gain_rows[:8]
    for at in range(0, channels, LANES):
        chan_ref[:, at : at + LANES] = channel_ref[at : at + LANES, LANES:].astype(jnp.float32).T[:32]
    rate_ref[...] = -jnp.exp(chan_ref[8 : 8 + NS, :]) * LOG2E
    gain = gain_ref[0:1, :]

    def normed(values):
        x = values.astype(jnp.float32)
        return (x * lax.rsqrt(jnp.mean(x * x, axis=-1, keepdims=True) + EPS) * gain).astype(jnp.bfloat16)

    nx[:EDGE, :] = normed(prior_ref[:, :width])

    def norm_rows(index, unused):
        at = pl.ds(pl.multiple_of(index * 16, 16), 16)
        value = normed(in_ref[at, :])
        normed_ref[at, :] = value
        nx[pl.ds(pl.multiple_of(EDGE + index * 16, 16), 16), :] = value
        return unused

    lax.fori_loop(0, tokens // 16, norm_rows, 0)
    ids = jnp.where(mine > 0, prior_ref[:, width:].astype(jnp.float32), -1.0)
    own_ids = seg_ref[...]
    every_id = jnp.concatenate([ids, own_ids], axis=0)
    for j in range(1, KC):
        same_ref[j - 1] = (pltpu.roll(every_id, j, 0)[EDGE:] == own_ids).astype(jnp.float32)
    piece = 2 * LANES

    def conv_piece(index, unused):
        lanes = pl.ds(pl.multiple_of(index * piece, piece), piece)
        low = dot(nx[...], conv_w[:, lanes]).astype(jnp.bfloat16)
        ext[:, lanes] = low
        value = low.astype(jnp.float32)
        out = chan_ref[24:25, lanes] + chan_ref[3:4, lanes] * value[EDGE:]
        for j in range(1, KC):
            same = jnp.concatenate([same_ref[j - 1]] * 2, axis=1)
            out = out + chan_ref[3 - j : 4 - j, lanes] * pltpu.roll(value, j, 0)[EDGE:] * same
        conv[:, lanes] = out
        xs[:, lanes] = (out / (1.0 + jnp.exp(-out))).astype(jnp.bfloat16)
        return unused

    lax.fori_loop(0, channels // piece, conv_piece, 0)
    for save in saves[:3]:
        save.start()
    projected = dot(xs[...], channel_ref[:, :LANES])
    lane = lax.broadcasted_iota(jnp.int32, projected.shape, 1)
    delta_ref[...] = jnp.where(lane >= R + 2 * NS, pltpu.roll(projected, R + 2 * NS, 1), 0.0).astype(jnp.bfloat16)
    for at in range(0, tokens, LANES):
        block = projected[at : at + LANES].T
        bt_ref[:, at : at + LANES] = block[R : R + NS]
        ct_ref[:, at : at + LANES] = block[R + NS : R + 2 * NS]

    def step_piece(index, unused):
        lanes = pl.ds(pl.multiple_of(index * piece, piece), piece)
        value = contract(delta_ref[...], channel_ref[lanes, :LANES], 1, 1) + chan_ref[25:26, lanes]
        pre[:, lanes] = value
        size = jnp.maximum(value, 0.0) + jnp.log1p(jnp.exp(-jnp.abs(value)))
        push[:, lanes] = size * xs[:, lanes].astype(jnp.float32)
        keep = jnp.concatenate([same_ref[0]] * 2, axis=1)
        step[:, lanes] = jnp.where(keep > 0, size, 1e30)
        return unused

    lax.fori_loop(0, channels // piece, step_piece, 0)
    for save in saves[3:]:
        save.start()


def forward_kernel(places, streams, width, *refs):
    in_ref, prior_ref, conv_w, channel_ref, width_ref, seg_ref = refs[:6]
    shards, leaving = refs[6:8], refs[8]
    y_ref, product_ref = refs[9:11]
    front_outs = refs[11:19]
    kept_ref = refs[19]
    saved = refs[20:26]
    wholes, arriving = refs[26:28], refs[28]
    scratch = refs[29:36]
    (wide_b, wide_c, kept_buf, first_buf, state_ref, message, products, ends,
     kept_sems, first_sem, share_sems, save_sems, moved_sems, send_sems, recv_sems, local_sems) = refs[36:]
    bt_ref, ct_ref, rate_ref = front_outs[1:4]
    step_ref, push_ref = scratch[5:7]
    blocks = lax.axis_size("ctx")
    position = lax.axis_index("ctx")
    span = kept_buf.shape[1]
    flow = GatherFlow(places, streams, range(len(places)), shards, wholes, send_sems, recv_sems, local_sems)
    meet([place for place in places if place[0] == "exp"], *row_peers())
    flow.start()
    moves = row_halves(leaving, arriving, moved_sems, ("ctx", blocks.bit_length() - 2))
    moves[0].start()
    saves = [
        pltpu.make_async_copy(scratch[k + 1], saved[k], save_sems.at[k]) for k in range(6)
    ]
    front(in_ref, prior_ref, conv_w, channel_ref, width_ref, seg_ref, front_outs, scratch, saves)

    message[0] = jnp.exp2(jnp.sum(step_ref[...], axis=0, keepdims=True) * rate_ref[...]).astype(jnp.bfloat16)
    early = share(message.at[0], products, share_sems.at[0], share_sems.at[1])
    spread_columns(bt_ref, wide_b)
    spread_columns(ct_ref, wide_c)
    end_pass(width, step_ref, push_ref, wide_b, rate_ref, state_ref, lambda group: None)
    message[1] = state_ref[...].astype(jnp.bfloat16)
    late = share(message.at[1], ends, share_sems.at[2], share_sems.at[3])
    flow.advance(0)
    moves[1].start()
    for copy in early + late:
        copy.wait_recv()
    start = jnp.zeros(state_ref.shape, jnp.float32)
    for index in range(blocks):
        folded = products[index].astype(jnp.float32) * start + ends[index].astype(jnp.float32)
        start = jnp.where(index < position, folded, start)
    state_ref[...] = start
    product_ref[...] = products[...]
    first_buf[0] = start.astype(jnp.bfloat16)
    first_copy = pltpu.make_async_copy(first_buf, kept_ref.at[pl.ds(0, 1)], first_sem)
    first_copy.start()

    def kept_copy(number, slot):
        return pltpu.make_async_copy(
            kept_buf.at[slot], kept_ref.at[pl.ds(1 + number * span, span)], kept_sems.at[slot]
        )

    def hook(number):
        @pl.when(number == 3)
        def _():
            flow.advance(1)

    out_pass(width, step_ref, push_ref, wide_b, wide_c, rate_ref, state_ref, y_ref, kept_buf, kept_copy, hook)
    for stage in range(2, max(flow.stages(number) for number in range(len(streams)))):
        flow.advance(stage)
    flow.finish()
    first_copy.wait()
    for save in saves:
        save.wait()
    for copy in early + late:
        copy.wait_send()
    for move in moves:
        move.wait()


def scan_forward(sizes, rows_in, prior, conv_w, channel, by_width, seg_wide, shards, leaving, identity, span=64):
    places = bit_positions(sizes)
    stages = len(places)
    begin = len(far_of(places))
    streams = halves(shards, *gather_orders(places), begin=begin)
    tokens, width = rows_in.shape
    channels = conv_w.shape[1]
    blocks = sizes[0][1]
    inside = pl.BlockSpec(memory_space=pltpu.VMEM)
    anywhere = pl.BlockSpec(memory_space=pl.ANY)
    half, full = jnp.bfloat16, jnp.float32
    shape = jax.ShapeDtypeStruct
    saved = [
        shape((EDGE + tokens, channels), half),
        shape((tokens, channels), full),
        shape((tokens, channels), half),
        shape((tokens, channels), full),
        shape((tokens, channels), full),
        shape((tokens, channels), full),
    ]
    y, products, normed, bt, ct, rates, chan, gains, delta, same, kept, *rest = pl.pallas_call(
        functools.partial(forward_kernel, places, streams, pick(channels)),
        in_specs=[inside] * 6 + [anywhere] * 3,
        out_specs=[inside] * 10 + [anywhere] * 10,
        out_shape=[
            shape((tokens, channels), full),
            shape((blocks, NS, channels), half),
            shape((tokens, width), half),
            shape((NS, tokens), full),
            shape((NS, tokens), full),
            shape((NS, channels), full),
            shape((32, channels), full),
            shape((8, width), full),
            shape((tokens, LANES), half),
            shape((KC - 1, tokens, LANES), full),
            shape((tokens + 1, NS, channels), half),
        ]
        + saved
        + [shape((2,) * stages + shard.shape[begin:], shard.dtype) for shard in shards]
        + [shape(leaving.shape, leaving.dtype)],
        scratch_shapes=[pltpu.VMEM((EDGE + tokens, width), half)]
        + [pltpu.VMEM(value.shape, value.dtype) for value in saved]
        + [
            pltpu.VMEM((tokens, NS, LANES), full),
            pltpu.VMEM((tokens, NS, LANES), full),
            pltpu.VMEM((2, span, NS, channels), half),
            pltpu.VMEM((1, NS, channels), half),
            pltpu.VMEM((NS, channels), full),
            pltpu.VMEM((2, NS, channels), half),
            pltpu.VMEM((blocks, NS, channels), half),
            pltpu.VMEM((blocks, NS, channels), half),
            pltpu.SemaphoreType.DMA((2,)),
            pltpu.SemaphoreType.DMA,
            pltpu.SemaphoreType.DMA((4, blocks)),
            pltpu.SemaphoreType.DMA((6,)),
            pltpu.SemaphoreType.DMA((2, 2)),
            pltpu.SemaphoreType.DMA((len(streams), stages)),
            pltpu.SemaphoreType.DMA((len(streams), stages)),
            pltpu.SemaphoreType.DMA((len(streams),)),
        ],
        compiler_params=pltpu.CompilerParams(
            collective_id=identity, has_side_effects=True, vmem_limit_bytes=52 * 1024 * 1024
        ),
        cost_estimate=cost(tokens, channels, 9),
        name="scan_forward",
    )(rows_in, prior, conv_w, channel, by_width, seg_wide, *shards, leaving)
    saved, wholes, arrived = rest[:6], rest[6:8], rest[8]
    wholes = [whole.reshape((-1,) + whole.shape[stages + 1 :]) for whole in wholes]
    return y, products, normed, bt, ct, rates, chan, gains, delta, same, kept, saved, wholes, arrived


def backward_kernel(places, streams, marks, width, *refs):
    step_ref, push_ref, grad_ref, bt_ref, ct_ref, rate_ref, product_ref = refs[:7]
    parts = refs[7:9]
    kept_ref, leaving = refs[9:11]
    outs = refs[11:]
    along_ref, slope_ref, gb_ref, gc_ref, ga_ref = outs[:5]
    totals, arriving = outs[5:7], outs[7]
    scratch = outs[8:]
    landing = scratch[:marks]
    (wide_b, wide_c, part_b, part_c, kept_buf, flow_ref, message, inflows,
     kept_sems, share_sems, moved_sems, send_sems, recv_sems) = scratch[marks:]
    blocks = lax.axis_size("ctx")
    position = lax.axis_index("ctx")
    span = kept_buf.shape[1] - 1
    steps = step_ref.shape[0] // span
    flow = ReduceFlow(places, streams, range(len(places)), parts, totals, landing, send_sems, recv_sems)

    def kept_copy(number, slot):
        return pltpu.make_async_copy(
            kept_ref.at[pl.ds(number * span, span + 1)], kept_buf.at[slot], kept_sems.at[slot]
        )

    for order in range(min(2, steps)):
        kept_copy(steps - 1 - order, order).start()
    meet([place for place in places if place[0] == "exp"], *row_peers())
    flow.start()
    moves = row_halves(leaving, arriving, moved_sems, ("ctx", blocks.bit_length() - 2))
    moves[0].start()
    spread_columns(bt_ref, wide_b)
    spread_columns(ct_ref, wide_c)
    inflow_pass(width, step_ref, grad_ref, wide_c, rate_ref, flow_ref, lambda group: None)
    message[...] = flow_ref[...].astype(jnp.bfloat16)
    copies = share(message, inflows, share_sems.at[0], share_sems.at[1])
    for copy in copies:
        copy.wait_recv()
    end = jnp.zeros(flow_ref.shape, jnp.float32)
    for index in reversed(range(blocks)):
        folded = inflows[index].astype(jnp.float32) + product_ref[index].astype(jnp.float32) * end
        end = jnp.where(index > position, folded, end)
    flow_ref[...] = end
    flow.advance(0)
    moves[1].start()
    def hook(order):
        @pl.when(order == 2)
        def _():
            flow.advance(1)

        @pl.when(order == 4)
        def _():
            flow.advance(2)

    adjoint_pass(width, step_ref, push_ref, grad_ref, wide_b, wide_c, rate_ref, flow_ref, kept_buf, kept_copy,
                 along_ref, slope_ref, gb_ref, gc_ref, ga_ref, part_b, part_c, hook)
    for stage in range(3, len(streams[0][2])):
        flow.advance(stage)
    flow.finish()
    for copy in copies:
        copy.wait_send()
    for move in moves:
        move.wait()


def scan_backward(sizes, step, push, grad, b_turned, c_turned, rates, products, parts, kept, leaving, identity, span=64):
    places = bit_positions(sizes)
    stages = len(places)
    far = sorted(far_of(places))
    streams = halves(parts, *[tuple(order[: stages - len(far)]) for order in orders_of(places)])
    divided = [part.reshape((2,) * stages + (-1, part.shape[1])) for part in parts]
    tokens, channels = step.shape
    blocks = sizes[0][1]
    inside = pl.BlockSpec(memory_space=pltpu.VMEM)
    anywhere = pl.BlockSpec(memory_space=pl.ANY)
    half = jnp.bfloat16
    landing = landing_of(streams, range(stages), divided)
    row_sums = jax.ShapeDtypeStruct((tokens // span, UNROLL, span * NS), jnp.float32)
    out = pl.pallas_call(
        functools.partial(backward_kernel, places, streams, len(landing), pick(channels)),
        in_specs=[inside] * 9 + [anywhere] * 2,
        out_specs=[inside] * 7 + [anywhere],
        out_shape=[jax.ShapeDtypeStruct((tokens, channels), jnp.float32)] * 2
        + [row_sums, row_sums, jax.ShapeDtypeStruct((NS, channels), jnp.float32)]
        + [jax.ShapeDtypeStruct((2,) * len(far) + block.shape[-2:], half) for block in divided]
        + [jax.ShapeDtypeStruct(leaving.shape, leaving.dtype)],
        scratch_shapes=landing
        + [
            pltpu.VMEM((tokens, NS, LANES), jnp.float32),
            pltpu.VMEM((tokens, NS, LANES), jnp.float32),
            pltpu.VMEM((span, NS, LANES), jnp.float32),
            pltpu.VMEM((span, NS, LANES), jnp.float32),
            pltpu.VMEM((2, span + 1, NS, channels), half),
            pltpu.VMEM((NS, channels), jnp.float32),
            pltpu.VMEM((NS, channels), half),
            pltpu.VMEM((blocks, NS, channels), half),
            pltpu.SemaphoreType.DMA((2,)),
            pltpu.SemaphoreType.DMA((2, blocks)),
            pltpu.SemaphoreType.DMA((2, 2)),
        ]
        + flights(streams),
        compiler_params=pltpu.CompilerParams(
            collective_id=identity, has_side_effects=True, vmem_limit_bytes=56 * 1024 * 1024
        ),
        cost_estimate=cost(tokens, channels, 15),
        name="scan_backward",
    )(step, push, grad, b_turned, c_turned, rates, products, *divided, kept, leaving)
    along, slope, wide_b, wide_c, grad_a = out[:5]
    grad_bs, grad_cs = [values[:, 0].reshape(tokens, NS) for values in (wide_b, wide_c)]
    return along, slope, grad_bs, grad_cs, grad_a, out[5:7], out[7]


class PackedReduce(ReduceFlow):
    def __init__(self, places, streams, heads, parts, totals, landing, blocks, send_sems, recv_sems):
        super().__init__(places, streams, range(len(places)), parts, totals, landing, send_sems, recv_sems)
        self.heads, self.blocks = heads, blocks

    def side(self, number, stage, value):
        array, cols, order = self.streams[number]
        if stage == 0:
            index = tuple(value if p == order[0] else slice(None) for p in range(self.heads))
            return self.parts[array].at[index + (slice(None), cols)]
        left = [p for p in self.dims if p not in order[:stage]]
        index = tuple(value if p == order[stage] else slice(None) for p in left)
        held = self.blocks[number] if stage == 1 else self.spot(number, stage - 1)
        return held.at[index]

    def advance(self, stage):
        if stage:
            super().advance(stage)
            return
        for number, (array, cols, order) in enumerate(self.streams):
            self.flight(number, 0).wait_recv()
            mine = self.side(number, 0, self.bits[order[0]])
            there, held = self.spot(number, 0), self.blocks[number]
            tails = len(self.places) - self.heads
            size = held.shape[-2]

            def add(index, unused, mine=mine, there=there, held=held, tails=tails, size=size):
                at = tuple(lax.rem(index // 2 ** (self.heads - 2 - k), 2) for k in range(self.heads - 1))
                value = there[at].astype(jnp.float32) + mine[at].astype(jnp.float32)
                for block in range(2**tails):
                    spot = tuple(block // 2 ** (tails - 1 - k) % 2 for k in range(tails))
                    held[at + spot] = value[block * size : (block + 1) * size].astype(held.dtype)
                return unused

            lax.fori_loop(0, 2 ** (self.heads - 1), add, 0)
            self.flight(number, 1).start()


def turned(values):
    return jnp.concatenate([values[:, at : at + LANES].T for at in range(0, values.shape[1], LANES)], axis=0)


def finish_kernel(places, streams, third, late, far, marks, *refs):
    (along_h, slope_h, grad_h, pre_h, conv_h, xs_h, ext_h, gz_h, wc_h, wg_h) = refs[:10]
    (normed_ref, in_ref, resid_ref, mix_ref, bc_ref, delta_ref, same_ref, chan_ref, decay_ref, wide_ref) = refs[10:20]
    rest_parts = refs[20:22]
    gi_ref, own_in, own_out, own_x, own_dt, own_taps, own_decay, own_router = refs[22:30]
    own_vectors, own_gains = refs[30:33], refs[33:35]
    scratch = refs[35:]
    landing, scratch = scratch[: marks[0]], scratch[marks[0] :]
    blocks, scratch = scratch[: marks[1]], scratch[marks[1] :]
    landing3, scratch = scratch[: marks[2]], scratch[marks[2] :]
    blocks3, scratch = scratch[: marks[3]], scratch[marks[3] :]
    late_landing, scratch = scratch[: marks[4]], scratch[marks[4] :]
    (along, slope, grad, pre, conv, xs, ext, gz, wc, wg, gdt, gci, last, spill, arrived, sums, rows_s, wide_s, gn,
     part_conv, part_small, part_wide, tot_small, tot_wide,
     block_sems, whole_sems, spill_sems, send_sems, recv_sems, send3, recv3, late_send, late_recv) = scratch
    tokens, channels = xs.shape
    own_conv, own_gate = own_in.at[:, :channels], own_in.at[:, channels:]
    span = tokens // block_sems.shape[1]
    heads = len([place for place in places if place[0] == "ctx"])
    flow = PackedReduce(
        places, streams, heads, (part_conv, part_small), (own_conv, tot_small), landing, blocks, send_sems, recv_sems
    )
    flow3 = PackedReduce(places, third, heads, (part_wide,), (tot_wide,), landing3, blocks3, send3, recv3)
    rest = ReduceFlow(places, late, far, rest_parts, (own_gate, own_out), late_landing, late_send, late_recv)

    streamed = ((along_h, along), (slope_h, slope), (grad_h, grad), (pre_h, pre), (xs_h, xs))

    def block_copy(k, number):
        rows = pl.ds(number * span, span)
        source, target = streamed[k]
        return pltpu.make_async_copy(source.at[rows], target.at[rows], block_sems.at[k, number])

    for number in range(tokens // span):
        for k in range(len(streamed)):
            block_copy(k, number).start()
    wholes = [
        pltpu.make_async_copy(source, target, whole_sems.at[k])
        for k, (source, target) in enumerate(((conv_h, conv), (ext_h, ext), (gz_h, gz), (wc_h, wc), (wg_h, wg)))
    ]
    for copy in wholes:
        copy.start()
    count = lax.axis_size("ctx")
    here, line = lax.axis_index("ctx"), lax.axis_index("exp")
    before = (lax.rem(here + count - 1, count), line)
    meet(places, before, (lax.rem(here + 1, count), line))
    rest.start()

    sums[...] = jnp.zeros_like(sums)
    rows_s[...] = jnp.zeros_like(rows_s)

    def first_block(number, unused):
        for k in range(len(streamed)):
            block_copy(k, number).wait()

        def some(index, unused_inner):
            at = pl.ds(pl.multiple_of(number * span + index * 16, 16), 16)
            for low in range(0, channels, LANES):
                lanes = slice(low, low + LANES)
                a, g, x, p = along[at, lanes], grad[at, lanes], xs[at, lanes].astype(jnp.float32), pre[at, lanes]
                small = jnp.exp(-jnp.abs(p))
                gated = jnp.where(p >= 0, 1.0, small) / (1.0 + small)
                step = jnp.maximum(p, 0.0) + jnp.log1p(small)
                value = (a * x + slope[at, lanes] * (1.0 / LOG2E)) * gated
                gdt[at, lanes] = value.astype(jnp.bfloat16)
                sums[0, :, lanes] += value[:8] + value[8:]
                both = g * x
                sums[1, :, lanes] += both[:8] + both[8:]
                along[at, lanes] = chan_ref[4:5, lanes] * g + a * step
            return unused_inner

        lax.fori_loop(0, span // 16, some, 0)
        return unused

    lax.fori_loop(0, tokens // span, first_block, 0)
    rows_s[25:26, :] = jnp.sum(sums[0], axis=0, keepdims=True)
    rows_s[26:27, :] = jnp.sum(sums[1], axis=0, keepdims=True)
    rows_s[8:24, :] = decay_ref[...]

    lane = lax.broadcasted_iota(jnp.int32, (tokens, LANES), 1)
    mixed = pltpu.roll(dot(gdt[...], mix_ref[...]), R, 1)
    projected = jnp.where(lane < R, mixed, jnp.where(lane < R + 2 * NS, bc_ref[...], 0.0)).astype(jnp.bfloat16)
    wholes[0].wait()
    wholes[1].wait()
    piece = 2 * LANES
    tail_row = lax.broadcasted_iota(jnp.int32, (tokens, piece), 0)

    def conv_piece(index, unused):
        lanes = pl.ds(pl.multiple_of(index * piece, piece), piece)
        some = pl.ds(pl.multiple_of(index * piece, piece), piece)
        total = along[:, lanes] + contract(projected, mix_ref[some, :], 1, 1)
        value = conv[:, lanes]
        gate = 1.0 / (1.0 + jnp.exp(-value))
        out = total * gate * (1.0 + value * (1.0 - gate))
        rows_s[24:25, lanes] = jnp.sum(out, axis=0, keepdims=True)
        before_rows = ext[:, lanes].astype(jnp.float32)
        rows_s[3:4, lanes] = jnp.sum(out * before_rows[EDGE:], axis=0, keepdims=True)
        result = chan_ref[3:4, lanes] * out
        beyond = jnp.zeros((8, piece), jnp.float32)
        for j in range(1, KC):
            same = jnp.concatenate([same_ref[j - 1]] * 2, axis=1)
            masked = out * same
            shifted_rows = pltpu.roll(before_rows, j, 0)[EDGE:]
            rows_s[3 - j : 4 - j, lanes] = jnp.sum(masked * shifted_rows, axis=0, keepdims=True)
            moved = chan_ref[3 - j : 4 - j, lanes] * pltpu.roll(masked, tokens - j, 0)
            result = result + jnp.where(tail_row < tokens - j, moved, 0.0)
            beyond = beyond + jnp.where(tail_row < tokens - j, 0.0, moved)[tokens - 8 :]
        gci[:, lanes] = result.astype(jnp.bfloat16)
        last[:, lanes] = result[tokens - 16 :]
        spill[:, lanes] = beyond
        return unused

    lax.fori_loop(0, channels // piece, conv_piece, 0)
    handed = pltpu.make_async_remote_copy(
        src_ref=spill,
        dst_ref=arrived,
        send_sem=spill_sems.at[0],
        recv_sem=spill_sems.at[1],
        device_id=before,
        device_id_type=MESH,
    )
    handed.start()

    cut = part_small.shape[-2]
    for index in range(channels // cut):
        spot = tuple(index // 2 ** (heads - 1 - k) % 2 for k in range(heads))
        if cut % LANES == 0:
            some = slice(index * cut, (index + 1) * cut)
            value = contract(xs[:, some], projected, 0, 0) + contract(gdt[:, some], delta_ref[...], 0, 0)
        else:
            pair = slice(index // 2 * 2 * cut, (index // 2 * 2 + 2) * cut)
            value = contract(xs[:, pair], projected, 0, 0) + contract(gdt[:, pair], delta_ref[...], 0, 0)
            value = value[index % 2 * cut : (index % 2 + 1) * cut]
        part_small[spot + (slice(None), slice(0, LANES))] = value.astype(jnp.bfloat16)
    columns = turned(jnp.concatenate([rows_s[...], jnp.zeros((LANES - rows_s.shape[0], channels), jnp.float32)], axis=0))
    for index in range(channels // cut):
        spot = tuple(index // 2 ** (heads - 1 - k) % 2 for k in range(heads))
        part_small[spot + (slice(None), slice(LANES, 2 * LANES))] = columns[index * cut : (index + 1) * cut].astype(jnp.bfloat16)

    handed.wait_recv()
    closing = last[...] + jnp.concatenate([jnp.zeros((8, channels), jnp.float32), arrived[...]], axis=0)
    gci[tokens - 16 :, :] = closing.astype(jnp.bfloat16)

    long = part_conv.shape[-2]

    def product_piece(index, unused):
        lanes = pl.ds(pl.multiple_of(index * piece, piece), piece)
        value = contract(normed_ref[...], gci[:, lanes], 0, 0)
        for block in range(value.shape[0] // long):
            spot = tuple(block // 2 ** (heads - 1 - k) % 2 for k in range(heads))
            part_conv[spot + (slice(None), lanes)] = value[block * long : (block + 1) * long].astype(jnp.bfloat16)
        return unused

    lax.fori_loop(0, channels // piece, product_piece, 0)
    flow.start()

    for copy in wholes[2:]:
        copy.wait()
    width = gn.shape[1]

    def normed_piece(index, unused):
        lanes = pl.ds(pl.multiple_of(index * piece, piece), piece)
        gn[:, lanes] = contract(gci[...], wc[lanes, :], 1, 1) + contract(gz[...], wg[lanes, :], 1, 1)
        return unused

    lax.fori_loop(0, width // piece, normed_piece, 0)
    wide_s[...] = wide_ref[...]
    gain = wide_ref[0:1, :]

    def back(index, total):
        at = pl.ds(pl.multiple_of(index * 16, 16), 16)
        x, g = in_ref[at, :].astype(jnp.float32), gn[at, :]
        scale = lax.rsqrt(jnp.mean(x * x, axis=-1, keepdims=True) + EPS)
        scaled = g * gain
        share_of = jnp.mean(x * scaled, axis=-1, keepdims=True)
        gi_ref[at, :] = resid_ref[at, :] + scale * scaled - x * (scale * scale * scale * share_of)
        value = g * (x * scale)
        return total + value[:8] + value[8:]

    total = lax.fori_loop(0, tokens // 16, back, jnp.zeros((8, width), jnp.float32))
    wide_s[0:1, :] = jnp.sum(total, axis=0, keepdims=True)
    flow.advance(0)
    filler = jnp.zeros((LANES - wide_s.shape[0], width), jnp.float32)
    columns = turned(jnp.concatenate([wide_s[...], filler], axis=0))
    short = part_wide.shape[-2]
    for block in range(width // short):
        spot = tuple(block // 2 ** (heads - 1 - k) % 2 for k in range(heads))
        part_wide[spot] = columns[block * short : (block + 1) * short].astype(jnp.bfloat16)
    flow3.start()
    rest.advance(0)
    for stage in range(1, len(places)):
        flow.advance(stage)
        flow3.advance(stage - 1)
        rest.advance(stage)
    flow3.advance(len(places) - 1)

    def columns_of(values):
        return jnp.concatenate([values, jnp.zeros((LANES - values.shape[0], LANES), jnp.float32)], axis=0).T

    size = tot_small.shape[0]
    first, second, wide = tot_small[:, :LANES], tot_small[:, LANES:], tot_wide[...]
    own_x[...] = first[:, : R + 2 * NS]
    own_dt[...] = columns_of(first)[R + 2 * NS :, :size]
    by_row = columns_of(second)
    own_taps[...] = by_row[:KC, :size]
    own_decay[...] = by_row[8 : 8 + NS, :size]
    for k in range(3):
        own_vectors[k][...] = by_row[24 + k : 25 + k, :size]
    by_row = columns_of(wide)
    for k in range(2):
        own_gains[k][...] = by_row[k : k + 1, : wide.shape[0]]
    own_router[...] = by_row[8 : 8 + own_router.shape[0], : wide.shape[0]]
    flow.finish()
    flow3.finish()
    rest.finish()
    handed.wait_send()


def finish(sizes, streamed, inside_values, parts, experts, identity, span=64):
    places = bit_positions(sizes)
    stages = len(places)
    far = sorted(far_of(places))
    heads = sizes[0][1].bit_length() - 1
    tails = stages - heads
    along, slope, grad, pre, conv, xs, ext, gz, wc, wg = streamed
    normed = inside_values[0]
    tokens, channels = xs.shape
    width = normed.shape[1]
    devices = 2**stages
    half, wide = jnp.bfloat16, jnp.float32
    rows, thin = channels // devices, width // devices
    orders = [tuple(order) for order in orders_of(places)]
    conv_like = jax.ShapeDtypeStruct((width, channels), half)
    small_like = jax.ShapeDtypeStruct((channels, 2 * LANES), half)
    wide_like = jax.ShapeDtypeStruct((width, LANES), half)
    streams = halves((conv_like, small_like), *orders)
    third = halves((wide_like,), *orders)
    late = [(k, slice(0, part.shape[-1]), tuple(far_of(places))) for k, part in enumerate(parts)]

    def room(of, sizes_of):
        landing, blocks = [], []
        for array, cols, order in of:
            size, many = sizes_of[array], cols.stop - cols.start
            landing.append(pltpu.VMEM((2,) * (heads - 1) + (size * 2**tails, many), half))
            landing += [pltpu.VMEM((2,) * (stages - stage - 1) + (size, many), half) for stage in range(1, stages)]
            blocks.append(pltpu.VMEM((2,) * (stages - 1) + (size, many), half))
        return landing, blocks

    landing, blocks = room(streams, (thin, rows))
    landing3, blocks3 = room(third, (thin,))
    late_landing = landing_of(late, far, parts)
    marks = [len(landing), len(blocks), len(landing3), len(blocks3), len(late_landing)]
    inside = pl.BlockSpec(memory_space=pltpu.VMEM)
    anywhere = pl.BlockSpec(memory_space=pl.ANY)
    return pl.pallas_call(
        functools.partial(finish_kernel, places, streams, third, late, far, marks),
        in_specs=[anywhere] * 10 + [inside] * (len(inside_values) + 2),
        out_specs=[inside] * 13,
        out_shape=[
            jax.ShapeDtypeStruct(normed.shape, wide),
            jax.ShapeDtypeStruct((thin, 2 * channels), wide),
            jax.ShapeDtypeStruct(parts[1].shape[-2:], wide),
            jax.ShapeDtypeStruct((rows, R + 2 * NS), wide),
            jax.ShapeDtypeStruct((R, rows), wide),
            jax.ShapeDtypeStruct((KC, rows), wide),
            jax.ShapeDtypeStruct((NS, rows), wide),
            jax.ShapeDtypeStruct((experts, thin), wide),
        ]
        + [jax.ShapeDtypeStruct((1, rows), wide)] * 3
        + [jax.ShapeDtypeStruct((1, thin), wide)] * 2,
        scratch_shapes=landing + blocks + landing3 + blocks3 + late_landing
        + [pltpu.VMEM(value.shape, value.dtype) for value in streamed]
        + [
            pltpu.VMEM((tokens, channels), half),
            pltpu.VMEM((tokens, channels), half),
            pltpu.VMEM((16, channels), wide),
            pltpu.VMEM((8, channels), wide),
            pltpu.VMEM((8, channels), wide),
            pltpu.VMEM((2, 8, channels), wide),
            pltpu.VMEM((32, channels), wide),
            pltpu.VMEM(inside_values[-1].shape, wide),
            pltpu.VMEM((tokens, width), wide),
            pltpu.VMEM((2,) * heads + (thin * 2**tails, channels), half),
            pltpu.VMEM((2,) * heads + (rows * 2**tails, 2 * LANES), half),
            pltpu.VMEM((2,) * heads + (thin * 2**tails, LANES), half),
            pltpu.VMEM((rows, 2 * LANES), wide),
            pltpu.VMEM((thin, LANES), wide),
            pltpu.SemaphoreType.DMA((5, tokens // span)),
            pltpu.SemaphoreType.DMA((5,)),
            pltpu.SemaphoreType.DMA((2,)),
        ]
        + flights(streams)
        + flights(third)
        + flights(late),
        compiler_params=pltpu.CompilerParams(
            collective_id=identity, has_side_effects=True, vmem_limit_bytes=56 * 1024 * 1024
        ),
        name="finish",
    )(*streamed, *inside_values, *parts)


def expert_kernel(slices, *refs):
    tokens_ref, grads_ref, column_ref, row_ref = refs[:4]
    even = range(0, slices, 2)
    odd = range(1, slices, 2)
    weights_in, weight_out = refs[4 : 4 + len(even)], refs[4 + len(even)]
    outs = refs[5 + len(even) :]
    picked_ref, back_ref, own_out = outs[:3]
    sums_in = outs[3 : 3 + len(even)]
    (sent, got, answer, returned, w_in, w_out, hidden, total, active, slope, inner, sum_out, pair_out, pair_in, far_out,
     send_sems, recv_sems, weight_sems, sum_sems, spread_sems, mate_sems, far_sems) = outs[3 + len(even) :]
    experts, room, width = sent.shape[1:]
    places = experts * room
    me = lax.axis_index("exp")
    here = lax.axis_index("ctx")
    levels = slices.bit_length() - 1

    loads = [pltpu.make_async_copy(weight_out, w_out.at[0], weight_sems.at[slices])]
    for k, s in enumerate(even):
        loads.append(pltpu.make_async_copy(weights_in[k], w_in.at[s], weight_sems.at[s]))
    for load in loads:
        load.start()

    barrier = pltpu.get_barrier_semaphore()
    mates = [partner(("ctx", level)) for level in range(levels)]
    for step in range(1, experts):
        pl.semaphore_signal(barrier, inc=1, device_id=(here, lax.rem(me + step, experts)), device_id_type=MESH)
    for mate in mates:
        pl.semaphore_signal(barrier, inc=1, device_id=mate, device_id_type=MESH)
    pl.semaphore_wait(barrier, experts - 1 + levels)

    def exchange(source, target, kind):
        copies = []
        for step in range(1, experts):
            peer = lax.rem(me + step, experts)
            copy = pltpu.make_async_remote_copy(
                src_ref=source.at[peer],
                dst_ref=target.at[me],
                send_sem=send_sems.at[kind, step],
                recv_sem=recv_sems.at[kind, step],
                device_id=(here, peer),
                device_id_type=MESH,
            )
            copy.start()
            copies.append(copy)
        target[me] = source[me]
        return copies

    def hand(source, target, sems, level):
        copy = pltpu.make_async_remote_copy(
            src_ref=source,
            dst_ref=target,
            send_sem=sems.at[0],
            recv_sem=sems.at[1],
            device_id=mates[level],
            device_id_type=MESH,
        )
        copy.start()
        return copy

    def arrive(copies):
        for copy in copies:
            copy.wait_recv()

    open_sends = []

    def spread(level):
        step = 2**level
        copies = [hand(w_out.at[s], w_out.at[s + step], spread_sems.at[1, s + step], level) for s in range(0, slices, 2 * step)]
        open_sends.extend(copies)
        return copies

    chooser = (lax.broadcasted_iota(jnp.int32, (places, row_ref.shape[1]), 0) == row_ref[...]).astype(jnp.float32).astype(jnp.bfloat16)
    sent[0] = dot(chooser, tokens_ref[...]).astype(jnp.bfloat16).reshape(experts, room, width)
    first = exchange(sent.at[0], got.at[0], 0)
    for load in loads:
        load.wait()
    widening = [spread(levels - 1)]
    paired = [hand(w_in.at[s], w_in.at[s + 1], spread_sems.at[0, s], 0) for s in even]
    sent[1] = dot(chooser, grads_ref[...]).astype(jnp.bfloat16).reshape(experts, room, width)
    second = exchange(sent.at[1], got.at[1], 1)

    arrive(first)
    rows = got[0].reshape(places, width)
    for s in list(even) + list(odd):
        if s == 1:
            arrive(paired)
        hidden[...] = dot(rows, w_in[s])

        def curve(index, unused):
            at = pl.ds(pl.multiple_of(index * ROWS_AT_ONCE, ROWS_AT_ONCE), ROWS_AT_ONCE)
            value = hidden[at, :]
            bell = 0.5 + 0.5 * lax.erf(value * 0.7071067811865476)
            active[s, at, :] = (value * bell).astype(jnp.bfloat16)
            slope[s, at, :] = bell + value * (jnp.exp(-0.5 * value * value) * 0.3989422804014327)
            return unused

        lax.fori_loop(0, places // ROWS_AT_ONCE, curve, 0)

    for level in reversed(range(levels - 1)):
        arrive(widening[-1])
        widening.append(spread(level))
    for s in list(even) + list(odd):
        if s == 1:
            arrive(widening[-1])
        product = dot(active[s], w_out[s])
        total[...] = product if s == 0 else total[...] + product
    answer[0] = total[...].astype(jnp.bfloat16).reshape(experts, room, width)
    third = exchange(answer.at[0], returned.at[0], 2)

    arrive(second)
    pulled = got[1].reshape(places, width)
    joining = []
    for s in list(odd) + list(even):
        sum_out[s] = contract(active[s], pulled, 0, 0).astype(jnp.bfloat16)
        if s % 2:
            joining.append(hand(sum_out.at[s], pair_out.at[s // 2], mate_sems.at[0, s // 2], 0))
    for s in range(slices):
        inner[s] = (contract(pulled, w_out[s], 1, 1) * slope[s]).astype(jnp.bfloat16)
        product = contract(inner[s], w_in[s], 1, 1)
        total[...] = product if s == 0 else total[...] + product
    answer[1] = total[...].astype(jnp.bfloat16).reshape(experts, room, width)
    fourth = exchange(answer.at[1], returned.at[1], 3)

    def add_into(target, addend):
        def some(index, unused):
            at = pl.ds(pl.multiple_of(index * 4 * ROWS_AT_ONCE, 4 * ROWS_AT_ONCE), 4 * ROWS_AT_ONCE)
            target[at, :] = (target[at, :].astype(jnp.float32) + addend[at, :].astype(jnp.float32)).astype(jnp.bfloat16)
            return unused

        lax.fori_loop(0, target.shape[0] // (4 * ROWS_AT_ONCE), some, 0)

    arrive(joining)
    for k, s in enumerate(even):
        add_into(sum_out.at[s], pair_out.at[k])

    def pass_on(level):
        step = 2**level
        return [
            hand(sum_out.at[s + step], far_out.at[slices // step // 2 - 1 + s // (2 * step)], far_sems.at[level, s // (2 * step)], level)
            for s in range(0, slices, 2 * step)
        ]

    passing = pass_on(1)
    open_sends.extend(joining)
    for copy in paired:
        copy.wait_send()
    joined = []
    for s in list(odd) + list(even):
        w_in[s] = contract(rows, inner[s], 0, 0).astype(jnp.bfloat16)
        if s % 2:
            joined.append(hand(w_in.at[s], pair_in.at[s // 2], mate_sems.at[1, s // 2], 0))
    arrive(joined)
    stores = []
    for k, s in enumerate(even):
        add_into(w_in.at[s], pair_in.at[k])
        stores.append(pltpu.make_async_copy(w_in.at[s], sums_in[k], sum_sems.at[k]))
        stores[-1].start()

    finder = (lax.broadcasted_iota(jnp.int32, (column_ref.shape[0], places), 1) == column_ref[...]).astype(jnp.float32).astype(jnp.bfloat16)
    arrive(third)
    picked_ref[...] = dot(finder, returned[0].reshape(places, width)).astype(jnp.bfloat16)
    for level in range(1, levels):
        arrive(passing)
        open_sends.extend(passing)
        step = 2**level
        if level + 1 < levels:
            for s in range(0, slices, 2 * step):
                add_into(sum_out.at[s], far_out.at[slices // step // 2 - 1 + s // (2 * step)])
            passing = pass_on(level + 1)
    own_out[...] = sum_out[0].astype(jnp.float32) + far_out[0].astype(jnp.float32)
    arrive(fourth)
    back_ref[...] = dot(finder, returned[1].reshape(places, width)).astype(jnp.bfloat16)
    for store in stores:
        store.wait()
    for copies in (first, second, third, fourth, joined, open_sends):
        for copy in copies:
            copy.wait_send()


def run_experts(rows, grads, target, weights_in, weight_out, experts, room, identity):
    slices = 2 * len(weights_in)
    tokens, width = rows.shape
    inner_width = weight_out.shape[0]
    places = experts * room
    inside = pl.BlockSpec(memory_space=pltpu.VMEM)
    anywhere = pl.BlockSpec(memory_space=pl.ANY)
    half = jnp.bfloat16
    count = len(weights_in)
    out = pl.pallas_call(
        functools.partial(expert_kernel, slices),
        in_specs=[inside] * 4 + [anywhere] * (count + 1),
        out_specs=[inside] * 3 + [anywhere] * count,
        out_shape=[jax.ShapeDtypeStruct(rows.shape, half)] * 2
        + [jax.ShapeDtypeStruct(weight_out.shape, jnp.float32)]
        + [jax.ShapeDtypeStruct(weight.shape, half) for weight in weights_in],
        scratch_shapes=[pltpu.VMEM((2, experts, room, width), half)] * 4
        + [
            pltpu.VMEM((slices, width, inner_width), half),
            pltpu.VMEM((slices, inner_width, width), half),
            pltpu.VMEM((places, inner_width), jnp.float32),
            pltpu.VMEM((places, width), jnp.float32),
            pltpu.VMEM((slices, places, inner_width), half),
            pltpu.VMEM((slices, places, inner_width), jnp.float32),
            pltpu.VMEM((slices, places, inner_width), half),
            pltpu.VMEM((slices, inner_width, width), half),
            pltpu.VMEM((count, inner_width, width), half),
            pltpu.VMEM((count, width, inner_width), half),
            pltpu.VMEM((count, inner_width, width), half),
            pltpu.SemaphoreType.DMA((4, experts)),
            pltpu.SemaphoreType.DMA((4, experts)),
            pltpu.SemaphoreType.DMA((slices + 1,)),
            pltpu.SemaphoreType.DMA((count,)),
            pltpu.SemaphoreType.DMA((2, slices, 2)),
            pltpu.SemaphoreType.DMA((2, count, 2)),
            pltpu.SemaphoreType.DMA((slices, count, 2)),
        ],
        compiler_params=pltpu.CompilerParams(
            collective_id=identity, has_side_effects=True, vmem_limit_bytes=60 * 1024 * 1024
        ),
        name="run_experts",
    )(rows, grads, target[:, None], target[None, :], *weights_in, weight_out)
    return out[0], out[1], list(out[3:]), out[2]


def flipped(value, level):
    count = lax.axis_size("ctx")
    return lax.ppermute(value, "ctx", [(source, source ^ (1 << level)) for source in range(count)])


def spread_slices(own, far):
    levels = lax.axis_size("ctx").bit_length() - 1
    slices = {0: own, 1 << (levels - 1): far}
    for level in reversed(range(1, levels - 1)):
        for offset in sorted(slices):
            slices[offset + (1 << level)] = flipped(slices[offset], level)
    return [slices[offset] for offset in sorted(slices)]


def collect_slices(sums):
    levels = lax.axis_size("ctx").bit_length() - 1
    for level in range(1, levels - 1):
        arrived = [flipped(values, level).astype(jnp.float32) for values in sums[1::2]]
        sums = [
            (values.astype(jnp.float32) + other).astype(jnp.bfloat16) for values, other in zip(sums[::2], arrived)
        ]
    return sums


def body(
    inputs,
    segments,
    routes,
    cotangent,
    norm_gain,
    in_proj,
    conv_taps,
    conv_bias,
    x_proj,
    dt_proj,
    dt_bias,
    log_decay,
    skip_gain,
    out_proj,
    moe_gain,
    router,
    expert_in,
    expert_out,
):
    experts = router.shape[1]
    half_rows = norm_gain.shape[0]
    half = jnp.bfloat16
    rows_part = jnp.concatenate(
        [
            conv_taps.T,
            jnp.zeros((4, 2 * half_rows), half),
            log_decay.T,
            jnp.stack([conv_bias, dt_bias, skip_gain]),
            jnp.zeros((5, 2 * half_rows), half),
        ]
    )
    thin_part = jnp.concatenate([jnp.stack([norm_gain, moe_gain]), jnp.zeros((6, half_rows), half), router.T])
    sizes = [(name, lax.axis_size(name)) for name in ("ctx", "exp")]
    tail_ids = segments[0, -EDGE:, None].astype(jnp.bfloat16)
    edge = jnp.concatenate([inputs[0, -EDGE:], jnp.broadcast_to(tail_ids, (EDGE, LANES))], axis=1)
    (full_conv, full_channel, full_width), partial, prior = gather_all(
        sizes, (x_proj, dt_proj, rows_part, thin_part), in_proj[:, :DI], (in_proj[:, DI:], out_proj), edge, 0
    )
    tokens_here = inputs.shape[1]
    capacity = 5 * tokens_here // (4 * experts)
    flat_in = inputs[0].astype(jnp.float32)
    seg_wide = jnp.broadcast_to(segments[0].astype(jnp.float32)[:, None], (tokens_here, LANES))
    (
        scan_rows,
        products,
        normed_one,
        b_turned,
        c_turned,
        rates,
        by_channel,
        gain_rows,
        delta_low,
        same_rows,
        kept,
        (conv_ext, conv_out, xs_val, dt_pre, masked_step, push),
        (full_gate, full_out),
        far_in,
    ) = scan_forward(
        sizes,
        inputs[0],
        prior,
        full_conv,
        full_channel,
        full_width,
        seg_wide,
        partial,
        expert_in[0],
        3,
    )
    weights_in = spread_slices(expert_in[0], far_in)
    mix = full_channel[:, :LANES]
    full_skip, full_moe, full_router = by_channel[26], gain_rows[1], full_width[:, 8 : 8 + experts]
    xs_wide = xs_val.astype(jnp.float32)
    gate_z = dot(normed_one, full_gate)
    skip_wide = full_skip
    scanned_y = scan_rows + skip_wide * xs_wide
    gated_wide, gated_pull = jax.vjp(
        lambda scan_in, gate_in: scan_in * jax.nn.silu(gate_in), scanned_y, gate_z
    )
    gated = gated_wide.astype(jnp.bfloat16)
    mixed = jnp.dot(gated, full_out, preferred_element_type=jnp.float32)
    residual = flat_in + mixed
    norm_two_value, norm_two_pull = jax.vjp(rms_scale, residual, full_moe.astype(jnp.float32))
    normed_two = norm_two_value.astype(jnp.bfloat16)
    logits = jnp.dot(normed_two, full_router, preferred_element_type=jnp.float32)
    probability = jax.nn.softmax(logits, axis=-1)
    route_ids = routes[0, :, 0]
    one_hot = route_ids[:, None] == jnp.arange(experts, dtype=jnp.int32)[None, :]
    one_float = one_hot.astype(jnp.float32)
    gate_val = jnp.sum(probability * one_float, axis=1)
    running = jnp.cumsum(one_hot.astype(jnp.int32), axis=0)
    slot_index = jnp.sum(running * one_hot.astype(jnp.int32), axis=1) - 1
    room = -(-capacity // 16) * 16
    target = route_ids * room + slot_index
    grad_out = cotangent[0].astype(jnp.float32)
    grad_pick = (grad_out * gate_val[:, None]).astype(jnp.bfloat16)
    picked, grad_from_experts, grad_expert_in, grad_w_out = run_experts(
        normed_two, grad_pick, target, weights_in, expert_out[0], experts, room, 2
    )
    kept_in, leaving = collect_slices(grad_expert_in)
    picked = picked.astype(jnp.float32)
    grad_from_experts = grad_from_experts.astype(jnp.float32)
    outcome = residual + gate_val[:, None] * picked
    out_block = outcome.astype(jnp.bfloat16)[None]
    grad_gate = jnp.sum(grad_out * picked, axis=1)
    grad_probs = grad_gate[:, None] * one_float
    grad_logits = (
        probability * (grad_probs - jnp.sum(grad_probs * probability, axis=1, keepdims=True))
    ).astype(jnp.bfloat16)
    grad_router = contract(grad_logits, normed_two, 0, 0)
    grad_normed_two = grad_from_experts + jnp.dot(
        grad_logits, full_router.T, preferred_element_type=jnp.float32
    )
    grad_resid_norm, grad_moe_gain = norm_two_pull(grad_normed_two)
    grad_resid = grad_out + grad_resid_norm
    grad_mixed = grad_resid.astype(jnp.bfloat16)
    grad_gated = jnp.dot(grad_mixed, full_out.T, preferred_element_type=jnp.float32)
    grad_out_proj = jnp.dot(gated.T, grad_mixed, preferred_element_type=jnp.float32)
    grad_y, grad_z = gated_pull(grad_gated)
    grad_z = grad_z.astype(jnp.bfloat16)
    along_b, slope, grad_bs, grad_cs, grad_a, partial_sums, arrived = scan_backward(
        sizes,
        masked_step,
        push,
        grad_y,
        b_turned,
        c_turned,
        rates,
        products,
        (dot(normed_one.T, grad_z).astype(jnp.bfloat16), grad_out_proj.astype(jnp.bfloat16)),
        kept,
        leaving,
        4,
    )
    grad_w_in = kept_in.astype(jnp.float32) + arrived.astype(jnp.float32)
    wide_rows = jnp.concatenate(
        [gain_rows[:1], grad_moe_gain[None], jnp.zeros((6, D), jnp.float32), grad_router]
    )
    grad_inputs, own_in, own_out, own_x, own_dt, own_taps, own_decay, own_router, *vectors = finish(
        sizes,
        (along_b, slope, grad_y, dt_pre, conv_out, xs_val, conv_ext, grad_z, full_conv, full_gate),
        (
            normed_one,
            inputs[0],
            grad_resid,
            mix,
            jnp.pad(jnp.concatenate([grad_bs, grad_cs], axis=1), ((0, 0), (R, LANES - R - 2 * NS))),
            delta_low,
            same_rows,
            jnp.concatenate([by_channel[:KC], by_channel[26:27], jnp.zeros((3, DI), jnp.float32)]),
            grad_a * rates * (1.0 / LOG2E),
            wide_rows,
        ),
        partial_sums,
        experts,
        1,
    )
    own_bias, own_dtbias, own_skip, own_norm, own_moe = [values[0] for values in vectors]
    return (
        out_block,
        grad_inputs[None],
        own_norm,
        own_in,
        own_taps.T,
        own_bias,
        own_x,
        own_dt,
        own_dtbias,
        own_decay.T,
        own_skip,
        own_out,
        own_moe,
        own_router.T,
        grad_w_in[None],
        grad_w_out[None],
    )


def solution(mesh):
    placed = (
        P("exp", "ctx", None),
        P("exp", "ctx"),
        P("exp", "ctx", None),
        P("exp", "ctx", None),
        P(("ctx", "exp")),
        P(("ctx", "exp"), None),
        P(("ctx", "exp"), None),
        P(("ctx", "exp")),
        P(("ctx", "exp"), None),
        P(None, ("ctx", "exp")),
        P(("ctx", "exp")),
        P(("ctx", "exp"), None),
        P(("ctx", "exp")),
        P(("ctx", "exp"), None),
        P(("ctx", "exp")),
        P(("ctx", "exp"), None),
        P("exp", None, "ctx"),
        P("exp", "ctx", None),
    )
    return jax.shard_map(
        body,
        mesh=mesh,
        in_specs=placed,
        out_specs=(
            P("exp", "ctx", None),
            P("exp", "ctx", None),
            P(("ctx", "exp")),
            P(("ctx", "exp"), None),
            P(("ctx", "exp"), None),
            P(("ctx", "exp")),
            P(("ctx", "exp"), None),
            P(None, ("ctx", "exp")),
            P(("ctx", "exp")),
            P(("ctx", "exp"), None),
            P(("ctx", "exp")),
            P(("ctx", "exp"), None),
            P(("ctx", "exp")),
            P(("ctx", "exp"), None),
            P("exp", None, "ctx"),
            P("exp", "ctx", None),
        ),
        check_vma=False,
    )
```

```python
import functools

import jax
import jax.numpy as jnp
from jax import lax
from jax.experimental import pallas as pl
from jax.experimental.pallas import tpu as pltpu
from jax.sharding import PartitionSpec as P

D = 768
DI = 1536
NS = 16
R = 48
KC = 4
LANES = 128
UNROLL = 8
LOG2E = 1.4426950408889634


EPS = 1e-05
MESH = pl.DeviceIdType.MESH
ROWS_AT_ONCE = 16
EDGE = 16

def tile(ref, base, lanes):
    return ref[pl.ds(pl.multiple_of(base, UNROLL), UNROLL), lanes]

def row(rows_now, place):
    return jnp.broadcast_to(rows_now[place : place + 1], (NS, LANES))

def cost(tokens, channels, share):
    size = tokens * channels * NS
    return pl.CostEstimate(flops=size * share, transcendentals=size, bytes_accessed=size * share)


def pick(channels):
    return 512 if channels % 512 == 0 else 128


def rms_scale(values, gain):
    return values * lax.rsqrt(jnp.mean(values * values, axis=-1, keepdims=True) + EPS) * gain


def bit_positions(sizes):
    return [(axis, size.bit_length() - 2 - k) for axis, size in sizes for k in range(size.bit_length() - 1)]


def own_bit(place):
    axis, level = place
    return lax.rem(lax.axis_index(axis) // 2**level, 2)


def partner(place):
    axis, level = place
    where = {"ctx": lax.axis_index("ctx"), "exp": lax.axis_index("exp")}
    where[axis] = where[axis] + (1 - 2 * own_bit(place)) * 2**level
    return (where["ctx"], where["exp"])


def meet(places, *others):
    barrier = pltpu.get_barrier_semaphore()
    for device in [partner(place) for place in places] + list(others):
        pl.semaphore_signal(barrier, inc=1, device_id=device, device_id_type=MESH)
    pl.semaphore_wait(barrier, len(places) + len(others))


class GatherFlow:
    def __init__(self, places, streams, dims, shards, wholes, send_sems, recv_sems, local_sems):
        self.places, self.streams, self.dims, self.shards, self.wholes = places, streams, dims, shards, wholes
        self.sems = send_sems, recv_sems, local_sems
        self.bits = [own_bit(place) for place in places]

    def view(self, number, have):
        array, cols, order, begin = self.streams[number]
        index = tuple(slice(None) if p in have else self.bits[p] for p in self.dims)
        return self.wholes[array].at[index + (slice(None), cols)]

    def shard(self, number):
        array, cols, order, begin = self.streams[number]
        return self.shards[array].at[(slice(None),) * (begin + 1) + (cols,)]

    def own(self, number):
        array, cols, order, begin = self.streams[number]
        return pltpu.make_async_copy(self.shard(number), self.view(number, order[:begin]), self.sems[2].at[number])

    def flight(self, number, stage):
        array, cols, order, begin = self.streams[number]
        target = self.view(number, order[: begin + stage])
        return pltpu.make_async_remote_copy(
            src_ref=self.shard(number) if stage == 0 else target,
            dst_ref=target,
            send_sem=self.sems[0].at[number, stage],
            recv_sem=self.sems[1].at[number, stage],
            device_id=partner(self.places[order[begin + stage]]),
            device_id_type=MESH,
        )

    def stages(self, number):
        array, cols, order, begin = self.streams[number]
        return len(order) - begin

    def start(self):
        for number in range(len(self.streams)):
            self.flight(number, 0).start()
        for number in range(len(self.streams)):
            self.own(number).start()

    def advance(self, stage):
        for number in range(len(self.streams)):
            if stage >= self.stages(number):
                continue
            if stage == 0:
                self.own(number).wait()
            self.flight(number, stage).wait_recv()
            if stage + 1 < self.stages(number):
                self.flight(number, stage + 1).start()

    def finish(self):
        for number in range(len(self.streams)):
            for stage in range(self.stages(number)):
                self.flight(number, stage).wait_send()


def pack_small(small, square, channel_pack, width_pack):
    x_ref, dt_ref, taps_ref, decay_ref, vector_ref, pair_ref, router_ref = small
    rows, thin = channel_pack.shape[0], width_pack.shape[0]

    def laid(*pieces):
        square[...] = jnp.zeros_like(square)
        for first, ref in pieces:
            square[first : first + ref.shape[0], : ref.shape[1]] = ref[...].astype(jnp.float32)
        return square[...]

    dt_part = pltpu.roll(laid((0, dt_ref)).T, R + 2 * NS, 1)
    mix = laid((0, x_ref)) + dt_part
    channel_pack[:, :LANES] = mix[:rows].astype(jnp.bfloat16)
    turned_rows = laid((0, taps_ref), (8, decay_ref), (24, vector_ref)).T
    channel_pack[:, LANES:] = turned_rows[:rows].astype(jnp.bfloat16)
    width_pack[...] = laid((0, pair_ref), (8, router_ref)).T[:thin].astype(jnp.bfloat16)


def gather_kernel(places, streams, extra_streams, far, *refs):
    small = refs[:7]
    in_ref, out_ref, rows_ref, ids_ref, leaving = refs[7:12]
    extra = 2
    wholes, prior_ref, prior_ids, arriving = refs[12:17], refs[17], refs[18], refs[19]
    (square, channel_pack, width_pack, send_sems, recv_sems, local_sems, late_send, late_recv, late_local,
     edge_sems, moved_sems) = refs[20:]
    split = in_ref.shape[1] // 2
    shards = (in_ref.at[:, :split], channel_pack, width_pack, in_ref.at[:, split:], out_ref)
    pack_small(small, square, channel_pack, width_pack)
    count = 3
    flow = GatherFlow(
        places, streams, range(len(places)), shards[:count], wholes[:count], send_sems, recv_sems, local_sems
    )
    late = GatherFlow(
        places, extra_streams, far, shards[count:], wholes[count:], late_send, late_recv, late_local
    )
    blocks = lax.axis_size("ctx")
    here, line = lax.axis_index("ctx"), lax.axis_index("exp")
    meet(places, (lax.rem(here + 1, blocks), line), (lax.rem(here + blocks - 1, blocks), line))
    flow.start()
    tokens = rows_ref.shape[0]
    edges = [
        pltpu.make_async_remote_copy(
            src_ref=source,
            dst_ref=target,
            send_sem=edge_sems.at[0, k],
            recv_sem=edge_sems.at[1, k],
            device_id=(lax.rem(here + 1, blocks), line),
            device_id_type=MESH,
        )
        for k, (source, target) in enumerate(
            (
                (rows_ref.at[pl.ds(tokens - EDGE, EDGE)], prior_ref),
                (ids_ref.at[:, pl.ds(tokens - LANES, LANES)], prior_ids),
            )
        )
    ]
    for edge in edges:
        edge.start()
    move = row_half(leaving, arriving, moved_sems, ("ctx", blocks.bit_length() - 2), 0)
    move.start()
    stages, behind = len(places), len(far)
    for stage in range(stages):
        flow.advance(stage)
        if stage == behind - 2:
            late.start()
        if stage >= behind and stage - behind < behind:
            late.advance(stage - behind)
    for stage in range(stages - behind, behind):
        late.advance(stage)
    flow.finish()
    late.finish()
    for edge in edges:
        edge.wait()
    move.wait()


def orders_of(places):
    core = places.index(("ctx", 0))
    rows = [k for k, place in enumerate(places) if place[0] == "ctx" and place[1] > 0]
    near = places.index(("exp", 0))
    return [core] + rows + [near] + far_of(places), [core, near] + rows + far_of(places)


def far_of(places):
    return [k for k, place in sorted(enumerate(places), key=lambda item: item[1][1]) if place[0] == "exp" and place[1] > 0]


def halves(arrays, first, second, begin=None):
    streams = []
    for array, values in enumerate(arrays):
        width = values.shape[-1]
        rest = () if begin is None else (begin,)
        if width % 256 == 0:
            streams.append((array, slice(0, width // 2), first) + rest)
            streams.append((array, slice(width // 2, width), second) + rest)
        else:
            streams.append((array, slice(0, width), first if array % 2 else second) + rest)
    return streams


def gather_orders(places):
    return [tuple(reversed(order)) for order in orders_of(places)]


def gather_all(sizes, small, in_proj, out_proj, rows_in, ids, leaving, identity):
    places = bit_positions(sizes)
    stages = len(places)
    far = sorted(far_of(places))
    half = jnp.bfloat16
    rows, thin, split = small[0].shape[0], in_proj.shape[0], in_proj.shape[1] // 2
    shape = jax.ShapeDtypeStruct
    shards = shape((thin, split), half), shape((rows, 2 * LANES), half), shape((thin, LANES), half)
    extra = shape((thin, split), half), shape(out_proj.shape, half)
    streams = halves(shards, *gather_orders(places), begin=0)
    late = [(k, slice(0, part.shape[1]), tuple(reversed(far_of(places))), 0) for k, part in enumerate(extra)]
    anywhere = pl.BlockSpec(memory_space=pl.ANY)
    inside = pl.BlockSpec(memory_space=pltpu.VMEM)
    out = pl.pallas_call(
        functools.partial(gather_kernel, places, streams, late, far),
        in_specs=[inside] * 7 + [anywhere] * 5,
        out_specs=[anywhere] * 8,
        out_shape=[shape((2,) * stages + shard.shape, half) for shard in shards]
        + [shape((2,) * len(far) + part.shape, half) for part in extra]
        + [shape((EDGE, rows_in.shape[1]), half), shape((1, LANES), jnp.int32), shape(leaving.shape, half)],
        scratch_shapes=[
            pltpu.VMEM((LANES, LANES), jnp.float32),
            pltpu.VMEM((rows, 2 * LANES), half),
            pltpu.VMEM((thin, LANES), half),
            pltpu.SemaphoreType.DMA((len(streams), stages)),
            pltpu.SemaphoreType.DMA((len(streams), stages)),
            pltpu.SemaphoreType.DMA((len(streams),)),
            pltpu.SemaphoreType.DMA((len(late), len(far))),
            pltpu.SemaphoreType.DMA((len(late), len(far))),
            pltpu.SemaphoreType.DMA((len(late),)),
            pltpu.SemaphoreType.DMA((2, 2)),
            pltpu.SemaphoreType.DMA((2, 2)),
        ],
        compiler_params=pltpu.CompilerParams(collective_id=identity, has_side_effects=True),
        name="gather_all",
    )(*small, in_proj, out_proj, rows_in, ids, leaving)
    return [whole.reshape((-1,) + whole.shape[stages + 1 :]) for whole in out[:3]], out[3:5], out[7], out[5], out[6]


class ReduceFlow:
    def __init__(self, places, streams, dims, parts, totals, landing, send_sems, recv_sems):
        self.places, self.streams, self.dims, self.parts, self.totals = places, streams, dims, parts, totals
        self.landing, self.sems = landing, (send_sems, recv_sems)
        self.bits = [own_bit(place) for place in places]
        self.first = []
        for array, cols, order in streams:
            self.first.append(sum(len(other[2]) for other in streams[: len(self.first)]))

    def spot(self, number, stage):
        return self.landing[self.first[number] + stage]

    def side(self, number, stage, value):
        array, cols, order = self.streams[number]
        left = [p for p in self.dims if p not in order[:stage]]
        index = tuple(value if p == order[stage] else slice(None) for p in left)
        if stage == 0:
            return self.parts[array].at[index + (slice(None), cols)]
        return self.spot(number, stage - 1).at[index]

    def flight(self, number, stage):
        order = self.streams[number][2]
        return pltpu.make_async_remote_copy(
            src_ref=self.side(number, stage, 1 - self.bits[order[stage]]),
            dst_ref=self.spot(number, stage),
            send_sem=self.sems[0].at[number, stage],
            recv_sem=self.sems[1].at[number, stage],
            device_id=partner(self.places[order[stage]]),
            device_id_type=MESH,
        )

    def start(self):
        for number in range(len(self.streams)):
            self.flight(number, 0).start()

    def advance(self, stage):
        for number, (array, cols, order) in enumerate(self.streams):
            if stage >= len(order):
                continue
            self.flight(number, stage).wait_recv()
            mine = self.side(number, stage, self.bits[order[stage]])
            there = self.spot(number, stage)
            depth = len(self.dims) - stage - 1
            final = stage + 1 == len(order)
            if depth == 0:
                self.totals[array][:, cols] = there[...].astype(jnp.float32) + mine[...].astype(jnp.float32)
                continue

            def add(index, unused, there=there, mine=mine, depth=depth, final=final, array=array, cols=cols):
                at = tuple(lax.rem(index // 2 ** (depth - 1 - k), 2) for k in range(depth))
                value = (there[at].astype(jnp.float32) + mine[at].astype(jnp.float32)).astype(there.dtype)
                if final:
                    self.totals[array][at + (slice(None), cols)] = value
                else:
                    there[at] = value
                return unused

            lax.fori_loop(0, 2**depth, add, 0)
            if not final:
                self.flight(number, stage + 1).start()

    def finish(self):
        for number in range(len(self.streams)):
            for stage in range(len(self.streams[number][2])):
                self.flight(number, stage).wait_send()


def landing_of(streams, dims, divided):
    landing = []
    for array, cols, order in streams:
        for stage in range(len(order)):
            rows = divided[array].shape[-2]
            landing.append(pltpu.VMEM((2,) * (len(dims) - stage - 1) + (rows, cols.stop - cols.start), jnp.bfloat16))
    return landing


def flights(streams):
    shape = (len(streams), max(len(order) for array, cols, order in streams))
    return [pltpu.SemaphoreType.DMA(shape)] * 2


def dot(left, right):
    return jnp.dot(left, right, preferred_element_type=jnp.float32)


def contract(left, right, left_dim, right_dim):
    return lax.dot_general(left, right, (((left_dim,), (right_dim,)), ((), ())), preferred_element_type=jnp.float32)


def lanes_of(group, width, k):
    return pl.ds(pl.multiple_of(group * width + k * LANES, LANES), LANES)


def spread_columns(source_ref, wide_ref):
    def chunk(index, unused):
        base = pl.multiple_of(index * LANES, LANES)
        now = source_ref[:, pl.ds(base, LANES)]
        for place in range(LANES):
            wide_ref[base + place] = jnp.broadcast_to(now[:, place : place + 1], (NS, LANES))
        return unused

    lax.fori_loop(0, source_ref.shape[1] // LANES, chunk, 0)


def end_pass(width, step_ref, push_ref, wide_b, rate_ref, state_ref, hook):
    rows, channels = step_ref.shape
    count = width // LANES

    def group_body(group, unused):
        pieces = [lanes_of(group, width, k) for k in range(count)]
        rates = [rate_ref[:, lanes] for lanes in pieces]

        def block(index, states):
            states = list(states)
            steps = [tile(step_ref, index * UNROLL, lanes) for lanes in pieces]
            pushes = [tile(push_ref, index * UNROLL, lanes) for lanes in pieces]
            for place in range(UNROLL):
                b_now = wide_b[index * UNROLL + place]
                for k in range(count):
                    decay = jnp.exp2(row(steps[k], place) * rates[k])
                    states[k] = decay * states[k] + b_now * row(pushes[k], place)
            return tuple(states)

        zero = jnp.zeros((NS, LANES), jnp.float32)
        states = lax.fori_loop(0, rows // UNROLL, block, (zero,) * count)
        for k, lanes in enumerate(pieces):
            state_ref[:, lanes] = states[k]
        hook(group)
        return unused

    lax.fori_loop(0, channels // width, group_body, 0)


def out_pass(width, step_ref, push_ref, wide_b, wide_c, rate_ref, state_ref, y_ref, kept_buf, kept_copy, hook):
    rows, channels = step_ref.shape
    count = width // LANES
    span = kept_buf.shape[1]
    blocks = rows // span

    def time_body(number, unused):
        slot = lax.rem(number, 2)

        @pl.when(number >= 2)
        def _():
            kept_copy(number - 2, slot).wait()

        def group_body(group, unused_inner):
            pieces = [lanes_of(group, width, k) for k in range(count)]
            rates = [rate_ref[:, lanes] for lanes in pieces]

            def block(index, states):
                states = list(states)
                base = number * span + index * UNROLL
                steps = [tile(step_ref, base, lanes) for lanes in pieces]
                pushes = [tile(push_ref, base, lanes) for lanes in pieces]
                trees = [Tree(True) for k in range(count)]
                for place in range(UNROLL):
                    b_now = wide_b[base + place]
                    c_now = wide_c[base + place]
                    for k, lanes in enumerate(pieces):
                        decay = jnp.exp2(row(steps[k], place) * rates[k])
                        states[k] = decay * states[k] + b_now * row(pushes[k], place)
                        kept_buf[slot, index * UNROLL + place, :, lanes] = states[k].astype(kept_buf.dtype)
                        trees[k].push(place, states[k] * c_now)
                for k, lanes in enumerate(pieces):
                    y_ref[pl.ds(pl.multiple_of(base, UNROLL), UNROLL), lanes] = trees[k].result
                return tuple(states)

            states = lax.fori_loop(0, span // UNROLL, block, tuple(state_ref[:, lanes] for lanes in pieces))
            for k, lanes in enumerate(pieces):
                state_ref[:, lanes] = states[k]
            return unused_inner

        lax.fori_loop(0, channels // width, group_body, 0)
        kept_copy(number, slot).start()
        hook(number)
        return unused

    lax.fori_loop(0, blocks, time_body, 0)
    for number in range(max(0, blocks - 2), blocks):
        kept_copy(number, number % 2).wait()


def inflow_pass(width, step_ref, grad_ref, wide_c, rate_ref, flow_ref, hook):
    rows, channels = step_ref.shape
    count = width // LANES

    def group_body(group, unused):
        hook(group)
        pieces = [lanes_of(group, width, k) for k in range(count)]
        rates = [rate_ref[:, lanes] for lanes in pieces]

        def block(index, flows):
            flows = list(flows)
            base = rows - UNROLL - index * UNROLL
            steps = [tile(step_ref, base, lanes) for lanes in pieces]
            grads = [tile(grad_ref, base, lanes) for lanes in pieces]
            for place in reversed(range(UNROLL)):
                c_now = wide_c[base + place]
                for k in range(count):
                    decay = jnp.exp2(row(steps[k], place) * rates[k])
                    flows[k] = decay * (c_now * row(grads[k], place) + flows[k])
            return tuple(flows)

        zero = jnp.zeros((NS, LANES), jnp.float32)
        flows = lax.fori_loop(0, rows // UNROLL, block, (zero,) * count)
        for k, lanes in enumerate(pieces):
            flow_ref[:, lanes] = flows[k]
        return unused

    lax.fori_loop(0, channels // width, group_body, 0)


class Tree:
    def __init__(self, rising):
        self.rising, self.held, self.result = rising, {}, None

    def push(self, place, value):
        now = value[:UNROLL] + value[UNROLL:]
        level = 0
        while 1 << level < UNROLL:
            if (place >> level) % 2 == (0 if self.rising else 1):
                self.held[level] = now
                return
            first, second = (self.held[level], now) if self.rising else (now, self.held[level])
            now = self.merge(first, second, 1 << level)
            level += 1
        self.result = now

    def merge(self, first, second, distance):
        low = (lax.broadcasted_iota(jnp.int32, (UNROLL, LANES), 0) & distance) == 0
        keep = jnp.where(low, first, second)
        give = jnp.where(low, second, first)
        other = pltpu.roll(give, distance, 0)
        if 2 * distance != UNROLL:
            other = jnp.where(low, pltpu.roll(give, UNROLL - distance, 0), other)
        return keep + other


def lane_sums(part_ref):
    values = part_ref[...].reshape(-1, LANES)
    high = values.astype(jnp.bfloat16)
    low = (values - high.astype(jnp.float32)).astype(jnp.bfloat16)
    ones = jnp.ones((UNROLL, LANES), jnp.bfloat16)
    return contract(ones, high, 1, 1) + contract(ones, low, 1, 1)


def adjoint_pass(width, step_ref, push_ref, grad_ref, wide_b, wide_c, rate_ref, flow_ref, kept_buf, kept_copy,
                 along_ref, slope_ref, gb_ref, gc_ref, ga_ref, part_b, part_c, hook):
    rows, channels = step_ref.shape
    count = width // LANES
    span = kept_buf.shape[1] - 1
    blocks = rows // span
    ga_ref[...] = jnp.zeros_like(ga_ref)

    def time_body(order, unused):
        slot = lax.rem(order, 2)
        number = blocks - 1 - order
        kept_copy(number, slot).wait()
        part_b[...] = jnp.zeros_like(part_b)
        part_c[...] = jnp.zeros_like(part_c)

        def group_body(group, unused_inner):
            pieces = [lanes_of(group, width, k) for k in range(count)]
            rates = [rate_ref[:, lanes] for lanes in pieces]

            def block(index, carried):
                flows = list(carried[:count])
                sums = list(carried[count : 2 * count])
                current = list(carried[2 * count :])
                local = span - UNROLL - index * UNROLL
                base = number * span + local
                steps = [tile(step_ref, base, lanes) for lanes in pieces]
                pushes = [tile(push_ref, base, lanes) for lanes in pieces]
                grads = [tile(grad_ref, base, lanes) for lanes in pieces]
                alongs = [Tree(False) for k in range(count)]
                slopes = [Tree(False) for k in range(count)]
                for place in reversed(range(UNROLL)):
                    b_now = wide_b[base + place]
                    c_now = wide_c[base + place]
                    gb = gc = None
                    for k, lanes in enumerate(pieces):
                        prior = kept_buf[slot, local + place, :, lanes].astype(jnp.float32)
                        step = row(steps[k], place)
                        grad = row(grads[k], place)
                        decay = jnp.exp2(step * rates[k])
                        adjoint = c_now * grad + flows[k]
                        flows[k] = decay * adjoint
                        decay_grad = flows[k] * prior
                        alongs[k].push(place, adjoint * b_now)
                        slopes[k].push(place, decay_grad * rates[k])
                        sums[k] = sums[k] + decay_grad * step
                        here_b = adjoint * row(pushes[k], place)
                        here_c = current[k] * grad
                        gb = here_b if gb is None else gb + here_b
                        gc = here_c if gc is None else gc + here_c
                        current[k] = prior
                    part_b[local + place] += gb
                    part_c[local + place] += gc
                where = pl.ds(pl.multiple_of(base, UNROLL), UNROLL)
                for k, lanes in enumerate(pieces):
                    along_ref[where, lanes] = alongs[k].result
                    slope_ref[where, lanes] = slopes[k].result
                return tuple(flows + sums + current)

            carried = lax.fori_loop(
                0,
                span // UNROLL,
                block,
                tuple(flow_ref[:, lanes] for lanes in pieces)
                + tuple(ga_ref[:, lanes] for lanes in pieces)
                + tuple(kept_buf[slot, span, :, lanes].astype(jnp.float32) for lanes in pieces),
            )
            for k, lanes in enumerate(pieces):
                flow_ref[:, lanes] = carried[k]
                ga_ref[:, lanes] = carried[count + k]
            return unused_inner

        lax.fori_loop(0, channels // width, group_body, 0)
        gb_ref[number] = lane_sums(part_b)
        gc_ref[number] = lane_sums(part_c)

        @pl.when(order + 2 < blocks)
        def _():
            kept_copy(number - 2, slot).start()

        hook(order)
        return unused

    lax.fori_loop(0, blocks, time_body, 0)


def share(source, target, send_sems, recv_sems):
    blocks = lax.axis_size("ctx")
    here, line = lax.axis_index("ctx"), lax.axis_index("exp")
    copies = []
    for step in range(1, blocks):
        copies.append(
            pltpu.make_async_remote_copy(
                src_ref=source,
                dst_ref=target.at[here],
                send_sem=send_sems.at[step],
                recv_sem=recv_sems.at[step],
                device_id=(lax.rem(here + step, blocks), line),
                device_id_type=MESH,
            )
        )
        copies[-1].start()
    target[here] = source[...]
    return copies


def row_peers():
    blocks = lax.axis_size("ctx")
    here, line = lax.axis_index("ctx"), lax.axis_index("exp")
    return [(lax.rem(here + step, blocks), line) for step in range(1, blocks)]


def row_half(source, target, sems, place, k):
    size = source.shape[0] // 2
    return pltpu.make_async_remote_copy(
        src_ref=source.at[pl.ds(k * size, size)],
        dst_ref=target.at[pl.ds(k * size, size)],
        send_sem=sems.at[0, k],
        recv_sem=sems.at[1, k],
        device_id=partner(place),
        device_id_type=MESH,
    )


def front(in_ref, prior_ref, prior_ids, ids_ref, routes_ref, weights, loads, room, outs, scratch, saves):
    normed_ref, bt_ref, ct_ref, rate_ref, chan_ref, gain_ref, delta_ref, same_ref, target_ref = outs
    nx, ext, conv, xs, pre, step, push = scratch
    conv_w, channel_ref, width_ref = weights
    for load in loads[1:]:
        load.wait()
    tokens, channels = xs.shape
    width = in_ref.shape[1]
    mine = lax.axis_index("ctx")
    gain_rows = jnp.concatenate(
        [width_ref[at : at + LANES, :].astype(jnp.float32).T for at in range(0, width, LANES)], axis=1
    )
    gain_ref[...] = gain_rows[:8]
    for at in range(0, channels, LANES):
        chan_ref[:, at : at + LANES] = channel_ref[at : at + LANES, LANES:].astype(jnp.float32).T[:32]
    rate_ref[...] = -jnp.exp(chan_ref[8 : 8 + NS, :]) * LOG2E
    gain = gain_ref[0:1, :]

    def normed(values):
        x = values.astype(jnp.float32)
        return (x * lax.rsqrt(jnp.mean(x * x, axis=-1, keepdims=True) + EPS) * gain).astype(jnp.bfloat16)

    nx[:EDGE, :] = normed(prior_ref[...])

    def norm_rows(index, unused):
        at = pl.ds(pl.multiple_of(index * 16, 16), 16)
        value = normed(in_ref[at, :])
        normed_ref[at, :] = value
        nx[pl.ds(pl.multiple_of(EDGE + index * 16, 16), 16), :] = value
        return unused

    lax.fori_loop(0, tokens // 16, norm_rows, 0)
    def column(values):
        return jnp.broadcast_to(values.astype(jnp.float32), (LANES, LANES)).T

    def columns(ref):
        return jnp.concatenate([column(ref[:, at : at + LANES]) for at in range(0, tokens, LANES)], axis=0)

    ids = jnp.where(mine > 0, column(prior_ids[...])[LANES - EDGE :], -1.0)
    own_ids = columns(ids_ref)
    every_id = jnp.concatenate([ids, own_ids], axis=0)
    for j in range(1, KC):
        same_ref[j - 1] = (pltpu.roll(every_id, j, 0)[EDGE:] == own_ids).astype(jnp.float32)
    routes = columns(routes_ref)
    chosen = (routes == lax.broadcasted_iota(jnp.int32, routes.shape, 1).astype(jnp.float32)).astype(jnp.float32)
    square = (tokens, tokens)
    until = lax.broadcasted_iota(jnp.int32, square, 0) >= lax.broadcasted_iota(jnp.int32, square, 1)
    running = dot(until.astype(jnp.float32).astype(jnp.bfloat16), chosen.astype(jnp.bfloat16))
    slot = jnp.sum(running * chosen, axis=1, keepdims=True) - 1.0
    target_ref[...] = routes * room + slot
    piece = 2 * LANES
    loads[0].wait()

    def conv_piece(index, unused):
        lanes = pl.ds(pl.multiple_of(index * piece, piece), piece)
        low = dot(nx[...], conv_w[:, lanes]).astype(jnp.bfloat16)
        ext[:, lanes] = low
        value = low.astype(jnp.float32)
        out = chan_ref[24:25, lanes] + chan_ref[3:4, lanes] * value[EDGE:]
        for j in range(1, KC):
            same = jnp.concatenate([same_ref[j - 1]] * 2, axis=1)
            out = out + chan_ref[3 - j : 4 - j, lanes] * pltpu.roll(value, j, 0)[EDGE:] * same
        conv[:, lanes] = out
        xs[:, lanes] = (out / (1.0 + jnp.exp(-out))).astype(jnp.bfloat16)
        return unused

    lax.fori_loop(0, channels // piece, conv_piece, 0)
    for save in saves[:3]:
        save.start()
    projected = dot(xs[...], channel_ref[:, :LANES])
    lane = lax.broadcasted_iota(jnp.int32, projected.shape, 1)
    delta_ref[...] = jnp.where(lane >= R + 2 * NS, pltpu.roll(projected, R + 2 * NS, 1), 0.0).astype(jnp.bfloat16)
    for at in range(0, tokens, LANES):
        block = projected[at : at + LANES].T
        bt_ref[:, at : at + LANES] = block[R : R + NS]
        ct_ref[:, at : at + LANES] = block[R + NS : R + 2 * NS]

    def step_piece(index, unused):
        lanes = pl.ds(pl.multiple_of(index * piece, piece), piece)
        value = contract(delta_ref[...], channel_ref[lanes, :LANES], 1, 1) + chan_ref[25:26, lanes]
        pre[:, lanes] = value
        size = jnp.maximum(value, 0.0) + jnp.log1p(jnp.exp(-jnp.abs(value)))
        push[:, lanes] = size * xs[:, lanes].astype(jnp.float32)
        keep = jnp.concatenate([same_ref[0]] * 2, axis=1)
        step[:, lanes] = jnp.where(keep > 0, size, 1e30)
        return unused

    lax.fori_loop(0, channels // piece, step_piece, 0)
    for save in saves[3:]:
        save.start()


def forward_kernel(places, streams, width, room, *refs):
    in_ref, prior_ref, prior_ids, ids_ref, routes_ref = refs[:5]
    weights_from = refs[5:8]
    shards, leaving = refs[8:10], refs[10]
    y_ref, product_ref = refs[12:14]
    front_outs = refs[14:23]
    kept_ref = refs[23]
    saved = refs[24:30]
    wholes, arriving = refs[30:32], refs[32]
    scratch = refs[33:40]
    weights = refs[40:43]
    (wide_b, wide_c, kept_buf, first_buf, state_ref, message, products, ends,
     load_sems, kept_sems, first_sem, share_sems, save_sems, moved_sems, send_sems, recv_sems, local_sems) = refs[43:]
    loads = [pltpu.make_async_copy(weights_from[k], weights[k], load_sems.at[k]) for k in range(3)]
    for load in reversed(loads):
        load.start()
    bt_ref, ct_ref, rate_ref = front_outs[1:4]
    step_ref, push_ref = scratch[5:7]
    blocks = lax.axis_size("ctx")
    position = lax.axis_index("ctx")
    span = kept_buf.shape[1]
    flow = GatherFlow(places, streams, range(len(places)), shards, wholes, send_sems, recv_sems, local_sems)
    meet([place for place in places if place[0] == "exp"], *row_peers())
    flow.start()
    move = row_half(leaving, arriving, moved_sems, ("ctx", blocks.bit_length() - 2), 1)
    move.start()
    saves = [
        pltpu.make_async_copy(scratch[k + 1], saved[k], save_sems.at[k]) for k in range(6)
    ]
    front(in_ref, prior_ref, prior_ids, ids_ref, routes_ref, weights, loads, room, front_outs, scratch, saves)

    message[0] = jnp.exp2(jnp.sum(step_ref[...], axis=0, keepdims=True) * rate_ref[...]).astype(jnp.bfloat16)
    early = share(message.at[0], products, share_sems.at[0], share_sems.at[1])
    spread_columns(bt_ref, wide_b)
    spread_columns(ct_ref, wide_c)
    end_pass(width, step_ref, push_ref, wide_b, rate_ref, state_ref, lambda group: None)
    message[1] = state_ref[...].astype(jnp.bfloat16)
    late = share(message.at[1], ends, share_sems.at[2], share_sems.at[3])
    flow.advance(0)
    for copy in early + late:
        copy.wait_recv()
    start = jnp.zeros(state_ref.shape, jnp.float32)
    for index in range(blocks):
        folded = products[index].astype(jnp.float32) * start + ends[index].astype(jnp.float32)
        start = jnp.where(index < position, folded, start)
    state_ref[...] = start
    product_ref[...] = products[...]
    first_buf[0] = start.astype(jnp.bfloat16)
    first_copy = pltpu.make_async_copy(first_buf, kept_ref.at[pl.ds(0, 1)], first_sem)
    first_copy.start()

    def kept_copy(number, slot):
        return pltpu.make_async_copy(
            kept_buf.at[slot], kept_ref.at[pl.ds(1 + number * span, span)], kept_sems.at[slot]
        )

    def hook(number):
        @pl.when(number == 3)
        def _():
            flow.advance(1)

    out_pass(width, step_ref, push_ref, wide_b, wide_c, rate_ref, state_ref, y_ref, kept_buf, kept_copy, hook)
    for stage in range(2, max(flow.stages(number) for number in range(len(streams)))):
        flow.advance(stage)
    flow.finish()
    first_copy.wait()
    for save in saves:
        save.wait()
    for copy in early + late:
        copy.wait_send()
    move.wait()


def scan_forward(sizes, rows_in, prior, ids, weights, room, shards, leaving, begun, identity, span=64):
    places = bit_positions(sizes)
    stages = len(places)
    begin = len(far_of(places))
    streams = halves(shards, *gather_orders(places), begin=begin)
    tokens, width = rows_in.shape
    channels = weights[0].shape[1]
    blocks = sizes[0][1]
    inside = pl.BlockSpec(memory_space=pltpu.VMEM)
    anywhere = pl.BlockSpec(memory_space=pl.ANY)
    half, full = jnp.bfloat16, jnp.float32
    shape = jax.ShapeDtypeStruct
    saved = [
        shape((EDGE + tokens, channels), half),
        shape((tokens, channels), full),
        shape((tokens, channels), half),
        shape((tokens, channels), full),
        shape((tokens, channels), full),
        shape((tokens, channels), full),
    ]
    y, products, normed, bt, ct, rates, chan, gains, delta, same, target, kept, *rest = pl.pallas_call(
        functools.partial(forward_kernel, places, streams, pick(channels), room),
        in_specs=[inside] * 5 + [anywhere] * 7,
        input_output_aliases={11: 20},
        out_specs=[inside] * 11 + [anywhere] * 10,
        out_shape=[
            shape((tokens, channels), full),
            shape((blocks, NS, channels), half),
            shape((tokens, width), half),
            shape((NS, tokens), full),
            shape((NS, tokens), full),
            shape((NS, channels), full),
            shape((32, channels), full),
            shape((8, width), full),
            shape((tokens, LANES), half),
            shape((KC - 1, tokens, LANES), full),
            shape((tokens, LANES), full),
            shape((tokens + 1, NS, channels), half),
        ]
        + saved
        + [shape((2,) * stages + shard.shape[begin:], shard.dtype) for shard in shards]
        + [shape(leaving.shape, leaving.dtype)],
        scratch_shapes=[pltpu.VMEM((EDGE + tokens, width), half)]
        + [pltpu.VMEM(value.shape, value.dtype) for value in saved]
        + [pltpu.VMEM(value.shape, value.dtype) for value in weights]
        + [
            pltpu.VMEM((tokens, NS, LANES), full),
            pltpu.VMEM((tokens, NS, LANES), full),
            pltpu.VMEM((2, span, NS, channels), half),
            pltpu.VMEM((1, NS, channels), half),
            pltpu.VMEM((NS, channels), full),
            pltpu.VMEM((2, NS, channels), half),
            pltpu.VMEM((blocks, NS, channels), half),
            pltpu.VMEM((blocks, NS, channels), half),
            pltpu.SemaphoreType.DMA((3,)),
            pltpu.SemaphoreType.DMA((2,)),
            pltpu.SemaphoreType.DMA,
            pltpu.SemaphoreType.DMA((4, blocks)),
            pltpu.SemaphoreType.DMA((6,)),
            pltpu.SemaphoreType.DMA((2, 2)),
            pltpu.SemaphoreType.DMA((len(streams), stages)),
            pltpu.SemaphoreType.DMA((len(streams), stages)),
            pltpu.SemaphoreType.DMA((len(streams),)),
        ],
        compiler_params=pltpu.CompilerParams(
            collective_id=identity, has_side_effects=True, vmem_limit_bytes=52 * 1024 * 1024
        ),
        cost_estimate=cost(tokens, channels, 9),
        name="scan_forward",
    )(rows_in, *prior, *ids, *weights, *shards, leaving, begun)
    saved, wholes, arrived = rest[:6], rest[6:8], rest[8]
    wholes = [whole.reshape((-1,) + whole.shape[stages + 1 :]) for whole in wholes]
    return y, products, normed, bt, ct, rates, chan, gains, delta, same, target, kept, saved, wholes, arrived


def backward_kernel(places, streams, marks, width, *refs):
    bt_ref, ct_ref, rate_ref, product_ref = refs[:4]
    parts = refs[4:6]
    streamed = refs[6:9]
    kept_ref, leaving = refs[9:11]
    outs = refs[11:]
    gb_ref, gc_ref, ga_ref = outs[:3]
    totals, arriving = outs[3:5], outs[5]
    rows_out = outs[6:8]
    scratch = outs[8:]
    landing = scratch[:marks]
    (step_ref, push_ref, grad_ref, along_ref, slope_ref, wide_b, wide_c, part_b, part_c, kept_buf, flow_ref, message,
     inflows, load_sems, push_sem, out_sems, kept_sems, share_sems, moved_sems, send_sems, recv_sems) = scratch[marks:]
    blocks = lax.axis_size("ctx")
    position = lax.axis_index("ctx")
    span = kept_buf.shape[1] - 1
    steps = step_ref.shape[0] // span

    def load(group, k):
        lanes = pl.ds(pl.multiple_of(group * width, LANES), width)
        source, target = ((streamed[0], step_ref), (streamed[2], grad_ref))[k]
        return pltpu.make_async_copy(source.at[:, lanes], target.at[:, lanes], load_sems.at[k, group])

    for group in range(step_ref.shape[1] // width):
        for k in range(2):
            load(group, k).start()
    push_load = pltpu.make_async_copy(streamed[1], push_ref, push_sem)
    push_load.start()

    def ready(group):
        for k in range(2):
            load(group, k).wait()

    def rows_copy(number, k):
        rows = pl.ds(number * span, span)
        return pltpu.make_async_copy((along_ref, slope_ref)[k].at[rows], rows_out[k].at[rows], out_sems.at[k, number])

    flow = ReduceFlow(places, streams, range(len(places)), parts, totals, landing, send_sems, recv_sems)

    def kept_copy(number, slot):
        return pltpu.make_async_copy(
            kept_ref.at[pl.ds(number * span, span + 1)], kept_buf.at[slot], kept_sems.at[slot]
        )

    for order in range(min(2, steps)):
        kept_copy(steps - 1 - order, order).start()
    meet([place for place in places if place[0] == "exp"], *row_peers())
    flow.start()
    move = row_half(leaving, arriving, moved_sems, ("ctx", blocks.bit_length() - 2), 0)
    move.start()
    spread_columns(bt_ref, wide_b)
    spread_columns(ct_ref, wide_c)
    inflow_pass(width, step_ref, grad_ref, wide_c, rate_ref, flow_ref, ready)
    message[...] = flow_ref[...].astype(jnp.bfloat16)
    copies = share(message, inflows, share_sems.at[0], share_sems.at[1])
    for copy in copies:
        copy.wait_recv()
    end = jnp.zeros(flow_ref.shape, jnp.float32)
    for index in reversed(range(blocks)):
        folded = inflows[index].astype(jnp.float32) + product_ref[index].astype(jnp.float32) * end
        end = jnp.where(index > position, folded, end)
    flow_ref[...] = end
    flow.advance(0)
    push_load.wait()

    def hook(order):
        for k in range(2):
            rows_copy(steps - 1 - order, k).start()

        @pl.when(order == 2)
        def _():
            flow.advance(1)

        @pl.when(order == 4)
        def _():
            flow.advance(2)

    adjoint_pass(width, step_ref, push_ref, grad_ref, wide_b, wide_c, rate_ref, flow_ref, kept_buf, kept_copy,
                 along_ref, slope_ref, gb_ref, gc_ref, ga_ref, part_b, part_c, hook)
    for stage in range(3, len(streams[0][2])):
        flow.advance(stage)
    flow.finish()
    for copy in copies:
        copy.wait_send()
    move.wait()
    for number in range(steps):
        for k in range(2):
            rows_copy(number, k).wait()


def scan_backward(sizes, step, push, grad, b_turned, c_turned, rates, products, parts, kept, leaving, identity, span=64):
    places = bit_positions(sizes)
    stages = len(places)
    far = sorted(far_of(places))
    streams = halves(parts, *[tuple(order[: stages - len(far)]) for order in orders_of(places)])
    divided = [part.reshape((2,) * stages + (-1, part.shape[1])) for part in parts]
    tokens, channels = step.shape
    blocks = sizes[0][1]
    inside = pl.BlockSpec(memory_space=pltpu.VMEM)
    anywhere = pl.BlockSpec(memory_space=pl.ANY)
    half = jnp.bfloat16
    landing = landing_of(streams, range(stages), divided)
    row_sums = jax.ShapeDtypeStruct((tokens // span, UNROLL, span * NS), jnp.float32)
    out = pl.pallas_call(
        functools.partial(backward_kernel, places, streams, len(landing), pick(channels)),
        in_specs=[inside] * 6 + [anywhere] * 5,
        out_specs=[inside] * 5 + [anywhere] * 3,
        out_shape=[row_sums, row_sums, jax.ShapeDtypeStruct((NS, channels), jnp.float32)]
        + [jax.ShapeDtypeStruct((2,) * len(far) + block.shape[-2:], half) for block in divided]
        + [jax.ShapeDtypeStruct(leaving.shape, leaving.dtype)]
        + [jax.ShapeDtypeStruct((tokens, channels), jnp.float32)] * 2,
        scratch_shapes=landing
        + [pltpu.VMEM((tokens, channels), jnp.float32)] * 5
        + [
            pltpu.VMEM((tokens, NS, LANES), jnp.float32),
            pltpu.VMEM((tokens, NS, LANES), jnp.float32),
            pltpu.VMEM((span, NS, LANES), jnp.float32),
            pltpu.VMEM((span, NS, LANES), jnp.float32),
            pltpu.VMEM((2, span + 1, NS, channels), half),
            pltpu.VMEM((NS, channels), jnp.float32),
            pltpu.VMEM((NS, channels), half),
            pltpu.VMEM((blocks, NS, channels), half),
            pltpu.SemaphoreType.DMA((2, channels // pick(channels))),
            pltpu.SemaphoreType.DMA,
            pltpu.SemaphoreType.DMA((2, tokens // span)),
            pltpu.SemaphoreType.DMA((2,)),
            pltpu.SemaphoreType.DMA((2, blocks)),
            pltpu.SemaphoreType.DMA((2, 2)),
        ]
        + flights(streams),
        compiler_params=pltpu.CompilerParams(
            collective_id=identity, has_side_effects=True, vmem_limit_bytes=56 * 1024 * 1024
        ),
        cost_estimate=cost(tokens, channels, 15),
        name="scan_backward",
    )(b_turned, c_turned, rates, products, *divided, step, push, grad, kept, leaving)
    wide_b, wide_c, grad_a, first, second, arrived, along, slope = out
    grad_bs, grad_cs = [values[:, 0].reshape(tokens, NS) for values in (wide_b, wide_c)]
    return along, slope, grad_bs, grad_cs, grad_a, (first, second), arrived


class PackedReduce(ReduceFlow):
    def __init__(self, places, streams, heads, parts, totals, landing, blocks, send_sems, recv_sems):
        super().__init__(places, streams, range(len(places)), parts, totals, landing, send_sems, recv_sems)
        self.heads, self.blocks = heads, blocks

    def side(self, number, stage, value):
        array, cols, order = self.streams[number]
        if stage == 0:
            index = tuple(value if p == order[0] else slice(None) for p in range(self.heads))
            return self.parts[array].at[index + (slice(None), cols)]
        left = [p for p in self.dims if p not in order[:stage]]
        index = tuple(value if p == order[stage] else slice(None) for p in left)
        held = self.blocks[number] if stage == 1 else self.spot(number, stage - 1)
        return held.at[index]

    def advance(self, stage):
        if stage:
            super().advance(stage)
            return
        for number, (array, cols, order) in enumerate(self.streams):
            self.flight(number, 0).wait_recv()
            mine = self.side(number, 0, self.bits[order[0]])
            there, held = self.spot(number, 0), self.blocks[number]
            tails = len(self.places) - self.heads
            size = held.shape[-2]

            def add(index, unused, mine=mine, there=there, held=held, tails=tails, size=size):
                at = tuple(lax.rem(index // 2 ** (self.heads - 2 - k), 2) for k in range(self.heads - 1))
                value = there[at].astype(jnp.float32) + mine[at].astype(jnp.float32)
                for block in range(2**tails):
                    spot = tuple(block // 2 ** (tails - 1 - k) % 2 for k in range(tails))
                    held[at + spot] = value[block * size : (block + 1) * size].astype(held.dtype)
                return unused

            lax.fori_loop(0, 2 ** (self.heads - 1), add, 0)
            self.flight(number, 1).start()


def turned(values):
    return jnp.concatenate([values[:, at : at + LANES].T for at in range(0, values.shape[1], LANES)], axis=0)


def finish_kernel(places, streams, third, late, far, marks, *refs):
    leaving = refs[22]
    refs = refs[:22] + refs[24:]
    (along_h, slope_h, grad_h, pre_h, conv_h, xs_h, ext_h, gz_h, wc_h, wg_h) = refs[:10]
    (normed_ref, in_ref, resid_ref, mix_ref, bc_ref, delta_ref, same_ref, chan_ref, decay_ref, wide_ref) = refs[10:20]
    rest_parts = refs[20:22]
    gi_ref, own_in, own_out, tot_small, tot_wide, arriving = refs[22:28]
    scratch = refs[28:]
    landing, scratch = scratch[: marks[0]], scratch[marks[0] :]
    blocks, scratch = scratch[: marks[1]], scratch[marks[1] :]
    landing3, scratch = scratch[: marks[2]], scratch[marks[2] :]
    blocks3, scratch = scratch[: marks[3]], scratch[marks[3] :]
    late_landing, scratch = scratch[: marks[4]], scratch[marks[4] :]
    (along, slope, grad, pre, conv, xs, ext, gz, wc, wg, gdt, gci, last, spill, arrived, sums, rows_s, wide_s, gn,
     part_conv, part_small, part_wide,
     block_sems, whole_sems, spill_sems, moved_sems, send_sems, recv_sems, send3, recv3, late_send, late_recv) = scratch
    tokens, channels = xs.shape
    own_conv, own_gate = own_in.at[:, :channels], own_in.at[:, channels:]
    span = tokens // block_sems.shape[1]
    heads = len([place for place in places if place[0] == "ctx"])
    flow = PackedReduce(
        places, streams, heads, (part_conv, part_small), (own_conv, tot_small), landing, blocks, send_sems, recv_sems
    )
    flow3 = PackedReduce(places, third, heads, (part_wide,), (tot_wide,), landing3, blocks3, send3, recv3)
    rest = ReduceFlow(places, late, far, rest_parts, (own_gate, own_out), late_landing, late_send, late_recv)

    streamed = ((along_h, along), (slope_h, slope), (grad_h, grad), (pre_h, pre), (xs_h, xs))

    def block_copy(k, number):
        rows = pl.ds(number * span, span)
        source, target = streamed[k]
        return pltpu.make_async_copy(source.at[rows], target.at[rows], block_sems.at[k, number])

    for number in range(tokens // span):
        for k in range(len(streamed)):
            block_copy(k, number).start()
    wholes = [
        pltpu.make_async_copy(source, target, whole_sems.at[k])
        for k, (source, target) in enumerate(((conv_h, conv), (ext_h, ext), (gz_h, gz), (wc_h, wc), (wg_h, wg)))
    ]
    for copy in wholes:
        copy.start()
    count = lax.axis_size("ctx")
    here, line = lax.axis_index("ctx"), lax.axis_index("exp")
    before = (lax.rem(here + count - 1, count), line)
    meet(places, before, (lax.rem(here + 1, count), line))
    rest.start()
    move = row_half(leaving, arriving, moved_sems, ("ctx", count.bit_length() - 2), 1)
    move.start()

    sums[...] = jnp.zeros_like(sums)
    rows_s[...] = jnp.zeros_like(rows_s)

    def first_block(number, unused):
        for k in range(len(streamed)):
            block_copy(k, number).wait()

        def some(index, unused_inner):
            at = pl.ds(pl.multiple_of(number * span + index * 16, 16), 16)
            for low in range(0, channels, LANES):
                lanes = slice(low, low + LANES)
                a, g, x, p = along[at, lanes], grad[at, lanes], xs[at, lanes].astype(jnp.float32), pre[at, lanes]
                small = jnp.exp(-jnp.abs(p))
                gated = jnp.where(p >= 0, 1.0, small) / (1.0 + small)
                step = jnp.maximum(p, 0.0) + jnp.log1p(small)
                value = (a * x + slope[at, lanes] * (1.0 / LOG2E)) * gated
                gdt[at, lanes] = value.astype(jnp.bfloat16)
                sums[0, :, lanes] += value[:8] + value[8:]
                both = g * x
                sums[1, :, lanes] += both[:8] + both[8:]
                along[at, lanes] = chan_ref[4:5, lanes] * g + a * step
            return unused_inner

        lax.fori_loop(0, span // 16, some, 0)
        return unused

    lax.fori_loop(0, tokens // span, first_block, 0)
    rows_s[25:26, :] = jnp.sum(sums[0], axis=0, keepdims=True)
    rows_s[26:27, :] = jnp.sum(sums[1], axis=0, keepdims=True)
    rows_s[8:24, :] = decay_ref[...]

    lane = lax.broadcasted_iota(jnp.int32, (tokens, LANES), 1)
    mixed = pltpu.roll(dot(gdt[...], mix_ref[:, :LANES]), R, 1)
    projected = jnp.where(lane < R, mixed, jnp.where(lane < R + 2 * NS, bc_ref[...], 0.0)).astype(jnp.bfloat16)
    wholes[0].wait()
    wholes[1].wait()
    piece = 2 * LANES
    tail_row = lax.broadcasted_iota(jnp.int32, (tokens, piece), 0)

    def conv_piece(index, unused):
        lanes = pl.ds(pl.multiple_of(index * piece, piece), piece)
        some = pl.ds(pl.multiple_of(index * piece, piece), piece)
        total = along[:, lanes] + contract(projected, mix_ref[some, :LANES], 1, 1)
        value = conv[:, lanes]
        gate = 1.0 / (1.0 + jnp.exp(-value))
        out = total * gate * (1.0 + value * (1.0 - gate))
        rows_s[24:25, lanes] = jnp.sum(out, axis=0, keepdims=True)
        before_rows = ext[:, lanes].astype(jnp.float32)
        rows_s[3:4, lanes] = jnp.sum(out * before_rows[EDGE:], axis=0, keepdims=True)
        result = chan_ref[3:4, lanes] * out
        beyond = jnp.zeros((8, piece), jnp.float32)
        for j in range(1, KC):
            same = jnp.concatenate([same_ref[j - 1]] * 2, axis=1)
            masked = out * same
            shifted_rows = pltpu.roll(before_rows, j, 0)[EDGE:]
            rows_s[3 - j : 4 - j, lanes] = jnp.sum(masked * shifted_rows, axis=0, keepdims=True)
            moved = chan_ref[3 - j : 4 - j, lanes] * pltpu.roll(masked, tokens - j, 0)
            result = result + jnp.where(tail_row < tokens - j, moved, 0.0)
            beyond = beyond + jnp.where(tail_row < tokens - j, 0.0, moved)[tokens - 8 :]
        gci[:, lanes] = result.astype(jnp.bfloat16)
        last[:, lanes] = result[tokens - 16 :]
        spill[:, lanes] = beyond
        return unused

    lax.fori_loop(0, channels // piece, conv_piece, 0)
    handed = pltpu.make_async_remote_copy(
        src_ref=spill,
        dst_ref=arrived,
        send_sem=spill_sems.at[0],
        recv_sem=spill_sems.at[1],
        device_id=before,
        device_id_type=MESH,
    )
    handed.start()

    cut = part_small.shape[-2]
    for index in range(channels // cut):
        spot = tuple(index // 2 ** (heads - 1 - k) % 2 for k in range(heads))
        if cut % LANES == 0:
            some = slice(index * cut, (index + 1) * cut)
            value = contract(xs[:, some], projected, 0, 0) + contract(gdt[:, some], delta_ref[...], 0, 0)
        else:
            pair = slice(index // 2 * 2 * cut, (index // 2 * 2 + 2) * cut)
            value = contract(xs[:, pair], projected, 0, 0) + contract(gdt[:, pair], delta_ref[...], 0, 0)
            value = value[index % 2 * cut : (index % 2 + 1) * cut]
        part_small[spot + (slice(None), slice(0, LANES))] = value.astype(jnp.bfloat16)
    columns = turned(jnp.concatenate([rows_s[...], jnp.zeros((LANES - rows_s.shape[0], channels), jnp.float32)], axis=0))
    for index in range(channels // cut):
        spot = tuple(index // 2 ** (heads - 1 - k) % 2 for k in range(heads))
        part_small[spot + (slice(None), slice(LANES, 2 * LANES))] = columns[index * cut : (index + 1) * cut].astype(jnp.bfloat16)

    handed.wait_recv()
    closing = last[...] + jnp.concatenate([jnp.zeros((8, channels), jnp.float32), arrived[...]], axis=0)
    gci[tokens - 16 :, :] = closing.astype(jnp.bfloat16)

    long = part_conv.shape[-2]

    def product_piece(index, unused):
        lanes = pl.ds(pl.multiple_of(index * piece, piece), piece)
        value = contract(normed_ref[...], gci[:, lanes], 0, 0)
        for block in range(value.shape[0] // long):
            spot = tuple(block // 2 ** (heads - 1 - k) % 2 for k in range(heads))
            part_conv[spot + (slice(None), lanes)] = value[block * long : (block + 1) * long].astype(jnp.bfloat16)
        return unused

    lax.fori_loop(0, channels // piece, product_piece, 0)
    flow.start()

    for copy in wholes[2:]:
        copy.wait()
    width = gn.shape[1]

    def normed_piece(index, unused):
        lanes = pl.ds(pl.multiple_of(index * piece, piece), piece)
        gn[:, lanes] = contract(gci[...], wc[lanes, :], 1, 1) + contract(gz[...], wg[lanes, :], 1, 1)
        return unused

    lax.fori_loop(0, width // piece, normed_piece, 0)
    wide_s[...] = wide_ref[...]
    gain = wide_ref[0:1, :]

    def back(index, total):
        at = pl.ds(pl.multiple_of(index * 16, 16), 16)
        x, g = in_ref[at, :].astype(jnp.float32), gn[at, :]
        scale = lax.rsqrt(jnp.mean(x * x, axis=-1, keepdims=True) + EPS)
        scaled = g * gain
        share_of = jnp.mean(x * scaled, axis=-1, keepdims=True)
        gi_ref[at, :] = resid_ref[at, :] + scale * scaled - x * (scale * scale * scale * share_of)
        value = g * (x * scale)
        return total + value[:8] + value[8:]

    total = lax.fori_loop(0, tokens // 16, back, jnp.zeros((8, width), jnp.float32))
    wide_s[0:1, :] = jnp.sum(total, axis=0, keepdims=True)
    flow.advance(0)
    filler = jnp.zeros((LANES - wide_s.shape[0], width), jnp.float32)
    columns = turned(jnp.concatenate([wide_s[...], filler], axis=0))
    short = part_wide.shape[-2]
    for block in range(width // short):
        spot = tuple(block // 2 ** (heads - 1 - k) % 2 for k in range(heads))
        part_wide[spot] = columns[block * short : (block + 1) * short].astype(jnp.bfloat16)
    flow3.start()
    rest.advance(0)
    for stage in range(1, len(places)):
        flow.advance(stage)
        flow3.advance(stage - 1)
        rest.advance(stage)
    flow3.advance(len(places) - 1)

    flow.finish()
    flow3.finish()
    rest.finish()
    handed.wait_send()
    move.wait()


def finish(sizes, streamed, inside_values, parts, leaving, arrived, identity, span=64):
    places = bit_positions(sizes)
    stages = len(places)
    far = sorted(far_of(places))
    heads = sizes[0][1].bit_length() - 1
    tails = stages - heads
    along, slope, grad, pre, conv, xs, ext, gz, wc, wg = streamed
    normed = inside_values[0]
    tokens, channels = xs.shape
    width = normed.shape[1]
    devices = 2**stages
    half, wide = jnp.bfloat16, jnp.float32
    rows, thin = channels // devices, width // devices
    orders = [tuple(order) for order in orders_of(places)]
    conv_like = jax.ShapeDtypeStruct((width, channels), half)
    small_like = jax.ShapeDtypeStruct((channels, 2 * LANES), half)
    wide_like = jax.ShapeDtypeStruct((width, LANES), half)
    streams = halves((conv_like, small_like), *orders)
    third = halves((wide_like,), *orders)
    late = [(k, slice(0, part.shape[-1]), tuple(far_of(places))) for k, part in enumerate(parts)]

    def room(of, sizes_of):
        landing, blocks = [], []
        for array, cols, order in of:
            size, many = sizes_of[array], cols.stop - cols.start
            landing.append(pltpu.VMEM((2,) * (heads - 1) + (size * 2**tails, many), half))
            landing += [pltpu.VMEM((2,) * (stages - stage - 1) + (size, many), half) for stage in range(1, stages)]
            blocks.append(pltpu.VMEM((2,) * (stages - 1) + (size, many), half))
        return landing, blocks

    landing, blocks = room(streams, (thin, rows))
    landing3, blocks3 = room(third, (thin,))
    late_landing = landing_of(late, far, parts)
    marks = [len(landing), len(blocks), len(landing3), len(blocks3), len(late_landing)]
    inside = pl.BlockSpec(memory_space=pltpu.VMEM)
    anywhere = pl.BlockSpec(memory_space=pl.ANY)
    return pl.pallas_call(
        functools.partial(finish_kernel, places, streams, third, late, far, marks),
        in_specs=[anywhere] * 10 + [inside] * (len(inside_values) + 2) + [anywhere] * 2,
        input_output_aliases={23: 5},
        out_specs=[inside] * 5 + [anywhere],
        out_shape=[
            jax.ShapeDtypeStruct(normed.shape, wide),
            jax.ShapeDtypeStruct((thin, 2 * channels), wide),
            jax.ShapeDtypeStruct(parts[1].shape[-2:], wide),
            jax.ShapeDtypeStruct((rows, 2 * LANES), wide),
            jax.ShapeDtypeStruct((thin, LANES), wide),
            jax.ShapeDtypeStruct(leaving.shape, half),
        ],
        scratch_shapes=landing + blocks + landing3 + blocks3 + late_landing
        + [pltpu.VMEM(value.shape, value.dtype) for value in streamed]
        + [
            pltpu.VMEM((tokens, channels), half),
            pltpu.VMEM((tokens, channels), half),
            pltpu.VMEM((16, channels), wide),
            pltpu.VMEM((8, channels), wide),
            pltpu.VMEM((8, channels), wide),
            pltpu.VMEM((2, 8, channels), wide),
            pltpu.VMEM((32, channels), wide),
            pltpu.VMEM(inside_values[-1].shape, wide),
            pltpu.VMEM((tokens, width), wide),
            pltpu.VMEM((2,) * heads + (thin * 2**tails, channels), half),
            pltpu.VMEM((2,) * heads + (rows * 2**tails, 2 * LANES), half),
            pltpu.VMEM((2,) * heads + (thin * 2**tails, LANES), half),
            pltpu.SemaphoreType.DMA((5, tokens // span)),
            pltpu.SemaphoreType.DMA((5,)),
            pltpu.SemaphoreType.DMA((2,)),
            pltpu.SemaphoreType.DMA((2, 2)),
        ]
        + flights(streams)
        + flights(third)
        + flights(late),
        compiler_params=pltpu.CompilerParams(
            collective_id=identity, has_side_effects=True, vmem_limit_bytes=56 * 1024 * 1024
        ),
        name="finish",
    )(*streamed, *inside_values, *parts, leaving, arrived)


def emit_kernel(gi_from, wo_from, wi_from, wi_other, in_from, out_from, small_ref, thin_ref,
                gi, w_out, w_in, own_in, own_out, own_x, own_dt, own_taps, own_decay, own_router, *singles):
    gi[...] = gi_from[...]
    w_out[...] = wo_from[...]
    w_in[...] = wi_from[...].astype(jnp.float32) + wi_other[...].astype(jnp.float32)
    own_in[...] = in_from[...]
    own_out[...] = out_from[...]

    def columns_of(values):
        return jnp.concatenate([values, jnp.zeros((LANES - values.shape[0], LANES), jnp.float32)], axis=0).T

    size, thin = small_ref.shape[0], thin_ref.shape[0]
    first = small_ref[:, :LANES]
    own_x[...] = first[:, : R + 2 * NS]
    own_dt[...] = columns_of(first)[R + 2 * NS :, :size]
    by_row = columns_of(small_ref[:, LANES:])
    own_taps[...] = by_row[:KC, :size]
    own_decay[...] = by_row[8 : 8 + NS, :size]
    for k in range(3):
        singles[k][...] = by_row[24 + k : 25 + k, :size]
    by_row = columns_of(thin_ref[...])
    for k in range(2):
        singles[3 + k][...] = by_row[k : k + 1, :thin]
    own_router[...] = by_row[8 : 8 + own_router.shape[0], :thin]


def emit_outputs(gi, w_out, w_in, other, own_in, own_out, small, thin_part, experts, pieces=4):
    rows, thin = small.shape[0], thin_part.shape[0]
    full = jnp.float32

    def cut(values):
        return pl.BlockSpec((values.shape[0] // pieces, values.shape[1]), lambda i: (i, 0))

    def whole(shape):
        return pl.BlockSpec(shape, lambda i: (0, 0))

    large = [gi, w_out, w_in, other]
    still = [own_in, own_out, small, thin_part]
    shapes = [own_in.shape, own_out.shape, (rows, R + 2 * NS), (R, rows), (KC, rows), (NS, rows), (experts, thin)]
    shapes += [(1, rows)] * 3 + [(1, thin)] * 2
    return pl.pallas_call(
        emit_kernel,
        grid=(pieces,),
        in_specs=[cut(values) for values in large] + [whole(values.shape) for values in still],
        out_specs=[cut(values) for values in large[:3]] + [whole(shape) for shape in shapes],
        out_shape=[jax.ShapeDtypeStruct(values.shape, full) for values in large[:3]]
        + [jax.ShapeDtypeStruct(shape, full) for shape in shapes],
        name="emit_outputs",
    )(*large, *still)


def expert_kernel(slices, *refs):
    tokens_ref, grads_ref, column_ref = refs[:3]
    even = range(0, slices, 2)
    odd = range(1, slices, 2)
    weights_in, weight_out = refs[3 : 3 + len(even)], refs[3 + len(even)]
    outs = refs[4 + len(even) :]
    picked_ref, back_ref, own_out = outs[:3]
    sums_in = outs[3 : 3 + len(even)]
    (sent, got, answer, returned, w_in, w_out, hidden, total, active, slope, inner, sum_out, pair_out, pair_in, far_out,
     send_sems, recv_sems, weight_sems, sum_sems, spread_sems, mate_sems, far_sems) = outs[3 + len(even) :]
    experts, room, width = sent.shape[1:]
    places = experts * room
    me = lax.axis_index("exp")
    here = lax.axis_index("ctx")
    levels = slices.bit_length() - 1

    loads = [pltpu.make_async_copy(weight_out, w_out.at[0], weight_sems.at[slices])]
    for k, s in enumerate(even):
        loads.append(pltpu.make_async_copy(weights_in[k], w_in.at[s], weight_sems.at[s]))
    for load in loads:
        load.start()

    barrier = pltpu.get_barrier_semaphore()
    mates = [partner(("ctx", level)) for level in range(levels)]
    for step in range(1, experts):
        pl.semaphore_signal(barrier, inc=1, device_id=(here, lax.rem(me + step, experts)), device_id_type=MESH)
    for mate in mates:
        pl.semaphore_signal(barrier, inc=1, device_id=mate, device_id_type=MESH)
    pl.semaphore_wait(barrier, experts - 1 + levels)

    def exchange(source, target, kind):
        copies = []
        for step in range(1, experts):
            peer = lax.rem(me + step, experts)
            copy = pltpu.make_async_remote_copy(
                src_ref=source.at[peer],
                dst_ref=target.at[me],
                send_sem=send_sems.at[kind, step],
                recv_sem=recv_sems.at[kind, step],
                device_id=(here, peer),
                device_id_type=MESH,
            )
            copy.start()
            copies.append(copy)
        target[me] = source[me]
        return copies

    def hand(source, target, sems, level):
        copy = pltpu.make_async_remote_copy(
            src_ref=source,
            dst_ref=target,
            send_sem=sems.at[0],
            recv_sem=sems.at[1],
            device_id=mates[level],
            device_id_type=MESH,
        )
        copy.start()
        return copy

    def arrive(copies):
        for copy in copies:
            copy.wait_recv()

    open_sends = []

    def spread(level):
        step = 2**level
        copies = [hand(w_out.at[s], w_out.at[s + step], spread_sems.at[1, s + step], level) for s in range(0, slices, 2 * step)]
        open_sends.extend(copies)
        return copies

    spots = lax.broadcasted_iota(jnp.int32, (column_ref.shape[0], places), 1).astype(jnp.float32)
    columns = jnp.concatenate([column_ref[...]] * (places // LANES), axis=1)
    finder = (spots == columns).astype(jnp.float32).astype(jnp.bfloat16)
    sent[0] = contract(finder, tokens_ref[...], 0, 0).astype(jnp.bfloat16).reshape(experts, room, width)
    first = exchange(sent.at[0], got.at[0], 0)
    for load in loads:
        load.wait()
    widening = [spread(levels - 1)]
    paired = [hand(w_in.at[s], w_in.at[s + 1], spread_sems.at[0, s], 0) for s in even]
    sent[1] = contract(finder, grads_ref[...], 0, 0).astype(jnp.bfloat16).reshape(experts, room, width)
    second = exchange(sent.at[1], got.at[1], 1)

    arrive(first)
    rows = got[0].reshape(places, width)
    for s in list(even) + list(odd):
        if s == 1:
            arrive(paired)
        hidden[...] = dot(rows, w_in[s])

        def curve(index, unused):
            at = pl.ds(pl.multiple_of(index * ROWS_AT_ONCE, ROWS_AT_ONCE), ROWS_AT_ONCE)
            value = hidden[at, :]
            bell = 0.5 + 0.5 * lax.erf(value * 0.7071067811865476)
            active[s, at, :] = (value * bell).astype(jnp.bfloat16)
            slope[s, at, :] = bell + value * (jnp.exp(-0.5 * value * value) * 0.3989422804014327)
            return unused

        lax.fori_loop(0, places // ROWS_AT_ONCE, curve, 0)

    for level in reversed(range(levels - 1)):
        arrive(widening[-1])
        widening.append(spread(level))
    for s in list(even) + list(odd):
        if s == 1:
            arrive(widening[-1])
        product = dot(active[s], w_out[s])
        total[...] = product if s == 0 else total[...] + product
    answer[0] = total[...].astype(jnp.bfloat16).reshape(experts, room, width)
    third = exchange(answer.at[0], returned.at[0], 2)

    arrive(second)
    pulled = got[1].reshape(places, width)
    joining = []
    for s in list(odd) + list(even):
        sum_out[s] = contract(active[s], pulled, 0, 0).astype(jnp.bfloat16)
        if s % 2:
            joining.append(hand(sum_out.at[s], pair_out.at[s // 2], mate_sems.at[0, s // 2], 0))
    for s in range(slices):
        inner[s] = (contract(pulled, w_out[s], 1, 1) * slope[s]).astype(jnp.bfloat16)
        product = contract(inner[s], w_in[s], 1, 1)
        total[...] = product if s == 0 else total[...] + product
    answer[1] = total[...].astype(jnp.bfloat16).reshape(experts, room, width)
    fourth = exchange(answer.at[1], returned.at[1], 3)

    def add_into(target, addend):
        def some(index, unused):
            at = pl.ds(pl.multiple_of(index * 4 * ROWS_AT_ONCE, 4 * ROWS_AT_ONCE), 4 * ROWS_AT_ONCE)
            target[at, :] = (target[at, :].astype(jnp.float32) + addend[at, :].astype(jnp.float32)).astype(jnp.bfloat16)
            return unused

        lax.fori_loop(0, target.shape[0] // (4 * ROWS_AT_ONCE), some, 0)

    arrive(joining)
    for k, s in enumerate(even):
        add_into(sum_out.at[s], pair_out.at[k])

    def pass_on(level):
        step = 2**level
        return [
            hand(sum_out.at[s + step], far_out.at[slices // step // 2 - 1 + s // (2 * step)], far_sems.at[level, s // (2 * step)], level)
            for s in range(0, slices, 2 * step)
        ]

    passing = pass_on(1)
    open_sends.extend(joining)
    for copy in paired:
        copy.wait_send()
    joined = []
    for s in list(odd) + list(even):
        w_in[s] = contract(rows, inner[s], 0, 0).astype(jnp.bfloat16)
        if s % 2:
            joined.append(hand(w_in.at[s], pair_in.at[s // 2], mate_sems.at[1, s // 2], 0))
    arrive(joined)
    stores = []
    for k, s in enumerate(even):
        add_into(w_in.at[s], pair_in.at[k])
        stores.append(pltpu.make_async_copy(w_in.at[s], sums_in[k], sum_sems.at[k]))
        stores[-1].start()

    arrive(third)
    picked_ref[...] = dot(finder, returned[0].reshape(places, width)).astype(jnp.bfloat16)
    for level in range(1, levels):
        arrive(passing)
        open_sends.extend(passing)
        step = 2**level
        if level + 1 < levels:
            for s in range(0, slices, 2 * step):
                add_into(sum_out.at[s], far_out.at[slices // step // 2 - 1 + s // (2 * step)])
            passing = pass_on(level + 1)
    own_out[...] = sum_out[0].astype(jnp.float32) + far_out[0].astype(jnp.float32)
    arrive(fourth)
    back_ref[...] = dot(finder, returned[1].reshape(places, width)).astype(jnp.bfloat16)
    for store in stores:
        store.wait()
    for copies in (first, second, third, fourth, joined, open_sends):
        for copy in copies:
            copy.wait_send()


def run_experts(rows, grads, target, weights_in, weight_out, experts, room, identity):
    slices = 2 * len(weights_in)
    tokens, width = rows.shape
    inner_width = weight_out.shape[0]
    places = experts * room
    inside = pl.BlockSpec(memory_space=pltpu.VMEM)
    anywhere = pl.BlockSpec(memory_space=pl.ANY)
    half = jnp.bfloat16
    count = len(weights_in)
    out = pl.pallas_call(
        functools.partial(expert_kernel, slices),
        in_specs=[inside] * 3 + [anywhere] * (count + 1),
        out_specs=[inside] * 3 + [anywhere] * count,
        out_shape=[jax.ShapeDtypeStruct(rows.shape, half)] * 2
        + [jax.ShapeDtypeStruct(weight_out.shape, jnp.float32)]
        + [jax.ShapeDtypeStruct(weight.shape, half) for weight in weights_in],
        scratch_shapes=[pltpu.VMEM((2, experts, room, width), half)] * 4
        + [
            pltpu.VMEM((slices, width, inner_width), half),
            pltpu.VMEM((slices, inner_width, width), half),
            pltpu.VMEM((places, inner_width), jnp.float32),
            pltpu.VMEM((places, width), jnp.float32),
            pltpu.VMEM((slices, places, inner_width), half),
            pltpu.VMEM((slices, places, inner_width), jnp.float32),
            pltpu.VMEM((slices, places, inner_width), half),
            pltpu.VMEM((slices, inner_width, width), half),
            pltpu.VMEM((count, inner_width, width), half),
            pltpu.VMEM((count, width, inner_width), half),
            pltpu.VMEM((count, inner_width, width), half),
            pltpu.SemaphoreType.DMA((4, experts)),
            pltpu.SemaphoreType.DMA((4, experts)),
            pltpu.SemaphoreType.DMA((slices + 1,)),
            pltpu.SemaphoreType.DMA((count,)),
            pltpu.SemaphoreType.DMA((2, slices, 2)),
            pltpu.SemaphoreType.DMA((2, count, 2)),
            pltpu.SemaphoreType.DMA((slices, count, 2)),
        ],
        compiler_params=pltpu.CompilerParams(
            collective_id=identity, has_side_effects=True, vmem_limit_bytes=60 * 1024 * 1024
        ),
        name="run_experts",
    )(rows, grads, target, *weights_in, weight_out)
    return out[0], out[1], list(out[3:]), out[2]


def flipped(value, level):
    count = lax.axis_size("ctx")
    return lax.ppermute(value, "ctx", [(source, source ^ (1 << level)) for source in range(count)])


def spread_slices(own, far):
    levels = lax.axis_size("ctx").bit_length() - 1
    slices = {0: own, 1 << (levels - 1): far}
    for level in reversed(range(1, levels - 1)):
        for offset in sorted(slices):
            slices[offset + (1 << level)] = flipped(slices[offset], level)
    return [slices[offset] for offset in sorted(slices)]


def collect_slices(sums):
    levels = lax.axis_size("ctx").bit_length() - 1
    for level in range(1, levels - 1):
        arrived = [flipped(values, level).astype(jnp.float32) for values in sums[1::2]]
        sums = [
            (values.astype(jnp.float32) + other).astype(jnp.bfloat16) for values, other in zip(sums[::2], arrived)
        ]
    return sums


def body(
    inputs,
    segments,
    routes,
    cotangent,
    norm_gain,
    in_proj,
    conv_taps,
    conv_bias,
    x_proj,
    dt_proj,
    dt_bias,
    log_decay,
    skip_gain,
    out_proj,
    moe_gain,
    router,
    expert_in,
    expert_out,
):
    experts = router.shape[1]
    half_rows = norm_gain.shape[0]
    small = (
        x_proj,
        dt_proj,
        conv_taps.T,
        log_decay.T,
        jnp.stack([conv_bias, dt_bias, skip_gain]),
        jnp.stack([norm_gain, moe_gain]),
        router.T,
    )
    sizes = [(name, lax.axis_size(name)) for name in ("ctx", "exp")]
    weights, partial, begun, *prior = gather_all(
        sizes, small, in_proj, out_proj, inputs[0], segments, expert_in[0], 0
    )
    tokens_here = inputs.shape[1]
    capacity = 5 * tokens_here // (4 * experts)
    room = -(-capacity // 16) * 16
    flat_in = inputs[0].astype(jnp.float32)
    (
        scan_rows,
        products,
        normed_one,
        b_turned,
        c_turned,
        rates,
        by_channel,
        gain_rows,
        delta_low,
        same_rows,
        target,
        kept,
        (conv_ext, conv_out, xs_val, dt_pre, masked_step, push),
        (full_gate, full_out),
        far_in,
    ) = scan_forward(
        sizes,
        inputs[0],
        prior,
        (segments, routes.reshape(1, tokens_here)),
        weights,
        room,
        partial,
        expert_in[0],
        begun,
        3,
    )
    weights_in = spread_slices(expert_in[0], far_in)
    full_conv, full_channel, full_width = weights
    full_skip, full_moe, full_router = by_channel[26], gain_rows[1], full_width[:, 8 : 8 + experts]
    xs_wide = xs_val.astype(jnp.float32)
    gate_z = dot(normed_one, full_gate)
    skip_wide = full_skip
    scanned_y = scan_rows + skip_wide * xs_wide
    gated_wide, gated_pull = jax.vjp(
        lambda scan_in, gate_in: scan_in * jax.nn.silu(gate_in), scanned_y, gate_z
    )
    gated = gated_wide.astype(jnp.bfloat16)
    mixed = jnp.dot(gated, full_out, preferred_element_type=jnp.float32)
    residual = flat_in + mixed
    norm_two_value, norm_two_pull = jax.vjp(rms_scale, residual, full_moe.astype(jnp.float32))
    normed_two = norm_two_value.astype(jnp.bfloat16)
    logits = jnp.dot(normed_two, full_router, preferred_element_type=jnp.float32)
    probability = jax.nn.softmax(logits, axis=-1)
    route_ids = routes[0, :, 0]
    one_hot = route_ids[:, None] == jnp.arange(experts, dtype=jnp.int32)[None, :]
    one_float = one_hot.astype(jnp.float32)
    gate_val = jnp.sum(probability * one_float, axis=1)
    grad_out = cotangent[0].astype(jnp.float32)
    grad_pick = (grad_out * gate_val[:, None]).astype(jnp.bfloat16)
    picked, grad_from_experts, grad_expert_in, grad_w_out = run_experts(
        normed_two, grad_pick, target, weights_in, expert_out[0], experts, room, 2
    )
    kept_in, leaving = collect_slices(grad_expert_in)
    picked = picked.astype(jnp.float32)
    grad_from_experts = grad_from_experts.astype(jnp.float32)
    outcome = residual + gate_val[:, None] * picked
    out_block = outcome.astype(jnp.bfloat16)[None]
    grad_gate = jnp.sum(grad_out * picked, axis=1)
    grad_probs = grad_gate[:, None] * one_float
    grad_logits = (
        probability * (grad_probs - jnp.sum(grad_probs * probability, axis=1, keepdims=True))
    ).astype(jnp.bfloat16)
    grad_router = contract(grad_logits, normed_two, 0, 0)
    grad_normed_two = grad_from_experts + jnp.dot(
        grad_logits, full_router.T, preferred_element_type=jnp.float32
    )
    grad_resid_norm, grad_moe_gain = norm_two_pull(grad_normed_two)
    grad_resid = grad_out + grad_resid_norm
    grad_mixed = grad_resid.astype(jnp.bfloat16)
    grad_gated = jnp.dot(grad_mixed, full_out.T, preferred_element_type=jnp.float32)
    grad_out_proj = jnp.dot(gated.T, grad_mixed, preferred_element_type=jnp.float32)
    grad_y, grad_z = gated_pull(grad_gated)
    grad_z = grad_z.astype(jnp.bfloat16)
    along_b, slope, grad_bs, grad_cs, grad_a, partial_sums, arrived = scan_backward(
        sizes,
        masked_step,
        push,
        grad_y,
        b_turned,
        c_turned,
        rates,
        products,
        (dot(normed_one.T, grad_z).astype(jnp.bfloat16), grad_out_proj.astype(jnp.bfloat16)),
        kept,
        leaving,
        4,
    )
    wide_rows = jnp.concatenate(
        [gain_rows[:1], grad_moe_gain[None], jnp.zeros((6, D), jnp.float32), grad_router]
    )
    finished = finish(
        sizes,
        (along_b, slope, grad_y, dt_pre, conv_out, xs_val, conv_ext, grad_z, full_conv, full_gate),
        (
            normed_one,
            inputs[0],
            grad_resid,
            full_channel,
            jnp.pad(jnp.concatenate([grad_bs, grad_cs], axis=1), ((0, 0), (R, LANES - R - 2 * NS))),
            delta_low,
            same_rows,
            jnp.concatenate([by_channel[:KC], by_channel[26:27], jnp.zeros((3, DI), jnp.float32)]),
            grad_a * rates * (1.0 / LOG2E),
            wide_rows,
        ),
        partial_sums,
        leaving,
        arrived,
        1,
    )
    grad_inputs, own_in, own_out, own_small, own_thin, arrived = finished
    grad_inputs, grad_w_out, grad_w_in, own_in, own_out, own_x, own_dt, own_taps, own_decay, own_router, *vectors = (
        emit_outputs(grad_inputs, grad_w_out, kept_in, arrived, own_in, own_out, own_small, own_thin, experts)
    )
    own_bias, own_dtbias, own_skip, own_norm, own_moe = [values[0] for values in vectors]
    return (
        out_block,
        grad_inputs[None],
        own_norm,
        own_in,
        own_taps.T,
        own_bias,
        own_x,
        own_dt,
        own_dtbias,
        own_decay.T,
        own_skip,
        own_out,
        own_moe,
        own_router.T,
        grad_w_in[None],
        grad_w_out[None],
    )


def solution(mesh):
    placed = (
        P("exp", "ctx", None),
        P("exp", "ctx"),
        P("exp", "ctx", None),
        P("exp", "ctx", None),
        P(("ctx", "exp")),
        P(("ctx", "exp"), None),
        P(("ctx", "exp"), None),
        P(("ctx", "exp")),
        P(("ctx", "exp"), None),
        P(None, ("ctx", "exp")),
        P(("ctx", "exp")),
        P(("ctx", "exp"), None),
        P(("ctx", "exp")),
        P(("ctx", "exp"), None),
        P(("ctx", "exp")),
        P(("ctx", "exp"), None),
        P("exp", None, "ctx"),
        P("exp", "ctx", None),
    )
    return jax.shard_map(
        body,
        mesh=mesh,
        in_specs=placed,
        out_specs=(
            P("exp", "ctx", None),
            P("exp", "ctx", None),
            P(("ctx", "exp")),
            P(("ctx", "exp"), None),
            P(("ctx", "exp"), None),
            P(("ctx", "exp")),
            P(("ctx", "exp"), None),
            P(None, ("ctx", "exp")),
            P(("ctx", "exp")),
            P(("ctx", "exp"), None),
            P(("ctx", "exp")),
            P(("ctx", "exp"), None),
            P(("ctx", "exp")),
            P(("ctx", "exp"), None),
            P("exp", None, "ctx"),
            P("exp", "ctx", None),
        ),
        check_vma=False,
    )
```

```python
import functools

import jax
import jax.numpy as jnp
from jax import lax
from jax.experimental import pallas as pl
from jax.experimental.pallas import tpu as pltpu
from jax.sharding import PartitionSpec as P

D = 768
DI = 1536
NS = 16
R = 48
KC = 4
LANES = 128
UNROLL = 8
LOG2E = 1.4426950408889634


EPS = 1e-05
MESH = pl.DeviceIdType.MESH
ROWS_AT_ONCE = 16
EDGE = 16

def tile(ref, base, lanes):
    return ref[pl.ds(pl.multiple_of(base, UNROLL), UNROLL), lanes]

def row(rows_now, place):
    return jnp.broadcast_to(rows_now[place : place + 1], (NS, LANES))

def cost(tokens, channels, share):
    size = tokens * channels * NS
    return pl.CostEstimate(flops=size * share, transcendentals=size, bytes_accessed=size * share)


def pick(channels):
    return 512 if channels % 512 == 0 else 128


def rms_scale(values, gain):
    return values * lax.rsqrt(jnp.mean(values * values, axis=-1, keepdims=True) + EPS) * gain


def bit_positions(sizes):
    return [(axis, size.bit_length() - 2 - k) for axis, size in sizes for k in range(size.bit_length() - 1)]


def own_bit(place):
    axis, level = place
    return lax.rem(lax.axis_index(axis) // 2**level, 2)


def partner(place):
    axis, level = place
    where = {"ctx": lax.axis_index("ctx"), "exp": lax.axis_index("exp")}
    where[axis] = where[axis] + (1 - 2 * own_bit(place)) * 2**level
    return (where["ctx"], where["exp"])


def meet(places, *others):
    barrier = pltpu.get_barrier_semaphore()
    for device in [partner(place) for place in places] + list(others):
        pl.semaphore_signal(barrier, inc=1, device_id=device, device_id_type=MESH)
    pl.semaphore_wait(barrier, len(places) + len(others))


class GatherFlow:
    def __init__(self, places, streams, dims, shards, wholes, send_sems, recv_sems, local_sems):
        self.places, self.streams, self.dims, self.shards, self.wholes = places, streams, dims, shards, wholes
        self.sems = send_sems, recv_sems, local_sems
        self.bits = [own_bit(place) for place in places]

    def view(self, number, have):
        array, cols, order, begin = self.streams[number]
        index = tuple(slice(None) if p in have else self.bits[p] for p in self.dims)
        return self.wholes[array].at[index + (slice(None), cols)]

    def shard(self, number):
        array, cols, order, begin = self.streams[number]
        return self.shards[array].at[(slice(None),) * (begin + 1) + (cols,)]

    def own(self, number):
        array, cols, order, begin = self.streams[number]
        return pltpu.make_async_copy(self.shard(number), self.view(number, order[:begin]), self.sems[2].at[number])

    def flight(self, number, stage):
        array, cols, order, begin = self.streams[number]
        target = self.view(number, order[: begin + stage])
        return pltpu.make_async_remote_copy(
            src_ref=self.shard(number) if stage == 0 else target,
            dst_ref=target,
            send_sem=self.sems[0].at[number, stage],
            recv_sem=self.sems[1].at[number, stage],
            device_id=partner(self.places[order[begin + stage]]),
            device_id_type=MESH,
        )

    def stages(self, number):
        array, cols, order, begin = self.streams[number]
        return len(order) - begin

    def start(self):
        for number in range(len(self.streams)):
            self.flight(number, 0).start()
        for number in range(len(self.streams)):
            self.own(number).start()

    def advance(self, stage):
        for number in range(len(self.streams)):
            if stage >= self.stages(number):
                continue
            if stage == 0:
                self.own(number).wait()
            self.flight(number, stage).wait_recv()
            if stage + 1 < self.stages(number):
                self.flight(number, stage + 1).start()

    def finish(self):
        for number in range(len(self.streams)):
            for stage in range(self.stages(number)):
                self.flight(number, stage).wait_send()


def pack_small(small, square, channel_pack, width_pack):
    x_ref, dt_ref, taps_ref, decay_ref, vector_ref, pair_ref, router_ref = small
    rows, thin = channel_pack.shape[0], width_pack.shape[0]

    def laid(*pieces):
        square[...] = jnp.zeros_like(square)
        for first, ref in pieces:
            square[first : first + ref.shape[0], : ref.shape[1]] = ref[...].astype(jnp.float32)
        return square[...]

    dt_part = pltpu.roll(laid((0, dt_ref)).T, R + 2 * NS, 1)
    mix = laid((0, x_ref)) + dt_part
    channel_pack[:, :LANES] = mix[:rows].astype(jnp.bfloat16)
    turned_rows = laid((0, taps_ref), (8, decay_ref), (24, vector_ref)).T
    channel_pack[:, LANES:] = turned_rows[:rows].astype(jnp.bfloat16)
    width_pack[...] = laid((0, pair_ref), (8, router_ref)).T[:thin].astype(jnp.bfloat16)


def gather_kernel(places, streams, extra_streams, far, *refs):
    small = refs[:7]
    in_ref, out_ref, rows_ref, ids_ref, leaving = refs[7:12]
    extra = 2
    wholes, prior_ref, prior_ids, arriving = refs[12:17], refs[17], refs[18], refs[19]
    (square, channel_pack, width_pack, send_sems, recv_sems, local_sems, late_send, late_recv, late_local,
     edge_sems, moved_sems) = refs[20:]
    split = in_ref.shape[1] // 2
    shards = (in_ref.at[:, :split], channel_pack, width_pack, in_ref.at[:, split:], out_ref)
    pack_small(small, square, channel_pack, width_pack)
    count = 3
    flow = GatherFlow(
        places, streams, range(len(places)), shards[:count], wholes[:count], send_sems, recv_sems, local_sems
    )
    late = GatherFlow(
        places, extra_streams, far, shards[count:], wholes[count:], late_send, late_recv, late_local
    )
    blocks = lax.axis_size("ctx")
    here, line = lax.axis_index("ctx"), lax.axis_index("exp")
    meet(places, (lax.rem(here + 1, blocks), line), (lax.rem(here + blocks - 1, blocks), line))
    flow.start()
    tokens = rows_ref.shape[0]
    edges = [
        pltpu.make_async_remote_copy(
            src_ref=source,
            dst_ref=target,
            send_sem=edge_sems.at[0, k],
            recv_sem=edge_sems.at[1, k],
            device_id=(lax.rem(here + 1, blocks), line),
            device_id_type=MESH,
        )
        for k, (source, target) in enumerate(
            (
                (rows_ref.at[pl.ds(tokens - EDGE, EDGE)], prior_ref),
                (ids_ref.at[:, pl.ds(tokens - LANES, LANES)], prior_ids),
            )
        )
    ]
    for edge in edges:
        edge.start()
    move = row_half(leaving, arriving, moved_sems, ("ctx", blocks.bit_length() - 2), 0)
    move.start()
    stages, behind = len(places), len(far)
    for stage in range(stages):
        flow.advance(stage)
        if stage == behind - 2:
            late.start()
        if stage >= behind and stage - behind < behind:
            late.advance(stage - behind)
    for stage in range(stages - behind, behind):
        late.advance(stage)
    flow.finish()
    late.finish()
    for edge in edges:
        edge.wait()
    move.wait()


def orders_of(places):
    core = places.index(("ctx", 0))
    rows = [k for k, place in enumerate(places) if place[0] == "ctx" and place[1] > 0]
    near = places.index(("exp", 0))
    return [core] + rows + [near] + far_of(places), [core, near] + rows + far_of(places)


def far_of(places):
    return [k for k, place in sorted(enumerate(places), key=lambda item: item[1][1]) if place[0] == "exp" and place[1] > 0]


def halves(arrays, first, second, begin=None):
    streams = []
    for array, values in enumerate(arrays):
        width = values.shape[-1]
        rest = () if begin is None else (begin,)
        if width % (2 * LANES) == 0:
            count = 4 if width % (4 * LANES) == 0 and width >= 1024 else 2
            for k in range(count):
                part = (k % 2) * (count // 2) + k // 2
                cols = slice(part * width // count, (part + 1) * width // count)
                streams.append((array, cols, second if k % 2 else first) + rest)
        else:
            streams.append((array, slice(0, width), first if array % 2 else second) + rest)
    return streams


def gather_orders(places):
    return [tuple(reversed(order)) for order in orders_of(places)]


def gather_all(sizes, small, in_proj, out_proj, rows_in, ids, leaving, identity):
    places = bit_positions(sizes)
    stages = len(places)
    far = sorted(far_of(places))
    half = jnp.bfloat16
    rows, thin, split = small[0].shape[0], in_proj.shape[0], in_proj.shape[1] // 2
    shape = jax.ShapeDtypeStruct
    shards = shape((thin, split), half), shape((rows, 2 * LANES), half), shape((thin, LANES), half)
    extra = shape((thin, split), half), shape(out_proj.shape, half)
    streams = halves(shards, *gather_orders(places), begin=0)
    late = [(k, slice(0, part.shape[1]), tuple(reversed(far_of(places))), 0) for k, part in enumerate(extra)]
    anywhere = pl.BlockSpec(memory_space=pl.ANY)
    inside = pl.BlockSpec(memory_space=pltpu.VMEM)
    out = pl.pallas_call(
        functools.partial(gather_kernel, places, streams, late, far),
        in_specs=[inside] * 7 + [anywhere] * 5,
        out_specs=[anywhere] * 8,
        out_shape=[shape((2,) * stages + shard.shape, half) for shard in shards]
        + [shape((2,) * len(far) + part.shape, half) for part in extra]
        + [shape((EDGE, rows_in.shape[1]), half), shape((1, LANES), jnp.int32), shape(leaving.shape, half)],
        scratch_shapes=[
            pltpu.VMEM((LANES, LANES), jnp.float32),
            pltpu.VMEM((rows, 2 * LANES), half),
            pltpu.VMEM((thin, LANES), half),
            pltpu.SemaphoreType.DMA((len(streams), stages)),
            pltpu.SemaphoreType.DMA((len(streams), stages)),
            pltpu.SemaphoreType.DMA((len(streams),)),
            pltpu.SemaphoreType.DMA((len(late), len(far))),
            pltpu.SemaphoreType.DMA((len(late), len(far))),
            pltpu.SemaphoreType.DMA((len(late),)),
            pltpu.SemaphoreType.DMA((2, 2)),
            pltpu.SemaphoreType.DMA((2, 2)),
        ],
        compiler_params=pltpu.CompilerParams(collective_id=identity, has_side_effects=True),
        name="gather_all",
    )(*small, in_proj, out_proj, rows_in, ids, leaving)
    return [whole.reshape((-1,) + whole.shape[stages + 1 :]) for whole in out[:3]], out[3:5], out[7], out[5], out[6]


class ReduceFlow:
    def __init__(self, places, streams, dims, parts, totals, landing, send_sems, recv_sems):
        self.places, self.streams, self.dims, self.parts, self.totals = places, streams, dims, parts, totals
        self.landing, self.sems = landing, (send_sems, recv_sems)
        self.bits = [own_bit(place) for place in places]
        self.first = []
        for array, cols, order in streams:
            self.first.append(sum(len(other[2]) for other in streams[: len(self.first)]))

    def spot(self, number, stage):
        return self.landing[self.first[number] + stage]

    def side(self, number, stage, value):
        array, cols, order = self.streams[number]
        left = [p for p in self.dims if p not in order[:stage]]
        index = tuple(value if p == order[stage] else slice(None) for p in left)
        if stage == 0:
            return self.parts[array].at[index + (slice(None), cols)]
        return self.spot(number, stage - 1).at[index]

    def flight(self, number, stage):
        order = self.streams[number][2]
        return pltpu.make_async_remote_copy(
            src_ref=self.side(number, stage, 1 - self.bits[order[stage]]),
            dst_ref=self.spot(number, stage),
            send_sem=self.sems[0].at[number, stage],
            recv_sem=self.sems[1].at[number, stage],
            device_id=partner(self.places[order[stage]]),
            device_id_type=MESH,
        )

    def start(self):
        for number in range(len(self.streams)):
            self.flight(number, 0).start()

    def advance(self, stage):
        for number, (array, cols, order) in enumerate(self.streams):
            if stage >= len(order):
                continue
            self.flight(number, stage).wait_recv()
            mine = self.side(number, stage, self.bits[order[stage]])
            there = self.spot(number, stage)
            depth = len(self.dims) - stage - 1
            final = stage + 1 == len(order)
            if depth == 0:
                self.totals[array][:, cols] = there[...].astype(jnp.float32) + mine[...].astype(jnp.float32)
                continue

            def add(index, unused, there=there, mine=mine, depth=depth, final=final, array=array, cols=cols):
                at = tuple(lax.rem(index // 2 ** (depth - 1 - k), 2) for k in range(depth))
                value = there[at] + mine[at]
                if final:
                    self.totals[array][at + (slice(None), cols)] = value
                else:
                    there[at] = value
                return unused

            lax.fori_loop(0, 2**depth, add, 0)
            if not final:
                self.flight(number, stage + 1).start()

    def finish(self):
        for number in range(len(self.streams)):
            for stage in range(len(self.streams[number][2])):
                self.flight(number, stage).wait_send()


def landing_of(streams, dims, divided):
    landing = []
    for array, cols, order in streams:
        for stage in range(len(order)):
            rows = divided[array].shape[-2]
            landing.append(pltpu.VMEM((2,) * (len(dims) - stage - 1) + (rows, cols.stop - cols.start), jnp.bfloat16))
    return landing


def flights(streams):
    shape = (len(streams), max(len(order) for array, cols, order in streams))
    return [pltpu.SemaphoreType.DMA(shape)] * 2


def dot(left, right):
    return jnp.dot(left, right, preferred_element_type=jnp.float32)


def contract(left, right, left_dim, right_dim):
    return lax.dot_general(left, right, (((left_dim,), (right_dim,)), ((), ())), preferred_element_type=jnp.float32)


def lanes_of(group, width, k):
    return pl.ds(pl.multiple_of(group * width + k * LANES, LANES), LANES)


def spread_columns(source_ref, wide_ref):
    def chunk(index, unused):
        base = pl.multiple_of(index * LANES, LANES)
        now = source_ref[:, pl.ds(base, LANES)]
        for place in range(LANES):
            wide_ref[base + place] = jnp.broadcast_to(now[:, place : place + 1], (NS, LANES))
        return unused

    lax.fori_loop(0, source_ref.shape[1] // LANES, chunk, 0)


def end_pass(width, step_ref, push_ref, wide_b, rate_ref, state_ref, hook):
    rows, channels = step_ref.shape
    count = width // LANES

    def group_body(group, unused):
        pieces = [lanes_of(group, width, k) for k in range(count)]
        rates = [rate_ref[:, lanes] for lanes in pieces]

        def block(index, states):
            states = list(states)
            steps = [tile(step_ref, index * UNROLL, lanes) for lanes in pieces]
            pushes = [tile(push_ref, index * UNROLL, lanes) for lanes in pieces]
            for place in range(UNROLL):
                b_now = wide_b[index * UNROLL + place]
                for k in range(count):
                    decay = jnp.exp2(row(steps[k], place) * rates[k])
                    states[k] = decay * states[k] + b_now * row(pushes[k], place)
            return tuple(states)

        zero = jnp.zeros((NS, LANES), jnp.float32)
        states = lax.fori_loop(0, rows // UNROLL, block, (zero,) * count)
        for k, lanes in enumerate(pieces):
            state_ref[:, lanes] = states[k]
        hook(group)
        return unused

    lax.fori_loop(0, channels // width, group_body, 0)


def out_pass(width, step_ref, push_ref, wide_b, wide_c, rate_ref, state_ref, y_ref, kept_buf, kept_copy, hook):
    rows, channels = step_ref.shape
    count = width // LANES
    span = kept_buf.shape[1]
    blocks = rows // span

    def time_body(number, unused):
        slot = lax.rem(number, 2)

        @pl.when(number >= 2)
        def _():
            kept_copy(number - 2, slot).wait()

        def group_body(group, unused_inner):
            pieces = [lanes_of(group, width, k) for k in range(count)]
            rates = [rate_ref[:, lanes] for lanes in pieces]

            def block(index, states):
                states = list(states)
                base = number * span + index * UNROLL
                steps = [tile(step_ref, base, lanes) for lanes in pieces]
                pushes = [tile(push_ref, base, lanes) for lanes in pieces]
                trees = [Tree(True) for k in range(count)]
                for place in range(UNROLL):
                    b_now = wide_b[base + place]
                    c_now = wide_c[base + place]
                    for k, lanes in enumerate(pieces):
                        decay = jnp.exp2(row(steps[k], place) * rates[k])
                        states[k] = decay * states[k] + b_now * row(pushes[k], place)
                        kept_buf[slot, index * UNROLL + place, :, lanes] = states[k].astype(kept_buf.dtype)
                        trees[k].push(place, states[k] * c_now)
                for k, lanes in enumerate(pieces):
                    y_ref[pl.ds(pl.multiple_of(base, UNROLL), UNROLL), lanes] = trees[k].result
                return tuple(states)

            states = lax.fori_loop(0, span // UNROLL, block, tuple(state_ref[:, lanes] for lanes in pieces))
            for k, lanes in enumerate(pieces):
                state_ref[:, lanes] = states[k]
            return unused_inner

        lax.fori_loop(0, channels // width, group_body, 0)
        kept_copy(number, slot).start()
        hook(number)
        return unused

    lax.fori_loop(0, blocks, time_body, 0)
    for number in range(max(0, blocks - 2), blocks):
        kept_copy(number, number % 2).wait()


def inflow_pass(width, step_ref, grad_ref, wide_c, rate_ref, flow_ref, hook):
    rows, channels = step_ref.shape
    count = width // LANES

    def group_body(group, unused):
        hook(group)
        pieces = [lanes_of(group, width, k) for k in range(count)]
        rates = [rate_ref[:, lanes] for lanes in pieces]

        def block(index, flows):
            flows = list(flows)
            base = rows - UNROLL - index * UNROLL
            steps = [tile(step_ref, base, lanes) for lanes in pieces]
            grads = [tile(grad_ref, base, lanes) for lanes in pieces]
            for place in reversed(range(UNROLL)):
                c_now = wide_c[base + place]
                for k in range(count):
                    decay = jnp.exp2(row(steps[k], place) * rates[k])
                    flows[k] = decay * (c_now * row(grads[k], place) + flows[k])
            return tuple(flows)

        zero = jnp.zeros((NS, LANES), jnp.float32)
        flows = lax.fori_loop(0, rows // UNROLL, block, (zero,) * count)
        for k, lanes in enumerate(pieces):
            flow_ref[:, lanes] = flows[k]
        return unused

    lax.fori_loop(0, channels // width, group_body, 0)


class Tree:
    def __init__(self, rising):
        self.rising, self.held, self.result = rising, {}, None

    def push(self, place, value):
        now = value[:UNROLL] + value[UNROLL:]
        level = 0
        while 1 << level < UNROLL:
            if (place >> level) % 2 == (0 if self.rising else 1):
                self.held[level] = now
                return
            first, second = (self.held[level], now) if self.rising else (now, self.held[level])
            now = self.merge(first, second, 1 << level)
            level += 1
        self.result = now

    def merge(self, first, second, distance):
        low = (lax.broadcasted_iota(jnp.int32, (UNROLL, LANES), 0) & distance) == 0
        keep = jnp.where(low, first, second)
        give = jnp.where(low, second, first)
        other = pltpu.roll(give, distance, 0)
        if 2 * distance != UNROLL:
            other = jnp.where(low, pltpu.roll(give, UNROLL - distance, 0), other)
        return keep + other


def lane_sums(part_ref):
    values = part_ref[...].reshape(-1, LANES).astype(jnp.bfloat16)
    return contract(jnp.ones((UNROLL, LANES), jnp.bfloat16), values, 1, 1)


def adjoint_pass(width, step_ref, push_ref, grad_ref, wide_b, wide_c, rate_ref, flow_ref, kept_buf, kept_copy,
                 along_ref, slope_ref, gb_ref, gc_ref, ga_ref, part_b, part_c, hook):
    rows, channels = step_ref.shape
    count = width // LANES
    span = kept_buf.shape[1] - 1
    blocks = rows // span
    ga_ref[...] = jnp.zeros_like(ga_ref)

    def time_body(order, unused):
        slot = lax.rem(order, 2)
        number = blocks - 1 - order
        kept_copy(number, slot).wait()
        part_b[...] = jnp.zeros_like(part_b)
        part_c[...] = jnp.zeros_like(part_c)

        def group_body(group, unused_inner):
            pieces = [lanes_of(group, width, k) for k in range(count)]
            rates = [rate_ref[:, lanes] for lanes in pieces]

            def block(index, carried):
                flows = list(carried[:count])
                sums = list(carried[count : 2 * count])
                current = list(carried[2 * count :])
                local = span - UNROLL - index * UNROLL
                base = number * span + local
                steps = [tile(step_ref, base, lanes) for lanes in pieces]
                pushes = [tile(push_ref, base, lanes) for lanes in pieces]
                grads = [tile(grad_ref, base, lanes) for lanes in pieces]
                alongs = [Tree(False) for k in range(count)]
                slopes = [Tree(False) for k in range(count)]
                for place in reversed(range(UNROLL)):
                    b_now = wide_b[base + place]
                    c_now = wide_c[base + place]
                    gb = gc = None
                    for k, lanes in enumerate(pieces):
                        prior = kept_buf[slot, local + place, :, lanes].astype(jnp.float32)
                        step = row(steps[k], place)
                        grad = row(grads[k], place)
                        decay = jnp.exp2(step * rates[k])
                        adjoint = c_now * grad + flows[k]
                        flows[k] = decay * adjoint
                        decay_grad = flows[k] * prior
                        alongs[k].push(place, adjoint * b_now)
                        slopes[k].push(place, decay_grad * rates[k])
                        sums[k] = sums[k] + decay_grad * step
                        here_b = adjoint * row(pushes[k], place)
                        here_c = current[k] * grad
                        gb = here_b if gb is None else gb + here_b
                        gc = here_c if gc is None else gc + here_c
                        current[k] = prior
                    part_b[local + place] += gb
                    part_c[local + place] += gc
                where = pl.ds(pl.multiple_of(base, UNROLL), UNROLL)
                for k, lanes in enumerate(pieces):
                    along_ref[where, lanes] = alongs[k].result
                    slope_ref[where, lanes] = slopes[k].result
                return tuple(flows + sums + current)

            carried = lax.fori_loop(
                0,
                span // UNROLL,
                block,
                tuple(flow_ref[:, lanes] for lanes in pieces)
                + tuple(ga_ref[:, lanes] for lanes in pieces)
                + tuple(kept_buf[slot, span, :, lanes].astype(jnp.float32) for lanes in pieces),
            )
            for k, lanes in enumerate(pieces):
                flow_ref[:, lanes] = carried[k]
                ga_ref[:, lanes] = carried[count + k]
            return unused_inner

        lax.fori_loop(0, channels // width, group_body, 0)
        gb_ref[number] = lane_sums(part_b)
        gc_ref[number] = lane_sums(part_c)

        @pl.when(order + 2 < blocks)
        def _():
            kept_copy(number - 2, slot).start()

        hook(order)
        return unused

    lax.fori_loop(0, blocks, time_body, 0)


def share(source, target, send_sems, recv_sems):
    blocks = lax.axis_size("ctx")
    here, line = lax.axis_index("ctx"), lax.axis_index("exp")
    copies = []
    for step in range(1, blocks):
        copies.append(
            pltpu.make_async_remote_copy(
                src_ref=source,
                dst_ref=target.at[here],
                send_sem=send_sems.at[step],
                recv_sem=recv_sems.at[step],
                device_id=(lax.rem(here + step, blocks), line),
                device_id_type=MESH,
            )
        )
        copies[-1].start()
    target[here] = source[...]
    return copies


def row_peers():
    blocks = lax.axis_size("ctx")
    here, line = lax.axis_index("ctx"), lax.axis_index("exp")
    return [(lax.rem(here + step, blocks), line) for step in range(1, blocks)]


def row_half(source, target, sems, place, k):
    size = source.shape[0] // 2
    return pltpu.make_async_remote_copy(
        src_ref=source.at[pl.ds(k * size, size)],
        dst_ref=target.at[pl.ds(k * size, size)],
        send_sem=sems.at[0, k],
        recv_sem=sems.at[1, k],
        device_id=partner(place),
        device_id_type=MESH,
    )


def front(loaded, loads, room, outs, scratch, saves):
    normed_ref, bt_ref, ct_ref, rate_ref, chan_ref, gain_ref, delta_ref, same_ref, target_ref = outs
    nx, ext, conv, xs, pre, step, push = scratch
    in_ref, prior_ref, prior_ids, ids_ref, routes_ref, conv_w, channel_ref, width_ref = loaded
    for load in loads[:5] + loads[6:]:
        load.wait()
    tokens, channels = xs.shape
    width = in_ref.shape[1]
    mine = lax.axis_index("ctx")
    gain_rows = jnp.concatenate(
        [width_ref[at : at + LANES, :].astype(jnp.float32).T for at in range(0, width, LANES)], axis=1
    )
    gain_ref[...] = gain_rows[:8]
    for at in range(0, channels, LANES):
        chan_ref[:, at : at + LANES] = channel_ref[at : at + LANES, LANES:].astype(jnp.float32).T[:32]
    rate_ref[...] = -jnp.exp(chan_ref[8 : 8 + NS, :]) * LOG2E
    gain = gain_ref[0:1, :]

    def normed(values):
        x = values.astype(jnp.float32)
        return (x * lax.rsqrt(jnp.mean(x * x, axis=-1, keepdims=True) + EPS) * gain).astype(jnp.bfloat16)

    nx[:EDGE, :] = normed(prior_ref[...])

    def norm_rows(index, unused):
        at = pl.ds(pl.multiple_of(index * 16, 16), 16)
        value = normed(in_ref[at, :])
        normed_ref[at, :] = value
        nx[pl.ds(pl.multiple_of(EDGE + index * 16, 16), 16), :] = value
        return unused

    lax.fori_loop(0, tokens // 16, norm_rows, 0)
    def column(values):
        return jnp.broadcast_to(values.astype(jnp.float32), (LANES, LANES)).T

    def columns(ref):
        return jnp.concatenate([column(ref[:, at : at + LANES]) for at in range(0, tokens, LANES)], axis=0)

    ids = jnp.where(mine > 0, column(prior_ids[...])[LANES - EDGE :], -1.0)
    own_ids = columns(ids_ref)
    every_id = jnp.concatenate([ids, own_ids], axis=0)
    for j in range(1, KC):
        same_ref[j - 1] = (pltpu.roll(every_id, j, 0)[EDGE:] == own_ids).astype(jnp.float32)
    routes = columns(routes_ref)
    chosen = (routes == lax.broadcasted_iota(jnp.int32, routes.shape, 1).astype(jnp.float32)).astype(jnp.float32)
    square = (tokens, tokens)
    until = lax.broadcasted_iota(jnp.int32, square, 0) >= lax.broadcasted_iota(jnp.int32, square, 1)
    running = dot(until.astype(jnp.float32).astype(jnp.bfloat16), chosen.astype(jnp.bfloat16))
    slot = jnp.sum(running * chosen, axis=1, keepdims=True) - 1.0
    target_ref[...] = routes * room + slot
    piece = 2 * LANES
    loads[5].wait()

    def conv_piece(index, unused):
        lanes = pl.ds(pl.multiple_of(index * piece, piece), piece)
        low = dot(nx[...], conv_w[:, lanes]).astype(jnp.bfloat16)
        ext[:, lanes] = low
        value = low.astype(jnp.float32)
        out = chan_ref[24:25, lanes] + chan_ref[3:4, lanes] * value[EDGE:]
        for j in range(1, KC):
            same = jnp.concatenate([same_ref[j - 1]] * 2, axis=1)
            out = out + chan_ref[3 - j : 4 - j, lanes] * pltpu.roll(value, j, 0)[EDGE:] * same
        conv[:, lanes] = out
        xs[:, lanes] = (out / (1.0 + jnp.exp(-out))).astype(jnp.bfloat16)
        return unused

    lax.fori_loop(0, channels // piece, conv_piece, 0)
    for save in saves[:3]:
        save.start()
    projected = dot(xs[...], channel_ref[:, :LANES])
    lane = lax.broadcasted_iota(jnp.int32, projected.shape, 1)
    delta_ref[...] = jnp.where(lane >= R + 2 * NS, pltpu.roll(projected, R + 2 * NS, 1), 0.0).astype(jnp.bfloat16)
    for at in range(0, tokens, LANES):
        block = projected[at : at + LANES].T
        bt_ref[:, at : at + LANES] = block[R : R + NS]
        ct_ref[:, at : at + LANES] = block[R + NS : R + 2 * NS]

    def step_piece(index, unused):
        lanes = pl.ds(pl.multiple_of(index * piece, piece), piece)
        value = contract(delta_ref[...], channel_ref[lanes, :LANES], 1, 1) + chan_ref[25:26, lanes]
        pre[:, lanes] = value
        size = jnp.maximum(value, 0.0) + jnp.log1p(jnp.exp(-jnp.abs(value)))
        push[:, lanes] = size * xs[:, lanes].astype(jnp.float32)
        keep = jnp.concatenate([same_ref[0]] * 2, axis=1)
        step[:, lanes] = jnp.where(keep > 0, size, 1e30)
        return unused

    lax.fori_loop(0, channels // piece, step_piece, 0)
    for save in saves[3:]:
        save.start()


def forward_kernel(places, streams, width, room, *refs):
    weights_from = refs[:8]
    shards, leaving = refs[8:10], refs[10]
    y_ref, product_ref = refs[12:14]
    front_outs = refs[14:23]
    kept_ref = refs[23]
    saved = refs[24:30]
    wholes, arriving = refs[30:32], refs[32]
    scratch = refs[33:40]
    weights = refs[40:48]
    (wide_b, wide_c, kept_buf, first_buf, state_ref, message, products, ends,
     load_sems, kept_sems, first_sem, share_sems, save_sems, moved_sems, send_sems, recv_sems, local_sems) = refs[48:]
    loads = [pltpu.make_async_copy(weights_from[k], weights[k], load_sems.at[k]) for k in range(8)]
    for load in loads[:5] + loads[:4:-1]:
        load.start()
    bt_ref, ct_ref, rate_ref = front_outs[1:4]
    step_ref, push_ref = scratch[5:7]
    blocks = lax.axis_size("ctx")
    position = lax.axis_index("ctx")
    span = kept_buf.shape[1]
    flow = GatherFlow(places, streams, range(len(places)), shards, wholes, send_sems, recv_sems, local_sems)
    meet([place for place in places if place[0] == "exp"], *row_peers())
    flow.start()
    move = row_half(leaving, arriving, moved_sems, ("ctx", blocks.bit_length() - 2), 1)
    move.start()
    saves = [
        pltpu.make_async_copy(scratch[k + 1], saved[k], save_sems.at[k]) for k in range(6)
    ]
    front(weights, loads, room, front_outs, scratch, saves)

    message[0] = jnp.exp2(jnp.sum(step_ref[...], axis=0, keepdims=True) * rate_ref[...]).astype(jnp.bfloat16)
    early = share(message.at[0], products, share_sems.at[0], share_sems.at[1])
    spread_columns(bt_ref, wide_b)
    spread_columns(ct_ref, wide_c)
    end_pass(width, step_ref, push_ref, wide_b, rate_ref, state_ref, lambda group: None)
    message[1] = state_ref[...].astype(jnp.bfloat16)
    late = share(message.at[1], ends, share_sems.at[2], share_sems.at[3])
    flow.advance(0)
    for copy in early + late:
        copy.wait_recv()
    start = jnp.zeros(state_ref.shape, jnp.float32)
    for index in range(blocks):
        folded = products[index].astype(jnp.float32) * start + ends[index].astype(jnp.float32)
        start = jnp.where(index < position, folded, start)
    state_ref[...] = start
    product_ref[...] = products[...]
    first_buf[0] = start.astype(jnp.bfloat16)
    first_copy = pltpu.make_async_copy(first_buf, kept_ref.at[pl.ds(0, 1)], first_sem)
    first_copy.start()

    def kept_copy(number, slot):
        return pltpu.make_async_copy(
            kept_buf.at[slot], kept_ref.at[pl.ds(1 + number * span, span)], kept_sems.at[slot]
        )

    def hook(number):
        @pl.when(number == 3)
        def _():
            flow.advance(1)

    out_pass(width, step_ref, push_ref, wide_b, wide_c, rate_ref, state_ref, y_ref, kept_buf, kept_copy, hook)
    for stage in range(2, max(flow.stages(number) for number in range(len(streams)))):
        flow.advance(stage)
    flow.finish()
    first_copy.wait()
    for save in saves:
        save.wait()
    for copy in early + late:
        copy.wait_send()
    move.wait()


def scan_forward(sizes, rows_in, prior, ids, weights, room, shards, leaving, begun, identity, span=64):
    places = bit_positions(sizes)
    stages = len(places)
    begin = len(far_of(places))
    streams = halves(shards, *gather_orders(places), begin=begin)
    tokens, width = rows_in.shape
    channels = weights[0].shape[1]
    blocks = sizes[0][1]
    inside = pl.BlockSpec(memory_space=pltpu.VMEM)
    anywhere = pl.BlockSpec(memory_space=pl.ANY)
    half, full = jnp.bfloat16, jnp.float32
    shape = jax.ShapeDtypeStruct
    saved = [
        shape((EDGE + tokens, channels), half),
        shape((tokens, channels), full),
        shape((tokens, channels), half),
        shape((tokens, channels), full),
        shape((tokens, channels), full),
        shape((tokens, channels), full),
    ]
    y, products, normed, bt, ct, rates, chan, gains, delta, same, target, kept, *rest = pl.pallas_call(
        functools.partial(forward_kernel, places, streams, pick(channels), room),
        in_specs=[anywhere] * 12,
        input_output_aliases={11: 20},
        out_specs=[inside] * 11 + [anywhere] * 10,
        out_shape=[
            shape((tokens, channels), full),
            shape((blocks, NS, channels), half),
            shape((tokens, width), half),
            shape((NS, tokens), full),
            shape((NS, tokens), full),
            shape((NS, channels), full),
            shape((32, channels), full),
            shape((8, width), full),
            shape((tokens, LANES), half),
            shape((KC - 1, tokens, LANES), full),
            shape((tokens, LANES), full),
            shape((tokens + 1, NS, channels), half),
        ]
        + saved
        + [shape((2,) * stages + shard.shape[begin:], shard.dtype) for shard in shards]
        + [shape(leaving.shape, leaving.dtype)],
        scratch_shapes=[pltpu.VMEM((EDGE + tokens, width), half)]
        + [pltpu.VMEM(value.shape, value.dtype) for value in saved]
        + [pltpu.VMEM(value.shape, value.dtype) for value in [rows_in, *prior, *ids, *weights]]
        + [
            pltpu.VMEM((tokens, NS, LANES), full),
            pltpu.VMEM((tokens, NS, LANES), full),
            pltpu.VMEM((2, span, NS, channels), half),
            pltpu.VMEM((1, NS, channels), half),
            pltpu.VMEM((NS, channels), full),
            pltpu.VMEM((2, NS, channels), half),
            pltpu.VMEM((blocks, NS, channels), half),
            pltpu.VMEM((blocks, NS, channels), half),
            pltpu.SemaphoreType.DMA((8,)),
            pltpu.SemaphoreType.DMA((2,)),
            pltpu.SemaphoreType.DMA,
            pltpu.SemaphoreType.DMA((4, blocks)),
            pltpu.SemaphoreType.DMA((6,)),
            pltpu.SemaphoreType.DMA((2, 2)),
            pltpu.SemaphoreType.DMA((len(streams), stages)),
            pltpu.SemaphoreType.DMA((len(streams), stages)),
            pltpu.SemaphoreType.DMA((len(streams),)),
        ],
        compiler_params=pltpu.CompilerParams(
            collective_id=identity, has_side_effects=True, vmem_limit_bytes=62 * 1024 * 1024
        ),
        cost_estimate=cost(tokens, channels, 9),
        name="scan_forward",
    )(rows_in, *prior, *ids, *weights, *shards, leaving, begun)
    saved, wholes, arrived = rest[:6], rest[6:8], rest[8]
    wholes = [whole.reshape((-1,) + whole.shape[stages + 1 :]) for whole in wholes]
    return y, products, normed, bt, ct, rates, chan, gains, delta, same, target, kept, saved, wholes, arrived


def backward_kernel(places, streams, marks, width, *refs):
    bt_ref, ct_ref, rate_ref, product_ref = refs[:4]
    parts = refs[4:6]
    streamed = refs[6:9]
    kept_ref, leaving = refs[9:11]
    outs = refs[11:]
    gb_ref, gc_ref, ga_ref = outs[:3]
    totals, arriving = outs[3:5], outs[5]
    rows_out = outs[6:8]
    scratch = outs[8:]
    landing = scratch[:marks]
    (step_ref, push_ref, grad_ref, along_ref, slope_ref, wide_b, wide_c, part_b, part_c, kept_buf, flow_ref, message,
     inflows, load_sems, push_sem, out_sems, kept_sems, share_sems, moved_sems, send_sems, recv_sems) = scratch[marks:]
    blocks = lax.axis_size("ctx")
    position = lax.axis_index("ctx")
    span = kept_buf.shape[1] - 1
    steps = step_ref.shape[0] // span

    def load(group, k):
        lanes = pl.ds(pl.multiple_of(group * width, LANES), width)
        source, target = ((streamed[0], step_ref), (streamed[2], grad_ref))[k]
        return pltpu.make_async_copy(source.at[:, lanes], target.at[:, lanes], load_sems.at[k, group])

    for group in range(step_ref.shape[1] // width):
        for k in range(2):
            load(group, k).start()
    push_load = pltpu.make_async_copy(streamed[1], push_ref, push_sem)
    push_load.start()

    def ready(group):
        for k in range(2):
            load(group, k).wait()

    def rows_copy(number, k):
        rows = pl.ds(number * span, span)
        return pltpu.make_async_copy((along_ref, slope_ref)[k].at[rows], rows_out[k].at[rows], out_sems.at[k, number])

    flow = ReduceFlow(places, streams, range(len(places)), parts, totals, landing, send_sems, recv_sems)

    def kept_copy(number, slot):
        return pltpu.make_async_copy(
            kept_ref.at[pl.ds(number * span, span + 1)], kept_buf.at[slot], kept_sems.at[slot]
        )

    for order in range(min(2, steps)):
        kept_copy(steps - 1 - order, order).start()
    meet([place for place in places if place[0] == "exp"], *row_peers())
    flow.start()
    move = row_half(leaving, arriving, moved_sems, ("ctx", blocks.bit_length() - 2), 0)
    move.start()
    spread_columns(bt_ref, wide_b)
    spread_columns(ct_ref, wide_c)
    inflow_pass(width, step_ref, grad_ref, wide_c, rate_ref, flow_ref, ready)
    message[...] = flow_ref[...].astype(jnp.bfloat16)
    copies = share(message, inflows, share_sems.at[0], share_sems.at[1])
    for copy in copies:
        copy.wait_recv()
    end = jnp.zeros(flow_ref.shape, jnp.float32)
    for index in reversed(range(blocks)):
        folded = inflows[index].astype(jnp.float32) + product_ref[index].astype(jnp.float32) * end
        end = jnp.where(index > position, folded, end)
    flow_ref[...] = end
    flow.advance(0)
    push_load.wait()

    def hook(order):
        for k in range(2):
            rows_copy(steps - 1 - order, k).start()

        @pl.when(order == 2)
        def _():
            flow.advance(1)

        @pl.when(order == 4)
        def _():
            flow.advance(2)

    adjoint_pass(width, step_ref, push_ref, grad_ref, wide_b, wide_c, rate_ref, flow_ref, kept_buf, kept_copy,
                 along_ref, slope_ref, gb_ref, gc_ref, ga_ref, part_b, part_c, hook)
    for stage in range(3, len(streams[0][2])):
        flow.advance(stage)
    flow.finish()
    for copy in copies:
        copy.wait_send()
    move.wait()
    for number in range(steps):
        for k in range(2):
            rows_copy(number, k).wait()


def scan_backward(sizes, step, push, grad, b_turned, c_turned, rates, products, parts, kept, leaving, identity, span=64):
    places = bit_positions(sizes)
    stages = len(places)
    far = sorted(far_of(places))
    streams = halves(parts, *[tuple(order[: stages - len(far)]) for order in orders_of(places)])
    divided = [part.reshape((2,) * stages + (-1, part.shape[1])) for part in parts]
    tokens, channels = step.shape
    blocks = sizes[0][1]
    inside = pl.BlockSpec(memory_space=pltpu.VMEM)
    anywhere = pl.BlockSpec(memory_space=pl.ANY)
    half = jnp.bfloat16
    landing = landing_of(streams, range(stages), divided)
    row_sums = jax.ShapeDtypeStruct((tokens // span, UNROLL, span * NS), jnp.float32)
    out = pl.pallas_call(
        functools.partial(backward_kernel, places, streams, len(landing), pick(channels)),
        in_specs=[inside] * 6 + [anywhere] * 5,
        out_specs=[inside] * 5 + [anywhere] * 3,
        out_shape=[row_sums, row_sums, jax.ShapeDtypeStruct((NS, channels), jnp.float32)]
        + [jax.ShapeDtypeStruct((2,) * len(far) + block.shape[-2:], half) for block in divided]
        + [jax.ShapeDtypeStruct(leaving.shape, leaving.dtype)]
        + [jax.ShapeDtypeStruct((tokens, channels), jnp.float32)] * 2,
        scratch_shapes=landing
        + [pltpu.VMEM((tokens, channels), jnp.float32)] * 5
        + [
            pltpu.VMEM((tokens, NS, LANES), jnp.float32),
            pltpu.VMEM((tokens, NS, LANES), jnp.float32),
            pltpu.VMEM((span, NS, LANES), jnp.float32),
            pltpu.VMEM((span, NS, LANES), jnp.float32),
            pltpu.VMEM((2, span + 1, NS, channels), half),
            pltpu.VMEM((NS, channels), jnp.float32),
            pltpu.VMEM((NS, channels), half),
            pltpu.VMEM((blocks, NS, channels), half),
            pltpu.SemaphoreType.DMA((2, channels // pick(channels))),
            pltpu.SemaphoreType.DMA,
            pltpu.SemaphoreType.DMA((2, tokens // span)),
            pltpu.SemaphoreType.DMA((2,)),
            pltpu.SemaphoreType.DMA((2, blocks)),
            pltpu.SemaphoreType.DMA((2, 2)),
        ]
        + flights(streams),
        compiler_params=pltpu.CompilerParams(
            collective_id=identity, has_side_effects=True, vmem_limit_bytes=56 * 1024 * 1024
        ),
        cost_estimate=cost(tokens, channels, 15),
        name="scan_backward",
    )(b_turned, c_turned, rates, products, *divided, step, push, grad, kept, leaving)
    wide_b, wide_c, grad_a, first, second, arrived, along, slope = out
    grad_bs, grad_cs = [values[:, 0].reshape(tokens, NS) for values in (wide_b, wide_c)]
    return along, slope, grad_bs, grad_cs, grad_a, (first, second), arrived


class PackedReduce(ReduceFlow):
    def __init__(self, places, streams, heads, parts, totals, landing, blocks, send_sems, recv_sems):
        super().__init__(places, streams, range(len(places)), parts, totals, landing, send_sems, recv_sems)
        self.heads, self.blocks = heads, blocks

    def side(self, number, stage, value):
        array, cols, order = self.streams[number]
        if stage == 0:
            index = tuple(value if p == order[0] else slice(None) for p in range(self.heads))
            return self.parts[array].at[index + (slice(None), cols)]
        left = [p for p in self.dims if p not in order[:stage]]
        index = tuple(value if p == order[stage] else slice(None) for p in left)
        held = self.blocks[number] if stage == 1 else self.spot(number, stage - 1)
        return held.at[index]

    def advance(self, stage):
        if stage:
            super().advance(stage)
            return
        for number, (array, cols, order) in enumerate(self.streams):
            self.flight(number, 0).wait_recv()
            mine = self.side(number, 0, self.bits[order[0]])
            there, held = self.spot(number, 0), self.blocks[number]
            tails = len(self.places) - self.heads
            size = held.shape[-2]

            def add(index, unused, mine=mine, there=there, held=held, tails=tails, size=size):
                at = tuple(lax.rem(index // 2 ** (self.heads - 2 - k), 2) for k in range(self.heads - 1))
                value = there[at].astype(jnp.float32) + mine[at].astype(jnp.float32)
                for block in range(2**tails):
                    spot = tuple(block // 2 ** (tails - 1 - k) % 2 for k in range(tails))
                    held[at + spot] = value[block * size : (block + 1) * size].astype(held.dtype)
                return unused

            lax.fori_loop(0, 2 ** (self.heads - 1), add, 0)
            self.flight(number, 1).start()


def turned(values):
    return jnp.concatenate([values[:, at : at + LANES].T for at in range(0, values.shape[1], LANES)], axis=0)


def finish_kernel(places, streams, third, late, far, marks, *refs):
    leaving = refs[22:24]
    refs = refs[:22] + refs[26:]
    (along_h, slope_h, grad_h, pre_h, conv_h, xs_h, ext_h, gz_h, wc_h, wg_h) = refs[:10]
    (normed_ref, in_ref, resid_ref, mix_ref, bc_ref, delta_ref, same_ref, chan_ref, decay_ref, wide_ref) = refs[10:20]
    rest_parts = refs[20:22]
    gi_ref, own_in, own_out, tot_small, tot_wide = refs[22:27]
    arriving, scratch = refs[27:29], refs[29:]
    landing, scratch = scratch[: marks[0]], scratch[marks[0] :]
    blocks, scratch = scratch[: marks[1]], scratch[marks[1] :]
    landing3, scratch = scratch[: marks[2]], scratch[marks[2] :]
    blocks3, scratch = scratch[: marks[3]], scratch[marks[3] :]
    late_landing, scratch = scratch[: marks[4]], scratch[marks[4] :]
    (along, slope, grad, pre, conv, xs, ext, gz, wc, wg, gdt, gci, last, spill, arrived, sums, rows_s, wide_s, gn,
     part_conv, part_small, part_wide, normed_t,
     block_sems, whole_sems, spill_sems, moved_sems, send_sems, recv_sems, send3, recv3, late_send, late_recv) = scratch
    tokens, channels = xs.shape
    own_conv, own_gate = own_in.at[:, :channels], own_in.at[:, channels:]
    span = tokens // block_sems.shape[1]
    heads = len([place for place in places if place[0] == "ctx"])
    flow = PackedReduce(
        places, streams, heads, (part_conv, part_small), (own_conv, tot_small), landing, blocks, send_sems, recv_sems
    )
    flow3 = PackedReduce(places, third, heads, (part_wide,), (tot_wide,), landing3, blocks3, send3, recv3)
    rest = ReduceFlow(places, late, far, rest_parts, (own_gate, own_out), late_landing, late_send, late_recv)

    streamed = ((along_h, along), (slope_h, slope), (grad_h, grad), (pre_h, pre), (xs_h, xs))

    def block_copy(k, number):
        rows = pl.ds(number * span, span)
        source, target = streamed[k]
        return pltpu.make_async_copy(source.at[rows], target.at[rows], block_sems.at[k, number])

    for number in range(tokens // span):
        for k in range(len(streamed)):
            block_copy(k, number).start()
    wholes = [
        pltpu.make_async_copy(source, target, whole_sems.at[k])
        for k, (source, target) in enumerate(((conv_h, conv), (ext_h, ext), (gz_h, gz), (wc_h, wc), (wg_h, wg)))
    ]
    for copy in wholes:
        copy.start()
    count = lax.axis_size("ctx")
    here, line = lax.axis_index("ctx"), lax.axis_index("exp")
    before = (lax.rem(here + count - 1, count), line)
    meet(places, before, (lax.rem(here + 1, count), line))
    rest.start()
    moves = [
        row_half(leaving[k], arriving[k], moved_sems.at[k], ("ctx", count.bit_length() - 2), 1) for k in range(2)
    ]
    moves[0].start()

    sums[...] = jnp.zeros_like(sums)
    rows_s[...] = jnp.zeros_like(rows_s)

    def first_block(number, unused):
        for k in range(len(streamed)):
            block_copy(k, number).wait()

        def some(index, unused_inner):
            at = pl.ds(pl.multiple_of(number * span + index * 16, 16), 16)
            for low in range(0, channels, LANES):
                lanes = slice(low, low + LANES)
                a, g, x, p = along[at, lanes], grad[at, lanes], xs[at, lanes].astype(jnp.float32), pre[at, lanes]
                small = jnp.exp(-jnp.abs(p))
                gated = jnp.where(p >= 0, 1.0, small) / (1.0 + small)
                step = jnp.maximum(p, 0.0) + jnp.log1p(small)
                value = (a * x + slope[at, lanes] * (1.0 / LOG2E)) * gated
                gdt[at, lanes] = value.astype(jnp.bfloat16)
                sums[0, :, lanes] += value[:8] + value[8:]
                both = g * x
                sums[1, :, lanes] += both[:8] + both[8:]
                along[at, lanes] = chan_ref[4:5, lanes] * g + a * step
            return unused_inner

        lax.fori_loop(0, span // 16, some, 0)
        return unused

    lax.fori_loop(0, tokens // span, first_block, 0)
    rows_s[25:26, :] = jnp.sum(sums[0], axis=0, keepdims=True)
    rows_s[26:27, :] = jnp.sum(sums[1], axis=0, keepdims=True)
    rows_s[8:24, :] = decay_ref[0] * decay_ref[1] * (1.0 / LOG2E)

    lane = lax.broadcasted_iota(jnp.int32, (tokens, LANES), 1)
    mixed = pltpu.roll(dot(gdt[...], mix_ref[:, :LANES]), R, 1)
    projected = jnp.where(lane < R, mixed, jnp.where(lane < R + 2 * NS, bc_ref[...], 0.0)).astype(jnp.bfloat16)
    wholes[0].wait()
    wholes[1].wait()
    piece = 2 * LANES
    tail_row = lax.broadcasted_iota(jnp.int32, (tokens, piece), 0)

    def conv_piece(index, unused):
        lanes = pl.ds(pl.multiple_of(index * piece, piece), piece)
        some = pl.ds(pl.multiple_of(index * piece, piece), piece)
        total = along[:, lanes] + contract(projected, mix_ref[some, :LANES], 1, 1)
        value = conv[:, lanes]
        gate = 1.0 / (1.0 + jnp.exp(-value))
        out = total * gate * (1.0 + value * (1.0 - gate))
        rows_s[24:25, lanes] = jnp.sum(out, axis=0, keepdims=True)
        before_rows = ext[:, lanes].astype(jnp.float32)
        rows_s[3:4, lanes] = jnp.sum(out * before_rows[EDGE:], axis=0, keepdims=True)
        result = chan_ref[3:4, lanes] * out
        beyond = jnp.zeros((8, piece), jnp.float32)
        for j in range(1, KC):
            same = jnp.concatenate([same_ref[j - 1]] * 2, axis=1)
            masked = out * same
            shifted_rows = pltpu.roll(before_rows, j, 0)[EDGE:]
            rows_s[3 - j : 4 - j, lanes] = jnp.sum(masked * shifted_rows, axis=0, keepdims=True)
            moved = chan_ref[3 - j : 4 - j, lanes] * pltpu.roll(masked, tokens - j, 0)
            result = result + jnp.where(tail_row < tokens - j, moved, 0.0)
            beyond = beyond + jnp.where(tail_row < tokens - j, 0.0, moved)[tokens - 8 :]
        gci[:, lanes] = result.astype(jnp.bfloat16)
        last[:, lanes] = result[tokens - 16 :]
        spill[:, lanes] = beyond
        return unused

    lax.fori_loop(0, channels // piece, conv_piece, 0)
    handed = pltpu.make_async_remote_copy(
        src_ref=spill,
        dst_ref=arrived,
        send_sem=spill_sems.at[0],
        recv_sem=spill_sems.at[1],
        device_id=before,
        device_id_type=MESH,
    )
    handed.start()

    cut = part_small.shape[-2]
    first_rows = contract(projected, xs[...], 0, 0) + contract(delta_ref[...], gdt[...], 0, 0)
    filler = jnp.zeros((LANES - rows_s.shape[0], channels), jnp.float32)
    for k, values in enumerate((first_rows, jnp.concatenate([rows_s[...], filler], axis=0))):
        columns = turned(values)
        for index in range(channels // cut):
            spot = tuple(index // 2 ** (heads - 1 - j) % 2 for j in range(heads))
            part_small[spot + (slice(None), slice(k * LANES, (k + 1) * LANES))] = columns[
                index * cut : (index + 1) * cut
            ].astype(jnp.bfloat16)
    for low in range(0, tokens, LANES):
        for left in range(0, normed_ref.shape[1], LANES):
            square = normed_ref[low : low + LANES, left : left + LANES].astype(jnp.float32).T
            normed_t[left : left + LANES, low : low + LANES] = square.astype(jnp.bfloat16)

    handed.wait_recv()
    closing = last[...] + jnp.concatenate([jnp.zeros((8, channels), jnp.float32), arrived[...]], axis=0)
    gci[tokens - 16 :, :] = closing.astype(jnp.bfloat16)

    long = part_conv.shape[-2]

    def product_piece(index, unused):
        lanes = pl.ds(pl.multiple_of(index * piece, piece), piece)
        value = dot(normed_t[...], gci[:, lanes])
        for block in range(value.shape[0] // long):
            spot = tuple(block // 2 ** (heads - 1 - k) % 2 for k in range(heads))
            part_conv[spot + (slice(None), lanes)] = value[block * long : (block + 1) * long].astype(jnp.bfloat16)
        return unused

    lax.fori_loop(0, channels // piece, product_piece, 0)
    flow.start()

    for copy in wholes[2:]:
        copy.wait()
    width = gn.shape[1]

    def normed_piece(index, unused):
        lanes = pl.ds(pl.multiple_of(index * piece, piece), piece)
        gn[:, lanes] = contract(gci[...], wc[lanes, :], 1, 1) + contract(gz[...], wg[lanes, :], 1, 1)
        return unused

    lax.fori_loop(0, width // piece, normed_piece, 0)
    wide_s[...] = wide_ref[...]
    gain = wide_ref[0:1, :]

    def back(index, total):
        at = pl.ds(pl.multiple_of(index * 16, 16), 16)
        x, g = in_ref[at, :].astype(jnp.float32), gn[at, :]
        scale = lax.rsqrt(jnp.mean(x * x, axis=-1, keepdims=True) + EPS)
        scaled = g * gain
        share_of = jnp.mean(x * scaled, axis=-1, keepdims=True)
        gi_ref[at, :] = resid_ref[at, :] + scale * scaled - x * (scale * scale * scale * share_of)
        value = g * (x * scale)
        return total + value[:8] + value[8:]

    total = lax.fori_loop(0, tokens // 16, back, jnp.zeros((8, width), jnp.float32))
    wide_s[0:1, :] = jnp.sum(total, axis=0, keepdims=True)
    flow.advance(0)
    filler = jnp.zeros((LANES - wide_s.shape[0], width), jnp.float32)
    columns = turned(jnp.concatenate([wide_s[...], filler], axis=0))
    short = part_wide.shape[-2]
    for block in range(width // short):
        spot = tuple(block // 2 ** (heads - 1 - k) % 2 for k in range(heads))
        part_wide[spot] = columns[block * short : (block + 1) * short].astype(jnp.bfloat16)
    flow3.start()
    rest.advance(0)
    for stage in range(1, len(places)):
        flow.advance(stage)
        flow3.advance(stage - 1)
        rest.advance(stage)
        if stage == 2:
            moves[1].start()
    flow3.advance(len(places) - 1)

    flow.finish()
    flow3.finish()
    rest.finish()
    handed.wait_send()
    for move in moves:
        move.wait()


def finish(sizes, streamed, inside_values, parts, leaving, arrived, identity, span=64):
    places = bit_positions(sizes)
    stages = len(places)
    far = sorted(far_of(places))
    heads = sizes[0][1].bit_length() - 1
    tails = stages - heads
    along, slope, grad, pre, conv, xs, ext, gz, wc, wg = streamed
    normed = inside_values[0]
    tokens, channels = xs.shape
    width = normed.shape[1]
    devices = 2**stages
    half, wide = jnp.bfloat16, jnp.float32
    rows, thin = channels // devices, width // devices
    orders = [tuple(order) for order in orders_of(places)]
    conv_like = jax.ShapeDtypeStruct((width, channels), half)
    small_like = jax.ShapeDtypeStruct((channels, 2 * LANES), half)
    wide_like = jax.ShapeDtypeStruct((width, LANES), half)
    streams = halves((conv_like, small_like), *orders)
    third = halves((wide_like,), *orders)
    late = [(k, slice(0, part.shape[-1]), tuple(far_of(places))) for k, part in enumerate(parts)]

    def room(of, sizes_of):
        landing, blocks = [], []
        for array, cols, order in of:
            size, many = sizes_of[array], cols.stop - cols.start
            landing.append(pltpu.VMEM((2,) * (heads - 1) + (size * 2**tails, many), half))
            landing += [pltpu.VMEM((2,) * (stages - stage - 1) + (size, many), half) for stage in range(1, stages)]
            blocks.append(pltpu.VMEM((2,) * (stages - 1) + (size, many), half))
        return landing, blocks

    landing, blocks = room(streams, (thin, rows))
    landing3, blocks3 = room(third, (thin,))
    late_landing = landing_of(late, far, parts)
    marks = [len(landing), len(blocks), len(landing3), len(blocks3), len(late_landing)]
    inside = pl.BlockSpec(memory_space=pltpu.VMEM)
    anywhere = pl.BlockSpec(memory_space=pl.ANY)
    return pl.pallas_call(
        functools.partial(finish_kernel, places, streams, third, late, far, marks),
        in_specs=[anywhere] * 10 + [inside] * (len(inside_values) + 2) + [anywhere] * 4,
        input_output_aliases={24: 5, 25: 6},
        out_specs=[inside] * 5 + [anywhere] * 2,
        out_shape=[
            jax.ShapeDtypeStruct(normed.shape, wide),
            jax.ShapeDtypeStruct((thin, 2 * channels), wide),
            jax.ShapeDtypeStruct(parts[1].shape[-2:], wide),
            jax.ShapeDtypeStruct((rows, 2 * LANES), wide),
            jax.ShapeDtypeStruct((thin, LANES), wide),
        ]
        + [jax.ShapeDtypeStruct(values.shape, half) for values in leaving],
        scratch_shapes=landing + blocks + landing3 + blocks3 + late_landing
        + [pltpu.VMEM(value.shape, value.dtype) for value in streamed]
        + [
            pltpu.VMEM((tokens, channels), half),
            pltpu.VMEM((tokens, channels), half),
            pltpu.VMEM((16, channels), wide),
            pltpu.VMEM((8, channels), wide),
            pltpu.VMEM((8, channels), wide),
            pltpu.VMEM((2, 8, channels), wide),
            pltpu.VMEM((32, channels), wide),
            pltpu.VMEM(inside_values[-1].shape, wide),
            pltpu.VMEM((tokens, width), wide),
            pltpu.VMEM((2,) * heads + (thin * 2**tails, channels), half),
            pltpu.VMEM((2,) * heads + (rows * 2**tails, 2 * LANES), half),
            pltpu.VMEM((2,) * heads + (thin * 2**tails, LANES), half),
            pltpu.VMEM((width, tokens), half),
            pltpu.SemaphoreType.DMA((5, tokens // span)),
            pltpu.SemaphoreType.DMA((5,)),
            pltpu.SemaphoreType.DMA((2,)),
            pltpu.SemaphoreType.DMA((2, 2, 2)),
        ]
        + flights(streams)
        + flights(third)
        + flights(late),
        compiler_params=pltpu.CompilerParams(
            collective_id=identity, has_side_effects=True, vmem_limit_bytes=56 * 1024 * 1024
        ),
        name="finish",
    )(*streamed, *inside_values, *parts, *leaving, *arrived)


def emit_kernel(gi_from, wo_from, wo_other, wi_from, wi_other, in_from, out_from, small_ref, thin_ref,
                gi, w_out, w_in, own_in, own_out, own_x, own_dt, own_taps, own_decay, own_router, *singles):
    gi[...] = gi_from[...]
    w_out[...] = wo_from[...].astype(jnp.float32) + wo_other[...].astype(jnp.float32)
    w_in[...] = wi_from[...].astype(jnp.float32) + wi_other[...].astype(jnp.float32)
    own_in[...] = in_from[...]
    own_out[...] = out_from[...]

    def columns_of(values):
        return jnp.concatenate([values, jnp.zeros((LANES - values.shape[0], LANES), jnp.float32)], axis=0).T

    size, thin = small_ref.shape[0], thin_ref.shape[0]
    first = small_ref[:, :LANES]
    own_x[...] = first[:, : R + 2 * NS]
    own_dt[...] = columns_of(first)[R + 2 * NS :, :size]
    by_row = columns_of(small_ref[:, LANES:])
    own_taps[...] = by_row[:KC, :size]
    own_decay[...] = by_row[8 : 8 + NS, :size]
    for k in range(3):
        singles[k][...] = by_row[24 + k : 25 + k, :size]
    by_row = columns_of(thin_ref[...])
    for k in range(2):
        singles[3 + k][...] = by_row[k : k + 1, :thin]
    own_router[...] = by_row[8 : 8 + own_router.shape[0], :thin]


def emit_outputs(gi, w_out, out_other, w_in, in_other, own_in, own_out, small, thin_part, experts, pieces=4):
    rows, thin = small.shape[0], thin_part.shape[0]
    full = jnp.float32

    def cut(values):
        return pl.BlockSpec((values.shape[0] // pieces, values.shape[1]), lambda i: (i, 0))

    def whole(shape):
        return pl.BlockSpec(shape, lambda i: (0, 0))

    large = [gi, w_out, out_other, w_in, in_other]
    results = [gi, w_out, w_in]
    still = [own_in, own_out, small, thin_part]
    shapes = [own_in.shape, own_out.shape, (rows, R + 2 * NS), (R, rows), (KC, rows), (NS, rows), (experts, thin)]
    shapes += [(1, rows)] * 3 + [(1, thin)] * 2
    return pl.pallas_call(
        emit_kernel,
        grid=(pieces,),
        in_specs=[cut(values) for values in large] + [whole(values.shape) for values in still],
        out_specs=[cut(values) for values in results] + [whole(shape) for shape in shapes],
        out_shape=[jax.ShapeDtypeStruct(values.shape, full) for values in results]
        + [jax.ShapeDtypeStruct(shape, full) for shape in shapes],
        name="emit_outputs",
    )(*large, *still)


def expert_kernel(slices, *refs):
    tokens_ref, grads_ref, column_ref = refs[:3]
    even = range(0, slices, 2)
    odd = range(1, slices, 2)
    weights_in, weight_out = refs[3 : 3 + len(even)], refs[3 + len(even)]
    outs = refs[4 + len(even) :]
    picked_ref, back_ref = outs[:2]
    sums_in = outs[2 : 2 + len(even)]
    kept_out, leaving_out, arriving_out = outs[2 + len(even) : 5 + len(even)]
    (sent, got, answer, returned, w_in, w_out, hidden, total, active, slope, inner, sum_out, pair_out, pair_in, far_out,
     rows_t, send_sems, recv_sems, weight_sems, sum_sems, spread_sems, mate_sems, far_sems, moved_sems) = outs[
        5 + len(even) :
    ]
    experts, room, width = sent.shape[1:]
    places = experts * room
    me = lax.axis_index("exp")
    here = lax.axis_index("ctx")
    levels = slices.bit_length() - 1

    loads = [pltpu.make_async_copy(weight_out, w_out.at[0], weight_sems.at[slices])]
    for k, s in enumerate(even):
        loads.append(pltpu.make_async_copy(weights_in[k], w_in.at[s], weight_sems.at[s]))
    for load in loads:
        load.start()

    barrier = pltpu.get_barrier_semaphore()
    mates = [partner(("ctx", level)) for level in range(levels)]
    for step in range(1, experts):
        pl.semaphore_signal(barrier, inc=1, device_id=(here, lax.rem(me + step, experts)), device_id_type=MESH)
    for mate in mates:
        pl.semaphore_signal(barrier, inc=1, device_id=mate, device_id_type=MESH)
    pl.semaphore_wait(barrier, experts - 1 + levels)

    def exchange(source, target, kind):
        copies = []
        for step in range(1, experts):
            peer = lax.rem(me + step, experts)
            copy = pltpu.make_async_remote_copy(
                src_ref=source.at[peer],
                dst_ref=target.at[me],
                send_sem=send_sems.at[kind, step],
                recv_sem=recv_sems.at[kind, step],
                device_id=(here, peer),
                device_id_type=MESH,
            )
            copy.start()
            copies.append(copy)
        target[me] = source[me]
        return copies

    def hand(source, target, sems, level):
        copy = pltpu.make_async_remote_copy(
            src_ref=source,
            dst_ref=target,
            send_sem=sems.at[0],
            recv_sem=sems.at[1],
            device_id=mates[level],
            device_id_type=MESH,
        )
        copy.start()
        return copy

    def arrive(copies):
        for copy in copies:
            copy.wait_recv()

    open_sends = []

    def spread(level):
        step = 2**level
        copies = [hand(w_out.at[s], w_out.at[s + step], spread_sems.at[1, s + step], level) for s in range(0, slices, 2 * step)]
        open_sends.extend(copies)
        return copies

    spots = lax.broadcasted_iota(jnp.int32, (column_ref.shape[0], places), 1).astype(jnp.float32)
    columns = jnp.concatenate([column_ref[...]] * (places // LANES), axis=1)
    finder = (spots == columns).astype(jnp.float32).astype(jnp.bfloat16)
    sent[0] = contract(finder, tokens_ref[...], 0, 0).astype(jnp.bfloat16).reshape(experts, room, width)
    first = exchange(sent.at[0], got.at[0], 0)
    for load in loads:
        load.wait()
    widening = [spread(levels - 1)]
    paired = [hand(w_in.at[s], w_in.at[s + 1], spread_sems.at[0, s], 0) for s in even]
    sent[1] = contract(finder, grads_ref[...], 0, 0).astype(jnp.bfloat16).reshape(experts, room, width)
    second = exchange(sent.at[1], got.at[1], 1)

    arrive(first)
    rows = got[0].reshape(places, width)
    for s in list(even) + list(odd):
        if s == 1:
            arrive(paired)
        hidden[...] = dot(rows, w_in[s])

        def curve(index, unused):
            at = pl.ds(pl.multiple_of(index * ROWS_AT_ONCE, ROWS_AT_ONCE), ROWS_AT_ONCE)
            value = hidden[at, :]
            bell = 0.5 + 0.5 * lax.erf(value * 0.7071067811865476)
            active[s, at, :] = (value * bell).astype(jnp.bfloat16)
            slope[s, at, :] = bell + value * (jnp.exp(-0.5 * value * value) * 0.3989422804014327)
            return unused

        lax.fori_loop(0, places // ROWS_AT_ONCE, curve, 0)

    for level in reversed(range(levels - 1)):
        arrive(widening[-1])
        widening.append(spread(level))
    for s in list(even) + list(odd):
        if s == 1:
            arrive(widening[-1])
        product = dot(active[s], w_out[s])
        total[...] = product if s == 0 else total[...] + product
    answer[0] = total[...].astype(jnp.bfloat16).reshape(experts, room, width)
    third = exchange(answer.at[0], returned.at[0], 2)

    arrive(second)
    pulled = got[1].reshape(places, width)
    for s in range(slices):
        inner[s] = (contract(pulled, w_out[s], 1, 1) * slope[s]).astype(jnp.bfloat16)
        product = contract(inner[s], w_in[s], 1, 1)
        total[...] = product if s == 0 else total[...] + product
    answer[1] = total[...].astype(jnp.bfloat16).reshape(experts, room, width)
    fourth = exchange(answer.at[1], returned.at[1], 3)
    joining = []
    for s in list(odd) + list(even):
        sum_out[s] = contract(active[s], pulled, 0, 0).astype(jnp.bfloat16)
        if s % 2:
            joining.append(hand(sum_out.at[s], pair_out.at[s // 2], mate_sems.at[0, s // 2], 0))

    def add_into(target, addend):
        def some(index, unused):
            at = pl.ds(pl.multiple_of(index * 4 * ROWS_AT_ONCE, 4 * ROWS_AT_ONCE), 4 * ROWS_AT_ONCE)
            target[at, :] = target[at, :] + addend[at, :]
            return unused

        lax.fori_loop(0, target.shape[0] // (4 * ROWS_AT_ONCE), some, 0)

    arrive(joining)
    for k, s in enumerate(even):
        add_into(sum_out.at[s], pair_out.at[k])

    def pass_on(level):
        step = 2**level
        return [
            hand(sum_out.at[s + step], far_out.at[slices // step // 2 - 1 + s // (2 * step)], far_sems.at[level, s // (2 * step)], level)
            for s in range(0, slices, 2 * step)
        ]

    open_sends.extend(joining)
    for level in range(1, levels - 1):
        passing = pass_on(level)
        arrive(passing)
        open_sends.extend(passing)
        step = 2**level
        for s in range(0, slices, 2 * step):
            add_into(sum_out.at[s], far_out.at[slices // step // 2 - 1 + s // (2 * step)])
    stores = [
        pltpu.make_async_copy(sum_out.at[0], kept_out, sum_sems.at[len(even)]),
        pltpu.make_async_copy(sum_out.at[slices // 2], leaving_out, sum_sems.at[len(even) + 1]),
    ]
    for store in stores:
        store.start()
    move = row_half(sum_out.at[slices // 2], arriving_out, moved_sems, ("ctx", levels - 1), 0)
    move.start()
    for low in range(0, places, LANES):
        for left in range(0, width, LANES):
            square = got[0].reshape(places, width)[low : low + LANES, left : left + LANES].astype(jnp.float32).T
            rows_t[left : left + LANES, low : low + LANES] = square.astype(jnp.bfloat16)
    for copy in paired:
        copy.wait_send()
    joined = []
    for s in list(odd) + list(even):
        w_in[s] = dot(rows_t[...], inner[s]).astype(jnp.bfloat16)
        if s % 2:
            joined.append(hand(w_in.at[s], pair_in.at[s // 2], mate_sems.at[1, s // 2], 0))
    arrive(joined)
    for k, s in enumerate(even):
        add_into(w_in.at[s], pair_in.at[k])
        stores.append(pltpu.make_async_copy(w_in.at[s], sums_in[k], sum_sems.at[k]))
        stores[-1].start()

    arrive(third)
    picked_ref[...] = dot(finder, returned[0].reshape(places, width)).astype(jnp.bfloat16)
    arrive(fourth)
    back_ref[...] = dot(finder, returned[1].reshape(places, width)).astype(jnp.bfloat16)
    for store in stores:
        store.wait()
    move.wait()
    for copies in (first, second, third, fourth, joined, open_sends):
        for copy in copies:
            copy.wait_send()


def run_experts(rows, grads, target, weights_in, weight_out, experts, room, identity):
    slices = 2 * len(weights_in)
    tokens, width = rows.shape
    inner_width = weight_out.shape[0]
    places = experts * room
    inside = pl.BlockSpec(memory_space=pltpu.VMEM)
    anywhere = pl.BlockSpec(memory_space=pl.ANY)
    half = jnp.bfloat16
    count = len(weights_in)
    out = pl.pallas_call(
        functools.partial(expert_kernel, slices),
        in_specs=[inside] * 3 + [anywhere] * (count + 1),
        out_specs=[inside] * 2 + [anywhere] * (count + 3),
        out_shape=[jax.ShapeDtypeStruct(rows.shape, half)] * 2
        + [jax.ShapeDtypeStruct(weight.shape, half) for weight in weights_in]
        + [jax.ShapeDtypeStruct(weight_out.shape, half)] * 3,
        scratch_shapes=[pltpu.VMEM((2, experts, room, width), half)] * 4
        + [
            pltpu.VMEM((slices, width, inner_width), half),
            pltpu.VMEM((slices, inner_width, width), half),
            pltpu.VMEM((places, inner_width), jnp.float32),
            pltpu.VMEM((places, width), jnp.float32),
            pltpu.VMEM((slices, places, inner_width), half),
            pltpu.VMEM((slices, places, inner_width), jnp.float32),
            pltpu.VMEM((slices, places, inner_width), half),
            pltpu.VMEM((slices, inner_width, width), half),
            pltpu.VMEM((count, inner_width, width), half),
            pltpu.VMEM((count, width, inner_width), half),
            pltpu.VMEM((count, inner_width, width), half),
            pltpu.VMEM((width, places), half),
            pltpu.SemaphoreType.DMA((4, experts)),
            pltpu.SemaphoreType.DMA((4, experts)),
            pltpu.SemaphoreType.DMA((slices + 1,)),
            pltpu.SemaphoreType.DMA((count + 2,)),
            pltpu.SemaphoreType.DMA((2, slices, 2)),
            pltpu.SemaphoreType.DMA((2, count, 2)),
            pltpu.SemaphoreType.DMA((slices, count, 2)),
            pltpu.SemaphoreType.DMA((2, 2)),
        ],
        compiler_params=pltpu.CompilerParams(
            collective_id=identity, has_side_effects=True, vmem_limit_bytes=60 * 1024 * 1024
        ),
        name="run_experts",
    )(rows, grads, target, *weights_in, weight_out)
    return out[0], out[1], list(out[2 : 2 + count]), out[2 + count :]


def flipped(value, level):
    count = lax.axis_size("ctx")
    return lax.ppermute(value, "ctx", [(source, source ^ (1 << level)) for source in range(count)])


def spread_slices(own, far):
    levels = lax.axis_size("ctx").bit_length() - 1
    slices = {0: own, 1 << (levels - 1): far}
    for level in reversed(range(1, levels - 1)):
        for offset in sorted(slices):
            slices[offset + (1 << level)] = flipped(slices[offset], level)
    return [slices[offset] for offset in sorted(slices)]


def collect_slices(sums):
    levels = lax.axis_size("ctx").bit_length() - 1
    for level in range(1, levels - 1):
        arrived = [flipped(values, level).astype(jnp.float32) for values in sums[1::2]]
        sums = [
            (values.astype(jnp.float32) + other).astype(jnp.bfloat16) for values, other in zip(sums[::2], arrived)
        ]
    return sums


def body(
    inputs,
    segments,
    routes,
    cotangent,
    norm_gain,
    in_proj,
    conv_taps,
    conv_bias,
    x_proj,
    dt_proj,
    dt_bias,
    log_decay,
    skip_gain,
    out_proj,
    moe_gain,
    router,
    expert_in,
    expert_out,
):
    experts = router.shape[1]
    half_rows = norm_gain.shape[0]
    small = (
        x_proj,
        dt_proj,
        conv_taps.T,
        log_decay.T,
        jnp.stack([conv_bias, dt_bias, skip_gain]),
        jnp.stack([norm_gain, moe_gain]),
        router.T,
    )
    sizes = [(name, lax.axis_size(name)) for name in ("ctx", "exp")]
    weights, partial, begun, *prior = gather_all(
        sizes, small, in_proj, out_proj, inputs[0], segments, expert_in[0], 0
    )
    tokens_here = inputs.shape[1]
    capacity = 5 * tokens_here // (4 * experts)
    room = -(-capacity // 16) * 16
    flat_in = inputs[0].astype(jnp.float32)
    (
        scan_rows,
        products,
        normed_one,
        b_turned,
        c_turned,
        rates,
        by_channel,
        gain_rows,
        delta_low,
        same_rows,
        target,
        kept,
        (conv_ext, conv_out, xs_val, dt_pre, masked_step, push),
        (full_gate, full_out),
        far_in,
    ) = scan_forward(
        sizes,
        inputs[0],
        prior,
        (segments, routes.reshape(1, tokens_here)),
        weights,
        room,
        partial,
        expert_in[0],
        begun,
        3,
    )
    weights_in = spread_slices(expert_in[0], far_in)
    full_conv, full_channel, full_width = weights
    full_skip, full_moe, full_router = by_channel[26], gain_rows[1], full_width[:, 8 : 8 + experts]
    xs_wide = xs_val.astype(jnp.float32)
    gate_z = dot(normed_one, full_gate)
    skip_wide = full_skip
    scanned_y = scan_rows + skip_wide * xs_wide
    gated_wide, gated_pull = jax.vjp(
        lambda scan_in, gate_in: scan_in * jax.nn.silu(gate_in), scanned_y, gate_z
    )
    gated = gated_wide.astype(jnp.bfloat16)
    mixed = jnp.dot(gated, full_out, preferred_element_type=jnp.float32)
    residual = flat_in + mixed
    norm_two_value, norm_two_pull = jax.vjp(rms_scale, residual, full_moe.astype(jnp.float32))
    normed_two = norm_two_value.astype(jnp.bfloat16)
    logits = jnp.dot(normed_two, full_router, preferred_element_type=jnp.float32)
    probability = jax.nn.softmax(logits, axis=-1)
    route_ids = routes[0, :, 0]
    one_hot = route_ids[:, None] == jnp.arange(experts, dtype=jnp.int32)[None, :]
    one_float = one_hot.astype(jnp.float32)
    gate_val = jnp.sum(probability * one_float, axis=1)
    grad_out = cotangent[0].astype(jnp.float32)
    grad_pick = (grad_out * gate_val[:, None]).astype(jnp.bfloat16)
    picked, grad_from_experts, grad_expert_in, (kept_out, leaving_out, begun_out) = run_experts(
        normed_two, grad_pick, target, weights_in, expert_out[0], experts, room, 2
    )
    kept_in, leaving = collect_slices(grad_expert_in)
    picked = picked.astype(jnp.float32)
    grad_from_experts = grad_from_experts.astype(jnp.float32)
    outcome = residual + gate_val[:, None] * picked
    out_block = outcome.astype(jnp.bfloat16)[None]
    grad_gate = jnp.sum(grad_out * picked, axis=1)
    grad_probs = grad_gate[:, None] * one_float
    grad_logits = (
        probability * (grad_probs - jnp.sum(grad_probs * probability, axis=1, keepdims=True))
    ).astype(jnp.bfloat16)
    grad_router = contract(grad_logits, normed_two, 0, 0)
    grad_normed_two = grad_from_experts + jnp.dot(
        grad_logits, full_router.T, preferred_element_type=jnp.float32
    )
    grad_resid_norm, grad_moe_gain = norm_two_pull(grad_normed_two)
    grad_resid = grad_out + grad_resid_norm
    grad_mixed = grad_resid.astype(jnp.bfloat16)
    grad_gated = jnp.dot(grad_mixed, full_out.T, preferred_element_type=jnp.float32)
    grad_out_proj = jnp.dot(gated.T, grad_mixed, preferred_element_type=jnp.float32)
    grad_y, grad_z = gated_pull(grad_gated)
    grad_z = grad_z.astype(jnp.bfloat16)
    along_b, slope, grad_bs, grad_cs, grad_a, partial_sums, begun_in = scan_backward(
        sizes,
        masked_step,
        push,
        grad_y,
        b_turned,
        c_turned,
        rates,
        products,
        (dot(normed_one.T, grad_z).astype(jnp.bfloat16), grad_out_proj.astype(jnp.bfloat16)),
        kept,
        leaving,
        4,
    )
    wide_rows = jnp.concatenate(
        [gain_rows[:1], grad_moe_gain[None], jnp.zeros((6, D), jnp.float32), grad_router]
    )
    finished = finish(
        sizes,
        (along_b, slope, grad_y, dt_pre, conv_out, xs_val, conv_ext, grad_z, full_conv, full_gate),
        (
            normed_one,
            inputs[0],
            grad_resid,
            full_channel,
            jnp.pad(jnp.concatenate([grad_bs, grad_cs], axis=1), ((0, 0), (R, LANES - R - 2 * NS))),
            delta_low,
            same_rows,
            jnp.concatenate([by_channel[:KC], by_channel[26:27], jnp.zeros((3, DI), jnp.float32)]),
            jnp.stack([grad_a, rates]),
            wide_rows,
        ),
        partial_sums,
        (leaving, leaving_out),
        (begun_in, begun_out),
        1,
    )
    grad_inputs, own_in, own_out, own_small, own_thin, arrived, arrived_out = finished
    grad_inputs, grad_w_out, grad_w_in, own_in, own_out, own_x, own_dt, own_taps, own_decay, own_router, *vectors = (
        emit_outputs(
            grad_inputs, kept_out, arrived_out, kept_in, arrived, own_in, own_out, own_small, own_thin, experts
        )
    )
    own_bias, own_dtbias, own_skip, own_norm, own_moe = [values[0] for values in vectors]
    return (
        out_block,
        grad_inputs[None],
        own_norm,
        own_in,
        own_taps.T,
        own_bias,
        own_x,
        own_dt,
        own_dtbias,
        own_decay.T,
        own_skip,
        own_out,
        own_moe,
        own_router.T,
        grad_w_in[None],
        grad_w_out[None],
    )


def solution(mesh):
    placed = (
        P("exp", "ctx", None),
        P("exp", "ctx"),
        P("exp", "ctx", None),
        P("exp", "ctx", None),
        P(("ctx", "exp")),
        P(("ctx", "exp"), None),
        P(("ctx", "exp"), None),
        P(("ctx", "exp")),
        P(("ctx", "exp"), None),
        P(None, ("ctx", "exp")),
        P(("ctx", "exp")),
        P(("ctx", "exp"), None),
        P(("ctx", "exp")),
        P(("ctx", "exp"), None),
        P(("ctx", "exp")),
        P(("ctx", "exp"), None),
        P("exp", None, "ctx"),
        P("exp", "ctx", None),
    )
    return jax.shard_map(
        body,
        mesh=mesh,
        in_specs=placed,
        out_specs=(
            P("exp", "ctx", None),
            P("exp", "ctx", None),
            P(("ctx", "exp")),
            P(("ctx", "exp"), None),
            P(("ctx", "exp"), None),
            P(("ctx", "exp")),
            P(("ctx", "exp"), None),
            P(None, ("ctx", "exp")),
            P(("ctx", "exp")),
            P(("ctx", "exp"), None),
            P(("ctx", "exp")),
            P(("ctx", "exp"), None),
            P(("ctx", "exp")),
            P(("ctx", "exp"), None),
            P("exp", None, "ctx"),
            P("exp", "ctx", None),
        ),
        check_vma=False,
    )
```

```python
import functools

import jax
import jax.numpy as jnp
from jax import lax
from jax.experimental import pallas as pl
from jax.experimental.pallas import tpu as pltpu
from jax.sharding import PartitionSpec as P

D = 768
DI = 1536
NS = 16
R = 48
KC = 4
LANES = 128
UNROLL = 8
LOG2E = 1.4426950408889634


EPS = 1e-05
MESH = pl.DeviceIdType.MESH
ROWS_AT_ONCE = 16
EDGE = 16

def tile(ref, base, lanes):
    return ref[pl.ds(pl.multiple_of(base, UNROLL), UNROLL), lanes]

def row(rows_now, place):
    return jnp.broadcast_to(rows_now[place : place + 1], (NS, LANES))

def cost(tokens, channels, share):
    size = tokens * channels * NS
    return pl.CostEstimate(flops=size * share, transcendentals=size, bytes_accessed=size * share)


def pick(channels):
    return 512 if channels % 512 == 0 else 128


def bit_positions(sizes):
    return [(axis, size.bit_length() - 2 - k) for axis, size in sizes for k in range(size.bit_length() - 1)]


def own_bit(place):
    axis, level = place
    return lax.rem(lax.axis_index(axis) // 2**level, 2)


def partner(place):
    axis, level = place
    where = {"ctx": lax.axis_index("ctx"), "exp": lax.axis_index("exp")}
    where[axis] = where[axis] + (1 - 2 * own_bit(place)) * 2**level
    return (where["ctx"], where["exp"])


def meet(places, *others):
    barrier = pltpu.get_barrier_semaphore()
    for device in [partner(place) for place in places] + list(others):
        pl.semaphore_signal(barrier, inc=1, device_id=device, device_id_type=MESH)
    pl.semaphore_wait(barrier, len(places) + len(others))


class GatherFlow:
    def __init__(self, places, streams, dims, shards, wholes, send_sems, recv_sems, local_sems):
        self.places, self.streams, self.dims, self.shards, self.wholes = places, streams, dims, shards, wholes
        self.sems = send_sems, recv_sems, local_sems
        self.bits = [own_bit(place) for place in places]

    def view(self, number, have):
        array, cols, order, begin = self.streams[number]
        index = tuple(slice(None) if p in have else self.bits[p] for p in self.dims)
        return self.wholes[array].at[index + (slice(None), cols)]

    def shard(self, number):
        array, cols, order, begin = self.streams[number]
        return self.shards[array].at[(slice(None),) * (begin + 1) + (cols,)]

    def own(self, number):
        array, cols, order, begin = self.streams[number]
        return pltpu.make_async_copy(self.shard(number), self.view(number, order[:begin]), self.sems[2].at[number])

    def flight(self, number, stage):
        array, cols, order, begin = self.streams[number]
        target = self.view(number, order[: begin + stage])
        return pltpu.make_async_remote_copy(
            src_ref=self.shard(number) if stage == 0 else target,
            dst_ref=target,
            send_sem=self.sems[0].at[number, stage],
            recv_sem=self.sems[1].at[number, stage],
            device_id=partner(self.places[order[begin + stage]]),
            device_id_type=MESH,
        )

    def stages(self, number):
        array, cols, order, begin = self.streams[number]
        return len(order) - begin

    def start(self):
        for number in range(len(self.streams)):
            self.flight(number, 0).start()
        for number in range(len(self.streams)):
            self.own(number).start()

    def advance(self, stage):
        for number in range(len(self.streams)):
            if stage >= self.stages(number):
                continue
            if stage == 0:
                self.own(number).wait()
            self.flight(number, stage).wait_recv()
            if stage + 1 < self.stages(number):
                self.flight(number, stage + 1).start()

    def finish(self):
        for number in range(len(self.streams)):
            for stage in range(self.stages(number)):
                self.flight(number, stage).wait_send()


def pack_small(small, square, channel_pack, width_pack):
    x_ref, dt_ref, taps_ref, decay_ref, vector_ref, pair_ref, router_ref = small
    rows, thin = channel_pack.shape[0], width_pack.shape[0]

    def laid(*pieces):
        square[...] = jnp.zeros_like(square)
        for first, ref in pieces:
            square[first : first + ref.shape[0], : ref.shape[1]] = ref[...].astype(jnp.float32)
        return square[...]

    dt_part = pltpu.roll(laid((0, dt_ref)).T, R + 2 * NS, 1)
    mix = laid((0, x_ref)) + dt_part
    channel_pack[:, :LANES] = mix[:rows].astype(jnp.bfloat16)
    turned_rows = laid((0, taps_ref), (8, decay_ref), (24, vector_ref)).T
    channel_pack[:, LANES:] = turned_rows[:rows].astype(jnp.bfloat16)
    width_pack[...] = laid((0, pair_ref), (8, router_ref)).T[:thin].astype(jnp.bfloat16)


def gather_kernel(places, streams, extra_streams, far, *refs):
    small = refs[:7]
    in_ref, out_ref, rows_ref, ids_ref, leaving = refs[7:12]
    extra = 2
    wholes, prior_ref, prior_ids, arriving = refs[12:17], refs[17], refs[18], refs[19]
    (square, channel_pack, width_pack, send_sems, recv_sems, local_sems, late_send, late_recv, late_local,
     edge_sems, moved_sems) = refs[20:]
    split = in_ref.shape[1] // 2
    shards = (in_ref.at[:, :split], channel_pack, width_pack, in_ref.at[:, split:], out_ref)
    pack_small(small, square, channel_pack, width_pack)
    count = 3
    flow = GatherFlow(
        places, streams, range(len(places)), shards[:count], wholes[:count], send_sems, recv_sems, local_sems
    )
    late = GatherFlow(
        places, extra_streams, far, shards[count:], wholes[count:], late_send, late_recv, late_local
    )
    blocks = lax.axis_size("ctx")
    here, line = lax.axis_index("ctx"), lax.axis_index("exp")
    meet(places, (lax.rem(here + 1, blocks), line), (lax.rem(here + blocks - 1, blocks), line))
    flow.start()
    tokens = rows_ref.shape[0]
    edges = [
        pltpu.make_async_remote_copy(
            src_ref=source,
            dst_ref=target,
            send_sem=edge_sems.at[0, k],
            recv_sem=edge_sems.at[1, k],
            device_id=(lax.rem(here + 1, blocks), line),
            device_id_type=MESH,
        )
        for k, (source, target) in enumerate(
            (
                (rows_ref.at[pl.ds(tokens - EDGE, EDGE)], prior_ref),
                (ids_ref.at[:, pl.ds(tokens - LANES, LANES)], prior_ids),
            )
        )
    ]
    for edge in edges:
        edge.start()
    move = row_half(leaving, arriving, moved_sems, ("ctx", blocks.bit_length() - 2), 0)
    move.start()
    stages, behind = len(places), len(far)
    for stage in range(stages):
        flow.advance(stage)
        if stage == behind - 2:
            late.start()
        if stage >= behind and stage - behind < behind:
            late.advance(stage - behind)
    for stage in range(stages - behind, behind):
        late.advance(stage)
    flow.finish()
    late.finish()
    for edge in edges:
        edge.wait()
    move.wait()


def orders_of(places):
    core = places.index(("ctx", 0))
    rows = [k for k, place in enumerate(places) if place[0] == "ctx" and place[1] > 0]
    near = places.index(("exp", 0))
    return [core] + rows + [near] + far_of(places), [core, near] + rows + far_of(places)


def far_of(places):
    return [k for k, place in sorted(enumerate(places), key=lambda item: item[1][1]) if place[0] == "exp" and place[1] > 0]


def halves(arrays, first, second, begin=None):
    streams = []
    for array, values in enumerate(arrays):
        width = values.shape[-1]
        rest = () if begin is None else (begin,)
        if width % (2 * LANES) == 0:
            count = 4 if width % (4 * LANES) == 0 and width >= 1024 else 2
            for k in range(count):
                part = (k % 2) * (count // 2) + k // 2
                cols = slice(part * width // count, (part + 1) * width // count)
                streams.append((array, cols, second if k % 2 else first) + rest)
        else:
            streams.append((array, slice(0, width), first if array % 2 else second) + rest)
    return streams


def gather_orders(places):
    return [tuple(reversed(order)) for order in orders_of(places)]


def gather_all(sizes, small, in_proj, out_proj, rows_in, ids, leaving, identity):
    places = bit_positions(sizes)
    stages = len(places)
    far = sorted(far_of(places))
    half = jnp.bfloat16
    rows, thin, split = small[0].shape[0], in_proj.shape[0], in_proj.shape[1] // 2
    shape = jax.ShapeDtypeStruct
    shards = shape((thin, split), half), shape((rows, 2 * LANES), half), shape((thin, LANES), half)
    extra = shape((thin, split), half), shape(out_proj.shape, half)
    streams = halves(shards, *gather_orders(places), begin=0)
    late = [(k, slice(0, part.shape[1]), tuple(reversed(far_of(places))), 0) for k, part in enumerate(extra)]
    anywhere = pl.BlockSpec(memory_space=pl.ANY)
    inside = pl.BlockSpec(memory_space=pltpu.VMEM)
    out = pl.pallas_call(
        functools.partial(gather_kernel, places, streams, late, far),
        in_specs=[inside] * 7 + [anywhere] * 5,
        out_specs=[anywhere] * 8,
        out_shape=[shape((2,) * stages + shard.shape, half) for shard in shards]
        + [shape((2,) * len(far) + part.shape, half) for part in extra]
        + [shape((EDGE, rows_in.shape[1]), half), shape((1, LANES), jnp.int32), shape(leaving.shape, half)],
        scratch_shapes=[
            pltpu.VMEM((LANES, LANES), jnp.float32),
            pltpu.VMEM((rows, 2 * LANES), half),
            pltpu.VMEM((thin, LANES), half),
            pltpu.SemaphoreType.DMA((len(streams), stages)),
            pltpu.SemaphoreType.DMA((len(streams), stages)),
            pltpu.SemaphoreType.DMA((len(streams),)),
            pltpu.SemaphoreType.DMA((len(late), len(far))),
            pltpu.SemaphoreType.DMA((len(late), len(far))),
            pltpu.SemaphoreType.DMA((len(late),)),
            pltpu.SemaphoreType.DMA((2, 2)),
            pltpu.SemaphoreType.DMA((2, 2)),
        ],
        compiler_params=pltpu.CompilerParams(
            collective_id=identity, has_side_effects=True, vmem_limit_bytes=63 * 1024 * 1024
        ),
        name="gather_all",
    )(*small, in_proj, out_proj, rows_in, ids, leaving)
    return [whole.reshape((-1,) + whole.shape[stages + 1 :]) for whole in out[:3]], out[3:5], out[7], out[5], out[6]


class ReduceFlow:
    def __init__(self, places, streams, dims, parts, totals, landing, send_sems, recv_sems):
        self.places, self.streams, self.dims, self.parts, self.totals = places, streams, dims, parts, totals
        self.landing, self.sems = landing, (send_sems, recv_sems)
        self.bits = [own_bit(place) for place in places]
        self.first = []
        for array, cols, order in streams:
            self.first.append(sum(len(other[2]) for other in streams[: len(self.first)]))

    def spot(self, number, stage):
        return self.landing[self.first[number] + stage]

    def side(self, number, stage, value):
        array, cols, order = self.streams[number]
        left = [p for p in self.dims if p not in order[:stage]]
        index = tuple(value if p == order[stage] else slice(None) for p in left)
        if stage == 0:
            return self.parts[array].at[index + (slice(None), cols)]
        return self.spot(number, stage - 1).at[index]

    def flight(self, number, stage):
        order = self.streams[number][2]
        return pltpu.make_async_remote_copy(
            src_ref=self.side(number, stage, 1 - self.bits[order[stage]]),
            dst_ref=self.spot(number, stage),
            send_sem=self.sems[0].at[number, stage],
            recv_sem=self.sems[1].at[number, stage],
            device_id=partner(self.places[order[stage]]),
            device_id_type=MESH,
        )

    def start(self):
        for number in range(len(self.streams)):
            self.flight(number, 0).start()

    def advance(self, stage):
        for number, (array, cols, order) in enumerate(self.streams):
            if stage >= len(order):
                continue
            self.flight(number, stage).wait_recv()
            mine = self.side(number, stage, self.bits[order[stage]])
            there = self.spot(number, stage)
            depth = len(self.dims) - stage - 1
            final = stage + 1 == len(order)
            if depth == 0:
                self.totals[array][:, cols] = there[...].astype(jnp.float32) + mine[...].astype(jnp.float32)
                continue

            def add(index, unused, there=there, mine=mine, depth=depth, final=final, array=array, cols=cols):
                at = tuple(lax.rem(index // 2 ** (depth - 1 - k), 2) for k in range(depth))
                value = there[at] + mine[at]
                if final:
                    self.totals[array][at + (slice(None), cols)] = value
                else:
                    there[at] = value
                return unused

            lax.fori_loop(0, 2**depth, add, 0)
            if not final:
                self.flight(number, stage + 1).start()

    def finish(self):
        for number in range(len(self.streams)):
            for stage in range(len(self.streams[number][2])):
                self.flight(number, stage).wait_send()


def landing_of(streams, dims, divided):
    landing = []
    for array, cols, order in streams:
        for stage in range(len(order)):
            rows = divided[array].shape[-2]
            landing.append(pltpu.VMEM((2,) * (len(dims) - stage - 1) + (rows, cols.stop - cols.start), jnp.bfloat16))
    return landing


def flights(streams):
    shape = (len(streams), max(len(order) for array, cols, order in streams))
    return [pltpu.SemaphoreType.DMA(shape)] * 2


def dot(left, right):
    return jnp.dot(left, right, preferred_element_type=jnp.float32)


def contract(left, right, left_dim, right_dim):
    return lax.dot_general(left, right, (((left_dim,), (right_dim,)), ((), ())), preferred_element_type=jnp.float32)


def lanes_of(group, width, k):
    return pl.ds(pl.multiple_of(group * width + k * LANES, LANES), LANES)


def spread_columns(source_ref, wide_ref):
    def chunk(index, unused):
        base = pl.multiple_of(index * LANES, LANES)
        now = source_ref[:, pl.ds(base, LANES)]
        for place in range(LANES):
            wide_ref[base + place] = jnp.broadcast_to(now[:, place : place + 1], (NS, LANES))
        return unused

    lax.fori_loop(0, source_ref.shape[1] // LANES, chunk, 0)


def end_pass(width, step_ref, push_ref, wide_b, rate_ref, state_ref, hook):
    rows, channels = step_ref.shape
    count = width // LANES

    def group_body(group, unused):
        pieces = [lanes_of(group, width, k) for k in range(count)]
        rates = [rate_ref[:, lanes] for lanes in pieces]

        def block(index, states):
            states = list(states)
            steps = [tile(step_ref, index * UNROLL, lanes) for lanes in pieces]
            pushes = [tile(push_ref, index * UNROLL, lanes) for lanes in pieces]
            for place in range(UNROLL):
                b_now = wide_b[index * UNROLL + place]
                for k in range(count):
                    decay = jnp.exp2(row(steps[k], place) * rates[k])
                    states[k] = decay * states[k] + b_now * row(pushes[k], place)
            return tuple(states)

        zero = jnp.zeros((NS, LANES), jnp.float32)
        states = lax.fori_loop(0, rows // UNROLL, block, (zero,) * count)
        for k, lanes in enumerate(pieces):
            state_ref[:, lanes] = states[k]
        hook(group)
        return unused

    lax.fori_loop(0, channels // width, group_body, 0)


def out_pass(width, step_ref, push_ref, wide_b, wide_c, rate_ref, state_ref, y_ref, kept_buf, kept_copy, hook):
    rows, channels = step_ref.shape
    count = width // LANES
    span = kept_buf.shape[1]
    blocks = rows // span

    def time_body(number, unused):
        slot = lax.rem(number, 2)

        @pl.when(number >= 2)
        def _():
            kept_copy(number - 2, slot).wait()

        def group_body(group, unused_inner):
            pieces = [lanes_of(group, width, k) for k in range(count)]
            rates = [rate_ref[:, lanes] for lanes in pieces]

            def block(index, states):
                states = list(states)
                base = number * span + index * UNROLL
                steps = [tile(step_ref, base, lanes) for lanes in pieces]
                pushes = [tile(push_ref, base, lanes) for lanes in pieces]
                trees = [Tree(True) for k in range(count)]
                for place in range(UNROLL):
                    b_now = wide_b[base + place]
                    c_now = wide_c[base + place]
                    for k, lanes in enumerate(pieces):
                        decay = jnp.exp2(row(steps[k], place) * rates[k])
                        states[k] = decay * states[k] + b_now * row(pushes[k], place)
                        kept_buf[slot, index * UNROLL + place, :, lanes] = states[k].astype(kept_buf.dtype)
                        trees[k].push(place, states[k] * c_now)
                for k, lanes in enumerate(pieces):
                    y_ref[pl.ds(pl.multiple_of(base, UNROLL), UNROLL), lanes] = trees[k].result
                return tuple(states)

            states = lax.fori_loop(0, span // UNROLL, block, tuple(state_ref[:, lanes] for lanes in pieces))
            for k, lanes in enumerate(pieces):
                state_ref[:, lanes] = states[k]
            return unused_inner

        lax.fori_loop(0, channels // width, group_body, 0)
        kept_copy(number, slot).start()
        hook(number)
        return unused

    lax.fori_loop(0, blocks, time_body, 0)
    for number in range(max(0, blocks - 2), blocks):
        kept_copy(number, number % 2).wait()


def inflow_pass(width, step_ref, grad_ref, wide_c, rate_ref, flow_ref, hook):
    rows, channels = step_ref.shape
    count = width // LANES

    def group_body(group, unused):
        hook(group)
        pieces = [lanes_of(group, width, k) for k in range(count)]
        rates = [rate_ref[:, lanes] for lanes in pieces]

        def block(index, flows):
            flows = list(flows)
            base = rows - UNROLL - index * UNROLL
            steps = [tile(step_ref, base, lanes) for lanes in pieces]
            grads = [tile(grad_ref, base, lanes) for lanes in pieces]
            for place in reversed(range(UNROLL)):
                c_now = wide_c[base + place]
                for k in range(count):
                    decay = jnp.exp2(row(steps[k], place) * rates[k])
                    flows[k] = decay * (c_now * row(grads[k], place) + flows[k])
            return tuple(flows)

        zero = jnp.zeros((NS, LANES), jnp.float32)
        flows = lax.fori_loop(0, rows // UNROLL, block, (zero,) * count)
        for k, lanes in enumerate(pieces):
            flow_ref[:, lanes] = flows[k]
        return unused

    lax.fori_loop(0, channels // width, group_body, 0)


class Tree:
    def __init__(self, rising):
        self.rising, self.held, self.result = rising, {}, None

    def push(self, place, value):
        now = value[:UNROLL] + value[UNROLL:]
        level = 0
        while 1 << level < UNROLL:
            if (place >> level) % 2 == (0 if self.rising else 1):
                self.held[level] = now
                return
            first, second = (self.held[level], now) if self.rising else (now, self.held[level])
            now = self.merge(first, second, 1 << level)
            level += 1
        self.result = now

    def merge(self, first, second, distance):
        low = (lax.broadcasted_iota(jnp.int32, (UNROLL, LANES), 0) & distance) == 0
        keep = jnp.where(low, first, second)
        give = jnp.where(low, second, first)
        other = pltpu.roll(give, distance, 0)
        if 2 * distance != UNROLL:
            other = jnp.where(low, pltpu.roll(give, UNROLL - distance, 0), other)
        return keep + other


def lane_sums(part_ref):
    values = part_ref[...].reshape(-1, LANES).astype(jnp.bfloat16)
    return contract(jnp.ones((UNROLL, LANES), jnp.bfloat16), values, 1, 1)


def adjoint_pass(width, step_ref, push_ref, grad_ref, wide_b, wide_c, rate_ref, flow_ref, kept_buf, kept_copy,
                 along_ref, slope_ref, gb_ref, gc_ref, ga_ref, part_b, part_c, hook):
    rows, channels = step_ref.shape
    count = width // LANES
    span = kept_buf.shape[1] - 1
    blocks = rows // span
    ga_ref[...] = jnp.zeros_like(ga_ref)

    def time_body(order, unused):
        slot = lax.rem(order, 2)
        number = blocks - 1 - order
        kept_copy(number, slot).wait()
        part_b[...] = jnp.zeros_like(part_b)
        part_c[...] = jnp.zeros_like(part_c)

        def group_body(group, unused_inner):
            pieces = [lanes_of(group, width, k) for k in range(count)]
            rates = [rate_ref[:, lanes] for lanes in pieces]

            def block(index, carried):
                flows = list(carried[:count])
                sums = list(carried[count : 2 * count])
                current = list(carried[2 * count :])
                local = span - UNROLL - index * UNROLL
                base = number * span + local
                steps = [tile(step_ref, base, lanes) for lanes in pieces]
                pushes = [tile(push_ref, base, lanes) for lanes in pieces]
                grads = [tile(grad_ref, base, lanes) for lanes in pieces]
                alongs = [Tree(False) for k in range(count)]
                slopes = [Tree(False) for k in range(count)]
                for place in reversed(range(UNROLL)):
                    b_now = wide_b[base + place]
                    c_now = wide_c[base + place]
                    gb = gc = None
                    for k, lanes in enumerate(pieces):
                        prior = kept_buf[slot, local + place, :, lanes].astype(jnp.float32)
                        step = row(steps[k], place)
                        grad = row(grads[k], place)
                        decay = jnp.exp2(step * rates[k])
                        adjoint = c_now * grad + flows[k]
                        flows[k] = decay * adjoint
                        decay_grad = flows[k] * prior
                        alongs[k].push(place, adjoint * b_now)
                        slopes[k].push(place, decay_grad * rates[k])
                        sums[k] = sums[k] + decay_grad * step
                        here_b = adjoint * row(pushes[k], place)
                        here_c = current[k] * grad
                        gb = here_b if gb is None else gb + here_b
                        gc = here_c if gc is None else gc + here_c
                        current[k] = prior
                    part_b[local + place] += gb
                    part_c[local + place] += gc
                where = pl.ds(pl.multiple_of(base, UNROLL), UNROLL)
                for k, lanes in enumerate(pieces):
                    along_ref[where, lanes] = alongs[k].result
                    slope_ref[where, lanes] = slopes[k].result
                return tuple(flows + sums + current)

            carried = lax.fori_loop(
                0,
                span // UNROLL,
                block,
                tuple(flow_ref[:, lanes] for lanes in pieces)
                + tuple(ga_ref[:, lanes] for lanes in pieces)
                + tuple(kept_buf[slot, span, :, lanes].astype(jnp.float32) for lanes in pieces),
            )
            for k, lanes in enumerate(pieces):
                flow_ref[:, lanes] = carried[k]
                ga_ref[:, lanes] = carried[count + k]
            return unused_inner

        lax.fori_loop(0, channels // width, group_body, 0)
        gb_ref[number] = lane_sums(part_b)
        gc_ref[number] = lane_sums(part_c)

        @pl.when(order + 2 < blocks)
        def _():
            kept_copy(number - 2, slot).start()

        hook(order)
        return unused

    lax.fori_loop(0, blocks, time_body, 0)


def share(source, target, send_sems, recv_sems):
    blocks = lax.axis_size("ctx")
    here, line = lax.axis_index("ctx"), lax.axis_index("exp")
    copies = []
    for step in range(1, blocks):
        copies.append(
            pltpu.make_async_remote_copy(
                src_ref=source,
                dst_ref=target.at[here],
                send_sem=send_sems.at[step],
                recv_sem=recv_sems.at[step],
                device_id=(lax.rem(here + step, blocks), line),
                device_id_type=MESH,
            )
        )
        copies[-1].start()
    target[here] = source[...]
    return copies


def row_peers():
    blocks = lax.axis_size("ctx")
    here, line = lax.axis_index("ctx"), lax.axis_index("exp")
    return [(lax.rem(here + step, blocks), line) for step in range(1, blocks)]


def row_half(source, target, sems, place, k):
    size = source.shape[0] // 2
    return pltpu.make_async_remote_copy(
        src_ref=source.at[pl.ds(k * size, size)],
        dst_ref=target.at[pl.ds(k * size, size)],
        send_sem=sems.at[0, k],
        recv_sem=sems.at[1, k],
        device_id=partner(place),
        device_id_type=MESH,
    )


def front(loaded, loads, room, outs, scratch, saves):
    normed_ref, bt_ref, ct_ref, rate_ref, chan_ref, gain_ref, delta_ref, same_ref, target_ref = outs
    nx, ext, conv, xs, pre, step, push = scratch
    in_ref, prior_ref, prior_ids, ids_ref, routes_ref, conv_w, channel_ref, width_ref = loaded
    for load in loads[:5] + loads[6:]:
        load.wait()
    tokens, channels = xs.shape
    width = in_ref.shape[1]
    mine = lax.axis_index("ctx")
    gain_rows = jnp.concatenate(
        [width_ref[at : at + LANES, :].astype(jnp.float32).T for at in range(0, width, LANES)], axis=1
    )
    gain_ref[...] = gain_rows[:8]
    for at in range(0, channels, LANES):
        chan_ref[:, at : at + LANES] = channel_ref[at : at + LANES, LANES:].astype(jnp.float32).T[:32]
    rate_ref[...] = -jnp.exp(chan_ref[8 : 8 + NS, :]) * LOG2E
    gain = gain_ref[0:1, :]

    def normed(values):
        x = values.astype(jnp.float32)
        return (x * lax.rsqrt(jnp.mean(x * x, axis=-1, keepdims=True) + EPS) * gain).astype(jnp.bfloat16)

    nx[:EDGE, :] = normed(prior_ref[...])

    def norm_rows(index, unused):
        at = pl.ds(pl.multiple_of(index * 16, 16), 16)
        value = normed(in_ref[at, :])
        normed_ref[at, :] = value
        nx[pl.ds(pl.multiple_of(EDGE + index * 16, 16), 16), :] = value
        return unused

    lax.fori_loop(0, tokens // 16, norm_rows, 0)
    def column(values):
        return jnp.broadcast_to(values.astype(jnp.float32), (LANES, LANES)).T

    def columns(ref):
        return jnp.concatenate([column(ref[:, at : at + LANES]) for at in range(0, tokens, LANES)], axis=0)

    ids = jnp.where(mine > 0, column(prior_ids[...])[LANES - EDGE :], -1.0)
    own_ids = columns(ids_ref)
    every_id = jnp.concatenate([ids, own_ids], axis=0)
    for j in range(1, KC):
        same_ref[j - 1] = (pltpu.roll(every_id, j, 0)[EDGE:] == own_ids).astype(jnp.float32)
    routes = columns(routes_ref)
    chosen = (routes == lax.broadcasted_iota(jnp.int32, routes.shape, 1).astype(jnp.float32)).astype(jnp.float32)
    square = (tokens, tokens)
    until = lax.broadcasted_iota(jnp.int32, square, 0) >= lax.broadcasted_iota(jnp.int32, square, 1)
    running = dot(until.astype(jnp.float32).astype(jnp.bfloat16), chosen.astype(jnp.bfloat16))
    slot = jnp.sum(running * chosen, axis=1, keepdims=True) - 1.0
    target_ref[...] = routes * room + slot
    piece = 2 * LANES
    loads[5].wait()

    def conv_piece(index, unused):
        lanes = pl.ds(pl.multiple_of(index * piece, piece), piece)
        low = dot(nx[...], conv_w[:, lanes]).astype(jnp.bfloat16)
        ext[:, lanes] = low
        value = low.astype(jnp.float32)
        out = chan_ref[24:25, lanes] + chan_ref[3:4, lanes] * value[EDGE:]
        for j in range(1, KC):
            same = jnp.concatenate([same_ref[j - 1]] * 2, axis=1)
            out = out + chan_ref[3 - j : 4 - j, lanes] * pltpu.roll(value, j, 0)[EDGE:] * same
        conv[:, lanes] = out
        xs[:, lanes] = (out / (1.0 + jnp.exp(-out))).astype(jnp.bfloat16)
        return unused

    lax.fori_loop(0, channels // piece, conv_piece, 0)
    for save in saves[:3]:
        save.start()
    projected = dot(xs[...], channel_ref[:, :LANES])
    lane = lax.broadcasted_iota(jnp.int32, projected.shape, 1)
    delta_ref[...] = jnp.where(lane >= R + 2 * NS, pltpu.roll(projected, R + 2 * NS, 1), 0.0).astype(jnp.bfloat16)
    for at in range(0, tokens, LANES):
        block = projected[at : at + LANES].T
        bt_ref[:, at : at + LANES] = block[R : R + NS]
        ct_ref[:, at : at + LANES] = block[R + NS : R + 2 * NS]

    def step_piece(index, unused):
        lanes = pl.ds(pl.multiple_of(index * piece, piece), piece)
        value = contract(delta_ref[...], channel_ref[lanes, :LANES], 1, 1) + chan_ref[25:26, lanes]
        pre[:, lanes] = value
        size = jnp.maximum(value, 0.0) + jnp.log1p(jnp.exp(-jnp.abs(value)))
        push[:, lanes] = size * xs[:, lanes].astype(jnp.float32)
        keep = jnp.concatenate([same_ref[0]] * 2, axis=1)
        step[:, lanes] = jnp.where(keep > 0, size, 1e30)
        return unused

    lax.fori_loop(0, channels // piece, step_piece, 0)
    for save in saves[3:]:
        save.start()


def forward_kernel(places, streams, width, room, *refs):
    weights_from = refs[:8]
    shards, leaving = refs[8:10], refs[10]
    y_ref, product_ref = refs[12:14]
    front_outs = refs[14:23]
    kept_ref = refs[23]
    saved = refs[24:30]
    wholes, arriving = refs[30:32], refs[32]
    scratch = refs[33:40]
    weights = refs[40:48]
    (wide_b, wide_c, kept_buf, first_buf, state_ref, message, products, ends,
     load_sems, kept_sems, first_sem, share_sems, save_sems, moved_sems, send_sems, recv_sems, local_sems) = refs[48:]
    loads = [pltpu.make_async_copy(weights_from[k], weights[k], load_sems.at[k]) for k in range(8)]
    for load in loads[:5] + loads[:4:-1]:
        load.start()
    bt_ref, ct_ref, rate_ref = front_outs[1:4]
    step_ref, push_ref = scratch[5:7]
    blocks = lax.axis_size("ctx")
    position = lax.axis_index("ctx")
    span = kept_buf.shape[1]
    flow = GatherFlow(places, streams, range(len(places)), shards, wholes, send_sems, recv_sems, local_sems)
    meet([place for place in places if place[0] == "exp"], *row_peers())
    flow.start()
    move = row_half(leaving, arriving, moved_sems, ("ctx", blocks.bit_length() - 2), 1)
    move.start()
    saves = [
        pltpu.make_async_copy(scratch[k + 1], saved[k], save_sems.at[k]) for k in range(6)
    ]
    front(weights, loads, room, front_outs, scratch, saves)

    message[0] = jnp.exp2(jnp.sum(step_ref[...], axis=0, keepdims=True) * rate_ref[...]).astype(jnp.bfloat16)
    early = share(message.at[0], products, share_sems.at[0], share_sems.at[1])
    spread_columns(bt_ref, wide_b)
    spread_columns(ct_ref, wide_c)
    end_pass(width, step_ref, push_ref, wide_b, rate_ref, state_ref, lambda group: None)
    message[1] = state_ref[...].astype(jnp.bfloat16)
    late = share(message.at[1], ends, share_sems.at[2], share_sems.at[3])
    flow.advance(0)
    for copy in early + late:
        copy.wait_recv()
    start = jnp.zeros(state_ref.shape, jnp.float32)
    for index in range(blocks):
        folded = products[index].astype(jnp.float32) * start + ends[index].astype(jnp.float32)
        start = jnp.where(index < position, folded, start)
    state_ref[...] = start
    product_ref[...] = products[...]
    first_buf[0] = start.astype(jnp.bfloat16)
    first_copy = pltpu.make_async_copy(first_buf, kept_ref.at[pl.ds(0, 1)], first_sem)
    first_copy.start()

    def kept_copy(number, slot):
        return pltpu.make_async_copy(
            kept_buf.at[slot], kept_ref.at[pl.ds(1 + number * span, span)], kept_sems.at[slot]
        )

    def hook(number):
        @pl.when(number == 3)
        def _():
            flow.advance(1)

    out_pass(width, step_ref, push_ref, wide_b, wide_c, rate_ref, state_ref, y_ref, kept_buf, kept_copy, hook)
    for stage in range(2, max(flow.stages(number) for number in range(len(streams)))):
        flow.advance(stage)
    flow.finish()
    first_copy.wait()
    for save in saves:
        save.wait()
    for copy in early + late:
        copy.wait_send()
    move.wait()


def scan_forward(sizes, rows_in, prior, ids, weights, room, shards, leaving, begun, identity, span=64):
    places = bit_positions(sizes)
    stages = len(places)
    begin = len(far_of(places))
    streams = halves(shards, *gather_orders(places), begin=begin)
    tokens, width = rows_in.shape
    channels = weights[0].shape[1]
    blocks = sizes[0][1]
    inside = pl.BlockSpec(memory_space=pltpu.VMEM)
    anywhere = pl.BlockSpec(memory_space=pl.ANY)
    half, full = jnp.bfloat16, jnp.float32
    shape = jax.ShapeDtypeStruct
    saved = [
        shape((EDGE + tokens, channels), half),
        shape((tokens, channels), full),
        shape((tokens, channels), half),
        shape((tokens, channels), full),
        shape((tokens, channels), full),
        shape((tokens, channels), full),
    ]
    y, products, normed, bt, ct, rates, chan, gains, delta, same, target, kept, *rest = pl.pallas_call(
        functools.partial(forward_kernel, places, streams, pick(channels), room),
        in_specs=[anywhere] * 12,
        input_output_aliases={11: 20},
        out_specs=[inside] * 11 + [anywhere] * 10,
        out_shape=[
            shape((tokens, channels), full),
            shape((blocks, NS, channels), half),
            shape((tokens, width), half),
            shape((NS, tokens), full),
            shape((NS, tokens), full),
            shape((NS, channels), full),
            shape((32, channels), full),
            shape((8, width), full),
            shape((tokens, LANES), half),
            shape((KC - 1, tokens, LANES), full),
            shape((tokens, LANES), full),
            shape((tokens + 1, NS, channels), half),
        ]
        + saved
        + [shape((2,) * stages + shard.shape[begin:], shard.dtype) for shard in shards]
        + [shape(leaving.shape, leaving.dtype)],
        scratch_shapes=[pltpu.VMEM((EDGE + tokens, width), half)]
        + [pltpu.VMEM(value.shape, value.dtype) for value in saved]
        + [pltpu.VMEM(value.shape, value.dtype) for value in [rows_in, *prior, *ids, *weights]]
        + [
            pltpu.VMEM((tokens, NS, LANES), full),
            pltpu.VMEM((tokens, NS, LANES), full),
            pltpu.VMEM((2, span, NS, channels), half),
            pltpu.VMEM((1, NS, channels), half),
            pltpu.VMEM((NS, channels), full),
            pltpu.VMEM((2, NS, channels), half),
            pltpu.VMEM((blocks, NS, channels), half),
            pltpu.VMEM((blocks, NS, channels), half),
            pltpu.SemaphoreType.DMA((8,)),
            pltpu.SemaphoreType.DMA((2,)),
            pltpu.SemaphoreType.DMA,
            pltpu.SemaphoreType.DMA((4, blocks)),
            pltpu.SemaphoreType.DMA((6,)),
            pltpu.SemaphoreType.DMA((2, 2)),
            pltpu.SemaphoreType.DMA((len(streams), stages)),
            pltpu.SemaphoreType.DMA((len(streams), stages)),
            pltpu.SemaphoreType.DMA((len(streams),)),
        ],
        compiler_params=pltpu.CompilerParams(
            collective_id=identity, has_side_effects=True, vmem_limit_bytes=63 * 1024 * 1024
        ),
        cost_estimate=cost(tokens, channels, 9),
        name="scan_forward",
    )(rows_in, *prior, *ids, *weights, *shards, leaving, begun)
    saved, wholes, arrived = rest[:6], rest[6:8], rest[8]
    wholes = [whole.reshape((-1,) + whole.shape[stages + 1 :]) for whole in wholes]
    return y, products, normed, bt, ct, rates, chan, gains, delta, same, target, kept, saved, wholes, arrived


def backward_kernel(places, streams, marks, width, *refs):
    bt_ref, ct_ref, rate_ref, product_ref = refs[:4]
    parts = refs[4:6]
    streamed = refs[6:9]
    kept_ref, leaving = refs[9:11]
    outs = refs[11:]
    gb_ref, gc_ref, ga_ref = outs[:3]
    totals, arriving = outs[3:5], outs[5]
    rows_out = outs[6:8]
    scratch = outs[8:]
    landing = scratch[:marks]
    (step_ref, push_ref, grad_ref, along_ref, slope_ref, wide_b, wide_c, part_b, part_c, kept_buf, flow_ref, message,
     inflows, load_sems, push_sem, out_sems, kept_sems, share_sems, moved_sems, send_sems, recv_sems) = scratch[marks:]
    blocks = lax.axis_size("ctx")
    position = lax.axis_index("ctx")
    span = kept_buf.shape[1] - 1
    steps = step_ref.shape[0] // span

    def load(group, k):
        lanes = pl.ds(pl.multiple_of(group * width, LANES), width)
        source, target = ((streamed[0], step_ref), (streamed[2], grad_ref))[k]
        return pltpu.make_async_copy(source.at[:, lanes], target.at[:, lanes], load_sems.at[k, group])

    for group in range(step_ref.shape[1] // width):
        for k in range(2):
            load(group, k).start()
    push_load = pltpu.make_async_copy(streamed[1], push_ref, push_sem)
    push_load.start()

    def ready(group):
        for k in range(2):
            load(group, k).wait()

    def rows_copy(number, k):
        rows = pl.ds(number * span, span)
        return pltpu.make_async_copy((along_ref, slope_ref)[k].at[rows], rows_out[k].at[rows], out_sems.at[k, number])

    flow = ReduceFlow(places, streams, range(len(places)), parts, totals, landing, send_sems, recv_sems)

    def kept_copy(number, slot):
        return pltpu.make_async_copy(
            kept_ref.at[pl.ds(number * span, span + 1)], kept_buf.at[slot], kept_sems.at[slot]
        )

    for order in range(min(2, steps)):
        kept_copy(steps - 1 - order, order).start()
    meet([place for place in places if place[0] == "exp"], *row_peers())
    flow.start()
    move = row_half(leaving, arriving, moved_sems, ("ctx", blocks.bit_length() - 2), 0)
    move.start()
    spread_columns(bt_ref, wide_b)
    spread_columns(ct_ref, wide_c)
    inflow_pass(width, step_ref, grad_ref, wide_c, rate_ref, flow_ref, ready)
    message[...] = flow_ref[...].astype(jnp.bfloat16)
    copies = share(message, inflows, share_sems.at[0], share_sems.at[1])
    for copy in copies:
        copy.wait_recv()
    end = jnp.zeros(flow_ref.shape, jnp.float32)
    for index in reversed(range(blocks)):
        folded = inflows[index].astype(jnp.float32) + product_ref[index].astype(jnp.float32) * end
        end = jnp.where(index > position, folded, end)
    flow_ref[...] = end
    flow.advance(0)
    push_load.wait()

    def hook(order):
        for k in range(2):
            rows_copy(steps - 1 - order, k).start()

        @pl.when(order == 2)
        def _():
            flow.advance(1)

        @pl.when(order == 4)
        def _():
            flow.advance(2)

    adjoint_pass(width, step_ref, push_ref, grad_ref, wide_b, wide_c, rate_ref, flow_ref, kept_buf, kept_copy,
                 along_ref, slope_ref, gb_ref, gc_ref, ga_ref, part_b, part_c, hook)
    for stage in range(3, len(streams[0][2])):
        flow.advance(stage)
    flow.finish()
    for copy in copies:
        copy.wait_send()
    move.wait()
    for number in range(steps):
        for k in range(2):
            rows_copy(number, k).wait()


def scan_backward(sizes, step, push, grad, b_turned, c_turned, rates, products, parts, kept, leaving, identity, span=64):
    places = bit_positions(sizes)
    stages = len(places)
    far = sorted(far_of(places))
    streams = halves(parts, *[tuple(order[: stages - len(far)]) for order in orders_of(places)])
    divided = [part.reshape((2,) * stages + (-1, part.shape[1])) for part in parts]
    tokens, channels = step.shape
    blocks = sizes[0][1]
    inside = pl.BlockSpec(memory_space=pltpu.VMEM)
    anywhere = pl.BlockSpec(memory_space=pl.ANY)
    half = jnp.bfloat16
    landing = landing_of(streams, range(stages), divided)
    row_sums = jax.ShapeDtypeStruct((tokens // span, UNROLL, span * NS), jnp.float32)
    out = pl.pallas_call(
        functools.partial(backward_kernel, places, streams, len(landing), pick(channels)),
        in_specs=[inside] * 6 + [anywhere] * 5,
        out_specs=[inside] * 5 + [anywhere] * 3,
        out_shape=[row_sums, row_sums, jax.ShapeDtypeStruct((NS, channels), jnp.float32)]
        + [jax.ShapeDtypeStruct((2,) * len(far) + block.shape[-2:], half) for block in divided]
        + [jax.ShapeDtypeStruct(leaving.shape, leaving.dtype)]
        + [jax.ShapeDtypeStruct((tokens, channels), jnp.float32)] * 2,
        scratch_shapes=landing
        + [pltpu.VMEM((tokens, channels), jnp.float32)] * 5
        + [
            pltpu.VMEM((tokens, NS, LANES), jnp.float32),
            pltpu.VMEM((tokens, NS, LANES), jnp.float32),
            pltpu.VMEM((span, NS, LANES), jnp.float32),
            pltpu.VMEM((span, NS, LANES), jnp.float32),
            pltpu.VMEM((2, span + 1, NS, channels), half),
            pltpu.VMEM((NS, channels), jnp.float32),
            pltpu.VMEM((NS, channels), half),
            pltpu.VMEM((blocks, NS, channels), half),
            pltpu.SemaphoreType.DMA((2, channels // pick(channels))),
            pltpu.SemaphoreType.DMA,
            pltpu.SemaphoreType.DMA((2, tokens // span)),
            pltpu.SemaphoreType.DMA((2,)),
            pltpu.SemaphoreType.DMA((2, blocks)),
            pltpu.SemaphoreType.DMA((2, 2)),
        ]
        + flights(streams),
        compiler_params=pltpu.CompilerParams(
            collective_id=identity, has_side_effects=True, vmem_limit_bytes=63 * 1024 * 1024
        ),
        cost_estimate=cost(tokens, channels, 15),
        name="scan_backward",
    )(b_turned, c_turned, rates, products, *divided, step, push, grad, kept, leaving)
    wide_b, wide_c, grad_a, first, second, arrived, along, slope = out
    grad_bs, grad_cs = [values[:, 0].reshape(tokens, NS) for values in (wide_b, wide_c)]
    return along, slope, grad_bs, grad_cs, grad_a, (first, second), arrived


class PackedReduce(ReduceFlow):
    def __init__(self, places, streams, heads, parts, totals, landing, blocks, send_sems, recv_sems):
        super().__init__(places, streams, range(len(places)), parts, totals, landing, send_sems, recv_sems)
        self.heads, self.blocks = heads, blocks

    def side(self, number, stage, value):
        array, cols, order = self.streams[number]
        if stage == 0:
            index = tuple(value if p == order[0] else slice(None) for p in range(self.heads))
            return self.parts[array].at[index + (slice(None), cols)]
        left = [p for p in self.dims if p not in order[:stage]]
        index = tuple(value if p == order[stage] else slice(None) for p in left)
        held = self.blocks[number] if stage == 1 else self.spot(number, stage - 1)
        return held.at[index]

    def advance(self, stage):
        if stage:
            super().advance(stage)
            return
        for number, (array, cols, order) in enumerate(self.streams):
            self.flight(number, 0).wait_recv()
            mine = self.side(number, 0, self.bits[order[0]])
            there, held = self.spot(number, 0), self.blocks[number]
            tails = len(self.places) - self.heads
            size = held.shape[-2]

            def add(index, unused, mine=mine, there=there, held=held, tails=tails, size=size):
                at = tuple(lax.rem(index // 2 ** (self.heads - 2 - k), 2) for k in range(self.heads - 1))
                value = there[at].astype(jnp.float32) + mine[at].astype(jnp.float32)
                for block in range(2**tails):
                    spot = tuple(block // 2 ** (tails - 1 - k) % 2 for k in range(tails))
                    held[at + spot] = value[block * size : (block + 1) * size].astype(held.dtype)
                return unused

            lax.fori_loop(0, 2 ** (self.heads - 1), add, 0)
            self.flight(number, 1).start()


def turned(values):
    return jnp.concatenate([values[:, at : at + LANES].T for at in range(0, values.shape[1], LANES)], axis=0)


def finish_kernel(places, streams, third, late, far, marks, *refs):
    leaving = refs[23:25]
    refs = refs[:23] + refs[27:]
    (along_h, slope_h, grad_h, pre_h, conv_h, xs_h, ext_h, gz_h, wc_h, wg_h) = refs[:10]
    (normed_ref, in_ref, resid_ref, mix_ref, bc_ref, delta_ref, same_ref, chan_ref, decay_ref, rate_ref, wide_ref) = refs[10:21]
    rest_parts = refs[21:23]
    gi_ref, own_in, own_out, tot_small, tot_wide = refs[23:28]
    arriving, scratch = refs[28:30], refs[30:]
    landing, scratch = scratch[: marks[0]], scratch[marks[0] :]
    blocks, scratch = scratch[: marks[1]], scratch[marks[1] :]
    landing3, scratch = scratch[: marks[2]], scratch[marks[2] :]
    blocks3, scratch = scratch[: marks[3]], scratch[marks[3] :]
    late_landing, scratch = scratch[: marks[4]], scratch[marks[4] :]
    (along, slope, grad, pre, conv, xs, ext, gz, wc, wg, gdt, gci, last, spill, arrived, sums, rows_s, wide_s, gn,
     part_conv, part_small, part_wide,
     block_sems, whole_sems, spill_sems, moved_sems, send_sems, recv_sems, send3, recv3, late_send, late_recv) = scratch
    tokens, channels = xs.shape
    own_conv, own_gate = own_in.at[:, :channels], own_in.at[:, channels:]
    span = tokens // block_sems.shape[1]
    heads = len([place for place in places if place[0] == "ctx"])
    flow = PackedReduce(
        places, streams, heads, (part_conv, part_small), (own_conv, tot_small), landing, blocks, send_sems, recv_sems
    )
    flow3 = PackedReduce(places, third, heads, (part_wide,), (tot_wide,), landing3, blocks3, send3, recv3)
    rest = ReduceFlow(places, late, far, rest_parts, (own_gate, own_out), late_landing, late_send, late_recv)

    streamed = ((along_h, along), (slope_h, slope), (grad_h, grad), (pre_h, pre), (xs_h, xs))

    def block_copy(k, number):
        rows = pl.ds(number * span, span)
        source, target = streamed[k]
        return pltpu.make_async_copy(source.at[rows], target.at[rows], block_sems.at[k, number])

    for number in range(tokens // span):
        for k in range(len(streamed)):
            block_copy(k, number).start()
    wholes = [
        pltpu.make_async_copy(source, target, whole_sems.at[k])
        for k, (source, target) in enumerate(((conv_h, conv), (ext_h, ext), (gz_h, gz), (wc_h, wc), (wg_h, wg)))
    ]
    for copy in wholes:
        copy.start()
    count = lax.axis_size("ctx")
    here, line = lax.axis_index("ctx"), lax.axis_index("exp")
    before = (lax.rem(here + count - 1, count), line)
    meet(places, before, (lax.rem(here + 1, count), line))
    rest.start()
    moves = [
        row_half(leaving[k], arriving[k], moved_sems.at[k], ("ctx", count.bit_length() - 2), 1) for k in range(2)
    ]
    moves[0].start()

    sums[...] = jnp.zeros_like(sums)
    rows_s[...] = jnp.zeros_like(rows_s)

    def first_block(number, unused):
        for k in range(len(streamed)):
            block_copy(k, number).wait()

        def some(index, unused_inner):
            at = pl.ds(pl.multiple_of(number * span + index * 16, 16), 16)
            for low in range(0, channels, LANES):
                lanes = slice(low, low + LANES)
                a, g, x, p = along[at, lanes], grad[at, lanes], xs[at, lanes].astype(jnp.float32), pre[at, lanes]
                small = jnp.exp(-jnp.abs(p))
                gated = jnp.where(p >= 0, 1.0, small) / (1.0 + small)
                step = jnp.maximum(p, 0.0) + jnp.log1p(small)
                value = (a * x + slope[at, lanes] * (1.0 / LOG2E)) * gated
                gdt[at, lanes] = value.astype(jnp.bfloat16)
                sums[0, :, lanes] += value[:8] + value[8:]
                both = g * x
                sums[1, :, lanes] += both[:8] + both[8:]
                along[at, lanes] = chan_ref[26:27, lanes] * g + a * step
            return unused_inner

        lax.fori_loop(0, span // 16, some, 0)
        return unused

    lax.fori_loop(0, tokens // span, first_block, 0)
    rows_s[25:26, :] = jnp.sum(sums[0], axis=0, keepdims=True)
    rows_s[26:27, :] = jnp.sum(sums[1], axis=0, keepdims=True)
    rows_s[8:24, :] = decay_ref[...] * rate_ref[...] * (1.0 / LOG2E)

    lane = lax.broadcasted_iota(jnp.int32, (tokens, LANES), 1)
    mixed = pltpu.roll(dot(gdt[...], mix_ref[:, :LANES]), R, 1)
    projected = jnp.where(lane < R, mixed, jnp.where(lane < R + 2 * NS, bc_ref[...], 0.0)).astype(jnp.bfloat16)
    wholes[0].wait()
    wholes[1].wait()
    piece = 2 * LANES
    tail_row = lax.broadcasted_iota(jnp.int32, (tokens, piece), 0)

    def conv_piece(index, unused):
        lanes = pl.ds(pl.multiple_of(index * piece, piece), piece)
        some = pl.ds(pl.multiple_of(index * piece, piece), piece)
        total = along[:, lanes] + contract(projected, mix_ref[some, :LANES], 1, 1)
        value = conv[:, lanes]
        gate = 1.0 / (1.0 + jnp.exp(-value))
        out = total * gate * (1.0 + value * (1.0 - gate))
        rows_s[24:25, lanes] = jnp.sum(out, axis=0, keepdims=True)
        before_rows = ext[:, lanes].astype(jnp.float32)
        rows_s[3:4, lanes] = jnp.sum(out * before_rows[EDGE:], axis=0, keepdims=True)
        result = chan_ref[3:4, lanes] * out
        beyond = jnp.zeros((8, piece), jnp.float32)
        for j in range(1, KC):
            same = jnp.concatenate([same_ref[j - 1]] * 2, axis=1)
            masked = out * same
            shifted_rows = pltpu.roll(before_rows, j, 0)[EDGE:]
            rows_s[3 - j : 4 - j, lanes] = jnp.sum(masked * shifted_rows, axis=0, keepdims=True)
            moved = chan_ref[3 - j : 4 - j, lanes] * pltpu.roll(masked, tokens - j, 0)
            result = result + jnp.where(tail_row < tokens - j, moved, 0.0)
            beyond = beyond + jnp.where(tail_row < tokens - j, 0.0, moved)[tokens - 8 :]
        gci[:, lanes] = result.astype(jnp.bfloat16)
        last[:, lanes] = result[tokens - 16 :]
        spill[:, lanes] = beyond
        return unused

    lax.fori_loop(0, channels // piece, conv_piece, 0)
    handed = pltpu.make_async_remote_copy(
        src_ref=spill,
        dst_ref=arrived,
        send_sem=spill_sems.at[0],
        recv_sem=spill_sems.at[1],
        device_id=before,
        device_id_type=MESH,
    )
    handed.start()

    cut = part_small.shape[-2]
    first_rows = contract(projected, xs[...], 0, 0) + contract(delta_ref[...], gdt[...], 0, 0)
    filler = jnp.zeros((LANES - rows_s.shape[0], channels), jnp.float32)
    for k, values in enumerate((first_rows, jnp.concatenate([rows_s[...], filler], axis=0))):
        columns = turned(values)
        for index in range(channels // cut):
            spot = tuple(index // 2 ** (heads - 1 - j) % 2 for j in range(heads))
            part_small[spot + (slice(None), slice(k * LANES, (k + 1) * LANES))] = columns[
                index * cut : (index + 1) * cut
            ].astype(jnp.bfloat16)
    handed.wait_recv()
    closing = last[...] + jnp.concatenate([jnp.zeros((8, channels), jnp.float32), arrived[...]], axis=0)
    gci[tokens - 16 :, :] = closing.astype(jnp.bfloat16)

    long = part_conv.shape[-2]

    def product_piece(index, unused):
        lanes = pl.ds(pl.multiple_of(index * piece, piece), piece)
        value = dot(normed_ref[...], gci[:, lanes])
        for block in range(value.shape[0] // long):
            spot = tuple(block // 2 ** (heads - 1 - k) % 2 for k in range(heads))
            part_conv[spot + (slice(None), lanes)] = value[block * long : (block + 1) * long].astype(jnp.bfloat16)
        return unused

    lax.fori_loop(0, channels // piece, product_piece, 0)
    flow.start()

    for copy in wholes[2:]:
        copy.wait()
    width = gn.shape[1]

    def normed_piece(index, unused):
        lanes = pl.ds(pl.multiple_of(index * piece, piece), piece)
        gn[:, lanes] = contract(gci[...], wc[lanes, :], 1, 1) + contract(gz[...], wg[lanes, :], 1, 1)
        return unused

    lax.fori_loop(0, width // piece, normed_piece, 0)
    wide_s[...] = wide_ref[...]
    gain = wide_ref[0:1, :]

    def back(index, total):
        at = pl.ds(pl.multiple_of(index * 16, 16), 16)
        x, g = in_ref[at, :].astype(jnp.float32), gn[at, :]
        scale = lax.rsqrt(jnp.mean(x * x, axis=-1, keepdims=True) + EPS)
        scaled = g * gain
        share_of = jnp.mean(x * scaled, axis=-1, keepdims=True)
        gi_ref[at, :] = resid_ref[at, :] + scale * scaled - x * (scale * scale * scale * share_of)
        value = g * (x * scale)
        return total + value[:8] + value[8:]

    total = lax.fori_loop(0, tokens // 16, back, jnp.zeros((8, width), jnp.float32))
    wide_s[0:1, :] = jnp.sum(total, axis=0, keepdims=True)
    flow.advance(0)
    filler = jnp.zeros((LANES - wide_s.shape[0], width), jnp.float32)
    columns = turned(jnp.concatenate([wide_s[...], filler], axis=0))
    short = part_wide.shape[-2]
    for block in range(width // short):
        spot = tuple(block // 2 ** (heads - 1 - k) % 2 for k in range(heads))
        part_wide[spot] = columns[block * short : (block + 1) * short].astype(jnp.bfloat16)
    flow3.start()
    rest.advance(0)
    for stage in range(1, len(places)):
        flow.advance(stage)
        flow3.advance(stage - 1)
        rest.advance(stage)
        if stage == 2:
            moves[1].start()
    flow3.advance(len(places) - 1)

    flow.finish()
    flow3.finish()
    rest.finish()
    handed.wait_send()
    for move in moves:
        move.wait()


def finish(sizes, streamed, inside_values, parts, leaving, arrived, identity, span=64):
    places = bit_positions(sizes)
    stages = len(places)
    far = sorted(far_of(places))
    heads = sizes[0][1].bit_length() - 1
    tails = stages - heads
    along, slope, grad, pre, conv, xs, ext, gz, wc, wg = streamed
    normed = inside_values[1]
    tokens, channels = xs.shape
    width = normed.shape[1]
    devices = 2**stages
    half, wide = jnp.bfloat16, jnp.float32
    rows, thin = channels // devices, width // devices
    orders = [tuple(order) for order in orders_of(places)]
    conv_like = jax.ShapeDtypeStruct((width, channels), half)
    small_like = jax.ShapeDtypeStruct((channels, 2 * LANES), half)
    wide_like = jax.ShapeDtypeStruct((width, LANES), half)
    streams = halves((conv_like, small_like), *orders)
    third = halves((wide_like,), *orders)
    late = [(k, slice(0, part.shape[-1]), tuple(far_of(places))) for k, part in enumerate(parts)]

    def room(of, sizes_of):
        landing, blocks = [], []
        for array, cols, order in of:
            size, many = sizes_of[array], cols.stop - cols.start
            landing.append(pltpu.VMEM((2,) * (heads - 1) + (size * 2**tails, many), half))
            landing += [pltpu.VMEM((2,) * (stages - stage - 1) + (size, many), half) for stage in range(1, stages)]
            blocks.append(pltpu.VMEM((2,) * (stages - 1) + (size, many), half))
        return landing, blocks

    landing, blocks = room(streams, (thin, rows))
    landing3, blocks3 = room(third, (thin,))
    late_landing = landing_of(late, far, parts)
    marks = [len(landing), len(blocks), len(landing3), len(blocks3), len(late_landing)]
    inside = pl.BlockSpec(memory_space=pltpu.VMEM)
    anywhere = pl.BlockSpec(memory_space=pl.ANY)
    return pl.pallas_call(
        functools.partial(finish_kernel, places, streams, third, late, far, marks),
        in_specs=[anywhere] * 10 + [inside] * (len(inside_values) + 2) + [anywhere] * 4,
        input_output_aliases={25: 5, 26: 6},
        out_specs=[inside] * 5 + [anywhere] * 2,
        out_shape=[
            jax.ShapeDtypeStruct(normed.shape, wide),
            jax.ShapeDtypeStruct((thin, 2 * channels), wide),
            jax.ShapeDtypeStruct(parts[1].shape[-2:], wide),
            jax.ShapeDtypeStruct((rows, 2 * LANES), wide),
            jax.ShapeDtypeStruct((thin, LANES), wide),
        ]
        + [jax.ShapeDtypeStruct(values.shape, half) for values in leaving],
        scratch_shapes=landing + blocks + landing3 + blocks3 + late_landing
        + [pltpu.VMEM(value.shape, value.dtype) for value in streamed]
        + [
            pltpu.VMEM((tokens, channels), half),
            pltpu.VMEM((tokens, channels), half),
            pltpu.VMEM((16, channels), wide),
            pltpu.VMEM((8, channels), wide),
            pltpu.VMEM((8, channels), wide),
            pltpu.VMEM((2, 8, channels), wide),
            pltpu.VMEM((32, channels), wide),
            pltpu.VMEM(inside_values[-1].shape, wide),
            pltpu.VMEM((tokens, width), wide),
            pltpu.VMEM((2,) * heads + (thin * 2**tails, channels), half),
            pltpu.VMEM((2,) * heads + (rows * 2**tails, 2 * LANES), half),
            pltpu.VMEM((2,) * heads + (thin * 2**tails, LANES), half),
            pltpu.SemaphoreType.DMA((5, tokens // span)),
            pltpu.SemaphoreType.DMA((5,)),
            pltpu.SemaphoreType.DMA((2,)),
            pltpu.SemaphoreType.DMA((2, 2, 2)),
        ]
        + flights(streams)
        + flights(third)
        + flights(late),
        compiler_params=pltpu.CompilerParams(
            collective_id=identity, has_side_effects=True, vmem_limit_bytes=63 * 1024 * 1024
        ),
        name="finish",
    )(*streamed, *inside_values, *parts, *leaving, *arrived)


def chosen_of(target, room):
    lane = lax.broadcasted_iota(jnp.int32, target.shape, 1).astype(jnp.float32) * room
    return ((target >= lane) & (target < lane + room)).astype(jnp.float32)


def gate_kernel(room, experts, y_ref, xs_ref, normed_ref, in_ref, cot_ref, target_ref, wg_ref, wo_ref, wide_ref, chan_ref,
                gain_ref, n2_ref, resid_ref, z_ref, prob_ref, pick_ref, gated_t, normed_t):
    skip, gain = chan_ref[26:27, :], gain_ref[1:2, :]
    gate_in = dot(normed_ref[...], wg_ref[...])
    z_ref[...] = gate_in
    scanned = y_ref[...] + skip * xs_ref[...].astype(jnp.float32)
    gated = scanned * gate_in / (1.0 + jnp.exp(-gate_in))
    for at in range(0, gated.shape[1], LANES):
        gated_t[at : at + LANES, :] = gated[:, at : at + LANES].T.astype(jnp.bfloat16)
    for at in range(0, normed_ref.shape[1], LANES):
        normed_t[at : at + LANES, :] = normed_ref[:, at : at + LANES].astype(jnp.float32).T.astype(jnp.bfloat16)
    residual = in_ref[...].astype(jnp.float32) + dot(gated.astype(jnp.bfloat16), wo_ref[...])
    resid_ref[...] = residual
    scale = lax.rsqrt(jnp.mean(residual * residual, axis=-1, keepdims=True) + EPS)
    normed_two = (residual * scale * gain).astype(jnp.bfloat16)
    n2_ref[...] = normed_two
    logits = pltpu.roll(dot(normed_two, wide_ref[...]), LANES - 8, 1)
    lane = lax.broadcasted_iota(jnp.int32, logits.shape, 1)
    logits = jnp.where(lane < experts, logits, -1e30)
    powers = jnp.exp(logits - jnp.max(logits, axis=1, keepdims=True))
    powers = jnp.where(lane < experts, powers, 0.0)
    probability = powers / jnp.sum(powers, axis=1, keepdims=True)
    prob_ref[...] = probability
    gate = jnp.sum(probability * chosen_of(target_ref[...], room), axis=1, keepdims=True)
    pick_ref[...] = (cot_ref[...].astype(jnp.float32) * gate).astype(jnp.bfloat16)


def open_gate(y, xs, normed, rows_in, cotangent, target, weights, room, experts, block=3 * LANES):
    tokens, channels = y.shape
    width = rows_in.shape[1]
    shape, half, full = jax.ShapeDtypeStruct, jnp.bfloat16, jnp.float32

    def cut(values):
        return pl.BlockSpec((block, values.shape[1]), lambda i: (i, 0))

    def whole(values):
        return pl.BlockSpec(values.shape, lambda i: (0, 0))

    results = [
        shape((tokens, width), half),
        shape((tokens, width), full),
        shape((tokens, channels), full),
        shape((tokens, LANES), full),
        shape((tokens, width), half),
    ]
    turned_specs = [pl.BlockSpec((rows, block), lambda i: (0, i)) for rows in (channels, width)]
    return pl.pallas_call(
        functools.partial(gate_kernel, room, experts),
        grid=(tokens // block,),
        in_specs=[cut(values) for values in (y, xs, normed, rows_in, cotangent, target)]
        + [whole(values) for values in weights],
        out_specs=[cut(values) for values in results] + turned_specs,
        out_shape=results + [shape((channels, tokens), half), shape((width, tokens), half)],
        compiler_params=pltpu.CompilerParams(vmem_limit_bytes=63 * 1024 * 1024),
        name="open_gate",
    )(y, xs, normed, rows_in, cotangent, target, *weights)


def middle_kernel(room, picked_ref, back_ref, cot_ref, resid_ref, z_ref, y_ref, xs_ref, n2_ref, prob_ref, target_ref,
                  gated_t, normed_t, wo_ref, wide_ref, chan_ref, gain_ref,
                  out_ref, gres_ref, gy_ref, gz_ref, rows_ref, sum_out, sum_gate, mix_all, gz_all):
    step, steps = pl.program_id(0), pl.num_programs(0)

    @pl.when(step == 0)
    def _():
        rows_ref[...] = jnp.zeros_like(rows_ref)
        rows_ref[0:1, :] = gain_ref[0:1, :]

    size = out_ref.shape[0]
    gain = gain_ref[1:2, :]
    grad, picked = cot_ref[...].astype(jnp.float32), picked_ref[...].astype(jnp.float32)
    probability, chosen = prob_ref[...], chosen_of(target_ref[...], room)
    gate = jnp.sum(probability * chosen, axis=1, keepdims=True)
    residual = resid_ref[...]
    out_ref[...] = (residual + gate * picked).astype(jnp.bfloat16)
    grad_gate = jnp.sum(grad * picked, axis=1, keepdims=True)
    grad_logits = probability * (grad_gate * (chosen - gate))
    shifted_logits = pltpu.roll(grad_logits, 8, 1).astype(jnp.bfloat16)
    grad_two = back_ref[...].astype(jnp.float32) + contract(shifted_logits, wide_ref[...], 1, 1)
    rows_ref[...] += contract(shifted_logits, n2_ref[...], 0, 0)[: rows_ref.shape[0]]
    scale = lax.rsqrt(jnp.mean(residual * residual, axis=-1, keepdims=True) + EPS)
    rows_ref[1:2, :] += jnp.sum(grad_two * residual * scale, axis=0, keepdims=True)
    scaled = grad_two * gain
    share_of = jnp.mean(residual * scaled, axis=-1, keepdims=True)
    total = grad + scale * scaled - residual * (scale * scale * scale * share_of)
    gres_ref[...] = total
    mix = total.astype(jnp.bfloat16)
    at = pl.ds(pl.multiple_of(step * size, size), size)
    mix_all[at, :] = mix
    grad_gated = contract(mix, wo_ref[...], 1, 1)
    value = z_ref[...]
    bend = 1.0 / (1.0 + jnp.exp(-value))
    gy_ref[...] = grad_gated * value * bend
    scanned = y_ref[...] + chan_ref[26:27, :] * xs_ref[...].astype(jnp.float32)
    grad_z = (grad_gated * scanned * bend * (1.0 + value * (1.0 - bend))).astype(jnp.bfloat16)
    gz_ref[...] = grad_z
    gz_all[at, :] = grad_z

    @pl.when(step == steps - 1)
    def _():
        piece = 2 * LANES

        def some(index, unused):
            lanes = pl.ds(pl.multiple_of(index * piece, piece), piece)
            sum_out[:, lanes] = dot(gated_t[...], mix_all[:, lanes]).astype(jnp.bfloat16)
            return unused

        def other(index, unused):
            lanes = pl.ds(pl.multiple_of(index * piece, piece), piece)
            sum_gate[:, lanes] = dot(normed_t[...], gz_all[:, lanes]).astype(jnp.bfloat16)
            return unused

        lax.fori_loop(0, sum_out.shape[1] // piece, some, 0)
        lax.fori_loop(0, sum_gate.shape[1] // piece, other, 0)


def middle(blocks, turned_parts, weights, room, experts, block=3 * LANES):
    tokens, width = blocks[0].shape
    channels = turned_parts[0].shape[0]
    shape, half, full = jax.ShapeDtypeStruct, jnp.bfloat16, jnp.float32

    def cut(values):
        return pl.BlockSpec((block, values.shape[1]), lambda i: (i, 0))

    def whole(values):
        return pl.BlockSpec(values.shape, lambda i: (0, 0))

    results = [
        shape((tokens, width), half),
        shape((tokens, width), full),
        shape((tokens, channels), full),
        shape((tokens, channels), half),
    ]
    sums = [shape((8 + experts, width), full), shape((channels, width), half), shape((width, channels), half)]
    return pl.pallas_call(
        functools.partial(middle_kernel, room),
        grid=(tokens // block,),
        in_specs=[cut(values) for values in blocks] + [whole(values) for values in turned_parts + weights],
        out_specs=[cut(values) for values in results] + [whole(values) for values in sums],
        out_shape=results + sums,
        scratch_shapes=[pltpu.VMEM((tokens, width), half), pltpu.VMEM((tokens, channels), half)],
        compiler_params=pltpu.CompilerParams(vmem_limit_bytes=63 * 1024 * 1024),
        name="middle",
    )(*blocks, *turned_parts, *weights)


def emit_kernel(gi_from, wo_from, wo_other, wi_from, wi_other, in_from, out_from, small_ref, thin_ref,
                gi, w_out, w_in, own_in, own_out, own_x, own_dt, own_taps, own_decay, own_router, *singles):
    gi[...] = gi_from[...]
    w_out[...] = wo_from[...].astype(jnp.float32) + wo_other[...].astype(jnp.float32)
    w_in[...] = wi_from[...].astype(jnp.float32) + wi_other[...].astype(jnp.float32)
    own_in[...] = in_from[...]
    own_out[...] = out_from[...]

    def columns_of(values):
        return jnp.concatenate([values, jnp.zeros((LANES - values.shape[0], LANES), jnp.float32)], axis=0).T

    size, thin = small_ref.shape[0], thin_ref.shape[0]
    first = small_ref[:, :LANES]
    own_x[...] = first[:, : R + 2 * NS]
    own_dt[...] = columns_of(first)[R + 2 * NS :, :size]
    by_row = columns_of(small_ref[:, LANES:])
    own_taps[...] = by_row[:KC, :size]
    own_decay[...] = by_row[8 : 8 + NS, :size]
    for k in range(3):
        singles[k][...] = by_row[24 + k : 25 + k, :size]
    by_row = columns_of(thin_ref[...])
    for k in range(2):
        singles[3 + k][...] = by_row[k : k + 1, :thin]
    own_router[...] = by_row[8 : 8 + own_router.shape[0], :thin]


def emit_outputs(gi, w_out, out_other, w_in, in_other, own_in, own_out, small, thin_part, experts, pieces=4):
    rows, thin = small.shape[0], thin_part.shape[0]
    full = jnp.float32

    def cut(values):
        return pl.BlockSpec((values.shape[0] // pieces, values.shape[1]), lambda i: (i, 0))

    def whole(shape):
        return pl.BlockSpec(shape, lambda i: (0, 0))

    large = [gi, w_out, out_other, w_in, in_other]
    results = [gi, w_out, w_in]
    still = [own_in, own_out, small, thin_part]
    shapes = [own_in.shape, own_out.shape, (rows, R + 2 * NS), (R, rows), (KC, rows), (NS, rows), (experts, thin)]
    shapes += [(1, rows)] * 3 + [(1, thin)] * 2
    return pl.pallas_call(
        emit_kernel,
        grid=(pieces,),
        in_specs=[cut(values) for values in large] + [whole(values.shape) for values in still],
        out_specs=[cut(values) for values in results] + [whole(shape) for shape in shapes],
        out_shape=[jax.ShapeDtypeStruct(values.shape, full) for values in results]
        + [jax.ShapeDtypeStruct(shape, full) for shape in shapes],
        name="emit_outputs",
    )(*large, *still)


def expert_kernel(slices, *refs):
    tokens_ref, grads_ref, column_ref = refs[:3]
    even = range(0, slices, 2)
    odd = range(1, slices, 2)
    weights_in, weight_out = refs[3 : 3 + len(even)], refs[3 + len(even)]
    outs = refs[4 + len(even) :]
    picked_ref, back_ref = outs[:2]
    sums_in = outs[2 : 2 + len(even)]
    kept_out, leaving_out, arriving_out = outs[2 + len(even) : 5 + len(even)]
    (sent, got, answer, returned, w_in, w_out, hidden, total, active, slope, inner, sum_out, pair_out, pair_in, far_out,
     rows_t, send_sems, recv_sems, weight_sems, sum_sems, spread_sems, mate_sems, far_sems, moved_sems) = outs[
        5 + len(even) :
    ]
    experts, room, width = sent.shape[1:]
    places = experts * room
    me = lax.axis_index("exp")
    here = lax.axis_index("ctx")
    levels = slices.bit_length() - 1

    loads = [pltpu.make_async_copy(weight_out, w_out.at[0], weight_sems.at[slices])]
    for k, s in enumerate(even):
        loads.append(pltpu.make_async_copy(weights_in[k], w_in.at[s], weight_sems.at[s]))
    for load in loads:
        load.start()

    barrier = pltpu.get_barrier_semaphore()
    mates = [partner(("ctx", level)) for level in range(levels)]
    for step in range(1, experts):
        pl.semaphore_signal(barrier, inc=1, device_id=(here, lax.rem(me + step, experts)), device_id_type=MESH)
    for mate in mates:
        pl.semaphore_signal(barrier, inc=1, device_id=mate, device_id_type=MESH)
    pl.semaphore_wait(barrier, experts - 1 + levels)

    def exchange(source, target, kind):
        copies = []
        for step in range(1, experts):
            peer = lax.rem(me + step, experts)
            copy = pltpu.make_async_remote_copy(
                src_ref=source.at[peer],
                dst_ref=target.at[me],
                send_sem=send_sems.at[kind, step],
                recv_sem=recv_sems.at[kind, step],
                device_id=(here, peer),
                device_id_type=MESH,
            )
            copy.start()
            copies.append(copy)
        target[me] = source[me]
        return copies

    def hand(source, target, sems, level):
        copy = pltpu.make_async_remote_copy(
            src_ref=source,
            dst_ref=target,
            send_sem=sems.at[0],
            recv_sem=sems.at[1],
            device_id=mates[level],
            device_id_type=MESH,
        )
        copy.start()
        return copy

    def arrive(copies):
        for copy in copies:
            copy.wait_recv()

    open_sends = []

    def spread(level):
        step = 2**level
        copies = [hand(w_out.at[s], w_out.at[s + step], spread_sems.at[1, s + step], level) for s in range(0, slices, 2 * step)]
        open_sends.extend(copies)
        return copies

    spots = lax.broadcasted_iota(jnp.int32, (column_ref.shape[0], places), 1).astype(jnp.float32)
    columns = jnp.concatenate([column_ref[...]] * (places // LANES), axis=1)
    finder = (spots == columns).astype(jnp.float32).astype(jnp.bfloat16)
    sent[0] = contract(finder, tokens_ref[...], 0, 0).astype(jnp.bfloat16).reshape(experts, room, width)
    first = exchange(sent.at[0], got.at[0], 0)
    for load in loads:
        load.wait()
    widening = [spread(levels - 1)]
    paired = [hand(w_in.at[s], w_in.at[s + 1], spread_sems.at[0, s], 0) for s in even]
    sent[1] = contract(finder, grads_ref[...], 0, 0).astype(jnp.bfloat16).reshape(experts, room, width)
    second = exchange(sent.at[1], got.at[1], 1)

    arrive(first)
    rows = got[0].reshape(places, width)
    for s in list(even) + list(odd):
        if s == 1:
            arrive(paired)
        hidden[...] = dot(rows, w_in[s])

        def curve(index, unused):
            at = pl.ds(pl.multiple_of(index * ROWS_AT_ONCE, ROWS_AT_ONCE), ROWS_AT_ONCE)
            value = hidden[at, :]
            bell = 0.5 + 0.5 * lax.erf(value * 0.7071067811865476)
            active[s, at, :] = (value * bell).astype(jnp.bfloat16)
            slope[s, at, :] = bell + value * (jnp.exp(-0.5 * value * value) * 0.3989422804014327)
            return unused

        lax.fori_loop(0, places // ROWS_AT_ONCE, curve, 0)

    for level in reversed(range(levels - 1)):
        arrive(widening[-1])
        widening.append(spread(level))
    for s in list(even) + list(odd):
        if s == 1:
            arrive(widening[-1])
        product = dot(active[s], w_out[s])
        total[...] = product if s == 0 else total[...] + product
    answer[0] = total[...].astype(jnp.bfloat16).reshape(experts, room, width)
    third = exchange(answer.at[0], returned.at[0], 2)

    arrive(second)
    pulled = got[1].reshape(places, width)
    for s in range(slices):
        inner[s] = (contract(pulled, w_out[s], 1, 1) * slope[s]).astype(jnp.bfloat16)
        product = contract(inner[s], w_in[s], 1, 1)
        total[...] = product if s == 0 else total[...] + product
    answer[1] = total[...].astype(jnp.bfloat16).reshape(experts, room, width)
    fourth = exchange(answer.at[1], returned.at[1], 3)
    joining = []
    for s in list(odd) + list(even):
        sum_out[s] = contract(active[s], pulled, 0, 0).astype(jnp.bfloat16)
        if s % 2:
            joining.append(hand(sum_out.at[s], pair_out.at[s // 2], mate_sems.at[0, s // 2], 0))

    def add_into(target, addend):
        def some(index, unused):
            at = pl.ds(pl.multiple_of(index * 4 * ROWS_AT_ONCE, 4 * ROWS_AT_ONCE), 4 * ROWS_AT_ONCE)
            target[at, :] = target[at, :] + addend[at, :]
            return unused

        lax.fori_loop(0, target.shape[0] // (4 * ROWS_AT_ONCE), some, 0)

    arrive(joining)
    for k, s in enumerate(even):
        add_into(sum_out.at[s], pair_out.at[k])

    def pass_on(level):
        step = 2**level
        return [
            hand(sum_out.at[s + step], far_out.at[slices // step // 2 - 1 + s // (2 * step)], far_sems.at[level, s // (2 * step)], level)
            for s in range(0, slices, 2 * step)
        ]

    open_sends.extend(joining)
    for level in range(1, levels - 1):
        passing = pass_on(level)
        arrive(passing)
        open_sends.extend(passing)
        step = 2**level
        for s in range(0, slices, 2 * step):
            add_into(sum_out.at[s], far_out.at[slices // step // 2 - 1 + s // (2 * step)])
    stores = [
        pltpu.make_async_copy(sum_out.at[0], kept_out, sum_sems.at[len(even)]),
        pltpu.make_async_copy(sum_out.at[slices // 2], leaving_out, sum_sems.at[len(even) + 1]),
    ]
    for store in stores:
        store.start()
    move = row_half(sum_out.at[slices // 2], arriving_out, moved_sems, ("ctx", levels - 1), 0)
    move.start()
    for low in range(0, places, LANES):
        for left in range(0, width, LANES):
            square = got[0].reshape(places, width)[low : low + LANES, left : left + LANES].astype(jnp.float32).T
            rows_t[left : left + LANES, low : low + LANES] = square.astype(jnp.bfloat16)
    for copy in paired:
        copy.wait_send()
    joined = []
    for s in list(odd) + list(even):
        w_in[s] = dot(rows_t[...], inner[s]).astype(jnp.bfloat16)
        if s % 2:
            joined.append(hand(w_in.at[s], pair_in.at[s // 2], mate_sems.at[1, s // 2], 0))
    arrive(joined)
    for k, s in enumerate(even):
        add_into(w_in.at[s], pair_in.at[k])
        stores.append(pltpu.make_async_copy(w_in.at[s], sums_in[k], sum_sems.at[k]))
        stores[-1].start()

    arrive(third)
    picked_ref[...] = dot(finder, returned[0].reshape(places, width)).astype(jnp.bfloat16)
    arrive(fourth)
    back_ref[...] = dot(finder, returned[1].reshape(places, width)).astype(jnp.bfloat16)
    for store in stores:
        store.wait()
    move.wait()
    for copies in (first, second, third, fourth, joined, open_sends):
        for copy in copies:
            copy.wait_send()


def run_experts(rows, grads, target, weights_in, weight_out, experts, room, identity):
    slices = 2 * len(weights_in)
    tokens, width = rows.shape
    inner_width = weight_out.shape[0]
    places = experts * room
    inside = pl.BlockSpec(memory_space=pltpu.VMEM)
    anywhere = pl.BlockSpec(memory_space=pl.ANY)
    half = jnp.bfloat16
    count = len(weights_in)
    out = pl.pallas_call(
        functools.partial(expert_kernel, slices),
        in_specs=[inside] * 3 + [anywhere] * (count + 1),
        out_specs=[inside] * 2 + [anywhere] * (count + 3),
        out_shape=[jax.ShapeDtypeStruct(rows.shape, half)] * 2
        + [jax.ShapeDtypeStruct(weight.shape, half) for weight in weights_in]
        + [jax.ShapeDtypeStruct(weight_out.shape, half)] * 3,
        scratch_shapes=[pltpu.VMEM((2, experts, room, width), half)] * 4
        + [
            pltpu.VMEM((slices, width, inner_width), half),
            pltpu.VMEM((slices, inner_width, width), half),
            pltpu.VMEM((places, inner_width), jnp.float32),
            pltpu.VMEM((places, width), jnp.float32),
            pltpu.VMEM((slices, places, inner_width), half),
            pltpu.VMEM((slices, places, inner_width), jnp.float32),
            pltpu.VMEM((slices, places, inner_width), half),
            pltpu.VMEM((slices, inner_width, width), half),
            pltpu.VMEM((count, inner_width, width), half),
            pltpu.VMEM((count, width, inner_width), half),
            pltpu.VMEM((count, inner_width, width), half),
            pltpu.VMEM((width, places), half),
            pltpu.SemaphoreType.DMA((4, experts)),
            pltpu.SemaphoreType.DMA((4, experts)),
            pltpu.SemaphoreType.DMA((slices + 1,)),
            pltpu.SemaphoreType.DMA((count + 2,)),
            pltpu.SemaphoreType.DMA((2, slices, 2)),
            pltpu.SemaphoreType.DMA((2, count, 2)),
            pltpu.SemaphoreType.DMA((slices, count, 2)),
            pltpu.SemaphoreType.DMA((2, 2)),
        ],
        compiler_params=pltpu.CompilerParams(
            collective_id=identity, has_side_effects=True, vmem_limit_bytes=63 * 1024 * 1024
        ),
        name="run_experts",
    )(rows, grads, target, *weights_in, weight_out)
    return out[0], out[1], list(out[2 : 2 + count]), out[2 + count :]


def flipped(value, level):
    count = lax.axis_size("ctx")
    return lax.ppermute(value, "ctx", [(source, source ^ (1 << level)) for source in range(count)])


def spread_slices(own, far):
    levels = lax.axis_size("ctx").bit_length() - 1
    slices = {0: own, 1 << (levels - 1): far}
    for level in reversed(range(1, levels - 1)):
        for offset in sorted(slices):
            slices[offset + (1 << level)] = flipped(slices[offset], level)
    return [slices[offset] for offset in sorted(slices)]


def collect_slices(sums):
    levels = lax.axis_size("ctx").bit_length() - 1
    for level in range(1, levels - 1):
        arrived = [flipped(values, level).astype(jnp.float32) for values in sums[1::2]]
        sums = [
            (values.astype(jnp.float32) + other).astype(jnp.bfloat16) for values, other in zip(sums[::2], arrived)
        ]
    return sums


def body(
    inputs,
    segments,
    routes,
    cotangent,
    norm_gain,
    in_proj,
    conv_taps,
    conv_bias,
    x_proj,
    dt_proj,
    dt_bias,
    log_decay,
    skip_gain,
    out_proj,
    moe_gain,
    router,
    expert_in,
    expert_out,
):
    experts = router.shape[1]
    half_rows = norm_gain.shape[0]
    small = (
        x_proj,
        dt_proj,
        conv_taps.T,
        log_decay.T,
        jnp.stack([conv_bias, dt_bias, skip_gain]),
        jnp.stack([norm_gain, moe_gain]),
        router.T,
    )
    sizes = [(name, lax.axis_size(name)) for name in ("ctx", "exp")]
    weights, partial, begun, *prior = gather_all(
        sizes, small, in_proj, out_proj, inputs[0], segments, expert_in[0], 0
    )
    tokens_here = inputs.shape[1]
    capacity = 5 * tokens_here // (4 * experts)
    room = -(-capacity // 16) * 16
    (
        scan_rows,
        products,
        normed_one,
        b_turned,
        c_turned,
        rates,
        by_channel,
        gain_rows,
        delta_low,
        same_rows,
        target,
        kept,
        (conv_ext, conv_out, xs_val, dt_pre, masked_step, push),
        (full_gate, full_out),
        far_in,
    ) = scan_forward(
        sizes,
        inputs[0],
        prior,
        (segments, routes.reshape(1, tokens_here)),
        weights,
        room,
        partial,
        expert_in[0],
        begun,
        3,
    )
    weights_in = spread_slices(expert_in[0], far_in)
    full_conv, full_channel, full_width = weights
    normed_two, residual, gate_z, probability, grad_pick, gated_turned, normed_turned = open_gate(
        scan_rows,
        xs_val,
        normed_one,
        inputs[0],
        cotangent[0],
        target,
        [full_gate, full_out, full_width, by_channel, gain_rows],
        room,
        experts,
    )
    picked, grad_from_experts, grad_expert_in, (kept_out, leaving_out, begun_out) = run_experts(
        normed_two, grad_pick, target, weights_in, expert_out[0], experts, room, 2
    )
    kept_in, leaving = collect_slices(grad_expert_in)
    out_block, grad_resid, grad_y, grad_z, wide_rows, grad_out_proj, grad_gate_proj = middle(
        [picked, grad_from_experts, cotangent[0], residual, gate_z, scan_rows, xs_val, normed_two, probability, target],
        [gated_turned, normed_turned],
        [full_out, full_width, by_channel, gain_rows],
        room,
        experts,
    )
    along_b, slope, grad_bs, grad_cs, grad_a, partial_sums, begun_in = scan_backward(
        sizes,
        masked_step,
        push,
        grad_y,
        b_turned,
        c_turned,
        rates,
        products,
        (grad_gate_proj, grad_out_proj),
        kept,
        leaving,
        4,
    )
    finished = finish(
        sizes,
        (along_b, slope, grad_y, dt_pre, conv_out, xs_val, conv_ext, grad_z, full_conv, full_gate),
        (
            normed_turned,
            inputs[0],
            grad_resid,
            full_channel,
            jnp.pad(jnp.concatenate([grad_bs, grad_cs], axis=1), ((0, 0), (R, LANES - R - 2 * NS))),
            delta_low,
            same_rows,
            by_channel,
            grad_a,
            rates,
            wide_rows,
        ),
        partial_sums,
        (leaving, leaving_out),
        (begun_in, begun_out),
        1,
    )
    grad_inputs, own_in, own_out, own_small, own_thin, arrived, arrived_out = finished
    grad_inputs, grad_w_out, grad_w_in, own_in, own_out, own_x, own_dt, own_taps, own_decay, own_router, *vectors = (
        emit_outputs(
            grad_inputs, kept_out, arrived_out, kept_in, arrived, own_in, own_out, own_small, own_thin, experts
        )
    )
    own_bias, own_dtbias, own_skip, own_norm, own_moe = [values[0] for values in vectors]
    return (
        out_block[None],
        grad_inputs[None],
        own_norm,
        own_in,
        own_taps.T,
        own_bias,
        own_x,
        own_dt,
        own_dtbias,
        own_decay.T,
        own_skip,
        own_out,
        own_moe,
        own_router.T,
        grad_w_in[None],
        grad_w_out[None],
    )


def solution(mesh):
    placed = (
        P("exp", "ctx", None),
        P("exp", "ctx"),
        P("exp", "ctx", None),
        P("exp", "ctx", None),
        P(("ctx", "exp")),
        P(("ctx", "exp"), None),
        P(("ctx", "exp"), None),
        P(("ctx", "exp")),
        P(("ctx", "exp"), None),
        P(None, ("ctx", "exp")),
        P(("ctx", "exp")),
        P(("ctx", "exp"), None),
        P(("ctx", "exp")),
        P(("ctx", "exp"), None),
        P(("ctx", "exp")),
        P(("ctx", "exp"), None),
        P("exp", None, "ctx"),
        P("exp", "ctx", None),
    )
    return jax.shard_map(
        body,
        mesh=mesh,
        in_specs=placed,
        out_specs=(
            P("exp", "ctx", None),
            P("exp", "ctx", None),
            P(("ctx", "exp")),
            P(("ctx", "exp"), None),
            P(("ctx", "exp"), None),
            P(("ctx", "exp")),
            P(("ctx", "exp"), None),
            P(None, ("ctx", "exp")),
            P(("ctx", "exp")),
            P(("ctx", "exp"), None),
            P(("ctx", "exp")),
            P(("ctx", "exp"), None),
            P(("ctx", "exp")),
            P(("ctx", "exp"), None),
            P("exp", None, "ctx"),
            P("exp", "ctx", None),
        ),
        check_vma=False,
    )
```

```python
import functools

import jax
import jax.numpy as jnp
from jax import lax
from jax.experimental import pallas as pl
from jax.experimental.pallas import tpu as pltpu
from jax.sharding import PartitionSpec as P

D = 768
DI = 1536
NS = 16
R = 48
KC = 4
LANES = 128
UNROLL = 8
LOG2E = 1.4426950408889634


EPS = 1e-05
MESH = pl.DeviceIdType.MESH
ROWS_AT_ONCE = 16
EDGE = 16

def tile(ref, base, lanes):
    return ref[pl.ds(pl.multiple_of(base, UNROLL), UNROLL), lanes]

def row(rows_now, place):
    return jnp.broadcast_to(rows_now[place : place + 1], (NS, LANES))

def cost(tokens, channels, share):
    size = tokens * channels * NS
    return pl.CostEstimate(flops=size * share, transcendentals=size, bytes_accessed=size * share)


def pick(channels):
    return 512 if channels % 512 == 0 else 128


def bit_positions(sizes):
    return [(axis, size.bit_length() - 2 - k) for axis, size in sizes for k in range(size.bit_length() - 1)]


def own_bit(place):
    axis, level = place
    return lax.rem(lax.axis_index(axis) // 2**level, 2)


def partner(place):
    axis, level = place
    where = {"ctx": lax.axis_index("ctx"), "exp": lax.axis_index("exp")}
    where[axis] = where[axis] + (1 - 2 * own_bit(place)) * 2**level
    return (where["ctx"], where["exp"])


def greet(places, *others):
    barrier = pltpu.get_barrier_semaphore()
    for device in [partner(place) for place in places] + list(others):
        pl.semaphore_signal(barrier, inc=1, device_id=device, device_id_type=MESH)
    return len(places) + len(others)


def meet(places, *others):
    count = greet(places, *others)
    pl.semaphore_wait(pltpu.get_barrier_semaphore(), count)


class GatherFlow:
    def __init__(self, places, streams, dims, shards, wholes, send_sems, recv_sems, local_sems):
        self.places, self.streams, self.dims, self.shards, self.wholes = places, streams, dims, shards, wholes
        self.sems = send_sems, recv_sems, local_sems
        self.bits = [own_bit(place) for place in places]

    def view(self, number, have):
        array, cols, order, begin = self.streams[number]
        index = tuple(slice(None) if p in have else self.bits[p] for p in self.dims)
        return self.wholes[array].at[index + (slice(None), cols)]

    def shard(self, number):
        array, cols, order, begin = self.streams[number]
        return self.shards[array].at[(slice(None),) * (begin + 1) + (cols,)]

    def own(self, number):
        array, cols, order, begin = self.streams[number]
        return pltpu.make_async_copy(self.shard(number), self.view(number, order[:begin]), self.sems[2].at[number])

    def flight(self, number, stage):
        array, cols, order, begin = self.streams[number]
        target = self.view(number, order[: begin + stage])
        return pltpu.make_async_remote_copy(
            src_ref=self.shard(number) if stage == 0 else target,
            dst_ref=target,
            send_sem=self.sems[0].at[number, stage],
            recv_sem=self.sems[1].at[number, stage],
            device_id=partner(self.places[order[begin + stage]]),
            device_id_type=MESH,
        )

    def stages(self, number):
        array, cols, order, begin = self.streams[number]
        return len(order) - begin

    def start(self):
        for number in range(len(self.streams)):
            self.flight(number, 0).start()
        for number in range(len(self.streams)):
            self.own(number).start()

    def advance(self, stage):
        for number in range(len(self.streams)):
            if stage >= self.stages(number):
                continue
            if stage == 0:
                self.own(number).wait()
            self.flight(number, stage).wait_recv()
            if stage + 1 < self.stages(number):
                self.flight(number, stage + 1).start()

    def finish(self):
        for number in range(len(self.streams)):
            for stage in range(self.stages(number)):
                self.flight(number, stage).wait_send()


def pack_small(small, square, channel_pack, width_pack):
    x_ref, dt_ref, taps_ref, decay_ref, vector_ref, pair_ref, router_ref = small
    rows, thin = channel_pack.shape[0], width_pack.shape[0]

    def laid(*pieces):
        square[...] = jnp.zeros_like(square)
        for first, ref in pieces:
            square[first : first + ref.shape[0], : ref.shape[1]] = ref[...].astype(jnp.float32)
        return square[...]

    dt_part = pltpu.roll(laid((0, dt_ref)).T, R + 2 * NS, 1)
    mix = laid((0, x_ref)) + dt_part
    channel_pack[:, :LANES] = mix[:rows].astype(jnp.bfloat16)
    turned_rows = laid((0, taps_ref), (8, decay_ref), (24, vector_ref)).T
    channel_pack[:, LANES:] = turned_rows[:rows].astype(jnp.bfloat16)
    width_pack[...] = laid((0, pair_ref), (8, router_ref)).T[:thin].astype(jnp.bfloat16)


def gather_kernel(places, streams, extra_streams, far, *refs):
    small = refs[:7]
    in_ref, out_ref, rows_ref, ids_ref, leaving = refs[7:12]
    extra = 2
    wholes, prior_ref, prior_ids, arriving = refs[12:17], refs[17], refs[18], refs[19]
    (square, channel_pack, width_pack, send_sems, recv_sems, local_sems, late_send, late_recv, late_local,
     edge_sems, moved_sems) = refs[20:]
    split = in_ref.shape[1] // 2
    shards = (in_ref.at[:, :split], channel_pack, width_pack, in_ref.at[:, split:], out_ref)
    count = 3
    flow = GatherFlow(
        places, streams, range(len(places)), shards[:count], wholes[:count], send_sems, recv_sems, local_sems
    )
    late = GatherFlow(
        places, extra_streams, far, shards[count:], wholes[count:], late_send, late_recv, late_local
    )
    blocks = lax.axis_size("ctx")
    here, line = lax.axis_index("ctx"), lax.axis_index("exp")
    count_met = greet(places, (lax.rem(here + 1, blocks), line), (lax.rem(here + blocks - 1, blocks), line))
    pack_small(small, square, channel_pack, width_pack)
    pl.semaphore_wait(pltpu.get_barrier_semaphore(), count_met)
    flow.start()
    tokens = rows_ref.shape[0]
    edges = [
        pltpu.make_async_remote_copy(
            src_ref=source,
            dst_ref=target,
            send_sem=edge_sems.at[0, k],
            recv_sem=edge_sems.at[1, k],
            device_id=(lax.rem(here + 1, blocks), line),
            device_id_type=MESH,
        )
        for k, (source, target) in enumerate(
            (
                (rows_ref.at[pl.ds(tokens - EDGE, EDGE)], prior_ref),
                (ids_ref.at[:, pl.ds(tokens - LANES, LANES)], prior_ids),
            )
        )
    ]
    for edge in edges:
        edge.start()
    move = row_half(leaving, arriving, moved_sems, ("ctx", blocks.bit_length() - 2), 0)
    move.start()
    stages, behind = len(places), len(far)
    for stage in range(stages):
        flow.advance(stage)
        if stage == behind - 2:
            late.start()
        if stage >= behind and stage - behind < behind:
            late.advance(stage - behind)
    for stage in range(stages - behind, behind):
        late.advance(stage)
    flow.finish()
    late.finish()
    for edge in edges:
        edge.wait()
    move.wait()


def orders_of(places):
    core = places.index(("ctx", 0))
    rows = [k for k, place in enumerate(places) if place[0] == "ctx" and place[1] > 0]
    near = places.index(("exp", 0))
    return [core] + rows + [near] + far_of(places), [core, near] + rows + far_of(places)


def far_of(places):
    return [k for k, place in sorted(enumerate(places), key=lambda item: item[1][1]) if place[0] == "exp" and place[1] > 0]


def halves(arrays, first, second, begin=None):
    streams = []
    for array, values in enumerate(arrays):
        width = values.shape[-1]
        rest = () if begin is None else (begin,)
        if width % (2 * LANES) == 0:
            count = 4 if width % (4 * LANES) == 0 and width >= 1024 else 2
            for k in range(count):
                part = (k % 2) * (count // 2) + k // 2
                cols = slice(part * width // count, (part + 1) * width // count)
                streams.append((array, cols, second if k % 2 else first) + rest)
        else:
            streams.append((array, slice(0, width), first if array % 2 else second) + rest)
    return streams


def gather_orders(places):
    return [tuple(reversed(order)) for order in orders_of(places)]


def gather_all(sizes, small, in_proj, out_proj, rows_in, ids, leaving, identity):
    places = bit_positions(sizes)
    stages = len(places)
    far = sorted(far_of(places))
    half = jnp.bfloat16
    rows, thin, split = small[0].shape[0], in_proj.shape[0], in_proj.shape[1] // 2
    shape = jax.ShapeDtypeStruct
    shards = shape((thin, split), half), shape((rows, 2 * LANES), half), shape((thin, LANES), half)
    extra = shape((thin, split), half), shape(out_proj.shape, half)
    streams = halves(shards, *gather_orders(places), begin=0)
    late = [(k, slice(0, part.shape[1]), tuple(reversed(far_of(places))), 0) for k, part in enumerate(extra)]
    anywhere = pl.BlockSpec(memory_space=pl.ANY)
    inside = pl.BlockSpec(memory_space=pltpu.VMEM)
    out = pl.pallas_call(
        functools.partial(gather_kernel, places, streams, late, far),
        in_specs=[inside] * 7 + [anywhere] * 5,
        out_specs=[anywhere] * 8,
        out_shape=[shape((2,) * stages + shard.shape, half) for shard in shards]
        + [shape((2,) * len(far) + part.shape, half) for part in extra]
        + [shape((EDGE, rows_in.shape[1]), half), shape((1, LANES), jnp.int32), shape(leaving.shape, half)],
        scratch_shapes=[
            pltpu.VMEM((LANES, LANES), jnp.float32),
            pltpu.VMEM((rows, 2 * LANES), half),
            pltpu.VMEM((thin, LANES), half),
            pltpu.SemaphoreType.DMA((len(streams), stages)),
            pltpu.SemaphoreType.DMA((len(streams), stages)),
            pltpu.SemaphoreType.DMA((len(streams),)),
            pltpu.SemaphoreType.DMA((len(late), len(far))),
            pltpu.SemaphoreType.DMA((len(late), len(far))),
            pltpu.SemaphoreType.DMA((len(late),)),
            pltpu.SemaphoreType.DMA((2, 2)),
            pltpu.SemaphoreType.DMA((2, 2)),
        ],
        compiler_params=pltpu.CompilerParams(
            collective_id=identity, has_side_effects=True, vmem_limit_bytes=63 * 1024 * 1024
        ),
        name="gather_all",
    )(*small, in_proj, out_proj, rows_in, ids, leaving)
    return [whole.reshape((-1,) + whole.shape[stages + 1 :]) for whole in out[:3]], out[3:5], out[7], out[5], out[6]


class ReduceFlow:
    def __init__(self, places, streams, dims, parts, totals, landing, send_sems, recv_sems):
        self.places, self.streams, self.dims, self.parts, self.totals = places, streams, dims, parts, totals
        self.landing, self.sems = landing, (send_sems, recv_sems)
        self.bits = [own_bit(place) for place in places]
        self.first = []
        for array, cols, order in streams:
            self.first.append(sum(len(other[2]) for other in streams[: len(self.first)]))

    def spot(self, number, stage):
        return self.landing[self.first[number] + stage]

    def side(self, number, stage, value):
        array, cols, order = self.streams[number]
        left = [p for p in self.dims if p not in order[:stage]]
        index = tuple(value if p == order[stage] else slice(None) for p in left)
        if stage == 0:
            return self.parts[array].at[index + (slice(None), cols)]
        return self.spot(number, stage - 1).at[index]

    def flight(self, number, stage):
        order = self.streams[number][2]
        return pltpu.make_async_remote_copy(
            src_ref=self.side(number, stage, 1 - self.bits[order[stage]]),
            dst_ref=self.spot(number, stage),
            send_sem=self.sems[0].at[number, stage],
            recv_sem=self.sems[1].at[number, stage],
            device_id=partner(self.places[order[stage]]),
            device_id_type=MESH,
        )

    def start(self):
        for number in range(len(self.streams)):
            self.flight(number, 0).start()

    def advance(self, stage):
        for number, (array, cols, order) in enumerate(self.streams):
            if stage >= len(order):
                continue
            self.flight(number, stage).wait_recv()
            mine = self.side(number, stage, self.bits[order[stage]])
            there = self.spot(number, stage)
            depth = len(self.dims) - stage - 1
            final = stage + 1 == len(order)
            if depth == 0:
                self.totals[array][:, cols] = there[...].astype(jnp.float32) + mine[...].astype(jnp.float32)
                continue

            def add(index, unused, there=there, mine=mine, depth=depth, final=final, array=array, cols=cols):
                at = tuple(lax.rem(index // 2 ** (depth - 1 - k), 2) for k in range(depth))
                value = there[at] + mine[at]
                if final:
                    self.totals[array][at + (slice(None), cols)] = value
                else:
                    there[at] = value
                return unused

            lax.fori_loop(0, 2**depth, add, 0)
            if not final:
                self.flight(number, stage + 1).start()

    def finish(self):
        for number in range(len(self.streams)):
            for stage in range(len(self.streams[number][2])):
                self.flight(number, stage).wait_send()


def landing_of(streams, dims, divided):
    landing = []
    for array, cols, order in streams:
        for stage in range(len(order)):
            rows = divided[array].shape[-2]
            landing.append(pltpu.VMEM((2,) * (len(dims) - stage - 1) + (rows, cols.stop - cols.start), jnp.bfloat16))
    return landing


def flights(streams):
    shape = (len(streams), max(len(order) for array, cols, order in streams))
    return [pltpu.SemaphoreType.DMA(shape)] * 2


def dot(left, right):
    return jnp.dot(left, right, preferred_element_type=jnp.float32)


def contract(left, right, left_dim, right_dim):
    return lax.dot_general(left, right, (((left_dim,), (right_dim,)), ((), ())), preferred_element_type=jnp.float32)


def lanes_of(group, width, k):
    return pl.ds(pl.multiple_of(group * width + k * LANES, LANES), LANES)


def spread_columns(source_ref, wide_ref):
    def chunk(index, unused):
        base = pl.multiple_of(index * LANES, LANES)
        now = source_ref[:, pl.ds(base, LANES)]
        for place in range(LANES):
            wide_ref[base + place] = jnp.broadcast_to(now[:, place : place + 1], (NS, LANES))
        return unused

    lax.fori_loop(0, source_ref.shape[1] // LANES, chunk, 0)


def end_pass(width, step_ref, push_ref, wide_b, rate_ref, state_ref, hook):
    rows, channels = step_ref.shape
    count = width // LANES

    def group_body(group, unused):
        pieces = [lanes_of(group, width, k) for k in range(count)]
        rates = [rate_ref[:, lanes] for lanes in pieces]

        def block(index, states):
            states = list(states)
            steps = [tile(step_ref, index * UNROLL, lanes) for lanes in pieces]
            pushes = [tile(push_ref, index * UNROLL, lanes) for lanes in pieces]
            for place in range(UNROLL):
                b_now = wide_b[index * UNROLL + place]
                for k in range(count):
                    decay = jnp.exp2(row(steps[k], place) * rates[k])
                    states[k] = decay * states[k] + b_now * row(pushes[k], place)
            return tuple(states)

        zero = jnp.zeros((NS, LANES), jnp.float32)
        states = lax.fori_loop(0, rows // UNROLL, block, (zero,) * count)
        for k, lanes in enumerate(pieces):
            state_ref[:, lanes] = states[k]
        hook(group)
        return unused

    lax.fori_loop(0, channels // width, group_body, 0)


def out_pass(width, step_ref, push_ref, wide_b, wide_c, rate_ref, state_ref, y_ref, kept_buf, kept_copy, hook):
    rows, channels = step_ref.shape
    count = width // LANES
    span = kept_buf.shape[1]
    blocks = rows // span

    def time_body(number, unused):
        slot = lax.rem(number, 2)

        @pl.when(number >= 2)
        def _():
            kept_copy(number - 2, slot).wait()

        def group_body(group, unused_inner):
            pieces = [lanes_of(group, width, k) for k in range(count)]
            rates = [rate_ref[:, lanes] for lanes in pieces]

            def block(index, states):
                states = list(states)
                base = number * span + index * UNROLL
                steps = [tile(step_ref, base, lanes) for lanes in pieces]
                pushes = [tile(push_ref, base, lanes) for lanes in pieces]
                trees = [Tree(True) for k in range(count)]
                for place in range(UNROLL):
                    b_now = wide_b[base + place]
                    c_now = wide_c[base + place]
                    for k, lanes in enumerate(pieces):
                        decay = jnp.exp2(row(steps[k], place) * rates[k])
                        states[k] = decay * states[k] + b_now * row(pushes[k], place)
                        kept_buf[slot, index * UNROLL + place, :, lanes] = states[k].astype(kept_buf.dtype)
                        trees[k].push(place, states[k] * c_now)
                for k, lanes in enumerate(pieces):
                    y_ref[pl.ds(pl.multiple_of(base, UNROLL), UNROLL), lanes] = trees[k].result
                return tuple(states)

            states = lax.fori_loop(0, span // UNROLL, block, tuple(state_ref[:, lanes] for lanes in pieces))
            for k, lanes in enumerate(pieces):
                state_ref[:, lanes] = states[k]
            return unused_inner

        lax.fori_loop(0, channels // width, group_body, 0)
        kept_copy(number, slot).start()
        hook(number)
        return unused

    lax.fori_loop(0, blocks, time_body, 0)
    for number in range(max(0, blocks - 2), blocks):
        kept_copy(number, number % 2).wait()


def inflow_pass(width, step_ref, grad_ref, wide_c, rate_ref, flow_ref, hook):
    rows, channels = step_ref.shape
    count = width // LANES

    def group_body(group, unused):
        hook(group)
        pieces = [lanes_of(group, width, k) for k in range(count)]
        rates = [rate_ref[:, lanes] for lanes in pieces]

        def block(index, flows):
            flows = list(flows)
            base = rows - UNROLL - index * UNROLL
            steps = [tile(step_ref, base, lanes) for lanes in pieces]
            grads = [tile(grad_ref, base, lanes) for lanes in pieces]
            for place in reversed(range(UNROLL)):
                c_now = wide_c[base + place]
                for k in range(count):
                    decay = jnp.exp2(row(steps[k], place) * rates[k])
                    flows[k] = decay * (c_now * row(grads[k], place) + flows[k])
            return tuple(flows)

        zero = jnp.zeros((NS, LANES), jnp.float32)
        flows = lax.fori_loop(0, rows // UNROLL, block, (zero,) * count)
        for k, lanes in enumerate(pieces):
            flow_ref[:, lanes] = flows[k]
        return unused

    lax.fori_loop(0, channels // width, group_body, 0)


class Tree:
    def __init__(self, rising):
        self.rising, self.held, self.result = rising, {}, None

    def push(self, place, value):
        now = value[:UNROLL] + value[UNROLL:]
        level = 0
        while 1 << level < UNROLL:
            if (place >> level) % 2 == (0 if self.rising else 1):
                self.held[level] = now
                return
            first, second = (self.held[level], now) if self.rising else (now, self.held[level])
            now = self.merge(first, second, 1 << level)
            level += 1
        self.result = now

    def merge(self, first, second, distance):
        low = (lax.broadcasted_iota(jnp.int32, (UNROLL, LANES), 0) & distance) == 0
        keep = jnp.where(low, first, second)
        give = jnp.where(low, second, first)
        other = pltpu.roll(give, distance, 0)
        if 2 * distance != UNROLL:
            other = jnp.where(low, pltpu.roll(give, UNROLL - distance, 0), other)
        return keep + other


def lane_sums(part_ref):
    values = part_ref[...].reshape(-1, LANES).astype(jnp.bfloat16)
    return contract(jnp.ones((UNROLL, LANES), jnp.bfloat16), values, 1, 1)


def adjoint_pass(width, step_ref, push_ref, grad_ref, wide_b, wide_c, rate_ref, flow_ref, kept_buf, kept_copy,
                 along_ref, slope_ref, gb_ref, gc_ref, ga_ref, part_b, part_c, hook):
    rows, channels = step_ref.shape
    count = width // LANES
    span = kept_buf.shape[1] - 1
    blocks = rows // span
    ga_ref[...] = jnp.zeros_like(ga_ref)

    def time_body(order, unused):
        slot = lax.rem(order, 2)
        number = blocks - 1 - order
        kept_copy(number, slot).wait()
        part_b[...] = jnp.zeros_like(part_b)
        part_c[...] = jnp.zeros_like(part_c)

        def group_body(group, unused_inner):
            pieces = [lanes_of(group, width, k) for k in range(count)]
            rates = [rate_ref[:, lanes] for lanes in pieces]

            def block(index, carried):
                flows = list(carried[:count])
                sums = list(carried[count : 2 * count])
                current = list(carried[2 * count :])
                local = span - UNROLL - index * UNROLL
                base = number * span + local
                steps = [tile(step_ref, base, lanes) for lanes in pieces]
                pushes = [tile(push_ref, base, lanes) for lanes in pieces]
                grads = [tile(grad_ref, base, lanes) for lanes in pieces]
                alongs = [Tree(False) for k in range(count)]
                slopes = [Tree(False) for k in range(count)]
                for place in reversed(range(UNROLL)):
                    b_now = wide_b[base + place]
                    c_now = wide_c[base + place]
                    gb = gc = None
                    for k, lanes in enumerate(pieces):
                        prior = kept_buf[slot, local + place, :, lanes].astype(jnp.float32)
                        step = row(steps[k], place)
                        grad = row(grads[k], place)
                        decay = jnp.exp2(step * rates[k])
                        adjoint = c_now * grad + flows[k]
                        flows[k] = decay * adjoint
                        decay_grad = flows[k] * prior
                        alongs[k].push(place, adjoint * b_now)
                        slopes[k].push(place, decay_grad * rates[k])
                        sums[k] = sums[k] + decay_grad * step
                        here_b = adjoint * row(pushes[k], place)
                        here_c = current[k] * grad
                        gb = here_b if gb is None else gb + here_b
                        gc = here_c if gc is None else gc + here_c
                        current[k] = prior
                    part_b[local + place] += gb
                    part_c[local + place] += gc
                where = pl.ds(pl.multiple_of(base, UNROLL), UNROLL)
                for k, lanes in enumerate(pieces):
                    along_ref[where, lanes] = alongs[k].result
                    slope_ref[where, lanes] = slopes[k].result
                return tuple(flows + sums + current)

            carried = lax.fori_loop(
                0,
                span // UNROLL,
                block,
                tuple(flow_ref[:, lanes] for lanes in pieces)
                + tuple(ga_ref[:, lanes] for lanes in pieces)
                + tuple(kept_buf[slot, span, :, lanes].astype(jnp.float32) for lanes in pieces),
            )
            for k, lanes in enumerate(pieces):
                flow_ref[:, lanes] = carried[k]
                ga_ref[:, lanes] = carried[count + k]
            return unused_inner

        lax.fori_loop(0, channels // width, group_body, 0)
        gb_ref[number] = lane_sums(part_b)
        gc_ref[number] = lane_sums(part_c)

        @pl.when(order + 2 < blocks)
        def _():
            kept_copy(number - 2, slot).start()

        hook(order)
        return unused

    lax.fori_loop(0, blocks, time_body, 0)


def share(source, target, send_sems, recv_sems):
    blocks = lax.axis_size("ctx")
    here, line = lax.axis_index("ctx"), lax.axis_index("exp")
    copies = []
    for step in range(1, blocks):
        copies.append(
            pltpu.make_async_remote_copy(
                src_ref=source,
                dst_ref=target.at[here],
                send_sem=send_sems.at[step],
                recv_sem=recv_sems.at[step],
                device_id=(lax.rem(here + step, blocks), line),
                device_id_type=MESH,
            )
        )
        copies[-1].start()
    target[here] = source[...]
    return copies


def row_peers():
    blocks = lax.axis_size("ctx")
    here, line = lax.axis_index("ctx"), lax.axis_index("exp")
    return [(lax.rem(here + step, blocks), line) for step in range(1, blocks)]


def row_half(source, target, sems, place, k):
    size = source.shape[0] // 2
    return pltpu.make_async_remote_copy(
        src_ref=source.at[pl.ds(k * size, size)],
        dst_ref=target.at[pl.ds(k * size, size)],
        send_sem=sems.at[0, k],
        recv_sem=sems.at[1, k],
        device_id=partner(place),
        device_id_type=MESH,
    )


def front(loaded, loads, room, outs, scratch, saves):
    normed_ref, bt_ref, ct_ref, rate_ref, chan_ref, gain_ref, delta_ref, same_ref, target_ref = outs
    nx, ext, conv, xs, pre, step, push = scratch
    in_ref, prior_ref, prior_ids, ids_ref, routes_ref, conv_w, channel_ref, width_ref = loaded
    for load in loads[:5] + loads[6:]:
        load.wait()
    tokens, channels = xs.shape
    width = in_ref.shape[1]
    mine = lax.axis_index("ctx")
    gain_rows = jnp.concatenate(
        [width_ref[at : at + LANES, :].astype(jnp.float32).T for at in range(0, width, LANES)], axis=1
    )
    gain_ref[...] = gain_rows[:8]
    for at in range(0, channels, LANES):
        chan_ref[:, at : at + LANES] = channel_ref[at : at + LANES, LANES:].astype(jnp.float32).T[:32]
    rate_ref[...] = -jnp.exp(chan_ref[8 : 8 + NS, :]) * LOG2E
    gain = gain_ref[0:1, :]

    def normed(values):
        x = values.astype(jnp.float32)
        return (x * lax.rsqrt(jnp.mean(x * x, axis=-1, keepdims=True) + EPS) * gain).astype(jnp.bfloat16)

    nx[:EDGE, :] = normed(prior_ref[...])

    def norm_rows(index, unused):
        at = pl.ds(pl.multiple_of(index * 16, 16), 16)
        value = normed(in_ref[at, :])
        normed_ref[at, :] = value
        nx[pl.ds(pl.multiple_of(EDGE + index * 16, 16), 16), :] = value
        return unused

    lax.fori_loop(0, tokens // 16, norm_rows, 0)
    def column(values):
        return jnp.broadcast_to(values.astype(jnp.float32), (LANES, LANES)).T

    def columns(ref):
        return jnp.concatenate([column(ref[:, at : at + LANES]) for at in range(0, tokens, LANES)], axis=0)

    ids = jnp.where(mine > 0, column(prior_ids[...])[LANES - EDGE :], -1.0)
    own_ids = columns(ids_ref)
    every_id = jnp.concatenate([ids, own_ids], axis=0)
    for j in range(1, KC):
        same_ref[j - 1] = (pltpu.roll(every_id, j, 0)[EDGE:] == own_ids).astype(jnp.float32)
    routes = columns(routes_ref)
    chosen = (routes == lax.broadcasted_iota(jnp.int32, routes.shape, 1).astype(jnp.float32)).astype(jnp.float32)
    square = (tokens, tokens)
    until = lax.broadcasted_iota(jnp.int32, square, 0) >= lax.broadcasted_iota(jnp.int32, square, 1)
    running = dot(until.astype(jnp.float32).astype(jnp.bfloat16), chosen.astype(jnp.bfloat16))
    slot = jnp.sum(running * chosen, axis=1, keepdims=True) - 1.0
    target_ref[...] = routes * room + slot
    piece = 2 * LANES
    loads[5].wait()

    def conv_piece(index, unused):
        lanes = pl.ds(pl.multiple_of(index * piece, piece), piece)
        low = dot(nx[...], conv_w[:, lanes]).astype(jnp.bfloat16)
        ext[:, lanes] = low
        value = low.astype(jnp.float32)
        out = chan_ref[24:25, lanes] + chan_ref[3:4, lanes] * value[EDGE:]
        for j in range(1, KC):
            same = jnp.concatenate([same_ref[j - 1]] * 2, axis=1)
            out = out + chan_ref[3 - j : 4 - j, lanes] * pltpu.roll(value, j, 0)[EDGE:] * same
        conv[:, lanes] = out
        xs[:, lanes] = (out / (1.0 + jnp.exp(-out))).astype(jnp.bfloat16)
        return unused

    lax.fori_loop(0, channels // piece, conv_piece, 0)
    for save in saves[:3]:
        save.start()
    projected = dot(xs[...], channel_ref[:, :LANES])
    lane = lax.broadcasted_iota(jnp.int32, projected.shape, 1)
    delta_ref[...] = jnp.where(lane >= R + 2 * NS, pltpu.roll(projected, R + 2 * NS, 1), 0.0).astype(jnp.bfloat16)
    for at in range(0, tokens, LANES):
        block = projected[at : at + LANES].T
        bt_ref[:, at : at + LANES] = block[R : R + NS]
        ct_ref[:, at : at + LANES] = block[R + NS : R + 2 * NS]

    def step_piece(index, unused):
        lanes = pl.ds(pl.multiple_of(index * piece, piece), piece)
        value = contract(delta_ref[...], channel_ref[lanes, :LANES], 1, 1) + chan_ref[25:26, lanes]
        pre[:, lanes] = value
        size = jnp.maximum(value, 0.0) + jnp.log1p(jnp.exp(-jnp.abs(value)))
        push[:, lanes] = size * xs[:, lanes].astype(jnp.float32)
        keep = jnp.concatenate([same_ref[0]] * 2, axis=1)
        step[:, lanes] = jnp.where(keep > 0, size, 1e30)
        return unused

    lax.fori_loop(0, channels // piece, step_piece, 0)
    for save in saves[3:]:
        save.start()


def forward_kernel(places, streams, width, room, *refs):
    weights_from = refs[:8]
    shards, leaving = refs[8:10], refs[10]
    y_ref, product_ref = refs[12:14]
    front_outs = refs[14:23]
    kept_ref = refs[23]
    saved = refs[24:30]
    wholes, arriving = refs[30:32], refs[32]
    scratch = refs[33:40]
    weights = refs[40:48]
    (wide_b, wide_c, kept_buf, first_buf, state_ref, message, products, ends,
     load_sems, kept_sems, first_sem, share_sems, save_sems, moved_sems, send_sems, recv_sems, local_sems) = refs[48:]
    loads = [pltpu.make_async_copy(weights_from[k], weights[k], load_sems.at[k]) for k in range(8)]
    for load in loads[:5] + loads[:4:-1]:
        load.start()
    bt_ref, ct_ref, rate_ref = front_outs[1:4]
    step_ref, push_ref = scratch[5:7]
    blocks = lax.axis_size("ctx")
    position = lax.axis_index("ctx")
    span = kept_buf.shape[1]
    flow = GatherFlow(places, streams, range(len(places)), shards, wholes, send_sems, recv_sems, local_sems)
    meet([place for place in places if place[0] == "exp"], *row_peers())
    flow.start()
    move = row_half(leaving, arriving, moved_sems, ("ctx", blocks.bit_length() - 2), 1)
    move.start()
    saves = [
        pltpu.make_async_copy(scratch[k + 1], saved[k], save_sems.at[k]) for k in range(6)
    ]
    front(weights, loads, room, front_outs, scratch, saves)

    message[0] = jnp.exp2(jnp.sum(step_ref[...], axis=0, keepdims=True) * rate_ref[...]).astype(jnp.bfloat16)
    early = share(message.at[0], products, share_sems.at[0], share_sems.at[1])
    spread_columns(bt_ref, wide_b)
    spread_columns(ct_ref, wide_c)
    end_pass(width, step_ref, push_ref, wide_b, rate_ref, state_ref, lambda group: None)
    message[1] = state_ref[...].astype(jnp.bfloat16)
    late = share(message.at[1], ends, share_sems.at[2], share_sems.at[3])
    flow.advance(0)
    for copy in early + late:
        copy.wait_recv()
    start = jnp.zeros(state_ref.shape, jnp.float32)
    for index in range(blocks):
        folded = products[index].astype(jnp.float32) * start + ends[index].astype(jnp.float32)
        start = jnp.where(index < position, folded, start)
    state_ref[...] = start
    product_ref[...] = products[...]
    first_buf[0] = start.astype(jnp.bfloat16)
    first_copy = pltpu.make_async_copy(first_buf, kept_ref.at[pl.ds(0, 1)], first_sem)
    first_copy.start()

    def kept_copy(number, slot):
        return pltpu.make_async_copy(
            kept_buf.at[slot], kept_ref.at[pl.ds(1 + number * span, span)], kept_sems.at[slot]
        )

    def hook(number):
        @pl.when(number == 3)
        def _():
            flow.advance(1)

    out_pass(width, step_ref, push_ref, wide_b, wide_c, rate_ref, state_ref, y_ref, kept_buf, kept_copy, hook)
    for stage in range(2, max(flow.stages(number) for number in range(len(streams)))):
        flow.advance(stage)
    flow.finish()
    first_copy.wait()
    for save in saves:
        save.wait()
    for copy in early + late:
        copy.wait_send()
    move.wait()


def scan_forward(sizes, rows_in, prior, ids, weights, room, shards, leaving, begun, identity, span=64):
    places = bit_positions(sizes)
    stages = len(places)
    begin = len(far_of(places))
    streams = halves(shards, *gather_orders(places), begin=begin)
    tokens, width = rows_in.shape
    channels = weights[0].shape[1]
    blocks = sizes[0][1]
    inside = pl.BlockSpec(memory_space=pltpu.VMEM)
    anywhere = pl.BlockSpec(memory_space=pl.ANY)
    half, full = jnp.bfloat16, jnp.float32
    shape = jax.ShapeDtypeStruct
    saved = [
        shape((EDGE + tokens, channels), half),
        shape((tokens, channels), full),
        shape((tokens, channels), half),
        shape((tokens, channels), full),
        shape((tokens, channels), full),
        shape((tokens, channels), full),
    ]
    y, products, normed, bt, ct, rates, chan, gains, delta, same, target, kept, *rest = pl.pallas_call(
        functools.partial(forward_kernel, places, streams, pick(channels), room),
        in_specs=[anywhere] * 12,
        input_output_aliases={11: 20},
        out_specs=[inside] * 11 + [anywhere] * 10,
        out_shape=[
            shape((tokens, channels), full),
            shape((blocks, NS, channels), half),
            shape((tokens, width), half),
            shape((NS, tokens), full),
            shape((NS, tokens), full),
            shape((NS, channels), full),
            shape((32, channels), full),
            shape((8, width), full),
            shape((tokens, LANES), half),
            shape((KC - 1, tokens, LANES), full),
            shape((tokens, LANES), full),
            shape((tokens + 1, NS, channels), half),
        ]
        + saved
        + [shape((2,) * stages + shard.shape[begin:], shard.dtype) for shard in shards]
        + [shape(leaving.shape, leaving.dtype)],
        scratch_shapes=[pltpu.VMEM((EDGE + tokens, width), half)]
        + [pltpu.VMEM(value.shape, value.dtype) for value in saved]
        + [pltpu.VMEM(value.shape, value.dtype) for value in [rows_in, *prior, *ids, *weights]]
        + [
            pltpu.VMEM((tokens, NS, LANES), full),
            pltpu.VMEM((tokens, NS, LANES), full),
            pltpu.VMEM((2, span, NS, channels), half),
            pltpu.VMEM((1, NS, channels), half),
            pltpu.VMEM((NS, channels), full),
            pltpu.VMEM((2, NS, channels), half),
            pltpu.VMEM((blocks, NS, channels), half),
            pltpu.VMEM((blocks, NS, channels), half),
            pltpu.SemaphoreType.DMA((8,)),
            pltpu.SemaphoreType.DMA((2,)),
            pltpu.SemaphoreType.DMA,
            pltpu.SemaphoreType.DMA((4, blocks)),
            pltpu.SemaphoreType.DMA((6,)),
            pltpu.SemaphoreType.DMA((2, 2)),
            pltpu.SemaphoreType.DMA((len(streams), stages)),
            pltpu.SemaphoreType.DMA((len(streams), stages)),
            pltpu.SemaphoreType.DMA((len(streams),)),
        ],
        compiler_params=pltpu.CompilerParams(
            collective_id=identity, has_side_effects=True, vmem_limit_bytes=63 * 1024 * 1024
        ),
        cost_estimate=cost(tokens, channels, 9),
        name="scan_forward",
    )(rows_in, *prior, *ids, *weights, *shards, leaving, begun)
    saved, wholes, arrived = rest[:6], rest[6:8], rest[8]
    wholes = [whole.reshape((-1,) + whole.shape[stages + 1 :]) for whole in wholes]
    return y, products, normed, bt, ct, rates, chan, gains, delta, same, target, kept, saved, wholes, arrived


def backward_kernel(places, streams, marks, width, *refs):
    bt_ref, ct_ref, rate_ref, product_ref = refs[:4]
    parts = refs[4:6]
    streamed = refs[6:9]
    kept_ref, leaving = refs[9:11]
    outs = refs[11:]
    gb_ref, gc_ref, ga_ref = outs[:3]
    totals, arriving = outs[3:5], outs[5]
    rows_out = outs[6:8]
    scratch = outs[8:]
    landing = scratch[:marks]
    (step_ref, push_ref, grad_ref, along_ref, slope_ref, wide_b, wide_c, part_b, part_c, kept_buf, flow_ref, message,
     inflows, load_sems, push_sem, out_sems, kept_sems, share_sems, moved_sems, send_sems, recv_sems) = scratch[marks:]
    blocks = lax.axis_size("ctx")
    position = lax.axis_index("ctx")
    span = kept_buf.shape[1] - 1
    steps = step_ref.shape[0] // span

    def load(group, k):
        lanes = pl.ds(pl.multiple_of(group * width, LANES), width)
        source, target = ((streamed[0], step_ref), (streamed[2], grad_ref))[k]
        return pltpu.make_async_copy(source.at[:, lanes], target.at[:, lanes], load_sems.at[k, group])

    for group in range(step_ref.shape[1] // width):
        for k in range(2):
            load(group, k).start()
    push_load = pltpu.make_async_copy(streamed[1], push_ref, push_sem)
    push_load.start()

    def ready(group):
        for k in range(2):
            load(group, k).wait()

    def rows_copy(number, k):
        rows = pl.ds(number * span, span)
        return pltpu.make_async_copy((along_ref, slope_ref)[k].at[rows], rows_out[k].at[rows], out_sems.at[k, number])

    flow = ReduceFlow(places, streams, range(len(places)), parts, totals, landing, send_sems, recv_sems)

    def kept_copy(number, slot):
        return pltpu.make_async_copy(
            kept_ref.at[pl.ds(number * span, span + 1)], kept_buf.at[slot], kept_sems.at[slot]
        )

    for order in range(min(2, steps)):
        kept_copy(steps - 1 - order, order).start()
    meet([place for place in places if place[0] == "exp"], *row_peers())
    flow.start()
    move = row_half(leaving, arriving, moved_sems, ("ctx", blocks.bit_length() - 2), 0)
    move.start()
    spread_columns(ct_ref, wide_c)
    inflow_pass(width, step_ref, grad_ref, wide_c, rate_ref, flow_ref, ready)
    message[...] = flow_ref[...].astype(jnp.bfloat16)
    copies = share(message, inflows, share_sems.at[0], share_sems.at[1])
    flow.advance(0)
    spread_columns(bt_ref, wide_b)
    for copy in copies:
        copy.wait_recv()
    end = jnp.zeros(flow_ref.shape, jnp.float32)
    for index in reversed(range(blocks)):
        folded = inflows[index].astype(jnp.float32) + product_ref[index].astype(jnp.float32) * end
        end = jnp.where(index > position, folded, end)
    flow_ref[...] = end
    push_load.wait()

    def hook(order):
        for k in range(2):
            rows_copy(steps - 1 - order, k).start()

        @pl.when(order == 3)
        def _():
            flow.advance(1)

        @pl.when(order == 5)
        def _():
            flow.advance(2)

    adjoint_pass(width, step_ref, push_ref, grad_ref, wide_b, wide_c, rate_ref, flow_ref, kept_buf, kept_copy,
                 along_ref, slope_ref, gb_ref, gc_ref, ga_ref, part_b, part_c, hook)
    for stage in range(3, len(streams[0][2])):
        flow.advance(stage)
    flow.finish()
    for copy in copies:
        copy.wait_send()
    move.wait()
    for number in range(steps):
        for k in range(2):
            rows_copy(number, k).wait()


def scan_backward(sizes, step, push, grad, b_turned, c_turned, rates, products, parts, kept, leaving, identity, span=64):
    places = bit_positions(sizes)
    stages = len(places)
    far = sorted(far_of(places))
    streams = halves(parts, *[tuple(order[: stages - len(far)]) for order in orders_of(places)])
    divided = [part.reshape((2,) * stages + (-1, part.shape[1])) for part in parts]
    tokens, channels = step.shape
    blocks = sizes[0][1]
    inside = pl.BlockSpec(memory_space=pltpu.VMEM)
    anywhere = pl.BlockSpec(memory_space=pl.ANY)
    half = jnp.bfloat16
    landing = landing_of(streams, range(stages), divided)
    row_sums = jax.ShapeDtypeStruct((tokens // span, UNROLL, span * NS), jnp.float32)
    out = pl.pallas_call(
        functools.partial(backward_kernel, places, streams, len(landing), pick(channels)),
        in_specs=[inside] * 6 + [anywhere] * 5,
        out_specs=[inside] * 5 + [anywhere] * 3,
        out_shape=[row_sums, row_sums, jax.ShapeDtypeStruct((NS, channels), jnp.float32)]
        + [jax.ShapeDtypeStruct((2,) * len(far) + block.shape[-2:], half) for block in divided]
        + [jax.ShapeDtypeStruct(leaving.shape, leaving.dtype)]
        + [jax.ShapeDtypeStruct((tokens, channels), jnp.float32)] * 2,
        scratch_shapes=landing
        + [pltpu.VMEM((tokens, channels), jnp.float32)] * 5
        + [
            pltpu.VMEM((tokens, NS, LANES), jnp.float32),
            pltpu.VMEM((tokens, NS, LANES), jnp.float32),
            pltpu.VMEM((span, NS, LANES), jnp.float32),
            pltpu.VMEM((span, NS, LANES), jnp.float32),
            pltpu.VMEM((2, span + 1, NS, channels), half),
            pltpu.VMEM((NS, channels), jnp.float32),
            pltpu.VMEM((NS, channels), half),
            pltpu.VMEM((blocks, NS, channels), half),
            pltpu.SemaphoreType.DMA((2, channels // pick(channels))),
            pltpu.SemaphoreType.DMA,
            pltpu.SemaphoreType.DMA((2, tokens // span)),
            pltpu.SemaphoreType.DMA((2,)),
            pltpu.SemaphoreType.DMA((2, blocks)),
            pltpu.SemaphoreType.DMA((2, 2)),
        ]
        + flights(streams),
        compiler_params=pltpu.CompilerParams(
            collective_id=identity, has_side_effects=True, vmem_limit_bytes=63 * 1024 * 1024
        ),
        cost_estimate=cost(tokens, channels, 15),
        name="scan_backward",
    )(b_turned, c_turned, rates, products, *divided, step, push, grad, kept, leaving)
    wide_b, wide_c, grad_a, first, second, arrived, along, slope = out
    grad_bs, grad_cs = [values[:, 0].reshape(tokens, NS) for values in (wide_b, wide_c)]
    return along, slope, grad_bs, grad_cs, grad_a, (first, second), arrived


class PackedReduce(ReduceFlow):
    def __init__(self, places, streams, heads, parts, totals, landing, blocks, send_sems, recv_sems):
        super().__init__(places, streams, range(len(places)), parts, totals, landing, send_sems, recv_sems)
        self.heads, self.blocks = heads, blocks

    def side(self, number, stage, value):
        array, cols, order = self.streams[number]
        if stage == 0:
            index = tuple(value if p == order[0] else slice(None) for p in range(self.heads))
            return self.parts[array].at[index + (slice(None), cols)]
        left = [p for p in self.dims if p not in order[:stage]]
        index = tuple(value if p == order[stage] else slice(None) for p in left)
        held = self.blocks[number] if stage == 1 else self.spot(number, stage - 1)
        return held.at[index]

    def advance(self, stage):
        if stage:
            super().advance(stage)
            return
        for number, (array, cols, order) in enumerate(self.streams):
            self.flight(number, 0).wait_recv()
            mine = self.side(number, 0, self.bits[order[0]])
            there, held = self.spot(number, 0), self.blocks[number]
            tails = len(self.places) - self.heads
            size = held.shape[-2]

            def add(index, unused, mine=mine, there=there, held=held, tails=tails, size=size):
                at = tuple(lax.rem(index // 2 ** (self.heads - 2 - k), 2) for k in range(self.heads - 1))
                value = there[at].astype(jnp.float32) + mine[at].astype(jnp.float32)
                for block in range(2**tails):
                    spot = tuple(block // 2 ** (tails - 1 - k) % 2 for k in range(tails))
                    held[at + spot] = value[block * size : (block + 1) * size].astype(held.dtype)
                return unused

            lax.fori_loop(0, 2 ** (self.heads - 1), add, 0)
            self.flight(number, 1).start()


def turned(values):
    return jnp.concatenate([values[:, at : at + LANES].T for at in range(0, values.shape[1], LANES)], axis=0)


def finish_kernel(places, streams, third, late, far, marks, *refs):
    leaving = refs[23:25]
    refs = refs[:23] + refs[27:]
    (along_h, slope_h, grad_h, pre_h, conv_h, xs_h, ext_h, gz_h, wc_h, wg_h) = refs[:10]
    (normed_ref, in_ref, resid_ref, mix_ref, bc_ref, delta_ref, same_ref, chan_ref, decay_ref, rate_ref, wide_ref) = refs[10:21]
    rest_parts = refs[21:23]
    gi_ref, own_in, own_out, tot_small, tot_wide = refs[23:28]
    arriving, scratch = refs[28:30], refs[30:]
    landing, scratch = scratch[: marks[0]], scratch[marks[0] :]
    blocks, scratch = scratch[: marks[1]], scratch[marks[1] :]
    landing3, scratch = scratch[: marks[2]], scratch[marks[2] :]
    blocks3, scratch = scratch[: marks[3]], scratch[marks[3] :]
    late_landing, scratch = scratch[: marks[4]], scratch[marks[4] :]
    (along, slope, grad, pre, conv, xs, ext, gz, wc, wg, gdt, gci, last, spill, arrived, sums, rows_s, wide_s, gn,
     part_conv, part_small, part_wide,
     block_sems, whole_sems, spill_sems, moved_sems, send_sems, recv_sems, send3, recv3, late_send, late_recv) = scratch
    tokens, channels = xs.shape
    own_conv, own_gate = own_in.at[:, :channels], own_in.at[:, channels:]
    span = tokens // block_sems.shape[1]
    heads = len([place for place in places if place[0] == "ctx"])
    flow = PackedReduce(
        places, streams, heads, (part_conv, part_small), (own_conv, tot_small), landing, blocks, send_sems, recv_sems
    )
    flow3 = PackedReduce(places, third, heads, (part_wide,), (tot_wide,), landing3, blocks3, send3, recv3)
    rest = ReduceFlow(places, late, far, rest_parts, (own_gate, own_out), late_landing, late_send, late_recv)

    streamed = ((along_h, along), (slope_h, slope), (grad_h, grad), (pre_h, pre), (xs_h, xs))

    def block_copy(k, number):
        rows = pl.ds(number * span, span)
        source, target = streamed[k]
        return pltpu.make_async_copy(source.at[rows], target.at[rows], block_sems.at[k, number])

    for number in range(tokens // span):
        for k in range(len(streamed)):
            block_copy(k, number).start()
    wholes = [
        pltpu.make_async_copy(source, target, whole_sems.at[k])
        for k, (source, target) in enumerate(((conv_h, conv), (ext_h, ext), (gz_h, gz), (wc_h, wc), (wg_h, wg)))
    ]
    for copy in wholes:
        copy.start()
    count = lax.axis_size("ctx")
    here, line = lax.axis_index("ctx"), lax.axis_index("exp")
    before = (lax.rem(here + count - 1, count), line)
    meet(places, before, (lax.rem(here + 1, count), line))
    rest.start()
    moves = [
        row_half(leaving[k], arriving[k], moved_sems.at[k], ("ctx", count.bit_length() - 2), 1) for k in range(2)
    ]
    moves[0].start()

    sums[...] = jnp.zeros_like(sums)
    rows_s[...] = jnp.zeros_like(rows_s)

    def first_block(number, unused):
        for k in range(len(streamed)):
            block_copy(k, number).wait()

        def some(index, unused_inner):
            at = pl.ds(pl.multiple_of(number * span + index * 16, 16), 16)
            for low in range(0, channels, LANES):
                lanes = slice(low, low + LANES)
                a, g, x, p = along[at, lanes], grad[at, lanes], xs[at, lanes].astype(jnp.float32), pre[at, lanes]
                small = jnp.exp(-jnp.abs(p))
                gated = jnp.where(p >= 0, 1.0, small) / (1.0 + small)
                step = jnp.maximum(p, 0.0) + jnp.log1p(small)
                value = (a * x + slope[at, lanes] * (1.0 / LOG2E)) * gated
                gdt[at, lanes] = value.astype(jnp.bfloat16)
                sums[0, :, lanes] += value[:8] + value[8:]
                both = g * x
                sums[1, :, lanes] += both[:8] + both[8:]
                along[at, lanes] = chan_ref[26:27, lanes] * g + a * step
            return unused_inner

        lax.fori_loop(0, span // 16, some, 0)
        return unused

    lax.fori_loop(0, tokens // span, first_block, 0)
    rows_s[25:26, :] = jnp.sum(sums[0], axis=0, keepdims=True)
    rows_s[26:27, :] = jnp.sum(sums[1], axis=0, keepdims=True)
    rows_s[8:24, :] = decay_ref[...] * rate_ref[...] * (1.0 / LOG2E)

    lane = lax.broadcasted_iota(jnp.int32, (tokens, LANES), 1)
    mixed = pltpu.roll(dot(gdt[...], mix_ref[:, :LANES]), R, 1)
    projected = jnp.where(lane < R, mixed, jnp.where(lane < R + 2 * NS, bc_ref[...], 0.0)).astype(jnp.bfloat16)
    wholes[0].wait()
    wholes[1].wait()
    piece = 2 * LANES
    tail_row = lax.broadcasted_iota(jnp.int32, (tokens, piece), 0)

    def conv_piece(index, unused):
        lanes = pl.ds(pl.multiple_of(index * piece, piece), piece)
        some = pl.ds(pl.multiple_of(index * piece, piece), piece)
        total = along[:, lanes] + contract(projected, mix_ref[some, :LANES], 1, 1)
        value = conv[:, lanes]
        gate = 1.0 / (1.0 + jnp.exp(-value))
        out = total * gate * (1.0 + value * (1.0 - gate))
        rows_s[24:25, lanes] = jnp.sum(out, axis=0, keepdims=True)
        before_rows = ext[:, lanes].astype(jnp.float32)
        rows_s[3:4, lanes] = jnp.sum(out * before_rows[EDGE:], axis=0, keepdims=True)
        result = chan_ref[3:4, lanes] * out
        beyond = jnp.zeros((8, piece), jnp.float32)
        for j in range(1, KC):
            same = jnp.concatenate([same_ref[j - 1]] * 2, axis=1)
            masked = out * same
            shifted_rows = pltpu.roll(before_rows, j, 0)[EDGE:]
            rows_s[3 - j : 4 - j, lanes] = jnp.sum(masked * shifted_rows, axis=0, keepdims=True)
            moved = chan_ref[3 - j : 4 - j, lanes] * pltpu.roll(masked, tokens - j, 0)
            result = result + jnp.where(tail_row < tokens - j, moved, 0.0)
            beyond = beyond + jnp.where(tail_row < tokens - j, 0.0, moved)[tokens - 8 :]
        gci[:, lanes] = result.astype(jnp.bfloat16)
        last[:, lanes] = result[tokens - 16 :]
        spill[:, lanes] = beyond
        return unused

    lax.fori_loop(0, channels // piece, conv_piece, 0)
    handed = pltpu.make_async_remote_copy(
        src_ref=spill,
        dst_ref=arrived,
        send_sem=spill_sems.at[0],
        recv_sem=spill_sems.at[1],
        device_id=before,
        device_id_type=MESH,
    )
    handed.start()

    cut = part_small.shape[-2]
    first_rows = contract(projected, xs[...], 0, 0) + contract(delta_ref[...], gdt[...], 0, 0)
    filler = jnp.zeros((LANES - rows_s.shape[0], channels), jnp.float32)
    for k, values in enumerate((first_rows, jnp.concatenate([rows_s[...], filler], axis=0))):
        columns = turned(values)
        for index in range(channels // cut):
            spot = tuple(index // 2 ** (heads - 1 - j) % 2 for j in range(heads))
            part_small[spot + (slice(None), slice(k * LANES, (k + 1) * LANES))] = columns[
                index * cut : (index + 1) * cut
            ].astype(jnp.bfloat16)
    handed.wait_recv()
    closing = last[...] + jnp.concatenate([jnp.zeros((8, channels), jnp.float32), arrived[...]], axis=0)
    gci[tokens - 16 :, :] = closing.astype(jnp.bfloat16)

    long = part_conv.shape[-2]

    def product_piece(index, unused):
        lanes = pl.ds(pl.multiple_of(index * piece, piece), piece)
        value = dot(normed_ref[...], gci[:, lanes])
        for block in range(value.shape[0] // long):
            spot = tuple(block // 2 ** (heads - 1 - k) % 2 for k in range(heads))
            part_conv[spot + (slice(None), lanes)] = value[block * long : (block + 1) * long].astype(jnp.bfloat16)
        return unused

    lax.fori_loop(0, channels // piece, product_piece, 0)
    flow.start()

    for copy in wholes[2:]:
        copy.wait()
    width = gn.shape[1]

    def normed_piece(index, unused):
        lanes = pl.ds(pl.multiple_of(index * piece, piece), piece)
        gn[:, lanes] = contract(gci[...], wc[lanes, :], 1, 1) + contract(gz[...], wg[lanes, :], 1, 1)
        return unused

    lax.fori_loop(0, width // piece, normed_piece, 0)
    wide_s[...] = wide_ref[...]
    gain = wide_ref[0:1, :]

    def back(index, total):
        at = pl.ds(pl.multiple_of(index * 16, 16), 16)
        x, g = in_ref[at, :].astype(jnp.float32), gn[at, :]
        scale = lax.rsqrt(jnp.mean(x * x, axis=-1, keepdims=True) + EPS)
        scaled = g * gain
        share_of = jnp.mean(x * scaled, axis=-1, keepdims=True)
        gi_ref[at, :] = resid_ref[at, :] + scale * scaled - x * (scale * scale * scale * share_of)
        value = g * (x * scale)
        return total + value[:8] + value[8:]

    total = lax.fori_loop(0, tokens // 16, back, jnp.zeros((8, width), jnp.float32))
    wide_s[0:1, :] = jnp.sum(total, axis=0, keepdims=True)
    flow.advance(0)
    filler = jnp.zeros((LANES - wide_s.shape[0], width), jnp.float32)
    columns = turned(jnp.concatenate([wide_s[...], filler], axis=0))
    short = part_wide.shape[-2]
    for block in range(width // short):
        spot = tuple(block // 2 ** (heads - 1 - k) % 2 for k in range(heads))
        part_wide[spot] = columns[block * short : (block + 1) * short].astype(jnp.bfloat16)
    flow3.start()
    rest.advance(0)
    for stage in range(1, len(places)):
        flow.advance(stage)
        flow3.advance(stage - 1)
        rest.advance(stage)
        if stage == 2:
            moves[1].start()
    flow3.advance(len(places) - 1)

    flow.finish()
    flow3.finish()
    rest.finish()
    handed.wait_send()
    for move in moves:
        move.wait()


def finish(sizes, streamed, inside_values, parts, leaving, arrived, identity, span=64):
    places = bit_positions(sizes)
    stages = len(places)
    far = sorted(far_of(places))
    heads = sizes[0][1].bit_length() - 1
    tails = stages - heads
    along, slope, grad, pre, conv, xs, ext, gz, wc, wg = streamed
    normed = inside_values[1]
    tokens, channels = xs.shape
    width = normed.shape[1]
    devices = 2**stages
    half, wide = jnp.bfloat16, jnp.float32
    rows, thin = channels // devices, width // devices
    orders = [tuple(order) for order in orders_of(places)]
    conv_like = jax.ShapeDtypeStruct((width, channels), half)
    small_like = jax.ShapeDtypeStruct((channels, 2 * LANES), half)
    wide_like = jax.ShapeDtypeStruct((width, LANES), half)
    streams = halves((conv_like, small_like), *orders)
    third = halves((wide_like,), *orders)
    late = [(k, slice(0, part.shape[-1]), tuple(far_of(places))) for k, part in enumerate(parts)]

    def room(of, sizes_of):
        landing, blocks = [], []
        for array, cols, order in of:
            size, many = sizes_of[array], cols.stop - cols.start
            landing.append(pltpu.VMEM((2,) * (heads - 1) + (size * 2**tails, many), half))
            landing += [pltpu.VMEM((2,) * (stages - stage - 1) + (size, many), half) for stage in range(1, stages)]
            blocks.append(pltpu.VMEM((2,) * (stages - 1) + (size, many), half))
        return landing, blocks

    landing, blocks = room(streams, (thin, rows))
    landing3, blocks3 = room(third, (thin,))
    late_landing = landing_of(late, far, parts)
    marks = [len(landing), len(blocks), len(landing3), len(blocks3), len(late_landing)]
    inside = pl.BlockSpec(memory_space=pltpu.VMEM)
    anywhere = pl.BlockSpec(memory_space=pl.ANY)
    return pl.pallas_call(
        functools.partial(finish_kernel, places, streams, third, late, far, marks),
        in_specs=[anywhere] * 10 + [inside] * (len(inside_values) + 2) + [anywhere] * 4,
        input_output_aliases={25: 5, 26: 6},
        out_specs=[inside] * 5 + [anywhere] * 2,
        out_shape=[
            jax.ShapeDtypeStruct(normed.shape, wide),
            jax.ShapeDtypeStruct((thin, 2 * channels), wide),
            jax.ShapeDtypeStruct(parts[1].shape[-2:], wide),
            jax.ShapeDtypeStruct((rows, 2 * LANES), wide),
            jax.ShapeDtypeStruct((thin, LANES), wide),
        ]
        + [jax.ShapeDtypeStruct(values.shape, half) for values in leaving],
        scratch_shapes=landing + blocks + landing3 + blocks3 + late_landing
        + [pltpu.VMEM(value.shape, value.dtype) for value in streamed]
        + [
            pltpu.VMEM((tokens, channels), half),
            pltpu.VMEM((tokens, channels), half),
            pltpu.VMEM((16, channels), wide),
            pltpu.VMEM((8, channels), wide),
            pltpu.VMEM((8, channels), wide),
            pltpu.VMEM((2, 8, channels), wide),
            pltpu.VMEM((32, channels), wide),
            pltpu.VMEM(inside_values[-1].shape, wide),
            pltpu.VMEM((tokens, width), wide),
            pltpu.VMEM((2,) * heads + (thin * 2**tails, channels), half),
            pltpu.VMEM((2,) * heads + (rows * 2**tails, 2 * LANES), half),
            pltpu.VMEM((2,) * heads + (thin * 2**tails, LANES), half),
            pltpu.SemaphoreType.DMA((5, tokens // span)),
            pltpu.SemaphoreType.DMA((5,)),
            pltpu.SemaphoreType.DMA((2,)),
            pltpu.SemaphoreType.DMA((2, 2, 2)),
        ]
        + flights(streams)
        + flights(third)
        + flights(late),
        compiler_params=pltpu.CompilerParams(
            collective_id=identity, has_side_effects=True, vmem_limit_bytes=63 * 1024 * 1024
        ),
        name="finish",
    )(*streamed, *inside_values, *parts, *leaving, *arrived)


def chosen_of(target, room):
    lane = lax.broadcasted_iota(jnp.int32, target.shape, 1).astype(jnp.float32) * room
    return ((target >= lane) & (target < lane + room)).astype(jnp.float32)


def gate_kernel(room, experts, y_ref, xs_ref, normed_ref, in_ref, cot_ref, target_ref, wg_ref, wo_ref, wide_ref, chan_ref,
                gain_ref, n2_ref, resid_ref, z_ref, prob_ref, pick_ref, gated_t, normed_t):
    skip, gain = chan_ref[26:27, :], gain_ref[1:2, :]
    gate_in = dot(normed_ref[...], wg_ref[...])
    z_ref[...] = gate_in
    scanned = y_ref[...] + skip * xs_ref[...].astype(jnp.float32)
    gated = scanned * gate_in / (1.0 + jnp.exp(-gate_in))
    for at in range(0, gated.shape[1], LANES):
        gated_t[at : at + LANES, :] = gated[:, at : at + LANES].T.astype(jnp.bfloat16)
    for at in range(0, normed_ref.shape[1], LANES):
        normed_t[at : at + LANES, :] = normed_ref[:, at : at + LANES].astype(jnp.float32).T.astype(jnp.bfloat16)
    residual = in_ref[...].astype(jnp.float32) + dot(gated.astype(jnp.bfloat16), wo_ref[...])
    resid_ref[...] = residual
    scale = lax.rsqrt(jnp.mean(residual * residual, axis=-1, keepdims=True) + EPS)
    normed_two = (residual * scale * gain).astype(jnp.bfloat16)
    n2_ref[...] = normed_two
    logits = pltpu.roll(dot(normed_two, wide_ref[...]), LANES - 8, 1)
    lane = lax.broadcasted_iota(jnp.int32, logits.shape, 1)
    logits = jnp.where(lane < experts, logits, -1e30)
    powers = jnp.exp(logits - jnp.max(logits, axis=1, keepdims=True))
    powers = jnp.where(lane < experts, powers, 0.0)
    probability = powers / jnp.sum(powers, axis=1, keepdims=True)
    prob_ref[...] = probability
    gate = jnp.sum(probability * chosen_of(target_ref[...], room), axis=1, keepdims=True)
    pick_ref[...] = (cot_ref[...].astype(jnp.float32) * gate).astype(jnp.bfloat16)


def open_gate(y, xs, normed, rows_in, cotangent, target, weights, room, experts, block=3 * LANES):
    tokens, channels = y.shape
    width = rows_in.shape[1]
    shape, half, full = jax.ShapeDtypeStruct, jnp.bfloat16, jnp.float32

    def cut(values):
        return pl.BlockSpec((block, values.shape[1]), lambda i: (i, 0))

    def whole(values):
        return pl.BlockSpec(values.shape, lambda i: (0, 0))

    results = [
        shape((tokens, width), half),
        shape((tokens, width), full),
        shape((tokens, channels), full),
        shape((tokens, LANES), full),
        shape((tokens, width), half),
    ]
    turned_specs = [pl.BlockSpec((rows, block), lambda i: (0, i)) for rows in (channels, width)]
    return pl.pallas_call(
        functools.partial(gate_kernel, room, experts),
        grid=(tokens // block,),
        in_specs=[cut(values) for values in (y, xs, normed, rows_in, cotangent, target)]
        + [whole(values) for values in weights],
        out_specs=[cut(values) for values in results] + turned_specs,
        out_shape=results + [shape((channels, tokens), half), shape((width, tokens), half)],
        compiler_params=pltpu.CompilerParams(vmem_limit_bytes=63 * 1024 * 1024),
        name="open_gate",
    )(y, xs, normed, rows_in, cotangent, target, *weights)


def middle_kernel(room, picked_ref, back_ref, cot_ref, resid_ref, z_ref, y_ref, xs_ref, n2_ref, prob_ref, target_ref,
                  gated_t, normed_t, wo_ref, wide_ref, chan_ref, gain_ref,
                  out_ref, gres_ref, gy_ref, gz_ref, rows_ref, sum_out, sum_gate, mix_all, gz_all):
    step, steps = pl.program_id(0), pl.num_programs(0)

    @pl.when(step == 0)
    def _():
        rows_ref[...] = jnp.zeros_like(rows_ref)
        rows_ref[0:1, :] = gain_ref[0:1, :]

    size = out_ref.shape[0]
    gain = gain_ref[1:2, :]
    grad, picked = cot_ref[...].astype(jnp.float32), picked_ref[...].astype(jnp.float32)
    probability, chosen = prob_ref[...], chosen_of(target_ref[...], room)
    gate = jnp.sum(probability * chosen, axis=1, keepdims=True)
    residual = resid_ref[...]
    out_ref[...] = (residual + gate * picked).astype(jnp.bfloat16)
    grad_gate = jnp.sum(grad * picked, axis=1, keepdims=True)
    grad_logits = probability * (grad_gate * (chosen - gate))
    shifted_logits = pltpu.roll(grad_logits, 8, 1).astype(jnp.bfloat16)
    grad_two = back_ref[...].astype(jnp.float32) + contract(shifted_logits, wide_ref[...], 1, 1)
    rows_ref[...] += contract(shifted_logits, n2_ref[...], 0, 0)[: rows_ref.shape[0]]
    scale = lax.rsqrt(jnp.mean(residual * residual, axis=-1, keepdims=True) + EPS)
    rows_ref[1:2, :] += jnp.sum(grad_two * residual * scale, axis=0, keepdims=True)
    scaled = grad_two * gain
    share_of = jnp.mean(residual * scaled, axis=-1, keepdims=True)
    total = grad + scale * scaled - residual * (scale * scale * scale * share_of)
    gres_ref[...] = total
    mix = total.astype(jnp.bfloat16)
    at = pl.ds(pl.multiple_of(step * size, size), size)
    mix_all[at, :] = mix
    grad_gated = contract(mix, wo_ref[...], 1, 1)
    value = z_ref[...]
    bend = 1.0 / (1.0 + jnp.exp(-value))
    gy_ref[...] = grad_gated * value * bend
    scanned = y_ref[...] + chan_ref[26:27, :] * xs_ref[...].astype(jnp.float32)
    grad_z = (grad_gated * scanned * bend * (1.0 + value * (1.0 - bend))).astype(jnp.bfloat16)
    gz_ref[...] = grad_z
    gz_all[at, :] = grad_z

    @pl.when(step == steps - 1)
    def _():
        piece = 2 * LANES

        def some(index, unused):
            lanes = pl.ds(pl.multiple_of(index * piece, piece), piece)
            sum_out[:, lanes] = dot(gated_t[...], mix_all[:, lanes]).astype(jnp.bfloat16)
            return unused

        def other(index, unused):
            lanes = pl.ds(pl.multiple_of(index * piece, piece), piece)
            sum_gate[:, lanes] = dot(normed_t[...], gz_all[:, lanes]).astype(jnp.bfloat16)
            return unused

        lax.fori_loop(0, sum_out.shape[1] // piece, some, 0)
        lax.fori_loop(0, sum_gate.shape[1] // piece, other, 0)


def middle(blocks, turned_parts, weights, room, experts, block=192):
    tokens, width = blocks[0].shape
    channels = turned_parts[0].shape[0]
    shape, half, full = jax.ShapeDtypeStruct, jnp.bfloat16, jnp.float32

    def cut(values):
        return pl.BlockSpec((block, values.shape[1]), lambda i: (i, 0))

    def whole(values):
        return pl.BlockSpec(values.shape, lambda i: (0, 0))

    results = [
        shape((tokens, width), half),
        shape((tokens, width), full),
        shape((tokens, channels), full),
        shape((tokens, channels), half),
    ]
    sums = [shape((8 + experts, width), full), shape((channels, width), half), shape((width, channels), half)]
    return pl.pallas_call(
        functools.partial(middle_kernel, room),
        grid=(tokens // block,),
        in_specs=[cut(values) for values in blocks] + [whole(values) for values in turned_parts + weights],
        out_specs=[cut(values) for values in results] + [whole(values) for values in sums],
        out_shape=results + sums,
        scratch_shapes=[pltpu.VMEM((tokens, width), half), pltpu.VMEM((tokens, channels), half)],
        compiler_params=pltpu.CompilerParams(vmem_limit_bytes=63 * 1024 * 1024),
        name="middle",
    )(*blocks, *turned_parts, *weights)


def emit_kernel(gi_from, wo_from, wo_other, wi_from, wi_other, in_from, out_from, small_ref, thin_ref,
                gi, w_out, w_in, own_in, own_out, own_x, own_dt, own_taps, own_decay, own_router, *singles):
    gi[...] = gi_from[...]
    w_out[...] = wo_from[...].astype(jnp.float32) + wo_other[...].astype(jnp.float32)
    w_in[...] = wi_from[...].astype(jnp.float32) + wi_other[...].astype(jnp.float32)
    own_in[...] = in_from[...]
    own_out[...] = out_from[...]

    def columns_of(values):
        return jnp.concatenate([values, jnp.zeros((LANES - values.shape[0], LANES), jnp.float32)], axis=0).T

    size, thin = small_ref.shape[0], thin_ref.shape[0]
    first = small_ref[:, :LANES]
    own_x[...] = first[:, : R + 2 * NS]
    own_dt[...] = columns_of(first)[R + 2 * NS :, :size]
    by_row = columns_of(small_ref[:, LANES:])
    own_taps[...] = by_row[:KC, :size]
    own_decay[...] = by_row[8 : 8 + NS, :size]
    for k in range(3):
        singles[k][...] = by_row[24 + k : 25 + k, :size]
    by_row = columns_of(thin_ref[...])
    for k in range(2):
        singles[3 + k][...] = by_row[k : k + 1, :thin]
    own_router[...] = by_row[8 : 8 + own_router.shape[0], :thin]


def emit_outputs(gi, w_out, out_other, w_in, in_other, own_in, own_out, small, thin_part, experts, pieces=2):
    rows, thin = small.shape[0], thin_part.shape[0]
    full = jnp.float32

    def cut(values):
        return pl.BlockSpec((values.shape[0] // pieces, values.shape[1]), lambda i: (i, 0))

    def whole(shape):
        return pl.BlockSpec(shape, lambda i: (0, 0))

    large = [gi, w_out, out_other, w_in, in_other]
    results = [gi, w_out, w_in]
    still = [own_in, own_out, small, thin_part]
    shapes = [own_in.shape, own_out.shape, (rows, R + 2 * NS), (R, rows), (KC, rows), (NS, rows), (experts, thin)]
    shapes += [(1, rows)] * 3 + [(1, thin)] * 2
    return pl.pallas_call(
        emit_kernel,
        grid=(pieces,),
        in_specs=[cut(values) for values in large] + [whole(values.shape) for values in still],
        out_specs=[cut(values) for values in results] + [whole(shape) for shape in shapes],
        out_shape=[jax.ShapeDtypeStruct(values.shape, full) for values in results]
        + [jax.ShapeDtypeStruct(shape, full) for shape in shapes],
        name="emit_outputs",
    )(*large, *still)


def expert_kernel(slices, *refs):
    tokens_ref, grads_ref, column_ref = refs[:3]
    even = range(0, slices, 2)
    odd = range(1, slices, 2)
    weights_in, weight_out = refs[3 : 3 + len(even)], refs[3 + len(even)]
    outs = refs[4 + len(even) :]
    picked_ref, back_ref = outs[:2]
    sums_in = outs[2 : 2 + len(even)]
    kept_out, leaving_out, arriving_out = outs[2 + len(even) : 5 + len(even)]
    (sent, got, answer, returned, w_in, w_out, hidden, total, active, slope, inner, sum_out, pair_out, pair_in, far_out,
     rows_t, send_sems, recv_sems, weight_sems, sum_sems, spread_sems, mate_sems, far_sems, moved_sems) = outs[
        5 + len(even) :
    ]
    experts, room, width = sent.shape[1:]
    places = experts * room
    me = lax.axis_index("exp")
    here = lax.axis_index("ctx")
    levels = slices.bit_length() - 1

    loads = [pltpu.make_async_copy(weight_out, w_out.at[0], weight_sems.at[slices])]
    for k, s in enumerate(even):
        loads.append(pltpu.make_async_copy(weights_in[k], w_in.at[s], weight_sems.at[s]))
    for load in loads:
        load.start()

    barrier = pltpu.get_barrier_semaphore()
    mates = [partner(("ctx", level)) for level in range(levels)]
    for step in range(1, experts):
        pl.semaphore_signal(barrier, inc=1, device_id=(here, lax.rem(me + step, experts)), device_id_type=MESH)
    for mate in mates:
        pl.semaphore_signal(barrier, inc=1, device_id=mate, device_id_type=MESH)

    def exchange(source, target, kind):
        copies = []
        for step in range(1, experts):
            peer = lax.rem(me + step, experts)
            copy = pltpu.make_async_remote_copy(
                src_ref=source.at[peer],
                dst_ref=target.at[me],
                send_sem=send_sems.at[kind, step],
                recv_sem=recv_sems.at[kind, step],
                device_id=(here, peer),
                device_id_type=MESH,
            )
            copy.start()
            copies.append(copy)
        target[me] = source[me]
        return copies

    def hand(source, target, sems, level):
        copy = pltpu.make_async_remote_copy(
            src_ref=source,
            dst_ref=target,
            send_sem=sems.at[0],
            recv_sem=sems.at[1],
            device_id=mates[level],
            device_id_type=MESH,
        )
        copy.start()
        return copy

    def arrive(copies):
        for copy in copies:
            copy.wait_recv()

    open_sends = []

    def spread(level):
        step = 2**level
        copies = [hand(w_out.at[s], w_out.at[s + step], spread_sems.at[1, s + step], level) for s in range(0, slices, 2 * step)]
        open_sends.extend(copies)
        return copies

    spots = lax.broadcasted_iota(jnp.int32, (column_ref.shape[0], places), 1).astype(jnp.float32)
    columns = jnp.concatenate([column_ref[...]] * (places // LANES), axis=1)
    finder = (spots == columns).astype(jnp.float32).astype(jnp.bfloat16)
    sent[0] = contract(finder, tokens_ref[...], 0, 0).astype(jnp.bfloat16).reshape(experts, room, width)
    pl.semaphore_wait(barrier, experts - 1 + levels)
    first = exchange(sent.at[0], got.at[0], 0)
    for load in loads:
        load.wait()
    widening = [spread(levels - 1)]
    paired = [hand(w_in.at[s], w_in.at[s + 1], spread_sems.at[0, s], 0) for s in even]
    sent[1] = contract(finder, grads_ref[...], 0, 0).astype(jnp.bfloat16).reshape(experts, room, width)
    second = exchange(sent.at[1], got.at[1], 1)

    arrive(first)
    rows = got[0].reshape(places, width)
    for s in list(even) + list(odd):
        if s == 1:
            arrive(paired)
        hidden[...] = dot(rows, w_in[s])

        def curve(index, unused):
            at = pl.ds(pl.multiple_of(index * ROWS_AT_ONCE, ROWS_AT_ONCE), ROWS_AT_ONCE)
            value = hidden[at, :]
            bell = 0.5 + 0.5 * lax.erf(value * 0.7071067811865476)
            active[s, at, :] = (value * bell).astype(jnp.bfloat16)
            slope[s, at, :] = bell + value * (jnp.exp(-0.5 * value * value) * 0.3989422804014327)
            return unused

        lax.fori_loop(0, places // ROWS_AT_ONCE, curve, 0)

    for level in reversed(range(levels - 1)):
        arrive(widening[-1])
        widening.append(spread(level))
    for s in list(even) + list(odd):
        if s == 1:
            arrive(widening[-1])
        product = dot(active[s], w_out[s])
        total[...] = product if s == 0 else total[...] + product
    answer[0] = total[...].astype(jnp.bfloat16).reshape(experts, room, width)
    third = exchange(answer.at[0], returned.at[0], 2)

    arrive(second)
    pulled = got[1].reshape(places, width)
    for s in range(slices):
        inner[s] = (contract(pulled, w_out[s], 1, 1) * slope[s]).astype(jnp.bfloat16)
        product = contract(inner[s], w_in[s], 1, 1)
        total[...] = product if s == 0 else total[...] + product
    answer[1] = total[...].astype(jnp.bfloat16).reshape(experts, room, width)
    fourth = exchange(answer.at[1], returned.at[1], 3)
    joining = []
    for s in list(odd) + list(even):
        sum_out[s] = contract(active[s], pulled, 0, 0).astype(jnp.bfloat16)
        if s % 2:
            joining.append(hand(sum_out.at[s], pair_out.at[s // 2], mate_sems.at[0, s // 2], 0))

    def add_into(target, addend):
        def some(index, unused):
            at = pl.ds(pl.multiple_of(index * 4 * ROWS_AT_ONCE, 4 * ROWS_AT_ONCE), 4 * ROWS_AT_ONCE)
            target[at, :] = target[at, :] + addend[at, :]
            return unused

        lax.fori_loop(0, target.shape[0] // (4 * ROWS_AT_ONCE), some, 0)

    arrive(joining)
    for k, s in enumerate(even):
        add_into(sum_out.at[s], pair_out.at[k])

    def pass_on(level):
        step = 2**level
        return [
            hand(sum_out.at[s + step], far_out.at[slices // step // 2 - 1 + s // (2 * step)], far_sems.at[level, s // (2 * step)], level)
            for s in range(0, slices, 2 * step)
        ]

    open_sends.extend(joining)
    for level in range(1, levels - 1):
        passing = pass_on(level)
        arrive(passing)
        open_sends.extend(passing)
        step = 2**level
        for s in range(0, slices, 2 * step):
            add_into(sum_out.at[s], far_out.at[slices // step // 2 - 1 + s // (2 * step)])
    stores = [
        pltpu.make_async_copy(sum_out.at[0], kept_out, sum_sems.at[len(even)]),
        pltpu.make_async_copy(sum_out.at[slices // 2], leaving_out, sum_sems.at[len(even) + 1]),
    ]
    for store in stores:
        store.start()
    move = row_half(sum_out.at[slices // 2], arriving_out, moved_sems, ("ctx", levels - 1), 0)
    move.start()
    for low in range(0, places, LANES):
        for left in range(0, width, LANES):
            square = got[0].reshape(places, width)[low : low + LANES, left : left + LANES].astype(jnp.float32).T
            rows_t[left : left + LANES, low : low + LANES] = square.astype(jnp.bfloat16)
    for copy in paired:
        copy.wait_send()
    joined = []
    for s in list(odd) + list(even):
        w_in[s] = dot(rows_t[...], inner[s]).astype(jnp.bfloat16)
        if s % 2:
            joined.append(hand(w_in.at[s], pair_in.at[s // 2], mate_sems.at[1, s // 2], 0))
    arrive(joined)
    for k, s in enumerate(even):
        add_into(w_in.at[s], pair_in.at[k])
        stores.append(pltpu.make_async_copy(w_in.at[s], sums_in[k], sum_sems.at[k]))
        stores[-1].start()

    arrive(third)
    picked_ref[...] = dot(finder, returned[0].reshape(places, width)).astype(jnp.bfloat16)
    arrive(fourth)
    back_ref[...] = dot(finder, returned[1].reshape(places, width)).astype(jnp.bfloat16)
    for store in stores:
        store.wait()
    move.wait()
    for copies in (first, second, third, fourth, joined, open_sends):
        for copy in copies:
            copy.wait_send()


def run_experts(rows, grads, target, weights_in, weight_out, experts, room, identity):
    slices = 2 * len(weights_in)
    tokens, width = rows.shape
    inner_width = weight_out.shape[0]
    places = experts * room
    inside = pl.BlockSpec(memory_space=pltpu.VMEM)
    anywhere = pl.BlockSpec(memory_space=pl.ANY)
    half = jnp.bfloat16
    count = len(weights_in)
    out = pl.pallas_call(
        functools.partial(expert_kernel, slices),
        in_specs=[inside] * 3 + [anywhere] * (count + 1),
        out_specs=[inside] * 2 + [anywhere] * (count + 3),
        out_shape=[jax.ShapeDtypeStruct(rows.shape, half)] * 2
        + [jax.ShapeDtypeStruct(weight.shape, half) for weight in weights_in]
        + [jax.ShapeDtypeStruct(weight_out.shape, half)] * 3,
        scratch_shapes=[pltpu.VMEM((2, experts, room, width), half)] * 4
        + [
            pltpu.VMEM((slices, width, inner_width), half),
            pltpu.VMEM((slices, inner_width, width), half),
            pltpu.VMEM((places, inner_width), jnp.float32),
            pltpu.VMEM((places, width), jnp.float32),
            pltpu.VMEM((slices, places, inner_width), half),
            pltpu.VMEM((slices, places, inner_width), jnp.float32),
            pltpu.VMEM((slices, places, inner_width), half),
            pltpu.VMEM((slices, inner_width, width), half),
            pltpu.VMEM((count, inner_width, width), half),
            pltpu.VMEM((count, width, inner_width), half),
            pltpu.VMEM((count, inner_width, width), half),
            pltpu.VMEM((width, places), half),
            pltpu.SemaphoreType.DMA((4, experts)),
            pltpu.SemaphoreType.DMA((4, experts)),
            pltpu.SemaphoreType.DMA((slices + 1,)),
            pltpu.SemaphoreType.DMA((count + 2,)),
            pltpu.SemaphoreType.DMA((2, slices, 2)),
            pltpu.SemaphoreType.DMA((2, count, 2)),
            pltpu.SemaphoreType.DMA((slices, count, 2)),
            pltpu.SemaphoreType.DMA((2, 2)),
        ],
        compiler_params=pltpu.CompilerParams(
            collective_id=identity, has_side_effects=True, vmem_limit_bytes=63 * 1024 * 1024
        ),
        name="run_experts",
    )(rows, grads, target, *weights_in, weight_out)
    return out[0], out[1], list(out[2 : 2 + count]), out[2 + count :]


def flipped(value, level):
    count = lax.axis_size("ctx")
    return lax.ppermute(value, "ctx", [(source, source ^ (1 << level)) for source in range(count)])


def spread_slices(own, far):
    levels = lax.axis_size("ctx").bit_length() - 1
    slices = {0: own, 1 << (levels - 1): far}
    for level in reversed(range(1, levels - 1)):
        for offset in sorted(slices):
            slices[offset + (1 << level)] = flipped(slices[offset], level)
    return [slices[offset] for offset in sorted(slices)]


def collect_slices(sums):
    levels = lax.axis_size("ctx").bit_length() - 1
    for level in range(1, levels - 1):
        arrived = [flipped(values, level).astype(jnp.float32) for values in sums[1::2]]
        sums = [
            (values.astype(jnp.float32) + other).astype(jnp.bfloat16) for values, other in zip(sums[::2], arrived)
        ]
    return sums


def body(
    inputs,
    segments,
    routes,
    cotangent,
    norm_gain,
    in_proj,
    conv_taps,
    conv_bias,
    x_proj,
    dt_proj,
    dt_bias,
    log_decay,
    skip_gain,
    out_proj,
    moe_gain,
    router,
    expert_in,
    expert_out,
):
    experts = router.shape[1]
    half_rows = norm_gain.shape[0]
    small = (
        x_proj,
        dt_proj,
        conv_taps.T,
        log_decay.T,
        jnp.stack([conv_bias, dt_bias, skip_gain]),
        jnp.stack([norm_gain, moe_gain]),
        router.T,
    )
    sizes = [(name, lax.axis_size(name)) for name in ("ctx", "exp")]
    weights, partial, begun, *prior = gather_all(
        sizes, small, in_proj, out_proj, inputs[0], segments, expert_in[0], 0
    )
    tokens_here = inputs.shape[1]
    capacity = 5 * tokens_here // (4 * experts)
    room = -(-capacity // 16) * 16
    (
        scan_rows,
        products,
        normed_one,
        b_turned,
        c_turned,
        rates,
        by_channel,
        gain_rows,
        delta_low,
        same_rows,
        target,
        kept,
        (conv_ext, conv_out, xs_val, dt_pre, masked_step, push),
        (full_gate, full_out),
        far_in,
    ) = scan_forward(
        sizes,
        inputs[0],
        prior,
        (segments, routes.reshape(1, tokens_here)),
        weights,
        room,
        partial,
        expert_in[0],
        begun,
        3,
    )
    weights_in = spread_slices(expert_in[0], far_in)
    full_conv, full_channel, full_width = weights
    normed_two, residual, gate_z, probability, grad_pick, gated_turned, normed_turned = open_gate(
        scan_rows,
        xs_val,
        normed_one,
        inputs[0],
        cotangent[0],
        target,
        [full_gate, full_out, full_width, by_channel, gain_rows],
        room,
        experts,
    )
    picked, grad_from_experts, grad_expert_in, (kept_out, leaving_out, begun_out) = run_experts(
        normed_two, grad_pick, target, weights_in, expert_out[0], experts, room, 2
    )
    kept_in, leaving = collect_slices(grad_expert_in)
    out_block, grad_resid, grad_y, grad_z, wide_rows, grad_out_proj, grad_gate_proj = middle(
        [picked, grad_from_experts, cotangent[0], residual, gate_z, scan_rows, xs_val, normed_two, probability, target],
        [gated_turned, normed_turned],
        [full_out, full_width, by_channel, gain_rows],
        room,
        experts,
    )
    along_b, slope, grad_bs, grad_cs, grad_a, partial_sums, begun_in = scan_backward(
        sizes,
        masked_step,
        push,
        grad_y,
        b_turned,
        c_turned,
        rates,
        products,
        (grad_gate_proj, grad_out_proj),
        kept,
        leaving,
        4,
    )
    finished = finish(
        sizes,
        (along_b, slope, grad_y, dt_pre, conv_out, xs_val, conv_ext, grad_z, full_conv, full_gate),
        (
            normed_turned,
            inputs[0],
            grad_resid,
            full_channel,
            jnp.pad(jnp.concatenate([grad_bs, grad_cs], axis=1), ((0, 0), (R, LANES - R - 2 * NS))),
            delta_low,
            same_rows,
            by_channel,
            grad_a,
            rates,
            wide_rows,
        ),
        partial_sums,
        (leaving, leaving_out),
        (begun_in, begun_out),
        1,
    )
    grad_inputs, own_in, own_out, own_small, own_thin, arrived, arrived_out = finished
    grad_inputs, grad_w_out, grad_w_in, own_in, own_out, own_x, own_dt, own_taps, own_decay, own_router, *vectors = (
        emit_outputs(
            grad_inputs, kept_out, arrived_out, kept_in, arrived, own_in, own_out, own_small, own_thin, experts
        )
    )
    own_bias, own_dtbias, own_skip, own_norm, own_moe = [values[0] for values in vectors]
    return (
        out_block[None],
        grad_inputs[None],
        own_norm,
        own_in,
        own_taps.T,
        own_bias,
        own_x,
        own_dt,
        own_dtbias,
        own_decay.T,
        own_skip,
        own_out,
        own_moe,
        own_router.T,
        grad_w_in[None],
        grad_w_out[None],
    )


def solution(mesh):
    placed = (
        P("exp", "ctx", None),
        P("exp", "ctx"),
        P("exp", "ctx", None),
        P("exp", "ctx", None),
        P(("ctx", "exp")),
        P(("ctx", "exp"), None),
        P(("ctx", "exp"), None),
        P(("ctx", "exp")),
        P(("ctx", "exp"), None),
        P(None, ("ctx", "exp")),
        P(("ctx", "exp")),
        P(("ctx", "exp"), None),
        P(("ctx", "exp")),
        P(("ctx", "exp"), None),
        P(("ctx", "exp")),
        P(("ctx", "exp"), None),
        P("exp", None, "ctx"),
        P("exp", "ctx", None),
    )
    return jax.shard_map(
        body,
        mesh=mesh,
        in_specs=placed,
        out_specs=(
            P("exp", "ctx", None),
            P("exp", "ctx", None),
            P(("ctx", "exp")),
            P(("ctx", "exp"), None),
            P(("ctx", "exp"), None),
            P(("ctx", "exp")),
            P(("ctx", "exp"), None),
            P(None, ("ctx", "exp")),
            P(("ctx", "exp")),
            P(("ctx", "exp"), None),
            P(("ctx", "exp")),
            P(("ctx", "exp"), None),
            P(("ctx", "exp")),
            P(("ctx", "exp"), None),
            P("exp", None, "ctx"),
            P("exp", "ctx", None),
        ),
        check_vma=False,
    )
```

```python
import functools

import jax
import jax.numpy as jnp
from jax import lax
from jax.experimental import pallas as pl
from jax.experimental.pallas import tpu as pltpu
from jax.sharding import PartitionSpec as P

D = 768
DI = 1536
NS = 16
R = 48
KC = 4
LANES = 128
UNROLL = 8
LOG2E = 1.4426950408889634


EPS = 1e-05
MESH = pl.DeviceIdType.MESH
ROWS_AT_ONCE = 16
EDGE = 16

def tile(ref, base, lanes):
    return ref[pl.ds(pl.multiple_of(base, UNROLL), UNROLL), lanes]

def row(rows_now, place):
    return jnp.broadcast_to(rows_now[place : place + 1], (NS, LANES))

def cost(tokens, channels, share):
    size = tokens * channels * NS
    return pl.CostEstimate(flops=size * share, transcendentals=size, bytes_accessed=size * share)


def pick(channels):
    return 512 if channels % 512 == 0 else 128


def bit_positions(sizes):
    return [(axis, size.bit_length() - 2 - k) for axis, size in sizes for k in range(size.bit_length() - 1)]


def own_bit(place):
    axis, level = place
    return lax.rem(lax.axis_index(axis) // 2**level, 2)


def partner(place):
    axis, level = place
    where = {"ctx": lax.axis_index("ctx"), "exp": lax.axis_index("exp")}
    where[axis] = where[axis] + (1 - 2 * own_bit(place)) * 2**level
    return (where["ctx"], where["exp"])


def greet(places, *others):
    barrier = pltpu.get_barrier_semaphore()
    for device in [partner(place) for place in places] + list(others):
        pl.semaphore_signal(barrier, inc=1, device_id=device, device_id_type=MESH)
    return len(places) + len(others)


def meet(places, *others):
    count = greet(places, *others)
    pl.semaphore_wait(pltpu.get_barrier_semaphore(), count)


class GatherFlow:
    def __init__(self, places, streams, dims, shards, wholes, send_sems, recv_sems, local_sems):
        self.places, self.streams, self.dims, self.shards, self.wholes = places, streams, dims, shards, wholes
        self.sems = send_sems, recv_sems, local_sems
        self.bits = [own_bit(place) for place in places]

    def view(self, number, have):
        array, cols, order, begin = self.streams[number]
        index = tuple(slice(None) if p in have else self.bits[p] for p in self.dims)
        return self.wholes[array].at[index + (slice(None), cols)]

    def shard(self, number):
        array, cols, order, begin = self.streams[number]
        return self.shards[array].at[(slice(None),) * (begin + 1) + (cols,)]

    def own(self, number):
        array, cols, order, begin = self.streams[number]
        return pltpu.make_async_copy(self.shard(number), self.view(number, order[:begin]), self.sems[2].at[number])

    def flight(self, number, stage):
        array, cols, order, begin = self.streams[number]
        target = self.view(number, order[: begin + stage])
        return pltpu.make_async_remote_copy(
            src_ref=self.shard(number) if stage == 0 else target,
            dst_ref=target,
            send_sem=self.sems[0].at[number, stage],
            recv_sem=self.sems[1].at[number, stage],
            device_id=partner(self.places[order[begin + stage]]),
            device_id_type=MESH,
        )

    def stages(self, number):
        array, cols, order, begin = self.streams[number]
        return len(order) - begin

    def start(self):
        for number in range(len(self.streams)):
            self.flight(number, 0).start()
        for number in range(len(self.streams)):
            self.own(number).start()

    def advance(self, stage):
        for number in range(len(self.streams)):
            if stage >= self.stages(number):
                continue
            if stage == 0:
                self.own(number).wait()
            self.flight(number, stage).wait_recv()
            if stage + 1 < self.stages(number):
                self.flight(number, stage + 1).start()

    def finish(self):
        for number in range(len(self.streams)):
            for stage in range(self.stages(number)):
                self.flight(number, stage).wait_send()


def pack_small(small, square, channel_pack, width_pack):
    x_ref, dt_ref, taps_ref, decay_ref, vector_ref, pair_ref, router_ref = small
    rows, thin = channel_pack.shape[0], width_pack.shape[0]

    def laid(*pieces):
        square[...] = jnp.zeros_like(square)
        for first, ref in pieces:
            square[first : first + ref.shape[0], : ref.shape[1]] = ref[...].astype(jnp.float32)
        return square[...]

    dt_part = pltpu.roll(laid((0, dt_ref)).T, R + 2 * NS, 1)
    mix = laid((0, x_ref)) + dt_part
    channel_pack[:, :LANES] = mix[:rows].astype(jnp.bfloat16)
    turned_rows = laid((0, taps_ref), (8, decay_ref), (24, vector_ref)).T
    channel_pack[:, LANES:] = turned_rows[:rows].astype(jnp.bfloat16)
    width_pack[...] = laid((0, pair_ref), (8, router_ref)).T[:thin].astype(jnp.bfloat16)


def gather_kernel(places, streams, extra_streams, far, *refs):
    small = refs[:7]
    in_ref, out_ref, rows_ref, ids_ref, leaving = refs[7:12]
    extra = 2
    wholes, prior_ref, prior_ids, arriving = refs[12:17], refs[17], refs[18], refs[19]
    (square, channel_pack, width_pack, send_sems, recv_sems, local_sems, late_send, late_recv, late_local,
     edge_sems, moved_sems) = refs[20:]
    split = in_ref.shape[1] // 2
    shards = (in_ref.at[:, :split], channel_pack, width_pack, in_ref.at[:, split:], out_ref)
    count = 3
    flow = GatherFlow(
        places, streams, range(len(places)), shards[:count], wholes[:count], send_sems, recv_sems, local_sems
    )
    late = GatherFlow(
        places, extra_streams, far, shards[count:], wholes[count:], late_send, late_recv, late_local
    )
    blocks = lax.axis_size("ctx")
    here, line = lax.axis_index("ctx"), lax.axis_index("exp")
    count_met = greet(places, (lax.rem(here + 1, blocks), line), (lax.rem(here + blocks - 1, blocks), line))
    pack_small(small, square, channel_pack, width_pack)
    pl.semaphore_wait(pltpu.get_barrier_semaphore(), count_met)
    flow.start()
    tokens = rows_ref.shape[0]
    edges = [
        pltpu.make_async_remote_copy(
            src_ref=source,
            dst_ref=target,
            send_sem=edge_sems.at[0, k],
            recv_sem=edge_sems.at[1, k],
            device_id=(lax.rem(here + 1, blocks), line),
            device_id_type=MESH,
        )
        for k, (source, target) in enumerate(
            (
                (rows_ref.at[pl.ds(tokens - EDGE, EDGE)], prior_ref),
                (ids_ref.at[:, pl.ds(tokens - LANES, LANES)], prior_ids),
            )
        )
    ]
    for edge in edges:
        edge.start()
    move = row_half(leaving, arriving, moved_sems, ("ctx", blocks.bit_length() - 2), 0)
    move.start()
    stages, behind = len(places), len(far)
    for stage in range(stages):
        flow.advance(stage)
        if stage == behind - 2:
            late.start()
        if stage >= behind and stage - behind < behind:
            late.advance(stage - behind)
    for stage in range(stages - behind, behind):
        late.advance(stage)
    flow.finish()
    late.finish()
    for edge in edges:
        edge.wait()
    move.wait()


def orders_of(places):
    core = places.index(("ctx", 0))
    rows = [k for k, place in enumerate(places) if place[0] == "ctx" and place[1] > 0]
    near = places.index(("exp", 0))
    return [core] + rows + [near] + far_of(places), [core, near] + rows + far_of(places)


def far_of(places):
    return [k for k, place in sorted(enumerate(places), key=lambda item: item[1][1]) if place[0] == "exp" and place[1] > 0]


def halves(arrays, first, second, begin=None):
    streams = []
    for array, values in enumerate(arrays):
        width = values.shape[-1]
        rest = () if begin is None else (begin,)
        if width % (2 * LANES) == 0:
            count = 4 if width % (4 * LANES) == 0 and width >= 1024 else 2
            for k in range(count):
                part = (k % 2) * (count // 2) + k // 2
                cols = slice(part * width // count, (part + 1) * width // count)
                streams.append((array, cols, second if k % 2 else first) + rest)
        else:
            streams.append((array, slice(0, width), first if array % 2 else second) + rest)
    return streams


def gather_orders(places):
    return [tuple(reversed(order)) for order in orders_of(places)]


def gather_all(sizes, small, in_proj, out_proj, rows_in, ids, leaving, identity):
    places = bit_positions(sizes)
    stages = len(places)
    far = sorted(far_of(places))
    half = jnp.bfloat16
    rows, thin, split = small[0].shape[0], in_proj.shape[0], in_proj.shape[1] // 2
    shape = jax.ShapeDtypeStruct
    shards = shape((thin, split), half), shape((rows, 2 * LANES), half), shape((thin, LANES), half)
    extra = shape((thin, split), half), shape(out_proj.shape, half)
    streams = halves(shards, *gather_orders(places), begin=0)
    late = [(k, slice(0, part.shape[1]), tuple(reversed(far_of(places))), 0) for k, part in enumerate(extra)]
    anywhere = pl.BlockSpec(memory_space=pl.ANY)
    inside = pl.BlockSpec(memory_space=pltpu.VMEM)
    out = pl.pallas_call(
        functools.partial(gather_kernel, places, streams, late, far),
        in_specs=[inside] * 7 + [anywhere] * 5,
        out_specs=[anywhere] * 8,
        out_shape=[shape((2,) * stages + shard.shape, half) for shard in shards]
        + [shape((2,) * len(far) + part.shape, half) for part in extra]
        + [shape((EDGE, rows_in.shape[1]), half), shape((1, LANES), jnp.int32), shape(leaving.shape, half)],
        scratch_shapes=[
            pltpu.VMEM((LANES, LANES), jnp.float32),
            pltpu.VMEM((rows, 2 * LANES), half),
            pltpu.VMEM((thin, LANES), half),
            pltpu.SemaphoreType.DMA((len(streams), stages)),
            pltpu.SemaphoreType.DMA((len(streams), stages)),
            pltpu.SemaphoreType.DMA((len(streams),)),
            pltpu.SemaphoreType.DMA((len(late), len(far))),
            pltpu.SemaphoreType.DMA((len(late), len(far))),
            pltpu.SemaphoreType.DMA((len(late),)),
            pltpu.SemaphoreType.DMA((2, 2)),
            pltpu.SemaphoreType.DMA((2, 2)),
        ],
        compiler_params=pltpu.CompilerParams(
            collective_id=identity, has_side_effects=True, vmem_limit_bytes=63 * 1024 * 1024
        ),
        name="gather_all",
    )(*small, in_proj, out_proj, rows_in, ids, leaving)
    return [whole.reshape((-1,) + whole.shape[stages + 1 :]) for whole in out[:3]], out[3:5], out[7], out[5], out[6]


class ReduceFlow:
    def __init__(self, places, streams, dims, parts, totals, landing, send_sems, recv_sems):
        self.places, self.streams, self.dims, self.parts, self.totals = places, streams, dims, parts, totals
        self.landing, self.sems = landing, (send_sems, recv_sems)
        self.bits = [own_bit(place) for place in places]
        self.first = []
        for array, cols, order in streams:
            self.first.append(sum(len(other[2]) for other in streams[: len(self.first)]))

    def spot(self, number, stage):
        return self.landing[self.first[number] + stage]

    def side(self, number, stage, value):
        array, cols, order = self.streams[number]
        left = [p for p in self.dims if p not in order[:stage]]
        index = tuple(value if p == order[stage] else slice(None) for p in left)
        if stage == 0:
            return self.parts[array].at[index + (slice(None), cols)]
        return self.spot(number, stage - 1).at[index]

    def flight(self, number, stage):
        order = self.streams[number][2]
        return pltpu.make_async_remote_copy(
            src_ref=self.side(number, stage, 1 - self.bits[order[stage]]),
            dst_ref=self.spot(number, stage),
            send_sem=self.sems[0].at[number, stage],
            recv_sem=self.sems[1].at[number, stage],
            device_id=partner(self.places[order[stage]]),
            device_id_type=MESH,
        )

    def start(self):
        for number in range(len(self.streams)):
            self.flight(number, 0).start()

    def advance(self, stage):
        for number, (array, cols, order) in enumerate(self.streams):
            if stage >= len(order):
                continue
            self.flight(number, stage).wait_recv()
            mine = self.side(number, stage, self.bits[order[stage]])
            there = self.spot(number, stage)
            depth = len(self.dims) - stage - 1
            final = stage + 1 == len(order)
            if depth == 0:
                self.totals[array][:, cols] = there[...].astype(jnp.float32) + mine[...].astype(jnp.float32)
                continue

            def add(index, unused, there=there, mine=mine, depth=depth, final=final, array=array, cols=cols):
                at = tuple(lax.rem(index // 2 ** (depth - 1 - k), 2) for k in range(depth))
                value = there[at] + mine[at]
                if final:
                    self.totals[array][at + (slice(None), cols)] = value
                else:
                    there[at] = value
                return unused

            lax.fori_loop(0, 2**depth, add, 0)
            if not final:
                self.flight(number, stage + 1).start()

    def finish(self):
        for number in range(len(self.streams)):
            for stage in range(len(self.streams[number][2])):
                self.flight(number, stage).wait_send()


def landing_of(streams, dims, divided):
    landing = []
    for array, cols, order in streams:
        for stage in range(len(order)):
            rows = divided[array].shape[-2]
            landing.append(pltpu.VMEM((2,) * (len(dims) - stage - 1) + (rows, cols.stop - cols.start), jnp.bfloat16))
    return landing


def flights(streams):
    shape = (len(streams), max(len(order) for array, cols, order in streams))
    return [pltpu.SemaphoreType.DMA(shape)] * 2


def dot(left, right):
    return jnp.dot(left, right, preferred_element_type=jnp.float32)


def contract(left, right, left_dim, right_dim):
    return lax.dot_general(left, right, (((left_dim,), (right_dim,)), ((), ())), preferred_element_type=jnp.float32)


def lanes_of(group, width, k):
    return pl.ds(pl.multiple_of(group * width + k * LANES, LANES), LANES)


def spread_columns(source_ref, wide_ref):
    def chunk(index, unused):
        base = pl.multiple_of(index * LANES, LANES)
        now = source_ref[:, pl.ds(base, LANES)]
        for place in range(LANES):
            wide_ref[base + place] = jnp.broadcast_to(now[:, place : place + 1], (NS, LANES))
        return unused

    lax.fori_loop(0, source_ref.shape[1] // LANES, chunk, 0)


def end_pass(width, step_ref, push_ref, wide_b, rate_ref, state_ref, hook):
    rows, channels = step_ref.shape
    count = width // LANES

    def group_body(group, unused):
        pieces = [lanes_of(group, width, k) for k in range(count)]
        rates = [rate_ref[:, lanes] for lanes in pieces]

        def block(index, states):
            states = list(states)
            steps = [tile(step_ref, index * UNROLL, lanes) for lanes in pieces]
            pushes = [tile(push_ref, index * UNROLL, lanes) for lanes in pieces]
            for place in range(UNROLL):
                b_now = wide_b[index * UNROLL + place]
                for k in range(count):
                    decay = jnp.exp2(row(steps[k], place) * rates[k])
                    states[k] = decay * states[k] + b_now * row(pushes[k], place)
            return tuple(states)

        zero = jnp.zeros((NS, LANES), jnp.float32)
        states = lax.fori_loop(0, rows // UNROLL, block, (zero,) * count)
        for k, lanes in enumerate(pieces):
            state_ref[:, lanes] = states[k]
        hook(group)
        return unused

    lax.fori_loop(0, channels // width, group_body, 0)


def out_pass(width, step_ref, push_ref, wide_b, wide_c, rate_ref, state_ref, y_ref, kept_buf, kept_copy, hook):
    rows, channels = step_ref.shape
    count = width // LANES
    span = kept_buf.shape[1]
    blocks = rows // span

    def time_body(number, unused):
        slot = lax.rem(number, 2)

        @pl.when(number >= 2)
        def _():
            kept_copy(number - 2, slot).wait()

        def group_body(group, unused_inner):
            pieces = [lanes_of(group, width, k) for k in range(count)]
            rates = [rate_ref[:, lanes] for lanes in pieces]

            def block(index, states):
                states = list(states)
                base = number * span + index * UNROLL
                steps = [tile(step_ref, base, lanes) for lanes in pieces]
                pushes = [tile(push_ref, base, lanes) for lanes in pieces]
                trees = [Tree(True) for k in range(count)]
                for place in range(UNROLL):
                    b_now = wide_b[base + place]
                    c_now = wide_c[base + place]
                    for k, lanes in enumerate(pieces):
                        decay = jnp.exp2(row(steps[k], place) * rates[k])
                        states[k] = decay * states[k] + b_now * row(pushes[k], place)
                        kept_buf[slot, index * UNROLL + place, :, lanes] = states[k].astype(kept_buf.dtype)
                        trees[k].push(place, states[k] * c_now)
                for k, lanes in enumerate(pieces):
                    y_ref[pl.ds(pl.multiple_of(base, UNROLL), UNROLL), lanes] = trees[k].result
                return tuple(states)

            states = lax.fori_loop(0, span // UNROLL, block, tuple(state_ref[:, lanes] for lanes in pieces))
            for k, lanes in enumerate(pieces):
                state_ref[:, lanes] = states[k]
            return unused_inner

        lax.fori_loop(0, channels // width, group_body, 0)
        kept_copy(number, slot).start()
        hook(number)
        return unused

    lax.fori_loop(0, blocks, time_body, 0)
    for number in range(max(0, blocks - 2), blocks):
        kept_copy(number, number % 2).wait()


def inflow_pass(width, step_ref, grad_ref, wide_c, rate_ref, flow_ref, hook):
    rows, channels = step_ref.shape
    count = width // LANES

    def group_body(group, unused):
        hook(group)
        pieces = [lanes_of(group, width, k) for k in range(count)]
        rates = [rate_ref[:, lanes] for lanes in pieces]

        def block(index, flows):
            flows = list(flows)
            base = rows - UNROLL - index * UNROLL
            steps = [tile(step_ref, base, lanes) for lanes in pieces]
            grads = [tile(grad_ref, base, lanes) for lanes in pieces]
            for place in reversed(range(UNROLL)):
                c_now = wide_c[base + place]
                for k in range(count):
                    decay = jnp.exp2(row(steps[k], place) * rates[k])
                    flows[k] = decay * (c_now * row(grads[k], place) + flows[k])
            return tuple(flows)

        zero = jnp.zeros((NS, LANES), jnp.float32)
        flows = lax.fori_loop(0, rows // UNROLL, block, (zero,) * count)
        for k, lanes in enumerate(pieces):
            flow_ref[:, lanes] = flows[k]
        return unused

    lax.fori_loop(0, channels // width, group_body, 0)


class Tree:
    def __init__(self, rising):
        self.rising, self.held, self.result = rising, {}, None

    def push(self, place, value):
        now = value[:UNROLL] + value[UNROLL:]
        level = 0
        while 1 << level < UNROLL:
            if (place >> level) % 2 == (0 if self.rising else 1):
                self.held[level] = now
                return
            first, second = (self.held[level], now) if self.rising else (now, self.held[level])
            now = self.merge(first, second, 1 << level)
            level += 1
        self.result = now

    def merge(self, first, second, distance):
        low = (lax.broadcasted_iota(jnp.int32, (UNROLL, LANES), 0) & distance) == 0
        keep = jnp.where(low, first, second)
        give = jnp.where(low, second, first)
        other = pltpu.roll(give, distance, 0)
        if 2 * distance != UNROLL:
            other = jnp.where(low, pltpu.roll(give, UNROLL - distance, 0), other)
        return keep + other


def lane_sums(part_ref):
    values = part_ref[...].reshape(-1, LANES).astype(jnp.bfloat16)
    return contract(jnp.ones((UNROLL, LANES), jnp.bfloat16), values, 1, 1)


def adjoint_pass(width, step_ref, push_ref, grad_ref, wide_b, wide_c, rate_ref, flow_ref, kept_buf, kept_copy,
                 along_ref, slope_ref, gb_ref, gc_ref, ga_ref, part_b, part_c, hook):
    rows, channels = step_ref.shape
    count = width // LANES
    span = kept_buf.shape[1] - 1
    blocks = rows // span
    ga_ref[...] = jnp.zeros_like(ga_ref)

    def time_body(order, unused):
        slot = lax.rem(order, 2)
        number = blocks - 1 - order
        kept_copy(number, slot).wait()
        part_b[...] = jnp.zeros_like(part_b)
        part_c[...] = jnp.zeros_like(part_c)

        def group_body(group, unused_inner):
            pieces = [lanes_of(group, width, k) for k in range(count)]
            rates = [rate_ref[:, lanes] for lanes in pieces]

            def block(index, carried):
                flows = list(carried[:count])
                sums = list(carried[count : 2 * count])
                current = list(carried[2 * count :])
                local = span - UNROLL - index * UNROLL
                base = number * span + local
                steps = [tile(step_ref, base, lanes) for lanes in pieces]
                pushes = [tile(push_ref, base, lanes) for lanes in pieces]
                grads = [tile(grad_ref, base, lanes) for lanes in pieces]
                alongs = [Tree(False) for k in range(count)]
                slopes = [Tree(False) for k in range(count)]
                for place in reversed(range(UNROLL)):
                    b_now = wide_b[base + place]
                    c_now = wide_c[base + place]
                    gb = gc = None
                    for k, lanes in enumerate(pieces):
                        prior = kept_buf[slot, local + place, :, lanes].astype(jnp.float32)
                        step = row(steps[k], place)
                        grad = row(grads[k], place)
                        decay = jnp.exp2(step * rates[k])
                        adjoint = c_now * grad + flows[k]
                        flows[k] = decay * adjoint
                        decay_grad = flows[k] * prior
                        alongs[k].push(place, adjoint * b_now)
                        slopes[k].push(place, decay_grad * rates[k])
                        sums[k] = sums[k] + decay_grad * step
                        here_b = adjoint * row(pushes[k], place)
                        here_c = current[k] * grad
                        gb = here_b if gb is None else gb + here_b
                        gc = here_c if gc is None else gc + here_c
                        current[k] = prior
                    part_b[local + place] += gb
                    part_c[local + place] += gc
                where = pl.ds(pl.multiple_of(base, UNROLL), UNROLL)
                for k, lanes in enumerate(pieces):
                    along_ref[where, lanes] = alongs[k].result
                    slope_ref[where, lanes] = slopes[k].result
                return tuple(flows + sums + current)

            carried = lax.fori_loop(
                0,
                span // UNROLL,
                block,
                tuple(flow_ref[:, lanes] for lanes in pieces)
                + tuple(ga_ref[:, lanes] for lanes in pieces)
                + tuple(kept_buf[slot, span, :, lanes].astype(jnp.float32) for lanes in pieces),
            )
            for k, lanes in enumerate(pieces):
                flow_ref[:, lanes] = carried[k]
                ga_ref[:, lanes] = carried[count + k]
            return unused_inner

        lax.fori_loop(0, channels // width, group_body, 0)
        gb_ref[number] = lane_sums(part_b)
        gc_ref[number] = lane_sums(part_c)

        @pl.when(order + 2 < blocks)
        def _():
            kept_copy(number - 2, slot).start()

        hook(order)
        return unused

    lax.fori_loop(0, blocks, time_body, 0)


def share(source, target, send_sems, recv_sems):
    blocks = lax.axis_size("ctx")
    here, line = lax.axis_index("ctx"), lax.axis_index("exp")
    copies = []
    for step in range(1, blocks):
        copies.append(
            pltpu.make_async_remote_copy(
                src_ref=source,
                dst_ref=target.at[here],
                send_sem=send_sems.at[step],
                recv_sem=recv_sems.at[step],
                device_id=(lax.rem(here + step, blocks), line),
                device_id_type=MESH,
            )
        )
        copies[-1].start()
    target[here] = source[...]
    return copies


def row_peers():
    blocks = lax.axis_size("ctx")
    here, line = lax.axis_index("ctx"), lax.axis_index("exp")
    return [(lax.rem(here + step, blocks), line) for step in range(1, blocks)]


def row_half(source, target, sems, place, k):
    size = source.shape[0] // 2
    return pltpu.make_async_remote_copy(
        src_ref=source.at[pl.ds(k * size, size)],
        dst_ref=target.at[pl.ds(k * size, size)],
        send_sem=sems.at[0, k],
        recv_sem=sems.at[1, k],
        device_id=partner(place),
        device_id_type=MESH,
    )


def front(loaded, loads, room, outs, scratch, saves):
    normed_ref, bt_ref, ct_ref, rate_ref, chan_ref, gain_ref, delta_ref, same_ref, target_ref = outs
    nx, ext, conv, xs, pre, step, push = scratch
    in_ref, prior_ref, prior_ids, ids_ref, routes_ref, conv_w, channel_ref, width_ref = loaded
    for load in loads[:5] + loads[6:]:
        load.wait()
    tokens, channels = xs.shape
    width = in_ref.shape[1]
    mine = lax.axis_index("ctx")
    gain_rows = jnp.concatenate(
        [width_ref[at : at + LANES, :].astype(jnp.float32).T for at in range(0, width, LANES)], axis=1
    )
    gain_ref[...] = gain_rows[:8]
    for at in range(0, channels, LANES):
        chan_ref[:, at : at + LANES] = channel_ref[at : at + LANES, LANES:].astype(jnp.float32).T[:32]
    rate_ref[...] = -jnp.exp(chan_ref[8 : 8 + NS, :]) * LOG2E
    gain = gain_ref[0:1, :]

    def normed(values):
        x = values.astype(jnp.float32)
        return (x * lax.rsqrt(jnp.mean(x * x, axis=-1, keepdims=True) + EPS) * gain).astype(jnp.bfloat16)

    nx[:EDGE, :] = normed(prior_ref[...])

    def norm_rows(index, unused):
        at = pl.ds(pl.multiple_of(index * 16, 16), 16)
        value = normed(in_ref[at, :])
        normed_ref[at, :] = value
        nx[pl.ds(pl.multiple_of(EDGE + index * 16, 16), 16), :] = value
        return unused

    lax.fori_loop(0, tokens // 16, norm_rows, 0)
    def column(values):
        return jnp.broadcast_to(values.astype(jnp.float32), (LANES, LANES)).T

    def columns(ref):
        return jnp.concatenate([column(ref[:, at : at + LANES]) for at in range(0, tokens, LANES)], axis=0)

    ids = jnp.where(mine > 0, column(prior_ids[...])[LANES - EDGE :], -1.0)
    own_ids = columns(ids_ref)
    every_id = jnp.concatenate([ids, own_ids], axis=0)
    for j in range(1, KC):
        same_ref[j - 1] = (pltpu.roll(every_id, j, 0)[EDGE:] == own_ids).astype(jnp.float32)
    routes = columns(routes_ref)
    chosen = (routes == lax.broadcasted_iota(jnp.int32, routes.shape, 1).astype(jnp.float32)).astype(jnp.float32)
    square = (tokens, tokens)
    until = lax.broadcasted_iota(jnp.int32, square, 0) >= lax.broadcasted_iota(jnp.int32, square, 1)
    running = dot(until.astype(jnp.float32).astype(jnp.bfloat16), chosen.astype(jnp.bfloat16))
    slot = jnp.sum(running * chosen, axis=1, keepdims=True) - 1.0
    target_ref[...] = routes * room + slot
    piece = 2 * LANES
    loads[5].wait()

    def conv_piece(index, unused):
        lanes = pl.ds(pl.multiple_of(index * piece, piece), piece)
        low = dot(nx[...], conv_w[:, lanes]).astype(jnp.bfloat16)
        ext[:, lanes] = low
        value = low.astype(jnp.float32)
        out = chan_ref[24:25, lanes] + chan_ref[3:4, lanes] * value[EDGE:]
        for j in range(1, KC):
            same = jnp.concatenate([same_ref[j - 1]] * 2, axis=1)
            out = out + chan_ref[3 - j : 4 - j, lanes] * pltpu.roll(value, j, 0)[EDGE:] * same
        conv[:, lanes] = out
        xs[:, lanes] = (out / (1.0 + jnp.exp(-out))).astype(jnp.bfloat16)
        return unused

    lax.fori_loop(0, channels // piece, conv_piece, 0)
    for save in saves[:3]:
        save.start()
    projected = dot(xs[...], channel_ref[:, :LANES])
    lane = lax.broadcasted_iota(jnp.int32, projected.shape, 1)
    delta_ref[...] = jnp.where(lane >= R + 2 * NS, pltpu.roll(projected, R + 2 * NS, 1), 0.0).astype(jnp.bfloat16)
    for at in range(0, tokens, LANES):
        block = projected[at : at + LANES].T
        bt_ref[:, at : at + LANES] = block[R : R + NS]
        ct_ref[:, at : at + LANES] = block[R + NS : R + 2 * NS]

    def step_piece(index, unused):
        lanes = pl.ds(pl.multiple_of(index * piece, piece), piece)
        value = contract(delta_ref[...], channel_ref[lanes, :LANES], 1, 1) + chan_ref[25:26, lanes]
        pre[:, lanes] = value
        size = jnp.maximum(value, 0.0) + jnp.log1p(jnp.exp(-jnp.abs(value)))
        push[:, lanes] = size * xs[:, lanes].astype(jnp.float32)
        keep = jnp.concatenate([same_ref[0]] * 2, axis=1)
        step[:, lanes] = jnp.where(keep > 0, size, 1e30)
        return unused

    lax.fori_loop(0, channels // piece, step_piece, 0)
    for save in saves[3:]:
        save.start()


def forward_kernel(places, streams, width, room, *refs):
    weights_from = refs[:8]
    shards, leaving = refs[8:10], refs[10]
    y_ref, product_ref = refs[12:14]
    front_outs = refs[14:23]
    kept_ref = refs[23]
    saved = refs[24:30]
    wholes, arriving = refs[30:32], refs[32]
    scratch = refs[33:40]
    weights = refs[40:48]
    (wide_b, wide_c, kept_buf, first_buf, state_ref, message, products, ends,
     load_sems, kept_sems, first_sem, share_sems, save_sems, moved_sems, send_sems, recv_sems, local_sems) = refs[48:]
    loads = [pltpu.make_async_copy(weights_from[k], weights[k], load_sems.at[k]) for k in range(8)]
    for load in loads[:5] + loads[:4:-1]:
        load.start()
    bt_ref, ct_ref, rate_ref = front_outs[1:4]
    step_ref, push_ref = scratch[5:7]
    blocks = lax.axis_size("ctx")
    position = lax.axis_index("ctx")
    span = kept_buf.shape[1]
    flow = GatherFlow(places, streams, range(len(places)), shards, wholes, send_sems, recv_sems, local_sems)
    meet([place for place in places if place[0] == "exp"], *row_peers())
    flow.start()
    move = row_half(leaving, arriving, moved_sems, ("ctx", blocks.bit_length() - 2), 1)
    move.start()
    saves = [
        pltpu.make_async_copy(scratch[k + 1], saved[k], save_sems.at[k]) for k in range(6)
    ]
    front(weights, loads, room, front_outs, scratch, saves)

    message[0] = jnp.exp2(jnp.sum(step_ref[...], axis=0, keepdims=True) * rate_ref[...]).astype(jnp.bfloat16)
    early = share(message.at[0], products, share_sems.at[0], share_sems.at[1])
    spread_columns(bt_ref, wide_b)
    spread_columns(ct_ref, wide_c)
    end_pass(width, step_ref, push_ref, wide_b, rate_ref, state_ref, lambda group: None)
    message[1] = state_ref[...].astype(jnp.bfloat16)
    late = share(message.at[1], ends, share_sems.at[2], share_sems.at[3])
    flow.advance(0)
    for copy in early + late:
        copy.wait_recv()
    start = jnp.zeros(state_ref.shape, jnp.float32)
    for index in range(blocks):
        folded = products[index].astype(jnp.float32) * start + ends[index].astype(jnp.float32)
        start = jnp.where(index < position, folded, start)
    state_ref[...] = start
    product_ref[...] = products[...]
    first_buf[0] = start.astype(jnp.bfloat16)
    first_copy = pltpu.make_async_copy(first_buf, kept_ref.at[pl.ds(0, 1)], first_sem)
    first_copy.start()

    def kept_copy(number, slot):
        return pltpu.make_async_copy(
            kept_buf.at[slot], kept_ref.at[pl.ds(1 + number * span, span)], kept_sems.at[slot]
        )

    def hook(number):
        @pl.when(number == 4)
        def _():
            flow.advance(1)

    out_pass(width, step_ref, push_ref, wide_b, wide_c, rate_ref, state_ref, y_ref, kept_buf, kept_copy, hook)
    for stage in range(2, max(flow.stages(number) for number in range(len(streams)))):
        flow.advance(stage)
    flow.finish()
    first_copy.wait()
    for save in saves:
        save.wait()
    for copy in early + late:
        copy.wait_send()
    move.wait()


def scan_forward(sizes, rows_in, prior, ids, weights, room, shards, leaving, begun, identity, span=64):
    places = bit_positions(sizes)
    stages = len(places)
    begin = len(far_of(places))
    streams = halves(shards, *gather_orders(places), begin=begin)
    tokens, width = rows_in.shape
    channels = weights[0].shape[1]
    blocks = sizes[0][1]
    inside = pl.BlockSpec(memory_space=pltpu.VMEM)
    anywhere = pl.BlockSpec(memory_space=pl.ANY)
    half, full = jnp.bfloat16, jnp.float32
    shape = jax.ShapeDtypeStruct
    saved = [
        shape((EDGE + tokens, channels), half),
        shape((tokens, channels), full),
        shape((tokens, channels), half),
        shape((tokens, channels), full),
        shape((tokens, channels), full),
        shape((tokens, channels), full),
    ]
    y, products, normed, bt, ct, rates, chan, gains, delta, same, target, kept, *rest = pl.pallas_call(
        functools.partial(forward_kernel, places, streams, pick(channels), room),
        in_specs=[anywhere] * 12,
        input_output_aliases={11: 20},
        out_specs=[inside] * 11 + [anywhere] * 10,
        out_shape=[
            shape((tokens, channels), full),
            shape((blocks, NS, channels), half),
            shape((tokens, width), half),
            shape((NS, tokens), full),
            shape((NS, tokens), full),
            shape((NS, channels), full),
            shape((32, channels), full),
            shape((8, width), full),
            shape((tokens, LANES), half),
            shape((KC - 1, tokens, LANES), full),
            shape((tokens, LANES), full),
            shape((tokens + 1, NS, channels), half),
        ]
        + saved
        + [shape((2,) * stages + shard.shape[begin:], shard.dtype) for shard in shards]
        + [shape(leaving.shape, leaving.dtype)],
        scratch_shapes=[pltpu.VMEM((EDGE + tokens, width), half)]
        + [pltpu.VMEM(value.shape, value.dtype) for value in saved]
        + [pltpu.VMEM(value.shape, value.dtype) for value in [rows_in, *prior, *ids, *weights]]
        + [
            pltpu.VMEM((tokens, NS, LANES), full),
            pltpu.VMEM((tokens, NS, LANES), full),
            pltpu.VMEM((2, span, NS, channels), half),
            pltpu.VMEM((1, NS, channels), half),
            pltpu.VMEM((NS, channels), full),
            pltpu.VMEM((2, NS, channels), half),
            pltpu.VMEM((blocks, NS, channels), half),
            pltpu.VMEM((blocks, NS, channels), half),
            pltpu.SemaphoreType.DMA((8,)),
            pltpu.SemaphoreType.DMA((2,)),
            pltpu.SemaphoreType.DMA,
            pltpu.SemaphoreType.DMA((4, blocks)),
            pltpu.SemaphoreType.DMA((6,)),
            pltpu.SemaphoreType.DMA((2, 2)),
            pltpu.SemaphoreType.DMA((len(streams), stages)),
            pltpu.SemaphoreType.DMA((len(streams), stages)),
            pltpu.SemaphoreType.DMA((len(streams),)),
        ],
        compiler_params=pltpu.CompilerParams(
            collective_id=identity, has_side_effects=True, vmem_limit_bytes=63 * 1024 * 1024
        ),
        cost_estimate=cost(tokens, channels, 9),
        name="scan_forward",
    )(rows_in, *prior, *ids, *weights, *shards, leaving, begun)
    saved, wholes, arrived = rest[:6], rest[6:8], rest[8]
    wholes = [whole.reshape((-1,) + whole.shape[stages + 1 :]) for whole in wholes]
    return y, products, normed, bt, ct, rates, chan, gains, delta, same, target, kept, saved, wholes, arrived


def backward_kernel(places, streams, marks, width, *refs):
    bt_ref, ct_ref, rate_ref, product_ref = refs[:4]
    parts = refs[4:6]
    streamed = refs[6:9]
    kept_ref, leaving = refs[9:11]
    outs = refs[11:]
    gb_ref, gc_ref, ga_ref = outs[:3]
    totals, arriving = outs[3:5], outs[5]
    rows_out = outs[6:8]
    scratch = outs[8:]
    landing = scratch[:marks]
    (step_ref, push_ref, grad_ref, along_ref, slope_ref, wide_b, wide_c, part_b, part_c, kept_buf, flow_ref, message,
     inflows, load_sems, push_sem, out_sems, kept_sems, share_sems, moved_sems, send_sems, recv_sems) = scratch[marks:]
    blocks = lax.axis_size("ctx")
    position = lax.axis_index("ctx")
    span = kept_buf.shape[1] - 1
    steps = step_ref.shape[0] // span

    def load(group, k):
        lanes = pl.ds(pl.multiple_of(group * width, LANES), width)
        source, target = ((streamed[0], step_ref), (streamed[2], grad_ref))[k]
        return pltpu.make_async_copy(source.at[:, lanes], target.at[:, lanes], load_sems.at[k, group])

    for group in range(step_ref.shape[1] // width):
        for k in range(2):
            load(group, k).start()
    push_load = pltpu.make_async_copy(streamed[1], push_ref, push_sem)
    push_load.start()

    def ready(group):
        for k in range(2):
            load(group, k).wait()

    def rows_copy(number, k):
        rows = pl.ds(number * span, span)
        return pltpu.make_async_copy((along_ref, slope_ref)[k].at[rows], rows_out[k].at[rows], out_sems.at[k, number])

    flow = ReduceFlow(places, streams, range(len(places)), parts, totals, landing, send_sems, recv_sems)

    def kept_copy(number, slot):
        return pltpu.make_async_copy(
            kept_ref.at[pl.ds(number * span, span + 1)], kept_buf.at[slot], kept_sems.at[slot]
        )

    for order in range(min(2, steps)):
        kept_copy(steps - 1 - order, order).start()
    meet([place for place in places if place[0] == "exp"], *row_peers())
    flow.start()
    move = row_half(leaving, arriving, moved_sems, ("ctx", blocks.bit_length() - 2), 0)
    move.start()
    spread_columns(ct_ref, wide_c)
    inflow_pass(width, step_ref, grad_ref, wide_c, rate_ref, flow_ref, ready)
    message[...] = flow_ref[...].astype(jnp.bfloat16)
    copies = share(message, inflows, share_sems.at[0], share_sems.at[1])
    flow.advance(0)
    spread_columns(bt_ref, wide_b)
    for copy in copies:
        copy.wait_recv()
    end = jnp.zeros(flow_ref.shape, jnp.float32)
    for index in reversed(range(blocks)):
        folded = inflows[index].astype(jnp.float32) + product_ref[index].astype(jnp.float32) * end
        end = jnp.where(index > position, folded, end)
    flow_ref[...] = end
    push_load.wait()

    def hook(order):
        for k in range(2):
            rows_copy(steps - 1 - order, k).start()

        @pl.when(order == 3)
        def _():
            flow.advance(1)

        @pl.when(order == 5)
        def _():
            flow.advance(2)

    adjoint_pass(width, step_ref, push_ref, grad_ref, wide_b, wide_c, rate_ref, flow_ref, kept_buf, kept_copy,
                 along_ref, slope_ref, gb_ref, gc_ref, ga_ref, part_b, part_c, hook)
    for stage in range(3, len(streams[0][2])):
        flow.advance(stage)
    flow.finish()
    for copy in copies:
        copy.wait_send()
    move.wait()
    for number in range(steps):
        for k in range(2):
            rows_copy(number, k).wait()


def scan_backward(sizes, step, push, grad, b_turned, c_turned, rates, products, parts, kept, leaving, identity, span=64):
    places = bit_positions(sizes)
    stages = len(places)
    far = sorted(far_of(places))
    streams = halves(parts, *[tuple(order[: stages - len(far)]) for order in orders_of(places)])
    divided = [part.reshape((2,) * stages + (-1, part.shape[1])) for part in parts]
    tokens, channels = step.shape
    blocks = sizes[0][1]
    inside = pl.BlockSpec(memory_space=pltpu.VMEM)
    anywhere = pl.BlockSpec(memory_space=pl.ANY)
    half = jnp.bfloat16
    landing = landing_of(streams, range(stages), divided)
    row_sums = jax.ShapeDtypeStruct((tokens // span, UNROLL, span * NS), jnp.float32)
    out = pl.pallas_call(
        functools.partial(backward_kernel, places, streams, len(landing), pick(channels)),
        in_specs=[inside] * 6 + [anywhere] * 5,
        out_specs=[inside] * 5 + [anywhere] * 3,
        out_shape=[row_sums, row_sums, jax.ShapeDtypeStruct((NS, channels), jnp.float32)]
        + [jax.ShapeDtypeStruct((2,) * len(far) + block.shape[-2:], half) for block in divided]
        + [jax.ShapeDtypeStruct(leaving.shape, leaving.dtype)]
        + [jax.ShapeDtypeStruct((tokens, channels), jnp.float32)] * 2,
        scratch_shapes=landing
        + [pltpu.VMEM((tokens, channels), jnp.float32)] * 5
        + [
            pltpu.VMEM((tokens, NS, LANES), jnp.float32),
            pltpu.VMEM((tokens, NS, LANES), jnp.float32),
            pltpu.VMEM((span, NS, LANES), jnp.float32),
            pltpu.VMEM((span, NS, LANES), jnp.float32),
            pltpu.VMEM((2, span + 1, NS, channels), half),
            pltpu.VMEM((NS, channels), jnp.float32),
            pltpu.VMEM((NS, channels), half),
            pltpu.VMEM((blocks, NS, channels), half),
            pltpu.SemaphoreType.DMA((2, channels // pick(channels))),
            pltpu.SemaphoreType.DMA,
            pltpu.SemaphoreType.DMA((2, tokens // span)),
            pltpu.SemaphoreType.DMA((2,)),
            pltpu.SemaphoreType.DMA((2, blocks)),
            pltpu.SemaphoreType.DMA((2, 2)),
        ]
        + flights(streams),
        compiler_params=pltpu.CompilerParams(
            collective_id=identity, has_side_effects=True, vmem_limit_bytes=63 * 1024 * 1024
        ),
        cost_estimate=cost(tokens, channels, 15),
        name="scan_backward",
    )(b_turned, c_turned, rates, products, *divided, step, push, grad, kept, leaving)
    wide_b, wide_c, grad_a, first, second, arrived, along, slope = out
    grad_bs, grad_cs = [values[:, 0].reshape(tokens, NS) for values in (wide_b, wide_c)]
    return along, slope, grad_bs, grad_cs, grad_a, (first, second), arrived


class PackedReduce(ReduceFlow):
    def __init__(self, places, streams, heads, parts, totals, landing, blocks, send_sems, recv_sems):
        super().__init__(places, streams, range(len(places)), parts, totals, landing, send_sems, recv_sems)
        self.heads, self.blocks = heads, blocks

    def side(self, number, stage, value):
        array, cols, order = self.streams[number]
        if stage == 0:
            index = tuple(value if p == order[0] else slice(None) for p in range(self.heads))
            return self.parts[array].at[index + (slice(None), cols)]
        left = [p for p in self.dims if p not in order[:stage]]
        index = tuple(value if p == order[stage] else slice(None) for p in left)
        held = self.blocks[number] if stage == 1 else self.spot(number, stage - 1)
        return held.at[index]

    def advance(self, stage):
        if stage:
            super().advance(stage)
            return
        for number, (array, cols, order) in enumerate(self.streams):
            self.flight(number, 0).wait_recv()
            mine = self.side(number, 0, self.bits[order[0]])
            there, held = self.spot(number, 0), self.blocks[number]
            tails = len(self.places) - self.heads
            size = held.shape[-2]

            def add(index, unused, mine=mine, there=there, held=held, tails=tails, size=size):
                at = tuple(lax.rem(index // 2 ** (self.heads - 2 - k), 2) for k in range(self.heads - 1))
                value = there[at].astype(jnp.float32) + mine[at].astype(jnp.float32)
                for block in range(2**tails):
                    spot = tuple(block // 2 ** (tails - 1 - k) % 2 for k in range(tails))
                    held[at + spot] = value[block * size : (block + 1) * size].astype(held.dtype)
                return unused

            lax.fori_loop(0, 2 ** (self.heads - 1), add, 0)
            self.flight(number, 1).start()


def turned(values):
    return jnp.concatenate([values[:, at : at + LANES].T for at in range(0, values.shape[1], LANES)], axis=0)


def finish_kernel(places, streams, third, late, far, marks, *refs):
    leaving = refs[23:25]
    refs = refs[:23] + refs[27:]
    (along_h, slope_h, grad_h, pre_h, conv_h, xs_h, ext_h, gz_h, wc_h, wg_h) = refs[:10]
    (normed_ref, in_ref, resid_ref, mix_ref, bc_ref, delta_ref, same_ref, chan_ref, decay_ref, rate_ref, wide_ref) = refs[10:21]
    rest_parts = refs[21:23]
    gi_ref, own_in, own_out, tot_small, tot_wide = refs[23:28]
    arriving, scratch = refs[28:30], refs[30:]
    landing, scratch = scratch[: marks[0]], scratch[marks[0] :]
    blocks, scratch = scratch[: marks[1]], scratch[marks[1] :]
    landing3, scratch = scratch[: marks[2]], scratch[marks[2] :]
    blocks3, scratch = scratch[: marks[3]], scratch[marks[3] :]
    late_landing, scratch = scratch[: marks[4]], scratch[marks[4] :]
    (along, slope, grad, pre, conv, xs, ext, gz, wc, wg, gdt, gci, last, spill, arrived, sums, rows_s, wide_s, gn,
     part_conv, part_small, part_wide,
     block_sems, whole_sems, spill_sems, moved_sems, send_sems, recv_sems, send3, recv3, late_send, late_recv) = scratch
    tokens, channels = xs.shape
    own_conv, own_gate = own_in.at[:, :channels], own_in.at[:, channels:]
    span = tokens // block_sems.shape[1]
    heads = len([place for place in places if place[0] == "ctx"])
    flow = PackedReduce(
        places, streams, heads, (part_conv, part_small), (own_conv, tot_small), landing, blocks, send_sems, recv_sems
    )
    flow3 = PackedReduce(places, third, heads, (part_wide,), (tot_wide,), landing3, blocks3, send3, recv3)
    rest = ReduceFlow(places, late, far, rest_parts, (own_gate, own_out), late_landing, late_send, late_recv)

    streamed = ((along_h, along), (slope_h, slope), (grad_h, grad), (pre_h, pre), (xs_h, xs))

    def block_copy(k, number):
        rows = pl.ds(number * span, span)
        source, target = streamed[k]
        return pltpu.make_async_copy(source.at[rows], target.at[rows], block_sems.at[k, number])

    for number in range(tokens // span):
        for k in range(len(streamed)):
            block_copy(k, number).start()
    wholes = [
        pltpu.make_async_copy(source, target, whole_sems.at[k])
        for k, (source, target) in enumerate(((conv_h, conv), (ext_h, ext), (gz_h, gz), (wc_h, wc), (wg_h, wg)))
    ]
    for copy in wholes:
        copy.start()
    count = lax.axis_size("ctx")
    here, line = lax.axis_index("ctx"), lax.axis_index("exp")
    before = (lax.rem(here + count - 1, count), line)
    meet(places, before, (lax.rem(here + 1, count), line))
    rest.start()
    moves = [
        row_half(leaving[k], arriving[k], moved_sems.at[k], ("ctx", count.bit_length() - 2), 1) for k in range(2)
    ]
    moves[0].start()

    sums[...] = jnp.zeros_like(sums)
    rows_s[...] = jnp.zeros_like(rows_s)

    def first_block(number, unused):
        for k in range(len(streamed)):
            block_copy(k, number).wait()

        def some(index, unused_inner):
            at = pl.ds(pl.multiple_of(number * span + index * 16, 16), 16)
            for low in range(0, channels, LANES):
                lanes = slice(low, low + LANES)
                a, g, x, p = along[at, lanes], grad[at, lanes], xs[at, lanes].astype(jnp.float32), pre[at, lanes]
                small = jnp.exp(-jnp.abs(p))
                gated = jnp.where(p >= 0, 1.0, small) / (1.0 + small)
                step = jnp.maximum(p, 0.0) + jnp.log1p(small)
                value = (a * x + slope[at, lanes] * (1.0 / LOG2E)) * gated
                gdt[at, lanes] = value.astype(jnp.bfloat16)
                sums[0, :, lanes] += value[:8] + value[8:]
                both = g * x
                sums[1, :, lanes] += both[:8] + both[8:]
                along[at, lanes] = chan_ref[26:27, lanes] * g + a * step
            return unused_inner

        lax.fori_loop(0, span // 16, some, 0)
        return unused

    lax.fori_loop(0, tokens // span, first_block, 0)
    rows_s[25:26, :] = jnp.sum(sums[0], axis=0, keepdims=True)
    rows_s[26:27, :] = jnp.sum(sums[1], axis=0, keepdims=True)
    rows_s[8:24, :] = decay_ref[...] * rate_ref[...] * (1.0 / LOG2E)

    lane = lax.broadcasted_iota(jnp.int32, (tokens, LANES), 1)
    mixed = pltpu.roll(dot(gdt[...], mix_ref[:, :LANES]), R, 1)
    projected = jnp.where(lane < R, mixed, jnp.where(lane < R + 2 * NS, bc_ref[...], 0.0)).astype(jnp.bfloat16)
    wholes[0].wait()
    wholes[1].wait()
    piece = 2 * LANES
    tail_row = lax.broadcasted_iota(jnp.int32, (tokens, piece), 0)

    def conv_piece(index, unused):
        lanes = pl.ds(pl.multiple_of(index * piece, piece), piece)
        some = pl.ds(pl.multiple_of(index * piece, piece), piece)
        total = along[:, lanes] + contract(projected, mix_ref[some, :LANES], 1, 1)
        value = conv[:, lanes]
        gate = 1.0 / (1.0 + jnp.exp(-value))
        out = total * gate * (1.0 + value * (1.0 - gate))
        rows_s[24:25, lanes] = jnp.sum(out, axis=0, keepdims=True)
        before_rows = ext[:, lanes].astype(jnp.float32)
        rows_s[3:4, lanes] = jnp.sum(out * before_rows[EDGE:], axis=0, keepdims=True)
        result = chan_ref[3:4, lanes] * out
        beyond = jnp.zeros((8, piece), jnp.float32)
        for j in range(1, KC):
            same = jnp.concatenate([same_ref[j - 1]] * 2, axis=1)
            masked = out * same
            shifted_rows = pltpu.roll(before_rows, j, 0)[EDGE:]
            rows_s[3 - j : 4 - j, lanes] = jnp.sum(masked * shifted_rows, axis=0, keepdims=True)
            moved = chan_ref[3 - j : 4 - j, lanes] * pltpu.roll(masked, tokens - j, 0)
            result = result + jnp.where(tail_row < tokens - j, moved, 0.0)
            beyond = beyond + jnp.where(tail_row < tokens - j, 0.0, moved)[tokens - 8 :]
        gci[:, lanes] = result.astype(jnp.bfloat16)
        last[:, lanes] = result[tokens - 16 :]
        spill[:, lanes] = beyond
        return unused

    lax.fori_loop(0, channels // piece, conv_piece, 0)
    handed = pltpu.make_async_remote_copy(
        src_ref=spill,
        dst_ref=arrived,
        send_sem=spill_sems.at[0],
        recv_sem=spill_sems.at[1],
        device_id=before,
        device_id_type=MESH,
    )
    handed.start()

    cut = part_small.shape[-2]
    first_rows = contract(projected, xs[...], 0, 0) + contract(delta_ref[...], gdt[...], 0, 0)
    filler = jnp.zeros((LANES - rows_s.shape[0], channels), jnp.float32)
    for k, values in enumerate((first_rows, jnp.concatenate([rows_s[...], filler], axis=0))):
        columns = turned(values)
        for index in range(channels // cut):
            spot = tuple(index // 2 ** (heads - 1 - j) % 2 for j in range(heads))
            part_small[spot + (slice(None), slice(k * LANES, (k + 1) * LANES))] = columns[
                index * cut : (index + 1) * cut
            ].astype(jnp.bfloat16)
    handed.wait_recv()
    closing = last[...] + jnp.concatenate([jnp.zeros((8, channels), jnp.float32), arrived[...]], axis=0)
    gci[tokens - 16 :, :] = closing.astype(jnp.bfloat16)

    long = part_conv.shape[-2]

    def product_piece(index, unused):
        lanes = pl.ds(pl.multiple_of(index * piece, piece), piece)
        value = dot(normed_ref[...], gci[:, lanes])
        for block in range(value.shape[0] // long):
            spot = tuple(block // 2 ** (heads - 1 - k) % 2 for k in range(heads))
            part_conv[spot + (slice(None), lanes)] = value[block * long : (block + 1) * long].astype(jnp.bfloat16)
        return unused

    lax.fori_loop(0, channels // piece, product_piece, 0)
    flow.start()

    for copy in wholes[2:]:
        copy.wait()
    width = gn.shape[1]

    def normed_piece(index, unused):
        lanes = pl.ds(pl.multiple_of(index * piece, piece), piece)
        gn[:, lanes] = contract(gci[...], wc[lanes, :], 1, 1) + contract(gz[...], wg[lanes, :], 1, 1)
        return unused

    lax.fori_loop(0, width // piece, normed_piece, 0)
    wide_s[...] = wide_ref[...]
    gain = wide_ref[0:1, :]

    def back(index, total):
        at = pl.ds(pl.multiple_of(index * 16, 16), 16)
        x, g = in_ref[at, :].astype(jnp.float32), gn[at, :]
        scale = lax.rsqrt(jnp.mean(x * x, axis=-1, keepdims=True) + EPS)
        scaled = g * gain
        share_of = jnp.mean(x * scaled, axis=-1, keepdims=True)
        gi_ref[at, :] = resid_ref[at, :] + scale * scaled - x * (scale * scale * scale * share_of)
        value = g * (x * scale)
        return total + value[:8] + value[8:]

    total = lax.fori_loop(0, tokens // 16, back, jnp.zeros((8, width), jnp.float32))
    wide_s[0:1, :] = jnp.sum(total, axis=0, keepdims=True)
    flow.advance(0)
    filler = jnp.zeros((LANES - wide_s.shape[0], width), jnp.float32)
    columns = turned(jnp.concatenate([wide_s[...], filler], axis=0))
    short = part_wide.shape[-2]
    for block in range(width // short):
        spot = tuple(block // 2 ** (heads - 1 - k) % 2 for k in range(heads))
        part_wide[spot] = columns[block * short : (block + 1) * short].astype(jnp.bfloat16)
    flow3.start()
    rest.advance(0)
    for stage in range(1, len(places)):
        flow.advance(stage)
        flow3.advance(stage - 1)
        rest.advance(stage)
        if stage == 2:
            moves[1].start()
    flow3.advance(len(places) - 1)

    flow.finish()
    flow3.finish()
    rest.finish()
    handed.wait_send()
    for move in moves:
        move.wait()


def finish(sizes, streamed, inside_values, parts, leaving, arrived, identity, span=64):
    places = bit_positions(sizes)
    stages = len(places)
    far = sorted(far_of(places))
    heads = sizes[0][1].bit_length() - 1
    tails = stages - heads
    along, slope, grad, pre, conv, xs, ext, gz, wc, wg = streamed
    normed = inside_values[1]
    tokens, channels = xs.shape
    width = normed.shape[1]
    devices = 2**stages
    half, wide = jnp.bfloat16, jnp.float32
    rows, thin = channels // devices, width // devices
    orders = [tuple(order) for order in orders_of(places)]
    conv_like = jax.ShapeDtypeStruct((width, channels), half)
    small_like = jax.ShapeDtypeStruct((channels, 2 * LANES), half)
    wide_like = jax.ShapeDtypeStruct((width, LANES), half)
    streams = halves((conv_like, small_like), *orders)
    third = halves((wide_like,), *orders)
    late = [(k, slice(0, part.shape[-1]), tuple(far_of(places))) for k, part in enumerate(parts)]

    def room(of, sizes_of):
        landing, blocks = [], []
        for array, cols, order in of:
            size, many = sizes_of[array], cols.stop - cols.start
            landing.append(pltpu.VMEM((2,) * (heads - 1) + (size * 2**tails, many), half))
            landing += [pltpu.VMEM((2,) * (stages - stage - 1) + (size, many), half) for stage in range(1, stages)]
            blocks.append(pltpu.VMEM((2,) * (stages - 1) + (size, many), half))
        return landing, blocks

    landing, blocks = room(streams, (thin, rows))
    landing3, blocks3 = room(third, (thin,))
    late_landing = landing_of(late, far, parts)
    marks = [len(landing), len(blocks), len(landing3), len(blocks3), len(late_landing)]
    inside = pl.BlockSpec(memory_space=pltpu.VMEM)
    anywhere = pl.BlockSpec(memory_space=pl.ANY)
    return pl.pallas_call(
        functools.partial(finish_kernel, places, streams, third, late, far, marks),
        in_specs=[anywhere] * 10 + [inside] * (len(inside_values) + 2) + [anywhere] * 4,
        input_output_aliases={25: 5, 26: 6},
        out_specs=[inside] * 5 + [anywhere] * 2,
        out_shape=[
            jax.ShapeDtypeStruct(normed.shape, wide),
            jax.ShapeDtypeStruct((thin, 2 * channels), wide),
            jax.ShapeDtypeStruct(parts[1].shape[-2:], wide),
            jax.ShapeDtypeStruct((rows, 2 * LANES), wide),
            jax.ShapeDtypeStruct((thin, LANES), wide),
        ]
        + [jax.ShapeDtypeStruct(values.shape, half) for values in leaving],
        scratch_shapes=landing + blocks + landing3 + blocks3 + late_landing
        + [pltpu.VMEM(value.shape, value.dtype) for value in streamed]
        + [
            pltpu.VMEM((tokens, channels), half),
            pltpu.VMEM((tokens, channels), half),
            pltpu.VMEM((16, channels), wide),
            pltpu.VMEM((8, channels), wide),
            pltpu.VMEM((8, channels), wide),
            pltpu.VMEM((2, 8, channels), wide),
            pltpu.VMEM((32, channels), wide),
            pltpu.VMEM(inside_values[-1].shape, wide),
            pltpu.VMEM((tokens, width), wide),
            pltpu.VMEM((2,) * heads + (thin * 2**tails, channels), half),
            pltpu.VMEM((2,) * heads + (rows * 2**tails, 2 * LANES), half),
            pltpu.VMEM((2,) * heads + (thin * 2**tails, LANES), half),
            pltpu.SemaphoreType.DMA((5, tokens // span)),
            pltpu.SemaphoreType.DMA((5,)),
            pltpu.SemaphoreType.DMA((2,)),
            pltpu.SemaphoreType.DMA((2, 2, 2)),
        ]
        + flights(streams)
        + flights(third)
        + flights(late),
        compiler_params=pltpu.CompilerParams(
            collective_id=identity, has_side_effects=True, vmem_limit_bytes=63 * 1024 * 1024
        ),
        name="finish",
    )(*streamed, *inside_values, *parts, *leaving, *arrived)


def chosen_of(target, room):
    lane = lax.broadcasted_iota(jnp.int32, target.shape, 1).astype(jnp.float32) * room
    return ((target >= lane) & (target < lane + room)).astype(jnp.float32)


def gate_kernel(room, experts, y_ref, xs_ref, normed_ref, in_ref, cot_ref, target_ref, wg_ref, wo_ref, wide_ref, chan_ref,
                gain_ref, n2_ref, resid_ref, z_ref, prob_ref, pick_ref, gated_t, normed_t):
    skip, gain = chan_ref[26:27, :], gain_ref[1:2, :]
    gate_in = dot(normed_ref[...], wg_ref[...])
    z_ref[...] = gate_in
    scanned = y_ref[...] + skip * xs_ref[...].astype(jnp.float32)
    gated = scanned * gate_in / (1.0 + jnp.exp(-gate_in))
    for at in range(0, gated.shape[1], LANES):
        gated_t[at : at + LANES, :] = gated[:, at : at + LANES].T.astype(jnp.bfloat16)
    for at in range(0, normed_ref.shape[1], LANES):
        normed_t[at : at + LANES, :] = normed_ref[:, at : at + LANES].astype(jnp.float32).T.astype(jnp.bfloat16)
    residual = in_ref[...].astype(jnp.float32) + dot(gated.astype(jnp.bfloat16), wo_ref[...])
    resid_ref[...] = residual
    scale = lax.rsqrt(jnp.mean(residual * residual, axis=-1, keepdims=True) + EPS)
    normed_two = (residual * scale * gain).astype(jnp.bfloat16)
    n2_ref[...] = normed_two
    logits = pltpu.roll(dot(normed_two, wide_ref[...]), LANES - 8, 1)
    lane = lax.broadcasted_iota(jnp.int32, logits.shape, 1)
    logits = jnp.where(lane < experts, logits, -1e30)
    powers = jnp.exp(logits - jnp.max(logits, axis=1, keepdims=True))
    powers = jnp.where(lane < experts, powers, 0.0)
    probability = powers / jnp.sum(powers, axis=1, keepdims=True)
    prob_ref[...] = probability
    gate = jnp.sum(probability * chosen_of(target_ref[...], room), axis=1, keepdims=True)
    pick_ref[...] = (cot_ref[...].astype(jnp.float32) * gate).astype(jnp.bfloat16)


def open_gate(y, xs, normed, rows_in, cotangent, target, weights, room, experts, block=3 * LANES):
    tokens, channels = y.shape
    width = rows_in.shape[1]
    shape, half, full = jax.ShapeDtypeStruct, jnp.bfloat16, jnp.float32

    def cut(values):
        return pl.BlockSpec((block, values.shape[1]), lambda i: (i, 0))

    def whole(values):
        return pl.BlockSpec(values.shape, lambda i: (0, 0))

    results = [
        shape((tokens, width), half),
        shape((tokens, width), full),
        shape((tokens, channels), full),
        shape((tokens, LANES), full),
        shape((tokens, width), half),
    ]
    turned_specs = [pl.BlockSpec((rows, block), lambda i: (0, i)) for rows in (channels, width)]
    return pl.pallas_call(
        functools.partial(gate_kernel, room, experts),
        grid=(tokens // block,),
        in_specs=[cut(values) for values in (y, xs, normed, rows_in, cotangent, target)]
        + [whole(values) for values in weights],
        out_specs=[cut(values) for values in results] + turned_specs,
        out_shape=results + [shape((channels, tokens), half), shape((width, tokens), half)],
        compiler_params=pltpu.CompilerParams(vmem_limit_bytes=63 * 1024 * 1024),
        name="open_gate",
    )(y, xs, normed, rows_in, cotangent, target, *weights)


def middle_kernel(room, picked_ref, back_ref, cot_ref, resid_ref, z_ref, y_ref, xs_ref, n2_ref, prob_ref, target_ref,
                  gated_t, normed_t, wo_ref, wide_ref, chan_ref, gain_ref,
                  out_ref, gres_ref, gy_ref, gz_ref, rows_ref, sum_out, sum_gate, mix_all, gz_all):
    step, steps = pl.program_id(0), pl.num_programs(0)

    @pl.when(step == 0)
    def _():
        rows_ref[...] = jnp.zeros_like(rows_ref)
        rows_ref[0:1, :] = gain_ref[0:1, :]

    size = out_ref.shape[0]
    gain = gain_ref[1:2, :]
    grad, picked = cot_ref[...].astype(jnp.float32), picked_ref[...].astype(jnp.float32)
    probability, chosen = prob_ref[...], chosen_of(target_ref[...], room)
    gate = jnp.sum(probability * chosen, axis=1, keepdims=True)
    residual = resid_ref[...]
    out_ref[...] = (residual + gate * picked).astype(jnp.bfloat16)
    grad_gate = jnp.sum(grad * picked, axis=1, keepdims=True)
    grad_logits = probability * (grad_gate * (chosen - gate))
    shifted_logits = pltpu.roll(grad_logits, 8, 1).astype(jnp.bfloat16)
    grad_two = back_ref[...].astype(jnp.float32) + contract(shifted_logits, wide_ref[...], 1, 1)
    rows_ref[...] += contract(shifted_logits, n2_ref[...], 0, 0)[: rows_ref.shape[0]]
    scale = lax.rsqrt(jnp.mean(residual * residual, axis=-1, keepdims=True) + EPS)
    rows_ref[1:2, :] += jnp.sum(grad_two * residual * scale, axis=0, keepdims=True)
    scaled = grad_two * gain
    share_of = jnp.mean(residual * scaled, axis=-1, keepdims=True)
    total = grad + scale * scaled - residual * (scale * scale * scale * share_of)
    gres_ref[...] = total
    mix = total.astype(jnp.bfloat16)
    at = pl.ds(pl.multiple_of(step * size, size), size)
    mix_all[at, :] = mix
    grad_gated = contract(mix, wo_ref[...], 1, 1)
    value = z_ref[...]
    bend = 1.0 / (1.0 + jnp.exp(-value))
    gy_ref[...] = grad_gated * value * bend
    scanned = y_ref[...] + chan_ref[26:27, :] * xs_ref[...].astype(jnp.float32)
    grad_z = (grad_gated * scanned * bend * (1.0 + value * (1.0 - bend))).astype(jnp.bfloat16)
    gz_ref[...] = grad_z
    gz_all[at, :] = grad_z

    @pl.when(step == steps - 1)
    def _():
        piece = 2 * LANES

        def some(index, unused):
            lanes = pl.ds(pl.multiple_of(index * piece, piece), piece)
            sum_out[:, lanes] = dot(gated_t[...], mix_all[:, lanes]).astype(jnp.bfloat16)
            return unused

        def other(index, unused):
            lanes = pl.ds(pl.multiple_of(index * piece, piece), piece)
            sum_gate[:, lanes] = dot(normed_t[...], gz_all[:, lanes]).astype(jnp.bfloat16)
            return unused

        lax.fori_loop(0, sum_out.shape[1] // piece, some, 0)
        lax.fori_loop(0, sum_gate.shape[1] // piece, other, 0)


def middle(blocks, turned_parts, weights, room, experts, block=192):
    tokens, width = blocks[0].shape
    channels = turned_parts[0].shape[0]
    shape, half, full = jax.ShapeDtypeStruct, jnp.bfloat16, jnp.float32

    def cut(values):
        return pl.BlockSpec((block, values.shape[1]), lambda i: (i, 0))

    def whole(values):
        return pl.BlockSpec(values.shape, lambda i: (0, 0))

    results = [
        shape((tokens, width), half),
        shape((tokens, width), full),
        shape((tokens, channels), full),
        shape((tokens, channels), half),
    ]
    sums = [shape((8 + experts, width), full), shape((channels, width), half), shape((width, channels), half)]
    return pl.pallas_call(
        functools.partial(middle_kernel, room),
        grid=(tokens // block,),
        in_specs=[cut(values) for values in blocks] + [whole(values) for values in turned_parts + weights],
        out_specs=[cut(values) for values in results] + [whole(values) for values in sums],
        out_shape=results + sums,
        scratch_shapes=[pltpu.VMEM((tokens, width), half), pltpu.VMEM((tokens, channels), half)],
        compiler_params=pltpu.CompilerParams(vmem_limit_bytes=63 * 1024 * 1024),
        name="middle",
    )(*blocks, *turned_parts, *weights)


def emit_kernel(gi_from, wo_from, wo_other, wi_from, wi_other, in_from, out_from, small_ref, thin_ref,
                gi, w_out, w_in, own_in, own_out, own_x, own_dt, own_taps, own_decay, own_router, *singles):
    gi[...] = gi_from[...]
    w_out[...] = wo_from[...].astype(jnp.float32) + wo_other[...].astype(jnp.float32)
    w_in[...] = wi_from[...].astype(jnp.float32) + wi_other[...].astype(jnp.float32)
    own_in[...] = in_from[...]
    own_out[...] = out_from[...]

    def columns_of(values):
        return jnp.concatenate([values, jnp.zeros((LANES - values.shape[0], LANES), jnp.float32)], axis=0).T

    size, thin = small_ref.shape[0], thin_ref.shape[0]
    first = small_ref[:, :LANES]
    own_x[...] = first[:, : R + 2 * NS]
    own_dt[...] = columns_of(first)[R + 2 * NS :, :size]
    by_row = columns_of(small_ref[:, LANES:])
    own_taps[...] = by_row[:KC, :size]
    own_decay[...] = by_row[8 : 8 + NS, :size]
    for k in range(3):
        singles[k][...] = by_row[24 + k : 25 + k, :size]
    by_row = columns_of(thin_ref[...])
    for k in range(2):
        singles[3 + k][...] = by_row[k : k + 1, :thin]
    own_router[...] = by_row[8 : 8 + own_router.shape[0], :thin]


def emit_outputs(gi, w_out, out_other, w_in, in_other, own_in, own_out, small, thin_part, experts, pieces=2):
    rows, thin = small.shape[0], thin_part.shape[0]
    full = jnp.float32

    def cut(values):
        return pl.BlockSpec((values.shape[0] // pieces, values.shape[1]), lambda i: (i, 0))

    def whole(shape):
        return pl.BlockSpec(shape, lambda i: (0, 0))

    large = [gi, w_out, out_other, w_in, in_other]
    results = [gi, w_out, w_in]
    still = [own_in, own_out, small, thin_part]
    shapes = [own_in.shape, own_out.shape, (rows, R + 2 * NS), (R, rows), (KC, rows), (NS, rows), (experts, thin)]
    shapes += [(1, rows)] * 3 + [(1, thin)] * 2
    return pl.pallas_call(
        emit_kernel,
        grid=(pieces,),
        in_specs=[cut(values) for values in large] + [whole(values.shape) for values in still],
        out_specs=[cut(values) for values in results] + [whole(shape) for shape in shapes],
        out_shape=[jax.ShapeDtypeStruct(values.shape, full) for values in results]
        + [jax.ShapeDtypeStruct(shape, full) for shape in shapes],
        name="emit_outputs",
    )(*large, *still)


def expert_kernel(slices, *refs):
    tokens_ref, grads_ref, column_ref = refs[:3]
    even = range(0, slices, 2)
    odd = range(1, slices, 2)
    weights_in, weight_out = refs[3 : 3 + len(even)], refs[3 + len(even)]
    outs = refs[4 + len(even) :]
    picked_ref, back_ref = outs[:2]
    sums_in = outs[2 : 2 + len(even)]
    kept_out, leaving_out, arriving_out = outs[2 + len(even) : 5 + len(even)]
    (sent, got, answer, returned, w_in, w_out, hidden, total, active, slope, inner, sum_out, pair_out, pair_in, far_out,
     rows_t, send_sems, recv_sems, weight_sems, sum_sems, spread_sems, mate_sems, far_sems, moved_sems) = outs[
        5 + len(even) :
    ]
    experts, room, width = sent.shape[1:]
    places = experts * room
    me = lax.axis_index("exp")
    here = lax.axis_index("ctx")
    levels = slices.bit_length() - 1

    loads = [pltpu.make_async_copy(weight_out, w_out.at[0], weight_sems.at[slices])]
    for k, s in enumerate(even):
        loads.append(pltpu.make_async_copy(weights_in[k], w_in.at[s], weight_sems.at[s]))
    for load in loads:
        load.start()

    barrier = pltpu.get_barrier_semaphore()
    mates = [partner(("ctx", level)) for level in range(levels)]
    for step in range(1, experts):
        pl.semaphore_signal(barrier, inc=1, device_id=(here, lax.rem(me + step, experts)), device_id_type=MESH)
    for mate in mates:
        pl.semaphore_signal(barrier, inc=1, device_id=mate, device_id_type=MESH)

    def exchange(source, target, kind):
        copies = []
        for step in range(1, experts):
            peer = lax.rem(me + step, experts)
            copy = pltpu.make_async_remote_copy(
                src_ref=source.at[peer],
                dst_ref=target.at[me],
                send_sem=send_sems.at[kind, step],
                recv_sem=recv_sems.at[kind, step],
                device_id=(here, peer),
                device_id_type=MESH,
            )
            copy.start()
            copies.append(copy)
        target[me] = source[me]
        return copies

    def hand(source, target, sems, level):
        copy = pltpu.make_async_remote_copy(
            src_ref=source,
            dst_ref=target,
            send_sem=sems.at[0],
            recv_sem=sems.at[1],
            device_id=mates[level],
            device_id_type=MESH,
        )
        copy.start()
        return copy

    def arrive(copies):
        for copy in copies:
            copy.wait_recv()

    open_sends = []

    def spread(level):
        step = 2**level
        copies = [hand(w_out.at[s], w_out.at[s + step], spread_sems.at[1, s + step], level) for s in range(0, slices, 2 * step)]
        open_sends.extend(copies)
        return copies

    spots = lax.broadcasted_iota(jnp.int32, (column_ref.shape[0], places), 1).astype(jnp.float32)
    columns = jnp.concatenate([column_ref[...]] * (places // LANES), axis=1)
    finder = (spots == columns).astype(jnp.float32).astype(jnp.bfloat16)
    sent[0] = contract(finder, tokens_ref[...], 0, 0).astype(jnp.bfloat16).reshape(experts, room, width)
    pl.semaphore_wait(barrier, experts - 1 + levels)
    first = exchange(sent.at[0], got.at[0], 0)
    for load in loads:
        load.wait()
    widening = [spread(levels - 1)]
    paired = [hand(w_in.at[s], w_in.at[s + 1], spread_sems.at[0, s], 0) for s in even]
    sent[1] = contract(finder, grads_ref[...], 0, 0).astype(jnp.bfloat16).reshape(experts, room, width)
    second = exchange(sent.at[1], got.at[1], 1)

    arrive(first)
    rows = got[0].reshape(places, width)
    for s in list(even) + list(odd):
        if s == 1:
            arrive(paired)
        hidden[...] = dot(rows, w_in[s])

        def curve(index, unused):
            at = pl.ds(pl.multiple_of(index * ROWS_AT_ONCE, ROWS_AT_ONCE), ROWS_AT_ONCE)
            value = hidden[at, :]
            bell = 0.5 + 0.5 * lax.erf(value * 0.7071067811865476)
            active[s, at, :] = (value * bell).astype(jnp.bfloat16)
            slope[s, at, :] = bell + value * (jnp.exp(-0.5 * value * value) * 0.3989422804014327)
            return unused

        lax.fori_loop(0, places // ROWS_AT_ONCE, curve, 0)

    for level in reversed(range(levels - 1)):
        arrive(widening[-1])
        widening.append(spread(level))
    for s in list(even) + list(odd):
        if s == 1:
            arrive(widening[-1])
        product = dot(active[s], w_out[s])
        total[...] = product if s == 0 else total[...] + product
    answer[0] = total[...].astype(jnp.bfloat16).reshape(experts, room, width)
    third = exchange(answer.at[0], returned.at[0], 2)

    arrive(second)
    pulled = got[1].reshape(places, width)
    for s in range(slices):
        inner[s] = (contract(pulled, w_out[s], 1, 1) * slope[s]).astype(jnp.bfloat16)
        product = contract(inner[s], w_in[s], 1, 1)
        total[...] = product if s == 0 else total[...] + product
    answer[1] = total[...].astype(jnp.bfloat16).reshape(experts, room, width)
    fourth = exchange(answer.at[1], returned.at[1], 3)
    joining = []
    for s in list(odd) + list(even):
        sum_out[s] = contract(active[s], pulled, 0, 0).astype(jnp.bfloat16)
        if s % 2:
            joining.append(hand(sum_out.at[s], pair_out.at[s // 2], mate_sems.at[0, s // 2], 0))

    def add_into(target, addend):
        def some(index, unused):
            at = pl.ds(pl.multiple_of(index * 4 * ROWS_AT_ONCE, 4 * ROWS_AT_ONCE), 4 * ROWS_AT_ONCE)
            target[at, :] = target[at, :] + addend[at, :]
            return unused

        lax.fori_loop(0, target.shape[0] // (4 * ROWS_AT_ONCE), some, 0)

    arrive(joining)
    for k, s in enumerate(even):
        add_into(sum_out.at[s], pair_out.at[k])

    def pass_on(level):
        step = 2**level
        return [
            hand(sum_out.at[s + step], far_out.at[slices // step // 2 - 1 + s // (2 * step)], far_sems.at[level, s // (2 * step)], level)
            for s in range(0, slices, 2 * step)
        ]

    open_sends.extend(joining)
    for level in range(1, levels - 1):
        passing = pass_on(level)
        arrive(passing)
        open_sends.extend(passing)
        step = 2**level
        for s in range(0, slices, 2 * step):
            add_into(sum_out.at[s], far_out.at[slices // step // 2 - 1 + s // (2 * step)])
    stores = [
        pltpu.make_async_copy(sum_out.at[0], kept_out, sum_sems.at[len(even)]),
        pltpu.make_async_copy(sum_out.at[slices // 2], leaving_out, sum_sems.at[len(even) + 1]),
    ]
    for store in stores:
        store.start()
    move = row_half(sum_out.at[slices // 2], arriving_out, moved_sems, ("ctx", levels - 1), 0)
    move.start()
    for low in range(0, places, LANES):
        for left in range(0, width, LANES):
            square = got[0].reshape(places, width)[low : low + LANES, left : left + LANES].astype(jnp.float32).T
            rows_t[left : left + LANES, low : low + LANES] = square.astype(jnp.bfloat16)
    for copy in paired:
        copy.wait_send()
    joined = []
    for s in list(odd) + list(even):
        w_in[s] = dot(rows_t[...], inner[s]).astype(jnp.bfloat16)
        if s % 2:
            joined.append(hand(w_in.at[s], pair_in.at[s // 2], mate_sems.at[1, s // 2], 0))
    arrive(joined)
    for k, s in enumerate(even):
        add_into(w_in.at[s], pair_in.at[k])
        stores.append(pltpu.make_async_copy(w_in.at[s], sums_in[k], sum_sems.at[k]))
        stores[-1].start()

    arrive(third)
    picked_ref[...] = dot(finder, returned[0].reshape(places, width)).astype(jnp.bfloat16)
    arrive(fourth)
    back_ref[...] = dot(finder, returned[1].reshape(places, width)).astype(jnp.bfloat16)
    for store in stores:
        store.wait()
    move.wait()
    for copies in (first, second, third, fourth, joined, open_sends):
        for copy in copies:
            copy.wait_send()


def run_experts(rows, grads, target, weights_in, weight_out, experts, room, identity):
    slices = 2 * len(weights_in)
    tokens, width = rows.shape
    inner_width = weight_out.shape[0]
    places = experts * room
    inside = pl.BlockSpec(memory_space=pltpu.VMEM)
    anywhere = pl.BlockSpec(memory_space=pl.ANY)
    half = jnp.bfloat16
    count = len(weights_in)
    out = pl.pallas_call(
        functools.partial(expert_kernel, slices),
        in_specs=[inside] * 3 + [anywhere] * (count + 1),
        out_specs=[inside] * 2 + [anywhere] * (count + 3),
        out_shape=[jax.ShapeDtypeStruct(rows.shape, half)] * 2
        + [jax.ShapeDtypeStruct(weight.shape, half) for weight in weights_in]
        + [jax.ShapeDtypeStruct(weight_out.shape, half)] * 3,
        scratch_shapes=[pltpu.VMEM((2, experts, room, width), half)] * 4
        + [
            pltpu.VMEM((slices, width, inner_width), half),
            pltpu.VMEM((slices, inner_width, width), half),
            pltpu.VMEM((places, inner_width), jnp.float32),
            pltpu.VMEM((places, width), jnp.float32),
            pltpu.VMEM((slices, places, inner_width), half),
            pltpu.VMEM((slices, places, inner_width), jnp.float32),
            pltpu.VMEM((slices, places, inner_width), half),
            pltpu.VMEM((slices, inner_width, width), half),
            pltpu.VMEM((count, inner_width, width), half),
            pltpu.VMEM((count, width, inner_width), half),
            pltpu.VMEM((count, inner_width, width), half),
            pltpu.VMEM((width, places), half),
            pltpu.SemaphoreType.DMA((4, experts)),
            pltpu.SemaphoreType.DMA((4, experts)),
            pltpu.SemaphoreType.DMA((slices + 1,)),
            pltpu.SemaphoreType.DMA((count + 2,)),
            pltpu.SemaphoreType.DMA((2, slices, 2)),
            pltpu.SemaphoreType.DMA((2, count, 2)),
            pltpu.SemaphoreType.DMA((slices, count, 2)),
            pltpu.SemaphoreType.DMA((2, 2)),
        ],
        compiler_params=pltpu.CompilerParams(
            collective_id=identity, has_side_effects=True, vmem_limit_bytes=63 * 1024 * 1024
        ),
        name="run_experts",
    )(rows, grads, target, *weights_in, weight_out)
    return out[0], out[1], list(out[2 : 2 + count]), out[2 + count :]


def flipped(value, level):
    count = lax.axis_size("ctx")
    return lax.ppermute(value, "ctx", [(source, source ^ (1 << level)) for source in range(count)])


def spread_slices(own, far):
    levels = lax.axis_size("ctx").bit_length() - 1
    slices = {0: own, 1 << (levels - 1): far}
    for level in reversed(range(1, levels - 1)):
        for offset in sorted(slices):
            slices[offset + (1 << level)] = flipped(slices[offset], level)
    return [slices[offset] for offset in sorted(slices)]


def collect_slices(sums):
    levels = lax.axis_size("ctx").bit_length() - 1
    for level in range(1, levels - 1):
        arrived = [flipped(values, level).astype(jnp.float32) for values in sums[1::2]]
        sums = [
            (values.astype(jnp.float32) + other).astype(jnp.bfloat16) for values, other in zip(sums[::2], arrived)
        ]
    return sums


def body(
    inputs,
    segments,
    routes,
    cotangent,
    norm_gain,
    in_proj,
    conv_taps,
    conv_bias,
    x_proj,
    dt_proj,
    dt_bias,
    log_decay,
    skip_gain,
    out_proj,
    moe_gain,
    router,
    expert_in,
    expert_out,
):
    experts = router.shape[1]
    half_rows = norm_gain.shape[0]
    small = (
        x_proj,
        dt_proj,
        conv_taps.T,
        log_decay.T,
        jnp.stack([conv_bias, dt_bias, skip_gain]),
        jnp.stack([norm_gain, moe_gain]),
        router.T,
    )
    sizes = [(name, lax.axis_size(name)) for name in ("ctx", "exp")]
    weights, partial, begun, *prior = gather_all(
        sizes, small, in_proj, out_proj, inputs[0], segments, expert_in[0], 0
    )
    tokens_here = inputs.shape[1]
    capacity = 5 * tokens_here // (4 * experts)
    room = -(-capacity // 16) * 16
    (
        scan_rows,
        products,
        normed_one,
        b_turned,
        c_turned,
        rates,
        by_channel,
        gain_rows,
        delta_low,
        same_rows,
        target,
        kept,
        (conv_ext, conv_out, xs_val, dt_pre, masked_step, push),
        (full_gate, full_out),
        far_in,
    ) = scan_forward(
        sizes,
        inputs[0],
        prior,
        (segments, routes.reshape(1, tokens_here)),
        weights,
        room,
        partial,
        expert_in[0],
        begun,
        3,
    )
    weights_in = spread_slices(expert_in[0], far_in)
    full_conv, full_channel, full_width = weights
    normed_two, residual, gate_z, probability, grad_pick, gated_turned, normed_turned = open_gate(
        scan_rows,
        xs_val,
        normed_one,
        inputs[0],
        cotangent[0],
        target,
        [full_gate, full_out, full_width, by_channel, gain_rows],
        room,
        experts,
    )
    picked, grad_from_experts, grad_expert_in, (kept_out, leaving_out, begun_out) = run_experts(
        normed_two, grad_pick, target, weights_in, expert_out[0], experts, room, 2
    )
    kept_in, leaving = collect_slices(grad_expert_in)
    out_block, grad_resid, grad_y, grad_z, wide_rows, grad_out_proj, grad_gate_proj = middle(
        [picked, grad_from_experts, cotangent[0], residual, gate_z, scan_rows, xs_val, normed_two, probability, target],
        [gated_turned, normed_turned],
        [full_out, full_width, by_channel, gain_rows],
        room,
        experts,
    )
    along_b, slope, grad_bs, grad_cs, grad_a, partial_sums, begun_in = scan_backward(
        sizes,
        masked_step,
        push,
        grad_y,
        b_turned,
        c_turned,
        rates,
        products,
        (grad_gate_proj, grad_out_proj),
        kept,
        leaving,
        4,
    )
    finished = finish(
        sizes,
        (along_b, slope, grad_y, dt_pre, conv_out, xs_val, conv_ext, grad_z, full_conv, full_gate),
        (
            normed_turned,
            inputs[0],
            grad_resid,
            full_channel,
            jnp.pad(jnp.concatenate([grad_bs, grad_cs], axis=1), ((0, 0), (R, LANES - R - 2 * NS))),
            delta_low,
            same_rows,
            by_channel,
            grad_a,
            rates,
            wide_rows,
        ),
        partial_sums,
        (leaving, leaving_out),
        (begun_in, begun_out),
        1,
    )
    grad_inputs, own_in, own_out, own_small, own_thin, arrived, arrived_out = finished
    grad_inputs, grad_w_out, grad_w_in, own_in, own_out, own_x, own_dt, own_taps, own_decay, own_router, *vectors = (
        emit_outputs(
            grad_inputs, kept_out, arrived_out, kept_in, arrived, own_in, own_out, own_small, own_thin, experts
        )
    )
    own_bias, own_dtbias, own_skip, own_norm, own_moe = [values[0] for values in vectors]
    return (
        out_block[None],
        grad_inputs[None],
        own_norm,
        own_in,
        own_taps.T,
        own_bias,
        own_x,
        own_dt,
        own_dtbias,
        own_decay.T,
        own_skip,
        own_out,
        own_moe,
        own_router.T,
        grad_w_in[None],
        grad_w_out[None],
    )


def solution(mesh):
    placed = (
        P("exp", "ctx", None),
        P("exp", "ctx"),
        P("exp", "ctx", None),
        P("exp", "ctx", None),
        P(("ctx", "exp")),
        P(("ctx", "exp"), None),
        P(("ctx", "exp"), None),
        P(("ctx", "exp")),
        P(("ctx", "exp"), None),
        P(None, ("ctx", "exp")),
        P(("ctx", "exp")),
        P(("ctx", "exp"), None),
        P(("ctx", "exp")),
        P(("ctx", "exp"), None),
        P(("ctx", "exp")),
        P(("ctx", "exp"), None),
        P("exp", None, "ctx"),
        P("exp", "ctx", None),
    )
    return jax.shard_map(
        body,
        mesh=mesh,
        in_specs=placed,
        out_specs=(
            P("exp", "ctx", None),
            P("exp", "ctx", None),
            P(("ctx", "exp")),
            P(("ctx", "exp"), None),
            P(("ctx", "exp"), None),
            P(("ctx", "exp")),
            P(("ctx", "exp"), None),
            P(None, ("ctx", "exp")),
            P(("ctx", "exp")),
            P(("ctx", "exp"), None),
            P(("ctx", "exp")),
            P(("ctx", "exp"), None),
            P(("ctx", "exp")),
            P(("ctx", "exp"), None),
            P("exp", None, "ctx"),
            P("exp", "ctx", None),
        ),
        check_vma=False,
    )
```
